32 devices in a mesh: dp: 4 (over z), row: 2 (over x), col: 4 (over y, core).
Axes of the slice: x: 2, y: 2, z: 4, core: 2. Of those that a mesh axis runs over, the one named last changes fastest.
Arguments:
- tokens: bfloat16 [4096, 2048], P(('dp', 'row'), 'col'), may hold values from -6 to 6
- cotangent: bfloat16 [4096, 2048], P(('dp', 'row'), 'col'), may hold values from -6 to 6
- query_master: float32 [2048, 2048], P('col', ('row', 'dp')), may hold values from -0.1875 to 0.1875
- key_master: float32 [2048, 2048], P('col', ('row', 'dp')), may hold values from -0.125 to 0.125
- value_master: float32 [2048, 2048], P('col', ('row', 'dp')), may hold values from -0.125 to 0.125
- out_master: float32 [2048, 2048], P(('row', 'dp'), 'col'), may hold values from -2 to 2
- gate_master: float32 [2048, 8192], P('col', ('row', 'dp')), may hold values from -0.125 to 0.125
- up_master: float32 [2048, 8192], P('col', ('row', 'dp')), may hold values from -0.125 to 0.125
- down_master: float32 [8192, 2048], P(('row', 'dp'), 'col'), may hold values from -0.0625 to 0.0625
- attn_gain: float32 [2048], P('col'), may hold values from 0.1 to 1.9
- ffn_gain: float32 [2048], P('col'), may hold values from 0.1 to 1.9
- lengths: int32 [28], replicated, may hold values from 1 to 768, as said below
- permutation: int32 [4096], replicated, may hold values from 0 to 4095, as said below
Outputs:
- grad_tokens: float32 [4096, 2048], P(('dp', 'row'), 'col')
- grad_query: float32 [2048, 2048], P('col', ('row', 'dp'))
- grad_key: float32 [2048, 2048], P('col', ('row', 'dp'))
- grad_value: float32 [2048, 2048], P('col', ('row', 'dp'))
- grad_out: float32 [2048, 2048], P(('row', 'dp'), 'col')
- grad_gate: float32 [2048, 8192], P('col', ('row', 'dp'))
- grad_up: float32 [2048, 8192], P('col', ('row', 'dp'))
- grad_down: float32 [8192, 2048], P(('row', 'dp'), 'col')
- grad_attn_gain: float32 [2048], P('col')
- grad_ffn_gain: float32 [2048], P('col')
The draws below stay inside these ranges and needn't reach their ends.
Inputs may be any that keep to these rules, and one draw needn't show every extreme that they name: 28 lengths; those of each group's 7 sequences sum to 1024, and the largest of every group is 768. A permutation of all token indices; the slots of group d hold exactly the tokens of 7 whole sequences; laid one after another, these sequences are cut into blocks of 32 tokens, and block b goes to the quarter b % 4 of the group's slots, in order.
All inputs are finite; a program needn't handle non-finite values.
Results may differ from the reference program's by a relative error of at most 0.015.
The reference program's roundings to bfloat16 on the way count: a program that leaves them out, or rounds other values in their place, can miss the bound.
Values may be sent and summed in bfloat16 or wider, within the bound.
A program may use at most 256 MiB of HBM per device.

```python
import jax
import jax.numpy as jnp
from jax import lax

D = 2048
HEADS = 16
HEAD_DIM = 128
FF = 8192
BLOCK_TOK = 32
SEQ_GROUP = 7
GROUP = 1024
TOKENS = 4096
LONGEST = 768
N_DP = 4
N_COL = 4


def shuffle_one(subkey):
    return jax.random.permutation(subkey, SEQ_GROUP).astype(jnp.int32)


def packing(key):
    base_key = jax.random.fold_in(key, 4242)
    key_list = jax.random.split(base_key, 3)
    remainder = GROUP - LONGEST
    even_share = remainder // (SEQ_GROUP - 1)
    leftover = remainder - even_share * (SEQ_GROUP - 1)
    jitter = jax.random.randint(key_list[0], (N_DP, (SEQ_GROUP - 1) // 2), -(even_share // 2), even_share // 2 + 1).astype(jnp.int32)
    pieces = jnp.concatenate([even_share + jitter, even_share - jitter], axis=1).astype(jnp.int32)
    pieces = pieces.at[:, 0].add(leftover)
    longest = jnp.full((N_DP, 1), LONGEST, jnp.int32)
    group_len = jnp.concatenate([longest, pieces], axis=1).astype(jnp.int32)
    shuffle = jax.vmap(shuffle_one)(jax.random.split(key_list[1], N_DP))
    group_len = jnp.take_along_axis(group_len, shuffle, axis=1).astype(jnp.int32)
    flat_len = group_len.reshape(-1)
    seq_total = N_DP * SEQ_GROUP
    given_order = jax.random.permutation(key_list[2], seq_total).astype(jnp.int32)
    lengths = jnp.take(flat_len, given_order).astype(jnp.int32)
    rank_of = jnp.zeros((seq_total,), jnp.int32).at[given_order].set(jnp.arange(seq_total, dtype=jnp.int32))
    given_start = (jnp.cumsum(lengths).astype(jnp.int32) - lengths).astype(jnp.int32)
    seq_start = jnp.take(given_start, rank_of).astype(jnp.int32)
    group_ends = jnp.cumsum(group_len, axis=1).astype(jnp.int32)
    offset = jnp.arange(GROUP, dtype=jnp.int32)
    passed = group_ends[:, None, :] <= offset[None, :, None]
    member = jnp.sum(passed.astype(jnp.int32), axis=2).astype(jnp.int32)
    begin = jnp.max(jnp.where(passed, group_ends[:, None, :], 0), axis=2).astype(jnp.int32)
    within = (offset[None, :] - begin).astype(jnp.int32)
    seq_id = (jnp.arange(N_DP, dtype=jnp.int32)[:, None] * SEQ_GROUP + member).astype(jnp.int32)
    source = (jnp.take(seq_start, seq_id) + within).astype(jnp.int32)
    block_of = offset // BLOCK_TOK
    slot_place = block_of % N_COL * (GROUP // N_COL) + block_of // N_COL * BLOCK_TOK + offset % BLOCK_TOK
    target = (jnp.arange(N_DP, dtype=jnp.int32)[:, None] * GROUP + slot_place[None, :]).astype(jnp.int32)
    owners = jnp.zeros((TOKENS,), jnp.int32).at[target.reshape(-1)].set(source.reshape(-1))
    return (lengths, owners)


def draw_lengths(key, part):
    lengths, owners = packing(key)
    return lengths


def draw_permutation(key, part):
    lengths, owners = packing(key)
    return owners


def levels(key, extent, shards, low, largest):
    factor_of = 1.0
    for axis_at, shards_of in shards:
        steps = jax.random.uniform(jax.random.fold_in(jax.random.fold_in(key, 6), axis_at), (shards_of,), jnp.float32, low / len(shards), largest / len(shards))
        factor_of = factor_of * jnp.repeat(jnp.exp(steps), extent[axis_at] // shards_of).reshape((-1,) + (1,) * (len(extent) - 1 - axis_at))
    return factor_of


def gaussian(key, extent, width, reach, cuts=(), kind=jnp.bfloat16):
    values = jax.random.normal(key, extent, jnp.float32) * width
    if len(cuts) > 0:
        values = levels(key, extent, cuts, -0.22, 0.18) * values
    return jnp.clip(values, min=-reach, max=reach).astype(kind)


def setup_inputs(seed: int = 0) -> dict:
    arg_keys = jax.random.split(jax.random.key(seed), 14)
    tokens = gaussian(arg_keys[0], (TOKENS, D), 1.0, 6.0, ((0, 8), (1, 4)))
    cotangent = gaussian(arg_keys[1], (TOKENS, D), 1.0, 6.0, ((0, 8), (1, 4)))
    query_master = gaussian(arg_keys[2], (D, D), (D // 2) ** -0.5, 0.1875, ((0, 4), (1, 8)), jnp.float32)
    key_master = gaussian(arg_keys[3], (D, D), D ** -0.5, 0.125, ((0, 4), (1, 8)), jnp.float32)
    value_master = gaussian(arg_keys[4], (D, D), D ** -0.5, 0.125, ((0, 4), (1, 8)), jnp.float32)
    out_master = gaussian(arg_keys[5], (D, D), (max(1, D // 256)) ** -0.5, 2.0, ((0, 8), (1, 4)), jnp.float32)
    gate_master = gaussian(arg_keys[6], (D, FF), D ** -0.5, 0.125, ((0, 4), (1, 8)), jnp.float32)
    up_master = gaussian(arg_keys[7], (D, FF), D ** -0.5, 0.125, ((0, 4), (1, 8)), jnp.float32)
    down_master = gaussian(arg_keys[8], (FF, D), FF ** -0.5, 0.0625, ((0, 8), (1, 4)), jnp.float32)
    attn_gain = jnp.clip(1.0 + 0.18 * jax.random.normal(arg_keys[9], (D,), jnp.float32), 0.1, 1.9)
    ffn_gain = jnp.clip(1.0 + 0.18 * jax.random.normal(arg_keys[10], (D,), jnp.float32), 0.1, 1.9)
    lengths = draw_lengths(jax.random.fold_in(arg_keys[13], 71), 0)
    permutation = draw_permutation(jax.random.fold_in(arg_keys[13], 71), 0)
    return dict(tokens=tokens, cotangent=cotangent, query_master=query_master, key_master=key_master, value_master=value_master, out_master=out_master, gate_master=gate_master, up_master=up_master, down_master=down_master, attn_gain=attn_gain, ffn_gain=ffn_gain, lengths=lengths, permutation=permutation)


@jax.custom_vjp
def low(v):
    return lax.optimization_barrier(v.astype(jnp.bfloat16)).astype(jnp.float32)

@jax.custom_vjp
def low_back(v):
    return v

def low_keep(v):
    return (low(v), None)

def low_pass(kept, grad):
    return (grad,)

def back_keep(v):
    return (v, None)

def back_low(kept, grad):
    return (low(grad),)
low.defvjp(low_keep, low_pass)
low_back.defvjp(back_keep, back_low)
EPSILON = 1e-06
NEG_FILL = -1e+30

def matmul(left_rows, right_rows):
    return jnp.dot(left_rows, right_rows, precision=lax.Precision.HIGHEST)

def layer(inputs_f, weights_all, member, position):
    query_w, key_w, value_w, out_w, gate_w, up_w, down_w, gain_one, gain_two = weights_all
    group_rows = inputs_f.shape[0]
    scale_one = lax.rsqrt(lax.optimization_barrier(jnp.mean(inputs_f * inputs_f, axis=1, keepdims=True)) + EPSILON)
    normed_one = low(inputs_f * scale_one * gain_one[None, :])
    queries = low_back(low(matmul(normed_one, low(query_w))))
    keys_all = low_back(low(matmul(normed_one, low(key_w))))
    values_all = low_back(low(matmul(normed_one, low(value_w))))
    visible = (member[:, None] == member[None, :]) & (position[None, :] <= position[:, None])

    def attend_head(head_inputs):
        query_h, key_h, value_h = head_inputs
        scores = low_back(matmul(query_h, key_h.T) * HEAD_DIM ** (-0.5))
        scores = jnp.where(visible, scores, NEG_FILL)
        highest = lax.optimization_barrier(jnp.max(scores, axis=1, keepdims=True))
        expo = jnp.exp(scores - highest)
        probability = expo / lax.optimization_barrier(jnp.sum(expo, axis=1, keepdims=True))
        return matmul(low(probability), value_h)

    def split_heads(matrix):
        return matrix.reshape(group_rows, HEADS, HEAD_DIM).transpose(1, 0, 2)
    head_out = lax.map(jax.checkpoint(attend_head), (split_heads(queries), split_heads(keys_all), split_heads(values_all)))
    attended = low_back(low(head_out.transpose(1, 0, 2).reshape(group_rows, D)))
    midway = inputs_f + low_back(matmul(attended, low(out_w)))
    scale_two = lax.rsqrt(lax.optimization_barrier(jnp.mean(midway * midway, axis=1, keepdims=True)) + EPSILON)
    normed_two = low(midway * scale_two * gain_two[None, :])
    gate_value = low_back(matmul(normed_two, low(gate_w)))
    up_value = low_back(matmul(normed_two, low(up_w)))
    hidden = low(jax.nn.silu(gate_value) * up_value)
    return midway + low_back(matmul(hidden, low(down_w)))

def reference(tokens, cotangent, query_master, key_master, value_master, out_master, gate_master, up_master, down_master, attn_gain, ffn_gain, lengths, permutation):
    seq_ends = jnp.cumsum(lengths).astype(jnp.int32)
    passed = seq_ends[None, :] <= permutation[:, None]
    member = lax.optimization_barrier(jnp.sum(passed.astype(jnp.int32), axis=1)).astype(jnp.int32)
    begins = lax.optimization_barrier(jnp.max(jnp.where(passed, seq_ends[None, :], 0), axis=1)).astype(jnp.int32)
    position = (permutation - begins).astype(jnp.int32)
    own_tokens = jnp.take(tokens.astype(jnp.float32), permutation, axis=0).reshape(N_DP, GROUP, D)
    own_cotangent = jnp.take(cotangent.astype(jnp.float32), permutation, axis=0).reshape(N_DP, GROUP, D)
    params = (query_master, key_master, value_master, out_master, gate_master, up_master, down_master, attn_gain, ffn_gain)

    def one_group(running, group_inputs):
        group_tokens, group_cotangent, group_member, group_position = group_inputs

        def forward(inputs_f, weights_all):
            return layer(inputs_f, weights_all, group_member, group_position)
        layer_out, pullback = jax.vjp(forward, group_tokens, params)
        grad_in, grad_params = pullback(group_cotangent)
        return (jax.tree.map(jnp.add, running, grad_params), grad_in)
    start_sums = jax.tree.map(jnp.zeros_like, params)
    running, grad_own = lax.scan(one_group, start_sums, (own_tokens, own_cotangent, member.reshape(N_DP, GROUP), position.reshape(N_DP, GROUP)))
    grad_tokens = jnp.zeros((TOKENS, D), jnp.float32).at[permutation].set(grad_own.reshape(TOKENS, D))
    return (grad_tokens, running[0], running[1], running[2], running[3], running[4], running[5], running[6], running[7], running[8])
```

```python
import functools

import jax
import jax.numpy as jnp
from jax import lax
from jax.experimental import pallas as pl
from jax.experimental.pallas import tpu as pltpu
from jax.sharding import PartitionSpec as P

D = 2048
HEAD_DIM = 128


EPSILON = 1e-06
NEG_FILL = -1e30
AXES = ("dp", "row", "col")
DP, ROW, COL = 4, 2, 4
REACH = 768
BF = jnp.bfloat16
F32 = jnp.float32


def running_sum(lengths):
    count = lengths.shape[0]
    earlier = jnp.arange(count)[:, None] <= jnp.arange(count)[None, :]
    return jnp.sum(jnp.where(earlier, lengths[:, None], 0), axis=0)

def make_picker(wanted, carried, pieces):
    amount = pieces[0].shape[0]
    inside = (wanted >= 0) & (wanted < amount)
    chosen = jnp.clip(wanted, 0, amount - 1)
    return tuple(
        (
            jnp.where(inside[:, None], jnp.take(shard_rows, chosen, axis=0), current)
            for shard_rows, current in zip(pieces, carried)
        )
    )


def sequence_marks(permutation, lengths, first_slot, amount):
    source = lax.dynamic_slice_in_dim(permutation, first_slot, amount)
    seq_ends = running_sum(lengths)
    passed = seq_ends[None, :] <= source[:, None]
    member = jnp.sum(passed.astype(jnp.int32), axis=1)
    begins = jnp.max(jnp.where(passed, seq_ends[None, :], 0), axis=1)
    return (member, source - begins)


def col_total(values):
    return lax.psum(jnp.sum(values, axis=1), "col")


def row_gather(values):
    return lax.all_gather(values, "row", axis=0, tiled=True)


def col_gather(values):
    return lax.all_gather(values, "col", axis=0, tiled=True)


def key_gather(keys_here, values_here):
    return (
        lax.all_gather(keys_here, "col", axis=0, tiled=True),
        lax.all_gather(values_here, "col", axis=0, tiled=True),
    )


def multiply(row_block, weight, transpose_right):
    if transpose_right:
        return lax.dot_general(
            row_block, weight, (((1,), (1,)), ((), ())), preferred_element_type=jnp.float32
        )
    return jnp.dot(row_block, weight, preferred_element_type=jnp.float32)


def outer_sum(left_rows, right_rows):
    return lax.dot_general(
        left_rows, right_rows, (((0,), (0,)), ((), ())), preferred_element_type=jnp.float32
    )


def col_reduce(spread, weight, transpose_right):
    return lax.psum_scatter(
        multiply(spread, weight, transpose_right), "col", scatter_dimension=0, tiled=True
    )


def row_reduce(spread, weight, transpose_right):
    return lax.psum_scatter(
        multiply(spread, weight, transpose_right), "row", scatter_dimension=0, tiled=True
    )


def visible(query_member, query_position, member, position):
    same = query_member[:, None] == member[None, :]
    behind = position[None, :] <= query_position[:, None]
    return same & behind


def attend_scores(query_block, key_all, allowed):
    scores = jnp.einsum(
        "qhd,khd->hqk", query_block, key_all, preferred_element_type=jnp.float32
    ) * HEAD_DIM ** (-0.5)
    return jnp.where(allowed[None, :, :], scores, NEG_FILL)


def norm_back(grad_normed, inputs_f, scale_rows, gain):
    gain_part = jnp.sum(grad_normed * inputs_f * scale_rows[:, None], axis=0)
    scaled = grad_normed * gain[None, :]
    inner = col_total(scaled * inputs_f)
    grad_inputs = scale_rows[:, None] * scaled - inputs_f * (scale_rows**3 * inner / D)[:, None]
    return (grad_inputs, gain_part)


def on_any_mesh(
    tokens,
    cotangent,
    query_master,
    key_master,
    value_master,
    out_master,
    gate_master,
    up_master,
    down_master,
    attn_gain,
    ffn_gain,
    lengths,
    permutation,
):
    own_rows = tokens.shape[0]
    group_rows = own_rows * lax.axis_size("row")
    quarter = group_rows // lax.axis_size("col")
    device_slot = lax.axis_index(("dp", "row"))
    group_slot = lax.axis_index("dp")
    col_slot = lax.axis_index("col")
    own_sources = lax.dynamic_slice_in_dim(permutation, device_slot * own_rows, own_rows)
    own_tokens, own_cotangent = make_picker(
        own_sources,
        (jnp.zeros_like(tokens), jnp.zeros_like(cotangent)),
        (
            lax.all_gather(tokens, ("dp", "row"), axis=0, tiled=True),
            lax.all_gather(cotangent, ("dp", "row"), axis=0, tiled=True),
        ),
    )
    masters = tuple(
        (
            matrix.astype(jnp.bfloat16)
            for matrix in (
                query_master,
                key_master,
                value_master,
                out_master,
                gate_master,
                up_master,
                down_master,
            )
        )
    )
    query_weight, key_weight, value_weight, out_weight, gate_weight, up_weight, down_weight = (
        lax.all_gather(masters[0], "dp", axis=1, tiled=True),
        lax.all_gather(masters[1], "dp", axis=1, tiled=True),
        lax.all_gather(masters[2], "dp", axis=1, tiled=True),
        lax.all_gather(masters[3], "dp", axis=0, tiled=True),
        lax.all_gather(masters[4], "dp", axis=1, tiled=True),
        lax.all_gather(masters[5], "dp", axis=1, tiled=True),
        lax.all_gather(masters[6], "dp", axis=0, tiled=True),
    )
    attention_in = jnp.concatenate([query_weight, key_weight, value_weight], axis=1)
    feedforward_in = jnp.concatenate([gate_weight, up_weight], axis=1)
    width_row = query_weight.shape[1]
    heads_row = width_row // HEAD_DIM
    hidden_row = gate_weight.shape[1]
    member, position = sequence_marks(permutation, lengths, group_slot * group_rows, group_rows)
    query_member = lax.dynamic_slice_in_dim(member, col_slot * quarter, quarter)
    query_position = lax.dynamic_slice_in_dim(position, col_slot * quarter, quarter)
    block_rows = min(512, quarter)
    block_count = quarter // block_rows
    residual_in = own_tokens.astype(jnp.float32)
    scale_one = lax.rsqrt(col_total(residual_in * residual_in) / D + EPSILON)
    normed_one = (residual_in * scale_one[:, None] * attn_gain[None, :]).astype(jnp.bfloat16)
    spread_one = row_gather(normed_one)
    projected = col_reduce(spread_one, attention_in, False).astype(jnp.bfloat16)
    queries = projected[:, :width_row].reshape(quarter, heads_row, HEAD_DIM)
    keys_here = projected[:, width_row : 2 * width_row]
    values_here = projected[:, 2 * width_row :]
    key_flat, value_flat = key_gather(keys_here, values_here)
    key_all = key_flat.reshape(group_rows, heads_row, HEAD_DIM)
    value_all = value_flat.reshape(group_rows, heads_row, HEAD_DIM)

    def block_mask(first_row):
        return visible(
            lax.dynamic_slice_in_dim(query_member, first_row, block_rows),
            lax.dynamic_slice_in_dim(query_position, first_row, block_rows),
            member,
            position,
        )

    def forward_block(block_id):
        first_row = block_id * block_rows
        query_block = lax.dynamic_slice_in_dim(queries, first_row, block_rows, 0)
        scores = attend_scores(query_block, key_all, block_mask(first_row))
        highest = jnp.max(scores, axis=2, keepdims=True)
        totals = jnp.sum(jnp.exp(scores - highest), axis=2, keepdims=True)
        log_total = highest + jnp.log(totals)
        probability = jnp.exp(scores - log_total)
        output = jnp.einsum(
            "hqk,khd->qhd",
            probability.astype(jnp.bfloat16),
            value_all,
            preferred_element_type=jnp.float32,
        )
        return (output.astype(jnp.bfloat16).reshape(block_rows, width_row), log_total[:, :, 0])

    blocks_out, log_totals = lax.map(forward_block, jnp.arange(block_count, dtype=jnp.int32))
    attended = blocks_out.reshape(quarter, width_row)
    spread_attn = col_gather(attended)
    midway = residual_in + row_reduce(spread_attn, out_weight, False)
    scale_two = lax.rsqrt(col_total(midway * midway) / D + EPSILON)
    normed_two = (midway * scale_two[:, None] * ffn_gain[None, :]).astype(jnp.bfloat16)
    spread_two = row_gather(normed_two)
    gate_and_up = col_reduce(spread_two, feedforward_in, False)
    gate_value = gate_and_up[:, :hidden_row]
    up_value = gate_and_up[:, hidden_row:]
    sigmoid_gate = jax.nn.sigmoid(gate_value)
    hidden = (gate_value * sigmoid_gate * up_value).astype(jnp.bfloat16)
    grad_output = own_cotangent.astype(jnp.float32)
    spread_down = row_gather(own_cotangent)
    grad_hidden = col_reduce(spread_down, down_weight, True)
    spread_hidden = col_gather(hidden)
    grad_down = outer_sum(spread_hidden, spread_down)
    grad_gate_value = (
        grad_hidden * up_value * sigmoid_gate * (1.0 + gate_value * (1.0 - sigmoid_gate))
    ).astype(jnp.bfloat16)
    grad_up_value = (grad_hidden * gate_value * sigmoid_gate).astype(jnp.bfloat16)
    spread_gate_up = col_gather(jnp.concatenate([grad_gate_value, grad_up_value], axis=1))
    grad_normed_two = row_reduce(spread_gate_up, feedforward_in, True)
    spread_two = row_gather(normed_two)
    grad_feedforward = outer_sum(spread_two, spread_gate_up)
    grad_mid_norm, gain_two_part = norm_back(grad_normed_two, midway, scale_two, ffn_gain)
    grad_midway = grad_output + grad_mid_norm
    rounded_midway = grad_midway.astype(jnp.bfloat16)
    spread_back = row_gather(rounded_midway)
    grad_attended = col_reduce(spread_back, out_weight, True).astype(jnp.bfloat16)
    spread_attn = col_gather(attended)
    key_flat, value_flat = key_gather(keys_here, values_here)
    key_all = key_flat.reshape(group_rows, heads_row, HEAD_DIM)
    value_all = value_flat.reshape(group_rows, heads_row, HEAD_DIM)
    grad_out_local = outer_sum(spread_attn, spread_back)

    def backward_block(carried, block_id):
        first_row = block_id * block_rows
        query_block = lax.dynamic_slice_in_dim(queries, first_row, block_rows, 0)
        scores = attend_scores(query_block, key_all, block_mask(first_row))
        probability = jnp.exp(
            scores - lax.dynamic_index_in_dim(log_totals, block_id, 0, keepdims=False)[:, :, None]
        )
        weights_low = probability.astype(jnp.bfloat16)
        grad_block = lax.dynamic_slice_in_dim(grad_attended, first_row, block_rows, 0).reshape(
            block_rows, heads_row, HEAD_DIM
        )
        grad_soft = jnp.einsum(
            "qhd,khd->hqk", grad_block, value_all, preferred_element_type=jnp.float32
        )
        row_inner = jnp.sum(probability * grad_soft, axis=2, keepdims=True)
        grad_scores = (probability * (grad_soft - row_inner)).astype(jnp.bfloat16)
        grad_query_block = jnp.einsum(
            "hqk,khd->qhd", grad_scores, key_all, preferred_element_type=jnp.float32
        ) * HEAD_DIM ** (-0.5)
        grad_key_all = carried[0] + jnp.einsum(
            "hqk,qhd->khd", grad_scores, query_block, preferred_element_type=jnp.float32
        ) * HEAD_DIM ** (-0.5)
        grad_value_all = carried[1] + jnp.einsum(
            "hqk,qhd->khd", weights_low, grad_block, preferred_element_type=jnp.float32
        )
        return (
            (grad_key_all, grad_value_all),
            grad_query_block.astype(jnp.bfloat16).reshape(block_rows, width_row),
        )

    start_grads = jnp.zeros((group_rows, heads_row, HEAD_DIM), jnp.float32)
    key_value_grads, grad_queries = lax.scan(
        backward_block, (start_grads, start_grads), jnp.arange(block_count, dtype=jnp.int32)
    )
    grad_queries = grad_queries.reshape(quarter, width_row)
    grad_key_part = key_value_grads[0].reshape(group_rows, width_row)
    grad_value_part = key_value_grads[1].reshape(group_rows, width_row)
    grad_key_mine, grad_value_mine = (
        lax.psum_scatter(grad_key_part, "col", scatter_dimension=0, tiled=True),
        lax.psum_scatter(grad_value_part, "col", scatter_dimension=0, tiled=True),
    )
    spread_projected = col_gather(
        jnp.concatenate(
            [
                grad_queries,
                grad_key_mine.astype(jnp.bfloat16),
                grad_value_mine.astype(jnp.bfloat16),
            ],
            axis=1,
        )
    )
    grad_normed_one = row_reduce(spread_projected, attention_in, True)
    spread_one = row_gather(normed_one)
    grad_attention = outer_sum(spread_one, spread_projected)
    grad_in_norm, gain_one_part = norm_back(grad_normed_one, residual_in, scale_one, attn_gain)
    grad_own_tokens = grad_midway + grad_in_norm
    grad_attn_gain, grad_ffn_gain = lax.psum((gain_one_part, gain_two_part), ("dp", "row"))
    grad_query, grad_key, grad_value, grad_out, grad_gate, grad_up, grad_down_mine = (
        lax.psum_scatter(
            grad_attention[:, :width_row].astype(jnp.bfloat16),
            "dp",
            scatter_dimension=1,
            tiled=True,
        ).astype(jnp.float32),
        lax.psum_scatter(
            grad_attention[:, width_row : 2 * width_row].astype(jnp.bfloat16),
            "dp",
            scatter_dimension=1,
            tiled=True,
        ).astype(jnp.float32),
        lax.psum_scatter(
            grad_attention[:, 2 * width_row :].astype(jnp.bfloat16),
            "dp",
            scatter_dimension=1,
            tiled=True,
        ).astype(jnp.float32),
        lax.psum_scatter(
            grad_out_local.astype(jnp.bfloat16), "dp", scatter_dimension=0, tiled=True
        ).astype(jnp.float32),
        lax.psum_scatter(
            grad_feedforward[:, :hidden_row].astype(jnp.bfloat16),
            "dp",
            scatter_dimension=1,
            tiled=True,
        ).astype(jnp.float32),
        lax.psum_scatter(
            grad_feedforward[:, hidden_row:].astype(jnp.bfloat16),
            "dp",
            scatter_dimension=1,
            tiled=True,
        ).astype(jnp.float32),
        lax.psum_scatter(
            grad_down.astype(jnp.bfloat16), "dp", scatter_dimension=0, tiled=True
        ).astype(jnp.float32),
    )
    total_tokens = permutation.shape[0]
    inverse = (
        jnp.zeros((total_tokens,), jnp.int32)
        .at[permutation]
        .set(jnp.arange(total_tokens, dtype=jnp.int32))
    )
    wanted_slots = lax.dynamic_slice_in_dim(inverse, device_slot * own_rows, own_rows)
    (grad_tokens,) = make_picker(
        wanted_slots,
        (jnp.zeros_like(grad_own_tokens),),
        (
            (
                lax.all_gather(
                    grad_own_tokens.astype(jnp.bfloat16), ("dp", "row"), axis=0, tiled=True
                ),
            )[0].astype(jnp.float32),
        ),
    )
    return (
        grad_tokens,
        grad_query,
        grad_key,
        grad_value,
        grad_out,
        grad_gate,
        grad_up,
        grad_down_mine,
        grad_attn_gain,
        grad_ffn_gain,
    )


def move(array, to):
    pairs = []
    for d in range(DP):
        for r in range(ROW):
            for c in range(COL):
                target = to(d, r, c)
                if target is not None:
                    e, s, b = target
                    pairs.append(((d * ROW + r) * COL + c, (e * ROW + s) * COL + b))
    return lax.ppermute(array, AXES, pairs)


def by_col(array, step):
    return move(array, lambda d, r, c: (d, r, c ^ step))


def by_plane(array, step):
    return move(array, lambda d, r, c: (d ^ step, r, c))


def by_chip(array, over_x, over_y):
    return move(array, lambda d, r, c: (d, r ^ over_x, c ^ (2 * over_y)))


def col_sum(values):
    return values + by_col(values, 2) + by_col(values, 1) + by_col(values, 3)


def same_sum(values):
    for step in (1, 2):
        values = values + by_plane(values, step)
    return values + by_chip(values, 1, 0)


def plane_gather(block):
    beside = by_chip(block, 1, 0)
    across = by_chip(block, 0, 1)
    corner = by_chip(block, 1, 1)
    rail = jnp.concatenate(
        [jnp.concatenate([block, across], 1), jnp.concatenate([beside, corner], 1)], 0
    )
    return jnp.concatenate([rail, by_col(rail, 1)], 1)


def plane_scatter(left, weight, contract):
    rows = left.shape[0] // 2
    half = D // 2
    numbers = (((1,), (contract,)), ((), ()))
    kept, given = (weight[:, :half], weight[:, half:]) if contract == 0 else (weight[:half], weight[half:])
    theirs = lax.dot_general(left, given, numbers, preferred_element_type=F32).astype(BF)
    arrived = by_col(theirs, 1)
    mine = lax.dot_general(left, kept, numbers, preferred_element_type=F32)
    mine = mine + arrived.astype(F32)
    low = mine.astype(BF)
    part = half // 2
    return (
        mine[:rows, :part]
        + by_chip(low[rows:, :part], 1, 0).astype(F32)
        + by_chip(low[:rows, part:], 0, 1).astype(F32)
        + by_chip(low[rows:, part:], 1, 1).astype(F32)
    )


def hidden_from(step):
    def to(d, s, c):
        b = c ^ step
        return (d, s ^ (b & 1), b)

    return to


def hidden_back(step):
    def to(d, r, c):
        return (d, r ^ (c & 1), c ^ step)

    return to


def begins_of(lengths, first, amount):
    ends = running_sum(lengths)
    place = first + jnp.arange(amount, dtype=jnp.int32)
    passed = ends[None, :] <= place[:, None]
    return jnp.max(jnp.where(passed, ends[None, :], 0), axis=1)


def seen(begin_ref, block, rows, span):
    query = lax.broadcasted_iota(jnp.int32, (rows, span), 0)
    key = lax.broadcasted_iota(jnp.int32, (rows, span), 1)
    begin = begin_ref[:, 0:1] + (REACH - block * rows)
    return (key <= query + REACH) & (key >= begin)


def scores_of(query, key):
    return lax.dot_general(
        query, key, (((1,), (1,)), ((), ())), preferred_element_type=F32
    ) * HEAD_DIM ** (-0.5)


def attend_kernel(begin_ref, q_ref, k_ref, v_ref, o_ref, lse_ref):
    block = pl.program_id(1)
    rows = q_ref.shape[0]
    span = rows + REACH
    window = pl.ds(pl.multiple_of(block * rows, rows), span)
    scores = scores_of(q_ref[...], k_ref[window, :])
    scores = jnp.where(seen(begin_ref, block, rows, span), scores, NEG_FILL)
    highest = jnp.max(scores, axis=1, keepdims=True)
    expo = jnp.exp(scores - highest)
    total = jnp.sum(expo, axis=1, keepdims=True)
    probability = (expo * (1.0 / total)).astype(BF)
    o_ref[...] = jnp.dot(probability, v_ref[window, :], preferred_element_type=F32).astype(BF)
    lse_ref[...] = jnp.broadcast_to(highest + jnp.log(total), lse_ref.shape)


def attend_back_kernel(
    begin_ref, q_ref, k_ref, v_ref, do_ref, lse_ref, dq_ref, dk_ref, dv_ref
):
    block = pl.program_id(1)
    rows = q_ref.shape[0]
    span = rows + REACH
    window = pl.ds(pl.multiple_of(block * rows, rows), span)

    @pl.when(block == 0)
    def _():
        dk_ref[...] = jnp.zeros_like(dk_ref)
        dv_ref[...] = jnp.zeros_like(dv_ref)

    query, key = q_ref[...], k_ref[window, :]
    grad = do_ref[...]
    scores = scores_of(query, key)
    allowed = seen(begin_ref, block, rows, span)
    probability = jnp.where(allowed, jnp.exp(jnp.where(allowed, scores - lse_ref[:, 0:1], 0.0)), 0.0)
    grad_soft = lax.dot_general(
        grad, v_ref[window, :], (((1,), (1,)), ((), ())), preferred_element_type=F32
    )
    inner = jnp.sum(probability * grad_soft, axis=1, keepdims=True)
    grad_scores = (probability * (grad_soft - inner)).astype(BF)
    scale = HEAD_DIM ** (-0.5)
    dq_ref[...] = (jnp.dot(grad_scores, key, preferred_element_type=F32) * scale).astype(BF)
    over = (((0,), (0,)), ((), ()))
    dk_ref[window, :] += lax.dot_general(grad_scores, query, over, preferred_element_type=F32) * scale
    dv_ref[window, :] += lax.dot_general(
        probability.astype(BF), grad, over, preferred_element_type=F32
    )


QROWS = 256


def attention_specs(rows, width):
    by_block = pl.BlockSpec((QROWS, HEAD_DIM), lambda h, i: (i, h))
    whole = pl.BlockSpec((rows + REACH, HEAD_DIM), lambda h, i: (0, h))
    begin = pl.BlockSpec((QROWS, 1), lambda h, i: (i, 0))
    grid = (width // HEAD_DIM, rows // QROWS)
    params = pltpu.CompilerParams(vmem_limit_bytes=40 << 20)
    return grid, by_block, whole, begin, params


def attend(begin, q, k, v):
    rows, width = q.shape
    grid, by_block, whole, begin_spec, params = attention_specs(rows, width)
    area = grid[0] * rows * (QROWS + REACH)
    return pl.pallas_call(
        attend_kernel,
        grid=grid,
        in_specs=[begin_spec, by_block, whole, whole],
        out_specs=[by_block, by_block],
        out_shape=[
            jax.ShapeDtypeStruct((rows, width), BF),
            jax.ShapeDtypeStruct((rows, width), F32),
        ],
        compiler_params=params,
        cost_estimate=pl.CostEstimate(
            flops=4 * area * HEAD_DIM, bytes_accessed=8 * rows * width, transcendentals=area
        ),
    )(begin, q, k, v)


def attend_back(begin, q, k, v, grad, lse):
    rows, width = q.shape
    grid, by_block, whole, begin_spec, params = attention_specs(rows, width)
    area = grid[0] * rows * (QROWS + REACH)
    return pl.pallas_call(
        attend_back_kernel,
        grid=grid,
        in_specs=[begin_spec, by_block, whole, whole, by_block, by_block],
        out_specs=[by_block, whole, whole],
        out_shape=[
            jax.ShapeDtypeStruct((rows, width), BF),
            jax.ShapeDtypeStruct((rows + REACH, width), F32),
            jax.ShapeDtypeStruct((rows + REACH, width), F32),
        ],
        compiler_params=params,
        cost_estimate=pl.CostEstimate(
            flops=10 * area * HEAD_DIM, bytes_accessed=24 * rows * width, transcendentals=area
        ),
    )(begin, q, k, v, grad, lse)


def rounded_norm(values, scale, gain):
    return (values * scale[:, None] * gain[None, :]).astype(BF)


def norm_grads(grad_normed, inputs_f, scale_rows, gain):
    gain_part = jnp.sum(grad_normed * inputs_f * scale_rows[:, None], axis=0)
    scaled = grad_normed * gain[None, :]
    inner = col_sum(jnp.sum(scaled * inputs_f, axis=1))
    grad_inputs = scale_rows[:, None] * scaled - inputs_f * (scale_rows**3 * inner / D)[:, None]
    return grad_inputs, gain_part


def on_small_mesh(
    tokens,
    cotangent,
    query_master,
    key_master,
    value_master,
    out_master,
    gate_master,
    up_master,
    down_master,
    attn_gain,
    ffn_gain,
    lengths,
    permutation,
):
    del permutation
    d, r, c = (lax.axis_index(name) for name in AXES)
    rows = tokens.shape[0]
    group = rows * ROW
    half_rows = rows // 2
    width = query_master.shape[1]
    y = c // 2

    def pick(stack, index):
        return lax.dynamic_index_in_dim(stack, index, 0, keepdims=False)

    def flip(array):
        swapped = jnp.concatenate([array[rows:], array[:rows]], 0)
        return jnp.where(r == 0, array, swapped)

    block_in = jnp.concatenate([query_master, key_master, value_master], 1).astype(BF)
    block_out = out_master.astype(BF)
    in_stack = jnp.stack([block_in] + [by_plane(block_in, j) for j in (1, 2, 3)])
    out_stack = jnp.stack([block_out] + [by_plane(block_out, j) for j in (1, 2, 3)])

    def spread_blocks(stack):
        return [pick(stack, d ^ c)] + [
            by_col(pick(stack, d ^ c ^ m), m) for m in (2, 1, 3)
        ]

    weight_in = jnp.concatenate(spread_blocks(in_stack), 0)
    weight_out = jnp.concatenate(spread_blocks(out_stack), 1)

    x = tokens.astype(F32)
    scale_one = lax.rsqrt(col_sum(jnp.sum(x * x, axis=1)) / D + EPSILON)
    normed_one = plane_gather(rounded_norm(x, scale_one, attn_gain))
    projected = flip(jnp.dot(normed_one, weight_in, preferred_element_type=F32).astype(BF))
    q = projected[:, :width]
    halo = move(
        projected[group - REACH :, width:],
        lambda e, s, b: (e + 1, s, b) if e + 1 < DP else None,
    )
    key_value = jnp.concatenate([halo, projected[:, width:]], 0)
    k, v = key_value[:, :width], key_value[:, width:]
    begin = (begins_of(lengths, d * group, group) - d * group)[:, None]
    attended, lse = attend(begin, q, k, v)
    own_attended = flip(attended)
    midway = x + plane_scatter(own_attended, weight_out, 0)

    hidden_in = jnp.concatenate([gate_master, up_master], 1).astype(BF)
    hidden_out = down_master.astype(BF)
    order = (0, 2, 1, 3)
    weight_hidden = jnp.concatenate([move(hidden_in, hidden_from(i)) for i in order], 0)
    weight_down = jnp.concatenate([move(hidden_out, hidden_from(i)) for i in order], 1)

    def spread_tokens(block):
        kept = lax.dynamic_slice_in_dim(block, y * half_rows, half_rows, 0)
        given = lax.dynamic_slice_in_dim(block, (1 - y) * half_rows, half_rows, 0)
        mine = jnp.concatenate([kept, by_chip(given, 0, 1)], 1)
        rail = jnp.concatenate([mine] + [by_plane(mine, j) for j in (1, 2, 3)], 0)
        return jnp.concatenate([rail, by_col(rail, 1)], 1)

    over = (((0,), (0,)), ((), ()))
    across = (((1,), (1,)), ((), ()))
    grad_all = spread_tokens(cotangent)
    grad_hidden = lax.dot_general(grad_all, weight_down, across, preferred_element_type=F32)
    scale_two = lax.rsqrt(col_sum(jnp.sum(midway * midway, axis=1)) / D + EPSILON)
    normed_two = spread_tokens(rounded_norm(midway, scale_two, ffn_gain))
    gate_and_up = jnp.dot(normed_two, weight_hidden, preferred_element_type=F32)
    units = hidden_out.shape[0]
    gate, up = gate_and_up[:, :units], gate_and_up[:, units:]
    sigmoid = jax.nn.sigmoid(gate)
    hidden = (gate * sigmoid * up).astype(BF)
    grad_gate = (grad_hidden * up * sigmoid * (1.0 + gate * (1.0 - sigmoid))).astype(BF)
    grad_up = (grad_hidden * gate * sigmoid).astype(BF)
    grad_both = jnp.concatenate([grad_gate, grad_up], 1)

    half = D // 2
    theirs = lax.dot_general(
        grad_both, weight_hidden[half:], across, preferred_element_type=F32
    ).astype(BF)
    arrived = by_col(theirs, 1)
    mine = lax.dot_general(grad_both, weight_hidden[:half], across, preferred_element_type=F32)
    mine = mine + arrived.astype(F32)
    low = mine.astype(BF)
    mine = mine[:half_rows]
    for j in (1, 2, 3):
        mine = mine + by_plane(low[j * half_rows : (j + 1) * half_rows], j).astype(F32)
    part = half // 2
    crossed = by_chip(mine[:, part:].astype(BF), 0, 1).astype(F32)
    grad_normed_two = jnp.where(
        y == 0,
        jnp.concatenate([mine[:, :part], crossed], 0),
        jnp.concatenate([crossed, mine[:, :part]], 0),
    )

    def plane_total(partial, axis):
        size = D // COL
        total = None
        for place, i in enumerate(order):
            piece = lax.slice_in_dim(partial, place * size, (place + 1) * size, axis=axis)
            piece = move(piece, hidden_back(i)).astype(F32)
            total = piece if total is None else total + piece
        return total

    down_part = lax.dot_general(hidden, grad_all, over, preferred_element_type=F32).astype(BF)
    both_part = lax.dot_general(normed_two, grad_both, over, preferred_element_type=F32).astype(BF)
    grad_down_own = plane_total(down_part, 1)
    grad_both_own = plane_total(both_part, 0)

    grad_mid_norm, gain_two_part = norm_grads(grad_normed_two, midway, scale_two, ffn_gain)
    grad_midway = cotangent.astype(F32) + grad_mid_norm
    back_all = plane_gather(grad_midway.astype(BF))
    grad_attended = flip(
        lax.dot_general(back_all, weight_out, across, preferred_element_type=F32).astype(BF)
    )
    dq, dk, dv = attend_back(begin, q, k, v, grad_attended, lse)
    dkv = jnp.concatenate([dk, dv], 1)
    spill = move(
        dkv[:REACH].astype(BF), lambda e, s, b: (e - 1, s, b) if e > 0 else None
    )
    dkv = dkv[REACH:]
    start = group - REACH
    dkv = jnp.concatenate([dkv[:start], dkv[start:] + spill.astype(F32)], 0).astype(BF)
    grad_projected = flip(jnp.concatenate([dq, dkv], 1))

    in_part = lax.dot_general(normed_one, grad_projected, over, preferred_element_type=F32).astype(BF)
    out_part = lax.dot_general(own_attended, back_all, over, preferred_element_type=F32).astype(BF)

    def owners_total(partial, axis):
        size = D // COL
        parts = [
            lax.slice_in_dim(partial, i * size, (i + 1) * size, axis=axis) for i in range(COL)
        ]
        by_step = {0: parts[0], 2: by_col(parts[1], 2), 1: by_col(parts[2], 1), 3: by_col(parts[3], 3)}
        stack = jnp.stack([by_step[m] for m in range(COL)])
        total = pick(stack, d ^ c).astype(F32)
        for j in (1, 2, 3):
            total = total + by_plane(pick(stack, d ^ c ^ j), j).astype(F32)
        return total

    grad_in = owners_total(in_part, 0)
    grad_out = owners_total(out_part, 1)

    grad_normed_one = plane_scatter(grad_projected, weight_in, 1)
    grad_in_norm, gain_one_part = norm_grads(grad_normed_one, x, scale_one, attn_gain)
    grad_tokens = grad_midway + grad_in_norm
    gains = same_sum(jnp.stack([gain_one_part, gain_two_part]))
    return (
        grad_tokens,
        grad_in[:, :width],
        grad_in[:, width : 2 * width],
        grad_in[:, 2 * width :],
        grad_out,
        grad_both_own[:, :units],
        grad_both_own[:, units:],
        grad_down_own,
        gains[0],
        gains[1],
    )


def solution(mesh):
    placed = (
        P(("dp", "row"), "col"),
        P(("dp", "row"), "col"),
        P("col", ("row", "dp")),
        P("col", ("row", "dp")),
        P("col", ("row", "dp")),
        P(("row", "dp"), "col"),
        P("col", ("row", "dp")),
        P("col", ("row", "dp")),
        P(("row", "dp"), "col"),
        P("col"),
        P("col"),
        P(),
        P(),
    )
    small = tuple(mesh.shape[name] for name in AXES) == (DP, ROW, COL)
    return jax.shard_map(
        on_small_mesh if small else on_any_mesh,
        mesh=mesh,
        in_specs=placed,
        out_specs=(
            P(("dp", "row"), "col"),
            P("col", ("row", "dp")),
            P("col", ("row", "dp")),
            P("col", ("row", "dp")),
            P(("row", "dp"), "col"),
            P("col", ("row", "dp")),
            P("col", ("row", "dp")),
            P(("row", "dp"), "col"),
            P("col"),
            P("col"),
        ),
        check_vma=False,
    )
```

```python
import functools

import jax
import jax.numpy as jnp
from jax import lax
from jax.experimental import pallas as pl
from jax.experimental.pallas import tpu as pltpu
from jax.sharding import PartitionSpec as P

D = 2048
HEAD_DIM = 128


EPSILON = 1e-06
NEG_FILL = -1e30
AXES = ("dp", "row", "col")
DP, ROW, COL = 4, 2, 4
REACH = 768
BF = jnp.bfloat16
F32 = jnp.float32


def running_sum(lengths):
    count = lengths.shape[0]
    earlier = jnp.arange(count)[:, None] <= jnp.arange(count)[None, :]
    return jnp.sum(jnp.where(earlier, lengths[:, None], 0), axis=0)

def make_picker(wanted, carried, pieces):
    amount = pieces[0].shape[0]
    inside = (wanted >= 0) & (wanted < amount)
    chosen = jnp.clip(wanted, 0, amount - 1)
    return tuple(
        (
            jnp.where(inside[:, None], jnp.take(shard_rows, chosen, axis=0), current)
            for shard_rows, current in zip(pieces, carried)
        )
    )


def sequence_marks(permutation, lengths, first_slot, amount):
    source = lax.dynamic_slice_in_dim(permutation, first_slot, amount)
    seq_ends = running_sum(lengths)
    passed = seq_ends[None, :] <= source[:, None]
    member = jnp.sum(passed.astype(jnp.int32), axis=1)
    begins = jnp.max(jnp.where(passed, seq_ends[None, :], 0), axis=1)
    return (member, source - begins)


def col_total(values):
    return lax.psum(jnp.sum(values, axis=1), "col")


def row_gather(values):
    return lax.all_gather(values, "row", axis=0, tiled=True)


def col_gather(values):
    return lax.all_gather(values, "col", axis=0, tiled=True)


def key_gather(keys_here, values_here):
    return (
        lax.all_gather(keys_here, "col", axis=0, tiled=True),
        lax.all_gather(values_here, "col", axis=0, tiled=True),
    )


def multiply(row_block, weight, transpose_right):
    if transpose_right:
        return lax.dot_general(
            row_block, weight, (((1,), (1,)), ((), ())), preferred_element_type=jnp.float32
        )
    return jnp.dot(row_block, weight, preferred_element_type=jnp.float32)


def outer_sum(left_rows, right_rows):
    return lax.dot_general(
        left_rows, right_rows, (((0,), (0,)), ((), ())), preferred_element_type=jnp.float32
    )


def col_reduce(spread, weight, transpose_right):
    return lax.psum_scatter(
        multiply(spread, weight, transpose_right), "col", scatter_dimension=0, tiled=True
    )


def row_reduce(spread, weight, transpose_right):
    return lax.psum_scatter(
        multiply(spread, weight, transpose_right), "row", scatter_dimension=0, tiled=True
    )


def visible(query_member, query_position, member, position):
    same = query_member[:, None] == member[None, :]
    behind = position[None, :] <= query_position[:, None]
    return same & behind


def attend_scores(query_block, key_all, allowed):
    scores = jnp.einsum(
        "qhd,khd->hqk", query_block, key_all, preferred_element_type=jnp.float32
    ) * HEAD_DIM ** (-0.5)
    return jnp.where(allowed[None, :, :], scores, NEG_FILL)


def norm_back(grad_normed, inputs_f, scale_rows, gain):
    gain_part = jnp.sum(grad_normed * inputs_f * scale_rows[:, None], axis=0)
    scaled = grad_normed * gain[None, :]
    inner = col_total(scaled * inputs_f)
    grad_inputs = scale_rows[:, None] * scaled - inputs_f * (scale_rows**3 * inner / D)[:, None]
    return (grad_inputs, gain_part)


def on_any_mesh(
    tokens,
    cotangent,
    query_master,
    key_master,
    value_master,
    out_master,
    gate_master,
    up_master,
    down_master,
    attn_gain,
    ffn_gain,
    lengths,
    permutation,
):
    own_rows = tokens.shape[0]
    group_rows = own_rows * lax.axis_size("row")
    quarter = group_rows // lax.axis_size("col")
    device_slot = lax.axis_index(("dp", "row"))
    group_slot = lax.axis_index("dp")
    col_slot = lax.axis_index("col")
    own_sources = lax.dynamic_slice_in_dim(permutation, device_slot * own_rows, own_rows)
    own_tokens, own_cotangent = make_picker(
        own_sources,
        (jnp.zeros_like(tokens), jnp.zeros_like(cotangent)),
        (
            lax.all_gather(tokens, ("dp", "row"), axis=0, tiled=True),
            lax.all_gather(cotangent, ("dp", "row"), axis=0, tiled=True),
        ),
    )
    masters = tuple(
        (
            matrix.astype(jnp.bfloat16)
            for matrix in (
                query_master,
                key_master,
                value_master,
                out_master,
                gate_master,
                up_master,
                down_master,
            )
        )
    )
    query_weight, key_weight, value_weight, out_weight, gate_weight, up_weight, down_weight = (
        lax.all_gather(masters[0], "dp", axis=1, tiled=True),
        lax.all_gather(masters[1], "dp", axis=1, tiled=True),
        lax.all_gather(masters[2], "dp", axis=1, tiled=True),
        lax.all_gather(masters[3], "dp", axis=0, tiled=True),
        lax.all_gather(masters[4], "dp", axis=1, tiled=True),
        lax.all_gather(masters[5], "dp", axis=1, tiled=True),
        lax.all_gather(masters[6], "dp", axis=0, tiled=True),
    )
    attention_in = jnp.concatenate([query_weight, key_weight, value_weight], axis=1)
    feedforward_in = jnp.concatenate([gate_weight, up_weight], axis=1)
    width_row = query_weight.shape[1]
    heads_row = width_row // HEAD_DIM
    hidden_row = gate_weight.shape[1]
    member, position = sequence_marks(permutation, lengths, group_slot * group_rows, group_rows)
    query_member = lax.dynamic_slice_in_dim(member, col_slot * quarter, quarter)
    query_position = lax.dynamic_slice_in_dim(position, col_slot * quarter, quarter)
    block_rows = min(512, quarter)
    block_count = quarter // block_rows
    residual_in = own_tokens.astype(jnp.float32)
    scale_one = lax.rsqrt(col_total(residual_in * residual_in) / D + EPSILON)
    normed_one = (residual_in * scale_one[:, None] * attn_gain[None, :]).astype(jnp.bfloat16)
    spread_one = row_gather(normed_one)
    projected = col_reduce(spread_one, attention_in, False).astype(jnp.bfloat16)
    queries = projected[:, :width_row].reshape(quarter, heads_row, HEAD_DIM)
    keys_here = projected[:, width_row : 2 * width_row]
    values_here = projected[:, 2 * width_row :]
    key_flat, value_flat = key_gather(keys_here, values_here)
    key_all = key_flat.reshape(group_rows, heads_row, HEAD_DIM)
    value_all = value_flat.reshape(group_rows, heads_row, HEAD_DIM)

    def block_mask(first_row):
        return visible(
            lax.dynamic_slice_in_dim(query_member, first_row, block_rows),
            lax.dynamic_slice_in_dim(query_position, first_row, block_rows),
            member,
            position,
        )

    def forward_block(block_id):
        first_row = block_id * block_rows
        query_block = lax.dynamic_slice_in_dim(queries, first_row, block_rows, 0)
        scores = attend_scores(query_block, key_all, block_mask(first_row))
        highest = jnp.max(scores, axis=2, keepdims=True)
        totals = jnp.sum(jnp.exp(scores - highest), axis=2, keepdims=True)
        log_total = highest + jnp.log(totals)
        probability = jnp.exp(scores - log_total)
        output = jnp.einsum(
            "hqk,khd->qhd",
            probability.astype(jnp.bfloat16),
            value_all,
            preferred_element_type=jnp.float32,
        )
        return (output.astype(jnp.bfloat16).reshape(block_rows, width_row), log_total[:, :, 0])

    blocks_out, log_totals = lax.map(forward_block, jnp.arange(block_count, dtype=jnp.int32))
    attended = blocks_out.reshape(quarter, width_row)
    spread_attn = col_gather(attended)
    midway = residual_in + row_reduce(spread_attn, out_weight, False)
    scale_two = lax.rsqrt(col_total(midway * midway) / D + EPSILON)
    normed_two = (midway * scale_two[:, None] * ffn_gain[None, :]).astype(jnp.bfloat16)
    spread_two = row_gather(normed_two)
    gate_and_up = col_reduce(spread_two, feedforward_in, False)
    gate_value = gate_and_up[:, :hidden_row]
    up_value = gate_and_up[:, hidden_row:]
    sigmoid_gate = jax.nn.sigmoid(gate_value)
    hidden = (gate_value * sigmoid_gate * up_value).astype(jnp.bfloat16)
    grad_output = own_cotangent.astype(jnp.float32)
    spread_down = row_gather(own_cotangent)
    grad_hidden = col_reduce(spread_down, down_weight, True)
    spread_hidden = col_gather(hidden)
    grad_down = outer_sum(spread_hidden, spread_down)
    grad_gate_value = (
        grad_hidden * up_value * sigmoid_gate * (1.0 + gate_value * (1.0 - sigmoid_gate))
    ).astype(jnp.bfloat16)
    grad_up_value = (grad_hidden * gate_value * sigmoid_gate).astype(jnp.bfloat16)
    spread_gate_up = col_gather(jnp.concatenate([grad_gate_value, grad_up_value], axis=1))
    grad_normed_two = row_reduce(spread_gate_up, feedforward_in, True)
    spread_two = row_gather(normed_two)
    grad_feedforward = outer_sum(spread_two, spread_gate_up)
    grad_mid_norm, gain_two_part = norm_back(grad_normed_two, midway, scale_two, ffn_gain)
    grad_midway = grad_output + grad_mid_norm
    rounded_midway = grad_midway.astype(jnp.bfloat16)
    spread_back = row_gather(rounded_midway)
    grad_attended = col_reduce(spread_back, out_weight, True).astype(jnp.bfloat16)
    spread_attn = col_gather(attended)
    key_flat, value_flat = key_gather(keys_here, values_here)
    key_all = key_flat.reshape(group_rows, heads_row, HEAD_DIM)
    value_all = value_flat.reshape(group_rows, heads_row, HEAD_DIM)
    grad_out_local = outer_sum(spread_attn, spread_back)

    def backward_block(carried, block_id):
        first_row = block_id * block_rows
        query_block = lax.dynamic_slice_in_dim(queries, first_row, block_rows, 0)
        scores = attend_scores(query_block, key_all, block_mask(first_row))
        probability = jnp.exp(
            scores - lax.dynamic_index_in_dim(log_totals, block_id, 0, keepdims=False)[:, :, None]
        )
        weights_low = probability.astype(jnp.bfloat16)
        grad_block = lax.dynamic_slice_in_dim(grad_attended, first_row, block_rows, 0).reshape(
            block_rows, heads_row, HEAD_DIM
        )
        grad_soft = jnp.einsum(
            "qhd,khd->hqk", grad_block, value_all, preferred_element_type=jnp.float32
        )
        row_inner = jnp.sum(probability * grad_soft, axis=2, keepdims=True)
        grad_scores = (probability * (grad_soft - row_inner)).astype(jnp.bfloat16)
        grad_query_block = jnp.einsum(
            "hqk,khd->qhd", grad_scores, key_all, preferred_element_type=jnp.float32
        ) * HEAD_DIM ** (-0.5)
        grad_key_all = carried[0] + jnp.einsum(
            "hqk,qhd->khd", grad_scores, query_block, preferred_element_type=jnp.float32
        ) * HEAD_DIM ** (-0.5)
        grad_value_all = carried[1] + jnp.einsum(
            "hqk,qhd->khd", weights_low, grad_block, preferred_element_type=jnp.float32
        )
        return (
            (grad_key_all, grad_value_all),
            grad_query_block.astype(jnp.bfloat16).reshape(block_rows, width_row),
        )

    start_grads = jnp.zeros((group_rows, heads_row, HEAD_DIM), jnp.float32)
    key_value_grads, grad_queries = lax.scan(
        backward_block, (start_grads, start_grads), jnp.arange(block_count, dtype=jnp.int32)
    )
    grad_queries = grad_queries.reshape(quarter, width_row)
    grad_key_part = key_value_grads[0].reshape(group_rows, width_row)
    grad_value_part = key_value_grads[1].reshape(group_rows, width_row)
    grad_key_mine, grad_value_mine = (
        lax.psum_scatter(grad_key_part, "col", scatter_dimension=0, tiled=True),
        lax.psum_scatter(grad_value_part, "col", scatter_dimension=0, tiled=True),
    )
    spread_projected = col_gather(
        jnp.concatenate(
            [
                grad_queries,
                grad_key_mine.astype(jnp.bfloat16),
                grad_value_mine.astype(jnp.bfloat16),
            ],
            axis=1,
        )
    )
    grad_normed_one = row_reduce(spread_projected, attention_in, True)
    spread_one = row_gather(normed_one)
    grad_attention = outer_sum(spread_one, spread_projected)
    grad_in_norm, gain_one_part = norm_back(grad_normed_one, residual_in, scale_one, attn_gain)
    grad_own_tokens = grad_midway + grad_in_norm
    grad_attn_gain, grad_ffn_gain = lax.psum((gain_one_part, gain_two_part), ("dp", "row"))
    grad_query, grad_key, grad_value, grad_out, grad_gate, grad_up, grad_down_mine = (
        lax.psum_scatter(
            grad_attention[:, :width_row].astype(jnp.bfloat16),
            "dp",
            scatter_dimension=1,
            tiled=True,
        ).astype(jnp.float32),
        lax.psum_scatter(
            grad_attention[:, width_row : 2 * width_row].astype(jnp.bfloat16),
            "dp",
            scatter_dimension=1,
            tiled=True,
        ).astype(jnp.float32),
        lax.psum_scatter(
            grad_attention[:, 2 * width_row :].astype(jnp.bfloat16),
            "dp",
            scatter_dimension=1,
            tiled=True,
        ).astype(jnp.float32),
        lax.psum_scatter(
            grad_out_local.astype(jnp.bfloat16), "dp", scatter_dimension=0, tiled=True
        ).astype(jnp.float32),
        lax.psum_scatter(
            grad_feedforward[:, :hidden_row].astype(jnp.bfloat16),
            "dp",
            scatter_dimension=1,
            tiled=True,
        ).astype(jnp.float32),
        lax.psum_scatter(
            grad_feedforward[:, hidden_row:].astype(jnp.bfloat16),
            "dp",
            scatter_dimension=1,
            tiled=True,
        ).astype(jnp.float32),
        lax.psum_scatter(
            grad_down.astype(jnp.bfloat16), "dp", scatter_dimension=0, tiled=True
        ).astype(jnp.float32),
    )
    total_tokens = permutation.shape[0]
    inverse = (
        jnp.zeros((total_tokens,), jnp.int32)
        .at[permutation]
        .set(jnp.arange(total_tokens, dtype=jnp.int32))
    )
    wanted_slots = lax.dynamic_slice_in_dim(inverse, device_slot * own_rows, own_rows)
    (grad_tokens,) = make_picker(
        wanted_slots,
        (jnp.zeros_like(grad_own_tokens),),
        (
            (
                lax.all_gather(
                    grad_own_tokens.astype(jnp.bfloat16), ("dp", "row"), axis=0, tiled=True
                ),
            )[0].astype(jnp.float32),
        ),
    )
    return (
        grad_tokens,
        grad_query,
        grad_key,
        grad_value,
        grad_out,
        grad_gate,
        grad_up,
        grad_down_mine,
        grad_attn_gain,
        grad_ffn_gain,
    )


def move(array, to):
    pairs = []
    for d in range(DP):
        for r in range(ROW):
            for c in range(COL):
                target = to(d, r, c)
                if target is not None:
                    e, s, b = target
                    pairs.append(((d * ROW + r) * COL + c, (e * ROW + s) * COL + b))
    return lax.ppermute(array, AXES, pairs)


def by_col(array, step):
    return move(array, lambda d, r, c: (d, r, c ^ step))


def by_plane(array, step):
    return move(array, lambda d, r, c: (d ^ step, r, c))


def by_chip(array, over_x, over_y):
    return move(array, lambda d, r, c: (d, r ^ over_x, c ^ (2 * over_y)))


def col_sum(values):
    return values + by_col(values, 2) + by_col(values, 1) + by_col(values, 3)


def same_sum(values):
    for step in (1, 2):
        values = values + by_plane(values, step)
    return values + by_chip(values, 1, 0)


def plane_gather(block):
    beside = by_chip(block, 1, 0)
    across = by_chip(block, 0, 1)
    corner = by_chip(block, 1, 1)
    rail = jnp.concatenate(
        [jnp.concatenate([block, across], 1), jnp.concatenate([beside, corner], 1)], 0
    )
    return jnp.concatenate([rail, by_col(rail, 1)], 1)


def plane_scatter(left, weight, contract):
    rows = left.shape[0] // 2
    half = D // 2
    numbers = (((1,), (contract,)), ((), ()))
    kept, given = (weight[:, :half], weight[:, half:]) if contract == 0 else (weight[:half], weight[half:])
    theirs = lax.dot_general(left, given, numbers, preferred_element_type=F32).astype(BF)
    arrived = by_col(theirs, 1)
    mine = lax.dot_general(left, kept, numbers, preferred_element_type=F32)
    mine = mine + arrived.astype(F32)
    low = mine.astype(BF)
    part = half // 2
    return (
        mine[:rows, :part]
        + by_chip(low[rows:, :part], 1, 0).astype(F32)
        + by_chip(low[:rows, part:], 0, 1).astype(F32)
        + by_chip(low[rows:, part:], 1, 1).astype(F32)
    )


def hidden_from(step):
    def to(d, s, c):
        b = c ^ step
        return (d, s ^ (b & 1), b)

    return to


def hidden_back(step):
    def to(d, r, c):
        return (d, r ^ (c & 1), c ^ step)

    return to


def begins_of(lengths, first, amount):
    ends = running_sum(lengths)
    place = first + jnp.arange(amount, dtype=jnp.int32)
    passed = ends[None, :] <= place[:, None]
    return jnp.max(jnp.where(passed, ends[None, :], 0), axis=1)


def seen(begin_ref, block, rows, span):
    query = lax.broadcasted_iota(jnp.int32, (rows, span), 0)
    key = lax.broadcasted_iota(jnp.int32, (rows, span), 1)
    begin = begin_ref[:, 0:1] + (REACH - block * rows)
    return (key <= query + REACH) & (key >= begin)


def scores_of(query, key):
    return lax.dot_general(
        query, key, (((1,), (1,)), ((), ())), preferred_element_type=F32
    ) * HEAD_DIM ** (-0.5)


def attend_kernel(begin_ref, q_ref, k_ref, v_ref, o_ref, lse_ref):
    block = pl.program_id(1)
    rows = q_ref.shape[0]
    span = rows + REACH
    window = pl.ds(pl.multiple_of(block * rows, rows), span)
    scores = scores_of(q_ref[...], k_ref[window, :])
    scores = jnp.where(seen(begin_ref, block, rows, span), scores, NEG_FILL)
    highest = jnp.max(scores, axis=1, keepdims=True)
    expo = jnp.exp(scores - highest)
    total = jnp.sum(expo, axis=1, keepdims=True)
    probability = (expo * (1.0 / total)).astype(BF)
    o_ref[...] = jnp.dot(probability, v_ref[window, :], preferred_element_type=F32).astype(BF)
    lse_ref[...] = jnp.broadcast_to(highest + jnp.log(total), lse_ref.shape)


def attend_back_kernel(
    begin_ref, q_ref, k_ref, v_ref, do_ref, lse_ref, dq_ref, dk_ref, dv_ref
):
    block = pl.program_id(1)
    rows = q_ref.shape[0]
    span = rows + REACH
    window = pl.ds(pl.multiple_of(block * rows, rows), span)

    @pl.when(block == 0)
    def _():
        dk_ref[...] = jnp.zeros_like(dk_ref)
        dv_ref[...] = jnp.zeros_like(dv_ref)

    query, key = q_ref[...], k_ref[window, :]
    grad = do_ref[...]
    scores = scores_of(query, key)
    allowed = seen(begin_ref, block, rows, span)
    probability = jnp.where(allowed, jnp.exp(jnp.where(allowed, scores - lse_ref[:, 0:1], 0.0)), 0.0)
    grad_soft = lax.dot_general(
        grad, v_ref[window, :], (((1,), (1,)), ((), ())), preferred_element_type=F32
    )
    inner = jnp.sum(probability * grad_soft, axis=1, keepdims=True)
    grad_scores = (probability * (grad_soft - inner)).astype(BF)
    scale = HEAD_DIM ** (-0.5)
    dq_ref[...] = (jnp.dot(grad_scores, key, preferred_element_type=F32) * scale).astype(BF)
    over = (((0,), (0,)), ((), ()))
    dk_ref[window, :] += lax.dot_general(grad_scores, query, over, preferred_element_type=F32) * scale
    dv_ref[window, :] += lax.dot_general(
        probability.astype(BF), grad, over, preferred_element_type=F32
    )


QROWS = 256


def attention_specs(rows, width):
    by_block = pl.BlockSpec((QROWS, HEAD_DIM), lambda h, i: (i, h))
    whole = pl.BlockSpec((rows + REACH, HEAD_DIM), lambda h, i: (0, h))
    begin = pl.BlockSpec((QROWS, 1), lambda h, i: (i, 0))
    grid = (width // HEAD_DIM, rows // QROWS)
    params = pltpu.CompilerParams(vmem_limit_bytes=40 << 20)
    return grid, by_block, whole, begin, params


def attend(begin, q, k, v):
    rows, width = q.shape
    grid, by_block, whole, begin_spec, params = attention_specs(rows, width)
    area = grid[0] * rows * (QROWS + REACH)
    return pl.pallas_call(
        attend_kernel,
        grid=grid,
        in_specs=[begin_spec, by_block, whole, whole],
        out_specs=[by_block, by_block],
        out_shape=[
            jax.ShapeDtypeStruct((rows, width), BF),
            jax.ShapeDtypeStruct((rows, width), F32),
        ],
        compiler_params=params,
        cost_estimate=pl.CostEstimate(
            flops=4 * area * HEAD_DIM, bytes_accessed=8 * rows * width, transcendentals=area
        ),
    )(begin, q, k, v)


def attend_back(begin, q, k, v, grad, lse):
    rows, width = q.shape
    grid, by_block, whole, begin_spec, params = attention_specs(rows, width)
    area = grid[0] * rows * (QROWS + REACH)
    return pl.pallas_call(
        attend_back_kernel,
        grid=grid,
        in_specs=[begin_spec, by_block, whole, whole, by_block, by_block],
        out_specs=[by_block, whole, whole],
        out_shape=[
            jax.ShapeDtypeStruct((rows, width), BF),
            jax.ShapeDtypeStruct((rows + REACH, width), F32),
            jax.ShapeDtypeStruct((rows + REACH, width), F32),
        ],
        compiler_params=params,
        cost_estimate=pl.CostEstimate(
            flops=10 * area * HEAD_DIM, bytes_accessed=24 * rows * width, transcendentals=area
        ),
    )(begin, q, k, v, grad, lse)


MESH = pl.DeviceIdType.MESH
PLACE = {0: 0, 2: 1, 1: 2, 3: 3}
TILE = 256


class Post:
    def __init__(self, send_sem, recv_sem):
        self.send_sem, self.recv_sem, self.used = send_sem, recv_sem, 0

    def ready(self, src, dst, target, slot=None):
        if slot is None:
            slot = self.used
            self.used += 1
        return pltpu.make_async_remote_copy(
            src_ref=src,
            dst_ref=dst,
            send_sem=self.send_sem.at[slot],
            recv_sem=self.recv_sem.at[slot],
            device_id=target,
            device_id_type=MESH,
        )

    def take(self, count):
        first = self.used
        self.used += count
        return first

    def send(self, src, dst, target):
        copy = self.ready(src, dst, target)
        copy.start()
        return copy


def greet(peers):
    barrier = pltpu.get_barrier_semaphore()
    for peer in peers:
        pl.semaphore_signal(barrier, inc=1, device_id=peer, device_id_type=MESH)
    pl.semaphore_wait(barrier, len(peers))


def as_row(column):
    return jnp.transpose(jnp.broadcast_to(column, (column.shape[0], 128)))[0:8]


def as_column(row):
    return jnp.transpose(row)[:, 0:1]


def forward_kernel(
    x_ref, gain_one_ref, gain_two_ref, begin_ref, own_in, own_out, own_hidden, own_down, own_grad,
    normed_ref, weight_in, weight_out, q_ref, kv_ref, att_ref, lse_ref, mid_ref, scale_ref, n2_ref,
    hidden_all, down_all, grad_all,
    zin, zout, sums, wide, given, arrived, low, landed, x32,
    send_sem, recv_sem, local_sem,
):
    d, r, c = (lax.axis_index(name) for name in AXES)
    y, core = c // 2, lax.rem(c, 2)
    rows = x_ref.shape[0]
    fc = x_ref.shape[1]
    group = 2 * rows
    width = q_ref.shape[1]
    half = 2 * fc
    post = Post(send_sem, recv_sem)
    in_plane = [(d, r ^ a, c ^ b) for a in (0, 1) for b in range(COL) if (a, b) != (0, 0)]
    greet([(d ^ j, r, c) for j in (1, 2, 3)] + in_plane)

    first = post.take(DP)

    def line(p, target_plane):
        return post.ready(zin.at[p], zin.at[p], (target_plane, r, c), first + p)

    first_down = post.take(DP)

    def line_down(p, target_plane):
        return pltpu.make_async_remote_copy(
            src_ref=zin.at[p], dst_ref=zin.at[p],
            send_sem=send_sem.at[first_down + p], recv_sem=recv_sem.at[first + p],
            device_id=(target_plane, r, c), device_id_type=MESH,
        )

    mine = pltpu.make_async_copy(own_in, zin.at[d], local_sem.at[0])
    mine.start()
    mine.wait()

    @pl.when(d < DP - 1)
    def _():
        line(d, d + 1).start()

    @pl.when(d > 0)
    def _():
        line_down(d, d - 1).start()

    first_cols = post.take(DP)
    first_keep = 1

    def to_column(p):
        return pltpu.make_async_remote_copy(
            src_ref=zin.at[p],
            dst_ref=weight_in.at[pl.ds(pl.multiple_of(place_of(p ^ c) * fc, fc), fc), :],
            send_sem=send_sem.at[first_cols + p],
            recv_sem=recv_sem.at[first_cols + (p ^ c)],
            device_id=(d, r, p), device_id_type=MESH,
        )

    def place_of(m):
        return lax.rem(m, 2) * 2 + m // 2

    keep = pltpu.make_async_copy(zin.at[c], weight_in.at[pl.ds(0, fc), :], local_sem.at[first_keep])

    def pass_on(p):
        @pl.when(p == c)
        def _():
            keep.start()

        @pl.when(p != c)
        def _():
            to_column(p).start()

    pass_on(d)

    def fill_x(t, total):
        part = pl.ds(pl.multiple_of(t * 128, 128), 128)
        value = x_ref[part, :].astype(F32)
        x32[part, :] = value
        sums[0, :, part] = as_row(jnp.sum(value * value, axis=1, keepdims=True))
        return total

    lax.fori_loop(0, rows // 128, fill_x, 0)
    small = [post.send(sums.at[0], sums.at[m], (d, r, c ^ m)) for m in (1, 2, 3)]
    half_rows = rows // 2
    grad_cross = post.send(
        own_grad.at[pl.ds(pl.multiple_of((1 - y) * half_rows, half_rows), half_rows), :],
        grad_all.at[pl.ds(0, half_rows), pl.ds(fc, fc)],
        (d, r, c ^ 2),
    )
    grad_keep = pltpu.make_async_copy(
        own_grad.at[pl.ds(pl.multiple_of(y * half_rows, half_rows), half_rows), :],
        grad_all.at[pl.ds(0, half_rows), pl.ds(0, fc)],
        local_sem.at[2],
    )
    grad_keep.start()
    for copy in small:
        copy.wait_recv()

    def norm_one(t, total):
        part = pl.ds(pl.multiple_of(t * 128, 128), 128)
        square = sums[0, :, part] + sums[2, :, part] + sums[1, :, part] + sums[3, :, part]
        scale = lax.rsqrt(as_column(square) / D + EPSILON)
        normed_ref[part, 0:fc] = (x32[part, :] * scale * gain_one_ref[...]).astype(BF)
        return total

    lax.fori_loop(0, rows // 128, norm_one, 0)
    own_rows, other_rows = pl.ds(0, rows), pl.ds(rows, rows)

    def columns(place):
        return pl.ds(place * fc, fc)

    own_block = normed_ref.at[own_rows, columns(0)]
    beside = post.send(own_block, normed_ref.at[other_rows, columns(0)], (d, r ^ 1, c))
    beyond = post.send(own_block, normed_ref.at[own_rows, columns(1)], (d, r, c ^ 2))
    corner = post.send(own_block, normed_ref.at[other_rows, columns(1)], (d, r ^ 1, c ^ 2))
    sibling = (d, r, c ^ 1)
    shared = [post.send(own_block, normed_ref.at[own_rows, columns(2)], sibling)]

    def line_step(s):
        for p, valid, onward, forward in (
            (d - s, d - s >= 0, d < DP - 1, lambda p: line(p, d + 1)),
            (d + s, d + s < DP, d > 0, lambda p: line_down(p, d - 1)),
        ):
            @pl.when(valid)
            def _(p=p, onward=onward, forward=forward):
                line(p, d).wait_recv()

                @pl.when(onward)
                def _():
                    forward(p).start()

                pass_on(p)

    line_step(1)
    for copy, where, place in ((beside, other_rows, 0), (beyond, own_rows, 1), (corner, other_rows, 1)):
        copy.wait_recv()
        shared.append(
            post.send(normed_ref.at[where, columns(place)], normed_ref.at[where, columns(place + 2)], sibling)
        )

    bulk = []
    first_hidden = post.take(8)
    for i in (0, 2, 1, 3):
        b = c ^ i
        target = (d, r ^ lax.rem(b, 2), b)
        place = PLACE[i]
        for kind, (src, dst) in enumerate((
            (own_down, down_all.at[:, columns(place)]),
            (own_hidden, hidden_all.at[pl.ds(place * fc, fc), :]),
        )):
            bulk.append((i, kind, post.ready(src, dst, target, first_hidden + 2 * place + kind),
                         pltpu.make_async_copy(src, dst, local_sem.at[3 + kind])))
    for i, kind, copy, local in bulk:
        if i == 0:
            @pl.when(core == 0)
            def _(local=local):
                local.start()

            @pl.when(core == 1)
            def _(copy=copy):
                copy.start()
        else:
            copy.start()

    line_step(2)
    line_step(3)
    outs = [
        post.send(own_out, zout.at[j], (d ^ j, r, c)) for j in (1, 2, 3)
    ]
    mine = pltpu.make_async_copy(own_out, zout.at[0], local_sem.at[5])
    mine.start()
    mine.wait()

    for copy in shared:
        copy.wait_recv()
    keep.wait()
    for m in (1, 2, 3):
        pltpu.make_async_remote_copy(
            src_ref=zin.at[0], dst_ref=weight_in.at[pl.ds(0, fc), :],
            send_sem=send_sem.at[first_cols], recv_sem=recv_sem.at[first_cols + m],
            device_id=(d, r, c), device_id_type=MESH,
        ).wait_recv()

    def turned(t):
        return lax.rem(t + 2 * r, group // TILE)

    def project_kv(t, total):
        part = pl.ds(pl.multiple_of(t * TILE, TILE), TILE)
        to = pl.ds(pl.multiple_of(REACH + turned(t) * TILE, TILE), TILE)
        kv_ref[to, :] = jnp.dot(
            normed_ref[part, :], weight_in[:, width:], preferred_element_type=F32
        ).astype(BF)
        return total

    lax.fori_loop(0, group // TILE, project_kv, 0)
    halo = post.ready(kv_ref.at[pl.ds(group, REACH), :], kv_ref.at[pl.ds(0, REACH), :], (lax.rem(d + 1, DP), r, c))

    @pl.when(d < DP - 1)
    def _():
        halo.start()

    def project_q(t, total):
        part = pl.ds(pl.multiple_of(t * TILE, TILE), TILE)
        to = pl.ds(pl.multiple_of(turned(t) * TILE, TILE), TILE)
        q_ref[to, :] = jnp.dot(
            normed_ref[part, :], weight_in[:, :width], preferred_element_type=F32
        ).astype(BF)
        return total

    lax.fori_loop(0, group // TILE, project_q, 0)

    for copy in outs:
        copy.wait_recv()
    out_cols = [
        post.send(zout.at[d ^ c ^ m], weight_out.at[:, columns(PLACE[m])], (d, r, c ^ m)) for m in (1, 2, 3)
    ]
    out_keep = pltpu.make_async_copy(zout.at[d ^ c], weight_out.at[:, columns(0)], local_sem.at[6])
    out_keep.start()
    grad_cross.wait_recv()
    grad_keep.wait()
    grads = [
        post.send(
            grad_all.at[pl.ds(0, half_rows), pl.ds(0, half)],
            grad_all.at[pl.ds(j * half_rows, half_rows), pl.ds(0, half)],
            (d ^ j, r, c),
        )
        for j in (1, 2, 3)
    ]
    grads_shared = [
        post.send(
            grad_all.at[pl.ds(0, half_rows), pl.ds(0, half)],
            grad_all.at[pl.ds(0, half_rows), pl.ds(half, half)],
            sibling,
        )
    ]

    @pl.when(d == 0)
    def _():
        kv_ref[pl.ds(0, REACH), :] = jnp.zeros((REACH, 2 * width), BF)

    @pl.when(d > 0)
    def _():
        halo.wait_recv()

    span = TILE + REACH
    for h in range(width // HEAD_DIM):
        lanes = pl.ds(h * HEAD_DIM, HEAD_DIM)
        value_lanes = pl.ds(width + h * HEAD_DIM, HEAD_DIM)

        def one(t, total, lanes=lanes, value_lanes=value_lanes):
            part = pl.ds(pl.multiple_of(t * TILE, TILE), TILE)
            to = pl.ds(pl.multiple_of(turned(t) * TILE, TILE), TILE)
            window = pl.ds(pl.multiple_of(t * TILE, TILE), span)
            scores = scores_of(q_ref[part, lanes], kv_ref[window, lanes])
            query = lax.broadcasted_iota(jnp.int32, (TILE, span), 0)
            key = lax.broadcasted_iota(jnp.int32, (TILE, span), 1)
            begin = begin_ref[part, 0:1] + (REACH - t * TILE)
            allowed = (key <= query + REACH) & (key >= begin)
            scores = jnp.where(allowed, scores, NEG_FILL)
            highest = jnp.max(scores, axis=1, keepdims=True)
            expo = jnp.exp(scores - highest)
            total_e = jnp.sum(expo, axis=1, keepdims=True)
            probability = (expo * (1.0 / total_e)).astype(BF)
            att_ref[to, lanes] = jnp.dot(
                probability, kv_ref[window, value_lanes], preferred_element_type=F32
            ).astype(BF)
            lse_ref[part, lanes] = jnp.broadcast_to(highest + jnp.log(total_e), (TILE, HEAD_DIM))
            return total

        lax.fori_loop(0, group // TILE, one, 0)

    for copy in out_cols:
        copy.wait_recv()
    out_keep.wait()

    def out_given(t, total):
        part = pl.ds(pl.multiple_of(t * TILE, TILE), TILE)
        given[part, :] = jnp.dot(
            att_ref[part, :], weight_out[:, half:], preferred_element_type=F32
        ).astype(BF)
        return total

    lax.fori_loop(0, group // TILE, out_given, 0)
    to_sibling = post.send(given, arrived, sibling)

    def out_kept(t, total):
        part = pl.ds(pl.multiple_of(t * TILE, TILE), TILE)
        wide[part, :] = jnp.dot(att_ref[part, :], weight_out[:, :half], preferred_element_type=F32)
        return total

    lax.fori_loop(0, group // TILE, out_kept, 0)
    to_sibling.wait_recv()

    def add_low(t, total):
        part = pl.ds(pl.multiple_of(t * 128, 128), 128)
        value = wide[part, :] + arrived[part, :].astype(F32)
        wide[part, :] = value
        low[part, :] = value.astype(BF)
        return total

    lax.fori_loop(0, group // 128, add_low, 0)
    pieces = [
        post.send(low.at[other_rows, columns(1)], landed.at[2], (d, r ^ 1, c ^ 2)),
        post.send(low.at[other_rows, columns(0)], landed.at[0], (d, r ^ 1, c)),
        post.send(low.at[own_rows, columns(1)], landed.at[1], (d, r, c ^ 2)),
    ]
    for copy in pieces:
        copy.wait_recv()

    def middle(t, total):
        part = pl.ds(pl.multiple_of(t * 128, 128), 128)
        value = (
            x32[part, :] + wide[part, 0:fc] + landed[0, part, :].astype(F32)
            + landed[1, part, :].astype(F32) + landed[2, part, :].astype(F32)
        )
        mid_ref[part, :] = value
        sums[4, :, part] = as_row(jnp.sum(value * value, axis=1, keepdims=True))
        return total

    lax.fori_loop(0, rows // 128, middle, 0)
    again = [post.send(sums.at[4], sums.at[4 + m], (d, r, c ^ m)) for m in (1, 2, 3)]
    for copy in again:
        copy.wait_recv()

    def norm_two(t, total):
        part = pl.ds(pl.multiple_of(t * 128, 128), 128)
        square = sums[4, :, part] + sums[6, :, part] + sums[5, :, part] + sums[7, :, part]
        scale = lax.rsqrt(as_column(square) / D + EPSILON)
        scale_ref[part, :] = scale
        n2_ref[part, :] = (mid_ref[part, :] * scale * gain_two_ref[...]).astype(BF)
        return total

    lax.fori_loop(0, rows // 128, norm_two, 0)

    for j, copy in zip((1, 2, 3), grads):
        copy.wait_recv()
        there = pl.ds(j * half_rows, half_rows)
        grads_shared.append(
            post.send(grad_all.at[there, pl.ds(0, half)], grad_all.at[there, pl.ds(half, half)], sibling)
        )
    for copy in grads_shared:
        copy.wait_recv()
    for i, kind, copy, local in bulk:
        if i == 0:
            @pl.when(core == 0)
            def _(local=local):
                local.wait()

            @pl.when(core == 1)
            def _(copy=copy):
                copy.wait()
        else:
            copy.wait()

    for copy in (
        small + [grad_cross, beside, beyond, corner] + shared + outs + out_cols + grads + grads_shared
        + [to_sibling] + pieces + again
    ):
        copy.wait_send()

    @pl.when(d < DP - 1)
    def _():
        halo.wait_send()

    for p in range(DP):
        @pl.when((d < DP - 1) & (p <= d))
        def _(p=p):
            line(p, d).wait_send()

        @pl.when((d > 0) & (p >= d))
        def _(p=p):
            line_down(p, d).wait_send()

        @pl.when(c != p)
        def _(p=p):
            to_column(p).wait_send()


SENDS = 64


def forward(x, gain_one, gain_two, begin, own_in, own_out, own_hidden, own_down, own_grad):
    rows, fc = x.shape
    group = 2 * rows
    width = own_out.shape[0]
    units = own_down.shape[0]
    vmem = pl.BlockSpec(memory_space=pltpu.VMEM)
    hbm = pl.BlockSpec(memory_space=pl.ANY)

    def like(shape, dtype=BF):
        return jax.ShapeDtypeStruct(shape, dtype)

    return pl.pallas_call(
        forward_kernel,
        in_specs=[vmem] * 4 + [hbm] * 5,
        out_specs=[vmem] * 10 + [hbm] * 3,
        out_shape=[
            like((group, D)),
            like((D, 3 * width)),
            like((width, D)),
            like((group, width)),
            like((REACH + group, 2 * width)),
            like((group, width)),
            like((group, width), F32),
            like((rows, fc), F32),
            like((rows, 1), F32),
            like((rows, fc)),
            like((D, 2 * units)),
            like((units, D)),
            like((group, D)),
        ],
        scratch_shapes=[
            pltpu.VMEM((DP, fc, 3 * width), BF),
            pltpu.VMEM((DP, width, fc), BF),
            pltpu.VMEM((8, 8, rows), F32),
            pltpu.VMEM((group, 2 * fc), F32),
            pltpu.VMEM((group, 2 * fc), BF),
            pltpu.VMEM((group, 2 * fc), BF),
            pltpu.VMEM((group, 2 * fc), BF),
            pltpu.VMEM((3, rows, fc), BF),
            pltpu.VMEM((rows, fc), F32),
            pltpu.SemaphoreType.DMA((SENDS,)),
            pltpu.SemaphoreType.DMA((SENDS,)),
            pltpu.SemaphoreType.DMA((8,)),
        ],
        compiler_params=pltpu.CompilerParams(
            collective_id=1, has_side_effects=True, vmem_limit_bytes=56 << 20
        ),
        cost_estimate=pl.CostEstimate(
            flops=6 * group * D * width, bytes_accessed=64 << 20, transcendentals=0
        ),
    )(x, gain_one, gain_two, begin, own_in, own_out, own_hidden, own_down, own_grad)


def rounded_norm(values, scale, gain):
    return (values * scale[:, None] * gain[None, :]).astype(BF)


def norm_grads(grad_normed, inputs_f, scale_rows, gain):
    gain_part = jnp.sum(grad_normed * inputs_f * scale_rows[:, None], axis=0)
    scaled = grad_normed * gain[None, :]
    inner = col_sum(jnp.sum(scaled * inputs_f, axis=1))
    grad_inputs = scale_rows[:, None] * scaled - inputs_f * (scale_rows**3 * inner / D)[:, None]
    return grad_inputs, gain_part


def on_small_mesh(
    tokens,
    cotangent,
    query_master,
    key_master,
    value_master,
    out_master,
    gate_master,
    up_master,
    down_master,
    attn_gain,
    ffn_gain,
    lengths,
    permutation,
):
    del permutation
    d, r, c = (lax.axis_index(name) for name in AXES)
    rows = tokens.shape[0]
    group = rows * ROW
    half_rows = rows // 2
    width = query_master.shape[1]
    y = c // 2

    def pick(stack, index):
        return lax.dynamic_index_in_dim(stack, index, 0, keepdims=False)

    def flip(array):
        swapped = jnp.concatenate([array[rows:], array[:rows]], 0)
        return jnp.where(r == 0, array, swapped)

    x = tokens.astype(F32)
    begin = (begins_of(lengths, d * group, group) - d * group)[:, None]
    block_in = jnp.concatenate([query_master, key_master, value_master], 1).astype(BF)
    hidden_in = jnp.concatenate([gate_master, up_master], 1).astype(BF)
    hidden_out = down_master.astype(BF)
    (
        normed_one, weight_in, weight_out, q, key_value, own_attended, lse, midway, scale_two,
        n2, weight_hidden, weight_down, grad_all,
    ) = forward(
        tokens, attn_gain[None, :], ffn_gain[None, :], begin, block_in, out_master.astype(BF),
        hidden_in, hidden_out, cotangent,
    )
    scale_two = scale_two[:, 0]
    scale_one = lax.rsqrt(col_sum(jnp.sum(x * x, axis=1)) / D + EPSILON)
    k, v = key_value[:, :width], key_value[:, width:]
    order = (0, 2, 1, 3)

    def spread_tokens(block):
        kept = lax.dynamic_slice_in_dim(block, y * half_rows, half_rows, 0)
        given = lax.dynamic_slice_in_dim(block, (1 - y) * half_rows, half_rows, 0)
        mine = jnp.concatenate([kept, by_chip(given, 0, 1)], 1)
        rail = jnp.concatenate([mine] + [by_plane(mine, j) for j in (1, 2, 3)], 0)
        return jnp.concatenate([rail, by_col(rail, 1)], 1)

    over = (((0,), (0,)), ((), ()))
    across = (((1,), (1,)), ((), ()))
    grad_hidden = lax.dot_general(grad_all, weight_down, across, preferred_element_type=F32)
    normed_two = spread_tokens(n2)
    gate_and_up = jnp.dot(normed_two, weight_hidden, preferred_element_type=F32)
    units = hidden_out.shape[0]
    gate, up = gate_and_up[:, :units], gate_and_up[:, units:]
    sigmoid = jax.nn.sigmoid(gate)
    hidden = (gate * sigmoid * up).astype(BF)
    grad_gate = (grad_hidden * up * sigmoid * (1.0 + gate * (1.0 - sigmoid))).astype(BF)
    grad_up = (grad_hidden * gate * sigmoid).astype(BF)
    grad_both = jnp.concatenate([grad_gate, grad_up], 1)

    half = D // 2
    theirs = lax.dot_general(
        grad_both, weight_hidden[half:], across, preferred_element_type=F32
    ).astype(BF)
    arrived = by_col(theirs, 1)
    mine = lax.dot_general(grad_both, weight_hidden[:half], across, preferred_element_type=F32)
    mine = mine + arrived.astype(F32)
    low = mine.astype(BF)
    mine = mine[:half_rows]
    for j in (1, 2, 3):
        mine = mine + by_plane(low[j * half_rows : (j + 1) * half_rows], j).astype(F32)
    part = half // 2
    crossed = by_chip(mine[:, part:].astype(BF), 0, 1).astype(F32)
    grad_normed_two = jnp.where(
        y == 0,
        jnp.concatenate([mine[:, :part], crossed], 0),
        jnp.concatenate([crossed, mine[:, :part]], 0),
    )

    def plane_total(partial, axis):
        size = D // COL
        total = None
        for place, i in enumerate(order):
            piece = lax.slice_in_dim(partial, place * size, (place + 1) * size, axis=axis)
            piece = move(piece, hidden_back(i)).astype(F32)
            total = piece if total is None else total + piece
        return total

    down_part = lax.dot_general(hidden, grad_all, over, preferred_element_type=F32).astype(BF)
    both_part = lax.dot_general(normed_two, grad_both, over, preferred_element_type=F32).astype(BF)
    grad_down_own = plane_total(down_part, 1)
    grad_both_own = plane_total(both_part, 0)

    grad_mid_norm, gain_two_part = norm_grads(grad_normed_two, midway, scale_two, ffn_gain)
    grad_midway = cotangent.astype(F32) + grad_mid_norm
    back_all = plane_gather(grad_midway.astype(BF))
    grad_attended = flip(
        lax.dot_general(back_all, weight_out, across, preferred_element_type=F32).astype(BF)
    )
    dq, dk, dv = attend_back(begin, q, k, v, grad_attended, lse)
    dkv = jnp.concatenate([dk, dv], 1)
    spill = move(
        dkv[:REACH].astype(BF), lambda e, s, b: (e - 1, s, b) if e > 0 else None
    )
    dkv = dkv[REACH:]
    start = group - REACH
    dkv = jnp.concatenate([dkv[:start], dkv[start:] + spill.astype(F32)], 0).astype(BF)
    grad_projected = flip(jnp.concatenate([dq, dkv], 1))

    in_part = lax.dot_general(normed_one, grad_projected, over, preferred_element_type=F32).astype(BF)
    out_part = lax.dot_general(own_attended, back_all, over, preferred_element_type=F32).astype(BF)

    def owners_total(partial, axis):
        size = D // COL
        parts = [
            lax.slice_in_dim(partial, i * size, (i + 1) * size, axis=axis) for i in range(COL)
        ]
        by_step = {0: parts[0], 2: by_col(parts[1], 2), 1: by_col(parts[2], 1), 3: by_col(parts[3], 3)}
        stack = jnp.stack([by_step[m] for m in range(COL)])
        total = pick(stack, d ^ c).astype(F32)
        for j in (1, 2, 3):
            total = total + by_plane(pick(stack, d ^ c ^ j), j).astype(F32)
        return total

    grad_in = owners_total(in_part, 0)
    grad_out = owners_total(out_part, 1)

    grad_normed_one = plane_scatter(grad_projected, weight_in, 1)
    grad_in_norm, gain_one_part = norm_grads(grad_normed_one, x, scale_one, attn_gain)
    grad_tokens = grad_midway + grad_in_norm
    gains = same_sum(jnp.stack([gain_one_part, gain_two_part]))
    return (
        grad_tokens,
        grad_in[:, :width],
        grad_in[:, width : 2 * width],
        grad_in[:, 2 * width :],
        grad_out,
        grad_both_own[:, :units],
        grad_both_own[:, units:],
        grad_down_own,
        gains[0],
        gains[1],
    )


def solution(mesh):
    placed = (
        P(("dp", "row"), "col"),
        P(("dp", "row"), "col"),
        P("col", ("row", "dp")),
        P("col", ("row", "dp")),
        P("col", ("row", "dp")),
        P(("row", "dp"), "col"),
        P("col", ("row", "dp")),
        P("col", ("row", "dp")),
        P(("row", "dp"), "col"),
        P("col"),
        P("col"),
        P(),
        P(),
    )
    small = tuple(mesh.shape[name] for name in AXES) == (DP, ROW, COL)
    return jax.shard_map(
        on_small_mesh if small else on_any_mesh,
        mesh=mesh,
        in_specs=placed,
        out_specs=(
            P(("dp", "row"), "col"),
            P("col", ("row", "dp")),
            P("col", ("row", "dp")),
            P("col", ("row", "dp")),
            P(("row", "dp"), "col"),
            P("col", ("row", "dp")),
            P("col", ("row", "dp")),
            P(("row", "dp"), "col"),
            P("col"),
            P("col"),
        ),
        check_vma=False,
    )
```

```python
import functools

import jax
import jax.numpy as jnp
from jax import lax
from jax.experimental import pallas as pl
from jax.experimental.pallas import tpu as pltpu
from jax.sharding import PartitionSpec as P

D = 2048
HEAD_DIM = 128


EPSILON = 1e-06
NEG_FILL = -1e30
AXES = ("dp", "row", "col")
DP, ROW, COL = 4, 2, 4
REACH = 768
BF = jnp.bfloat16
F32 = jnp.float32


def running_sum(lengths):
    count = lengths.shape[0]
    earlier = jnp.arange(count)[:, None] <= jnp.arange(count)[None, :]
    return jnp.sum(jnp.where(earlier, lengths[:, None], 0), axis=0)

def make_picker(wanted, carried, pieces):
    amount = pieces[0].shape[0]
    inside = (wanted >= 0) & (wanted < amount)
    chosen = jnp.clip(wanted, 0, amount - 1)
    return tuple(
        (
            jnp.where(inside[:, None], jnp.take(shard_rows, chosen, axis=0), current)
            for shard_rows, current in zip(pieces, carried)
        )
    )


def sequence_marks(permutation, lengths, first_slot, amount):
    source = lax.dynamic_slice_in_dim(permutation, first_slot, amount)
    seq_ends = running_sum(lengths)
    passed = seq_ends[None, :] <= source[:, None]
    member = jnp.sum(passed.astype(jnp.int32), axis=1)
    begins = jnp.max(jnp.where(passed, seq_ends[None, :], 0), axis=1)
    return (member, source - begins)


def col_total(values):
    return lax.psum(jnp.sum(values, axis=1), "col")


def row_gather(values):
    return lax.all_gather(values, "row", axis=0, tiled=True)


def col_gather(values):
    return lax.all_gather(values, "col", axis=0, tiled=True)


def key_gather(keys_here, values_here):
    return (
        lax.all_gather(keys_here, "col", axis=0, tiled=True),
        lax.all_gather(values_here, "col", axis=0, tiled=True),
    )


def multiply(row_block, weight, transpose_right):
    if transpose_right:
        return lax.dot_general(
            row_block, weight, (((1,), (1,)), ((), ())), preferred_element_type=jnp.float32
        )
    return jnp.dot(row_block, weight, preferred_element_type=jnp.float32)


def outer_sum(left_rows, right_rows):
    return lax.dot_general(
        left_rows, right_rows, (((0,), (0,)), ((), ())), preferred_element_type=jnp.float32
    )


def col_reduce(spread, weight, transpose_right):
    return lax.psum_scatter(
        multiply(spread, weight, transpose_right), "col", scatter_dimension=0, tiled=True
    )


def row_reduce(spread, weight, transpose_right):
    return lax.psum_scatter(
        multiply(spread, weight, transpose_right), "row", scatter_dimension=0, tiled=True
    )


def visible(query_member, query_position, member, position):
    same = query_member[:, None] == member[None, :]
    behind = position[None, :] <= query_position[:, None]
    return same & behind


def attend_scores(query_block, key_all, allowed):
    scores = jnp.einsum(
        "qhd,khd->hqk", query_block, key_all, preferred_element_type=jnp.float32
    ) * HEAD_DIM ** (-0.5)
    return jnp.where(allowed[None, :, :], scores, NEG_FILL)


def norm_back(grad_normed, inputs_f, scale_rows, gain):
    gain_part = jnp.sum(grad_normed * inputs_f * scale_rows[:, None], axis=0)
    scaled = grad_normed * gain[None, :]
    inner = col_total(scaled * inputs_f)
    grad_inputs = scale_rows[:, None] * scaled - inputs_f * (scale_rows**3 * inner / D)[:, None]
    return (grad_inputs, gain_part)


def on_any_mesh(
    tokens,
    cotangent,
    query_master,
    key_master,
    value_master,
    out_master,
    gate_master,
    up_master,
    down_master,
    attn_gain,
    ffn_gain,
    lengths,
    permutation,
):
    own_rows = tokens.shape[0]
    group_rows = own_rows * lax.axis_size("row")
    quarter = group_rows // lax.axis_size("col")
    device_slot = lax.axis_index(("dp", "row"))
    group_slot = lax.axis_index("dp")
    col_slot = lax.axis_index("col")
    own_sources = lax.dynamic_slice_in_dim(permutation, device_slot * own_rows, own_rows)
    own_tokens, own_cotangent = make_picker(
        own_sources,
        (jnp.zeros_like(tokens), jnp.zeros_like(cotangent)),
        (
            lax.all_gather(tokens, ("dp", "row"), axis=0, tiled=True),
            lax.all_gather(cotangent, ("dp", "row"), axis=0, tiled=True),
        ),
    )
    masters = tuple(
        (
            matrix.astype(jnp.bfloat16)
            for matrix in (
                query_master,
                key_master,
                value_master,
                out_master,
                gate_master,
                up_master,
                down_master,
            )
        )
    )
    query_weight, key_weight, value_weight, out_weight, gate_weight, up_weight, down_weight = (
        lax.all_gather(masters[0], "dp", axis=1, tiled=True),
        lax.all_gather(masters[1], "dp", axis=1, tiled=True),
        lax.all_gather(masters[2], "dp", axis=1, tiled=True),
        lax.all_gather(masters[3], "dp", axis=0, tiled=True),
        lax.all_gather(masters[4], "dp", axis=1, tiled=True),
        lax.all_gather(masters[5], "dp", axis=1, tiled=True),
        lax.all_gather(masters[6], "dp", axis=0, tiled=True),
    )
    attention_in = jnp.concatenate([query_weight, key_weight, value_weight], axis=1)
    feedforward_in = jnp.concatenate([gate_weight, up_weight], axis=1)
    width_row = query_weight.shape[1]
    heads_row = width_row // HEAD_DIM
    hidden_row = gate_weight.shape[1]
    member, position = sequence_marks(permutation, lengths, group_slot * group_rows, group_rows)
    query_member = lax.dynamic_slice_in_dim(member, col_slot * quarter, quarter)
    query_position = lax.dynamic_slice_in_dim(position, col_slot * quarter, quarter)
    block_rows = min(512, quarter)
    block_count = quarter // block_rows
    residual_in = own_tokens.astype(jnp.float32)
    scale_one = lax.rsqrt(col_total(residual_in * residual_in) / D + EPSILON)
    normed_one = (residual_in * scale_one[:, None] * attn_gain[None, :]).astype(jnp.bfloat16)
    spread_one = row_gather(normed_one)
    projected = col_reduce(spread_one, attention_in, False).astype(jnp.bfloat16)
    queries = projected[:, :width_row].reshape(quarter, heads_row, HEAD_DIM)
    keys_here = projected[:, width_row : 2 * width_row]
    values_here = projected[:, 2 * width_row :]
    key_flat, value_flat = key_gather(keys_here, values_here)
    key_all = key_flat.reshape(group_rows, heads_row, HEAD_DIM)
    value_all = value_flat.reshape(group_rows, heads_row, HEAD_DIM)

    def block_mask(first_row):
        return visible(
            lax.dynamic_slice_in_dim(query_member, first_row, block_rows),
            lax.dynamic_slice_in_dim(query_position, first_row, block_rows),
            member,
            position,
        )

    def forward_block(block_id):
        first_row = block_id * block_rows
        query_block = lax.dynamic_slice_in_dim(queries, first_row, block_rows, 0)
        scores = attend_scores(query_block, key_all, block_mask(first_row))
        highest = jnp.max(scores, axis=2, keepdims=True)
        totals = jnp.sum(jnp.exp(scores - highest), axis=2, keepdims=True)
        log_total = highest + jnp.log(totals)
        probability = jnp.exp(scores - log_total)
        output = jnp.einsum(
            "hqk,khd->qhd",
            probability.astype(jnp.bfloat16),
            value_all,
            preferred_element_type=jnp.float32,
        )
        return (output.astype(jnp.bfloat16).reshape(block_rows, width_row), log_total[:, :, 0])

    blocks_out, log_totals = lax.map(forward_block, jnp.arange(block_count, dtype=jnp.int32))
    attended = blocks_out.reshape(quarter, width_row)
    spread_attn = col_gather(attended)
    midway = residual_in + row_reduce(spread_attn, out_weight, False)
    scale_two = lax.rsqrt(col_total(midway * midway) / D + EPSILON)
    normed_two = (midway * scale_two[:, None] * ffn_gain[None, :]).astype(jnp.bfloat16)
    spread_two = row_gather(normed_two)
    gate_and_up = col_reduce(spread_two, feedforward_in, False)
    gate_value = gate_and_up[:, :hidden_row]
    up_value = gate_and_up[:, hidden_row:]
    sigmoid_gate = jax.nn.sigmoid(gate_value)
    hidden = (gate_value * sigmoid_gate * up_value).astype(jnp.bfloat16)
    grad_output = own_cotangent.astype(jnp.float32)
    spread_down = row_gather(own_cotangent)
    grad_hidden = col_reduce(spread_down, down_weight, True)
    spread_hidden = col_gather(hidden)
    grad_down = outer_sum(spread_hidden, spread_down)
    grad_gate_value = (
        grad_hidden * up_value * sigmoid_gate * (1.0 + gate_value * (1.0 - sigmoid_gate))
    ).astype(jnp.bfloat16)
    grad_up_value = (grad_hidden * gate_value * sigmoid_gate).astype(jnp.bfloat16)
    spread_gate_up = col_gather(jnp.concatenate([grad_gate_value, grad_up_value], axis=1))
    grad_normed_two = row_reduce(spread_gate_up, feedforward_in, True)
    spread_two = row_gather(normed_two)
    grad_feedforward = outer_sum(spread_two, spread_gate_up)
    grad_mid_norm, gain_two_part = norm_back(grad_normed_two, midway, scale_two, ffn_gain)
    grad_midway = grad_output + grad_mid_norm
    rounded_midway = grad_midway.astype(jnp.bfloat16)
    spread_back = row_gather(rounded_midway)
    grad_attended = col_reduce(spread_back, out_weight, True).astype(jnp.bfloat16)
    spread_attn = col_gather(attended)
    key_flat, value_flat = key_gather(keys_here, values_here)
    key_all = key_flat.reshape(group_rows, heads_row, HEAD_DIM)
    value_all = value_flat.reshape(group_rows, heads_row, HEAD_DIM)
    grad_out_local = outer_sum(spread_attn, spread_back)

    def backward_block(carried, block_id):
        first_row = block_id * block_rows
        query_block = lax.dynamic_slice_in_dim(queries, first_row, block_rows, 0)
        scores = attend_scores(query_block, key_all, block_mask(first_row))
        probability = jnp.exp(
            scores - lax.dynamic_index_in_dim(log_totals, block_id, 0, keepdims=False)[:, :, None]
        )
        weights_low = probability.astype(jnp.bfloat16)
        grad_block = lax.dynamic_slice_in_dim(grad_attended, first_row, block_rows, 0).reshape(
            block_rows, heads_row, HEAD_DIM
        )
        grad_soft = jnp.einsum(
            "qhd,khd->hqk", grad_block, value_all, preferred_element_type=jnp.float32
        )
        row_inner = jnp.sum(probability * grad_soft, axis=2, keepdims=True)
        grad_scores = (probability * (grad_soft - row_inner)).astype(jnp.bfloat16)
        grad_query_block = jnp.einsum(
            "hqk,khd->qhd", grad_scores, key_all, preferred_element_type=jnp.float32
        ) * HEAD_DIM ** (-0.5)
        grad_key_all = carried[0] + jnp.einsum(
            "hqk,qhd->khd", grad_scores, query_block, preferred_element_type=jnp.float32
        ) * HEAD_DIM ** (-0.5)
        grad_value_all = carried[1] + jnp.einsum(
            "hqk,qhd->khd", weights_low, grad_block, preferred_element_type=jnp.float32
        )
        return (
            (grad_key_all, grad_value_all),
            grad_query_block.astype(jnp.bfloat16).reshape(block_rows, width_row),
        )

    start_grads = jnp.zeros((group_rows, heads_row, HEAD_DIM), jnp.float32)
    key_value_grads, grad_queries = lax.scan(
        backward_block, (start_grads, start_grads), jnp.arange(block_count, dtype=jnp.int32)
    )
    grad_queries = grad_queries.reshape(quarter, width_row)
    grad_key_part = key_value_grads[0].reshape(group_rows, width_row)
    grad_value_part = key_value_grads[1].reshape(group_rows, width_row)
    grad_key_mine, grad_value_mine = (
        lax.psum_scatter(grad_key_part, "col", scatter_dimension=0, tiled=True),
        lax.psum_scatter(grad_value_part, "col", scatter_dimension=0, tiled=True),
    )
    spread_projected = col_gather(
        jnp.concatenate(
            [
                grad_queries,
                grad_key_mine.astype(jnp.bfloat16),
                grad_value_mine.astype(jnp.bfloat16),
            ],
            axis=1,
        )
    )
    grad_normed_one = row_reduce(spread_projected, attention_in, True)
    spread_one = row_gather(normed_one)
    grad_attention = outer_sum(spread_one, spread_projected)
    grad_in_norm, gain_one_part = norm_back(grad_normed_one, residual_in, scale_one, attn_gain)
    grad_own_tokens = grad_midway + grad_in_norm
    grad_attn_gain, grad_ffn_gain = lax.psum((gain_one_part, gain_two_part), ("dp", "row"))
    grad_query, grad_key, grad_value, grad_out, grad_gate, grad_up, grad_down_mine = (
        lax.psum_scatter(
            grad_attention[:, :width_row].astype(jnp.bfloat16),
            "dp",
            scatter_dimension=1,
            tiled=True,
        ).astype(jnp.float32),
        lax.psum_scatter(
            grad_attention[:, width_row : 2 * width_row].astype(jnp.bfloat16),
            "dp",
            scatter_dimension=1,
            tiled=True,
        ).astype(jnp.float32),
        lax.psum_scatter(
            grad_attention[:, 2 * width_row :].astype(jnp.bfloat16),
            "dp",
            scatter_dimension=1,
            tiled=True,
        ).astype(jnp.float32),
        lax.psum_scatter(
            grad_out_local.astype(jnp.bfloat16), "dp", scatter_dimension=0, tiled=True
        ).astype(jnp.float32),
        lax.psum_scatter(
            grad_feedforward[:, :hidden_row].astype(jnp.bfloat16),
            "dp",
            scatter_dimension=1,
            tiled=True,
        ).astype(jnp.float32),
        lax.psum_scatter(
            grad_feedforward[:, hidden_row:].astype(jnp.bfloat16),
            "dp",
            scatter_dimension=1,
            tiled=True,
        ).astype(jnp.float32),
        lax.psum_scatter(
            grad_down.astype(jnp.bfloat16), "dp", scatter_dimension=0, tiled=True
        ).astype(jnp.float32),
    )
    total_tokens = permutation.shape[0]
    inverse = (
        jnp.zeros((total_tokens,), jnp.int32)
        .at[permutation]
        .set(jnp.arange(total_tokens, dtype=jnp.int32))
    )
    wanted_slots = lax.dynamic_slice_in_dim(inverse, device_slot * own_rows, own_rows)
    (grad_tokens,) = make_picker(
        wanted_slots,
        (jnp.zeros_like(grad_own_tokens),),
        (
            (
                lax.all_gather(
                    grad_own_tokens.astype(jnp.bfloat16), ("dp", "row"), axis=0, tiled=True
                ),
            )[0].astype(jnp.float32),
        ),
    )
    return (
        grad_tokens,
        grad_query,
        grad_key,
        grad_value,
        grad_out,
        grad_gate,
        grad_up,
        grad_down_mine,
        grad_attn_gain,
        grad_ffn_gain,
    )


def move(array, to):
    pairs = []
    for d in range(DP):
        for r in range(ROW):
            for c in range(COL):
                target = to(d, r, c)
                if target is not None:
                    e, s, b = target
                    pairs.append(((d * ROW + r) * COL + c, (e * ROW + s) * COL + b))
    return lax.ppermute(array, AXES, pairs)


def by_col(array, step):
    return move(array, lambda d, r, c: (d, r, c ^ step))


def by_plane(array, step):
    return move(array, lambda d, r, c: (d ^ step, r, c))


def by_chip(array, over_x, over_y):
    return move(array, lambda d, r, c: (d, r ^ over_x, c ^ (2 * over_y)))


def col_sum(values):
    return values + by_col(values, 2) + by_col(values, 1) + by_col(values, 3)


def same_sum(values):
    for step in (1, 2):
        values = values + by_plane(values, step)
    return values + by_chip(values, 1, 0)


def plane_gather(block):
    beside = by_chip(block, 1, 0)
    across = by_chip(block, 0, 1)
    corner = by_chip(block, 1, 1)
    rail = jnp.concatenate(
        [jnp.concatenate([block, across], 1), jnp.concatenate([beside, corner], 1)], 0
    )
    return jnp.concatenate([rail, by_col(rail, 1)], 1)


def plane_scatter(left, weight, contract):
    rows = left.shape[0] // 2
    half = D // 2
    numbers = (((1,), (contract,)), ((), ()))
    kept, given = (weight[:, :half], weight[:, half:]) if contract == 0 else (weight[:half], weight[half:])
    theirs = lax.dot_general(left, given, numbers, preferred_element_type=F32).astype(BF)
    arrived = by_col(theirs, 1)
    mine = lax.dot_general(left, kept, numbers, preferred_element_type=F32)
    mine = mine + arrived.astype(F32)
    low = mine.astype(BF)
    part = half // 2
    return (
        mine[:rows, :part]
        + by_chip(low[rows:, :part], 1, 0).astype(F32)
        + by_chip(low[:rows, part:], 0, 1).astype(F32)
        + by_chip(low[rows:, part:], 1, 1).astype(F32)
    )


def hidden_from(step):
    def to(d, s, c):
        b = c ^ step
        return (d, s ^ (b & 1), b)

    return to


def hidden_back(step):
    def to(d, r, c):
        return (d, r ^ (c & 1), c ^ step)

    return to


def begins_of(lengths, first, amount):
    ends = running_sum(lengths)
    place = first + jnp.arange(amount, dtype=jnp.int32)
    passed = ends[None, :] <= place[:, None]
    return jnp.max(jnp.where(passed, ends[None, :], 0), axis=1)


def seen(begin_ref, block, rows, span):
    query = lax.broadcasted_iota(jnp.int32, (rows, span), 0)
    key = lax.broadcasted_iota(jnp.int32, (rows, span), 1)
    begin = begin_ref[:, 0:1] + (REACH - block * rows)
    return (key <= query + REACH) & (key >= begin)


def scores_of(query, key):
    return lax.dot_general(
        query, key, (((1,), (1,)), ((), ())), preferred_element_type=F32
    ) * HEAD_DIM ** (-0.5)


def attend_kernel(begin_ref, q_ref, k_ref, v_ref, o_ref, lse_ref):
    block = pl.program_id(1)
    rows = q_ref.shape[0]
    span = rows + REACH
    window = pl.ds(pl.multiple_of(block * rows, rows), span)
    scores = scores_of(q_ref[...], k_ref[window, :])
    scores = jnp.where(seen(begin_ref, block, rows, span), scores, NEG_FILL)
    highest = jnp.max(scores, axis=1, keepdims=True)
    expo = jnp.exp(scores - highest)
    total = jnp.sum(expo, axis=1, keepdims=True)
    probability = (expo * (1.0 / total)).astype(BF)
    o_ref[...] = jnp.dot(probability, v_ref[window, :], preferred_element_type=F32).astype(BF)
    lse_ref[...] = jnp.broadcast_to(highest + jnp.log(total), lse_ref.shape)


def attend_back_kernel(
    begin_ref, q_ref, k_ref, v_ref, do_ref, lse_ref, dq_ref, dk_ref, dv_ref
):
    block = pl.program_id(1)
    rows = q_ref.shape[0]
    span = rows + REACH
    window = pl.ds(pl.multiple_of(block * rows, rows), span)

    @pl.when(block == 0)
    def _():
        dk_ref[...] = jnp.zeros_like(dk_ref)
        dv_ref[...] = jnp.zeros_like(dv_ref)

    query, key = q_ref[...], k_ref[window, :]
    grad = do_ref[...]
    scores = scores_of(query, key)
    allowed = seen(begin_ref, block, rows, span)
    probability = jnp.where(allowed, jnp.exp(jnp.where(allowed, scores - lse_ref[:, 0:1], 0.0)), 0.0)
    grad_soft = lax.dot_general(
        grad, v_ref[window, :], (((1,), (1,)), ((), ())), preferred_element_type=F32
    )
    inner = jnp.sum(probability * grad_soft, axis=1, keepdims=True)
    grad_scores = (probability * (grad_soft - inner)).astype(BF)
    scale = HEAD_DIM ** (-0.5)
    dq_ref[...] = (jnp.dot(grad_scores, key, preferred_element_type=F32) * scale).astype(BF)
    over = (((0,), (0,)), ((), ()))
    dk_ref[window, :] += lax.dot_general(grad_scores, query, over, preferred_element_type=F32) * scale
    dv_ref[window, :] += lax.dot_general(
        probability.astype(BF), grad, over, preferred_element_type=F32
    )


QROWS = 256


def attention_specs(rows, width):
    by_block = pl.BlockSpec((QROWS, HEAD_DIM), lambda h, i: (i, h))
    whole = pl.BlockSpec((rows + REACH, HEAD_DIM), lambda h, i: (0, h))
    begin = pl.BlockSpec((QROWS, 1), lambda h, i: (i, 0))
    grid = (width // HEAD_DIM, rows // QROWS)
    params = pltpu.CompilerParams(vmem_limit_bytes=40 << 20)
    return grid, by_block, whole, begin, params


def attend(begin, q, k, v):
    rows, width = q.shape
    grid, by_block, whole, begin_spec, params = attention_specs(rows, width)
    area = grid[0] * rows * (QROWS + REACH)
    return pl.pallas_call(
        attend_kernel,
        grid=grid,
        in_specs=[begin_spec, by_block, whole, whole],
        out_specs=[by_block, by_block],
        out_shape=[
            jax.ShapeDtypeStruct((rows, width), BF),
            jax.ShapeDtypeStruct((rows, width), F32),
        ],
        compiler_params=params,
        cost_estimate=pl.CostEstimate(
            flops=4 * area * HEAD_DIM, bytes_accessed=8 * rows * width, transcendentals=area
        ),
    )(begin, q, k, v)


def attend_back(begin, q, k, v, grad, lse):
    rows, width = q.shape
    grid, by_block, whole, begin_spec, params = attention_specs(rows, width)
    area = grid[0] * rows * (QROWS + REACH)
    return pl.pallas_call(
        attend_back_kernel,
        grid=grid,
        in_specs=[begin_spec, by_block, whole, whole, by_block, by_block],
        out_specs=[by_block, whole, whole],
        out_shape=[
            jax.ShapeDtypeStruct((rows, width), BF),
            jax.ShapeDtypeStruct((rows + REACH, width), F32),
            jax.ShapeDtypeStruct((rows + REACH, width), F32),
        ],
        compiler_params=params,
        cost_estimate=pl.CostEstimate(
            flops=10 * area * HEAD_DIM, bytes_accessed=24 * rows * width, transcendentals=area
        ),
    )(begin, q, k, v, grad, lse)


MESH = pl.DeviceIdType.MESH
PLACE = {0: 0, 2: 1, 1: 2, 3: 3}
TILE = 256


class Post:
    def __init__(self, send_sem, recv_sem):
        self.send_sem, self.recv_sem, self.used = send_sem, recv_sem, 0

    def ready(self, src, dst, target, slot=None):
        if slot is None:
            slot = self.used
            self.used += 1
        return pltpu.make_async_remote_copy(
            src_ref=src,
            dst_ref=dst,
            send_sem=self.send_sem.at[slot],
            recv_sem=self.recv_sem.at[slot],
            device_id=target,
            device_id_type=MESH,
        )

    def take(self, count):
        first = self.used
        self.used += count
        return first

    def send(self, src, dst, target):
        copy = self.ready(src, dst, target)
        copy.start()
        return copy


def greet(peers):
    barrier = pltpu.get_barrier_semaphore()
    for peer in peers:
        pl.semaphore_signal(barrier, inc=1, device_id=peer, device_id_type=MESH)
    pl.semaphore_wait(barrier, len(peers))


def as_row(column):
    return jnp.transpose(jnp.broadcast_to(column, (column.shape[0], 128)))[0:8]


def as_column(row):
    return jnp.transpose(row)[:, 0:1]


def forward_kernel(
    x_ref, gain_one_ref, gain_two_ref, lengths_ref, query_ref, key_ref, value_ref, out_ref, gate_ref, up_ref,
    own_grad,
    normed_ref, weight_in, weight_out, q_ref, kv_ref, att_ref, lse_ref, mid_ref, scale_ref, n2_ref, begin_ref, first_scale,
    gate_all, up_all, grad_all,
    zin, zout, sums, wide, given, arrived, low, landed, x32, hidden_own,
    send_sem, recv_sem, local_sem,
):
    d, r, c = (lax.axis_index(name) for name in AXES)
    y, core = c // 2, lax.rem(c, 2)
    rows = x_ref.shape[0]
    fc = x_ref.shape[1]
    group = 2 * rows
    width = q_ref.shape[1]
    half = 2 * fc
    post = Post(send_sem, recv_sem)
    in_plane = [(d, r ^ a, c ^ b) for a in (0, 1) for b in range(COL) if (a, b) != (0, 0)]
    greet([(d ^ j, r, c) for j in (1, 2, 3)] + in_plane)

    first = post.take(DP)

    def line(p, target_plane):
        return post.ready(zin.at[p], zin.at[p], (target_plane, r, c), first + p)

    first_down = post.take(DP)

    def line_down(p, target_plane):
        return pltpu.make_async_remote_copy(
            src_ref=zin.at[p], dst_ref=zin.at[p],
            send_sem=send_sem.at[first_down + p], recv_sem=recv_sem.at[first + p],
            device_id=(target_plane, r, c), device_id_type=MESH,
        )

    def cast_rows(src, dst, amount, step=64):
        def one(t, total):
            part = pl.ds(pl.multiple_of(t * step, step), step)
            dst(part, src[part, :].astype(BF))
            return total

        lax.fori_loop(0, amount // step, one, 0)

    for place, master in enumerate((query_ref, key_ref, value_ref)):
        def put(part, value, place=place):
            zin[d, part, place * width : (place + 1) * width] = value

        cast_rows(master, put, fc)

    @pl.when(d < DP - 1)
    def _():
        line(d, d + 1).start()

    @pl.when(d > 0)
    def _():
        line_down(d, d - 1).start()

    first_cols = post.take(DP)
    first_keep = 1

    def to_column(p):
        return pltpu.make_async_remote_copy(
            src_ref=zin.at[p],
            dst_ref=weight_in.at[pl.ds(pl.multiple_of(place_of(p ^ c) * fc, fc), fc), :],
            send_sem=send_sem.at[first_cols + p],
            recv_sem=recv_sem.at[first_cols + (p ^ c)],
            device_id=(d, r, p), device_id_type=MESH,
        )

    def place_of(m):
        return lax.rem(m, 2) * 2 + m // 2

    keep = pltpu.make_async_copy(zin.at[c], weight_in.at[pl.ds(0, fc), :], local_sem.at[first_keep])

    def pass_on(p):
        @pl.when(p == c)
        def _():
            keep.start()

        @pl.when(p != c)
        def _():
            to_column(p).start()

    pass_on(d)

    def fill_x(t, total):
        part = pl.ds(pl.multiple_of(t * 128, 128), 128)
        value = x_ref[part, :].astype(F32)
        x32[part, :] = value
        sums[0, :, part] = as_row(jnp.sum(value * value, axis=1, keepdims=True))
        return total

    lax.fori_loop(0, rows // 128, fill_x, 0)
    small = [post.send(sums.at[0], sums.at[m], (d, r, c ^ m)) for m in (1, 2, 3)]
    half_rows = rows // 2
    grad_cross = post.send(
        own_grad.at[pl.ds(pl.multiple_of((1 - y) * half_rows, half_rows), half_rows), :],
        grad_all.at[pl.ds(0, half_rows), pl.ds(fc, fc)],
        (d, r, c ^ 2),
    )
    grad_keep = pltpu.make_async_copy(
        own_grad.at[pl.ds(pl.multiple_of(y * half_rows, half_rows), half_rows), :],
        grad_all.at[pl.ds(0, half_rows), pl.ds(0, fc)],
        local_sem.at[2],
    )
    grad_keep.start()
    for kind, master in enumerate((gate_ref, up_ref)):
        def put(part, value, kind=kind):
            hidden_own[kind, part, :] = value

        cast_rows(master, put, fc)
    for copy in small:
        copy.wait_recv()

    def norm_one(t, total):
        part = pl.ds(pl.multiple_of(t * 128, 128), 128)
        square = sums[0, :, part] + sums[2, :, part] + sums[1, :, part] + sums[3, :, part]
        scale = lax.rsqrt(as_column(square) / D + EPSILON)
        first_scale[part, :] = scale
        normed_ref[part, 0:fc] = (x32[part, :] * scale * gain_one_ref[...]).astype(BF)
        return total

    lax.fori_loop(0, rows // 128, norm_one, 0)
    own_rows, other_rows = pl.ds(0, rows), pl.ds(rows, rows)

    def columns(place):
        return pl.ds(place * fc, fc)

    own_block = normed_ref.at[own_rows, columns(0)]
    beside = post.send(own_block, normed_ref.at[other_rows, columns(0)], (d, r ^ 1, c))
    beyond = post.send(own_block, normed_ref.at[own_rows, columns(1)], (d, r, c ^ 2))
    corner = post.send(own_block, normed_ref.at[other_rows, columns(1)], (d, r ^ 1, c ^ 2))
    sibling = (d, r, c ^ 1)
    shared = [post.send(own_block, normed_ref.at[own_rows, columns(2)], sibling)]

    hidden_all = (gate_all, up_all)
    first_sent = post.take(10)
    first_got = first_sent

    def slab(kind, i):
        return hidden_all[kind].at[pl.ds(pl.multiple_of(place_of(i) * fc, fc), fc), :]

    def ship(kind, way, i, target, src=None):
        return pltpu.make_async_remote_copy(
            src_ref=hidden_own.at[kind] if src is None else src,
            dst_ref=slab(kind, i),
            send_sem=send_sem.at[first_sent + 5 * kind + way],
            recv_sem=recv_sem.at[first_got + 4 * kind + i],
            device_id=target, device_id_type=MESH,
        )

    def keep_hidden(kind):
        return pltpu.make_async_copy(hidden_own.at[kind], slab(kind, 0), local_sem.at[3 + kind])

    def to_core(kind):
        return ship(kind, 0, 1, (d, r, c ^ 1))

    def over_y(kind):
        return ship(kind, 1, 2 + core, (d, r, 2 * (1 - y)))

    def over_x(kind):
        return ship(kind, 2, 1 - core, (d, r ^ 1, 2 * y + 1))

    def relay(kind, i):
        return ship(kind, i + 1, 5 - i, (d, r ^ 1, 2 * y + 1), slab(kind, i))

    def start_home(kind):
        over_x(kind).start()

        @pl.when(core == 0)
        def _():
            keep_hidden(kind).start()

        @pl.when(core == 1)
        def _():
            to_core(kind).start()

    def start_relay(kind):
        @pl.when(core == 0)
        def _():
            for i in (2, 3):
                ship(kind, 0, i, (d, r, c)).wait_recv()
                relay(kind, i).start()

    over_y(0).start()
    start_home(0)
    start_home(1)
    def put_out(part, value):
        zout[0, part, :] = value

    cast_rows(out_ref, put_out, width)

    def find_begins(t, total):
        part = pl.ds(pl.multiple_of(t * 128, 128), 128)
        place = lax.broadcasted_iota(jnp.int32, (128, 1), 0) + (d * group + t * 128)
        end = jnp.int32(0)
        begin = jnp.zeros((128, 1), jnp.int32)
        for n in range(lengths_ref.shape[0]):
            end = end + lengths_ref[n]
            begin = jnp.where(place >= end, end, begin)
        begin_ref[part, :] = begin - d * group
        return total

    lax.fori_loop(0, group // 128, find_begins, 0)

    def line_step(s):
        for p, valid, onward, forward in (
            (d - s, d - s >= 0, d < DP - 1, lambda p: line(p, d + 1)),
            (d + s, d + s < DP, d > 0, lambda p: line_down(p, d - 1)),
        ):
            @pl.when(valid)
            def _(p=p, onward=onward, forward=forward):
                line(p, d).wait_recv()

                @pl.when(onward)
                def _():
                    forward(p).start()

                pass_on(p)

    line_step(1)
    for copy, where, place in ((beside, other_rows, 0), (beyond, own_rows, 1), (corner, other_rows, 1)):
        copy.wait_recv()
        shared.append(
            post.send(normed_ref.at[where, columns(place)], normed_ref.at[where, columns(place + 2)], sibling)
        )

    line_step(2)
    line_step(3)
    outs = [post.send(zout.at[0], zout.at[j], (d ^ j, r, c)) for j in (1, 2, 3)]
    start_relay(0)

    for copy in shared:
        copy.wait_recv()
    keep.wait()
    for m in (1, 2, 3):
        pltpu.make_async_remote_copy(
            src_ref=zin.at[0], dst_ref=weight_in.at[pl.ds(0, fc), :],
            send_sem=send_sem.at[first_cols], recv_sem=recv_sem.at[first_cols + m],
            device_id=(d, r, c), device_id_type=MESH,
        ).wait_recv()
    over_y(1).start()

    def turned(t):
        return lax.rem(t + 2 * r, group // TILE)

    def project_kv(t, total):
        part = pl.ds(pl.multiple_of(t * TILE, TILE), TILE)
        to = pl.ds(pl.multiple_of(REACH + turned(t) * TILE, TILE), TILE)
        kv_ref[to, :] = jnp.dot(
            normed_ref[part, :], weight_in[:, width:], preferred_element_type=F32
        ).astype(BF)
        return total

    lax.fori_loop(0, group // TILE, project_kv, 0)
    halo = post.ready(kv_ref.at[pl.ds(group, REACH), :], kv_ref.at[pl.ds(0, REACH), :], (lax.rem(d + 1, DP), r, c))

    @pl.when(d < DP - 1)
    def _():
        halo.start()

    def project_q(t, total):
        part = pl.ds(pl.multiple_of(t * TILE, TILE), TILE)
        to = pl.ds(pl.multiple_of(turned(t) * TILE, TILE), TILE)
        q_ref[to, :] = jnp.dot(
            normed_ref[part, :], weight_in[:, :width], preferred_element_type=F32
        ).astype(BF)
        return total

    lax.fori_loop(0, group // TILE, project_q, 0)

    for copy in outs:
        copy.wait_recv()
    out_cols = [
        post.send(zout.at[d ^ c ^ m], weight_out.at[:, columns(PLACE[m])], (d, r, c ^ m)) for m in (1, 2, 3)
    ]
    out_keep = pltpu.make_async_copy(zout.at[d ^ c], weight_out.at[:, columns(0)], local_sem.at[6])
    out_keep.start()
    grad_cross.wait_recv()
    grad_keep.wait()
    grads = [
        post.send(
            grad_all.at[pl.ds(0, half_rows), pl.ds(0, half)],
            grad_all.at[pl.ds(j * half_rows, half_rows), pl.ds(0, half)],
            (d ^ j, r, c),
        )
        for j in (1, 2, 3)
    ]
    grads_shared = [
        post.send(
            grad_all.at[pl.ds(0, half_rows), pl.ds(0, half)],
            grad_all.at[pl.ds(0, half_rows), pl.ds(half, half)],
            sibling,
        )
    ]

    @pl.when(d == 0)
    def _():
        kv_ref[pl.ds(0, REACH), :] = jnp.zeros((REACH, 2 * width), BF)

    @pl.when(d > 0)
    def _():
        halo.wait_recv()

    span = TILE + REACH
    for h in range(width // HEAD_DIM):
        lanes = pl.ds(h * HEAD_DIM, HEAD_DIM)
        value_lanes = pl.ds(width + h * HEAD_DIM, HEAD_DIM)

        def one(t, total, lanes=lanes, value_lanes=value_lanes):
            part = pl.ds(pl.multiple_of(t * TILE, TILE), TILE)
            to = pl.ds(pl.multiple_of(turned(t) * TILE, TILE), TILE)
            window = pl.ds(pl.multiple_of(t * TILE, TILE), span)
            scores = scores_of(q_ref[part, lanes], kv_ref[window, lanes])
            query = lax.broadcasted_iota(jnp.int32, (TILE, span), 0)
            key = lax.broadcasted_iota(jnp.int32, (TILE, span), 1)
            begin = begin_ref[part, 0:1] + (REACH - t * TILE)
            allowed = (key <= query + REACH) & (key >= begin)
            scores = jnp.where(allowed, scores, NEG_FILL)
            highest = jnp.max(scores, axis=1, keepdims=True)
            expo = jnp.exp(scores - highest)
            total_e = jnp.sum(expo, axis=1, keepdims=True)
            probability = (expo * (1.0 / total_e)).astype(BF)
            att_ref[to, lanes] = jnp.dot(
                probability, kv_ref[window, value_lanes], preferred_element_type=F32
            ).astype(BF)
            lse_ref[part, lanes] = jnp.broadcast_to(highest + jnp.log(total_e), (TILE, HEAD_DIM))
            return total

        lax.fori_loop(0, group // TILE, one, 0)
    start_relay(1)

    for copy in out_cols:
        copy.wait_recv()
    out_keep.wait()

    def out_given(t, total):
        part = pl.ds(pl.multiple_of(t * TILE, TILE), TILE)
        given[part, :] = jnp.dot(
            att_ref[part, :], weight_out[:, half:], preferred_element_type=F32
        ).astype(BF)
        return total

    lax.fori_loop(0, group // TILE, out_given, 0)
    to_sibling = post.send(given, arrived, sibling)

    def out_kept(t, total):
        part = pl.ds(pl.multiple_of(t * TILE, TILE), TILE)
        wide[part, :] = jnp.dot(att_ref[part, :], weight_out[:, :half], preferred_element_type=F32)
        return total

    lax.fori_loop(0, group // TILE, out_kept, 0)
    to_sibling.wait_recv()

    def add_low(t, total):
        part = pl.ds(pl.multiple_of(t * 128, 128), 128)
        value = wide[part, :] + arrived[part, :].astype(F32)
        wide[part, :] = value
        low[part, :] = value.astype(BF)
        return total

    lax.fori_loop(0, group // 128, add_low, 0)
    pieces = [
        post.send(low.at[other_rows, columns(1)], landed.at[2], (d, r ^ 1, c ^ 2)),
        post.send(low.at[other_rows, columns(0)], landed.at[0], (d, r ^ 1, c)),
        post.send(low.at[own_rows, columns(1)], landed.at[1], (d, r, c ^ 2)),
    ]
    for copy in pieces:
        copy.wait_recv()

    def middle(t, total):
        part = pl.ds(pl.multiple_of(t * 128, 128), 128)
        value = (
            x32[part, :] + wide[part, 0:fc] + landed[0, part, :].astype(F32)
            + landed[1, part, :].astype(F32) + landed[2, part, :].astype(F32)
        )
        mid_ref[part, :] = value
        sums[4, :, part] = as_row(jnp.sum(value * value, axis=1, keepdims=True))
        return total

    lax.fori_loop(0, rows // 128, middle, 0)
    again = [post.send(sums.at[4], sums.at[4 + m], (d, r, c ^ m)) for m in (1, 2, 3)]
    for copy in again:
        copy.wait_recv()

    def norm_two(t, total):
        part = pl.ds(pl.multiple_of(t * 128, 128), 128)
        square = sums[4, :, part] + sums[6, :, part] + sums[5, :, part] + sums[7, :, part]
        scale = lax.rsqrt(as_column(square) / D + EPSILON)
        scale_ref[part, :] = scale
        n2_ref[part, :] = (mid_ref[part, :] * scale * gain_two_ref[...]).astype(BF)
        return total

    lax.fori_loop(0, rows // 128, norm_two, 0)

    for j, copy in zip((1, 2, 3), grads):
        copy.wait_recv()
        there = pl.ds(j * half_rows, half_rows)
        grads_shared.append(
            post.send(grad_all.at[there, pl.ds(0, half)], grad_all.at[there, pl.ds(half, half)], sibling)
        )
    for copy in grads_shared:
        copy.wait_recv()
    for kind in (0, 1):
        over_y(kind).wait_send()
        over_x(kind).wait_send()

        @pl.when(core == 0)
        def _(kind=kind):
            keep_hidden(kind).wait()
            ship(kind, 0, 1, (d, r, c)).wait_recv()
            for i in (2, 3):
                relay(kind, i).wait_send()

        @pl.when(core == 1)
        def _(kind=kind):
            to_core(kind).wait_send()
            for i in range(COL):
                ship(kind, 0, i, (d, r, c)).wait_recv()

    for copy in (
        small + [grad_cross, beside, beyond, corner] + shared + outs + out_cols + grads + grads_shared
        + [to_sibling] + pieces + again
    ):
        copy.wait_send()

    @pl.when(d < DP - 1)
    def _():
        halo.wait_send()

    for p in range(DP):
        @pl.when((d < DP - 1) & (p <= d))
        def _(p=p):
            line(p, d).wait_send()

        @pl.when((d > 0) & (p >= d))
        def _(p=p):
            line_down(p, d).wait_send()

        @pl.when(c != p)
        def _(p=p):
            to_column(p).wait_send()


SENDS = 64


def forward(x, gain_one, gain_two, lengths, query, key, value, out, gate, up, own_grad):
    rows, fc = x.shape
    group = 2 * rows
    width = out.shape[0]
    units = gate.shape[1]
    vmem = pl.BlockSpec(memory_space=pltpu.VMEM)
    smem = pl.BlockSpec(memory_space=pltpu.SMEM)
    hbm = pl.BlockSpec(memory_space=pl.ANY)

    def like(shape, dtype=BF):
        return jax.ShapeDtypeStruct(shape, dtype)

    return pl.pallas_call(
        forward_kernel,
        in_specs=[vmem] * 3 + [smem] + [vmem] * 6 + [hbm],
        out_specs=[vmem] * 12 + [hbm] * 3,
        out_shape=[
            like((group, D)),
            like((D, 3 * width)),
            like((width, D)),
            like((group, width)),
            like((REACH + group, 2 * width)),
            like((group, width)),
            like((group, width), F32),
            like((rows, fc), F32),
            like((rows, 1), F32),
            like((rows, fc)),
            like((group, 1), jnp.int32),
            like((rows, 1), F32),
            like((D, units)),
            like((D, units)),
            like((group, D)),
        ],
        scratch_shapes=[
            pltpu.VMEM((DP, fc, 3 * width), BF),
            pltpu.VMEM((DP, width, fc), BF),
            pltpu.VMEM((8, 8, rows), F32),
            pltpu.VMEM((group, 2 * fc), F32),
            pltpu.VMEM((group, 2 * fc), BF),
            pltpu.VMEM((group, 2 * fc), BF),
            pltpu.VMEM((group, 2 * fc), BF),
            pltpu.VMEM((3, rows, fc), BF),
            pltpu.VMEM((rows, fc), F32),
            pltpu.VMEM((2, fc, units), BF),
            pltpu.SemaphoreType.DMA((SENDS,)),
            pltpu.SemaphoreType.DMA((SENDS,)),
            pltpu.SemaphoreType.DMA((8,)),
        ],
        compiler_params=pltpu.CompilerParams(
            collective_id=1, has_side_effects=True, vmem_limit_bytes=60 << 20
        ),
        cost_estimate=pl.CostEstimate(
            flops=6 * group * D * width, bytes_accessed=64 << 20, transcendentals=0
        ),
    )(x, gain_one, gain_two, lengths, query, key, value, out, gate, up, own_grad)


POSTS = 112


def backward_kernel(
    x_ref, gain_ref, scale_ref, mid_ref, gain_two_ref, weight_in, weight_out, q_ref, kv_ref, att_ref, lse_ref,
    begin_ref, normed_hbm, n2_hbm, dgate_hbm, dup_hbm,
    tokens_out, in_out, out_out, gains_out, got, comb,
    n1, n2, dgu, dball, dotted, dproj, acc, spill, spilled, stage, own_f, arrived, landed,
    zq, zo, zkv, rq, ro, rkv, sums, gsum,
    send_sem, recv_sem, local_sem,
):
    d, r, c = (lax.axis_index(name) for name in AXES)
    y, core = c // 2, lax.rem(c, 2)
    rows, fc = x_ref.shape
    group = 2 * rows
    width = q_ref.shape[1]
    units = dgate_hbm.shape[1]
    half = 2 * fc
    tiles = group // TILE
    over = (((0,), (0,)), ((), ()))
    across = (((1,), (1,)), ((), ()))
    post = Post(send_sem, recv_sem)
    others = [(a, b) for a in (0, 1) for b in range(COL) if (a, b) != (0, 0)]
    greet(
        [(d, r ^ a, c ^ b) for a, b in others]
        + [(d ^ j, r ^ a, c) for j in (1, 2, 3) for a in (0, 1)]
    )

    def columns(place):
        return pl.ds(place * fc, fc)

    def at(t, size):
        return pl.ds(pl.multiple_of(t * size, size), size)

    def loop(count, body):
        def one(t, total):
            body(t)
            return total

        lax.fori_loop(0, count, one, 0)

    def turned(t):
        return lax.rem(t + 2 * r, tiles)

    def raw(src, dst, sent, got_at, target):
        return pltpu.make_async_remote_copy(
            src_ref=src, dst_ref=dst, send_sem=send_sem.at[sent], recv_sem=recv_sem.at[got_at],
            device_id=target, device_id_type=MESH,
        )

    me = (d, r, c)
    sibling = (d, r, c ^ 1)
    own_rows, other_rows = pl.ds(0, rows), pl.ds(rows, rows)
    loads = [
        pltpu.make_async_copy(src, dst, local_sem.at[n])
        for n, (src, dst) in enumerate((
            (n2_hbm, n2),
            (dgate_hbm, dgu.at[pl.ds(0, group), :]),
            (dup_hbm, dgu.at[pl.ds(group, group), :]),
            (normed_hbm, n1),
        ))
    ]
    for load in loads:
        load.start()

    def round_mid(t):
        dball[at(t, 128), 0:fc] = mid_ref[at(t, 128), :].astype(BF)

    loop(rows // 128, round_mid)
    own_block = dball.at[own_rows, columns(0)]
    beside = post.send(own_block, dball.at[other_rows, columns(0)], (d, r ^ 1, c))
    beyond = post.send(own_block, dball.at[own_rows, columns(1)], (d, r, c ^ 2))
    corner = post.send(own_block, dball.at[other_rows, columns(1)], (d, r ^ 1, c ^ 2))
    shared = [post.send(own_block, dball.at[own_rows, columns(2)], sibling)]

    for load in loads[:3]:
        load.wait()
    for i in (2, 3, 0, 1):
        for kind in (0, 1):
            def hidden_grad(t, i=i, kind=kind):
                left = n2[:, pl.ds(pl.multiple_of(PLACE[i] * fc + t * TILE, TILE), TILE)]
                stage[kind, i, at(t, TILE), :] = lax.dot_general(
                    left, dgu[pl.ds(kind * group, group), :], over, preferred_element_type=F32
                ).astype(BF)

            loop(fc // TILE, hidden_grad)
    loads[3].wait()

    for copy, where, place in ((beside, other_rows, 0), (beyond, own_rows, 1), (corner, other_rows, 1)):
        copy.wait_recv()
        shared.append(post.send(dball.at[where, columns(place)], dball.at[where, columns(place + 2)], sibling))
    bulk = post.take(20)

    def from_one(kind, i):
        if i < 2:
            return raw(stage.at[kind, i], got.at[kind, 0], bulk + 4 * kind + i, bulk + 10 * kind + 0,
                       (d, r ^ 1, 2 * y + 1 - i))
        return raw(stage.at[kind, i], comb.at[kind, 3 - i], bulk + 4 * kind + i,
                   bulk + 10 * kind + 3 + (3 - i), (d, r ^ 1, 2 * y))

    def from_zero(kind, i):
        if i == 1:
            return raw(stage.at[kind, i], got.at[kind, 1], bulk + 4 * kind + i, bulk + 10 * kind + 1, sibling)
        return raw(stage.at[kind, i], got.at[kind, 2], bulk + 4 * kind + i, bulk + 10 * kind + 2,
                   (d, r, 2 * (1 - y) + i - 2))

    def home(kind):
        return pltpu.make_async_copy(stage.at[kind, 0], got.at[kind, 1], local_sem.at[4 + kind])

    @pl.when(core == 1)
    def _():
        for i in (2, 3, 0, 1):
            for kind in (0, 1):
                from_one(kind, i).start()

    @pl.when(core == 0)
    def _():
        for kind in (0, 1):
            home(kind).start()
            from_zero(kind, 1).start()

    for copy in shared:
        copy.wait_recv()

    def head_grad(t):
        dotted[at(turned(t), TILE), :] = lax.dot_general(
            dball[at(t, TILE), :], weight_out[...], across, preferred_element_type=F32
        ).astype(BF)

    loop(tiles, head_grad)
    span = TILE + REACH
    scale = HEAD_DIM ** (-0.5)
    spills = []
    for h in range(width // HEAD_DIM):
        lanes = pl.ds(h * HEAD_DIM, HEAD_DIM)
        value_lanes = pl.ds(width + h * HEAD_DIM, HEAD_DIM)

        def clear(t, lanes=lanes, value_lanes=value_lanes):
            acc[at(t, TILE), lanes] = jnp.zeros((TILE, HEAD_DIM), F32)
            acc[at(t, TILE), value_lanes] = jnp.zeros((TILE, HEAD_DIM), F32)

        loop((group + REACH) // TILE, clear)

        def one(t, lanes=lanes, value_lanes=value_lanes):
            part = at(t, TILE)
            window = pl.ds(pl.multiple_of(t * TILE, TILE), span)
            query, key = q_ref[part, lanes], kv_ref[window, lanes]
            grad = dotted[part, lanes]
            scores = scores_of(query, key)
            query_at = lax.broadcasted_iota(jnp.int32, (TILE, span), 0)
            key_at = lax.broadcasted_iota(jnp.int32, (TILE, span), 1)
            begin = begin_ref[part, 0:1] + (REACH - t * TILE)
            allowed = (key_at <= query_at + REACH) & (key_at >= begin)
            scores = jnp.where(allowed, scores - lse_ref[part, lanes][:, 0:1], NEG_FILL)
            probability = jnp.exp(scores)
            grad_soft = lax.dot_general(grad, kv_ref[window, value_lanes], across, preferred_element_type=F32)
            inner = jnp.sum(probability * grad_soft, axis=1, keepdims=True)
            grad_scores = (probability * (grad_soft - inner)).astype(BF)
            dproj[at(turned(t), TILE), lanes] = (
                jnp.dot(grad_scores, key, preferred_element_type=F32) * scale
            ).astype(BF)
            acc[window, lanes] += lax.dot_general(grad_scores, query, over, preferred_element_type=F32) * scale
            acc[window, value_lanes] += lax.dot_general(
                probability.astype(BF), grad, over, preferred_element_type=F32
            )

        loop(tiles, one)

        def round_spill(t, h=h, lanes=lanes, value_lanes=value_lanes):
            spill[h, at(t, TILE), 0:HEAD_DIM] = acc[at(t, TILE), lanes].astype(BF)
            spill[h, at(t, TILE), HEAD_DIM:] = acc[at(t, TILE), value_lanes].astype(BF)

        loop(REACH // TILE, round_spill)
        copy = post.ready(spill.at[h], spilled.at[h], (lax.rem(d + DP - 1, DP), r, c))
        spills.append(copy)

        @pl.when(d > 0)
        def _(copy=copy):
            copy.start()

    sent_out = [None] + [post.take(1) for _ in (1, 2, 3)]
    outs = []
    for place, m in enumerate((0, 2, 1, 3)):
        value = lax.dot_general(
            att_ref[...], dball[:, place * fc : (place + 1) * fc], over, preferred_element_type=F32
        ).astype(BF)
        if m == 0:
            zo[c] = value
        else:
            n2[(m - 1) * width : m * width, half : half + fc] = value
            staged = n2.at[pl.ds((m - 1) * width, width), pl.ds(half, fc)]
            copy = raw(staged, zo.at[c], sent_out[m], sent_out[m], (d, r, c ^ m))
            copy.start()
            outs.append(copy)

    def attention_grads(first_lane, lane_count, dest):
        lanes = slice(first_lane, first_lane + lane_count)
        slots = [None] + [post.take(1) for _ in (1, 2, 3)]
        copies = []
        for place, m in enumerate((0, 2, 1, 3)):
            def tile(t, place=place, m=m):
                left = n1[:, pl.ds(pl.multiple_of(place * fc + t * TILE, TILE), TILE)]
                value = lax.dot_general(left, dproj[:, lanes], over, preferred_element_type=F32).astype(BF)
                if m == 0:
                    dest[c, at(t, TILE), :] = value
                else:
                    dgu[pl.ds(pl.multiple_of(place * fc + t * TILE, TILE), TILE), lanes] = value

            loop(fc // TILE, tile)
            if m:
                copy = raw(
                    dgu.at[pl.ds(place * fc, fc), pl.ds(first_lane, lane_count)], dest.at[c],
                    slots[m], slots[m], (d, r, c ^ m),
                )
                copy.start()
                copies.append(copy)
        return copies

    qs = attention_grads(0, width, zq)

    @pl.when(d < DP - 1)
    def _():
        for copy in spills:
            copy.wait_recv()

    @pl.when(d == DP - 1)
    def _():
        spilled[...] = jnp.zeros_like(spilled)

    for h in range(width // HEAD_DIM):
        for which in (0, 1):
            lanes = pl.ds(which * width + h * HEAD_DIM, HEAD_DIM)
            out_lanes = pl.ds((1 + which) * width + h * HEAD_DIM, HEAD_DIM)

            def whole(t, h=h, which=which, lanes=lanes, out_lanes=out_lanes):
                total = acc[pl.ds(pl.multiple_of(REACH + t * TILE, TILE), TILE), lanes]
                extra = spilled[
                    h, at(jnp.maximum(t - 1, 0), TILE), which * HEAD_DIM : (which + 1) * HEAD_DIM
                ].astype(F32)
                total = total + jnp.where(t > 0, extra, 0.0)
                dproj[at(turned(t), TILE), out_lanes] = total.astype(BF)

            loop(tiles, whole)

    kvs = attention_grads(width, 2 * width, zkv)

    def given_part(t):
        n2[at(t, TILE), 0:half] = lax.dot_general(
            dproj[at(t, TILE), :], weight_in[half:, :], across, preferred_element_type=F32
        ).astype(BF)

    loop(tiles, given_part)
    to_sibling = post.send(n2.at[:, pl.ds(0, half)], arrived, sibling)

    @pl.when(core == 0)
    def _():
        fetches = {}
        for i in (2, 3):
            for kind in (0, 1):
                raw(stage.at[kind, i], comb.at[kind, i - 2], bulk, bulk + 10 * kind + 3 + (i - 2), me).wait_recv()
                room = n1.at[pl.ds((i - 2) * fc, fc), pl.ds(kind * units, units)]
                fetches[i, kind] = pltpu.make_async_copy(
                    comb.at[kind, i - 2], room, local_sem.at[2 * kind + i - 2]
                )
                fetches[i, kind].start()
        for i in (2, 3):
            for kind in (0, 1):
                fetches[i, kind].wait()

                def add(t, kind=kind, i=i):
                    there = pl.ds(pl.multiple_of((i - 2) * fc + t * 64, 64), 64)
                    stage[kind, i, at(t, 64), :] = (
                        stage[kind, i, at(t, 64), :].astype(F32)
                        + n1[there, kind * units : (kind + 1) * units].astype(F32)
                    ).astype(BF)

                loop(fc // 64, add)
                from_zero(kind, i).start()

    to_sibling.wait_recv()
    for copy in outs:
        copy.wait_send()

    def kept_part(t):
        part = at(t, TILE)
        value = lax.dot_general(
            dproj[part, :], weight_in[:half, :], across, preferred_element_type=F32
        ) + arrived[part, :].astype(F32)
        n2[part, half:] = value.astype(BF)

        @pl.when(t < rows // TILE)
        def _():
            own_f[part, :] = value[:, 0:fc]

    loop(tiles, kept_part)

    def low(where, place):
        return n2.at[where, pl.ds(half + place * fc, fc)]

    pieces = [
        post.send(low(other_rows, 1), landed.at[2], (d, r ^ 1, c ^ 2)),
        post.send(low(other_rows, 0), landed.at[0], (d, r ^ 1, c)),
        post.send(low(own_rows, 1), landed.at[1], (d, r, c ^ 2)),
    ]

    def line_sum(arrays, base):
        def sem(n, p, down):
            return base + 8 * n + 4 * down + p

        def add(p):
            for z, got_z in arrays:
                def one(t, z=z, got_z=got_z):
                    z[p, at(t, 64), :] = (
                        z[p, at(t, 64), :].astype(F32) + got_z[p, at(t, 64), :].astype(F32)
                    ).astype(BF)

                loop(z.shape[1] // 64, one)

        def up(p):
            @pl.when((d > 0) & (d <= p))
            def _():
                for n, (z, got_z) in enumerate(arrays):
                    raw(z.at[p], got_z.at[p], sem(n, p, 0), sem(n, p, 0), me).wait_recv()

                @pl.when(d < p)
                def _():
                    add(p)

            @pl.when(d < p)
            def _():
                for n, (z, got_z) in enumerate(arrays):
                    raw(z.at[p], got_z.at[p], sem(n, p, 0), sem(n, p, 0), (d + 1, r, c)).start()

        def down(p):
            @pl.when((d < DP - 1) & (d >= p))
            def _():
                for n, (z, got_z) in enumerate(arrays):
                    raw(z.at[p], got_z.at[p], sem(n, p, 1), sem(n, p, 1), me).wait_recv()

                @pl.when(d > p)
                def _():
                    add(p)

            @pl.when(d > p)
            def _():
                slot = jnp.where(p < d - 1, p, DP)
                for n, (z, got_z) in enumerate(arrays):
                    raw(z.at[p], got_z.at[slot], sem(n, p, 1), sem(n, p, 1), (d - 1, r, c)).start()

        @pl.when(d < DP // 2)
        def _():
            for s in range(DP - 1):
                up(DP - 1 - s)
                down(s)

        @pl.when(d >= DP // 2)
        def _():
            for s in range(DP - 1):
                down(s)
                up(DP - 1 - s)

        def settle():
            for p in range(DP):
                for n, (z, got_z) in enumerate(arrays):
                    @pl.when(d < p)
                    def _(p=p, n=n, z=z, got_z=got_z):
                        raw(z.at[p], got_z.at[p], sem(n, p, 0), sem(n, p, 0), me).wait_send()

                    @pl.when(d > p)
                    def _(p=p, n=n, z=z, got_z=got_z):
                        raw(z.at[p], got_z.at[p], sem(n, p, 1), sem(n, p, 1), me).wait_send()

        return settle

    def finish(z, got_z, dest, lanes):
        def one(t):
            part = at(t, 64)
            value = z[d, part, :].astype(F32)
            value = value + jnp.where(d > 0, got_z[d, part, :].astype(F32), 0.0)
            value = value + jnp.where(d < DP - 1, got_z[DP, part, :].astype(F32), 0.0)
            dest[part, lanes] = value

        loop(z.shape[1] // 64, one)

    for copy in outs + qs:
        copy.wait_recv()
    first_line = post.take(24)
    settle_a = line_sum(((zq, rq), (zo, ro)), first_line)

    for copy in pieces:
        copy.wait_recv()

    def inner_sum(t):
        part = at(t, 128)
        value = own_f[part, :]
        for n in range(3):
            value = value + landed[n, part, :].astype(F32)
        own_f[part, :] = value
        inner = value * gain_ref[...] * x_ref[part, :].astype(F32)
        sums[0, :, part] = as_row(jnp.sum(inner, axis=1, keepdims=True))

    loop(rows // 128, inner_sum)
    small = [post.send(sums.at[0], sums.at[m], (d, r, c ^ m)) for m in (1, 2, 3)]
    seat = ROW * d + r
    gain_part = jnp.zeros((1, fc), F32)

    def gain_sum(t, total):
        part = at(t, 128)
        value = own_f[part, :] * x_ref[part, :].astype(F32) * scale_ref[part, :]
        return total + jnp.sum(value, axis=0, keepdims=True)

    gain_part = lax.fori_loop(0, rows // 128, gain_sum, gain_part)
    gsum[seat, 0:1, :] = gain_part
    gsum[seat, 1:2, :] = gain_two_ref[...]
    gsum[seat, 2:8, :] = jnp.zeros((6, fc), F32)
    gain_sent = post.take(8)
    gain_got = gain_sent

    def gain_copy(n, j, a):
        return raw(gsum.at[seat], gsum.at[seat], gain_sent + n, gain_got + seat, (d ^ j, r ^ a, c))

    far = [(j, a) for j in range(DP) for a in (0, 1) if (j, a) != (0, 0)]
    for n, (j, a) in enumerate(far):
        gain_copy(n, j, a).start()
    for copy in small:
        copy.wait_recv()

    def finish_tokens(t):
        part = at(t, 128)
        inner = as_column(sums[0, :, part] + sums[2, :, part] + sums[1, :, part] + sums[3, :, part])
        scale_rows = scale_ref[part, :]
        value = x_ref[part, :].astype(F32)
        tokens_out[part, :] = (
            mid_ref[part, :] + scale_rows * (own_f[part, :] * gain_ref[...])
            - value * (scale_rows * scale_rows * scale_rows * inner / D)
        )

    loop(rows // 128, finish_tokens)

    for copy in kvs:
        copy.wait_recv()
    settle_b = line_sum(((zkv, rkv),), first_line + 16)
    finish(zq, rq, in_out, slice(0, width))
    finish(zo, ro, out_out, slice(0, fc))
    finish(zkv, rkv, in_out, slice(width, 3 * width))
    for e in range(2 * DP):
        @pl.when(e != seat)
        def _(e=e):
            raw(gsum.at[e], gsum.at[e], gain_sent, gain_got + e, me).wait_recv()

    gains = gsum[0]
    for e in range(1, 2 * DP):
        gains = gains + gsum[e]
    gains_out[...] = gains

    for kind in (0, 1):
        for n in (0, 2):
            raw(stage.at[kind, 0], got.at[kind, n], bulk, bulk + 10 * kind + n, me).wait_recv()

        @pl.when(core == 1)
        def _(kind=kind):
            raw(stage.at[kind, 0], got.at[kind, 1], bulk, bulk + 10 * kind + 1, me).wait_recv()
            for i in range(COL):
                from_one(kind, i).wait_send()

        @pl.when(core == 0)
        def _(kind=kind):
            home(kind).wait()
            for i in (1, 2, 3):
                from_zero(kind, i).wait_send()

    settle_a()
    settle_b()
    for copy in [beside, beyond, corner] + shared + qs + kvs + [to_sibling] + pieces + small:
        copy.wait_send()
    for n, (j, a) in enumerate(far):
        gain_copy(n, j, a).wait_send()

    @pl.when(d > 0)
    def _():
        for copy in spills:
            copy.wait_send()


def backward(x, gain, scale, mid, gain_two, weight_in, weight_out, q, kv, att, lse, begin, normed, n2, dgate, dup):
    rows, fc = x.shape
    group = 2 * rows
    width = q.shape[1]
    units = dgate.shape[1]
    vmem = pl.BlockSpec(memory_space=pltpu.VMEM)
    hbm = pl.BlockSpec(memory_space=pl.ANY)

    def like(shape, dtype=BF):
        return jax.ShapeDtypeStruct(shape, dtype)

    return pl.pallas_call(
        backward_kernel,
        in_specs=[vmem] * 12 + [hbm] * 4,
        out_specs=[vmem] * 4 + [hbm] * 2,
        out_shape=[
            like((rows, fc), F32),
            like((fc, 3 * width), F32),
            like((width, fc), F32),
            like((8, fc), F32),
            like((2, 3, fc, units)),
            like((2, 2, fc, units)),
        ],
        scratch_shapes=[
            pltpu.VMEM((group, D), BF),
            pltpu.VMEM((group, D), BF),
            pltpu.VMEM((2 * group, units), BF),
            pltpu.VMEM((group, D), BF),
            pltpu.VMEM((group, width), BF),
            pltpu.VMEM((group, 3 * width), BF),
            pltpu.VMEM((group + REACH, 2 * width), F32),
            pltpu.VMEM((width // HEAD_DIM, REACH, 2 * HEAD_DIM), BF),
            pltpu.VMEM((width // HEAD_DIM, REACH, 2 * HEAD_DIM), BF),
            pltpu.VMEM((2, COL, fc, units), BF),
            pltpu.VMEM((rows, fc), F32),
            pltpu.VMEM((group, 2 * fc), BF),
            pltpu.VMEM((3, rows, fc), BF),
            pltpu.VMEM((DP, fc, width), BF),
            pltpu.VMEM((DP, width, fc), BF),
            pltpu.VMEM((DP, fc, 2 * width), BF),
            pltpu.VMEM((DP + 1, fc, width), BF),
            pltpu.VMEM((DP + 1, width, fc), BF),
            pltpu.VMEM((DP + 1, fc, 2 * width), BF),
            pltpu.VMEM((4, 8, rows), F32),
            pltpu.VMEM((2 * DP, 8, fc), F32),
            pltpu.SemaphoreType.DMA((POSTS,)),
            pltpu.SemaphoreType.DMA((POSTS,)),
            pltpu.SemaphoreType.DMA((8,)),
        ],
        compiler_params=pltpu.CompilerParams(
            collective_id=2, has_side_effects=True, vmem_limit_bytes=62 << 20
        ),
        cost_estimate=pl.CostEstimate(
            flops=12 * group * D * width + 4 * group * D * units, bytes_accessed=64 << 20, transcendentals=0
        ),
    )(x, gain, scale, mid, gain_two, weight_in, weight_out, q, kv, att, lse, begin, normed, n2, dgate, dup)


def rounded_norm(values, scale, gain):
    return (values * scale[:, None] * gain[None, :]).astype(BF)


def norm_grads(grad_normed, inputs_f, scale_rows, gain):
    gain_part = jnp.sum(grad_normed * inputs_f * scale_rows[:, None], axis=0)
    scaled = grad_normed * gain[None, :]
    inner = col_sum(jnp.sum(scaled * inputs_f, axis=1))
    grad_inputs = scale_rows[:, None] * scaled - inputs_f * (scale_rows**3 * inner / D)[:, None]
    return grad_inputs, gain_part


def on_small_mesh(
    tokens,
    cotangent,
    query_master,
    key_master,
    value_master,
    out_master,
    gate_master,
    up_master,
    down_master,
    attn_gain,
    ffn_gain,
    lengths,
    permutation,
):
    del permutation
    d, r, c = (lax.axis_index(name) for name in AXES)
    rows = tokens.shape[0]
    group = rows * ROW
    half_rows = rows // 2
    width = query_master.shape[1]
    y = c // 2

    def pick(stack, index):
        return lax.dynamic_index_in_dim(stack, index, 0, keepdims=False)

    def flip(array):
        swapped = jnp.concatenate([array[rows:], array[:rows]], 0)
        return jnp.where(r == 0, array, swapped)

    (
        normed_one, weight_in, weight_out, q, key_value, own_attended, lse, midway, scale_two,
        n2, begin, scale_one, weight_gate, weight_up, grad_all,
    ) = forward(
        tokens, attn_gain[None, :], ffn_gain[None, :], lengths, query_master, key_master,
        value_master, out_master, gate_master, up_master, cotangent,
    )
    hidden_out = down_master.astype(BF)
    scale_two = scale_two[:, 0]
    order = (0, 2, 1, 3)
    weight_hidden = jnp.concatenate([weight_gate, weight_up], 1)
    weight_down = jnp.concatenate([move(hidden_out, hidden_from(i)) for i in order], 1)

    def spread_tokens(block):
        kept = lax.dynamic_slice_in_dim(block, y * half_rows, half_rows, 0)
        given = lax.dynamic_slice_in_dim(block, (1 - y) * half_rows, half_rows, 0)
        mine = jnp.concatenate([kept, by_chip(given, 0, 1)], 1)
        rail = jnp.concatenate([mine] + [by_plane(mine, j) for j in (1, 2, 3)], 0)
        return jnp.concatenate([rail, by_col(rail, 1)], 1)

    over = (((0,), (0,)), ((), ()))
    across = (((1,), (1,)), ((), ()))
    grad_hidden = lax.dot_general(grad_all, weight_down, across, preferred_element_type=F32)
    normed_two = spread_tokens(n2)
    gate_and_up = jnp.dot(normed_two, weight_hidden, preferred_element_type=F32)
    units = hidden_out.shape[0]
    gate, up = gate_and_up[:, :units], gate_and_up[:, units:]
    sigmoid = jax.nn.sigmoid(gate)
    hidden = (gate * sigmoid * up).astype(BF)
    grad_gate = (grad_hidden * up * sigmoid * (1.0 + gate * (1.0 - sigmoid))).astype(BF)
    grad_up = (grad_hidden * gate * sigmoid).astype(BF)
    grad_both = jnp.concatenate([grad_gate, grad_up], 1)

    half = D // 2
    theirs = lax.dot_general(
        grad_both, weight_hidden[half:], across, preferred_element_type=F32
    ).astype(BF)
    arrived = by_col(theirs, 1)
    mine = lax.dot_general(grad_both, weight_hidden[:half], across, preferred_element_type=F32)
    mine = mine + arrived.astype(F32)
    low = mine.astype(BF)
    mine = mine[:half_rows]
    for j in (1, 2, 3):
        mine = mine + by_plane(low[j * half_rows : (j + 1) * half_rows], j).astype(F32)
    part = half // 2
    crossed = by_chip(mine[:, part:].astype(BF), 0, 1).astype(F32)
    grad_normed_two = jnp.where(
        y == 0,
        jnp.concatenate([mine[:, :part], crossed], 0),
        jnp.concatenate([crossed, mine[:, :part]], 0),
    )

    def plane_total(partial, axis):
        size = D // COL
        total = None
        for place, i in enumerate(order):
            piece = lax.slice_in_dim(partial, place * size, (place + 1) * size, axis=axis)
            piece = move(piece, hidden_back(i)).astype(F32)
            total = piece if total is None else total + piece
        return total

    down_part = lax.dot_general(hidden, grad_all, over, preferred_element_type=F32).astype(BF)
    grad_down_own = plane_total(down_part, 1)

    grad_mid_norm, gain_two_part = norm_grads(grad_normed_two, midway, scale_two, ffn_gain)
    grad_midway = cotangent.astype(F32) + grad_mid_norm
    grad_tokens, grad_in, grad_out, gains, got, _ = backward(
        tokens, attn_gain[None, :], scale_one, grad_midway, gain_two_part[None, :], weight_in, weight_out, q,
        key_value, own_attended, lse, begin, normed_one, normed_two, grad_gate, grad_up,
    )
    got = got.astype(F32)
    grad_hidden_own = got[:, 0] + got[:, 1] + got[:, 2]
    return (
        grad_tokens,
        grad_in[:, :width],
        grad_in[:, width : 2 * width],
        grad_in[:, 2 * width :],
        grad_out,
        grad_hidden_own[0],
        grad_hidden_own[1],
        grad_down_own,
        gains[0],
        gains[1],
    )


def solution(mesh):
    placed = (
        P(("dp", "row"), "col"),
        P(("dp", "row"), "col"),
        P("col", ("row", "dp")),
        P("col", ("row", "dp")),
        P("col", ("row", "dp")),
        P(("row", "dp"), "col"),
        P("col", ("row", "dp")),
        P("col", ("row", "dp")),
        P(("row", "dp"), "col"),
        P("col"),
        P("col"),
        P(),
        P(),
    )
    small = tuple(mesh.shape[name] for name in AXES) == (DP, ROW, COL)
    return jax.shard_map(
        on_small_mesh if small else on_any_mesh,
        mesh=mesh,
        in_specs=placed,
        out_specs=(
            P(("dp", "row"), "col"),
            P("col", ("row", "dp")),
            P("col", ("row", "dp")),
            P("col", ("row", "dp")),
            P(("row", "dp"), "col"),
            P("col", ("row", "dp")),
            P("col", ("row", "dp")),
            P(("row", "dp"), "col"),
            P("col"),
            P("col"),
        ),
        check_vma=False,
    )
```

```python
import functools

import jax
import jax.numpy as jnp
from jax import lax
from jax.experimental import pallas as pl
from jax.experimental.pallas import tpu as pltpu
from jax.sharding import PartitionSpec as P

D = 2048
HEAD_DIM = 128


EPSILON = 1e-06
NEG_FILL = -1e30
AXES = ("dp", "row", "col")
DP, ROW, COL = 4, 2, 4
REACH = 768
BF = jnp.bfloat16
F32 = jnp.float32


def running_sum(lengths):
    count = lengths.shape[0]
    earlier = jnp.arange(count)[:, None] <= jnp.arange(count)[None, :]
    return jnp.sum(jnp.where(earlier, lengths[:, None], 0), axis=0)

def make_picker(wanted, carried, pieces):
    amount = pieces[0].shape[0]
    inside = (wanted >= 0) & (wanted < amount)
    chosen = jnp.clip(wanted, 0, amount - 1)
    return tuple(
        (
            jnp.where(inside[:, None], jnp.take(shard_rows, chosen, axis=0), current)
            for shard_rows, current in zip(pieces, carried)
        )
    )


def sequence_marks(permutation, lengths, first_slot, amount):
    source = lax.dynamic_slice_in_dim(permutation, first_slot, amount)
    seq_ends = running_sum(lengths)
    passed = seq_ends[None, :] <= source[:, None]
    member = jnp.sum(passed.astype(jnp.int32), axis=1)
    begins = jnp.max(jnp.where(passed, seq_ends[None, :], 0), axis=1)
    return (member, source - begins)


def col_total(values):
    return lax.psum(jnp.sum(values, axis=1), "col")


def row_gather(values):
    return lax.all_gather(values, "row", axis=0, tiled=True)


def col_gather(values):
    return lax.all_gather(values, "col", axis=0, tiled=True)


def key_gather(keys_here, values_here):
    return (
        lax.all_gather(keys_here, "col", axis=0, tiled=True),
        lax.all_gather(values_here, "col", axis=0, tiled=True),
    )


def multiply(row_block, weight, transpose_right):
    if transpose_right:
        return lax.dot_general(
            row_block, weight, (((1,), (1,)), ((), ())), preferred_element_type=jnp.float32
        )
    return jnp.dot(row_block, weight, preferred_element_type=jnp.float32)


def outer_sum(left_rows, right_rows):
    return lax.dot_general(
        left_rows, right_rows, (((0,), (0,)), ((), ())), preferred_element_type=jnp.float32
    )


def col_reduce(spread, weight, transpose_right):
    return lax.psum_scatter(
        multiply(spread, weight, transpose_right), "col", scatter_dimension=0, tiled=True
    )


def row_reduce(spread, weight, transpose_right):
    return lax.psum_scatter(
        multiply(spread, weight, transpose_right), "row", scatter_dimension=0, tiled=True
    )


def visible(query_member, query_position, member, position):
    same = query_member[:, None] == member[None, :]
    behind = position[None, :] <= query_position[:, None]
    return same & behind


def attend_scores(query_block, key_all, allowed):
    scores = jnp.einsum(
        "qhd,khd->hqk", query_block, key_all, preferred_element_type=jnp.float32
    ) * HEAD_DIM ** (-0.5)
    return jnp.where(allowed[None, :, :], scores, NEG_FILL)


def norm_back(grad_normed, inputs_f, scale_rows, gain):
    gain_part = jnp.sum(grad_normed * inputs_f * scale_rows[:, None], axis=0)
    scaled = grad_normed * gain[None, :]
    inner = col_total(scaled * inputs_f)
    grad_inputs = scale_rows[:, None] * scaled - inputs_f * (scale_rows**3 * inner / D)[:, None]
    return (grad_inputs, gain_part)


def on_any_mesh(
    tokens,
    cotangent,
    query_master,
    key_master,
    value_master,
    out_master,
    gate_master,
    up_master,
    down_master,
    attn_gain,
    ffn_gain,
    lengths,
    permutation,
):
    own_rows = tokens.shape[0]
    group_rows = own_rows * lax.axis_size("row")
    quarter = group_rows // lax.axis_size("col")
    device_slot = lax.axis_index(("dp", "row"))
    group_slot = lax.axis_index("dp")
    col_slot = lax.axis_index("col")
    own_sources = lax.dynamic_slice_in_dim(permutation, device_slot * own_rows, own_rows)
    own_tokens, own_cotangent = make_picker(
        own_sources,
        (jnp.zeros_like(tokens), jnp.zeros_like(cotangent)),
        (
            lax.all_gather(tokens, ("dp", "row"), axis=0, tiled=True),
            lax.all_gather(cotangent, ("dp", "row"), axis=0, tiled=True),
        ),
    )
    masters = tuple(
        (
            matrix.astype(jnp.bfloat16)
            for matrix in (
                query_master,
                key_master,
                value_master,
                out_master,
                gate_master,
                up_master,
                down_master,
            )
        )
    )
    query_weight, key_weight, value_weight, out_weight, gate_weight, up_weight, down_weight = (
        lax.all_gather(masters[0], "dp", axis=1, tiled=True),
        lax.all_gather(masters[1], "dp", axis=1, tiled=True),
        lax.all_gather(masters[2], "dp", axis=1, tiled=True),
        lax.all_gather(masters[3], "dp", axis=0, tiled=True),
        lax.all_gather(masters[4], "dp", axis=1, tiled=True),
        lax.all_gather(masters[5], "dp", axis=1, tiled=True),
        lax.all_gather(masters[6], "dp", axis=0, tiled=True),
    )
    attention_in = jnp.concatenate([query_weight, key_weight, value_weight], axis=1)
    feedforward_in = jnp.concatenate([gate_weight, up_weight], axis=1)
    width_row = query_weight.shape[1]
    heads_row = width_row // HEAD_DIM
    hidden_row = gate_weight.shape[1]
    member, position = sequence_marks(permutation, lengths, group_slot * group_rows, group_rows)
    query_member = lax.dynamic_slice_in_dim(member, col_slot * quarter, quarter)
    query_position = lax.dynamic_slice_in_dim(position, col_slot * quarter, quarter)
    block_rows = min(512, quarter)
    block_count = quarter // block_rows
    residual_in = own_tokens.astype(jnp.float32)
    scale_one = lax.rsqrt(col_total(residual_in * residual_in) / D + EPSILON)
    normed_one = (residual_in * scale_one[:, None] * attn_gain[None, :]).astype(jnp.bfloat16)
    spread_one = row_gather(normed_one)
    projected = col_reduce(spread_one, attention_in, False).astype(jnp.bfloat16)
    queries = projected[:, :width_row].reshape(quarter, heads_row, HEAD_DIM)
    keys_here = projected[:, width_row : 2 * width_row]
    values_here = projected[:, 2 * width_row :]
    key_flat, value_flat = key_gather(keys_here, values_here)
    key_all = key_flat.reshape(group_rows, heads_row, HEAD_DIM)
    value_all = value_flat.reshape(group_rows, heads_row, HEAD_DIM)

    def block_mask(first_row):
        return visible(
            lax.dynamic_slice_in_dim(query_member, first_row, block_rows),
            lax.dynamic_slice_in_dim(query_position, first_row, block_rows),
            member,
            position,
        )

    def forward_block(block_id):
        first_row = block_id * block_rows
        query_block = lax.dynamic_slice_in_dim(queries, first_row, block_rows, 0)
        scores = attend_scores(query_block, key_all, block_mask(first_row))
        highest = jnp.max(scores, axis=2, keepdims=True)
        totals = jnp.sum(jnp.exp(scores - highest), axis=2, keepdims=True)
        log_total = highest + jnp.log(totals)
        probability = jnp.exp(scores - log_total)
        output = jnp.einsum(
            "hqk,khd->qhd",
            probability.astype(jnp.bfloat16),
            value_all,
            preferred_element_type=jnp.float32,
        )
        return (output.astype(jnp.bfloat16).reshape(block_rows, width_row), log_total[:, :, 0])

    blocks_out, log_totals = lax.map(forward_block, jnp.arange(block_count, dtype=jnp.int32))
    attended = blocks_out.reshape(quarter, width_row)
    spread_attn = col_gather(attended)
    midway = residual_in + row_reduce(spread_attn, out_weight, False)
    scale_two = lax.rsqrt(col_total(midway * midway) / D + EPSILON)
    normed_two = (midway * scale_two[:, None] * ffn_gain[None, :]).astype(jnp.bfloat16)
    spread_two = row_gather(normed_two)
    gate_and_up = col_reduce(spread_two, feedforward_in, False)
    gate_value = gate_and_up[:, :hidden_row]
    up_value = gate_and_up[:, hidden_row:]
    sigmoid_gate = jax.nn.sigmoid(gate_value)
    hidden = (gate_value * sigmoid_gate * up_value).astype(jnp.bfloat16)
    grad_output = own_cotangent.astype(jnp.float32)
    spread_down = row_gather(own_cotangent)
    grad_hidden = col_reduce(spread_down, down_weight, True)
    spread_hidden = col_gather(hidden)
    grad_down = outer_sum(spread_hidden, spread_down)
    grad_gate_value = (
        grad_hidden * up_value * sigmoid_gate * (1.0 + gate_value * (1.0 - sigmoid_gate))
    ).astype(jnp.bfloat16)
    grad_up_value = (grad_hidden * gate_value * sigmoid_gate).astype(jnp.bfloat16)
    spread_gate_up = col_gather(jnp.concatenate([grad_gate_value, grad_up_value], axis=1))
    grad_normed_two = row_reduce(spread_gate_up, feedforward_in, True)
    spread_two = row_gather(normed_two)
    grad_feedforward = outer_sum(spread_two, spread_gate_up)
    grad_mid_norm, gain_two_part = norm_back(grad_normed_two, midway, scale_two, ffn_gain)
    grad_midway = grad_output + grad_mid_norm
    rounded_midway = grad_midway.astype(jnp.bfloat16)
    spread_back = row_gather(rounded_midway)
    grad_attended = col_reduce(spread_back, out_weight, True).astype(jnp.bfloat16)
    spread_attn = col_gather(attended)
    key_flat, value_flat = key_gather(keys_here, values_here)
    key_all = key_flat.reshape(group_rows, heads_row, HEAD_DIM)
    value_all = value_flat.reshape(group_rows, heads_row, HEAD_DIM)
    grad_out_local = outer_sum(spread_attn, spread_back)

    def backward_block(carried, block_id):
        first_row = block_id * block_rows
        query_block = lax.dynamic_slice_in_dim(queries, first_row, block_rows, 0)
        scores = attend_scores(query_block, key_all, block_mask(first_row))
        probability = jnp.exp(
            scores - lax.dynamic_index_in_dim(log_totals, block_id, 0, keepdims=False)[:, :, None]
        )
        weights_low = probability.astype(jnp.bfloat16)
        grad_block = lax.dynamic_slice_in_dim(grad_attended, first_row, block_rows, 0).reshape(
            block_rows, heads_row, HEAD_DIM
        )
        grad_soft = jnp.einsum(
            "qhd,khd->hqk", grad_block, value_all, preferred_element_type=jnp.float32
        )
        row_inner = jnp.sum(probability * grad_soft, axis=2, keepdims=True)
        grad_scores = (probability * (grad_soft - row_inner)).astype(jnp.bfloat16)
        grad_query_block = jnp.einsum(
            "hqk,khd->qhd", grad_scores, key_all, preferred_element_type=jnp.float32
        ) * HEAD_DIM ** (-0.5)
        grad_key_all = carried[0] + jnp.einsum(
            "hqk,qhd->khd", grad_scores, query_block, preferred_element_type=jnp.float32
        ) * HEAD_DIM ** (-0.5)
        grad_value_all = carried[1] + jnp.einsum(
            "hqk,qhd->khd", weights_low, grad_block, preferred_element_type=jnp.float32
        )
        return (
            (grad_key_all, grad_value_all),
            grad_query_block.astype(jnp.bfloat16).reshape(block_rows, width_row),
        )

    start_grads = jnp.zeros((group_rows, heads_row, HEAD_DIM), jnp.float32)
    key_value_grads, grad_queries = lax.scan(
        backward_block, (start_grads, start_grads), jnp.arange(block_count, dtype=jnp.int32)
    )
    grad_queries = grad_queries.reshape(quarter, width_row)
    grad_key_part = key_value_grads[0].reshape(group_rows, width_row)
    grad_value_part = key_value_grads[1].reshape(group_rows, width_row)
    grad_key_mine, grad_value_mine = (
        lax.psum_scatter(grad_key_part, "col", scatter_dimension=0, tiled=True),
        lax.psum_scatter(grad_value_part, "col", scatter_dimension=0, tiled=True),
    )
    spread_projected = col_gather(
        jnp.concatenate(
            [
                grad_queries,
                grad_key_mine.astype(jnp.bfloat16),
                grad_value_mine.astype(jnp.bfloat16),
            ],
            axis=1,
        )
    )
    grad_normed_one = row_reduce(spread_projected, attention_in, True)
    spread_one = row_gather(normed_one)
    grad_attention = outer_sum(spread_one, spread_projected)
    grad_in_norm, gain_one_part = norm_back(grad_normed_one, residual_in, scale_one, attn_gain)
    grad_own_tokens = grad_midway + grad_in_norm
    grad_attn_gain, grad_ffn_gain = lax.psum((gain_one_part, gain_two_part), ("dp", "row"))
    grad_query, grad_key, grad_value, grad_out, grad_gate, grad_up, grad_down_mine = (
        lax.psum_scatter(
            grad_attention[:, :width_row].astype(jnp.bfloat16),
            "dp",
            scatter_dimension=1,
            tiled=True,
        ).astype(jnp.float32),
        lax.psum_scatter(
            grad_attention[:, width_row : 2 * width_row].astype(jnp.bfloat16),
            "dp",
            scatter_dimension=1,
            tiled=True,
        ).astype(jnp.float32),
        lax.psum_scatter(
            grad_attention[:, 2 * width_row :].astype(jnp.bfloat16),
            "dp",
            scatter_dimension=1,
            tiled=True,
        ).astype(jnp.float32),
        lax.psum_scatter(
            grad_out_local.astype(jnp.bfloat16), "dp", scatter_dimension=0, tiled=True
        ).astype(jnp.float32),
        lax.psum_scatter(
            grad_feedforward[:, :hidden_row].astype(jnp.bfloat16),
            "dp",
            scatter_dimension=1,
            tiled=True,
        ).astype(jnp.float32),
        lax.psum_scatter(
            grad_feedforward[:, hidden_row:].astype(jnp.bfloat16),
            "dp",
            scatter_dimension=1,
            tiled=True,
        ).astype(jnp.float32),
        lax.psum_scatter(
            grad_down.astype(jnp.bfloat16), "dp", scatter_dimension=0, tiled=True
        ).astype(jnp.float32),
    )
    total_tokens = permutation.shape[0]
    inverse = (
        jnp.zeros((total_tokens,), jnp.int32)
        .at[permutation]
        .set(jnp.arange(total_tokens, dtype=jnp.int32))
    )
    wanted_slots = lax.dynamic_slice_in_dim(inverse, device_slot * own_rows, own_rows)
    (grad_tokens,) = make_picker(
        wanted_slots,
        (jnp.zeros_like(grad_own_tokens),),
        (
            (
                lax.all_gather(
                    grad_own_tokens.astype(jnp.bfloat16), ("dp", "row"), axis=0, tiled=True
                ),
            )[0].astype(jnp.float32),
        ),
    )
    return (
        grad_tokens,
        grad_query,
        grad_key,
        grad_value,
        grad_out,
        grad_gate,
        grad_up,
        grad_down_mine,
        grad_attn_gain,
        grad_ffn_gain,
    )


def scores_of(query, key):
    return lax.dot_general(
        query, key, (((1,), (1,)), ((), ())), preferred_element_type=F32
    ) * HEAD_DIM ** (-0.5)


MESH = pl.DeviceIdType.MESH
PLACE = {0: 0, 2: 1, 1: 2, 3: 3}
TILE = 256


class Post:
    def __init__(self, send_sem, recv_sem):
        self.send_sem, self.recv_sem, self.used = send_sem, recv_sem, 0

    def ready(self, src, dst, target, slot=None):
        if slot is None:
            slot = self.used
            self.used += 1
        return pltpu.make_async_remote_copy(
            src_ref=src,
            dst_ref=dst,
            send_sem=self.send_sem.at[slot],
            recv_sem=self.recv_sem.at[slot],
            device_id=target,
            device_id_type=MESH,
        )

    def take(self, count):
        first = self.used
        self.used += count
        return first

    def send(self, src, dst, target):
        copy = self.ready(src, dst, target)
        copy.start()
        return copy


def greet(peers):
    barrier = pltpu.get_barrier_semaphore()
    for peer in peers:
        pl.semaphore_signal(barrier, inc=1, device_id=peer, device_id_type=MESH)
    pl.semaphore_wait(barrier, len(peers))


def as_row(column):
    return jnp.transpose(jnp.broadcast_to(column, (column.shape[0], 128)))[0:8]


def as_column(row):
    return jnp.transpose(row)[:, 0:1]


def forward_kernel(
    x_ref, gain_one_ref, gain_two_ref, lengths_ref, query_ref, key_ref, value_ref, out_ref, gate_ref, up_ref,
    own_grad,
    normed_ref, weight_in, weight_out, q_ref, kv_ref, att_ref, lse_ref, mid_ref, scale_ref, n2_ref, begin_ref, first_scale,
    gate_all, up_all, grad_all,
    zin, zout, sums, wide, given, arrived, low, landed, x32, hidden_own,
    send_sem, recv_sem, local_sem,
):
    d, r, c = (lax.axis_index(name) for name in AXES)
    y, core = c // 2, lax.rem(c, 2)
    rows = x_ref.shape[0]
    fc = x_ref.shape[1]
    group = 2 * rows
    width = q_ref.shape[1]
    half = 2 * fc
    post = Post(send_sem, recv_sem)
    in_plane = [(d, r ^ a, c ^ b) for a in (0, 1) for b in range(COL) if (a, b) != (0, 0)]
    greet([(d ^ j, r, c) for j in (1, 2, 3)] + in_plane)

    def fill_x(t, total):
        part = pl.ds(pl.multiple_of(t * 128, 128), 128)
        value = x_ref[part, :].astype(F32)
        x32[part, :] = value
        sums[0, :, part] = as_row(jnp.sum(value * value, axis=1, keepdims=True))
        return total

    lax.fori_loop(0, rows // 128, fill_x, 0)
    small = [post.send(sums.at[0], sums.at[m], (d, r, c ^ m)) for m in (1, 2, 3)]

    parts = (pl.ds(width, 2 * width), pl.ds(0, width))
    first, first_down = post.take(2 * DP), post.take(2 * DP)

    def line(n, p, target_plane):
        block = zin.at[p, :, parts[n]]
        return post.ready(block, block, (target_plane, r, c), first + DP * n + p)

    def line_down(n, p, target_plane):
        block = zin.at[p, :, parts[n]]
        return pltpu.make_async_remote_copy(
            src_ref=block, dst_ref=block,
            send_sem=send_sem.at[first_down + DP * n + p], recv_sem=recv_sem.at[first + DP * n + p],
            device_id=(target_plane, r, c), device_id_type=MESH,
        )

    def cast_rows(src, dst, amount, step=64):
        def one(t, total):
            part = pl.ds(pl.multiple_of(t * step, step), step)
            dst(part, src[part, :].astype(BF))
            return total

        lax.fori_loop(0, amount // step, one, 0)

    for place, master in enumerate((query_ref, key_ref, value_ref)):
        def put(part, value, place=place):
            zin[d, part, place * width : (place + 1) * width] = value

        cast_rows(master, put, fc)
    for n in (0, 1):
        @pl.when(d < DP - 1)
        def _(n=n):
            line(n, d, d + 1).start()

        @pl.when(d > 0)
        def _(n=n):
            line_down(n, d, d - 1).start()

    first_cols = post.take(2 * DP)

    def place_of(m):
        return lax.rem(m, 2) * 2 + m // 2

    def to_column(n, p):
        there = pl.ds(pl.multiple_of(place_of(p ^ c) * fc, fc), fc)
        return pltpu.make_async_remote_copy(
            src_ref=zin.at[p, :, parts[n]],
            dst_ref=weight_in.at[there, parts[n]],
            send_sem=send_sem.at[first_cols + DP * n + p],
            recv_sem=recv_sem.at[first_cols + DP * n + (p ^ c)],
            device_id=(d, r, p), device_id_type=MESH,
        )

    def keep(n):
        return pltpu.make_async_copy(
            zin.at[c, :, parts[n]], weight_in.at[pl.ds(0, fc), parts[n]], local_sem.at[n]
        )

    def pass_on(n, p):
        @pl.when(p == c)
        def _():
            keep(n).start()

        @pl.when(p != c)
        def _():
            to_column(n, p).start()

    hidden_all = (gate_all, up_all)
    first_sent = post.take(10)
    first_got = first_sent

    def slab(kind, i):
        return hidden_all[kind].at[pl.ds(pl.multiple_of(place_of(i) * fc, fc), fc), :]

    def ship(kind, way, i, target, src=None):
        return pltpu.make_async_remote_copy(
            src_ref=hidden_own.at[kind] if src is None else src,
            dst_ref=slab(kind, i),
            send_sem=send_sem.at[first_sent + 5 * kind + way],
            recv_sem=recv_sem.at[first_got + 4 * kind + i],
            device_id=target, device_id_type=MESH,
        )

    def keep_hidden(kind):
        return pltpu.make_async_copy(hidden_own.at[kind], slab(kind, 0), local_sem.at[3 + kind])

    def to_core(kind):
        return ship(kind, 0, 1, (d, r, c ^ 1))

    def over_y(kind):
        return ship(kind, 1, 2 + core, (d, r, 2 * (1 - y)))

    def over_x(kind):
        return ship(kind, 2, 1 - core, (d, r ^ 1, 2 * y + 1))

    def relay(kind, i):
        return ship(kind, i + 1, 5 - i, (d, r ^ 1, 2 * y + 1), slab(kind, i))

    def start_home(kind):
        @pl.when(core == 0)
        def _():
            keep_hidden(kind).start()

        @pl.when(core == 1)
        def _():
            to_core(kind).start()

    def start_relay(kind):
        @pl.when(core == 0)
        def _():
            for i in (2, 3):
                ship(kind, 0, i, (d, r, c)).wait_recv()
                relay(kind, i).start()

    def cast_hidden(kind):
        def put(part, value):
            hidden_own[kind, part, :] = value

        cast_rows((gate_ref, up_ref)[kind], put, fc)

    cast_hidden(0)
    over_x(0).start()
    over_y(0).start()
    for copy in small:
        copy.wait_recv()

    def norm_one(t, total):
        part = pl.ds(pl.multiple_of(t * 128, 128), 128)
        square = sums[0, :, part] + sums[2, :, part] + sums[1, :, part] + sums[3, :, part]
        scale = lax.rsqrt(as_column(square) / D + EPSILON)
        first_scale[part, :] = scale
        normed_ref[part, 0:fc] = (x32[part, :] * scale * gain_one_ref[...]).astype(BF)
        return total

    lax.fori_loop(0, rows // 128, norm_one, 0)
    own_rows, other_rows = pl.ds(0, rows), pl.ds(rows, rows)

    def columns(place):
        return pl.ds(place * fc, fc)

    own_block = normed_ref.at[own_rows, columns(0)]
    beside = post.send(own_block, normed_ref.at[other_rows, columns(0)], (d, r ^ 1, c))
    beyond = post.send(own_block, normed_ref.at[own_rows, columns(1)], (d, r, c ^ 2))
    corner = post.send(own_block, normed_ref.at[other_rows, columns(1)], (d, r ^ 1, c ^ 2))
    sibling = (d, r, c ^ 1)
    shared = [post.send(own_block, normed_ref.at[own_rows, columns(2)], sibling)]
    pass_on(0, d)
    pass_on(1, d)
    cast_hidden(1)
    start_home(0)
    start_home(1)
    over_x(1).start()
    half_rows = rows // 2
    grad_cross = post.send(
        own_grad.at[pl.ds(pl.multiple_of((1 - y) * half_rows, half_rows), half_rows), :],
        grad_all.at[pl.ds(0, half_rows), pl.ds(fc, fc)],
        (d, r, c ^ 2),
    )
    grad_keep = pltpu.make_async_copy(
        own_grad.at[pl.ds(pl.multiple_of(y * half_rows, half_rows), half_rows), :],
        grad_all.at[pl.ds(0, half_rows), pl.ds(0, fc)],
        local_sem.at[2],
    )
    grad_keep.start()

    def put_out(part, value):
        zout[0, part, :] = value

    cast_rows(out_ref, put_out, width)

    def find_begins(t, total):
        part = pl.ds(pl.multiple_of(t * 128, 128), 128)
        place = lax.broadcasted_iota(jnp.int32, (128, 1), 0) + (d * group + t * 128)
        end = jnp.int32(0)
        begin = jnp.zeros((128, 1), jnp.int32)
        for n in range(lengths_ref.shape[0]):
            end = end + lengths_ref[n]
            begin = jnp.where(place >= end, end, begin)
        begin_ref[part, :] = begin - d * group
        return total

    lax.fori_loop(0, group // 128, find_begins, 0)

    def line_step(s):
        for n in (0, 1):
            for p, valid, onward, forward in (
                (d - s, d - s >= 0, d < DP - 1, lambda n, p: line(n, p, d + 1)),
                (d + s, d + s < DP, d > 0, lambda n, p: line_down(n, p, d - 1)),
            ):
                @pl.when(valid)
                def _(n=n, p=p, onward=onward, forward=forward):
                    line(n, p, d).wait_recv()

                    @pl.when(onward)
                    def _():
                        forward(n, p).start()

                    pass_on(n, p)

    line_step(1)
    line_step(2)
    outs = [post.send(zout.at[0], zout.at[j], (d ^ j, r, c)) for j in (1, 2, 3)]
    over_y(1).start()
    for copy, where, place in ((beside, other_rows, 0), (beyond, own_rows, 1), (corner, other_rows, 1)):
        copy.wait_recv()
        shared.append(
            post.send(normed_ref.at[where, columns(place)], normed_ref.at[where, columns(place + 2)], sibling)
        )
    line_step(3)
    start_relay(0)

    def arrived_blocks(n):
        keep(n).wait()
        for m in (1, 2, 3):
            pltpu.make_async_remote_copy(
                src_ref=zin.at[0, :, parts[n]], dst_ref=weight_in.at[pl.ds(0, fc), parts[n]],
                send_sem=send_sem.at[first_cols], recv_sem=recv_sem.at[first_cols + DP * n + m],
                device_id=(d, r, c), device_id_type=MESH,
            ).wait_recv()

    for copy in shared:
        copy.wait_recv()
    arrived_blocks(0)

    def turned(t):
        return lax.rem(t + 2 * r, group // TILE)

    def project_kv(t, total):
        part = pl.ds(pl.multiple_of(t * TILE, TILE), TILE)
        to = pl.ds(pl.multiple_of(REACH + turned(t) * TILE, TILE), TILE)
        kv_ref[to, :] = jnp.dot(
            normed_ref[part, :], weight_in[:, width:], preferred_element_type=F32
        ).astype(BF)
        return total

    lax.fori_loop(0, group // TILE, project_kv, 0)
    halo = post.ready(kv_ref.at[pl.ds(group, REACH), :], kv_ref.at[pl.ds(0, REACH), :], (lax.rem(d + 1, DP), r, c))

    @pl.when(d < DP - 1)
    def _():
        halo.start()

    arrived_blocks(1)

    def project_q(t, total):
        part = pl.ds(pl.multiple_of(t * TILE, TILE), TILE)
        to = pl.ds(pl.multiple_of(turned(t) * TILE, TILE), TILE)
        q_ref[to, :] = jnp.dot(
            normed_ref[part, :], weight_in[:, :width], preferred_element_type=F32
        ).astype(BF)
        return total

    lax.fori_loop(0, group // TILE, project_q, 0)

    for copy in outs:
        copy.wait_recv()
    out_cols = [
        post.send(zout.at[d ^ c ^ m], weight_out.at[:, columns(PLACE[m])], (d, r, c ^ m)) for m in (1, 2, 3)
    ]
    out_keep = pltpu.make_async_copy(zout.at[d ^ c], weight_out.at[:, columns(0)], local_sem.at[6])
    out_keep.start()
    grad_cross.wait_recv()
    grad_keep.wait()
    grads = [
        post.send(
            grad_all.at[pl.ds(0, half_rows), pl.ds(0, half)],
            grad_all.at[pl.ds(j * half_rows, half_rows), pl.ds(0, half)],
            (d ^ j, r, c),
        )
        for j in (1, 2, 3)
    ]
    grads_shared = [
        post.send(
            grad_all.at[pl.ds(0, half_rows), pl.ds(0, half)],
            grad_all.at[pl.ds(0, half_rows), pl.ds(half, half)],
            sibling,
        )
    ]

    @pl.when(d == 0)
    def _():
        kv_ref[pl.ds(0, REACH), :] = jnp.zeros((REACH, 2 * width), BF)

    @pl.when(d > 0)
    def _():
        halo.wait_recv()

    span = TILE + REACH
    for h in range(width // HEAD_DIM):
        lanes = pl.ds(h * HEAD_DIM, HEAD_DIM)
        value_lanes = pl.ds(width + h * HEAD_DIM, HEAD_DIM)

        def one(t, total, lanes=lanes, value_lanes=value_lanes):
            part = pl.ds(pl.multiple_of(t * TILE, TILE), TILE)
            to = pl.ds(pl.multiple_of(turned(t) * TILE, TILE), TILE)
            window = pl.ds(pl.multiple_of(t * TILE, TILE), span)
            scores = scores_of(q_ref[part, lanes], kv_ref[window, lanes])
            query = lax.broadcasted_iota(jnp.int32, (TILE, span), 0)
            key = lax.broadcasted_iota(jnp.int32, (TILE, span), 1)
            begin = begin_ref[part, 0:1] + (REACH - t * TILE)
            allowed = (key <= query + REACH) & (key >= begin)
            scores = jnp.where(allowed, scores, NEG_FILL)
            highest = jnp.max(scores, axis=1, keepdims=True)
            expo = jnp.exp(scores - highest)
            total_e = jnp.sum(expo, axis=1, keepdims=True)
            probability = (expo * (1.0 / total_e)).astype(BF)
            att_ref[to, lanes] = jnp.dot(
                probability, kv_ref[window, value_lanes], preferred_element_type=F32
            ).astype(BF)
            lse_ref[part, lanes] = jnp.broadcast_to(highest + jnp.log(total_e), (TILE, HEAD_DIM))
            return total

        lax.fori_loop(0, group // TILE, one, 0)

    for copy in out_cols:
        copy.wait_recv()
    out_keep.wait()

    def out_given(t, total):
        part = pl.ds(pl.multiple_of(t * TILE, TILE), TILE)
        given[part, :] = jnp.dot(
            att_ref[part, :], weight_out[:, half:], preferred_element_type=F32
        ).astype(BF)
        return total

    lax.fori_loop(0, group // TILE, out_given, 0)
    to_sibling = post.send(given, arrived, sibling)

    def out_kept(t, total):
        part = pl.ds(pl.multiple_of(t * TILE, TILE), TILE)
        wide[part, :] = jnp.dot(att_ref[part, :], weight_out[:, :half], preferred_element_type=F32)
        return total

    lax.fori_loop(0, group // TILE, out_kept, 0)
    to_sibling.wait_recv()

    def add_low(t, total):
        part = pl.ds(pl.multiple_of(t * 128, 128), 128)
        value = wide[part, :] + arrived[part, :].astype(F32)
        wide[part, :] = value
        low[part, :] = value.astype(BF)
        return total

    lax.fori_loop(0, group // 128, add_low, 0)
    pieces = [
        post.send(low.at[other_rows, columns(1)], landed.at[2], (d, r ^ 1, c ^ 2)),
        post.send(low.at[other_rows, columns(0)], landed.at[0], (d, r ^ 1, c)),
        post.send(low.at[own_rows, columns(1)], landed.at[1], (d, r, c ^ 2)),
    ]
    start_relay(1)
    for copy in pieces:
        copy.wait_recv()

    def middle(t, total):
        part = pl.ds(pl.multiple_of(t * 128, 128), 128)
        value = (
            x32[part, :] + wide[part, 0:fc] + landed[0, part, :].astype(F32)
            + landed[1, part, :].astype(F32) + landed[2, part, :].astype(F32)
        )
        mid_ref[part, :] = value
        sums[4, :, part] = as_row(jnp.sum(value * value, axis=1, keepdims=True))
        return total

    lax.fori_loop(0, rows // 128, middle, 0)
    again = [post.send(sums.at[4], sums.at[4 + m], (d, r, c ^ m)) for m in (1, 2, 3)]
    for copy in again:
        copy.wait_recv()

    def norm_two(t, total):
        part = pl.ds(pl.multiple_of(t * 128, 128), 128)
        square = sums[4, :, part] + sums[6, :, part] + sums[5, :, part] + sums[7, :, part]
        scale = lax.rsqrt(as_column(square) / D + EPSILON)
        scale_ref[part, :] = scale
        n2_ref[part, :] = (mid_ref[part, :] * scale * gain_two_ref[...]).astype(BF)
        return total

    lax.fori_loop(0, rows // 128, norm_two, 0)

    for j, copy in zip((1, 2, 3), grads):
        copy.wait_recv()
        there = pl.ds(j * half_rows, half_rows)
        grads_shared.append(
            post.send(grad_all.at[there, pl.ds(0, half)], grad_all.at[there, pl.ds(half, half)], sibling)
        )
    for copy in grads_shared:
        copy.wait_recv()
    for kind in (0, 1):
        over_y(kind).wait_send()
        over_x(kind).wait_send()

        @pl.when(core == 0)
        def _(kind=kind):
            keep_hidden(kind).wait()
            ship(kind, 0, 1, (d, r, c)).wait_recv()
            for i in (2, 3):
                relay(kind, i).wait_send()

        @pl.when(core == 1)
        def _(kind=kind):
            to_core(kind).wait_send()
            for i in range(COL):
                ship(kind, 0, i, (d, r, c)).wait_recv()

    for copy in (
        small + [grad_cross, beside, beyond, corner] + shared + outs + out_cols + grads + grads_shared
        + [to_sibling] + pieces + again
    ):
        copy.wait_send()

    @pl.when(d < DP - 1)
    def _():
        halo.wait_send()

    for n in (0, 1):
        for p in range(DP):
            @pl.when((d < DP - 1) & (p <= d))
            def _(n=n, p=p):
                line(n, p, d).wait_send()

            @pl.when((d > 0) & (p >= d))
            def _(n=n, p=p):
                line_down(n, p, d).wait_send()

            @pl.when(c != p)
            def _(n=n, p=p):
                to_column(n, p).wait_send()


SENDS = 80


def forward(x, gain_one, gain_two, lengths, query, key, value, out, gate, up, own_grad):
    rows, fc = x.shape
    group = 2 * rows
    width = out.shape[0]
    units = gate.shape[1]
    vmem = pl.BlockSpec(memory_space=pltpu.VMEM)
    smem = pl.BlockSpec(memory_space=pltpu.SMEM)
    hbm = pl.BlockSpec(memory_space=pl.ANY)

    def like(shape, dtype=BF):
        return jax.ShapeDtypeStruct(shape, dtype)

    return pl.pallas_call(
        forward_kernel,
        in_specs=[vmem] * 3 + [smem] + [vmem] * 6 + [hbm],
        out_specs=[vmem] * 12 + [hbm] * 3,
        out_shape=[
            like((group, D)),
            like((D, 3 * width)),
            like((width, D)),
            like((group, width)),
            like((REACH + group, 2 * width)),
            like((group, width)),
            like((group, width), F32),
            like((rows, fc), F32),
            like((rows, 1), F32),
            like((rows, fc)),
            like((group, 1), jnp.int32),
            like((rows, 1), F32),
            like((D, units)),
            like((D, units)),
            like((group, D)),
        ],
        scratch_shapes=[
            pltpu.VMEM((DP, fc, 3 * width), BF),
            pltpu.VMEM((DP, width, fc), BF),
            pltpu.VMEM((8, 8, rows), F32),
            pltpu.VMEM((group, 2 * fc), F32),
            pltpu.VMEM((group, 2 * fc), BF),
            pltpu.VMEM((group, 2 * fc), BF),
            pltpu.VMEM((group, 2 * fc), BF),
            pltpu.VMEM((3, rows, fc), BF),
            pltpu.VMEM((rows, fc), F32),
            pltpu.VMEM((2, fc, units), BF),
            pltpu.SemaphoreType.DMA((SENDS,)),
            pltpu.SemaphoreType.DMA((SENDS,)),
            pltpu.SemaphoreType.DMA((8,)),
        ],
        compiler_params=pltpu.CompilerParams(
            collective_id=1, has_side_effects=True, vmem_limit_bytes=60 << 20
        ),
        cost_estimate=pl.CostEstimate(
            flops=6 * group * D * width, bytes_accessed=64 << 20, transcendentals=0
        ),
    )(x, gain_one, gain_two, lengths, query, key, value, out, gate, up, own_grad)


def at(t, size):
    return pl.ds(pl.multiple_of(t * size, size), size)


def loop(count, body):
    def one(t, total):
        body(t)
        return total

    lax.fori_loop(0, count, one, 0)


def maker(send_sem, recv_sem):
    def raw(src, dst, sent, got_at, target):
        return pltpu.make_async_remote_copy(
            src_ref=src, dst_ref=dst, send_sem=send_sem.at[sent], recv_sem=recv_sem.at[got_at],
            device_id=target, device_id_type=MESH,
        )

    return raw


class LineSum:
    def __init__(self, raw, arrays, base, me):
        self.raw, self.arrays, self.base, self.me = raw, arrays, base, me

    def sem(self, n, p, down):
        return self.base + 8 * n + 4 * down + p

    def take(self, p, down, done):
        d = self.me[0]
        for n, (z, got_z) in enumerate(self.arrays):
            self.raw(z.at[p], got_z.at[p], self.sem(n, p, down), self.sem(n, p, down), self.me).wait_recv()

        @pl.when(jnp.logical_not(done))
        def _():
            for z, got_z in self.arrays:
                def one(t, z=z, got_z=got_z):
                    z[p, at(t, 64), :] = (
                        z[p, at(t, 64), :].astype(F32) + got_z[p, at(t, 64), :].astype(F32)
                    ).astype(BF)

                loop(z.shape[1] // 64, one)

    def up(self, p):
        d, r, c = self.me

        @pl.when((d > 0) & (d <= p))
        def _():
            self.take(p, 0, d == p)

        @pl.when(d < p)
        def _():
            for n, (z, got_z) in enumerate(self.arrays):
                self.raw(z.at[p], got_z.at[p], self.sem(n, p, 0), self.sem(n, p, 0), (d + 1, r, c)).start()

    def down(self, p):
        d, r, c = self.me

        @pl.when((d < DP - 1) & (d >= p))
        def _():
            self.take(p, 1, d == p)

        @pl.when(d > p)
        def _():
            slot = jnp.where(p < d - 1, p, DP)
            for n, (z, got_z) in enumerate(self.arrays):
                self.raw(z.at[p], got_z.at[slot], self.sem(n, p, 1), self.sem(n, p, 1), (d - 1, r, c)).start()

    def step(self, s):
        d = self.me[0]

        @pl.when(d < DP // 2)
        def _():
            self.up(DP - 1 - s)
            self.down(s)

        @pl.when(d >= DP // 2)
        def _():
            self.down(s)
            self.up(DP - 1 - s)

    def settle(self):
        d = self.me[0]
        for p in range(DP):
            for n, (z, got_z) in enumerate(self.arrays):
                for down, sent in ((0, d < p), (1, d > p)):
                    @pl.when(sent)
                    def _(p=p, n=n, z=z, got_z=got_z, down=down):
                        self.raw(
                            z.at[p], got_z.at[p], self.sem(n, p, down), self.sem(n, p, down), self.me
                        ).wait_send()

    def total(self, z, got_z, part):
        d = self.me[0]
        value = z[d, part, :].astype(F32)
        value = value + jnp.where(d > 0, got_z[d, part, :].astype(F32), 0.0)
        return value + jnp.where(d < DP - 1, got_z[DP, part, :].astype(F32), 0.0)


class PlaneSum:
    def __init__(self, raw, stage, got, comb, base, local_sem, local_base, me):
        self.raw, self.stage, self.got, self.comb, self.base = raw, stage, got, comb, base
        self.local_sem, self.local_base, self.me = local_sem, local_base, me
        self.kinds = range(stage.shape[0])

    def from_one(self, kind, i):
        d, r, c = self.me
        y = c // 2
        sent, base = self.base + 10 * kind + i, self.base + 10 * kind
        if i < 2:
            return self.raw(self.stage.at[kind, i], self.got.at[kind, 0], sent, base, (d, r ^ 1, 2 * y + 1 - i))
        return self.raw(
            self.stage.at[kind, i], self.comb.at[kind, 3 - i], sent, base + 3 + (3 - i), (d, r ^ 1, 2 * y)
        )

    def from_zero(self, kind, i):
        d, r, c = self.me
        sent, base = self.base + 10 * kind + i, self.base + 10 * kind
        if i == 1:
            return self.raw(self.stage.at[kind, i], self.got.at[kind, 1], sent, base + 1, (d, r, c ^ 1))
        return self.raw(
            self.stage.at[kind, i], self.got.at[kind, 2], sent, base + 2, (d, r, 2 * (1 - c // 2) + i - 2)
        )

    def home(self, kind):
        return pltpu.make_async_copy(
            self.stage.at[kind, 0], self.got.at[kind, 1], self.local_sem.at[self.local_base + kind]
        )

    def start_far(self):
        @pl.when(lax.rem(self.me[2], 2) == 1)
        def _():
            for i in (2, 3):
                for kind in self.kinds:
                    self.from_one(kind, i).start()

    def start_near(self):
        core = lax.rem(self.me[2], 2)

        @pl.when(core == 1)
        def _():
            for i in (0, 1):
                for kind in self.kinds:
                    self.from_one(kind, i).start()

        @pl.when(core == 0)
        def _():
            for kind in self.kinds:
                self.home(kind).start()
                self.from_zero(kind, 1).start()

    def combine(self, room, local_base):
        core = lax.rem(self.me[2], 2)

        @pl.when(core == 0)
        def _():
            fetches = {}
            for i in (2, 3):
                for kind in self.kinds:
                    self.raw(
                        self.stage.at[kind, i], self.comb.at[kind, i - 2], self.base,
                        self.base + 10 * kind + 3 + (i - 2), self.me,
                    ).wait_recv()
                    fetches[i, kind] = pltpu.make_async_copy(
                        self.comb.at[kind, i - 2], room(kind, i - 2),
                        self.local_sem.at[local_base + 2 * kind + i - 2],
                    )
                    fetches[i, kind].start()
            for i in (2, 3):
                for kind in self.kinds:
                    fetches[i, kind].wait()

                    def add(t, kind=kind, i=i):
                        self.stage[kind, i, at(t, 64), :] = (
                            self.stage[kind, i, at(t, 64), :].astype(F32)
                            + room(kind, i - 2)[at(t, 64), :].astype(F32)
                        ).astype(BF)

                    loop(self.stage.shape[2] // 64, add)
                    self.from_zero(kind, i).start()

    def settle(self):
        core = lax.rem(self.me[2], 2)
        for kind in self.kinds:
            base = self.base + 10 * kind
            for n in (0, 2):
                self.raw(self.stage.at[kind, 0], self.got.at[kind, n], self.base, base + n, self.me).wait_recv()

            @pl.when(core == 1)
            def _(kind=kind, base=base):
                self.raw(self.stage.at[kind, 0], self.got.at[kind, 1], self.base, base + 1, self.me).wait_recv()
                for i in range(COL):
                    self.from_one(kind, i).wait_send()

            @pl.when(core == 0)
            def _(kind=kind):
                self.home(kind).wait()
                for i in (1, 2, 3):
                    self.from_zero(kind, i).wait_send()


def middle_kernel(
    n2_ref, mid_ref, scale_ref, gain_ref, own_grad, down_ref, gate_hbm, up_hbm, grad_hbm,
    n2, dgate, dup, grad_out, gain_out, got, comb,
    wg, wu, wd, gb, own_down, gate, up, du, hidden, given, arrived, z, got_z, crossing, crossed, gn, sums, stage,
    send_sem, recv_sem, local_sem,
):
    d, r, c = (lax.axis_index(name) for name in AXES)
    me = (d, r, c)
    y, core = c // 2, lax.rem(c, 2)
    rows, fc = n2_ref.shape
    block = rows // 2
    units = own_down.shape[0]
    half = 2 * fc
    over = (((0,), (0,)), ((), ()))
    across = (((1,), (1,)), ((), ()))
    post = Post(send_sem, recv_sem)
    raw = maker(send_sem, recv_sem)
    sibling = (d, r, c ^ 1)
    others = [(a, b) for a in (0, 1) for b in range(COL) if (a, b) != (0, 0)]
    greet([(d, r ^ a, c ^ b) for a, b in others] + [(d ^ j, r, c) for j in (1, 2, 3)])

    cross = post.send(
        n2_ref.at[pl.ds(pl.multiple_of((1 - y) * block, block), block), :],
        n2.at[pl.ds(0, block), pl.ds(fc, fc)],
        (d, r, c ^ 2),
    )
    loads = [
        pltpu.make_async_copy(src, dst, local_sem.at[n])
        for n, (src, dst) in enumerate(((gate_hbm, wg), (up_hbm, wu), (grad_hbm, gb)))
    ]
    for load in loads:
        load.start()

    def cast_down(t):
        own_down[at(t, 64), :] = down_ref[at(t, 64), :].astype(BF)

    loop(units // 64, cast_down)
    first_sent = post.take(5)

    def place_of(i):
        return lax.rem(i, 2) * 2 + i // 2

    def ship(way, i, target, src=None):
        return raw(
            own_down if src is None else src, wd.at[place_of(i)], first_sent + way, first_sent + i, target
        )

    keep_down = pltpu.make_async_copy(own_down, wd.at[0], local_sem.at[3])
    to_core = ship(0, 1, sibling)
    over_y = ship(1, 2 + core, (d, r, 2 * (1 - y)))
    over_x = ship(2, 1 - core, (d, r ^ 1, 2 * y + 1))

    def relay(i):
        return ship(i + 1, 5 - i, (d, r ^ 1, 2 * y + 1), wd.at[PLACE[i]])

    over_y.start()
    over_x.start()

    @pl.when(core == 0)
    def _():
        keep_down.start()

    @pl.when(core == 1)
    def _():
        to_core.start()

    n2[0:block, 0:fc] = n2_ref[pl.ds(pl.multiple_of(y * block, block), block), :]
    cross.wait_recv()

    first_up, first_down = post.take(DP), post.take(DP)
    first_shared = post.take(DP)

    def rail(p, e):
        return n2.at[at(p ^ e, block), pl.ds(0, half)]

    def go_up(p):
        return raw(rail(p, d), rail(p, d + 1), first_up + p, first_up + p, (d + 1, r, c))

    def go_down(p):
        return raw(rail(p, d), rail(p, d - 1), first_down + p, first_up + p, (d - 1, r, c))

    def share(p):
        return raw(
            rail(p, d), n2.at[at(p ^ d, block), pl.ds(half, half)], first_shared + p, first_shared + p, sibling
        )

    def onward(p):
        @pl.when((p <= d) & (d < DP - 1))
        def _():
            go_up(p).start()

        @pl.when((p >= d) & (d > 0))
        def _():
            go_down(p).start()

        share(p).start()

    def project(p):
        share(p).wait_recv()
        part = at(p ^ d, block)
        gate[part, :] = jnp.dot(n2[part, :], wg[...], preferred_element_type=F32)
        up[part, :] = jnp.dot(n2[part, :], wu[...], preferred_element_type=F32)

    def hidden_grads(first, fresh):
        def one(t):
            part = at(t, block)
            value = jnp.zeros((block, units), F32) if fresh else du[part, :]
            for i in (first, first + 1):
                place = PLACE[i]
                value = value + lax.dot_general(
                    gb[part, place * fc : (place + 1) * fc], wd[place], across, preferred_element_type=F32
                )
            du[part, :] = value

        loop(DP, one)

    onward(d)
    turns = [
        d,
        jnp.where(d == 0, 1, d - 1),
        jnp.where(d < 2, 2, jnp.where(d == 2, 3, 1)),
        jnp.where(d < 2, 3, 0),
    ]
    inner = (d == 1) | (d == 2)

    def arrival(n):
        raw(rail(turns[n], d), rail(turns[n], d), first_up, first_up + turns[n], me).wait_recv()
        onward(turns[n])

    for load in loads:
        load.wait()
    arrival(1)

    @pl.when(inner)
    def _():
        arrival(2)

    project(turns[0])

    @pl.when(core == 0)
    def _():
        keep_down.wait()
        ship(0, 1, me).wait_recv()
        for i in (2, 3):
            ship(0, i, me).wait_recv()
            relay(i).start()

    project(turns[1])

    @pl.when(jnp.logical_not(inner))
    def _():
        arrival(2)

    @pl.when(inner)
    def _():
        arrival(3)

    @pl.when(core == 1)
    def _():
        for i in (0, 1):
            ship(0, i, me).wait_recv()

    hidden_grads(0, True)
    project(turns[2])

    @pl.when(jnp.logical_not(inner))
    def _():
        arrival(3)

    project(turns[3])

    @pl.when(core == 1)
    def _():
        for i in (2, 3):
            ship(0, i, me).wait_recv()

    hidden_grads(2, False)

    def units_of(t):
        part = at(t, 64)
        g, u, grad = gate[part, :], up[part, :], du[part, :]
        sigmoid = 1.0 / (1.0 + jnp.exp(-g))
        silu = g * sigmoid
        hidden[part, :] = (silu * u).astype(BF)
        dgate[part, :] = (grad * u * sigmoid * (1.0 + g * (1.0 - sigmoid))).astype(BF)
        dup[part, :] = (grad * silu).astype(BF)

    loop(2 * rows // 64, units_of)

    def back(part, cols):
        return lax.dot_general(
            dgate[part, :], wg[cols, :], across, preferred_element_type=F32
        ) + lax.dot_general(dup[part, :], wu[cols, :], across, preferred_element_type=F32)

    def down_part(i):
        def down_grad(t):
            place = PLACE[i]
            stage[0, i, at(t, TILE), :] = lax.dot_general(
                hidden[:, at(t, TILE)], gb[:, place * fc : (place + 1) * fc], over, preferred_element_type=F32
            ).astype(BF)

        loop(units // TILE, down_grad)

    owners = PlaneSum(raw, stage, got, comb, post.take(10), local_sem, 4, me)
    down_part(2)
    down_part(3)
    owners.start_far()

    def given_part(t):
        given[at(t, block), :] = back(at(t, block), slice(half, None)).astype(BF)

    loop(DP, given_part)
    to_sibling = post.send(given, arrived, sibling)
    down_part(0)
    down_part(1)
    owners.start_near()
    to_sibling.wait_recv()

    def kept_part(t):
        part = at(t, block)
        z[t ^ d] = (back(part, slice(0, half)) + arrived[part, :].astype(F32)).astype(BF)

    loop(DP, kept_part)
    line = LineSum(raw, ((z, got_z),), post.take(8), me)
    line.step(0)
    line.step(1)
    owners.combine(lambda kind, j: wg.at[pl.ds(0, units), pl.ds(j * fc, fc)], 5)
    line.step(2)

    def settle_rows(t):
        part = at(t, 64)
        total = line.total(z, got_z, part)
        gn[pl.ds(pl.multiple_of(y * block + t * 64, 64), 64), :] = total[:, 0:fc]
        crossing[part, :] = total[:, fc:].astype(BF)

    loop(block // 64, settle_rows)
    other = post.send(crossing, crossed, (d, r, c ^ 2))
    other.wait_recv()

    def other_rows(t):
        gn[pl.ds(pl.multiple_of((1 - y) * block + t * 64, 64), 64), :] = crossed[at(t, 64), :].astype(F32)

    loop(block // 64, other_rows)

    def inner_sum(t):
        part = at(t, 128)
        inner = gn[part, :] * gain_ref[...] * mid_ref[part, :]
        sums[0, :, part] = as_row(jnp.sum(inner, axis=1, keepdims=True))

    loop(rows // 128, inner_sum)
    small = [post.send(sums.at[0], sums.at[m], (d, r, c ^ m)) for m in (1, 2, 3)]

    def gain_sum(t, total):
        part = at(t, 128)
        value = gn[part, :] * mid_ref[part, :] * scale_ref[part, :]
        return total + jnp.sum(value, axis=0, keepdims=True)

    gain_out[...] = lax.fori_loop(0, rows // 128, gain_sum, jnp.zeros((1, fc), F32))
    for copy in small:
        copy.wait_recv()

    def finish(t):
        part = at(t, 128)
        inner = as_column(sums[0, :, part] + sums[2, :, part] + sums[1, :, part] + sums[3, :, part])
        scale = scale_ref[part, :]
        grad_out[part, :] = (
            own_grad[part, :].astype(F32) + scale * (gn[part, :] * gain_ref[...])
            - mid_ref[part, :] * (scale * scale * scale * inner / D)
        )

    loop(rows // 128, finish)

    owners.settle()
    line.settle()
    for copy in [cross, to_sibling, other] + small:
        copy.wait_send()
    over_y.wait_send()
    over_x.wait_send()

    @pl.when(core == 0)
    def _():
        for i in (2, 3):
            relay(i).wait_send()

    @pl.when(core == 1)
    def _():
        to_core.wait_send()

    for p in range(DP):
        share(p).wait_send()

        @pl.when((p <= d) & (d < DP - 1))
        def _(p=p):
            go_up(p).wait_send()

        @pl.when((p >= d) & (d > 0))
        def _(p=p):
            go_down(p).wait_send()


def middle(n2, mid, scale, gain, own_grad, down, gate, up, grad_all):
    rows, fc = n2.shape
    group = 2 * rows
    block = rows // 2
    units = down.shape[0]
    vmem = pl.BlockSpec(memory_space=pltpu.VMEM)
    hbm = pl.BlockSpec(memory_space=pl.ANY)

    def like(shape, dtype=BF):
        return jax.ShapeDtypeStruct(shape, dtype)

    return pl.pallas_call(
        middle_kernel,
        in_specs=[vmem] * 6 + [hbm] * 3,
        out_specs=[vmem] * 5 + [hbm] * 2,
        out_shape=[
            like((group, D)),
            like((group, units)),
            like((group, units)),
            like((rows, fc), F32),
            like((1, fc), F32),
            like((1, 3, units, fc)),
            like((1, 2, units, fc)),
        ],
        scratch_shapes=[
            pltpu.VMEM((D, units), BF),
            pltpu.VMEM((D, units), BF),
            pltpu.VMEM((COL, units, fc), BF),
            pltpu.VMEM((group, D), BF),
            pltpu.VMEM((units, fc), BF),
            pltpu.VMEM((group, units), F32),
            pltpu.VMEM((group, units), F32),
            pltpu.VMEM((group, units), F32),
            pltpu.VMEM((group, units), BF),
            pltpu.VMEM((group, 2 * fc), BF),
            pltpu.VMEM((group, 2 * fc), BF),
            pltpu.VMEM((DP, block, 2 * fc), BF),
            pltpu.VMEM((DP + 1, block, 2 * fc), BF),
            pltpu.VMEM((block, fc), BF),
            pltpu.VMEM((block, fc), BF),
            pltpu.VMEM((rows, fc), F32),
            pltpu.VMEM((4, 8, rows), F32),
            pltpu.VMEM((1, COL, units, fc), BF),
            pltpu.SemaphoreType.DMA((SENDS,)),
            pltpu.SemaphoreType.DMA((SENDS,)),
            pltpu.SemaphoreType.DMA((8,)),
        ],
        compiler_params=pltpu.CompilerParams(
            collective_id=3, has_side_effects=True, vmem_limit_bytes=62 << 20
        ),
        cost_estimate=pl.CostEstimate(
            flops=14 * group * D * units, bytes_accessed=48 << 20, transcendentals=group * units
        ),
    )(n2, mid, scale, gain, own_grad, down, gate, up, grad_all)


POSTS = 112


def backward_kernel(
    x_ref, gain_ref, scale_ref, mid_ref, gain_two_ref, weight_in, weight_out, q_ref, kv_ref, att_ref, lse_ref,
    begin_ref, normed_hbm, n2_hbm, dgate_hbm, dup_hbm,
    tokens_out, in_out, out_out, gains_out, got, comb,
    n1, n2, dgu, dball, dotted, dproj, acc, spill, spilled, stage, own_f, arrived, landed,
    zq, zo, zkv, rq, ro, rkv, sums, gsum,
    send_sem, recv_sem, local_sem,
):
    d, r, c = (lax.axis_index(name) for name in AXES)
    y, core = c // 2, lax.rem(c, 2)
    rows, fc = x_ref.shape
    group = 2 * rows
    width = q_ref.shape[1]
    units = dgate_hbm.shape[1]
    half = 2 * fc
    tiles = group // TILE
    over = (((0,), (0,)), ((), ()))
    across = (((1,), (1,)), ((), ()))
    post = Post(send_sem, recv_sem)
    loads = [
        pltpu.make_async_copy(src, dst, local_sem.at[n])
        for n, (src, dst) in enumerate((
            (n2_hbm, n2),
            (dgate_hbm, dgu.at[pl.ds(0, group), :]),
            (dup_hbm, dgu.at[pl.ds(group, group), :]),
            (normed_hbm, n1),
        ))
    ]
    for load in loads:
        load.start()

    others = [(a, b) for a in (0, 1) for b in range(COL) if (a, b) != (0, 0)]
    greet(
        [(d, r ^ a, c ^ b) for a, b in others]
        + [(d ^ j, r ^ a, c) for j in (1, 2, 3) for a in (0, 1)]
    )

    def columns(place):
        return pl.ds(place * fc, fc)

    def turned(t):
        return lax.rem(t + 2 * r, tiles)

    raw = maker(send_sem, recv_sem)
    me = (d, r, c)
    sibling = (d, r, c ^ 1)
    own_rows, other_rows = pl.ds(0, rows), pl.ds(rows, rows)
    def round_mid(t):
        dball[at(t, 128), 0:fc] = mid_ref[at(t, 128), :].astype(BF)

    loop(rows // 128, round_mid)
    own_block = dball.at[own_rows, columns(0)]
    beside = post.send(own_block, dball.at[other_rows, columns(0)], (d, r ^ 1, c))
    beyond = post.send(own_block, dball.at[own_rows, columns(1)], (d, r, c ^ 2))
    corner = post.send(own_block, dball.at[other_rows, columns(1)], (d, r ^ 1, c ^ 2))
    shared = [post.send(own_block, dball.at[own_rows, columns(2)], sibling)]

    for load in loads[:3]:
        load.wait()
    owners = PlaneSum(raw, stage, got, comb, post.take(20), local_sem, 4, me)

    def hidden_part(i):
        for kind in (0, 1):
            def hidden_grad(t, kind=kind):
                left = n2[:, pl.ds(pl.multiple_of(PLACE[i] * fc + t * TILE, TILE), TILE)]
                stage[kind, i, at(t, TILE), :] = lax.dot_general(
                    left, dgu[pl.ds(kind * group, group), :], over, preferred_element_type=F32
                ).astype(BF)

            loop(fc // TILE, hidden_grad)

    hidden_part(2)
    hidden_part(3)
    owners.start_far()
    hidden_part(0)
    hidden_part(1)
    loads[3].wait()

    for copy, where, place in ((beside, other_rows, 0), (beyond, own_rows, 1), (corner, other_rows, 1)):
        copy.wait_recv()
        shared.append(post.send(dball.at[where, columns(place)], dball.at[where, columns(place + 2)], sibling))
    for copy in shared:
        copy.wait_recv()

    def head_grad(t):
        dotted[at(turned(t), TILE), :] = lax.dot_general(
            dball[at(t, TILE), :], weight_out[...], across, preferred_element_type=F32
        ).astype(BF)

    loop(tiles, head_grad)
    span = TILE + REACH
    scale = HEAD_DIM ** (-0.5)
    spills = []
    for h in range(width // HEAD_DIM):
        lanes = pl.ds(h * HEAD_DIM, HEAD_DIM)
        value_lanes = pl.ds(width + h * HEAD_DIM, HEAD_DIM)

        def clear(t, lanes=lanes, value_lanes=value_lanes):
            acc[at(t, TILE), lanes] = jnp.zeros((TILE, HEAD_DIM), F32)
            acc[at(t, TILE), value_lanes] = jnp.zeros((TILE, HEAD_DIM), F32)

        loop((group + REACH) // TILE, clear)

        def one(t, lanes=lanes, value_lanes=value_lanes):
            part = at(t, TILE)
            window = pl.ds(pl.multiple_of(t * TILE, TILE), span)
            query, key = q_ref[part, lanes], kv_ref[window, lanes]
            grad = dotted[part, lanes]
            scores = scores_of(query, key)
            query_at = lax.broadcasted_iota(jnp.int32, (TILE, span), 0)
            key_at = lax.broadcasted_iota(jnp.int32, (TILE, span), 1)
            begin = begin_ref[part, 0:1] + (REACH - t * TILE)
            allowed = (key_at <= query_at + REACH) & (key_at >= begin)
            scores = jnp.where(allowed, scores - lse_ref[part, lanes][:, 0:1], NEG_FILL)
            probability = jnp.exp(scores)
            grad_soft = lax.dot_general(grad, kv_ref[window, value_lanes], across, preferred_element_type=F32)
            inner = jnp.sum(probability * grad_soft, axis=1, keepdims=True)
            grad_scores = (probability * (grad_soft - inner)).astype(BF)
            dproj[at(turned(t), TILE), lanes] = (
                jnp.dot(grad_scores, key, preferred_element_type=F32) * scale
            ).astype(BF)
            acc[window, lanes] += lax.dot_general(grad_scores, query, over, preferred_element_type=F32) * scale
            acc[window, value_lanes] += lax.dot_general(
                probability.astype(BF), grad, over, preferred_element_type=F32
            )

        loop(tiles, one)

        def round_spill(t, h=h, lanes=lanes, value_lanes=value_lanes):
            spill[h, at(t, TILE), 0:HEAD_DIM] = acc[at(t, TILE), lanes].astype(BF)
            spill[h, at(t, TILE), HEAD_DIM:] = acc[at(t, TILE), value_lanes].astype(BF)

        loop(REACH // TILE, round_spill)
        copy = post.ready(spill.at[h], spilled.at[h], (lax.rem(d + DP - 1, DP), r, c))
        spills.append(copy)

        @pl.when(d > 0)
        def _(copy=copy):
            copy.start()

    sent_out = [None] + [post.take(1) for _ in (1, 2, 3)]
    outs = []
    for place, m in enumerate((0, 2, 1, 3)):
        value = lax.dot_general(
            att_ref[...], dball[:, place * fc : (place + 1) * fc], over, preferred_element_type=F32
        ).astype(BF)
        if m == 0:
            zo[c] = value
        else:
            n2[(m - 1) * width : m * width, half : half + fc] = value
            staged = n2.at[pl.ds((m - 1) * width, width), pl.ds(half, fc)]
            copy = raw(staged, zo.at[c], sent_out[m], sent_out[m], (d, r, c ^ m))
            copy.start()
            outs.append(copy)

    def attention_grads(first_lane, lane_count, dest):
        lanes = slice(first_lane, first_lane + lane_count)
        slots = [None] + [post.take(1) for _ in (1, 2, 3)]
        copies = []
        for place, m in enumerate((0, 2, 1, 3)):
            def tile(t, place=place, m=m):
                left = n1[:, pl.ds(pl.multiple_of(place * fc + t * TILE, TILE), TILE)]
                value = lax.dot_general(left, dproj[:, lanes], over, preferred_element_type=F32).astype(BF)
                if m == 0:
                    dest[c, at(t, TILE), :] = value
                else:
                    dgu[pl.ds(pl.multiple_of(place * fc + t * TILE, TILE), TILE), lanes] = value

            loop(fc // TILE, tile)
            if m:
                copy = raw(
                    dgu.at[pl.ds(place * fc, fc), pl.ds(first_lane, lane_count)], dest.at[c],
                    slots[m], slots[m], (d, r, c ^ m),
                )
                copy.start()
                copies.append(copy)
        return copies

    qs = attention_grads(0, width, zq)

    @pl.when(d < DP - 1)
    def _():
        for copy in spills:
            copy.wait_recv()

    @pl.when(d == DP - 1)
    def _():
        spilled[...] = jnp.zeros_like(spilled)

    for h in range(width // HEAD_DIM):
        for which in (0, 1):
            lanes = pl.ds(which * width + h * HEAD_DIM, HEAD_DIM)
            out_lanes = pl.ds((1 + which) * width + h * HEAD_DIM, HEAD_DIM)

            def whole(t, h=h, which=which, lanes=lanes, out_lanes=out_lanes):
                total = acc[pl.ds(pl.multiple_of(REACH + t * TILE, TILE), TILE), lanes]
                extra = spilled[
                    h, at(jnp.maximum(t - 1, 0), TILE), which * HEAD_DIM : (which + 1) * HEAD_DIM
                ].astype(F32)
                total = total + jnp.where(t > 0, extra, 0.0)
                dproj[at(turned(t), TILE), out_lanes] = total.astype(BF)

            loop(tiles, whole)

    kvs = attention_grads(width, 2 * width, zkv)

    def given_part(t):
        n2[at(t, TILE), 0:half] = lax.dot_general(
            dproj[at(t, TILE), :], weight_in[half:, :], across, preferred_element_type=F32
        ).astype(BF)

    loop(tiles, given_part)
    to_sibling = post.send(n2.at[:, pl.ds(0, half)], arrived, sibling)

    to_sibling.wait_recv()
    for copy in outs:
        copy.wait_send()

    def kept_part(t):
        part = at(t, TILE)
        value = lax.dot_general(
            dproj[part, :], weight_in[:half, :], across, preferred_element_type=F32
        ) + arrived[part, :].astype(F32)
        n2[part, half:] = value.astype(BF)

        @pl.when(t < rows // TILE)
        def _():
            own_f[part, :] = value[:, 0:fc]

    loop(tiles, kept_part)

    def low(where, place):
        return n2.at[where, pl.ds(half + place * fc, fc)]

    pieces = [
        post.send(low(other_rows, 1), landed.at[2], (d, r ^ 1, c ^ 2)),
        post.send(low(other_rows, 0), landed.at[0], (d, r ^ 1, c)),
        post.send(low(own_rows, 1), landed.at[1], (d, r, c ^ 2)),
    ]

    owners.start_near()
    owners.combine(lambda kind, j: n1.at[pl.ds(j * fc, fc), pl.ds(kind * units, units)], 0)

    def finish(line, z, got_z, dest, lanes):
        def one(t):
            dest[at(t, 64), lanes] = line.total(z, got_z, at(t, 64))

        loop(z.shape[1] // 64, one)

    for copy in outs + qs:
        copy.wait_recv()
    first_line = post.take(24)
    line_a = LineSum(raw, ((zq, rq), (zo, ro)), first_line, me)
    for s in range(DP - 1):
        line_a.step(s)

    for copy in kvs:
        copy.wait_recv()
    line_b = LineSum(raw, ((zkv, rkv),), first_line + 16, me)
    for s in range(DP - 1):
        line_b.step(s)
    for copy in pieces:
        copy.wait_recv()

    def inner_sum(t):
        part = at(t, 128)
        value = own_f[part, :]
        for n in range(3):
            value = value + landed[n, part, :].astype(F32)
        own_f[part, :] = value
        inner = value * gain_ref[...] * x_ref[part, :].astype(F32)
        sums[0, :, part] = as_row(jnp.sum(inner, axis=1, keepdims=True))

    loop(rows // 128, inner_sum)
    small = [post.send(sums.at[0], sums.at[m], (d, r, c ^ m)) for m in (1, 2, 3)]
    seat = ROW * d + r
    gain_part = jnp.zeros((1, fc), F32)

    def gain_sum(t, total):
        part = at(t, 128)
        value = own_f[part, :] * x_ref[part, :].astype(F32) * scale_ref[part, :]
        return total + jnp.sum(value, axis=0, keepdims=True)

    gain_part = lax.fori_loop(0, rows // 128, gain_sum, gain_part)
    gsum[seat, 0:1, :] = gain_part
    gsum[seat, 1:2, :] = gain_two_ref[...]
    gsum[seat, 2:8, :] = jnp.zeros((6, fc), F32)
    gain_sent = post.take(8)
    gain_got = gain_sent

    def gain_copy(n, j, a):
        return raw(gsum.at[seat], gsum.at[seat], gain_sent + n, gain_got + seat, (d ^ j, r ^ a, c))

    far = [(j, a) for j in range(DP) for a in (0, 1) if (j, a) != (0, 0)]
    for n, (j, a) in enumerate(far):
        gain_copy(n, j, a).start()
    finish(line_a, zq, rq, in_out, slice(0, width))
    finish(line_a, zo, ro, out_out, slice(0, fc))
    finish(line_b, zkv, rkv, in_out, slice(width, 3 * width))
    for copy in small:
        copy.wait_recv()

    def finish_tokens(t):
        part = at(t, 128)
        inner = as_column(sums[0, :, part] + sums[2, :, part] + sums[1, :, part] + sums[3, :, part])
        scale_rows = scale_ref[part, :]
        value = x_ref[part, :].astype(F32)
        tokens_out[part, :] = (
            mid_ref[part, :] + scale_rows * (own_f[part, :] * gain_ref[...])
            - value * (scale_rows * scale_rows * scale_rows * inner / D)
        )

    loop(rows // 128, finish_tokens)

    for e in range(2 * DP):
        @pl.when(e != seat)
        def _(e=e):
            raw(gsum.at[e], gsum.at[e], gain_sent, gain_got + e, me).wait_recv()

    gains = gsum[0]
    for e in range(1, 2 * DP):
        gains = gains + gsum[e]
    gains_out[...] = gains

    owners.settle()
    line_a.settle()
    line_b.settle()
    for copy in [beside, beyond, corner] + shared + qs + kvs + [to_sibling] + pieces + small:
        copy.wait_send()
    for n, (j, a) in enumerate(far):
        gain_copy(n, j, a).wait_send()

    @pl.when(d > 0)
    def _():
        for copy in spills:
            copy.wait_send()


def backward(x, gain, scale, mid, gain_two, weight_in, weight_out, q, kv, att, lse, begin, normed, n2, dgate, dup):
    rows, fc = x.shape
    group = 2 * rows
    width = q.shape[1]
    units = dgate.shape[1]
    vmem = pl.BlockSpec(memory_space=pltpu.VMEM)
    hbm = pl.BlockSpec(memory_space=pl.ANY)

    def like(shape, dtype=BF):
        return jax.ShapeDtypeStruct(shape, dtype)

    return pl.pallas_call(
        backward_kernel,
        in_specs=[vmem] * 12 + [hbm] * 4,
        out_specs=[vmem] * 4 + [hbm] * 2,
        out_shape=[
            like((rows, fc), F32),
            like((fc, 3 * width), F32),
            like((width, fc), F32),
            like((8, fc), F32),
            like((2, 3, fc, units)),
            like((2, 2, fc, units)),
        ],
        scratch_shapes=[
            pltpu.VMEM((group, D), BF),
            pltpu.VMEM((group, D), BF),
            pltpu.VMEM((2 * group, units), BF),
            pltpu.VMEM((group, D), BF),
            pltpu.VMEM((group, width), BF),
            pltpu.VMEM((group, 3 * width), BF),
            pltpu.VMEM((group + REACH, 2 * width), F32),
            pltpu.VMEM((width // HEAD_DIM, REACH, 2 * HEAD_DIM), BF),
            pltpu.VMEM((width // HEAD_DIM, REACH, 2 * HEAD_DIM), BF),
            pltpu.VMEM((2, COL, fc, units), BF),
            pltpu.VMEM((rows, fc), F32),
            pltpu.VMEM((group, 2 * fc), BF),
            pltpu.VMEM((3, rows, fc), BF),
            pltpu.VMEM((DP, fc, width), BF),
            pltpu.VMEM((DP, width, fc), BF),
            pltpu.VMEM((DP, fc, 2 * width), BF),
            pltpu.VMEM((DP + 1, fc, width), BF),
            pltpu.VMEM((DP + 1, width, fc), BF),
            pltpu.VMEM((DP + 1, fc, 2 * width), BF),
            pltpu.VMEM((4, 8, rows), F32),
            pltpu.VMEM((2 * DP, 8, fc), F32),
            pltpu.SemaphoreType.DMA((POSTS,)),
            pltpu.SemaphoreType.DMA((POSTS,)),
            pltpu.SemaphoreType.DMA((8,)),
        ],
        compiler_params=pltpu.CompilerParams(
            collective_id=2, has_side_effects=True, vmem_limit_bytes=62 << 20
        ),
        cost_estimate=pl.CostEstimate(
            flops=12 * group * D * width + 4 * group * D * units, bytes_accessed=64 << 20, transcendentals=0
        ),
    )(x, gain, scale, mid, gain_two, weight_in, weight_out, q, kv, att, lse, begin, normed, n2, dgate, dup)


def on_small_mesh(
    tokens,
    cotangent,
    query_master,
    key_master,
    value_master,
    out_master,
    gate_master,
    up_master,
    down_master,
    attn_gain,
    ffn_gain,
    lengths,
    permutation,
):
    del permutation
    units = gate_master.shape[1]
    width = query_master.shape[1]
    (
        normed_one, weight_in, weight_out, q, key_value, own_attended, lse, mid, scale_two,
        n2, begin, scale_one, weight_gate, weight_up, grad_all,
    ) = forward(
        tokens, attn_gain[None, :], ffn_gain[None, :], lengths, query_master, key_master,
        value_master, out_master, gate_master, up_master, cotangent,
    )
    normed_two, grad_gate, grad_up, grad_mid, gain_two_part, got_down, _ = middle(
        n2, mid, scale_two, ffn_gain[None, :], cotangent, down_master, weight_gate, weight_up, grad_all
    )
    grad_tokens, grad_in, grad_out, gains, got, _ = backward(
        tokens, attn_gain[None, :], scale_one, grad_mid, gain_two_part, weight_in, weight_out, q,
        key_value, own_attended, lse, begin, normed_one, normed_two, grad_gate, grad_up,
    )
    got = got.astype(F32)
    grad_hidden_own = got[:, 0] + got[:, 1] + got[:, 2]
    got_down = got_down[0].astype(F32)
    return (
        grad_tokens,
        grad_in[:, :width],
        grad_in[:, width : 2 * width],
        grad_in[:, 2 * width :],
        grad_out,
        grad_hidden_own[0],
        grad_hidden_own[1],
        got_down[0] + got_down[1] + got_down[2],
        gains[0],
        gains[1],
    )


def solution(mesh):
    placed = (
        P(("dp", "row"), "col"),
        P(("dp", "row"), "col"),
        P("col", ("row", "dp")),
        P("col", ("row", "dp")),
        P("col", ("row", "dp")),
        P(("row", "dp"), "col"),
        P("col", ("row", "dp")),
        P("col", ("row", "dp")),
        P(("row", "dp"), "col"),
        P("col"),
        P("col"),
        P(),
        P(),
    )
    small = tuple(mesh.shape[name] for name in AXES) == (DP, ROW, COL)
    return jax.shard_map(
        on_small_mesh if small else on_any_mesh,
        mesh=mesh,
        in_specs=placed,
        out_specs=(
            P(("dp", "row"), "col"),
            P("col", ("row", "dp")),
            P("col", ("row", "dp")),
            P("col", ("row", "dp")),
            P(("row", "dp"), "col"),
            P("col", ("row", "dp")),
            P("col", ("row", "dp")),
            P(("row", "dp"), "col"),
            P("col"),
            P("col"),
        ),
        check_vma=False,
    )
```

```python
import functools

import jax
import jax.numpy as jnp
from jax import lax
from jax.experimental import pallas as pl
from jax.experimental.pallas import tpu as pltpu
from jax.sharding import PartitionSpec as P

D = 2048
HEAD_DIM = 128


EPSILON = 1e-06
NEG_FILL = -1e30
AXES = ("dp", "row", "col")
DP, ROW, COL = 4, 2, 4
REACH = 768
BF = jnp.bfloat16
F32 = jnp.float32


def running_sum(lengths):
    count = lengths.shape[0]
    earlier = jnp.arange(count)[:, None] <= jnp.arange(count)[None, :]
    return jnp.sum(jnp.where(earlier, lengths[:, None], 0), axis=0)

def make_picker(wanted, carried, pieces):
    amount = pieces[0].shape[0]
    inside = (wanted >= 0) & (wanted < amount)
    chosen = jnp.clip(wanted, 0, amount - 1)
    return tuple(
        (
            jnp.where(inside[:, None], jnp.take(shard_rows, chosen, axis=0), current)
            for shard_rows, current in zip(pieces, carried)
        )
    )


def sequence_marks(permutation, lengths, first_slot, amount):
    source = lax.dynamic_slice_in_dim(permutation, first_slot, amount)
    seq_ends = running_sum(lengths)
    passed = seq_ends[None, :] <= source[:, None]
    member = jnp.sum(passed.astype(jnp.int32), axis=1)
    begins = jnp.max(jnp.where(passed, seq_ends[None, :], 0), axis=1)
    return (member, source - begins)


def col_total(values):
    return lax.psum(jnp.sum(values, axis=1), "col")


def row_gather(values):
    return lax.all_gather(values, "row", axis=0, tiled=True)


def col_gather(values):
    return lax.all_gather(values, "col", axis=0, tiled=True)


def key_gather(keys_here, values_here):
    return (
        lax.all_gather(keys_here, "col", axis=0, tiled=True),
        lax.all_gather(values_here, "col", axis=0, tiled=True),
    )


def multiply(row_block, weight, transpose_right):
    if transpose_right:
        return lax.dot_general(
            row_block, weight, (((1,), (1,)), ((), ())), preferred_element_type=jnp.float32
        )
    return jnp.dot(row_block, weight, preferred_element_type=jnp.float32)


def outer_sum(left_rows, right_rows):
    return lax.dot_general(
        left_rows, right_rows, (((0,), (0,)), ((), ())), preferred_element_type=jnp.float32
    )


def col_reduce(spread, weight, transpose_right):
    return lax.psum_scatter(
        multiply(spread, weight, transpose_right), "col", scatter_dimension=0, tiled=True
    )


def row_reduce(spread, weight, transpose_right):
    return lax.psum_scatter(
        multiply(spread, weight, transpose_right), "row", scatter_dimension=0, tiled=True
    )


def visible(query_member, query_position, member, position):
    same = query_member[:, None] == member[None, :]
    behind = position[None, :] <= query_position[:, None]
    return same & behind


def attend_scores(query_block, key_all, allowed):
    scores = jnp.einsum(
        "qhd,khd->hqk", query_block, key_all, preferred_element_type=jnp.float32
    ) * HEAD_DIM ** (-0.5)
    return jnp.where(allowed[None, :, :], scores, NEG_FILL)


def norm_back(grad_normed, inputs_f, scale_rows, gain):
    gain_part = jnp.sum(grad_normed * inputs_f * scale_rows[:, None], axis=0)
    scaled = grad_normed * gain[None, :]
    inner = col_total(scaled * inputs_f)
    grad_inputs = scale_rows[:, None] * scaled - inputs_f * (scale_rows**3 * inner / D)[:, None]
    return (grad_inputs, gain_part)


def on_any_mesh(
    tokens,
    cotangent,
    query_master,
    key_master,
    value_master,
    out_master,
    gate_master,
    up_master,
    down_master,
    attn_gain,
    ffn_gain,
    lengths,
    permutation,
):
    own_rows = tokens.shape[0]
    group_rows = own_rows * lax.axis_size("row")
    quarter = group_rows // lax.axis_size("col")
    device_slot = lax.axis_index(("dp", "row"))
    group_slot = lax.axis_index("dp")
    col_slot = lax.axis_index("col")
    own_sources = lax.dynamic_slice_in_dim(permutation, device_slot * own_rows, own_rows)
    own_tokens, own_cotangent = make_picker(
        own_sources,
        (jnp.zeros_like(tokens), jnp.zeros_like(cotangent)),
        (
            lax.all_gather(tokens, ("dp", "row"), axis=0, tiled=True),
            lax.all_gather(cotangent, ("dp", "row"), axis=0, tiled=True),
        ),
    )
    masters = tuple(
        (
            matrix.astype(jnp.bfloat16)
            for matrix in (
                query_master,
                key_master,
                value_master,
                out_master,
                gate_master,
                up_master,
                down_master,
            )
        )
    )
    query_weight, key_weight, value_weight, out_weight, gate_weight, up_weight, down_weight = (
        lax.all_gather(masters[0], "dp", axis=1, tiled=True),
        lax.all_gather(masters[1], "dp", axis=1, tiled=True),
        lax.all_gather(masters[2], "dp", axis=1, tiled=True),
        lax.all_gather(masters[3], "dp", axis=0, tiled=True),
        lax.all_gather(masters[4], "dp", axis=1, tiled=True),
        lax.all_gather(masters[5], "dp", axis=1, tiled=True),
        lax.all_gather(masters[6], "dp", axis=0, tiled=True),
    )
    attention_in = jnp.concatenate([query_weight, key_weight, value_weight], axis=1)
    feedforward_in = jnp.concatenate([gate_weight, up_weight], axis=1)
    width_row = query_weight.shape[1]
    heads_row = width_row // HEAD_DIM
    hidden_row = gate_weight.shape[1]
    member, position = sequence_marks(permutation, lengths, group_slot * group_rows, group_rows)
    query_member = lax.dynamic_slice_in_dim(member, col_slot * quarter, quarter)
    query_position = lax.dynamic_slice_in_dim(position, col_slot * quarter, quarter)
    block_rows = min(512, quarter)
    block_count = quarter // block_rows
    residual_in = own_tokens.astype(jnp.float32)
    scale_one = lax.rsqrt(col_total(residual_in * residual_in) / D + EPSILON)
    normed_one = (residual_in * scale_one[:, None] * attn_gain[None, :]).astype(jnp.bfloat16)
    spread_one = row_gather(normed_one)
    projected = col_reduce(spread_one, attention_in, False).astype(jnp.bfloat16)
    queries = projected[:, :width_row].reshape(quarter, heads_row, HEAD_DIM)
    keys_here = projected[:, width_row : 2 * width_row]
    values_here = projected[:, 2 * width_row :]
    key_flat, value_flat = key_gather(keys_here, values_here)
    key_all = key_flat.reshape(group_rows, heads_row, HEAD_DIM)
    value_all = value_flat.reshape(group_rows, heads_row, HEAD_DIM)

    def block_mask(first_row):
        return visible(
            lax.dynamic_slice_in_dim(query_member, first_row, block_rows),
            lax.dynamic_slice_in_dim(query_position, first_row, block_rows),
            member,
            position,
        )

    def forward_block(block_id):
        first_row = block_id * block_rows
        query_block = lax.dynamic_slice_in_dim(queries, first_row, block_rows, 0)
        scores = attend_scores(query_block, key_all, block_mask(first_row))
        highest = jnp.max(scores, axis=2, keepdims=True)
        totals = jnp.sum(jnp.exp(scores - highest), axis=2, keepdims=True)
        log_total = highest + jnp.log(totals)
        probability = jnp.exp(scores - log_total)
        output = jnp.einsum(
            "hqk,khd->qhd",
            probability.astype(jnp.bfloat16),
            value_all,
            preferred_element_type=jnp.float32,
        )
        return (output.astype(jnp.bfloat16).reshape(block_rows, width_row), log_total[:, :, 0])

    blocks_out, log_totals = lax.map(forward_block, jnp.arange(block_count, dtype=jnp.int32))
    attended = blocks_out.reshape(quarter, width_row)
    spread_attn = col_gather(attended)
    midway = residual_in + row_reduce(spread_attn, out_weight, False)
    scale_two = lax.rsqrt(col_total(midway * midway) / D + EPSILON)
    normed_two = (midway * scale_two[:, None] * ffn_gain[None, :]).astype(jnp.bfloat16)
    spread_two = row_gather(normed_two)
    gate_and_up = col_reduce(spread_two, feedforward_in, False)
    gate_value = gate_and_up[:, :hidden_row]
    up_value = gate_and_up[:, hidden_row:]
    sigmoid_gate = jax.nn.sigmoid(gate_value)
    hidden = (gate_value * sigmoid_gate * up_value).astype(jnp.bfloat16)
    grad_output = own_cotangent.astype(jnp.float32)
    spread_down = row_gather(own_cotangent)
    grad_hidden = col_reduce(spread_down, down_weight, True)
    spread_hidden = col_gather(hidden)
    grad_down = outer_sum(spread_hidden, spread_down)
    grad_gate_value = (
        grad_hidden * up_value * sigmoid_gate * (1.0 + gate_value * (1.0 - sigmoid_gate))
    ).astype(jnp.bfloat16)
    grad_up_value = (grad_hidden * gate_value * sigmoid_gate).astype(jnp.bfloat16)
    spread_gate_up = col_gather(jnp.concatenate([grad_gate_value, grad_up_value], axis=1))
    grad_normed_two = row_reduce(spread_gate_up, feedforward_in, True)
    spread_two = row_gather(normed_two)
    grad_feedforward = outer_sum(spread_two, spread_gate_up)
    grad_mid_norm, gain_two_part = norm_back(grad_normed_two, midway, scale_two, ffn_gain)
    grad_midway = grad_output + grad_mid_norm
    rounded_midway = grad_midway.astype(jnp.bfloat16)
    spread_back = row_gather(rounded_midway)
    grad_attended = col_reduce(spread_back, out_weight, True).astype(jnp.bfloat16)
    spread_attn = col_gather(attended)
    key_flat, value_flat = key_gather(keys_here, values_here)
    key_all = key_flat.reshape(group_rows, heads_row, HEAD_DIM)
    value_all = value_flat.reshape(group_rows, heads_row, HEAD_DIM)
    grad_out_local = outer_sum(spread_attn, spread_back)

    def backward_block(carried, block_id):
        first_row = block_id * block_rows
        query_block = lax.dynamic_slice_in_dim(queries, first_row, block_rows, 0)
        scores = attend_scores(query_block, key_all, block_mask(first_row))
        probability = jnp.exp(
            scores - lax.dynamic_index_in_dim(log_totals, block_id, 0, keepdims=False)[:, :, None]
        )
        weights_low = probability.astype(jnp.bfloat16)
        grad_block = lax.dynamic_slice_in_dim(grad_attended, first_row, block_rows, 0).reshape(
            block_rows, heads_row, HEAD_DIM
        )
        grad_soft = jnp.einsum(
            "qhd,khd->hqk", grad_block, value_all, preferred_element_type=jnp.float32
        )
        row_inner = jnp.sum(probability * grad_soft, axis=2, keepdims=True)
        grad_scores = (probability * (grad_soft - row_inner)).astype(jnp.bfloat16)
        grad_query_block = jnp.einsum(
            "hqk,khd->qhd", grad_scores, key_all, preferred_element_type=jnp.float32
        ) * HEAD_DIM ** (-0.5)
        grad_key_all = carried[0] + jnp.einsum(
            "hqk,qhd->khd", grad_scores, query_block, preferred_element_type=jnp.float32
        ) * HEAD_DIM ** (-0.5)
        grad_value_all = carried[1] + jnp.einsum(
            "hqk,qhd->khd", weights_low, grad_block, preferred_element_type=jnp.float32
        )
        return (
            (grad_key_all, grad_value_all),
            grad_query_block.astype(jnp.bfloat16).reshape(block_rows, width_row),
        )

    start_grads = jnp.zeros((group_rows, heads_row, HEAD_DIM), jnp.float32)
    key_value_grads, grad_queries = lax.scan(
        backward_block, (start_grads, start_grads), jnp.arange(block_count, dtype=jnp.int32)
    )
    grad_queries = grad_queries.reshape(quarter, width_row)
    grad_key_part = key_value_grads[0].reshape(group_rows, width_row)
    grad_value_part = key_value_grads[1].reshape(group_rows, width_row)
    grad_key_mine, grad_value_mine = (
        lax.psum_scatter(grad_key_part, "col", scatter_dimension=0, tiled=True),
        lax.psum_scatter(grad_value_part, "col", scatter_dimension=0, tiled=True),
    )
    spread_projected = col_gather(
        jnp.concatenate(
            [
                grad_queries,
                grad_key_mine.astype(jnp.bfloat16),
                grad_value_mine.astype(jnp.bfloat16),
            ],
            axis=1,
        )
    )
    grad_normed_one = row_reduce(spread_projected, attention_in, True)
    spread_one = row_gather(normed_one)
    grad_attention = outer_sum(spread_one, spread_projected)
    grad_in_norm, gain_one_part = norm_back(grad_normed_one, residual_in, scale_one, attn_gain)
    grad_own_tokens = grad_midway + grad_in_norm
    grad_attn_gain, grad_ffn_gain = lax.psum((gain_one_part, gain_two_part), ("dp", "row"))
    grad_query, grad_key, grad_value, grad_out, grad_gate, grad_up, grad_down_mine = (
        lax.psum_scatter(
            grad_attention[:, :width_row].astype(jnp.bfloat16),
            "dp",
            scatter_dimension=1,
            tiled=True,
        ).astype(jnp.float32),
        lax.psum_scatter(
            grad_attention[:, width_row : 2 * width_row].astype(jnp.bfloat16),
            "dp",
            scatter_dimension=1,
            tiled=True,
        ).astype(jnp.float32),
        lax.psum_scatter(
            grad_attention[:, 2 * width_row :].astype(jnp.bfloat16),
            "dp",
            scatter_dimension=1,
            tiled=True,
        ).astype(jnp.float32),
        lax.psum_scatter(
            grad_out_local.astype(jnp.bfloat16), "dp", scatter_dimension=0, tiled=True
        ).astype(jnp.float32),
        lax.psum_scatter(
            grad_feedforward[:, :hidden_row].astype(jnp.bfloat16),
            "dp",
            scatter_dimension=1,
            tiled=True,
        ).astype(jnp.float32),
        lax.psum_scatter(
            grad_feedforward[:, hidden_row:].astype(jnp.bfloat16),
            "dp",
            scatter_dimension=1,
            tiled=True,
        ).astype(jnp.float32),
        lax.psum_scatter(
            grad_down.astype(jnp.bfloat16), "dp", scatter_dimension=0, tiled=True
        ).astype(jnp.float32),
    )
    total_tokens = permutation.shape[0]
    inverse = (
        jnp.zeros((total_tokens,), jnp.int32)
        .at[permutation]
        .set(jnp.arange(total_tokens, dtype=jnp.int32))
    )
    wanted_slots = lax.dynamic_slice_in_dim(inverse, device_slot * own_rows, own_rows)
    (grad_tokens,) = make_picker(
        wanted_slots,
        (jnp.zeros_like(grad_own_tokens),),
        (
            (
                lax.all_gather(
                    grad_own_tokens.astype(jnp.bfloat16), ("dp", "row"), axis=0, tiled=True
                ),
            )[0].astype(jnp.float32),
        ),
    )
    return (
        grad_tokens,
        grad_query,
        grad_key,
        grad_value,
        grad_out,
        grad_gate,
        grad_up,
        grad_down_mine,
        grad_attn_gain,
        grad_ffn_gain,
    )


def scores_of(query, key):
    return lax.dot_general(
        query, key, (((1,), (1,)), ((), ())), preferred_element_type=F32
    ) * HEAD_DIM ** (-0.5)


MESH = pl.DeviceIdType.MESH
PLACE = {0: 0, 2: 1, 1: 2, 3: 3}
TILE = 256


class Post:
    def __init__(self, send_sem, recv_sem):
        self.send_sem, self.recv_sem, self.used = send_sem, recv_sem, 0

    def ready(self, src, dst, target, slot=None):
        if slot is None:
            slot = self.used
            self.used += 1
        return pltpu.make_async_remote_copy(
            src_ref=src,
            dst_ref=dst,
            send_sem=self.send_sem.at[slot],
            recv_sem=self.recv_sem.at[slot],
            device_id=target,
            device_id_type=MESH,
        )

    def take(self, count):
        first = self.used
        self.used += count
        return first

    def send(self, src, dst, target):
        copy = self.ready(src, dst, target)
        copy.start()
        return copy


def greet(peers):
    barrier = pltpu.get_barrier_semaphore()
    for peer in peers:
        pl.semaphore_signal(barrier, inc=1, device_id=peer, device_id_type=MESH)
    pl.semaphore_wait(barrier, len(peers))


def as_row(column):
    return jnp.transpose(jnp.broadcast_to(column, (column.shape[0], 128)))[0:8]


def as_column(row):
    return jnp.transpose(row)[:, 0:1]


def forward_kernel(
    x_ref, gain_one_ref, gain_two_ref, lengths_ref, query_ref, key_ref, value_ref, out_ref, gate_ref, up_ref,
    own_grad,
    normed_ref, weight_in, weight_out, q_ref, kv_ref, att_ref, lse_ref, mid_ref, scale_ref, n2_ref, begin_ref, first_scale,
    gate_all, up_all, grad_all,
    zin, zout, sums, wide, given, arrived, low, landed, x32, hidden_own,
    send_sem, recv_sem, local_sem,
):
    d, r, c = (lax.axis_index(name) for name in AXES)
    y, core = c // 2, lax.rem(c, 2)
    rows = x_ref.shape[0]
    fc = x_ref.shape[1]
    group = 2 * rows
    width = q_ref.shape[1]
    half = 2 * fc
    post = Post(send_sem, recv_sem)
    in_plane = [(d, r ^ a, c ^ b) for a in (0, 1) for b in range(COL) if (a, b) != (0, 0)]
    greet([(d ^ j, r, c) for j in (1, 2, 3)] + in_plane)

    def fill_x(t, total):
        part = pl.ds(pl.multiple_of(t * 128, 128), 128)
        value = x_ref[part, :].astype(F32)
        x32[part, :] = value
        sums[0, :, part] = as_row(jnp.sum(value * value, axis=1, keepdims=True))
        return total

    lax.fori_loop(0, rows // 128, fill_x, 0)
    small = [post.send(sums.at[0], sums.at[m], (d, r, c ^ m)) for m in (1, 2, 3)]

    parts = (pl.ds(width, 2 * width), pl.ds(0, width))
    first, first_down = post.take(2 * DP), post.take(2 * DP)

    def line(n, p, target_plane):
        block = zin.at[p, :, parts[n]]
        return post.ready(block, block, (target_plane, r, c), first + DP * n + p)

    def line_down(n, p, target_plane):
        block = zin.at[p, :, parts[n]]
        return pltpu.make_async_remote_copy(
            src_ref=block, dst_ref=block,
            send_sem=send_sem.at[first_down + DP * n + p], recv_sem=recv_sem.at[first + DP * n + p],
            device_id=(target_plane, r, c), device_id_type=MESH,
        )

    def cast_rows(src, dst, amount, step=64):
        def one(t, total):
            part = pl.ds(pl.multiple_of(t * step, step), step)
            dst(part, src[part, :].astype(BF))
            return total

        lax.fori_loop(0, amount // step, one, 0)

    for place, master in enumerate((query_ref, key_ref, value_ref)):
        def put(part, value, place=place):
            zin[d, part, place * width : (place + 1) * width] = value

        cast_rows(master, put, fc)
    for n in (0, 1):
        @pl.when(d < DP - 1)
        def _(n=n):
            line(n, d, d + 1).start()

        @pl.when(d > 0)
        def _(n=n):
            line_down(n, d, d - 1).start()

    first_cols = post.take(2 * DP)

    def place_of(m):
        return lax.rem(m, 2) * 2 + m // 2

    def to_column(n, p):
        there = pl.ds(pl.multiple_of(place_of(p ^ c) * fc, fc), fc)
        return pltpu.make_async_remote_copy(
            src_ref=zin.at[p, :, parts[n]],
            dst_ref=weight_in.at[there, parts[n]],
            send_sem=send_sem.at[first_cols + DP * n + p],
            recv_sem=recv_sem.at[first_cols + DP * n + (p ^ c)],
            device_id=(d, r, p), device_id_type=MESH,
        )

    def keep(n):
        return pltpu.make_async_copy(
            zin.at[c, :, parts[n]], weight_in.at[pl.ds(0, fc), parts[n]], local_sem.at[n]
        )

    def pass_on(n, p):
        @pl.when(p == c)
        def _():
            keep(n).start()

        @pl.when(p != c)
        def _():
            to_column(n, p).start()

    hidden_all = (gate_all, up_all)
    first_sent = post.take(10)
    first_got = first_sent

    def slab(kind, i):
        return hidden_all[kind].at[pl.ds(pl.multiple_of(place_of(i) * fc, fc), fc), :]

    def ship(kind, way, i, target, src=None):
        return pltpu.make_async_remote_copy(
            src_ref=hidden_own.at[kind] if src is None else src,
            dst_ref=slab(kind, i),
            send_sem=send_sem.at[first_sent + 5 * kind + way],
            recv_sem=recv_sem.at[first_got + 4 * kind + i],
            device_id=target, device_id_type=MESH,
        )

    def keep_hidden(kind):
        return pltpu.make_async_copy(hidden_own.at[kind], slab(kind, 0), local_sem.at[3 + kind])

    def to_core(kind):
        return ship(kind, 0, 1, (d, r, c ^ 1))

    def over_y(kind):
        return ship(kind, 1, 2 + core, (d, r, 2 * (1 - y)))

    def over_x(kind):
        return ship(kind, 2, 1 - core, (d, r ^ 1, 2 * y + 1))

    def relay(kind, i):
        return ship(kind, i + 1, 5 - i, (d, r ^ 1, 2 * y + 1), slab(kind, i))

    def start_home(kind):
        @pl.when(core == 0)
        def _():
            keep_hidden(kind).start()

        @pl.when(core == 1)
        def _():
            to_core(kind).start()

    def start_relay(kind):
        @pl.when(core == 0)
        def _():
            for i in (2, 3):
                ship(kind, 0, i, (d, r, c)).wait_recv()
                relay(kind, i).start()

    def cast_hidden(kind):
        def put(part, value):
            hidden_own[kind, part, :] = value

        cast_rows((gate_ref, up_ref)[kind], put, fc)

    cast_hidden(0)
    over_x(0).start()
    over_y(0).start()
    for copy in small:
        copy.wait_recv()

    def norm_one(t, total):
        part = pl.ds(pl.multiple_of(t * 128, 128), 128)
        square = sums[0, :, part] + sums[2, :, part] + sums[1, :, part] + sums[3, :, part]
        scale = lax.rsqrt(as_column(square) / D + EPSILON)
        first_scale[part, :] = scale
        normed_ref[part, 0:fc] = (x32[part, :] * scale * gain_one_ref[...]).astype(BF)
        return total

    lax.fori_loop(0, rows // 128, norm_one, 0)
    own_rows, other_rows = pl.ds(0, rows), pl.ds(rows, rows)

    def columns(place):
        return pl.ds(place * fc, fc)

    own_block = normed_ref.at[own_rows, columns(0)]
    beside = post.send(own_block, normed_ref.at[other_rows, columns(0)], (d, r ^ 1, c))
    beyond = post.send(own_block, normed_ref.at[own_rows, columns(1)], (d, r, c ^ 2))
    corner = post.send(own_block, normed_ref.at[other_rows, columns(1)], (d, r ^ 1, c ^ 2))
    sibling = (d, r, c ^ 1)
    shared = [post.send(own_block, normed_ref.at[own_rows, columns(2)], sibling)]
    pass_on(0, d)
    pass_on(1, d)
    cast_hidden(1)
    start_home(0)
    start_home(1)
    over_x(1).start()
    half_rows = rows // 2
    grad_cross = post.send(
        own_grad.at[pl.ds(pl.multiple_of((1 - y) * half_rows, half_rows), half_rows), :],
        grad_all.at[pl.ds(0, half_rows), pl.ds(fc, fc)],
        (d, r, c ^ 2),
    )
    grad_keep = pltpu.make_async_copy(
        own_grad.at[pl.ds(pl.multiple_of(y * half_rows, half_rows), half_rows), :],
        grad_all.at[pl.ds(0, half_rows), pl.ds(0, fc)],
        local_sem.at[2],
    )
    grad_keep.start()

    def put_out(part, value):
        zout[0, part, :] = value

    cast_rows(out_ref, put_out, width)

    def find_begins(t, total):
        part = pl.ds(pl.multiple_of(t * 128, 128), 128)
        place = lax.broadcasted_iota(jnp.int32, (128, 1), 0) + (d * group + t * 128)
        end = jnp.int32(0)
        begin = jnp.zeros((128, 1), jnp.int32)
        for n in range(lengths_ref.shape[0]):
            end = end + lengths_ref[n]
            begin = jnp.where(place >= end, end, begin)
        begin_ref[part, :] = begin - d * group
        return total

    lax.fori_loop(0, group // 128, find_begins, 0)

    def line_step(s):
        for n in (0, 1):
            for p, valid, onward, forward in (
                (d - s, d - s >= 0, d < DP - 1, lambda n, p: line(n, p, d + 1)),
                (d + s, d + s < DP, d > 0, lambda n, p: line_down(n, p, d - 1)),
            ):
                @pl.when(valid)
                def _(n=n, p=p, onward=onward, forward=forward):
                    line(n, p, d).wait_recv()

                    @pl.when(onward)
                    def _():
                        forward(n, p).start()

                    pass_on(n, p)

    line_step(1)
    line_step(2)
    outs = [post.send(zout.at[0], zout.at[j], (d ^ j, r, c)) for j in (1, 2, 3)]
    over_y(1).start()
    for copy, where, place in ((beside, other_rows, 0), (beyond, own_rows, 1), (corner, other_rows, 1)):
        copy.wait_recv()
        shared.append(
            post.send(normed_ref.at[where, columns(place)], normed_ref.at[where, columns(place + 2)], sibling)
        )
    line_step(3)
    start_relay(0)

    def arrived_blocks(n):
        keep(n).wait()
        for m in (1, 2, 3):
            pltpu.make_async_remote_copy(
                src_ref=zin.at[0, :, parts[n]], dst_ref=weight_in.at[pl.ds(0, fc), parts[n]],
                send_sem=send_sem.at[first_cols], recv_sem=recv_sem.at[first_cols + DP * n + m],
                device_id=(d, r, c), device_id_type=MESH,
            ).wait_recv()

    for copy in shared:
        copy.wait_recv()
    arrived_blocks(0)

    def turned(t):
        return lax.rem(t + 2 * r, group // TILE)

    def project_kv(t, total):
        part = pl.ds(pl.multiple_of(t * TILE, TILE), TILE)
        to = pl.ds(pl.multiple_of(REACH + turned(t) * TILE, TILE), TILE)
        kv_ref[to, :] = jnp.dot(
            normed_ref[part, :], weight_in[:, width:], preferred_element_type=F32
        ).astype(BF)
        return total

    lax.fori_loop(0, group // TILE, project_kv, 0)
    halo = post.ready(kv_ref.at[pl.ds(group, REACH), :], kv_ref.at[pl.ds(0, REACH), :], (lax.rem(d + 1, DP), r, c))

    @pl.when(d < DP - 1)
    def _():
        halo.start()

    arrived_blocks(1)

    def project_q(t, total):
        part = pl.ds(pl.multiple_of(t * TILE, TILE), TILE)
        to = pl.ds(pl.multiple_of(turned(t) * TILE, TILE), TILE)
        q_ref[to, :] = jnp.dot(
            normed_ref[part, :], weight_in[:, :width], preferred_element_type=F32
        ).astype(BF)
        return total

    lax.fori_loop(0, group // TILE, project_q, 0)

    for copy in outs:
        copy.wait_recv()
    out_cols = [
        post.send(zout.at[d ^ c ^ m], weight_out.at[:, columns(PLACE[m])], (d, r, c ^ m)) for m in (1, 2, 3)
    ]
    out_keep = pltpu.make_async_copy(zout.at[d ^ c], weight_out.at[:, columns(0)], local_sem.at[6])
    out_keep.start()
    grad_cross.wait_recv()
    grad_keep.wait()
    grads = [
        post.send(
            grad_all.at[pl.ds(0, half_rows), pl.ds(0, half)],
            grad_all.at[pl.ds(j * half_rows, half_rows), pl.ds(0, half)],
            (d ^ j, r, c),
        )
        for j in (1, 2, 3)
    ]
    grads_shared = [
        post.send(
            grad_all.at[pl.ds(0, half_rows), pl.ds(0, half)],
            grad_all.at[pl.ds(0, half_rows), pl.ds(half, half)],
            sibling,
        )
    ]

    @pl.when(d == 0)
    def _():
        kv_ref[pl.ds(0, REACH), :] = jnp.zeros((REACH, 2 * width), BF)

    @pl.when(d > 0)
    def _():
        halo.wait_recv()

    span = TILE + REACH
    for h in range(width // HEAD_DIM):
        lanes = pl.ds(h * HEAD_DIM, HEAD_DIM)
        value_lanes = pl.ds(width + h * HEAD_DIM, HEAD_DIM)

        def one(t, total, lanes=lanes, value_lanes=value_lanes):
            part = pl.ds(pl.multiple_of(t * TILE, TILE), TILE)
            to = pl.ds(pl.multiple_of(turned(t) * TILE, TILE), TILE)
            window = pl.ds(pl.multiple_of(t * TILE, TILE), span)
            scores = scores_of(q_ref[part, lanes], kv_ref[window, lanes])
            query = lax.broadcasted_iota(jnp.int32, (TILE, span), 0)
            key = lax.broadcasted_iota(jnp.int32, (TILE, span), 1)
            begin = begin_ref[part, 0:1] + (REACH - t * TILE)
            allowed = (key <= query + REACH) & (key >= begin)
            scores = jnp.where(allowed, scores, NEG_FILL)
            highest = jnp.max(scores, axis=1, keepdims=True)
            expo = jnp.exp(scores - highest)
            total_e = jnp.sum(expo, axis=1, keepdims=True)
            probability = (expo * (1.0 / total_e)).astype(BF)
            att_ref[to, lanes] = jnp.dot(
                probability, kv_ref[window, value_lanes], preferred_element_type=F32
            ).astype(BF)
            lse_ref[part, lanes] = jnp.broadcast_to(highest + jnp.log(total_e), (TILE, HEAD_DIM))
            return total

        lax.fori_loop(0, group // TILE, one, 0)

    for copy in out_cols:
        copy.wait_recv()
    out_keep.wait()

    def out_given(t, total):
        part = pl.ds(pl.multiple_of(t * TILE, TILE), TILE)
        given[part, :] = jnp.dot(
            att_ref[part, :], weight_out[:, half:], preferred_element_type=F32
        ).astype(BF)
        return total

    lax.fori_loop(0, group // TILE, out_given, 0)
    to_sibling = post.send(given, arrived, sibling)

    def out_kept(t, total):
        part = pl.ds(pl.multiple_of(t * TILE, TILE), TILE)
        wide[part, :] = jnp.dot(att_ref[part, :], weight_out[:, :half], preferred_element_type=F32)
        return total

    lax.fori_loop(0, group // TILE, out_kept, 0)
    to_sibling.wait_recv()

    def add_low(t, total):
        part = pl.ds(pl.multiple_of(t * 128, 128), 128)
        value = wide[part, :] + arrived[part, :].astype(F32)
        wide[part, :] = value
        low[part, :] = value.astype(BF)
        return total

    lax.fori_loop(0, group // 128, add_low, 0)
    pieces = [
        post.send(low.at[other_rows, columns(1)], landed.at[2], (d, r ^ 1, c ^ 2)),
        post.send(low.at[other_rows, columns(0)], landed.at[0], (d, r ^ 1, c)),
        post.send(low.at[own_rows, columns(1)], landed.at[1], (d, r, c ^ 2)),
    ]
    start_relay(1)
    for copy in pieces:
        copy.wait_recv()

    def middle(t, total):
        part = pl.ds(pl.multiple_of(t * 128, 128), 128)
        value = (
            x32[part, :] + wide[part, 0:fc] + landed[0, part, :].astype(F32)
            + landed[1, part, :].astype(F32) + landed[2, part, :].astype(F32)
        )
        mid_ref[part, :] = value
        sums[4, :, part] = as_row(jnp.sum(value * value, axis=1, keepdims=True))
        return total

    lax.fori_loop(0, rows // 128, middle, 0)
    again = [post.send(sums.at[4], sums.at[4 + m], (d, r, c ^ m)) for m in (1, 2, 3)]
    for copy in again:
        copy.wait_recv()

    def norm_two(t, total):
        part = pl.ds(pl.multiple_of(t * 128, 128), 128)
        square = sums[4, :, part] + sums[6, :, part] + sums[5, :, part] + sums[7, :, part]
        scale = lax.rsqrt(as_column(square) / D + EPSILON)
        scale_ref[part, :] = scale
        n2_ref[part, :] = (mid_ref[part, :] * scale * gain_two_ref[...]).astype(BF)
        return total

    lax.fori_loop(0, rows // 128, norm_two, 0)

    for j, copy in zip((1, 2, 3), grads):
        copy.wait_recv()
        there = pl.ds(j * half_rows, half_rows)
        grads_shared.append(
            post.send(grad_all.at[there, pl.ds(0, half)], grad_all.at[there, pl.ds(half, half)], sibling)
        )
    for copy in grads_shared:
        copy.wait_recv()
    for kind in (0, 1):
        over_y(kind).wait_send()
        over_x(kind).wait_send()

        @pl.when(core == 0)
        def _(kind=kind):
            keep_hidden(kind).wait()
            ship(kind, 0, 1, (d, r, c)).wait_recv()
            for i in (2, 3):
                relay(kind, i).wait_send()

        @pl.when(core == 1)
        def _(kind=kind):
            to_core(kind).wait_send()
            for i in range(COL):
                ship(kind, 0, i, (d, r, c)).wait_recv()

    for copy in (
        small + [grad_cross, beside, beyond, corner] + shared + outs + out_cols + grads + grads_shared
        + [to_sibling] + pieces + again
    ):
        copy.wait_send()

    @pl.when(d < DP - 1)
    def _():
        halo.wait_send()

    for n in (0, 1):
        for p in range(DP):
            @pl.when((d < DP - 1) & (p <= d))
            def _(n=n, p=p):
                line(n, p, d).wait_send()

            @pl.when((d > 0) & (p >= d))
            def _(n=n, p=p):
                line_down(n, p, d).wait_send()

            @pl.when(c != p)
            def _(n=n, p=p):
                to_column(n, p).wait_send()


SENDS = 80


def forward(x, gain_one, gain_two, lengths, query, key, value, out, gate, up, own_grad):
    rows, fc = x.shape
    group = 2 * rows
    width = out.shape[0]
    units = gate.shape[1]
    vmem = pl.BlockSpec(memory_space=pltpu.VMEM)
    smem = pl.BlockSpec(memory_space=pltpu.SMEM)
    hbm = pl.BlockSpec(memory_space=pl.ANY)

    def like(shape, dtype=BF):
        return jax.ShapeDtypeStruct(shape, dtype)

    return pl.pallas_call(
        forward_kernel,
        in_specs=[vmem] * 3 + [smem] + [vmem] * 6 + [hbm],
        out_specs=[vmem] * 12 + [hbm] * 3,
        out_shape=[
            like((group, D)),
            like((D, 3 * width)),
            like((width, D)),
            like((group, width)),
            like((REACH + group, 2 * width)),
            like((group, width)),
            like((group, width), F32),
            like((rows, fc), F32),
            like((rows, 1), F32),
            like((rows, fc)),
            like((group, 1), jnp.int32),
            like((rows, 1), F32),
            like((D, units)),
            like((D, units)),
            like((group, D)),
        ],
        scratch_shapes=[
            pltpu.VMEM((DP, fc, 3 * width), BF),
            pltpu.VMEM((DP, width, fc), BF),
            pltpu.VMEM((8, 8, rows), F32),
            pltpu.VMEM((group, 2 * fc), F32),
            pltpu.VMEM((group, 2 * fc), BF),
            pltpu.VMEM((group, 2 * fc), BF),
            pltpu.VMEM((group, 2 * fc), BF),
            pltpu.VMEM((3, rows, fc), BF),
            pltpu.VMEM((rows, fc), F32),
            pltpu.VMEM((2, fc, units), BF),
            pltpu.SemaphoreType.DMA((SENDS,)),
            pltpu.SemaphoreType.DMA((SENDS,)),
            pltpu.SemaphoreType.DMA((8,)),
        ],
        compiler_params=pltpu.CompilerParams(
            collective_id=1, has_side_effects=True, vmem_limit_bytes=60 << 20
        ),
        cost_estimate=pl.CostEstimate(
            flops=6 * group * D * width, bytes_accessed=64 << 20, transcendentals=0
        ),
    )(x, gain_one, gain_two, lengths, query, key, value, out, gate, up, own_grad)


def at(t, size):
    return pl.ds(pl.multiple_of(t * size, size), size)


def loop(count, body):
    def one(t, total):
        body(t)
        return total

    lax.fori_loop(0, count, one, 0)


def maker(send_sem, recv_sem):
    def raw(src, dst, sent, got_at, target):
        return pltpu.make_async_remote_copy(
            src_ref=src, dst_ref=dst, send_sem=send_sem.at[sent], recv_sem=recv_sem.at[got_at],
            device_id=target, device_id_type=MESH,
        )

    return raw


class LineSum:
    def __init__(self, raw, arrays, base, me):
        self.raw, self.arrays, self.base, self.me = raw, arrays, base, me

    def sem(self, n, p, down):
        return self.base + 8 * n + 4 * down + p

    def take(self, p, down, done):
        d = self.me[0]
        for n, (z, got_z) in enumerate(self.arrays):
            self.raw(z.at[p], got_z.at[p], self.sem(n, p, down), self.sem(n, p, down), self.me).wait_recv()

        @pl.when(jnp.logical_not(done))
        def _():
            for z, got_z in self.arrays:
                def one(t, z=z, got_z=got_z):
                    z[p, at(t, 64), :] = (
                        z[p, at(t, 64), :].astype(F32) + got_z[p, at(t, 64), :].astype(F32)
                    ).astype(BF)

                loop(z.shape[1] // 64, one)

    def up(self, p):
        d, r, c = self.me

        @pl.when((d > 0) & (d <= p))
        def _():
            self.take(p, 0, d == p)

        @pl.when(d < p)
        def _():
            for n, (z, got_z) in enumerate(self.arrays):
                self.raw(z.at[p], got_z.at[p], self.sem(n, p, 0), self.sem(n, p, 0), (d + 1, r, c)).start()

    def down(self, p):
        d, r, c = self.me

        @pl.when((d < DP - 1) & (d >= p))
        def _():
            self.take(p, 1, d == p)

        @pl.when(d > p)
        def _():
            slot = jnp.where(p < d - 1, p, DP)
            for n, (z, got_z) in enumerate(self.arrays):
                self.raw(z.at[p], got_z.at[slot], self.sem(n, p, 1), self.sem(n, p, 1), (d - 1, r, c)).start()

    def begin(self):
        d = self.me[0]

        @pl.when(d == 0)
        def _():
            for p in (3, 2, 1):
                self.up(p)

        @pl.when(d == DP - 1)
        def _():
            for p in (0, 1, 2):
                self.down(p)

    def rest(self):
        d = self.me[0]

        @pl.when(d == 0)
        def _():
            self.down(0)

        @pl.when(d == 1)
        def _():
            self.up(3)
            self.up(2)
            self.down(0)
            self.down(1)
            self.up(1)

        @pl.when(d == 2)
        def _():
            self.down(0)
            self.down(1)
            self.up(3)
            self.up(2)
            self.down(2)

        @pl.when(d == DP - 1)
        def _():
            self.up(3)

    def settle(self):
        d = self.me[0]
        for p in range(DP):
            for n, (z, got_z) in enumerate(self.arrays):
                for down, sent in ((0, d < p), (1, d > p)):
                    @pl.when(sent)
                    def _(p=p, n=n, z=z, got_z=got_z, down=down):
                        self.raw(
                            z.at[p], got_z.at[p], self.sem(n, p, down), self.sem(n, p, down), self.me
                        ).wait_send()

    def total(self, z, got_z, part):
        d = self.me[0]
        value = z[d, part, :].astype(F32)
        value = value + jnp.where(d > 0, got_z[d, part, :].astype(F32), 0.0)
        return value + jnp.where(d < DP - 1, got_z[DP, part, :].astype(F32), 0.0)


class PlaneSum:
    def __init__(self, raw, stage, got, comb, base, local_sem, local_base, me):
        self.raw, self.stage, self.got, self.comb, self.base = raw, stage, got, comb, base
        self.local_sem, self.local_base, self.me = local_sem, local_base, me
        self.kinds = range(stage.shape[0])

    def from_one(self, kind, i):
        d, r, c = self.me
        y = c // 2
        sent, base = self.base + 10 * kind + i, self.base + 10 * kind
        if i < 2:
            return self.raw(self.stage.at[kind, i], self.got.at[kind, 0], sent, base, (d, r ^ 1, 2 * y + 1 - i))
        return self.raw(
            self.stage.at[kind, i], self.comb.at[kind, 3 - i], sent, base + 3 + (3 - i), (d, r ^ 1, 2 * y)
        )

    def from_zero(self, kind, i):
        d, r, c = self.me
        sent, base = self.base + 10 * kind + i, self.base + 10 * kind
        if i == 1:
            return self.raw(self.stage.at[kind, i], self.got.at[kind, 1], sent, base + 1, (d, r, c ^ 1))
        return self.raw(
            self.stage.at[kind, i], self.got.at[kind, 2], sent, base + 2, (d, r, 2 * (1 - c // 2) + i - 2)
        )

    def home(self, kind):
        return pltpu.make_async_copy(
            self.stage.at[kind, 0], self.got.at[kind, 1], self.local_sem.at[self.local_base + kind]
        )

    def start_far(self):
        @pl.when(lax.rem(self.me[2], 2) == 1)
        def _():
            for i in (2, 3):
                for kind in self.kinds:
                    self.from_one(kind, i).start()

    def start_near(self):
        core = lax.rem(self.me[2], 2)

        @pl.when(core == 1)
        def _():
            for i in (0, 1):
                for kind in self.kinds:
                    self.from_one(kind, i).start()

        @pl.when(core == 0)
        def _():
            for kind in self.kinds:
                self.home(kind).start()
                self.from_zero(kind, 1).start()

    def combine(self, room, local_base):
        core = lax.rem(self.me[2], 2)

        @pl.when(core == 0)
        def _():
            fetches = {}
            for i in (2, 3):
                for kind in self.kinds:
                    self.raw(
                        self.stage.at[kind, i], self.comb.at[kind, i - 2], self.base,
                        self.base + 10 * kind + 3 + (i - 2), self.me,
                    ).wait_recv()
                    fetches[i, kind] = pltpu.make_async_copy(
                        self.comb.at[kind, i - 2], room(kind, i - 2),
                        self.local_sem.at[local_base + 2 * kind + i - 2],
                    )
                    fetches[i, kind].start()
            for i in (2, 3):
                for kind in self.kinds:
                    fetches[i, kind].wait()

                    def add(t, kind=kind, i=i):
                        self.stage[kind, i, at(t, 64), :] = (
                            self.stage[kind, i, at(t, 64), :].astype(F32)
                            + room(kind, i - 2)[at(t, 64), :].astype(F32)
                        ).astype(BF)

                    loop(self.stage.shape[2] // 64, add)
                    self.from_zero(kind, i).start()

    def settle(self):
        core = lax.rem(self.me[2], 2)
        for kind in self.kinds:
            base = self.base + 10 * kind
            for n in (0, 2):
                self.raw(self.stage.at[kind, 0], self.got.at[kind, n], self.base, base + n, self.me).wait_recv()

            @pl.when(core == 1)
            def _(kind=kind, base=base):
                self.raw(self.stage.at[kind, 0], self.got.at[kind, 1], self.base, base + 1, self.me).wait_recv()
                for i in range(COL):
                    self.from_one(kind, i).wait_send()

            @pl.when(core == 0)
            def _(kind=kind):
                self.home(kind).wait()
                for i in (1, 2, 3):
                    self.from_zero(kind, i).wait_send()


def middle_kernel(
    n2_ref, mid_ref, scale_ref, gain_ref, own_grad, down_ref, gate_hbm, up_hbm, grad_hbm,
    n2, dgate, dup, grad_out, gain_out, got, comb,
    wg, wu, wd, gb, own_down, gate, up, du, hidden, given, arrived, z, got_z, crossing, crossed, gn, sums, stage,
    send_sem, recv_sem, local_sem,
):
    d, r, c = (lax.axis_index(name) for name in AXES)
    me = (d, r, c)
    y, core = c // 2, lax.rem(c, 2)
    rows, fc = n2_ref.shape
    block = rows // 2
    units = own_down.shape[0]
    half = 2 * fc
    over = (((0,), (0,)), ((), ()))
    across = (((1,), (1,)), ((), ()))
    post = Post(send_sem, recv_sem)
    raw = maker(send_sem, recv_sem)
    sibling = (d, r, c ^ 1)
    others = [(a, b) for a in (0, 1) for b in range(COL) if (a, b) != (0, 0)]
    greet([(d, r ^ a, c ^ b) for a, b in others] + [(d ^ j, r, c) for j in (1, 2, 3)])

    cross = post.send(
        n2_ref.at[pl.ds(pl.multiple_of((1 - y) * block, block), block), :],
        n2.at[pl.ds(0, block), pl.ds(fc, fc)],
        (d, r, c ^ 2),
    )
    loads = [
        pltpu.make_async_copy(src, dst, local_sem.at[n])
        for n, (src, dst) in enumerate(((gate_hbm, wg), (up_hbm, wu), (grad_hbm, gb)))
    ]
    for load in loads:
        load.start()

    def cast_down(t):
        own_down[at(t, 64), :] = down_ref[at(t, 64), :].astype(BF)

    loop(units // 64, cast_down)
    first_sent = post.take(10)

    def place_of(i):
        return lax.rem(i, 2) * 2 + i // 2

    def piece(ref, n):
        return ref.at[pl.ds(n * (units // 2), units // 2), :]

    def ship(n, way, i, target, src=None):
        return raw(
            piece(own_down if src is None else src, n), piece(wd.at[place_of(i)], n),
            first_sent + 5 * n + way, first_sent + 5 * n + i, target,
        )

    keep_down = pltpu.make_async_copy(own_down, wd.at[0], local_sem.at[3])

    def to_core(n):
        return ship(n, 0, 1, sibling)

    def over_y(n):
        return ship(n, 1, 2 + core, (d, r, 2 * (1 - y)))

    def over_x(n):
        return ship(n, 2, 1 - core, (d, r ^ 1, 2 * y + 1))

    def relay(n, i):
        return ship(n, i + 1, 5 - i, (d, r ^ 1, 2 * y + 1), wd.at[PLACE[i]])

    for n in (0, 1):
        over_y(n).start()
        over_x(n).start()

    @pl.when(core == 0)
    def _():
        keep_down.start()

    @pl.when(core == 1)
    def _():
        for n in (0, 1):
            to_core(n).start()

    def pass_down(n):
        @pl.when(core == 0)
        def _():
            for i in (2, 3):
                ship(n, 0, i, me).wait_recv()
                relay(n, i).start()

    n2[0:block, 0:fc] = n2_ref[pl.ds(pl.multiple_of(y * block, block), block), :]
    cross.wait_recv()

    first_up, first_down = post.take(DP), post.take(DP)
    first_shared = post.take(DP)

    def rail(p, e):
        return n2.at[at(p ^ e, block), pl.ds(0, half)]

    def go_up(p):
        return raw(rail(p, d), rail(p, d + 1), first_up + p, first_up + p, (d + 1, r, c))

    def go_down(p):
        return raw(rail(p, d), rail(p, d - 1), first_down + p, first_up + p, (d - 1, r, c))

    def share(p):
        return raw(
            rail(p, d), n2.at[at(p ^ d, block), pl.ds(half, half)], first_shared + p, first_shared + p, sibling
        )

    def onward(p):
        @pl.when((p <= d) & (d < DP - 1))
        def _():
            go_up(p).start()

        @pl.when((p >= d) & (d > 0))
        def _():
            go_down(p).start()

        share(p).start()

    def project(p):
        share(p).wait_recv()
        part = at(p ^ d, block)
        gate[part, :] = jnp.dot(n2[part, :], wg[...], preferred_element_type=F32)
        up[part, :] = jnp.dot(n2[part, :], wu[...], preferred_element_type=F32)

    def hidden_grads(first, fresh):
        def one(t):
            part = at(t, block)
            value = jnp.zeros((block, units), F32) if fresh else du[part, :]
            for i in (first, first + 1):
                place = PLACE[i]
                value = value + lax.dot_general(
                    gb[part, place * fc : (place + 1) * fc], wd[place], across, preferred_element_type=F32
                )
            du[part, :] = value

        loop(DP, one)

    onward(d)
    turns = [
        d,
        jnp.where(d == 0, 1, d - 1),
        jnp.where(d < 2, 2, jnp.where(d == 2, 3, 1)),
        jnp.where(d < 2, 3, 0),
    ]
    inner = (d == 1) | (d == 2)

    def arrival(n):
        raw(rail(turns[n], d), rail(turns[n], d), first_up, first_up + turns[n], me).wait_recv()
        onward(turns[n])

    for load in loads:
        load.wait()
    arrival(1)

    @pl.when(inner)
    def _():
        arrival(2)

    pass_down(0)
    project(turns[0])
    pass_down(1)
    project(turns[1])

    @pl.when(jnp.logical_not(inner))
    def _():
        arrival(2)

    @pl.when(inner)
    def _():
        arrival(3)

    @pl.when(core == 0)
    def _():
        keep_down.wait()
        for n in (0, 1):
            ship(n, 0, 1, me).wait_recv()

    @pl.when(core == 1)
    def _():
        for n in (0, 1):
            for i in (0, 1):
                ship(n, 0, i, me).wait_recv()

    hidden_grads(0, True)
    project(turns[2])

    @pl.when(jnp.logical_not(inner))
    def _():
        arrival(3)

    project(turns[3])

    @pl.when(core == 1)
    def _():
        for n in (0, 1):
            for i in (2, 3):
                ship(n, 0, i, me).wait_recv()

    hidden_grads(2, False)

    def units_of(t):
        part = at(t, 64)
        g, u, grad = gate[part, :], up[part, :], du[part, :]
        sigmoid = 1.0 / (1.0 + jnp.exp(-g))
        silu = g * sigmoid
        hidden[part, :] = (silu * u).astype(BF)
        dgate[part, :] = (grad * u * sigmoid * (1.0 + g * (1.0 - sigmoid))).astype(BF)
        dup[part, :] = (grad * silu).astype(BF)

    loop(2 * rows // 64, units_of)

    def back(part, cols):
        return lax.dot_general(
            dgate[part, :], wg[cols, :], across, preferred_element_type=F32
        ) + lax.dot_general(dup[part, :], wu[cols, :], across, preferred_element_type=F32)

    def down_part(i):
        def down_grad(t):
            place = PLACE[i]
            stage[0, i, at(t, TILE), :] = lax.dot_general(
                hidden[:, at(t, TILE)], gb[:, place * fc : (place + 1) * fc], over, preferred_element_type=F32
            ).astype(BF)

        loop(units // TILE, down_grad)

    owners = PlaneSum(raw, stage, got, comb, post.take(10), local_sem, 4, me)

    line = LineSum(raw, ((z, got_z),), post.take(8), me)

    def plane_of(t):
        return jnp.where(d < DP // 2, DP - 1 - t, t)

    def to_sibling(t):
        part = at(plane_of(t) ^ d, block)
        return raw(given.at[part, :], arrived.at[part, :], first_given + t, first_given + t, sibling)

    def give(t):
        part = at(plane_of(t) ^ d, block)
        given[part, :] = back(part, slice(half, None)).astype(BF)
        to_sibling(t).start()

    def keep(t):
        p = plane_of(t)
        part = at(p ^ d, block)
        value = back(part, slice(0, half))
        to_sibling(t).wait_recv()
        z[p] = (value + arrived[part, :].astype(F32)).astype(BF)

        if t < DP - 1:
            @pl.when(d == 0)
            def _():
                line.up(DP - 1 - t)

            @pl.when(d == DP - 1)
            def _():
                line.down(t)

    first_given = post.take(DP)
    give(0)
    give(1)
    down_part(2)
    down_part(3)
    owners.start_far()
    keep(0)
    give(2)
    keep(1)
    give(3)
    keep(2)
    down_part(0)
    down_part(1)
    owners.start_near()
    keep(3)
    owners.combine(lambda kind, j: wg.at[pl.ds(0, units), pl.ds(j * fc, fc)], 5)
    line.rest()

    def settle_rows(t):
        part = at(t, 64)
        total = line.total(z, got_z, part)
        gn[pl.ds(pl.multiple_of(y * block + t * 64, 64), 64), :] = total[:, 0:fc]
        crossing[part, :] = total[:, fc:].astype(BF)

    loop(block // 64, settle_rows)
    other = post.send(crossing, crossed, (d, r, c ^ 2))
    other.wait_recv()

    def other_rows(t):
        gn[pl.ds(pl.multiple_of((1 - y) * block + t * 64, 64), 64), :] = crossed[at(t, 64), :].astype(F32)

    loop(block // 64, other_rows)

    def inner_sum(t):
        part = at(t, 128)
        inner = gn[part, :] * gain_ref[...] * mid_ref[part, :]
        sums[0, :, part] = as_row(jnp.sum(inner, axis=1, keepdims=True))

    loop(rows // 128, inner_sum)
    small = [post.send(sums.at[0], sums.at[m], (d, r, c ^ m)) for m in (1, 2, 3)]

    def gain_sum(t, total):
        part = at(t, 128)
        value = gn[part, :] * mid_ref[part, :] * scale_ref[part, :]
        return total + jnp.sum(value, axis=0, keepdims=True)

    gain_out[...] = lax.fori_loop(0, rows // 128, gain_sum, jnp.zeros((1, fc), F32))
    for copy in small:
        copy.wait_recv()

    def finish(t):
        part = at(t, 128)
        inner = as_column(sums[0, :, part] + sums[2, :, part] + sums[1, :, part] + sums[3, :, part])
        scale = scale_ref[part, :]
        grad_out[part, :] = (
            own_grad[part, :].astype(F32) + scale * (gn[part, :] * gain_ref[...])
            - mid_ref[part, :] * (scale * scale * scale * inner / D)
        )

    loop(rows // 128, finish)

    owners.settle()
    line.settle()
    for copy in [cross, other] + small:
        copy.wait_send()
    for t in range(DP):
        to_sibling(t).wait_send()
    for n in (0, 1):
        over_y(n).wait_send()
        over_x(n).wait_send()

        @pl.when(core == 0)
        def _(n=n):
            for i in (2, 3):
                relay(n, i).wait_send()

        @pl.when(core == 1)
        def _(n=n):
            to_core(n).wait_send()

    for p in range(DP):
        share(p).wait_send()

        @pl.when((p <= d) & (d < DP - 1))
        def _(p=p):
            go_up(p).wait_send()

        @pl.when((p >= d) & (d > 0))
        def _(p=p):
            go_down(p).wait_send()


def middle(n2, mid, scale, gain, own_grad, down, gate, up, grad_all):
    rows, fc = n2.shape
    group = 2 * rows
    block = rows // 2
    units = down.shape[0]
    vmem = pl.BlockSpec(memory_space=pltpu.VMEM)
    hbm = pl.BlockSpec(memory_space=pl.ANY)

    def like(shape, dtype=BF):
        return jax.ShapeDtypeStruct(shape, dtype)

    return pl.pallas_call(
        middle_kernel,
        in_specs=[vmem] * 6 + [hbm] * 3,
        out_specs=[vmem] * 5 + [hbm] * 2,
        out_shape=[
            like((group, D)),
            like((group, units)),
            like((group, units)),
            like((rows, fc), F32),
            like((1, fc), F32),
            like((1, 3, units, fc)),
            like((1, 2, units, fc)),
        ],
        scratch_shapes=[
            pltpu.VMEM((D, units), BF),
            pltpu.VMEM((D, units), BF),
            pltpu.VMEM((COL, units, fc), BF),
            pltpu.VMEM((group, D), BF),
            pltpu.VMEM((units, fc), BF),
            pltpu.VMEM((group, units), F32),
            pltpu.VMEM((group, units), F32),
            pltpu.VMEM((group, units), F32),
            pltpu.VMEM((group, units), BF),
            pltpu.VMEM((group, 2 * fc), BF),
            pltpu.VMEM((group, 2 * fc), BF),
            pltpu.VMEM((DP, block, 2 * fc), BF),
            pltpu.VMEM((DP + 1, block, 2 * fc), BF),
            pltpu.VMEM((block, fc), BF),
            pltpu.VMEM((block, fc), BF),
            pltpu.VMEM((rows, fc), F32),
            pltpu.VMEM((4, 8, rows), F32),
            pltpu.VMEM((1, COL, units, fc), BF),
            pltpu.SemaphoreType.DMA((SENDS,)),
            pltpu.SemaphoreType.DMA((SENDS,)),
            pltpu.SemaphoreType.DMA((8,)),
        ],
        compiler_params=pltpu.CompilerParams(
            collective_id=3, has_side_effects=True, vmem_limit_bytes=62 << 20
        ),
        cost_estimate=pl.CostEstimate(
            flops=14 * group * D * units, bytes_accessed=48 << 20, transcendentals=group * units
        ),
    )(n2, mid, scale, gain, own_grad, down, gate, up, grad_all)


POSTS = 112


def backward_kernel(
    x_ref, gain_ref, scale_ref, mid_ref, gain_two_ref, weight_in, weight_out, q_ref, kv_ref, att_ref, lse_ref,
    begin_ref, normed_hbm, n2_hbm, dgate_hbm, dup_hbm,
    tokens_out, query_out, key_out, value_out, out_out, gains_out, got, comb,
    n1, n2, dgu, dball, dotted, dproj, acc, spill, spilled, stage, own_f, arrived, landed,
    zq, zo, zkv, rq, ro, rkv, sums, gsum,
    send_sem, recv_sem, local_sem,
):
    d, r, c = (lax.axis_index(name) for name in AXES)
    y, core = c // 2, lax.rem(c, 2)
    rows, fc = x_ref.shape
    group = 2 * rows
    width = q_ref.shape[1]
    units = dgate_hbm.shape[1]
    half = 2 * fc
    tiles = group // TILE
    over = (((0,), (0,)), ((), ()))
    across = (((1,), (1,)), ((), ()))
    post = Post(send_sem, recv_sem)
    loads = [
        pltpu.make_async_copy(src, dst, local_sem.at[n])
        for n, (src, dst) in enumerate((
            (n2_hbm, n2),
            (dgate_hbm, dgu.at[pl.ds(0, group), :]),
            (dup_hbm, dgu.at[pl.ds(group, group), :]),
            (normed_hbm, n1),
        ))
    ]
    for load in loads:
        load.start()

    others = [(a, b) for a in (0, 1) for b in range(COL) if (a, b) != (0, 0)]
    greet(
        [(d, r ^ a, c ^ b) for a, b in others]
        + [(d ^ j, r ^ a, c) for j in (1, 2, 3) for a in (0, 1)]
    )

    def columns(place):
        return pl.ds(place * fc, fc)

    def turned(t):
        return lax.rem(t + 2 * r, tiles)

    raw = maker(send_sem, recv_sem)
    me = (d, r, c)
    sibling = (d, r, c ^ 1)
    own_rows, other_rows = pl.ds(0, rows), pl.ds(rows, rows)
    def round_mid(t):
        dball[at(t, 128), 0:fc] = mid_ref[at(t, 128), :].astype(BF)

    loop(rows // 128, round_mid)
    own_block = dball.at[own_rows, columns(0)]
    beside = post.send(own_block, dball.at[other_rows, columns(0)], (d, r ^ 1, c))
    beyond = post.send(own_block, dball.at[own_rows, columns(1)], (d, r, c ^ 2))
    corner = post.send(own_block, dball.at[other_rows, columns(1)], (d, r ^ 1, c ^ 2))
    shared = [post.send(own_block, dball.at[own_rows, columns(2)], sibling)]

    for load in loads[:3]:
        load.wait()
    owners = PlaneSum(raw, stage, got, comb, post.take(20), local_sem, 4, me)

    def hidden_part(i):
        for kind in (0, 1):
            def hidden_grad(t, kind=kind):
                left = n2[:, pl.ds(pl.multiple_of(PLACE[i] * fc + t * TILE, TILE), TILE)]
                stage[kind, i, at(t, TILE), :] = lax.dot_general(
                    left, dgu[pl.ds(kind * group, group), :], over, preferred_element_type=F32
                ).astype(BF)

            loop(fc // TILE, hidden_grad)

    hidden_part(2)
    hidden_part(3)
    owners.start_far()
    hidden_part(0)
    hidden_part(1)
    loads[3].wait()

    for copy, where, place in ((beside, other_rows, 0), (beyond, own_rows, 1), (corner, other_rows, 1)):
        copy.wait_recv()
        shared.append(post.send(dball.at[where, columns(place)], dball.at[where, columns(place + 2)], sibling))
    for copy in shared:
        copy.wait_recv()

    def head_grad(t):
        dotted[at(turned(t), TILE), :] = lax.dot_general(
            dball[at(t, TILE), :], weight_out[...], across, preferred_element_type=F32
        ).astype(BF)

    loop(tiles, head_grad)

    sent_out = [None] + [post.take(1) for _ in (1, 2, 3)]
    outs = []
    for place, m in enumerate((0, 2, 1, 3)):
        value = lax.dot_general(
            att_ref[...], dball[:, place * fc : (place + 1) * fc], over, preferred_element_type=F32
        ).astype(BF)
        if m == 0:
            zo[c] = value
        else:
            n2[(m - 1) * width : m * width, half : half + fc] = value
            staged = n2.at[pl.ds((m - 1) * width, width), pl.ds(half, fc)]
            copy = raw(staged, zo.at[c], sent_out[m], sent_out[m], (d, r, c ^ m))
            copy.start()
            outs.append(copy)

    span = TILE + REACH
    scale = HEAD_DIM ** (-0.5)
    spills = []
    for h in range(width // HEAD_DIM):
        lanes = pl.ds(h * HEAD_DIM, HEAD_DIM)
        value_lanes = pl.ds(width + h * HEAD_DIM, HEAD_DIM)

        def clear(t, lanes=lanes, value_lanes=value_lanes):
            acc[at(t, TILE), lanes] = jnp.zeros((TILE, HEAD_DIM), F32)
            acc[at(t, TILE), value_lanes] = jnp.zeros((TILE, HEAD_DIM), F32)

        loop((group + REACH) // TILE, clear)

        def one(t, lanes=lanes, value_lanes=value_lanes):
            part = at(t, TILE)
            window = pl.ds(pl.multiple_of(t * TILE, TILE), span)
            query, key = q_ref[part, lanes], kv_ref[window, lanes]
            grad = dotted[part, lanes]
            scores = scores_of(query, key)
            query_at = lax.broadcasted_iota(jnp.int32, (TILE, span), 0)
            key_at = lax.broadcasted_iota(jnp.int32, (TILE, span), 1)
            begin = begin_ref[part, 0:1] + (REACH - t * TILE)
            allowed = (key_at <= query_at + REACH) & (key_at >= begin)
            scores = jnp.where(allowed, scores - lse_ref[part, lanes][:, 0:1], NEG_FILL)
            probability = jnp.exp(scores)
            grad_soft = lax.dot_general(grad, kv_ref[window, value_lanes], across, preferred_element_type=F32)
            inner = jnp.sum(probability * grad_soft, axis=1, keepdims=True)
            grad_scores = (probability * (grad_soft - inner)).astype(BF)
            dproj[at(turned(t), TILE), lanes] = (
                jnp.dot(grad_scores, key, preferred_element_type=F32) * scale
            ).astype(BF)
            acc[window, lanes] += lax.dot_general(grad_scores, query, over, preferred_element_type=F32) * scale
            acc[window, value_lanes] += lax.dot_general(
                probability.astype(BF), grad, over, preferred_element_type=F32
            )

        loop(tiles, one)

        def round_spill(t, h=h, lanes=lanes, value_lanes=value_lanes):
            spill[h, at(t, TILE), 0:HEAD_DIM] = acc[at(t, TILE), lanes].astype(BF)
            spill[h, at(t, TILE), HEAD_DIM:] = acc[at(t, TILE), value_lanes].astype(BF)

        loop(REACH // TILE, round_spill)
        copy = post.ready(spill.at[h], spilled.at[h], (lax.rem(d + DP - 1, DP), r, c))
        spills.append(copy)

        @pl.when(d > 0)
        def _(copy=copy):
            copy.start()

    def attention_grads(first_lane, lane_count, dest):
        lanes = slice(first_lane, first_lane + lane_count)
        slots = [None] + [post.take(1) for _ in (1, 2, 3)]
        copies = []
        for place, m in enumerate((0, 2, 1, 3)):
            def tile(t, place=place, m=m):
                left = n1[:, pl.ds(pl.multiple_of(place * fc + t * TILE, TILE), TILE)]
                value = lax.dot_general(left, dproj[:, lanes], over, preferred_element_type=F32).astype(BF)
                if m == 0:
                    dest[c, at(t, TILE), :] = value
                else:
                    dgu[pl.ds(pl.multiple_of(place * fc + t * TILE, TILE), TILE), lanes] = value

            loop(fc // TILE, tile)
            if m:
                copy = raw(
                    dgu.at[pl.ds(place * fc, fc), pl.ds(first_lane, lane_count)], dest.at[c],
                    slots[m], slots[m], (d, r, c ^ m),
                )
                copy.start()
                copies.append(copy)
        return copies

    qs = attention_grads(0, width, zq)

    @pl.when(d < DP - 1)
    def _():
        for copy in spills:
            copy.wait_recv()

    @pl.when(d == DP - 1)
    def _():
        spilled[...] = jnp.zeros_like(spilled)

    for h in range(width // HEAD_DIM):
        for which in (0, 1):
            lanes = pl.ds(which * width + h * HEAD_DIM, HEAD_DIM)
            out_lanes = pl.ds((1 + which) * width + h * HEAD_DIM, HEAD_DIM)

            def whole(t, h=h, which=which, lanes=lanes, out_lanes=out_lanes):
                total = acc[pl.ds(pl.multiple_of(REACH + t * TILE, TILE), TILE), lanes]
                extra = spilled[
                    h, at(jnp.maximum(t - 1, 0), TILE), which * HEAD_DIM : (which + 1) * HEAD_DIM
                ].astype(F32)
                total = total + jnp.where(t > 0, extra, 0.0)
                dproj[at(turned(t), TILE), out_lanes] = total.astype(BF)

            loop(tiles, whole)

    kvs = attention_grads(width, 2 * width, zkv)
    for copy in outs + qs:
        copy.wait_recv()
    first_line = post.take(24)
    line_a = LineSum(raw, ((zq, rq), (zo, ro)), first_line, me)
    line_b = LineSum(raw, ((zkv, rkv),), first_line + 16, me)
    line_a.begin()

    def given_part(t):
        n2[at(t, TILE), 0:half] = lax.dot_general(
            dproj[at(t, TILE), :], weight_in[half:, :], across, preferred_element_type=F32
        ).astype(BF)

    loop(tiles, given_part)
    to_sibling = post.send(n2.at[:, pl.ds(0, half)], arrived, sibling)

    to_sibling.wait_recv()
    for copy in outs:
        copy.wait_send()

    def kept_part(t):
        part = at(t, TILE)
        value = lax.dot_general(
            dproj[part, :], weight_in[:half, :], across, preferred_element_type=F32
        ) + arrived[part, :].astype(F32)
        n2[part, half:] = value.astype(BF)

        @pl.when(t < rows // TILE)
        def _():
            own_f[part, :] = value[:, 0:fc]

    loop(tiles, kept_part)

    def low(where, place):
        return n2.at[where, pl.ds(half + place * fc, fc)]

    pieces = [
        post.send(low(other_rows, 1), landed.at[2], (d, r ^ 1, c ^ 2)),
        post.send(low(other_rows, 0), landed.at[0], (d, r ^ 1, c)),
        post.send(low(own_rows, 1), landed.at[1], (d, r, c ^ 2)),
    ]

    def finish(line, z, got_z, dests):
        def one(t):
            value = line.total(z, got_z, at(t, 64))
            for dest, lanes in dests:
                dest[at(t, 64), :] = value[:, lanes]

        loop(z.shape[1] // 64, one)

    line_a.rest()

    for copy in pieces:
        copy.wait_recv()

    def inner_sum(t):
        part = at(t, 128)
        value = own_f[part, :]
        for n in range(3):
            value = value + landed[n, part, :].astype(F32)
        own_f[part, :] = value
        inner = value * gain_ref[...] * x_ref[part, :].astype(F32)
        sums[0, :, part] = as_row(jnp.sum(inner, axis=1, keepdims=True))

    loop(rows // 128, inner_sum)
    small = [post.send(sums.at[0], sums.at[m], (d, r, c ^ m)) for m in (1, 2, 3)]
    seat = ROW * d + r
    gain_part = jnp.zeros((1, fc), F32)

    def gain_sum(t, total):
        part = at(t, 128)
        value = own_f[part, :] * x_ref[part, :].astype(F32) * scale_ref[part, :]
        return total + jnp.sum(value, axis=0, keepdims=True)

    gain_part = lax.fori_loop(0, rows // 128, gain_sum, gain_part)
    gsum[seat, 0:1, :] = gain_part
    gsum[seat, 1:2, :] = gain_two_ref[...]
    gsum[seat, 2:8, :] = jnp.zeros((6, fc), F32)
    gain_sent = post.take(8)
    gain_got = gain_sent

    def gain_copy(n, j, a):
        return raw(gsum.at[seat], gsum.at[seat], gain_sent + n, gain_got + seat, (d ^ j, r ^ a, c))

    far = [(j, a) for j in range(DP) for a in (0, 1) if (j, a) != (0, 0)]
    for n, (j, a) in enumerate(far):
        gain_copy(n, j, a).start()
    owners.start_near()
    owners.combine(lambda kind, j: n1.at[pl.ds(j * fc, fc), pl.ds(kind * units, units)], 0)


    for copy in kvs:
        copy.wait_recv()
    line_b.begin()
    line_b.rest()
    finish(line_a, zq, rq, ((query_out, slice(None)),))
    finish(line_a, zo, ro, ((out_out, slice(None)),))
    finish(line_b, zkv, rkv, ((key_out, slice(0, width)), (value_out, slice(width, None))))
    for copy in small:
        copy.wait_recv()

    def finish_tokens(t):
        part = at(t, 128)
        inner = as_column(sums[0, :, part] + sums[2, :, part] + sums[1, :, part] + sums[3, :, part])
        scale_rows = scale_ref[part, :]
        value = x_ref[part, :].astype(F32)
        tokens_out[part, :] = (
            mid_ref[part, :] + scale_rows * (own_f[part, :] * gain_ref[...])
            - value * (scale_rows * scale_rows * scale_rows * inner / D)
        )

    loop(rows // 128, finish_tokens)

    for e in range(2 * DP):
        @pl.when(e != seat)
        def _(e=e):
            raw(gsum.at[e], gsum.at[e], gain_sent, gain_got + e, me).wait_recv()

    gains = gsum[0]
    for e in range(1, 2 * DP):
        gains = gains + gsum[e]
    gains_out[...] = gains

    owners.settle()
    line_a.settle()
    line_b.settle()
    for copy in [beside, beyond, corner] + shared + qs + kvs + [to_sibling] + pieces + small:
        copy.wait_send()
    for n, (j, a) in enumerate(far):
        gain_copy(n, j, a).wait_send()

    @pl.when(d > 0)
    def _():
        for copy in spills:
            copy.wait_send()


def backward(x, gain, scale, mid, gain_two, weight_in, weight_out, q, kv, att, lse, begin, normed, n2, dgate, dup):
    rows, fc = x.shape
    group = 2 * rows
    width = q.shape[1]
    units = dgate.shape[1]
    vmem = pl.BlockSpec(memory_space=pltpu.VMEM)
    hbm = pl.BlockSpec(memory_space=pl.ANY)

    def like(shape, dtype=BF):
        return jax.ShapeDtypeStruct(shape, dtype)

    return pl.pallas_call(
        backward_kernel,
        in_specs=[vmem] * 12 + [hbm] * 4,
        out_specs=[vmem] * 6 + [hbm] * 2,
        out_shape=[
            like((rows, fc), F32),
            like((fc, width), F32),
            like((fc, width), F32),
            like((fc, width), F32),
            like((width, fc), F32),
            like((8, fc), F32),
            like((2, 3, fc, units)),
            like((2, 2, fc, units)),
        ],
        scratch_shapes=[
            pltpu.VMEM((group, D), BF),
            pltpu.VMEM((group, D), BF),
            pltpu.VMEM((2 * group, units), BF),
            pltpu.VMEM((group, D), BF),
            pltpu.VMEM((group, width), BF),
            pltpu.VMEM((group, 3 * width), BF),
            pltpu.VMEM((group + REACH, 2 * width), F32),
            pltpu.VMEM((width // HEAD_DIM, REACH, 2 * HEAD_DIM), BF),
            pltpu.VMEM((width // HEAD_DIM, REACH, 2 * HEAD_DIM), BF),
            pltpu.VMEM((2, COL, fc, units), BF),
            pltpu.VMEM((rows, fc), F32),
            pltpu.VMEM((group, 2 * fc), BF),
            pltpu.VMEM((3, rows, fc), BF),
            pltpu.VMEM((DP, fc, width), BF),
            pltpu.VMEM((DP, width, fc), BF),
            pltpu.VMEM((DP, fc, 2 * width), BF),
            pltpu.VMEM((DP + 1, fc, width), BF),
            pltpu.VMEM((DP + 1, width, fc), BF),
            pltpu.VMEM((DP + 1, fc, 2 * width), BF),
            pltpu.VMEM((4, 8, rows), F32),
            pltpu.VMEM((2 * DP, 8, fc), F32),
            pltpu.SemaphoreType.DMA((POSTS,)),
            pltpu.SemaphoreType.DMA((POSTS,)),
            pltpu.SemaphoreType.DMA((8,)),
        ],
        compiler_params=pltpu.CompilerParams(
            collective_id=2, has_side_effects=True, vmem_limit_bytes=62 << 20
        ),
        cost_estimate=pl.CostEstimate(
            flops=12 * group * D * width + 4 * group * D * units, bytes_accessed=64 << 20, transcendentals=0
        ),
    )(x, gain, scale, mid, gain_two, weight_in, weight_out, q, kv, att, lse, begin, normed, n2, dgate, dup)


def on_small_mesh(
    tokens,
    cotangent,
    query_master,
    key_master,
    value_master,
    out_master,
    gate_master,
    up_master,
    down_master,
    attn_gain,
    ffn_gain,
    lengths,
    permutation,
):
    del permutation
    (
        normed_one, weight_in, weight_out, q, key_value, own_attended, lse, mid, scale_two,
        n2, begin, scale_one, weight_gate, weight_up, grad_all,
    ) = forward(
        tokens, attn_gain[None, :], ffn_gain[None, :], lengths, query_master, key_master,
        value_master, out_master, gate_master, up_master, cotangent,
    )
    normed_two, grad_gate, grad_up, grad_mid, gain_two_part, got_down, _ = middle(
        n2, mid, scale_two, ffn_gain[None, :], cotangent, down_master, weight_gate, weight_up, grad_all
    )
    grad_tokens, grad_query, grad_key, grad_value, grad_out, gains, got, _ = backward(
        tokens, attn_gain[None, :], scale_one, grad_mid, gain_two_part, weight_in, weight_out, q,
        key_value, own_attended, lse, begin, normed_one, normed_two, grad_gate, grad_up,
    )

    def whole(pieces):
        return pieces[0].astype(F32) + pieces[1].astype(F32) + pieces[2].astype(F32)

    return (
        grad_tokens,
        grad_query,
        grad_key,
        grad_value,
        grad_out,
        whole(got[0]),
        whole(got[1]),
        whole(got_down[0]),
        gains[0],
        gains[1],
    )


def solution(mesh):
    placed = (
        P(("dp", "row"), "col"),
        P(("dp", "row"), "col"),
        P("col", ("row", "dp")),
        P("col", ("row", "dp")),
        P("col", ("row", "dp")),
        P(("row", "dp"), "col"),
        P("col", ("row", "dp")),
        P("col", ("row", "dp")),
        P(("row", "dp"), "col"),
        P("col"),
        P("col"),
        P(),
        P(),
    )
    small = tuple(mesh.shape[name] for name in AXES) == (DP, ROW, COL)
    return jax.shard_map(
        on_small_mesh if small else on_any_mesh,
        mesh=mesh,
        in_specs=placed,
        out_specs=(
            P(("dp", "row"), "col"),
            P("col", ("row", "dp")),
            P("col", ("row", "dp")),
            P("col", ("row", "dp")),
            P(("row", "dp"), "col"),
            P("col", ("row", "dp")),
            P("col", ("row", "dp")),
            P(("row", "dp"), "col"),
            P("col"),
            P("col"),
        ),
        check_vma=False,
    )
```

```python
import functools

import jax
import jax.numpy as jnp
from jax import lax
from jax.experimental import pallas as pl
from jax.experimental.pallas import tpu as pltpu
from jax.sharding import PartitionSpec as P

D = 2048
HEAD_DIM = 128


EPSILON = 1e-06
NEG_FILL = -1e30
AXES = ("dp", "row", "col")
DP, ROW, COL = 4, 2, 4
REACH = 768
BF = jnp.bfloat16
F32 = jnp.float32


def running_sum(lengths):
    count = lengths.shape[0]
    earlier = jnp.arange(count)[:, None] <= jnp.arange(count)[None, :]
    return jnp.sum(jnp.where(earlier, lengths[:, None], 0), axis=0)

def make_picker(wanted, carried, pieces):
    amount = pieces[0].shape[0]
    inside = (wanted >= 0) & (wanted < amount)
    chosen = jnp.clip(wanted, 0, amount - 1)
    return tuple(
        (
            jnp.where(inside[:, None], jnp.take(shard_rows, chosen, axis=0), current)
            for shard_rows, current in zip(pieces, carried)
        )
    )


def sequence_marks(permutation, lengths, first_slot, amount):
    source = lax.dynamic_slice_in_dim(permutation, first_slot, amount)
    seq_ends = running_sum(lengths)
    passed = seq_ends[None, :] <= source[:, None]
    member = jnp.sum(passed.astype(jnp.int32), axis=1)
    begins = jnp.max(jnp.where(passed, seq_ends[None, :], 0), axis=1)
    return (member, source - begins)


def col_total(values):
    return lax.psum(jnp.sum(values, axis=1), "col")


def row_gather(values):
    return lax.all_gather(values, "row", axis=0, tiled=True)


def col_gather(values):
    return lax.all_gather(values, "col", axis=0, tiled=True)


def key_gather(keys_here, values_here):
    return (
        lax.all_gather(keys_here, "col", axis=0, tiled=True),
        lax.all_gather(values_here, "col", axis=0, tiled=True),
    )


def multiply(row_block, weight, transpose_right):
    if transpose_right:
        return lax.dot_general(
            row_block, weight, (((1,), (1,)), ((), ())), preferred_element_type=jnp.float32
        )
    return jnp.dot(row_block, weight, preferred_element_type=jnp.float32)


def outer_sum(left_rows, right_rows):
    return lax.dot_general(
        left_rows, right_rows, (((0,), (0,)), ((), ())), preferred_element_type=jnp.float32
    )


def col_reduce(spread, weight, transpose_right):
    return lax.psum_scatter(
        multiply(spread, weight, transpose_right), "col", scatter_dimension=0, tiled=True
    )


def row_reduce(spread, weight, transpose_right):
    return lax.psum_scatter(
        multiply(spread, weight, transpose_right), "row", scatter_dimension=0, tiled=True
    )


def visible(query_member, query_position, member, position):
    same = query_member[:, None] == member[None, :]
    behind = position[None, :] <= query_position[:, None]
    return same & behind


def attend_scores(query_block, key_all, allowed):
    scores = jnp.einsum(
        "qhd,khd->hqk", query_block, key_all, preferred_element_type=jnp.float32
    ) * HEAD_DIM ** (-0.5)
    return jnp.where(allowed[None, :, :], scores, NEG_FILL)


def norm_back(grad_normed, inputs_f, scale_rows, gain):
    gain_part = jnp.sum(grad_normed * inputs_f * scale_rows[:, None], axis=0)
    scaled = grad_normed * gain[None, :]
    inner = col_total(scaled * inputs_f)
    grad_inputs = scale_rows[:, None] * scaled - inputs_f * (scale_rows**3 * inner / D)[:, None]
    return (grad_inputs, gain_part)


def on_any_mesh(
    tokens,
    cotangent,
    query_master,
    key_master,
    value_master,
    out_master,
    gate_master,
    up_master,
    down_master,
    attn_gain,
    ffn_gain,
    lengths,
    permutation,
):
    own_rows = tokens.shape[0]
    group_rows = own_rows * lax.axis_size("row")
    quarter = group_rows // lax.axis_size("col")
    device_slot = lax.axis_index(("dp", "row"))
    group_slot = lax.axis_index("dp")
    col_slot = lax.axis_index("col")
    own_sources = lax.dynamic_slice_in_dim(permutation, device_slot * own_rows, own_rows)
    own_tokens, own_cotangent = make_picker(
        own_sources,
        (jnp.zeros_like(tokens), jnp.zeros_like(cotangent)),
        (
            lax.all_gather(tokens, ("dp", "row"), axis=0, tiled=True),
            lax.all_gather(cotangent, ("dp", "row"), axis=0, tiled=True),
        ),
    )
    masters = tuple(
        (
            matrix.astype(jnp.bfloat16)
            for matrix in (
                query_master,
                key_master,
                value_master,
                out_master,
                gate_master,
                up_master,
                down_master,
            )
        )
    )
    query_weight, key_weight, value_weight, out_weight, gate_weight, up_weight, down_weight = (
        lax.all_gather(masters[0], "dp", axis=1, tiled=True),
        lax.all_gather(masters[1], "dp", axis=1, tiled=True),
        lax.all_gather(masters[2], "dp", axis=1, tiled=True),
        lax.all_gather(masters[3], "dp", axis=0, tiled=True),
        lax.all_gather(masters[4], "dp", axis=1, tiled=True),
        lax.all_gather(masters[5], "dp", axis=1, tiled=True),
        lax.all_gather(masters[6], "dp", axis=0, tiled=True),
    )
    attention_in = jnp.concatenate([query_weight, key_weight, value_weight], axis=1)
    feedforward_in = jnp.concatenate([gate_weight, up_weight], axis=1)
    width_row = query_weight.shape[1]
    heads_row = width_row // HEAD_DIM
    hidden_row = gate_weight.shape[1]
    member, position = sequence_marks(permutation, lengths, group_slot * group_rows, group_rows)
    query_member = lax.dynamic_slice_in_dim(member, col_slot * quarter, quarter)
    query_position = lax.dynamic_slice_in_dim(position, col_slot * quarter, quarter)
    block_rows = min(512, quarter)
    block_count = quarter // block_rows
    residual_in = own_tokens.astype(jnp.float32)
    scale_one = lax.rsqrt(col_total(residual_in * residual_in) / D + EPSILON)
    normed_one = (residual_in * scale_one[:, None] * attn_gain[None, :]).astype(jnp.bfloat16)
    spread_one = row_gather(normed_one)
    projected = col_reduce(spread_one, attention_in, False).astype(jnp.bfloat16)
    queries = projected[:, :width_row].reshape(quarter, heads_row, HEAD_DIM)
    keys_here = projected[:, width_row : 2 * width_row]
    values_here = projected[:, 2 * width_row :]
    key_flat, value_flat = key_gather(keys_here, values_here)
    key_all = key_flat.reshape(group_rows, heads_row, HEAD_DIM)
    value_all = value_flat.reshape(group_rows, heads_row, HEAD_DIM)

    def block_mask(first_row):
        return visible(
            lax.dynamic_slice_in_dim(query_member, first_row, block_rows),
            lax.dynamic_slice_in_dim(query_position, first_row, block_rows),
            member,
            position,
        )

    def forward_block(block_id):
        first_row = block_id * block_rows
        query_block = lax.dynamic_slice_in_dim(queries, first_row, block_rows, 0)
        scores = attend_scores(query_block, key_all, block_mask(first_row))
        highest = jnp.max(scores, axis=2, keepdims=True)
        totals = jnp.sum(jnp.exp(scores - highest), axis=2, keepdims=True)
        log_total = highest + jnp.log(totals)
        probability = jnp.exp(scores - log_total)
        output = jnp.einsum(
            "hqk,khd->qhd",
            probability.astype(jnp.bfloat16),
            value_all,
            preferred_element_type=jnp.float32,
        )
        return (output.astype(jnp.bfloat16).reshape(block_rows, width_row), log_total[:, :, 0])

    blocks_out, log_totals = lax.map(forward_block, jnp.arange(block_count, dtype=jnp.int32))
    attended = blocks_out.reshape(quarter, width_row)
    spread_attn = col_gather(attended)
    midway = residual_in + row_reduce(spread_attn, out_weight, False)
    scale_two = lax.rsqrt(col_total(midway * midway) / D + EPSILON)
    normed_two = (midway * scale_two[:, None] * ffn_gain[None, :]).astype(jnp.bfloat16)
    spread_two = row_gather(normed_two)
    gate_and_up = col_reduce(spread_two, feedforward_in, False)
    gate_value = gate_and_up[:, :hidden_row]
    up_value = gate_and_up[:, hidden_row:]
    sigmoid_gate = jax.nn.sigmoid(gate_value)
    hidden = (gate_value * sigmoid_gate * up_value).astype(jnp.bfloat16)
    grad_output = own_cotangent.astype(jnp.float32)
    spread_down = row_gather(own_cotangent)
    grad_hidden = col_reduce(spread_down, down_weight, True)
    spread_hidden = col_gather(hidden)
    grad_down = outer_sum(spread_hidden, spread_down)
    grad_gate_value = (
        grad_hidden * up_value * sigmoid_gate * (1.0 + gate_value * (1.0 - sigmoid_gate))
    ).astype(jnp.bfloat16)
    grad_up_value = (grad_hidden * gate_value * sigmoid_gate).astype(jnp.bfloat16)
    spread_gate_up = col_gather(jnp.concatenate([grad_gate_value, grad_up_value], axis=1))
    grad_normed_two = row_reduce(spread_gate_up, feedforward_in, True)
    spread_two = row_gather(normed_two)
    grad_feedforward = outer_sum(spread_two, spread_gate_up)
    grad_mid_norm, gain_two_part = norm_back(grad_normed_two, midway, scale_two, ffn_gain)
    grad_midway = grad_output + grad_mid_norm
    rounded_midway = grad_midway.astype(jnp.bfloat16)
    spread_back = row_gather(rounded_midway)
    grad_attended = col_reduce(spread_back, out_weight, True).astype(jnp.bfloat16)
    spread_attn = col_gather(attended)
    key_flat, value_flat = key_gather(keys_here, values_here)
    key_all = key_flat.reshape(group_rows, heads_row, HEAD_DIM)
    value_all = value_flat.reshape(group_rows, heads_row, HEAD_DIM)
    grad_out_local = outer_sum(spread_attn, spread_back)

    def backward_block(carried, block_id):
        first_row = block_id * block_rows
        query_block = lax.dynamic_slice_in_dim(queries, first_row, block_rows, 0)
        scores = attend_scores(query_block, key_all, block_mask(first_row))
        probability = jnp.exp(
            scores - lax.dynamic_index_in_dim(log_totals, block_id, 0, keepdims=False)[:, :, None]
        )
        weights_low = probability.astype(jnp.bfloat16)
        grad_block = lax.dynamic_slice_in_dim(grad_attended, first_row, block_rows, 0).reshape(
            block_rows, heads_row, HEAD_DIM
        )
        grad_soft = jnp.einsum(
            "qhd,khd->hqk", grad_block, value_all, preferred_element_type=jnp.float32
        )
        row_inner = jnp.sum(probability * grad_soft, axis=2, keepdims=True)
        grad_scores = (probability * (grad_soft - row_inner)).astype(jnp.bfloat16)
        grad_query_block = jnp.einsum(
            "hqk,khd->qhd", grad_scores, key_all, preferred_element_type=jnp.float32
        ) * HEAD_DIM ** (-0.5)
        grad_key_all = carried[0] + jnp.einsum(
            "hqk,qhd->khd", grad_scores, query_block, preferred_element_type=jnp.float32
        ) * HEAD_DIM ** (-0.5)
        grad_value_all = carried[1] + jnp.einsum(
            "hqk,qhd->khd", weights_low, grad_block, preferred_element_type=jnp.float32
        )
        return (
            (grad_key_all, grad_value_all),
            grad_query_block.astype(jnp.bfloat16).reshape(block_rows, width_row),
        )

    start_grads = jnp.zeros((group_rows, heads_row, HEAD_DIM), jnp.float32)
    key_value_grads, grad_queries = lax.scan(
        backward_block, (start_grads, start_grads), jnp.arange(block_count, dtype=jnp.int32)
    )
    grad_queries = grad_queries.reshape(quarter, width_row)
    grad_key_part = key_value_grads[0].reshape(group_rows, width_row)
    grad_value_part = key_value_grads[1].reshape(group_rows, width_row)
    grad_key_mine, grad_value_mine = (
        lax.psum_scatter(grad_key_part, "col", scatter_dimension=0, tiled=True),
        lax.psum_scatter(grad_value_part, "col", scatter_dimension=0, tiled=True),
    )
    spread_projected = col_gather(
        jnp.concatenate(
            [
                grad_queries,
                grad_key_mine.astype(jnp.bfloat16),
                grad_value_mine.astype(jnp.bfloat16),
            ],
            axis=1,
        )
    )
    grad_normed_one = row_reduce(spread_projected, attention_in, True)
    spread_one = row_gather(normed_one)
    grad_attention = outer_sum(spread_one, spread_projected)
    grad_in_norm, gain_one_part = norm_back(grad_normed_one, residual_in, scale_one, attn_gain)
    grad_own_tokens = grad_midway + grad_in_norm
    grad_attn_gain, grad_ffn_gain = lax.psum((gain_one_part, gain_two_part), ("dp", "row"))
    grad_query, grad_key, grad_value, grad_out, grad_gate, grad_up, grad_down_mine = (
        lax.psum_scatter(
            grad_attention[:, :width_row].astype(jnp.bfloat16),
            "dp",
            scatter_dimension=1,
            tiled=True,
        ).astype(jnp.float32),
        lax.psum_scatter(
            grad_attention[:, width_row : 2 * width_row].astype(jnp.bfloat16),
            "dp",
            scatter_dimension=1,
            tiled=True,
        ).astype(jnp.float32),
        lax.psum_scatter(
            grad_attention[:, 2 * width_row :].astype(jnp.bfloat16),
            "dp",
            scatter_dimension=1,
            tiled=True,
        ).astype(jnp.float32),
        lax.psum_scatter(
            grad_out_local.astype(jnp.bfloat16), "dp", scatter_dimension=0, tiled=True
        ).astype(jnp.float32),
        lax.psum_scatter(
            grad_feedforward[:, :hidden_row].astype(jnp.bfloat16),
            "dp",
            scatter_dimension=1,
            tiled=True,
        ).astype(jnp.float32),
        lax.psum_scatter(
            grad_feedforward[:, hidden_row:].astype(jnp.bfloat16),
            "dp",
            scatter_dimension=1,
            tiled=True,
        ).astype(jnp.float32),
        lax.psum_scatter(
            grad_down.astype(jnp.bfloat16), "dp", scatter_dimension=0, tiled=True
        ).astype(jnp.float32),
    )
    total_tokens = permutation.shape[0]
    inverse = (
        jnp.zeros((total_tokens,), jnp.int32)
        .at[permutation]
        .set(jnp.arange(total_tokens, dtype=jnp.int32))
    )
    wanted_slots = lax.dynamic_slice_in_dim(inverse, device_slot * own_rows, own_rows)
    (grad_tokens,) = make_picker(
        wanted_slots,
        (jnp.zeros_like(grad_own_tokens),),
        (
            (
                lax.all_gather(
                    grad_own_tokens.astype(jnp.bfloat16), ("dp", "row"), axis=0, tiled=True
                ),
            )[0].astype(jnp.float32),
        ),
    )
    return (
        grad_tokens,
        grad_query,
        grad_key,
        grad_value,
        grad_out,
        grad_gate,
        grad_up,
        grad_down_mine,
        grad_attn_gain,
        grad_ffn_gain,
    )


def scores_of(query, key):
    return lax.dot_general(
        query, key, (((1,), (1,)), ((), ())), preferred_element_type=F32
    ) * HEAD_DIM ** (-0.5)


MESH = pl.DeviceIdType.MESH
PLACE = {0: 0, 2: 1, 1: 2, 3: 3}
TILE = 256


class Post:
    def __init__(self, send_sem, recv_sem):
        self.send_sem, self.recv_sem, self.used = send_sem, recv_sem, 0

    def ready(self, src, dst, target, slot=None):
        if slot is None:
            slot = self.used
            self.used += 1
        return pltpu.make_async_remote_copy(
            src_ref=src,
            dst_ref=dst,
            send_sem=self.send_sem.at[slot],
            recv_sem=self.recv_sem.at[slot],
            device_id=target,
            device_id_type=MESH,
        )

    def take(self, count):
        first = self.used
        self.used += count
        return first

    def send(self, src, dst, target):
        copy = self.ready(src, dst, target)
        copy.start()
        return copy


def greet(peers):
    barrier = pltpu.get_barrier_semaphore()
    for peer in peers:
        pl.semaphore_signal(barrier, inc=1, device_id=peer, device_id_type=MESH)
    pl.semaphore_wait(barrier, len(peers))


def as_row(column):
    return jnp.transpose(jnp.broadcast_to(column, (column.shape[0], 128)))[0:8]


def as_column(row):
    return jnp.transpose(row)[:, 0:1]


def forward_kernel(
    x_ref, gain_one_ref, gain_two_ref, lengths_ref, query_ref, key_ref, value_ref, out_ref, gate_hbm, up_hbm,
    own_grad,
    mid_ref, scale_ref, n2_ref, begin_ref, first_scale,
    normed_out, weight_in_out, weight_out_out, q_out, kv_out, att_out, lse_out, own_up, gate_all, up_all, grad_all,
    normed_ref, weight_in, weight_out, q_ref, kv_ref, att_ref, lse_ref, masters,
    zin, zout, sums, wide, given, arrived, low, landed, x32, hidden_own,
    send_sem, recv_sem, local_sem,
):
    d, r, c = (lax.axis_index(name) for name in AXES)
    y, core = c // 2, lax.rem(c, 2)
    rows = x_ref.shape[0]
    fc = x_ref.shape[1]
    group = 2 * rows
    width = q_ref.shape[1]
    half = 2 * fc
    post = Post(send_sem, recv_sem)
    fetches = [
        pltpu.make_async_copy(src, masters.at[n], local_sem.at[8 + n]) for n, src in enumerate((gate_hbm, up_hbm))
    ]
    for copy in fetches:
        copy.start()
    copies = []

    def copy_out(src, dst):
        copy = pltpu.make_async_copy(src, dst, local_sem.at[10 + len(copies)])
        copy.start()
        copies.append(copy)

    in_plane = [(d, r ^ a, c ^ b) for a in (0, 1) for b in range(COL) if (a, b) != (0, 0)]
    greet([(d ^ j, r, c) for j in (1, 2, 3)] + in_plane)

    def fill_x(t, total):
        part = pl.ds(pl.multiple_of(t * 128, 128), 128)
        value = x_ref[part, :].astype(F32)
        x32[part, :] = value
        sums[0, :, part] = as_row(jnp.sum(value * value, axis=1, keepdims=True))
        return total

    lax.fori_loop(0, rows // 128, fill_x, 0)
    small = [post.send(sums.at[0], sums.at[m], (d, r, c ^ m)) for m in (1, 2, 3)]

    parts = (pl.ds(width, 2 * width), pl.ds(0, width))
    first, first_down = post.take(3 * DP), post.take(3 * DP)

    def block_of(n, p):
        return zin.at[p, :, parts[n]] if n < 2 else zout.at[p]

    def line(n, p, target_plane):
        block = block_of(n, p)
        return post.ready(block, block, (target_plane, r, c), first + DP * n + p)

    def line_down(n, p, target_plane):
        block = block_of(n, p)
        return pltpu.make_async_remote_copy(
            src_ref=block, dst_ref=block,
            send_sem=send_sem.at[first_down + DP * n + p], recv_sem=recv_sem.at[first + DP * n + p],
            device_id=(target_plane, r, c), device_id_type=MESH,
        )

    def cast_rows(src, dst, amount, step=64):
        def one(t, total):
            part = pl.ds(pl.multiple_of(t * step, step), step)
            dst(part, src[part, :].astype(BF))
            return total

        lax.fori_loop(0, amount // step, one, 0)

    for place, master in enumerate((query_ref, key_ref, value_ref)):
        def put(part, value, place=place):
            zin[d, part, place * width : (place + 1) * width] = value

        cast_rows(master, put, fc)
    def leave(n):
        @pl.when(d < DP - 1)
        def _():
            line(n, d, d + 1).start()

        @pl.when(d > 0)
        def _():
            line_down(n, d, d - 1).start()

    leave(0)
    leave(1)

    first_cols = post.take(3 * DP)

    def place_of(m):
        return lax.rem(m, 2) * 2 + m // 2

    def seat_of(n, place):
        there = pl.ds(pl.multiple_of(place * fc, fc), fc)
        return weight_in.at[there, parts[n]] if n < 2 else weight_out.at[:, there]

    def to_column(n, p):
        return pltpu.make_async_remote_copy(
            src_ref=block_of(n, p),
            dst_ref=seat_of(n, place_of(p ^ c)),
            send_sem=send_sem.at[first_cols + DP * n + p],
            recv_sem=recv_sem.at[first_cols + DP * n + (p ^ c)],
            device_id=(d, r, p), device_id_type=MESH,
        )

    def keep(n):
        return pltpu.make_async_copy(block_of(n, c), seat_of(n, 0), local_sem.at[(0, 1, 5)[n]])

    def pass_on(n, p):
        @pl.when(p == c)
        def _():
            keep(n).start()

        @pl.when(p != c)
        def _():
            to_column(n, p).start()

    hidden_all = (gate_all, up_all)
    first_sent = post.take(10)
    first_got = first_sent

    def slab(kind, i):
        return hidden_all[kind].at[pl.ds(pl.multiple_of(place_of(i) * fc, fc), fc), :]

    def ship(kind, way, i, target, src=None):
        return pltpu.make_async_remote_copy(
            src_ref=hidden_own.at[kind] if src is None else src,
            dst_ref=slab(kind, i),
            send_sem=send_sem.at[first_sent + 5 * kind + way],
            recv_sem=recv_sem.at[first_got + 4 * kind + i],
            device_id=target, device_id_type=MESH,
        )

    def keep_hidden(kind):
        return pltpu.make_async_copy(hidden_own.at[kind], slab(kind, 0), local_sem.at[3 + kind])

    def to_core(kind):
        return ship(kind, 0, 1, (d, r, c ^ 1))

    def over_y(kind):
        return ship(kind, 1, 2 + core, (d, r, 2 * (1 - y)))

    def over_x(kind):
        return ship(kind, 2, 1 - core, (d, r ^ 1, 2 * y + 1))

    def relay(kind, i):
        return ship(kind, i + 1, 5 - i, (d, r ^ 1, 2 * y + 1), slab(kind, i))

    def start_home(kind):
        @pl.when(core == 0)
        def _():
            keep_hidden(kind).start()

        @pl.when(core == 1)
        def _():
            to_core(kind).start()

    def start_relay(kind):
        @pl.when(core == 0)
        def _():
            for i in (2, 3):
                ship(kind, 0, i, (d, r, c)).wait_recv()
                relay(kind, i).start()

    def cast_hidden(kind):
        def put(part, value):
            hidden_own[kind, part, :] = value

        fetches[kind].wait()
        cast_rows(masters.at[kind], put, fc)

    cast_hidden(0)
    over_x(0).start()
    over_y(0).start()
    for copy in small:
        copy.wait_recv()

    def norm_one(t, total):
        part = pl.ds(pl.multiple_of(t * 128, 128), 128)
        square = sums[0, :, part] + sums[2, :, part] + sums[1, :, part] + sums[3, :, part]
        scale = lax.rsqrt(as_column(square) / D + EPSILON)
        first_scale[part, :] = scale
        normed_ref[part, 0:fc] = (x32[part, :] * scale * gain_one_ref[...]).astype(BF)
        return total

    lax.fori_loop(0, rows // 128, norm_one, 0)
    own_rows, other_rows = pl.ds(0, rows), pl.ds(rows, rows)

    def columns(place):
        return pl.ds(place * fc, fc)

    own_block = normed_ref.at[own_rows, columns(0)]
    beside = post.send(own_block, normed_ref.at[other_rows, columns(0)], (d, r ^ 1, c))
    beyond = post.send(own_block, normed_ref.at[own_rows, columns(1)], (d, r, c ^ 2))
    corner = post.send(own_block, normed_ref.at[other_rows, columns(1)], (d, r ^ 1, c ^ 2))
    sibling = (d, r, c ^ 1)
    shared = [post.send(own_block, normed_ref.at[own_rows, columns(2)], sibling)]
    pass_on(0, d)
    pass_on(1, d)
    cast_hidden(1)
    start_home(0)
    start_home(1)
    copy_out(hidden_own.at[1], own_up)
    over_x(1).start()
    half_rows = rows // 2
    grad_cross = post.send(
        own_grad.at[pl.ds(pl.multiple_of((1 - y) * half_rows, half_rows), half_rows), :],
        grad_all.at[pl.ds(0, half_rows), pl.ds(fc, fc)],
        (d, r, c ^ 2),
    )
    grad_keep = pltpu.make_async_copy(
        own_grad.at[pl.ds(pl.multiple_of(y * half_rows, half_rows), half_rows), :],
        grad_all.at[pl.ds(0, half_rows), pl.ds(0, fc)],
        local_sem.at[2],
    )
    grad_keep.start()

    def put_out(part, value):
        zout[d, part, :] = value

    cast_rows(out_ref, put_out, width)

    def find_begins(t, total):
        part = pl.ds(pl.multiple_of(t * 128, 128), 128)
        place = lax.broadcasted_iota(jnp.int32, (128, 1), 0) + (d * group + t * 128)
        end = jnp.int32(0)
        begin = jnp.zeros((128, 1), jnp.int32)
        for n in range(lengths_ref.shape[0]):
            end = end + lengths_ref[n]
            begin = jnp.where(place >= end, end, begin)
        begin_ref[part, :] = begin - d * group
        return total

    lax.fori_loop(0, group // 128, find_begins, 0)

    def line_step(s, which=(0, 1)):
        for n in which:
            for p, valid, onward, forward in (
                (d - s, d - s >= 0, d < DP - 1, lambda n, p: line(n, p, d + 1)),
                (d + s, d + s < DP, d > 0, lambda n, p: line_down(n, p, d - 1)),
            ):
                @pl.when(valid)
                def _(n=n, p=p, onward=onward, forward=forward):
                    line(n, p, d).wait_recv()

                    @pl.when(onward)
                    def _():
                        forward(n, p).start()

                    pass_on(n, p)

    line_step(1)
    leave(2)
    line_step(2)
    pass_on(2, d)
    line_step(1, (2,))
    for copy, where, place in ((beside, other_rows, 0), (beyond, own_rows, 1), (corner, other_rows, 1)):
        copy.wait_recv()
        shared.append(
            post.send(normed_ref.at[where, columns(place)], normed_ref.at[where, columns(place + 2)], sibling)
        )
    line_step(3)
    line_step(2, (2,))
    start_relay(0)

    def arrived_blocks(n):
        keep(n).wait()
        for m in (1, 2, 3):
            pltpu.make_async_remote_copy(
                src_ref=block_of(n, 0), dst_ref=seat_of(n, 0),
                send_sem=send_sem.at[first_cols], recv_sem=recv_sem.at[first_cols + DP * n + m],
                device_id=(d, r, c), device_id_type=MESH,
            ).wait_recv()

    for copy in shared:
        copy.wait_recv()
    arrived_blocks(0)
    copy_out(normed_ref, normed_out)

    def turned(t):
        return lax.rem(t + 2 * r, group // TILE)

    def project_kv(t, total):
        part = pl.ds(pl.multiple_of(t * TILE, TILE), TILE)
        to = pl.ds(pl.multiple_of(REACH + turned(t) * TILE, TILE), TILE)
        kv_ref[to, :] = jnp.dot(
            normed_ref[part, :], weight_in[:, width:], preferred_element_type=F32
        ).astype(BF)
        return total

    lax.fori_loop(0, group // TILE, project_kv, 0)
    halo = post.ready(kv_ref.at[pl.ds(group, REACH), :], kv_ref.at[pl.ds(0, REACH), :], (lax.rem(d + 1, DP), r, c))

    @pl.when(d < DP - 1)
    def _():
        halo.start()

    arrived_blocks(1)

    def project_q(t, total):
        part = pl.ds(pl.multiple_of(t * TILE, TILE), TILE)
        to = pl.ds(pl.multiple_of(turned(t) * TILE, TILE), TILE)
        q_ref[to, :] = jnp.dot(
            normed_ref[part, :], weight_in[:, :width], preferred_element_type=F32
        ).astype(BF)
        return total

    lax.fori_loop(0, group // TILE, project_q, 0)

    copy_out(weight_in, weight_in_out)
    copy_out(q_ref, q_out)
    line_step(3, (2,))
    grad_cross.wait_recv()
    grad_keep.wait()
    grads = [
        post.send(
            grad_all.at[pl.ds(0, half_rows), pl.ds(0, half)],
            grad_all.at[pl.ds(j * half_rows, half_rows), pl.ds(0, half)],
            (d ^ j, r, c),
        )
        for j in (1, 2, 3)
    ]
    grads_shared = [
        post.send(
            grad_all.at[pl.ds(0, half_rows), pl.ds(0, half)],
            grad_all.at[pl.ds(0, half_rows), pl.ds(half, half)],
            sibling,
        )
    ]

    @pl.when(d == 0)
    def _():
        kv_ref[pl.ds(0, REACH), :] = jnp.zeros((REACH, 2 * width), BF)

    @pl.when(d > 0)
    def _():
        halo.wait_recv()

    copy_out(kv_ref, kv_out)

    span = TILE + REACH
    for h in range(width // HEAD_DIM):
        lanes = pl.ds(h * HEAD_DIM, HEAD_DIM)
        value_lanes = pl.ds(width + h * HEAD_DIM, HEAD_DIM)

        def one(t, total, lanes=lanes, value_lanes=value_lanes):
            part = pl.ds(pl.multiple_of(t * TILE, TILE), TILE)
            to = pl.ds(pl.multiple_of(turned(t) * TILE, TILE), TILE)
            window = pl.ds(pl.multiple_of(t * TILE, TILE), span)
            scores = scores_of(q_ref[part, lanes], kv_ref[window, lanes])
            query = lax.broadcasted_iota(jnp.int32, (TILE, span), 0)
            key = lax.broadcasted_iota(jnp.int32, (TILE, span), 1)
            begin = begin_ref[part, 0:1] + (REACH - t * TILE)
            allowed = (key <= query + REACH) & (key >= begin)
            scores = jnp.where(allowed, scores, NEG_FILL)
            highest = jnp.max(scores, axis=1, keepdims=True)
            expo = jnp.exp(scores - highest)
            total_e = jnp.sum(expo, axis=1, keepdims=True)
            probability = (expo * (1.0 / total_e)).astype(BF)
            att_ref[to, lanes] = jnp.dot(
                probability, kv_ref[window, value_lanes], preferred_element_type=F32
            ).astype(BF)
            lse_ref[part, lanes] = jnp.broadcast_to(highest + jnp.log(total_e), (TILE, HEAD_DIM))
            return total

        lax.fori_loop(0, group // TILE, one, 0)

    copy_out(att_ref, att_out)
    copy_out(lse_ref, lse_out)
    arrived_blocks(2)
    copy_out(weight_out, weight_out_out)

    def out_given(t, total):
        part = pl.ds(pl.multiple_of(t * TILE, TILE), TILE)
        given[part, :] = jnp.dot(
            att_ref[part, :], weight_out[:, half:], preferred_element_type=F32
        ).astype(BF)
        return total

    lax.fori_loop(0, group // TILE, out_given, 0)
    to_sibling = post.send(given, arrived, sibling)

    def out_kept(t, total):
        part = pl.ds(pl.multiple_of(t * TILE, TILE), TILE)
        wide[part, :] = jnp.dot(att_ref[part, :], weight_out[:, :half], preferred_element_type=F32)
        return total

    lax.fori_loop(0, group // TILE, out_kept, 0)
    to_sibling.wait_recv()

    def add_low(t, total):
        part = pl.ds(pl.multiple_of(t * 128, 128), 128)
        value = wide[part, :] + arrived[part, :].astype(F32)
        wide[part, :] = value
        low[part, :] = value.astype(BF)
        return total

    lax.fori_loop(0, group // 128, add_low, 0)
    pieces = [
        post.send(low.at[other_rows, columns(1)], landed.at[2], (d, r ^ 1, c ^ 2)),
        post.send(low.at[other_rows, columns(0)], landed.at[0], (d, r ^ 1, c)),
        post.send(low.at[own_rows, columns(1)], landed.at[1], (d, r, c ^ 2)),
    ]
    for copy in pieces:
        copy.wait_recv()

    def middle(t, total):
        part = pl.ds(pl.multiple_of(t * 128, 128), 128)
        value = (
            x32[part, :] + wide[part, 0:fc] + landed[0, part, :].astype(F32)
            + landed[1, part, :].astype(F32) + landed[2, part, :].astype(F32)
        )
        mid_ref[part, :] = value
        sums[4, :, part] = as_row(jnp.sum(value * value, axis=1, keepdims=True))
        return total

    lax.fori_loop(0, rows // 128, middle, 0)
    again = [post.send(sums.at[4], sums.at[4 + m], (d, r, c ^ m)) for m in (1, 2, 3)]
    for copy in again:
        copy.wait_recv()

    def norm_two(t, total):
        part = pl.ds(pl.multiple_of(t * 128, 128), 128)
        square = sums[4, :, part] + sums[6, :, part] + sums[5, :, part] + sums[7, :, part]
        scale = lax.rsqrt(as_column(square) / D + EPSILON)
        scale_ref[part, :] = scale
        n2_ref[part, :] = (mid_ref[part, :] * scale * gain_two_ref[...]).astype(BF)
        return total

    lax.fori_loop(0, rows // 128, norm_two, 0)

    for j, copy in zip((1, 2, 3), grads):
        copy.wait_recv()
        there = pl.ds(j * half_rows, half_rows)
        grads_shared.append(
            post.send(grad_all.at[there, pl.ds(0, half)], grad_all.at[there, pl.ds(half, half)], sibling)
        )
    for copy in grads_shared:
        copy.wait_recv()
    over_y(0).wait_send()
    for kind in (0, 1):
        over_x(kind).wait_send()

        @pl.when(core == 0)
        def _(kind=kind):
            keep_hidden(kind).wait()
            ship(kind, 0, 1, (d, r, c)).wait_recv()
            if kind == 0:
                for i in (2, 3):
                    relay(kind, i).wait_send()

        @pl.when(core == 1)
        def _(kind=kind):
            to_core(kind).wait_send()
            for i in range(COL if kind == 0 else 2):
                ship(kind, 0, i, (d, r, c)).wait_recv()

    for copy in (
        small + [grad_cross, beside, beyond, corner] + shared + grads + grads_shared
        + [to_sibling] + pieces + again
    ):
        copy.wait_send()

    @pl.when(d < DP - 1)
    def _():
        halo.wait_send()

    for copy in copies:
        copy.wait()
    for n in (0, 1, 2):
        for p in range(DP):
            @pl.when((d < DP - 1) & (p <= d))
            def _(n=n, p=p):
                line(n, p, d).wait_send()

            @pl.when((d > 0) & (p >= d))
            def _(n=n, p=p):
                line_down(n, p, d).wait_send()

            @pl.when(c != p)
            def _(n=n, p=p):
                to_column(n, p).wait_send()


SENDS = 96


def forward(x, gain_one, gain_two, lengths, query, key, value, out, gate, up, own_grad):
    rows, fc = x.shape
    group = 2 * rows
    width = out.shape[0]
    units = gate.shape[1]
    vmem = pl.BlockSpec(memory_space=pltpu.VMEM)
    smem = pl.BlockSpec(memory_space=pltpu.SMEM)
    hbm = pl.BlockSpec(memory_space=pl.ANY)

    def like(shape, dtype=BF):
        return jax.ShapeDtypeStruct(shape, dtype)

    return pl.pallas_call(
        forward_kernel,
        in_specs=[vmem] * 3 + [smem] + [vmem] * 4 + [hbm] * 3,
        out_specs=[vmem] * 5 + [hbm] * 11,
        out_shape=[
            like((rows, fc), F32),
            like((rows, 1), F32),
            like((rows, fc)),
            like((group, 1), jnp.int32),
            like((rows, 1), F32),
            like((group, D)),
            like((D, 3 * width)),
            like((width, D)),
            like((group, width)),
            like((REACH + group, 2 * width)),
            like((group, width)),
            like((group, width), F32),
            like((fc, units)),
            like((D, units)),
            like((D, units)),
            like((group, D)),
        ],
        scratch_shapes=[
            pltpu.VMEM((group, D), BF),
            pltpu.VMEM((D, 3 * width), BF),
            pltpu.VMEM((width, D), BF),
            pltpu.VMEM((group, width), BF),
            pltpu.VMEM((REACH + group, 2 * width), BF),
            pltpu.VMEM((group, width), BF),
            pltpu.VMEM((group, width), F32),
            pltpu.VMEM((2, fc, units), F32),
            pltpu.VMEM((DP, fc, 3 * width), BF),
            pltpu.VMEM((DP, width, fc), BF),
            pltpu.VMEM((8, 8, rows), F32),
            pltpu.VMEM((group, 2 * fc), F32),
            pltpu.VMEM((group, 2 * fc), BF),
            pltpu.VMEM((group, 2 * fc), BF),
            pltpu.VMEM((group, 2 * fc), BF),
            pltpu.VMEM((3, rows, fc), BF),
            pltpu.VMEM((rows, fc), F32),
            pltpu.VMEM((2, fc, units), BF),
            pltpu.SemaphoreType.DMA((SENDS,)),
            pltpu.SemaphoreType.DMA((SENDS,)),
            pltpu.SemaphoreType.DMA((20,)),
        ],
        compiler_params=pltpu.CompilerParams(
            collective_id=1, has_side_effects=True, vmem_limit_bytes=60 << 20
        ),
        cost_estimate=pl.CostEstimate(
            flops=6 * group * D * width, bytes_accessed=64 << 20, transcendentals=0
        ),
    )(x, gain_one, gain_two, lengths, query, key, value, out, gate, up, own_grad)


def at(t, size):
    return pl.ds(pl.multiple_of(t * size, size), size)


def loop(count, body):
    def one(t, total):
        body(t)
        return total

    lax.fori_loop(0, count, one, 0)


def maker(send_sem, recv_sem):
    def raw(src, dst, sent, got_at, target):
        return pltpu.make_async_remote_copy(
            src_ref=src, dst_ref=dst, send_sem=send_sem.at[sent], recv_sem=recv_sem.at[got_at],
            device_id=target, device_id_type=MESH,
        )

    return raw


class LineSum:
    def __init__(self, raw, arrays, base, me):
        self.raw, self.arrays, self.base, self.me = raw, arrays, base, me

    def sem(self, n, p, down):
        return self.base + 8 * n + 4 * down + p

    def take(self, p, down, done):
        d = self.me[0]
        for n, (z, got_z) in enumerate(self.arrays):
            self.raw(z.at[p], got_z.at[p], self.sem(n, p, down), self.sem(n, p, down), self.me).wait_recv()

        @pl.when(jnp.logical_not(done))
        def _():
            for z, got_z in self.arrays:
                def one(t, z=z, got_z=got_z):
                    z[p, at(t, 64), :] = (
                        z[p, at(t, 64), :].astype(F32) + got_z[p, at(t, 64), :].astype(F32)
                    ).astype(BF)

                loop(z.shape[1] // 64, one)

    def up(self, p):
        d, r, c = self.me

        @pl.when((d > 0) & (d <= p))
        def _():
            self.take(p, 0, d == p)

        @pl.when(d < p)
        def _():
            for n, (z, got_z) in enumerate(self.arrays):
                self.raw(z.at[p], got_z.at[p], self.sem(n, p, 0), self.sem(n, p, 0), (d + 1, r, c)).start()

    def down(self, p):
        d, r, c = self.me

        @pl.when((d < DP - 1) & (d >= p))
        def _():
            self.take(p, 1, d == p)

        @pl.when(d > p)
        def _():
            slot = jnp.where(p < d - 1, p, DP)
            for n, (z, got_z) in enumerate(self.arrays):
                self.raw(z.at[p], got_z.at[slot], self.sem(n, p, 1), self.sem(n, p, 1), (d - 1, r, c)).start()

    def begin(self):
        d = self.me[0]

        @pl.when(d == 0)
        def _():
            for p in (3, 2, 1):
                self.up(p)

        @pl.when(d == DP - 1)
        def _():
            for p in (0, 1, 2):
                self.down(p)

    def rest(self):
        d = self.me[0]

        @pl.when(d == 0)
        def _():
            self.down(0)

        @pl.when(d == 1)
        def _():
            self.up(3)
            self.up(2)
            self.down(0)
            self.down(1)
            self.up(1)

        @pl.when(d == 2)
        def _():
            self.down(0)
            self.down(1)
            self.up(3)
            self.up(2)
            self.down(2)

        @pl.when(d == DP - 1)
        def _():
            self.up(3)

    def settle(self):
        d = self.me[0]
        for p in range(DP):
            for n, (z, got_z) in enumerate(self.arrays):
                for down, sent in ((0, d < p), (1, d > p)):
                    @pl.when(sent)
                    def _(p=p, n=n, z=z, got_z=got_z, down=down):
                        self.raw(
                            z.at[p], got_z.at[p], self.sem(n, p, down), self.sem(n, p, down), self.me
                        ).wait_send()

    def total(self, z, got_z, part):
        d = self.me[0]
        value = z[d, part, :].astype(F32)
        value = value + jnp.where(d > 0, got_z[d, part, :].astype(F32), 0.0)
        return value + jnp.where(d < DP - 1, got_z[DP, part, :].astype(F32), 0.0)


class PlaneSum:
    def __init__(self, raw, stage, got, comb, base, local_sem, local_base, me):
        self.raw, self.stage, self.got, self.comb, self.base = raw, stage, got, comb, base
        self.local_sem, self.local_base, self.me = local_sem, local_base, me
        self.kinds = range(stage.shape[0])

    def from_one(self, kind, i):
        d, r, c = self.me
        y = c // 2
        sent, base = self.base + 10 * kind + i, self.base + 10 * kind
        if i < 2:
            return self.raw(self.stage.at[kind, i], self.got.at[kind, 0], sent, base, (d, r ^ 1, 2 * y + 1 - i))
        return self.raw(
            self.stage.at[kind, i], self.comb.at[kind, 3 - i], sent, base + 3 + (3 - i), (d, r ^ 1, 2 * y)
        )

    def from_zero(self, kind, i):
        d, r, c = self.me
        sent, base = self.base + 10 * kind + i, self.base + 10 * kind
        if i == 1:
            return self.raw(self.stage.at[kind, i], self.got.at[kind, 1], sent, base + 1, (d, r, c ^ 1))
        return self.raw(
            self.stage.at[kind, i], self.got.at[kind, 2], sent, base + 2, (d, r, 2 * (1 - c // 2) + i - 2)
        )

    def home(self, kind):
        return pltpu.make_async_copy(
            self.stage.at[kind, 0], self.got.at[kind, 1], self.local_sem.at[self.local_base + kind]
        )

    def start_far(self):
        @pl.when(lax.rem(self.me[2], 2) == 1)
        def _():
            for i in (2, 3):
                for kind in self.kinds:
                    self.from_one(kind, i).start()

    def start_near(self):
        core = lax.rem(self.me[2], 2)

        @pl.when(core == 1)
        def _():
            for i in (0, 1):
                for kind in self.kinds:
                    self.from_one(kind, i).start()

        @pl.when(core == 0)
        def _():
            for kind in self.kinds:
                self.home(kind).start()
                self.from_zero(kind, 1).start()

    def combine(self, room, local_base):
        core = lax.rem(self.me[2], 2)

        @pl.when(core == 0)
        def _():
            for i in (2, 3):
                for kind in self.kinds:
                    self.raw(
                        self.stage.at[kind, i], self.comb.at[kind, i - 2], self.base,
                        self.base + 10 * kind + 3 + (i - 2), self.me,
                    ).wait_recv()
                    fetch = pltpu.make_async_copy(
                        self.comb.at[kind, i - 2], room(kind, i - 2),
                        self.local_sem.at[local_base + 2 * kind + i - 2],
                    )
                    fetch.start()
                    fetch.wait()

                    def add(t, kind=kind, i=i):
                        self.stage[kind, i, at(t, 64), :] = (
                            self.stage[kind, i, at(t, 64), :].astype(F32)
                            + room(kind, i - 2)[at(t, 64), :].astype(F32)
                        ).astype(BF)

                    loop(self.stage.shape[2] // 64, add)
                    self.from_zero(kind, i).start()

    def settle(self):
        core = lax.rem(self.me[2], 2)
        for kind in self.kinds:
            base = self.base + 10 * kind
            for n in (0, 2):
                self.raw(self.stage.at[kind, 0], self.got.at[kind, n], self.base, base + n, self.me).wait_recv()

            @pl.when(core == 1)
            def _(kind=kind, base=base):
                self.raw(self.stage.at[kind, 0], self.got.at[kind, 1], self.base, base + 1, self.me).wait_recv()
                for i in range(COL):
                    self.from_one(kind, i).wait_send()

            @pl.when(core == 0)
            def _(kind=kind):
                self.home(kind).wait()
                for i in (1, 2, 3):
                    self.from_zero(kind, i).wait_send()


def middle_kernel(
    n2_ref, mid_ref, scale_ref, gain_ref, own_grad, down_ref, own_up, gate_hbm, up_hbm, grad_hbm,
    grad_out, gain_out, got, comb, n2_out, dgate_out, dup_out,
    n2, dgate, dup, wg, wu, wd, gb, own_down, gate, up, du, hidden, given, arrived, z, got_z, crossing, crossed, gn, sums, stage,
    send_sem, recv_sem, local_sem,
):
    d, r, c = (lax.axis_index(name) for name in AXES)
    me = (d, r, c)
    y, core = c // 2, lax.rem(c, 2)
    rows, fc = n2_ref.shape
    block = rows // 2
    units = own_down.shape[0]
    half = 2 * fc
    over = (((0,), (0,)), ((), ()))
    across = (((1,), (1,)), ((), ()))
    post = Post(send_sem, recv_sem)
    raw = maker(send_sem, recv_sem)
    sibling = (d, r, c ^ 1)
    others = [(a, b) for a in (0, 1) for b in range(COL) if (a, b) != (0, 0)]
    greet([(d, r ^ a, c ^ b) for a, b in others] + [(d ^ j, r, c) for j in (1, 2, 3)])

    cross = post.send(
        n2_ref.at[pl.ds(pl.multiple_of((1 - y) * block, block), block), :],
        n2.at[pl.ds(0, block), pl.ds(fc, fc)],
        (d, r, c ^ 2),
    )
    def half_of(ref, i, n):
        return ref.at[pl.ds(pl.multiple_of(place_of(i) * fc + n * (fc // 2), fc // 2), fc // 2), :]

    def place_of(i):
        return lax.rem(i, 2) * 2 + i // 2

    first_wide = post.take(8)

    def up_over_y(n):
        return raw(
            own_up.at[pl.ds(n * (fc // 2), fc // 2), :], half_of(wu, 2 + core, n),
            first_wide + 4 * n, first_wide + 4 * n + core, (d, r, 2 * (1 - y)),
        )

    def up_relay(n, i):
        return raw(
            half_of(wu, i, n), half_of(wu, 5 - i, n), first_wide + 4 * n + i - 1,
            first_wide + 4 * n + 3 - i, (d, r ^ 1, 2 * y + 1),
        )

    def up_came(n, i):
        return raw(half_of(wu, i, n), half_of(wu, i, n), first_wide, first_wide + 4 * n + i - 2, me)

    for n in (0, 1):
        up_over_y(n).start()
    loads = [
        pltpu.make_async_copy(src, dst, local_sem.at[n])
        for n, (src, dst) in zip((0, 1, 2, 9), (
            (gate_hbm, wg),
            (up_hbm.at[pl.ds(0, fc), :], wu.at[pl.ds(0, fc), :]),
            (grad_hbm, gb),
            (up_hbm.at[pl.ds(2 * fc, fc), :], wu.at[pl.ds(2 * fc, fc), :]),
        ))
    ]
    for load in loads:
        load.start()

    def cast_down(t):
        own_down[at(t, 64), :] = down_ref[at(t, 64), :].astype(BF)

    loop(units // 64, cast_down)
    first_sent = post.take(10)

    def piece(ref, n):
        return ref.at[pl.ds(n * (units // 2), units // 2), :]

    def ship(n, way, i, target, src=None):
        return raw(
            piece(own_down if src is None else src, n), piece(wd.at[place_of(i)], n),
            first_sent + 5 * n + way, first_sent + 5 * n + i, target,
        )

    keep_down = pltpu.make_async_copy(own_down, wd.at[0], local_sem.at[3])

    def to_core(n):
        return ship(n, 0, 1, sibling)

    def over_y(n):
        return ship(n, 1, 2 + core, (d, r, 2 * (1 - y)))

    def over_x(n):
        return ship(n, 2, 1 - core, (d, r ^ 1, 2 * y + 1))

    def relay(n, i):
        return ship(n, i + 1, 5 - i, (d, r ^ 1, 2 * y + 1), wd.at[PLACE[i]])

    for n in (0, 1):
        over_x(n).start()
        over_y(n).start()

    @pl.when(core == 0)
    def _():
        keep_down.start()

    @pl.when(core == 1)
    def _():
        for n in (0, 1):
            to_core(n).start()

    def pass_down(n):
        @pl.when(core == 0)
        def _():
            for i in (2, 3):
                ship(n, 0, i, me).wait_recv()
                relay(n, i).start()

    n2[0:block, 0:fc] = n2_ref[pl.ds(pl.multiple_of(y * block, block), block), :]
    cross.wait_recv()

    first_up, first_down = post.take(DP), post.take(DP)
    first_shared = post.take(DP)

    def rail(p, e):
        return n2.at[at(p ^ e, block), pl.ds(0, half)]

    def go_up(p):
        return raw(rail(p, d), rail(p, d + 1), first_up + p, first_up + p, (d + 1, r, c))

    def go_down(p):
        return raw(rail(p, d), rail(p, d - 1), first_down + p, first_up + p, (d - 1, r, c))

    def share(p):
        return raw(
            rail(p, d), n2.at[at(p ^ d, block), pl.ds(half, half)], first_shared + p, first_shared + p, sibling
        )

    def onward(p):
        @pl.when((p <= d) & (d < DP - 1))
        def _():
            go_up(p).start()

        @pl.when((p >= d) & (d > 0))
        def _():
            go_down(p).start()

        share(p).start()

    def project(p):
        share(p).wait_recv()
        part = at(p ^ d, block)
        gate[part, :] = jnp.dot(n2[part, :], wg[...], preferred_element_type=F32)

    def project_up(t):
        part = at(t, block)
        up[part, :] = jnp.dot(n2[part, :], wu[...], preferred_element_type=F32)

    def pass_up(n):
        @pl.when(core == 0)
        def _():
            for i in (2, 3):
                up_came(n, i).wait_recv()
                up_relay(n, i).start()

    def hidden_grads(first, fresh):
        def one(t):
            part = at(t, block)
            value = jnp.zeros((block, units), F32) if fresh else du[part, :]
            for i in (first, first + 1):
                place = PLACE[i]
                value = value + lax.dot_general(
                    gb[part, place * fc : (place + 1) * fc], wd[place], across, preferred_element_type=F32
                )
            du[part, :] = value

        loop(DP, one)

    onward(d)
    turns = [
        d,
        jnp.where(d == 0, 1, d - 1),
        jnp.where(d < 2, 2, jnp.where(d == 2, 3, 1)),
        jnp.where(d < 2, 3, 0),
    ]
    inner = (d == 1) | (d == 2)

    def arrival(n):
        raw(rail(turns[n], d), rail(turns[n], d), first_up, first_up + turns[n], me).wait_recv()
        onward(turns[n])

    for load in loads:
        load.wait()
    arrival(1)

    @pl.when(inner)
    def _():
        arrival(2)

    pass_up(0)
    project(turns[0])
    pass_up(1)
    project(turns[1])

    @pl.when(jnp.logical_not(inner))
    def _():
        arrival(2)

    @pl.when(inner)
    def _():
        arrival(3)

    pass_down(0)
    project(turns[2])

    @pl.when(core == 0)
    def _():
        keep_down.wait()
        for n in (0, 1):
            ship(n, 0, 1, me).wait_recv()

    @pl.when(core == 1)
    def _():
        for n in (0, 1):
            for i in (0, 1):
                ship(n, 0, i, me).wait_recv()

    @pl.when(jnp.logical_not(inner))
    def _():
        arrival(3)

    hidden_grads(0, True)
    pass_down(1)
    project(turns[3])
    outs = [pltpu.make_async_copy(n2, n2_out, local_sem.at[0])]
    outs[0].start()

    @pl.when(core == 1)
    def _():
        for n in (0, 1):
            for i in (2, 3):
                up_came(n, i).wait_recv()

    loop(DP, project_up)

    @pl.when(core == 1)
    def _():
        for n in (0, 1):
            for i in (2, 3):
                ship(n, 0, i, me).wait_recv()

    hidden_grads(2, False)

    def units_of(t):
        part = at(t, 64)
        g, u, grad = gate[part, :], up[part, :], du[part, :]
        sigmoid = 1.0 / (1.0 + jnp.exp(-g))
        silu = g * sigmoid
        hidden[part, :] = (silu * u).astype(BF)
        dgate[part, :] = (grad * u * sigmoid * (1.0 + g * (1.0 - sigmoid))).astype(BF)
        dup[part, :] = (grad * silu).astype(BF)

    loop(2 * rows // 64, units_of)
    for n, (src, dst) in enumerate(((dgate, dgate_out), (dup, dup_out))):
        outs.append(pltpu.make_async_copy(src, dst, local_sem.at[1 + n]))
        outs[-1].start()

    def back(part, cols):
        return lax.dot_general(
            dgate[part, :], wg[cols, :], across, preferred_element_type=F32
        ) + lax.dot_general(dup[part, :], wu[cols, :], across, preferred_element_type=F32)

    def down_part(i):
        def down_grad(t):
            place = PLACE[i]
            stage[0, i, at(t, TILE), :] = lax.dot_general(
                hidden[:, at(t, TILE)], gb[:, place * fc : (place + 1) * fc], over, preferred_element_type=F32
            ).astype(BF)

        loop(units // TILE, down_grad)

    owners = PlaneSum(raw, stage, got, comb, post.take(10), local_sem, 4, me)

    line = LineSum(raw, ((z, got_z),), post.take(8), me)

    def plane_of(t):
        return jnp.where(d < DP // 2, DP - 1 - t, t)

    def to_sibling(t):
        part = at(plane_of(t) ^ d, block)
        return raw(given.at[part, :], arrived.at[part, :], first_given + t, first_given + t, sibling)

    def give(t):
        part = at(plane_of(t) ^ d, block)
        given[part, :] = back(part, slice(half, None)).astype(BF)
        to_sibling(t).start()

    def keep(t):
        p = plane_of(t)
        part = at(p ^ d, block)
        value = back(part, slice(0, half))
        to_sibling(t).wait_recv()
        z[p] = (value + arrived[part, :].astype(F32)).astype(BF)

        if t < DP - 1:
            @pl.when(d == 0)
            def _():
                line.up(DP - 1 - t)

            @pl.when(d == DP - 1)
            def _():
                line.down(t)

    first_given = post.take(DP)
    give(0)
    give(1)
    down_part(2)
    down_part(3)
    owners.start_far()
    keep(0)
    give(2)
    keep(1)
    give(3)
    keep(2)
    down_part(0)
    down_part(1)
    owners.start_near()
    keep(3)
    owners.combine(lambda kind, j: wg.at[pl.ds(0, units), pl.ds(j * fc, fc)], 5)
    line.rest()

    def settle_rows(t):
        part = at(t, 64)
        total = line.total(z, got_z, part)
        gn[pl.ds(pl.multiple_of(y * block + t * 64, 64), 64), :] = total[:, 0:fc]
        crossing[part, :] = total[:, fc:].astype(BF)

    loop(block // 64, settle_rows)
    other = post.send(crossing, crossed, (d, r, c ^ 2))
    other.wait_recv()

    def other_rows(t):
        gn[pl.ds(pl.multiple_of((1 - y) * block + t * 64, 64), 64), :] = crossed[at(t, 64), :].astype(F32)

    loop(block // 64, other_rows)

    def inner_sum(t):
        part = at(t, 128)
        inner = gn[part, :] * gain_ref[...] * mid_ref[part, :]
        sums[0, :, part] = as_row(jnp.sum(inner, axis=1, keepdims=True))

    loop(rows // 128, inner_sum)
    small = [post.send(sums.at[0], sums.at[m], (d, r, c ^ m)) for m in (1, 2, 3)]

    def gain_sum(t, total):
        part = at(t, 128)
        value = gn[part, :] * mid_ref[part, :] * scale_ref[part, :]
        return total + jnp.sum(value, axis=0, keepdims=True)

    gain_out[...] = lax.fori_loop(0, rows // 128, gain_sum, jnp.zeros((1, fc), F32))
    for copy in small:
        copy.wait_recv()

    def finish(t):
        part = at(t, 128)
        inner = as_column(sums[0, :, part] + sums[2, :, part] + sums[1, :, part] + sums[3, :, part])
        scale = scale_ref[part, :]
        grad_out[part, :] = (
            own_grad[part, :].astype(F32) + scale * (gn[part, :] * gain_ref[...])
            - mid_ref[part, :] * (scale * scale * scale * inner / D)
        )

    loop(rows // 128, finish)

    owners.settle()
    line.settle()
    for copy in outs:
        copy.wait()
    for copy in [cross, other] + small:
        copy.wait_send()
    for t in range(DP):
        to_sibling(t).wait_send()
    for n in (0, 1):
        over_y(n).wait_send()
        over_x(n).wait_send()
        up_over_y(n).wait_send()

        @pl.when(core == 0)
        def _(n=n):
            for i in (2, 3):
                relay(n, i).wait_send()
                up_relay(n, i).wait_send()

        @pl.when(core == 1)
        def _(n=n):
            to_core(n).wait_send()

    for p in range(DP):
        share(p).wait_send()

        @pl.when((p <= d) & (d < DP - 1))
        def _(p=p):
            go_up(p).wait_send()

        @pl.when((p >= d) & (d > 0))
        def _(p=p):
            go_down(p).wait_send()


def middle(n2, mid, scale, gain, own_grad, down, own_up, gate, up, grad_all):
    rows, fc = n2.shape
    group = 2 * rows
    block = rows // 2
    units = down.shape[0]
    vmem = pl.BlockSpec(memory_space=pltpu.VMEM)
    hbm = pl.BlockSpec(memory_space=pl.ANY)

    def like(shape, dtype=BF):
        return jax.ShapeDtypeStruct(shape, dtype)

    return pl.pallas_call(
        middle_kernel,
        in_specs=[vmem] * 6 + [hbm] * 4,
        out_specs=[vmem] * 2 + [hbm] * 5,
        out_shape=[
            like((rows, fc), F32),
            like((1, fc), F32),
            like((1, 3, units, fc)),
            like((1, 2, units, fc)),
            like((group, D)),
            like((group, units)),
            like((group, units)),
        ],
        scratch_shapes=[
            pltpu.VMEM((group, D), BF),
            pltpu.VMEM((group, units), BF),
            pltpu.VMEM((group, units), BF),
            pltpu.VMEM((D, units), BF),
            pltpu.VMEM((D, units), BF),
            pltpu.VMEM((COL, units, fc), BF),
            pltpu.VMEM((group, D), BF),
            pltpu.VMEM((units, fc), BF),
            pltpu.VMEM((group, units), F32),
            pltpu.VMEM((group, units), F32),
            pltpu.VMEM((group, units), F32),
            pltpu.VMEM((group, units), BF),
            pltpu.VMEM((group, 2 * fc), BF),
            pltpu.VMEM((group, 2 * fc), BF),
            pltpu.VMEM((DP, block, 2 * fc), BF),
            pltpu.VMEM((DP + 1, block, 2 * fc), BF),
            pltpu.VMEM((block, fc), BF),
            pltpu.VMEM((block, fc), BF),
            pltpu.VMEM((rows, fc), F32),
            pltpu.VMEM((4, 8, rows), F32),
            pltpu.VMEM((1, COL, units, fc), BF),
            pltpu.SemaphoreType.DMA((SENDS,)),
            pltpu.SemaphoreType.DMA((SENDS,)),
            pltpu.SemaphoreType.DMA((12,)),
        ],
        compiler_params=pltpu.CompilerParams(
            collective_id=3, has_side_effects=True, vmem_limit_bytes=62 << 20
        ),
        cost_estimate=pl.CostEstimate(
            flops=14 * group * D * units, bytes_accessed=48 << 20, transcendentals=group * units
        ),
    )(n2, mid, scale, gain, own_grad, down, own_up, gate, up, grad_all)


POSTS = 112


def backward_kernel(
    x_ref, gain_ref, scale_ref, mid_ref, gain_two_ref, begin_ref, weight_in_hbm, weight_out_hbm, q_hbm, kv_hbm,
    att_hbm, lse_hbm, normed_hbm, n2_hbm, dgate_hbm, dup_hbm,
    tokens_out, query_out, key_out, value_out, out_out, gains_out, got, comb,
    weight_in, weight_out, q_ref, kv_ref, att_ref, lse_ref, n1, n2, dgu, dball, dotted, dproj, acc, spill, spilled, stage, own_f, arrived, landed,
    zq, zo, zkv, rq, ro, rkv, sums, gsum,
    send_sem, recv_sem, local_sem,
):
    d, r, c = (lax.axis_index(name) for name in AXES)
    y, core = c // 2, lax.rem(c, 2)
    rows, fc = x_ref.shape
    group = 2 * rows
    width = q_hbm.shape[1]
    units = dgate_hbm.shape[1]
    half = 2 * fc
    tiles = group // TILE
    over = (((0,), (0,)), ((), ()))
    across = (((1,), (1,)), ((), ()))
    post = Post(send_sem, recv_sem)
    loads = [
        pltpu.make_async_copy(src, dst, local_sem.at[8 + n])
        for n, (src, dst) in enumerate((
            (n2_hbm, n2),
            (dgate_hbm, dgu.at[pl.ds(0, group), :]),
            (dup_hbm, dgu.at[pl.ds(group, group), :]),
            (normed_hbm, n1),
            (weight_out_hbm, weight_out),
            (att_hbm, att_ref),
            (q_hbm, q_ref),
            (kv_hbm, kv_ref),
            (lse_hbm, lse_ref),
            (weight_in_hbm, weight_in),
        ))
    ]
    for load in loads:
        load.start()

    others = [(a, b) for a in (0, 1) for b in range(COL) if (a, b) != (0, 0)]
    greet(
        [(d, r ^ a, c ^ b) for a, b in others]
        + [(d ^ j, r ^ a, c) for j in (1, 2, 3) for a in (0, 1)]
    )

    def columns(place):
        return pl.ds(place * fc, fc)

    def turned(t):
        return lax.rem(t + 2 * r, tiles)

    raw = maker(send_sem, recv_sem)
    me = (d, r, c)
    sibling = (d, r, c ^ 1)
    own_rows, other_rows = pl.ds(0, rows), pl.ds(rows, rows)
    def round_mid(t):
        dball[at(t, 128), 0:fc] = mid_ref[at(t, 128), :].astype(BF)

    loop(rows // 128, round_mid)
    own_block = dball.at[own_rows, columns(0)]
    beside = post.send(own_block, dball.at[other_rows, columns(0)], (d, r ^ 1, c))
    beyond = post.send(own_block, dball.at[own_rows, columns(1)], (d, r, c ^ 2))
    shared = [post.send(own_block, dball.at[own_rows, columns(2)], sibling)]

    for load in loads[:3]:
        load.wait()
    owners = PlaneSum(raw, stage, got, comb, post.take(20), local_sem, 4, me)

    def hidden_part(i):
        for kind in (0, 1):
            def hidden_grad(t, kind=kind):
                left = n2[:, pl.ds(pl.multiple_of(PLACE[i] * fc + t * TILE, TILE), TILE)]
                stage[kind, i, at(t, TILE), :] = lax.dot_general(
                    left, dgu[pl.ds(kind * group, group), :], over, preferred_element_type=F32
                ).astype(BF)

            loop(fc // TILE, hidden_grad)

    hidden_part(2)
    hidden_part(3)
    for load in loads[3:]:
        load.wait()

    upper = pl.ds(rows, rows // 2)
    beside.wait_recv()
    corner = [post.send(dball.at[upper, columns(0)], dball.at[upper, columns(1)], (d, r, c ^ 2))]
    shared.append(post.send(dball.at[other_rows, columns(0)], dball.at[other_rows, columns(2)], sibling))
    beyond.wait_recv()
    corner.append(post.send(
        dball.at[pl.ds(rows // 2, rows // 2), columns(1)],
        dball.at[pl.ds(rows + rows // 2, rows // 2), columns(1)], (d, r ^ 1, c),
    ))
    shared.append(post.send(dball.at[own_rows, columns(1)], dball.at[own_rows, columns(3)], sibling))
    owners.start_far()
    hidden_part(0)
    hidden_part(1)
    for copy in corner:
        copy.wait_recv()
    shared.append(post.send(dball.at[other_rows, columns(1)], dball.at[other_rows, columns(3)], sibling))
    for copy in shared:
        copy.wait_recv()

    def head_grad(t):
        dotted[at(turned(t), TILE), :] = lax.dot_general(
            dball[at(t, TILE), :], weight_out[...], across, preferred_element_type=F32
        ).astype(BF)

    loop(tiles, head_grad)

    sent_out = [None] + [post.take(1) for _ in (1, 2, 3)]
    outs = []
    for place, m in enumerate((0, 2, 1, 3)):
        value = lax.dot_general(
            att_ref[...], dball[:, place * fc : (place + 1) * fc], over, preferred_element_type=F32
        ).astype(BF)
        if m == 0:
            zo[c] = value
        else:
            n2[(m - 1) * width : m * width, half : half + fc] = value
            staged = n2.at[pl.ds((m - 1) * width, width), pl.ds(half, fc)]
            copy = raw(staged, zo.at[c], sent_out[m], sent_out[m], (d, r, c ^ m))
            copy.start()
            outs.append(copy)

    span = TILE + REACH
    scale = HEAD_DIM ** (-0.5)
    spills = []
    for h in range(width // HEAD_DIM):
        lanes = pl.ds(h * HEAD_DIM, HEAD_DIM)
        value_lanes = pl.ds(width + h * HEAD_DIM, HEAD_DIM)

        def clear(t, lanes=lanes, value_lanes=value_lanes):
            acc[at(t, TILE), lanes] = jnp.zeros((TILE, HEAD_DIM), F32)
            acc[at(t, TILE), value_lanes] = jnp.zeros((TILE, HEAD_DIM), F32)

        loop((group + REACH) // TILE, clear)

        def one(t, lanes=lanes, value_lanes=value_lanes):
            part = at(t, TILE)
            window = pl.ds(pl.multiple_of(t * TILE, TILE), span)
            query, key = q_ref[part, lanes], kv_ref[window, lanes]
            grad = dotted[part, lanes]
            scores = scores_of(query, key)
            query_at = lax.broadcasted_iota(jnp.int32, (TILE, span), 0)
            key_at = lax.broadcasted_iota(jnp.int32, (TILE, span), 1)
            begin = begin_ref[part, 0:1] + (REACH - t * TILE)
            allowed = (key_at <= query_at + REACH) & (key_at >= begin)
            scores = jnp.where(allowed, scores - lse_ref[part, lanes][:, 0:1], NEG_FILL)
            probability = jnp.exp(scores)
            grad_soft = lax.dot_general(grad, kv_ref[window, value_lanes], across, preferred_element_type=F32)
            inner = jnp.sum(probability * grad_soft, axis=1, keepdims=True)
            grad_scores = (probability * (grad_soft - inner)).astype(BF)
            dproj[at(turned(t), TILE), lanes] = (
                jnp.dot(grad_scores, key, preferred_element_type=F32) * scale
            ).astype(BF)
            acc[window, lanes] += lax.dot_general(grad_scores, query, over, preferred_element_type=F32) * scale
            acc[window, value_lanes] += lax.dot_general(
                probability.astype(BF), grad, over, preferred_element_type=F32
            )

        loop(tiles, one)

        def round_spill(t, h=h, lanes=lanes, value_lanes=value_lanes):
            spill[h, at(t, TILE), 0:HEAD_DIM] = acc[at(t, TILE), lanes].astype(BF)
            spill[h, at(t, TILE), HEAD_DIM:] = acc[at(t, TILE), value_lanes].astype(BF)

        loop(REACH // TILE, round_spill)
        copy = post.ready(spill.at[h], spilled.at[h], (lax.rem(d + DP - 1, DP), r, c))
        spills.append(copy)

        @pl.when(d > 0)
        def _(copy=copy):
            copy.start()

    def attention_grads(first_lane, lane_count, dest):
        lanes = slice(first_lane, first_lane + lane_count)
        slots = [None] + [post.take(1) for _ in (1, 2, 3)]
        copies = []
        for place, m in enumerate((0, 2, 1, 3)):
            def tile(t, place=place, m=m):
                left = n1[:, pl.ds(pl.multiple_of(place * fc + t * TILE, TILE), TILE)]
                value = lax.dot_general(left, dproj[:, lanes], over, preferred_element_type=F32).astype(BF)
                if m == 0:
                    dest[c, at(t, TILE), :] = value
                else:
                    dgu[pl.ds(pl.multiple_of(place * fc + t * TILE, TILE), TILE), lanes] = value

            loop(fc // TILE, tile)
            if m:
                copy = raw(
                    dgu.at[pl.ds(place * fc, fc), pl.ds(first_lane, lane_count)], dest.at[c],
                    slots[m], slots[m], (d, r, c ^ m),
                )
                copy.start()
                copies.append(copy)
        return copies

    qs = attention_grads(0, width, zq)

    @pl.when(d < DP - 1)
    def _():
        for copy in spills:
            copy.wait_recv()

    @pl.when(d == DP - 1)
    def _():
        spilled[...] = jnp.zeros_like(spilled)

    for h in range(width // HEAD_DIM):
        for which in (0, 1):
            lanes = pl.ds(which * width + h * HEAD_DIM, HEAD_DIM)
            out_lanes = pl.ds((1 + which) * width + h * HEAD_DIM, HEAD_DIM)

            def whole(t, h=h, which=which, lanes=lanes, out_lanes=out_lanes):
                total = acc[pl.ds(pl.multiple_of(REACH + t * TILE, TILE), TILE), lanes]
                extra = spilled[
                    h, at(jnp.maximum(t - 1, 0), TILE), which * HEAD_DIM : (which + 1) * HEAD_DIM
                ].astype(F32)
                total = total + jnp.where(t > 0, extra, 0.0)
                dproj[at(turned(t), TILE), out_lanes] = total.astype(BF)

            loop(tiles, whole)

    kvs = attention_grads(width, 2 * width, zkv)
    for copy in outs + qs:
        copy.wait_recv()
    first_line = post.take(24)
    line_a = LineSum(raw, ((zq, rq), (zo, ro)), first_line, me)
    line_b = LineSum(raw, ((zkv, rkv),), first_line + 16, me)
    line_a.begin()

    def given_part(t):
        n2[at(t, TILE), 0:half] = lax.dot_general(
            dproj[at(t, TILE), :], weight_in[half:, :], across, preferred_element_type=F32
        ).astype(BF)

    loop(tiles, given_part)
    to_sibling = post.send(n2.at[:, pl.ds(0, half)], arrived, sibling)

    to_sibling.wait_recv()
    for copy in outs:
        copy.wait_send()

    def kept_part(t):
        part = at(t, TILE)
        value = lax.dot_general(
            dproj[part, :], weight_in[:half, :], across, preferred_element_type=F32
        ) + arrived[part, :].astype(F32)
        n2[part, half:] = value.astype(BF)

        @pl.when(t < rows // TILE)
        def _():
            own_f[part, :] = value[:, 0:fc]

    loop(tiles, kept_part)

    def low(where, place):
        return n2.at[where, pl.ds(half + place * fc, fc)]

    pieces = [
        post.send(low(other_rows, 1), landed.at[2], (d, r ^ 1, c ^ 2)),
        post.send(low(other_rows, 0), landed.at[0], (d, r ^ 1, c)),
        post.send(low(own_rows, 1), landed.at[1], (d, r, c ^ 2)),
    ]

    def finish(line, z, got_z, dests):
        def one(t):
            value = line.total(z, got_z, at(t, 64))
            for dest, lanes in dests:
                dest[at(t, 64), :] = value[:, lanes]

        loop(z.shape[1] // 64, one)

    owners.start_near()
    line_a.rest()
    for copy in kvs:
        copy.wait_recv()
    line_b.begin()

    for copy in pieces:
        copy.wait_recv()

    def inner_sum(t):
        part = at(t, 128)
        value = own_f[part, :]
        for n in range(3):
            value = value + landed[n, part, :].astype(F32)
        own_f[part, :] = value
        inner = value * gain_ref[...] * x_ref[part, :].astype(F32)
        sums[0, :, part] = as_row(jnp.sum(inner, axis=1, keepdims=True))

    loop(rows // 128, inner_sum)
    small = [post.send(sums.at[0], sums.at[m], (d, r, c ^ m)) for m in (1, 2, 3)]
    seat = ROW * d + r
    gain_part = jnp.zeros((1, fc), F32)

    def gain_sum(t, total):
        part = at(t, 128)
        value = own_f[part, :] * x_ref[part, :].astype(F32) * scale_ref[part, :]
        return total + jnp.sum(value, axis=0, keepdims=True)

    gain_part = lax.fori_loop(0, rows // 128, gain_sum, gain_part)
    gsum[seat, 0:1, :] = gain_part
    gsum[seat, 1:2, :] = gain_two_ref[...]
    gsum[seat, 2:8, :] = jnp.zeros((6, fc), F32)
    gain_sent = post.take(8)
    gain_got = gain_sent

    def gain_copy(n, j, a):
        return raw(gsum.at[seat], gsum.at[seat], gain_sent + n, gain_got + seat, (d ^ j, r ^ a, c))

    far = [(j, a) for j in range(DP) for a in (0, 1) if (j, a) != (0, 0)]
    for n, (j, a) in enumerate(far):
        gain_copy(n, j, a).start()
    owners.combine(lambda kind, j: n1.at[pl.ds(j * fc, fc), pl.ds(kind * units, units)], 0)


    line_b.rest()
    finish(line_a, zq, rq, ((query_out, slice(None)),))
    finish(line_a, zo, ro, ((out_out, slice(None)),))
    finish(line_b, zkv, rkv, ((key_out, slice(0, width)), (value_out, slice(width, None))))
    for copy in small:
        copy.wait_recv()

    def finish_tokens(t):
        part = at(t, 128)
        inner = as_column(sums[0, :, part] + sums[2, :, part] + sums[1, :, part] + sums[3, :, part])
        scale_rows = scale_ref[part, :]
        value = x_ref[part, :].astype(F32)
        tokens_out[part, :] = (
            mid_ref[part, :] + scale_rows * (own_f[part, :] * gain_ref[...])
            - value * (scale_rows * scale_rows * scale_rows * inner / D)
        )

    loop(rows // 128, finish_tokens)

    for e in range(2 * DP):
        @pl.when(e != seat)
        def _(e=e):
            raw(gsum.at[e], gsum.at[e], gain_sent, gain_got + e, me).wait_recv()

    gains = gsum[0]
    for e in range(1, 2 * DP):
        gains = gains + gsum[e]
    gains_out[...] = gains

    owners.settle()
    line_a.settle()
    line_b.settle()
    for copy in [beside, beyond] + corner + shared + qs + kvs + [to_sibling] + pieces + small:
        copy.wait_send()
    for n, (j, a) in enumerate(far):
        gain_copy(n, j, a).wait_send()

    @pl.when(d > 0)
    def _():
        for copy in spills:
            copy.wait_send()


def backward(x, gain, scale, mid, gain_two, weight_in, weight_out, q, kv, att, lse, begin, normed, n2, dgate, dup):
    rows, fc = x.shape
    group = 2 * rows
    width = q.shape[1]
    units = dgate.shape[1]
    vmem = pl.BlockSpec(memory_space=pltpu.VMEM)
    hbm = pl.BlockSpec(memory_space=pl.ANY)

    def like(shape, dtype=BF):
        return jax.ShapeDtypeStruct(shape, dtype)

    return pl.pallas_call(
        backward_kernel,
        in_specs=[vmem] * 6 + [hbm] * 10,
        out_specs=[vmem] * 6 + [hbm] * 2,
        out_shape=[
            like((rows, fc), F32),
            like((fc, width), F32),
            like((fc, width), F32),
            like((fc, width), F32),
            like((width, fc), F32),
            like((8, fc), F32),
            like((2, 3, fc, units)),
            like((2, 2, fc, units)),
        ],
        scratch_shapes=[
            pltpu.VMEM((D, 3 * width), BF),
            pltpu.VMEM((width, D), BF),
            pltpu.VMEM((group, width), BF),
            pltpu.VMEM((REACH + group, 2 * width), BF),
            pltpu.VMEM((group, width), BF),
            pltpu.VMEM((group, width), F32),
            pltpu.VMEM((group, D), BF),
            pltpu.VMEM((group, D), BF),
            pltpu.VMEM((2 * group, units), BF),
            pltpu.VMEM((group, D), BF),
            pltpu.VMEM((group, width), BF),
            pltpu.VMEM((group, 3 * width), BF),
            pltpu.VMEM((group + REACH, 2 * width), F32),
            pltpu.VMEM((width // HEAD_DIM, REACH, 2 * HEAD_DIM), BF),
            pltpu.VMEM((width // HEAD_DIM, REACH, 2 * HEAD_DIM), BF),
            pltpu.VMEM((2, COL, fc, units), BF),
            pltpu.VMEM((rows, fc), F32),
            pltpu.VMEM((group, 2 * fc), BF),
            pltpu.VMEM((3, rows, fc), BF),
            pltpu.VMEM((DP, fc, width), BF),
            pltpu.VMEM((DP, width, fc), BF),
            pltpu.VMEM((DP, fc, 2 * width), BF),
            pltpu.VMEM((DP + 1, fc, width), BF),
            pltpu.VMEM((DP + 1, width, fc), BF),
            pltpu.VMEM((DP + 1, fc, 2 * width), BF),
            pltpu.VMEM((4, 8, rows), F32),
            pltpu.VMEM((2 * DP, 8, fc), F32),
            pltpu.SemaphoreType.DMA((POSTS,)),
            pltpu.SemaphoreType.DMA((POSTS,)),
            pltpu.SemaphoreType.DMA((20,)),
        ],
        compiler_params=pltpu.CompilerParams(
            collective_id=2, has_side_effects=True, vmem_limit_bytes=62 << 20
        ),
        cost_estimate=pl.CostEstimate(
            flops=12 * group * D * width + 4 * group * D * units, bytes_accessed=64 << 20, transcendentals=0
        ),
    )(x, gain, scale, mid, gain_two, begin, weight_in, weight_out, q, kv, att, lse, normed, n2, dgate, dup)


def on_small_mesh(
    tokens,
    cotangent,
    query_master,
    key_master,
    value_master,
    out_master,
    gate_master,
    up_master,
    down_master,
    attn_gain,
    ffn_gain,
    lengths,
    permutation,
):
    del permutation
    (
        mid, scale_two, n2, begin, scale_one, normed_one, weight_in, weight_out, q, key_value,
        own_attended, lse, own_up, weight_gate, weight_up, grad_all,
    ) = forward(
        tokens, attn_gain[None, :], ffn_gain[None, :], lengths, query_master, key_master,
        value_master, out_master, gate_master, up_master, cotangent,
    )
    grad_mid, gain_two_part, got_down, _, normed_two, grad_gate, grad_up = middle(
        n2, mid, scale_two, ffn_gain[None, :], cotangent, down_master, own_up, weight_gate,
        weight_up, grad_all,
    )
    grad_tokens, grad_query, grad_key, grad_value, grad_out, gains, got, _ = backward(
        tokens, attn_gain[None, :], scale_one, grad_mid, gain_two_part, weight_in, weight_out, q,
        key_value, own_attended, lse, begin, normed_one, normed_two, grad_gate, grad_up,
    )

    def whole(pieces):
        return pieces[0].astype(F32) + pieces[1].astype(F32) + pieces[2].astype(F32)

    return (
        grad_tokens,
        grad_query,
        grad_key,
        grad_value,
        grad_out,
        whole(got[0]),
        whole(got[1]),
        whole(got_down[0]),
        gains[0],
        gains[1],
    )


def solution(mesh):
    placed = (
        P(("dp", "row"), "col"),
        P(("dp", "row"), "col"),
        P("col", ("row", "dp")),
        P("col", ("row", "dp")),
        P("col", ("row", "dp")),
        P(("row", "dp"), "col"),
        P("col", ("row", "dp")),
        P("col", ("row", "dp")),
        P(("row", "dp"), "col"),
        P("col"),
        P("col"),
        P(),
        P(),
    )
    small = tuple(mesh.shape[name] for name in AXES) == (DP, ROW, COL)
    return jax.shard_map(
        on_small_mesh if small else on_any_mesh,
        mesh=mesh,
        in_specs=placed,
        out_specs=(
            P(("dp", "row"), "col"),
            P("col", ("row", "dp")),
            P("col", ("row", "dp")),
            P("col", ("row", "dp")),
            P(("row", "dp"), "col"),
            P("col", ("row", "dp")),
            P("col", ("row", "dp")),
            P(("row", "dp"), "col"),
            P("col"),
            P("col"),
        ),
        check_vma=False,
    )
```

```python
import functools

import jax
import jax.numpy as jnp
from jax import lax
from jax.experimental import pallas as pl
from jax.experimental.pallas import tpu as pltpu
from jax.sharding import PartitionSpec as P

D = 2048
HEAD_DIM = 128


EPSILON = 1e-06
NEG_FILL = -1e30
AXES = ("dp", "row", "col")
DP, ROW, COL = 4, 2, 4
REACH = 768
BF = jnp.bfloat16
F32 = jnp.float32


def running_sum(lengths):
    count = lengths.shape[0]
    earlier = jnp.arange(count)[:, None] <= jnp.arange(count)[None, :]
    return jnp.sum(jnp.where(earlier, lengths[:, None], 0), axis=0)

def make_picker(wanted, carried, pieces):
    amount = pieces[0].shape[0]
    inside = (wanted >= 0) & (wanted < amount)
    chosen = jnp.clip(wanted, 0, amount - 1)
    return tuple(
        (
            jnp.where(inside[:, None], jnp.take(shard_rows, chosen, axis=0), current)
            for shard_rows, current in zip(pieces, carried)
        )
    )


def sequence_marks(permutation, lengths, first_slot, amount):
    source = lax.dynamic_slice_in_dim(permutation, first_slot, amount)
    seq_ends = running_sum(lengths)
    passed = seq_ends[None, :] <= source[:, None]
    member = jnp.sum(passed.astype(jnp.int32), axis=1)
    begins = jnp.max(jnp.where(passed, seq_ends[None, :], 0), axis=1)
    return (member, source - begins)


def col_total(values):
    return lax.psum(jnp.sum(values, axis=1), "col")


def row_gather(values):
    return lax.all_gather(values, "row", axis=0, tiled=True)


def col_gather(values):
    return lax.all_gather(values, "col", axis=0, tiled=True)


def key_gather(keys_here, values_here):
    return (
        lax.all_gather(keys_here, "col", axis=0, tiled=True),
        lax.all_gather(values_here, "col", axis=0, tiled=True),
    )


def multiply(row_block, weight, transpose_right):
    if transpose_right:
        return lax.dot_general(
            row_block, weight, (((1,), (1,)), ((), ())), preferred_element_type=jnp.float32
        )
    return jnp.dot(row_block, weight, preferred_element_type=jnp.float32)


def outer_sum(left_rows, right_rows):
    return lax.dot_general(
        left_rows, right_rows, (((0,), (0,)), ((), ())), preferred_element_type=jnp.float32
    )


def col_reduce(spread, weight, transpose_right):
    return lax.psum_scatter(
        multiply(spread, weight, transpose_right), "col", scatter_dimension=0, tiled=True
    )


def row_reduce(spread, weight, transpose_right):
    return lax.psum_scatter(
        multiply(spread, weight, transpose_right), "row", scatter_dimension=0, tiled=True
    )


def visible(query_member, query_position, member, position):
    same = query_member[:, None] == member[None, :]
    behind = position[None, :] <= query_position[:, None]
    return same & behind


def attend_scores(query_block, key_all, allowed):
    scores = jnp.einsum(
        "qhd,khd->hqk", query_block, key_all, preferred_element_type=jnp.float32
    ) * HEAD_DIM ** (-0.5)
    return jnp.where(allowed[None, :, :], scores, NEG_FILL)


def norm_back(grad_normed, inputs_f, scale_rows, gain):
    gain_part = jnp.sum(grad_normed * inputs_f * scale_rows[:, None], axis=0)
    scaled = grad_normed * gain[None, :]
    inner = col_total(scaled * inputs_f)
    grad_inputs = scale_rows[:, None] * scaled - inputs_f * (scale_rows**3 * inner / D)[:, None]
    return (grad_inputs, gain_part)


def on_any_mesh(
    tokens,
    cotangent,
    query_master,
    key_master,
    value_master,
    out_master,
    gate_master,
    up_master,
    down_master,
    attn_gain,
    ffn_gain,
    lengths,
    permutation,
):
    own_rows = tokens.shape[0]
    group_rows = own_rows * lax.axis_size("row")
    quarter = group_rows // lax.axis_size("col")
    device_slot = lax.axis_index(("dp", "row"))
    group_slot = lax.axis_index("dp")
    col_slot = lax.axis_index("col")
    own_sources = lax.dynamic_slice_in_dim(permutation, device_slot * own_rows, own_rows)
    own_tokens, own_cotangent = make_picker(
        own_sources,
        (jnp.zeros_like(tokens), jnp.zeros_like(cotangent)),
        (
            lax.all_gather(tokens, ("dp", "row"), axis=0, tiled=True),
            lax.all_gather(cotangent, ("dp", "row"), axis=0, tiled=True),
        ),
    )
    masters = tuple(
        (
            matrix.astype(jnp.bfloat16)
            for matrix in (
                query_master,
                key_master,
                value_master,
                out_master,
                gate_master,
                up_master,
                down_master,
            )
        )
    )
    query_weight, key_weight, value_weight, out_weight, gate_weight, up_weight, down_weight = (
        lax.all_gather(masters[0], "dp", axis=1, tiled=True),
        lax.all_gather(masters[1], "dp", axis=1, tiled=True),
        lax.all_gather(masters[2], "dp", axis=1, tiled=True),
        lax.all_gather(masters[3], "dp", axis=0, tiled=True),
        lax.all_gather(masters[4], "dp", axis=1, tiled=True),
        lax.all_gather(masters[5], "dp", axis=1, tiled=True),
        lax.all_gather(masters[6], "dp", axis=0, tiled=True),
    )
    attention_in = jnp.concatenate([query_weight, key_weight, value_weight], axis=1)
    feedforward_in = jnp.concatenate([gate_weight, up_weight], axis=1)
    width_row = query_weight.shape[1]
    heads_row = width_row // HEAD_DIM
    hidden_row = gate_weight.shape[1]
    member, position = sequence_marks(permutation, lengths, group_slot * group_rows, group_rows)
    query_member = lax.dynamic_slice_in_dim(member, col_slot * quarter, quarter)
    query_position = lax.dynamic_slice_in_dim(position, col_slot * quarter, quarter)
    block_rows = min(512, quarter)
    block_count = quarter // block_rows
    residual_in = own_tokens.astype(jnp.float32)
    scale_one = lax.rsqrt(col_total(residual_in * residual_in) / D + EPSILON)
    normed_one = (residual_in * scale_one[:, None] * attn_gain[None, :]).astype(jnp.bfloat16)
    spread_one = row_gather(normed_one)
    projected = col_reduce(spread_one, attention_in, False).astype(jnp.bfloat16)
    queries = projected[:, :width_row].reshape(quarter, heads_row, HEAD_DIM)
    keys_here = projected[:, width_row : 2 * width_row]
    values_here = projected[:, 2 * width_row :]
    key_flat, value_flat = key_gather(keys_here, values_here)
    key_all = key_flat.reshape(group_rows, heads_row, HEAD_DIM)
    value_all = value_flat.reshape(group_rows, heads_row, HEAD_DIM)

    def block_mask(first_row):
        return visible(
            lax.dynamic_slice_in_dim(query_member, first_row, block_rows),
            lax.dynamic_slice_in_dim(query_position, first_row, block_rows),
            member,
            position,
        )

    def forward_block(block_id):
        first_row = block_id * block_rows
        query_block = lax.dynamic_slice_in_dim(queries, first_row, block_rows, 0)
        scores = attend_scores(query_block, key_all, block_mask(first_row))
        highest = jnp.max(scores, axis=2, keepdims=True)
        totals = jnp.sum(jnp.exp(scores - highest), axis=2, keepdims=True)
        log_total = highest + jnp.log(totals)
        probability = jnp.exp(scores - log_total)
        output = jnp.einsum(
            "hqk,khd->qhd",
            probability.astype(jnp.bfloat16),
            value_all,
            preferred_element_type=jnp.float32,
        )
        return (output.astype(jnp.bfloat16).reshape(block_rows, width_row), log_total[:, :, 0])

    blocks_out, log_totals = lax.map(forward_block, jnp.arange(block_count, dtype=jnp.int32))
    attended = blocks_out.reshape(quarter, width_row)
    spread_attn = col_gather(attended)
    midway = residual_in + row_reduce(spread_attn, out_weight, False)
    scale_two = lax.rsqrt(col_total(midway * midway) / D + EPSILON)
    normed_two = (midway * scale_two[:, None] * ffn_gain[None, :]).astype(jnp.bfloat16)
    spread_two = row_gather(normed_two)
    gate_and_up = col_reduce(spread_two, feedforward_in, False)
    gate_value = gate_and_up[:, :hidden_row]
    up_value = gate_and_up[:, hidden_row:]
    sigmoid_gate = jax.nn.sigmoid(gate_value)
    hidden = (gate_value * sigmoid_gate * up_value).astype(jnp.bfloat16)
    grad_output = own_cotangent.astype(jnp.float32)
    spread_down = row_gather(own_cotangent)
    grad_hidden = col_reduce(spread_down, down_weight, True)
    spread_hidden = col_gather(hidden)
    grad_down = outer_sum(spread_hidden, spread_down)
    grad_gate_value = (
        grad_hidden * up_value * sigmoid_gate * (1.0 + gate_value * (1.0 - sigmoid_gate))
    ).astype(jnp.bfloat16)
    grad_up_value = (grad_hidden * gate_value * sigmoid_gate).astype(jnp.bfloat16)
    spread_gate_up = col_gather(jnp.concatenate([grad_gate_value, grad_up_value], axis=1))
    grad_normed_two = row_reduce(spread_gate_up, feedforward_in, True)
    spread_two = row_gather(normed_two)
    grad_feedforward = outer_sum(spread_two, spread_gate_up)
    grad_mid_norm, gain_two_part = norm_back(grad_normed_two, midway, scale_two, ffn_gain)
    grad_midway = grad_output + grad_mid_norm
    rounded_midway = grad_midway.astype(jnp.bfloat16)
    spread_back = row_gather(rounded_midway)
    grad_attended = col_reduce(spread_back, out_weight, True).astype(jnp.bfloat16)
    spread_attn = col_gather(attended)
    key_flat, value_flat = key_gather(keys_here, values_here)
    key_all = key_flat.reshape(group_rows, heads_row, HEAD_DIM)
    value_all = value_flat.reshape(group_rows, heads_row, HEAD_DIM)
    grad_out_local = outer_sum(spread_attn, spread_back)

    def backward_block(carried, block_id):
        first_row = block_id * block_rows
        query_block = lax.dynamic_slice_in_dim(queries, first_row, block_rows, 0)
        scores = attend_scores(query_block, key_all, block_mask(first_row))
        probability = jnp.exp(
            scores - lax.dynamic_index_in_dim(log_totals, block_id, 0, keepdims=False)[:, :, None]
        )
        weights_low = probability.astype(jnp.bfloat16)
        grad_block = lax.dynamic_slice_in_dim(grad_attended, first_row, block_rows, 0).reshape(
            block_rows, heads_row, HEAD_DIM
        )
        grad_soft = jnp.einsum(
            "qhd,khd->hqk", grad_block, value_all, preferred_element_type=jnp.float32
        )
        row_inner = jnp.sum(probability * grad_soft, axis=2, keepdims=True)
        grad_scores = (probability * (grad_soft - row_inner)).astype(jnp.bfloat16)
        grad_query_block = jnp.einsum(
            "hqk,khd->qhd", grad_scores, key_all, preferred_element_type=jnp.float32
        ) * HEAD_DIM ** (-0.5)
        grad_key_all = carried[0] + jnp.einsum(
            "hqk,qhd->khd", grad_scores, query_block, preferred_element_type=jnp.float32
        ) * HEAD_DIM ** (-0.5)
        grad_value_all = carried[1] + jnp.einsum(
            "hqk,qhd->khd", weights_low, grad_block, preferred_element_type=jnp.float32
        )
        return (
            (grad_key_all, grad_value_all),
            grad_query_block.astype(jnp.bfloat16).reshape(block_rows, width_row),
        )

    start_grads = jnp.zeros((group_rows, heads_row, HEAD_DIM), jnp.float32)
    key_value_grads, grad_queries = lax.scan(
        backward_block, (start_grads, start_grads), jnp.arange(block_count, dtype=jnp.int32)
    )
    grad_queries = grad_queries.reshape(quarter, width_row)
    grad_key_part = key_value_grads[0].reshape(group_rows, width_row)
    grad_value_part = key_value_grads[1].reshape(group_rows, width_row)
    grad_key_mine, grad_value_mine = (
        lax.psum_scatter(grad_key_part, "col", scatter_dimension=0, tiled=True),
        lax.psum_scatter(grad_value_part, "col", scatter_dimension=0, tiled=True),
    )
    spread_projected = col_gather(
        jnp.concatenate(
            [
                grad_queries,
                grad_key_mine.astype(jnp.bfloat16),
                grad_value_mine.astype(jnp.bfloat16),
            ],
            axis=1,
        )
    )
    grad_normed_one = row_reduce(spread_projected, attention_in, True)
    spread_one = row_gather(normed_one)
    grad_attention = outer_sum(spread_one, spread_projected)
    grad_in_norm, gain_one_part = norm_back(grad_normed_one, residual_in, scale_one, attn_gain)
    grad_own_tokens = grad_midway + grad_in_norm
    grad_attn_gain, grad_ffn_gain = lax.psum((gain_one_part, gain_two_part), ("dp", "row"))
    grad_query, grad_key, grad_value, grad_out, grad_gate, grad_up, grad_down_mine = (
        lax.psum_scatter(
            grad_attention[:, :width_row].astype(jnp.bfloat16),
            "dp",
            scatter_dimension=1,
            tiled=True,
        ).astype(jnp.float32),
        lax.psum_scatter(
            grad_attention[:, width_row : 2 * width_row].astype(jnp.bfloat16),
            "dp",
            scatter_dimension=1,
            tiled=True,
        ).astype(jnp.float32),
        lax.psum_scatter(
            grad_attention[:, 2 * width_row :].astype(jnp.bfloat16),
            "dp",
            scatter_dimension=1,
            tiled=True,
        ).astype(jnp.float32),
        lax.psum_scatter(
            grad_out_local.astype(jnp.bfloat16), "dp", scatter_dimension=0, tiled=True
        ).astype(jnp.float32),
        lax.psum_scatter(
            grad_feedforward[:, :hidden_row].astype(jnp.bfloat16),
            "dp",
            scatter_dimension=1,
            tiled=True,
        ).astype(jnp.float32),
        lax.psum_scatter(
            grad_feedforward[:, hidden_row:].astype(jnp.bfloat16),
            "dp",
            scatter_dimension=1,
            tiled=True,
        ).astype(jnp.float32),
        lax.psum_scatter(
            grad_down.astype(jnp.bfloat16), "dp", scatter_dimension=0, tiled=True
        ).astype(jnp.float32),
    )
    total_tokens = permutation.shape[0]
    inverse = (
        jnp.zeros((total_tokens,), jnp.int32)
        .at[permutation]
        .set(jnp.arange(total_tokens, dtype=jnp.int32))
    )
    wanted_slots = lax.dynamic_slice_in_dim(inverse, device_slot * own_rows, own_rows)
    (grad_tokens,) = make_picker(
        wanted_slots,
        (jnp.zeros_like(grad_own_tokens),),
        (
            (
                lax.all_gather(
                    grad_own_tokens.astype(jnp.bfloat16), ("dp", "row"), axis=0, tiled=True
                ),
            )[0].astype(jnp.float32),
        ),
    )
    return (
        grad_tokens,
        grad_query,
        grad_key,
        grad_value,
        grad_out,
        grad_gate,
        grad_up,
        grad_down_mine,
        grad_attn_gain,
        grad_ffn_gain,
    )


def scores_of(query, key):
    return lax.dot_general(
        query, key, (((1,), (1,)), ((), ())), preferred_element_type=F32
    ) * HEAD_DIM ** (-0.5)


MESH = pl.DeviceIdType.MESH
PLACE = {0: 0, 2: 1, 1: 2, 3: 3}
TILE = 256


class Post:
    def __init__(self, send_sem, recv_sem):
        self.send_sem, self.recv_sem, self.used = send_sem, recv_sem, 0

    def ready(self, src, dst, target, slot=None):
        if slot is None:
            slot = self.used
            self.used += 1
        return pltpu.make_async_remote_copy(
            src_ref=src,
            dst_ref=dst,
            send_sem=self.send_sem.at[slot],
            recv_sem=self.recv_sem.at[slot],
            device_id=target,
            device_id_type=MESH,
        )

    def take(self, count):
        first = self.used
        self.used += count
        return first

    def send(self, src, dst, target):
        copy = self.ready(src, dst, target)
        copy.start()
        return copy


def greet(peers):
    barrier = pltpu.get_barrier_semaphore()
    for peer in peers:
        pl.semaphore_signal(barrier, inc=1, device_id=peer, device_id_type=MESH)
    pl.semaphore_wait(barrier, len(peers))


def as_row(column):
    return jnp.transpose(jnp.broadcast_to(column, (column.shape[0], 128)))[0:8]


def as_column(row):
    return jnp.transpose(row)[:, 0:1]


def scatter_plane(post, low, landed, rows, me):
    d, r, c = me
    half = rows // 2
    x_at, y_at = (d, r ^ 1, c), (d, r, c ^ 2)
    upper, lower = pl.ds(0, half), pl.ds(half, half)
    corner_x = post.send(low(rows, half, 1), landed.at[2, upper], x_at)
    corner_y = post.send(low(rows + half, half, 1), landed.at[2, lower], y_at)
    sent = [
        post.send(low(rows, half, 0), landed.at[0, upper], x_at),
        post.send(low(half, half, 1), landed.at[1, lower], y_at),
    ]

    def add(ref, first):
        def one(t, total):
            part = pl.ds(pl.multiple_of(t * 64, 64), 64)
            there = pl.ds(pl.multiple_of(first + t * 64, 64), 64)
            ref[part, :] = (ref[part, :].astype(F32) + landed[2, there, :].astype(F32)).astype(BF)
            return total

        lax.fori_loop(0, half // 64, one, 0)

    corner_x.wait_recv()
    add(low(0, half, 1), 0)
    sent.append(post.send(low(0, half, 1), landed.at[1, upper], y_at))
    corner_y.wait_recv()
    add(low(rows + half, half, 0), half)
    sent.append(post.send(low(rows + half, half, 0), landed.at[0, lower], x_at))
    return sent, [corner_x, corner_y]


def forward_kernel(
    x_ref, gain_one_ref, gain_two_ref, lengths_ref, query_ref, key_ref, value_ref, out_ref, gate_hbm, up_hbm,
    own_grad,
    mid_ref, scale_ref, n2_ref, begin_ref, first_scale,
    normed_out, weight_in_out, weight_out_out, q_out, kv_out, att_out, lse_out, own_up, gate_all, up_all, grad_all,
    normed_ref, weight_in, weight_out, q_ref, kv_ref, att_ref, lse_ref, masters,
    zin, zout, sums, wide, given, arrived, low, landed, x32, hidden_own,
    send_sem, recv_sem, local_sem,
):
    d, r, c = (lax.axis_index(name) for name in AXES)
    y, core = c // 2, lax.rem(c, 2)
    rows = x_ref.shape[0]
    fc = x_ref.shape[1]
    group = 2 * rows
    width = q_ref.shape[1]
    half = 2 * fc
    post = Post(send_sem, recv_sem)
    fetches = [
        pltpu.make_async_copy(src, masters.at[n], local_sem.at[8 + n]) for n, src in enumerate((gate_hbm, up_hbm))
    ]
    for copy in fetches:
        copy.start()
    copies = []

    def copy_out(src, dst):
        copy = pltpu.make_async_copy(src, dst, local_sem.at[10 + len(copies)])
        copy.start()
        copies.append(copy)

    in_plane = [(d, r ^ a, c ^ b) for a in (0, 1) for b in range(COL) if (a, b) != (0, 0)]
    greet([(d ^ j, r, c) for j in (1, 2, 3)] + in_plane)

    def fill_x(t, total):
        part = pl.ds(pl.multiple_of(t * 128, 128), 128)
        value = x_ref[part, :].astype(F32)
        x32[part, :] = value
        sums[0, :, part] = as_row(jnp.sum(value * value, axis=1, keepdims=True))
        return total

    lax.fori_loop(0, rows // 128, fill_x, 0)
    small = [post.send(sums.at[0], sums.at[m], (d, r, c ^ m)) for m in (1, 2, 3)]

    parts = (pl.ds(width, 2 * width), pl.ds(0, width))
    first, first_down = post.take(3 * DP), post.take(3 * DP)

    def block_of(n, p):
        return zin.at[p, :, parts[n]] if n < 2 else zout.at[p]

    def line(n, p, target_plane):
        block = block_of(n, p)
        return post.ready(block, block, (target_plane, r, c), first + DP * n + p)

    def line_down(n, p, target_plane):
        block = block_of(n, p)
        return pltpu.make_async_remote_copy(
            src_ref=block, dst_ref=block,
            send_sem=send_sem.at[first_down + DP * n + p], recv_sem=recv_sem.at[first + DP * n + p],
            device_id=(target_plane, r, c), device_id_type=MESH,
        )

    def cast_rows(src, dst, amount, step=64):
        def one(t, total):
            part = pl.ds(pl.multiple_of(t * step, step), step)
            dst(part, src[part, :].astype(BF))
            return total

        lax.fori_loop(0, amount // step, one, 0)

    for place, master in enumerate((query_ref, key_ref, value_ref)):
        def put(part, value, place=place):
            zin[d, part, place * width : (place + 1) * width] = value

        cast_rows(master, put, fc)
    def leave(n):
        @pl.when(d < DP - 1)
        def _():
            line(n, d, d + 1).start()

        @pl.when(d > 0)
        def _():
            line_down(n, d, d - 1).start()

    leave(0)
    leave(1)

    first_cols = post.take(3 * DP)

    def place_of(m):
        return lax.rem(m, 2) * 2 + m // 2

    def seat_of(n, place):
        there = pl.ds(pl.multiple_of(place * fc, fc), fc)
        return weight_in.at[there, parts[n]] if n < 2 else weight_out.at[:, there]

    def to_column(n, p):
        return pltpu.make_async_remote_copy(
            src_ref=block_of(n, p),
            dst_ref=seat_of(n, place_of(p ^ c)),
            send_sem=send_sem.at[first_cols + DP * n + p],
            recv_sem=recv_sem.at[first_cols + DP * n + (p ^ c)],
            device_id=(d, r, p), device_id_type=MESH,
        )

    def keep(n):
        return pltpu.make_async_copy(block_of(n, c), seat_of(n, 0), local_sem.at[(0, 1, 5)[n]])

    def pass_on(n, p):
        @pl.when(p == c)
        def _():
            keep(n).start()

        @pl.when(p != c)
        def _():
            to_column(n, p).start()

    hidden_all = (gate_all, up_all)
    first_sent = post.take(10)
    first_got = first_sent

    def slab(kind, i):
        return hidden_all[kind].at[pl.ds(pl.multiple_of(place_of(i) * fc, fc), fc), :]

    def ship(kind, way, i, target, src=None):
        return pltpu.make_async_remote_copy(
            src_ref=hidden_own.at[kind] if src is None else src,
            dst_ref=slab(kind, i),
            send_sem=send_sem.at[first_sent + 5 * kind + way],
            recv_sem=recv_sem.at[first_got + 4 * kind + i],
            device_id=target, device_id_type=MESH,
        )

    def keep_hidden(kind):
        return pltpu.make_async_copy(hidden_own.at[kind], slab(kind, 0), local_sem.at[3 + kind])

    def to_core(kind):
        return ship(kind, 0, 1, (d, r, c ^ 1))

    def over_y(kind):
        return ship(kind, 1, 2 + core, (d, r, 2 * (1 - y)))

    def over_x(kind):
        return ship(kind, 2, 1 - core, (d, r ^ 1, 2 * y + 1))

    def relay(kind, i):
        return ship(kind, i + 1, 5 - i, (d, r ^ 1, 2 * y + 1), slab(kind, i))

    def start_home(kind):
        @pl.when(core == 0)
        def _():
            keep_hidden(kind).start()

        @pl.when(core == 1)
        def _():
            to_core(kind).start()

    def start_relay(kind):
        @pl.when(core == 0)
        def _():
            for i in (2, 3):
                ship(kind, 0, i, (d, r, c)).wait_recv()
                relay(kind, i).start()

    def cast_hidden(kind):
        def put(part, value):
            hidden_own[kind, part, :] = value

        fetches[kind].wait()
        cast_rows(masters.at[kind], put, fc)

    cast_hidden(0)
    over_x(0).start()
    over_y(0).start()
    for copy in small:
        copy.wait_recv()

    def norm_one(t, total):
        part = pl.ds(pl.multiple_of(t * 128, 128), 128)
        square = sums[0, :, part] + sums[2, :, part] + sums[1, :, part] + sums[3, :, part]
        scale = lax.rsqrt(as_column(square) / D + EPSILON)
        first_scale[part, :] = scale
        normed_ref[part, 0:fc] = (x32[part, :] * scale * gain_one_ref[...]).astype(BF)
        return total

    lax.fori_loop(0, rows // 128, norm_one, 0)
    own_rows, other_rows = pl.ds(0, rows), pl.ds(rows, rows)

    def columns(place):
        return pl.ds(place * fc, fc)

    own_block = normed_ref.at[own_rows, columns(0)]
    beside = post.send(own_block, normed_ref.at[other_rows, columns(0)], (d, r ^ 1, c))
    beyond = post.send(own_block, normed_ref.at[own_rows, columns(1)], (d, r, c ^ 2))
    corner = post.send(own_block, normed_ref.at[other_rows, columns(1)], (d, r ^ 1, c ^ 2))
    sibling = (d, r, c ^ 1)
    shared = [post.send(own_block, normed_ref.at[own_rows, columns(2)], sibling)]
    pass_on(0, d)
    pass_on(1, d)
    cast_hidden(1)
    start_home(0)
    start_home(1)
    copy_out(hidden_own.at[1], own_up)
    over_x(1).start()
    half_rows = rows // 2
    grad_cross = post.send(
        own_grad.at[pl.ds(pl.multiple_of((1 - y) * half_rows, half_rows), half_rows), :],
        grad_all.at[pl.ds(0, half_rows), pl.ds(fc, fc)],
        (d, r, c ^ 2),
    )
    grad_keep = pltpu.make_async_copy(
        own_grad.at[pl.ds(pl.multiple_of(y * half_rows, half_rows), half_rows), :],
        grad_all.at[pl.ds(0, half_rows), pl.ds(0, fc)],
        local_sem.at[2],
    )
    grad_keep.start()

    def put_out(part, value):
        zout[d, part, :] = value

    cast_rows(out_ref, put_out, width)

    def find_begins(t, total):
        part = pl.ds(pl.multiple_of(t * 128, 128), 128)
        place = lax.broadcasted_iota(jnp.int32, (128, 1), 0) + (d * group + t * 128)
        end = jnp.int32(0)
        begin = jnp.zeros((128, 1), jnp.int32)
        for n in range(lengths_ref.shape[0]):
            end = end + lengths_ref[n]
            begin = jnp.where(place >= end, end, begin)
        begin_ref[part, :] = begin - d * group
        return total

    lax.fori_loop(0, group // 128, find_begins, 0)

    def line_step(s, which=(0, 1)):
        for n in which:
            for p, valid, onward, forward in (
                (d - s, d - s >= 0, d < DP - 1, lambda n, p: line(n, p, d + 1)),
                (d + s, d + s < DP, d > 0, lambda n, p: line_down(n, p, d - 1)),
            ):
                @pl.when(valid)
                def _(n=n, p=p, onward=onward, forward=forward):
                    line(n, p, d).wait_recv()

                    @pl.when(onward)
                    def _():
                        forward(n, p).start()

                    pass_on(n, p)

    line_step(1)
    leave(2)
    line_step(2)
    pass_on(2, d)
    line_step(1, (2,))
    for copy, where, place in ((beside, other_rows, 0), (beyond, own_rows, 1), (corner, other_rows, 1)):
        copy.wait_recv()
        shared.append(
            post.send(normed_ref.at[where, columns(place)], normed_ref.at[where, columns(place + 2)], sibling)
        )
    line_step(3)
    line_step(2, (2,))
    start_relay(0)

    def arrived_blocks(n):
        keep(n).wait()
        for m in (1, 2, 3):
            pltpu.make_async_remote_copy(
                src_ref=block_of(n, 0), dst_ref=seat_of(n, 0),
                send_sem=send_sem.at[first_cols], recv_sem=recv_sem.at[first_cols + DP * n + m],
                device_id=(d, r, c), device_id_type=MESH,
            ).wait_recv()

    for copy in shared:
        copy.wait_recv()
    arrived_blocks(0)
    copy_out(normed_ref, normed_out)

    def turned(t):
        return lax.rem(t + 2 * r, group // TILE)

    def project_kv(t, total):
        part = pl.ds(pl.multiple_of(t * TILE, TILE), TILE)
        to = pl.ds(pl.multiple_of(REACH + turned(t) * TILE, TILE), TILE)
        kv_ref[to, :] = jnp.dot(
            normed_ref[part, :], weight_in[:, width:], preferred_element_type=F32
        ).astype(BF)
        return total

    lax.fori_loop(0, group // TILE, project_kv, 0)
    halo = post.ready(kv_ref.at[pl.ds(group, REACH), :], kv_ref.at[pl.ds(0, REACH), :], (lax.rem(d + 1, DP), r, c))

    @pl.when(d < DP - 1)
    def _():
        halo.start()

    arrived_blocks(1)

    def project_q(t, total):
        part = pl.ds(pl.multiple_of(t * TILE, TILE), TILE)
        to = pl.ds(pl.multiple_of(turned(t) * TILE, TILE), TILE)
        q_ref[to, :] = jnp.dot(
            normed_ref[part, :], weight_in[:, :width], preferred_element_type=F32
        ).astype(BF)
        return total

    lax.fori_loop(0, group // TILE, project_q, 0)

    copy_out(weight_in, weight_in_out)
    copy_out(q_ref, q_out)
    line_step(3, (2,))
    grad_cross.wait_recv()
    grad_keep.wait()
    grads = [
        post.send(
            grad_all.at[pl.ds(0, half_rows), pl.ds(0, half)],
            grad_all.at[pl.ds(j * half_rows, half_rows), pl.ds(0, half)],
            (d ^ j, r, c),
        )
        for j in (1, 2, 3)
    ]
    grads_shared = [
        post.send(
            grad_all.at[pl.ds(0, half_rows), pl.ds(0, half)],
            grad_all.at[pl.ds(0, half_rows), pl.ds(half, half)],
            sibling,
        )
    ]

    @pl.when(d == 0)
    def _():
        kv_ref[pl.ds(0, REACH), :] = jnp.zeros((REACH, 2 * width), BF)

    @pl.when(d > 0)
    def _():
        halo.wait_recv()

    copy_out(kv_ref, kv_out)

    span = TILE + REACH
    for h in range(width // HEAD_DIM):
        lanes = pl.ds(h * HEAD_DIM, HEAD_DIM)
        value_lanes = pl.ds(width + h * HEAD_DIM, HEAD_DIM)

        def one(t, total, lanes=lanes, value_lanes=value_lanes):
            part = pl.ds(pl.multiple_of(t * TILE, TILE), TILE)
            to = pl.ds(pl.multiple_of(turned(t) * TILE, TILE), TILE)
            window = pl.ds(pl.multiple_of(t * TILE, TILE), span)
            scores = scores_of(q_ref[part, lanes], kv_ref[window, lanes])
            query = lax.broadcasted_iota(jnp.int32, (TILE, span), 0)
            key = lax.broadcasted_iota(jnp.int32, (TILE, span), 1)
            begin = begin_ref[part, 0:1] + (REACH - t * TILE)
            allowed = (key <= query + REACH) & (key >= begin)
            scores = jnp.where(allowed, scores, NEG_FILL)
            highest = jnp.max(scores, axis=1, keepdims=True)
            expo = jnp.exp(scores - highest)
            total_e = jnp.sum(expo, axis=1, keepdims=True)
            probability = (expo * (1.0 / total_e)).astype(BF)
            att_ref[to, lanes] = jnp.dot(
                probability, kv_ref[window, value_lanes], preferred_element_type=F32
            ).astype(BF)
            lse_ref[part, lanes] = jnp.broadcast_to(highest + jnp.log(total_e), (TILE, HEAD_DIM))
            return total

        lax.fori_loop(0, group // TILE, one, 0)

    copy_out(att_ref, att_out)
    copy_out(lse_ref, lse_out)
    arrived_blocks(2)
    copy_out(weight_out, weight_out_out)

    def out_given(t, total):
        part = pl.ds(pl.multiple_of(t * TILE, TILE), TILE)
        given[part, :] = jnp.dot(
            att_ref[part, :], weight_out[:, half:], preferred_element_type=F32
        ).astype(BF)
        return total

    lax.fori_loop(0, group // TILE, out_given, 0)
    to_sibling = post.send(given, arrived, sibling)

    def out_kept(t, total):
        part = pl.ds(pl.multiple_of(t * TILE, TILE), TILE)
        wide[part, :] = jnp.dot(att_ref[part, :], weight_out[:, :half], preferred_element_type=F32)
        return total

    lax.fori_loop(0, group // TILE, out_kept, 0)
    to_sibling.wait_recv()

    def add_low(t, total):
        part = pl.ds(pl.multiple_of(t * 128, 128), 128)
        value = wide[part, :] + arrived[part, :].astype(F32)
        wide[part, :] = value
        low[part, :] = value.astype(BF)
        return total

    lax.fori_loop(0, group // 128, add_low, 0)
    pieces, corners = scatter_plane(
        post, lambda first, count, place: low.at[pl.ds(first, count), columns(place)], landed, rows, (d, r, c)
    )
    for copy in pieces:
        copy.wait_recv()

    def middle(t, total):
        part = pl.ds(pl.multiple_of(t * 128, 128), 128)
        value = (
            x32[part, :] + wide[part, 0:fc] + landed[0, part, :].astype(F32)
            + landed[1, part, :].astype(F32)
        )
        mid_ref[part, :] = value
        sums[4, :, part] = as_row(jnp.sum(value * value, axis=1, keepdims=True))
        return total

    lax.fori_loop(0, rows // 128, middle, 0)
    again = [post.send(sums.at[4], sums.at[4 + m], (d, r, c ^ m)) for m in (1, 2, 3)]
    for copy in again:
        copy.wait_recv()

    def norm_two(t, total):
        part = pl.ds(pl.multiple_of(t * 128, 128), 128)
        square = sums[4, :, part] + sums[6, :, part] + sums[5, :, part] + sums[7, :, part]
        scale = lax.rsqrt(as_column(square) / D + EPSILON)
        scale_ref[part, :] = scale
        n2_ref[part, :] = (mid_ref[part, :] * scale * gain_two_ref[...]).astype(BF)
        return total

    lax.fori_loop(0, rows // 128, norm_two, 0)

    for j, copy in zip((1, 2, 3), grads):
        copy.wait_recv()
        there = pl.ds(j * half_rows, half_rows)
        grads_shared.append(
            post.send(grad_all.at[there, pl.ds(0, half)], grad_all.at[there, pl.ds(half, half)], sibling)
        )
    for copy in grads_shared:
        copy.wait_recv()
    over_y(0).wait_send()
    for kind in (0, 1):
        over_x(kind).wait_send()

        @pl.when(core == 0)
        def _(kind=kind):
            keep_hidden(kind).wait()
            ship(kind, 0, 1, (d, r, c)).wait_recv()
            if kind == 0:
                for i in (2, 3):
                    relay(kind, i).wait_send()

        @pl.when(core == 1)
        def _(kind=kind):
            to_core(kind).wait_send()
            for i in range(COL if kind == 0 else 2):
                ship(kind, 0, i, (d, r, c)).wait_recv()

    for copy in (
        small + [grad_cross, beside, beyond, corner] + shared + grads + grads_shared
        + [to_sibling] + pieces + corners + again
    ):
        copy.wait_send()

    @pl.when(d < DP - 1)
    def _():
        halo.wait_send()

    for copy in copies:
        copy.wait()
    for n in (0, 1, 2):
        for p in range(DP):
            @pl.when((d < DP - 1) & (p <= d))
            def _(n=n, p=p):
                line(n, p, d).wait_send()

            @pl.when((d > 0) & (p >= d))
            def _(n=n, p=p):
                line_down(n, p, d).wait_send()

            @pl.when(c != p)
            def _(n=n, p=p):
                to_column(n, p).wait_send()


SENDS = 96


def forward(x, gain_one, gain_two, lengths, query, key, value, out, gate, up, own_grad):
    rows, fc = x.shape
    group = 2 * rows
    width = out.shape[0]
    units = gate.shape[1]
    vmem = pl.BlockSpec(memory_space=pltpu.VMEM)
    smem = pl.BlockSpec(memory_space=pltpu.SMEM)
    hbm = pl.BlockSpec(memory_space=pl.ANY)

    def like(shape, dtype=BF):
        return jax.ShapeDtypeStruct(shape, dtype)

    return pl.pallas_call(
        forward_kernel,
        in_specs=[vmem] * 3 + [smem] + [vmem] * 4 + [hbm] * 3,
        out_specs=[vmem] * 5 + [hbm] * 11,
        out_shape=[
            like((rows, fc), F32),
            like((rows, 1), F32),
            like((rows, fc)),
            like((group, 1), jnp.int32),
            like((rows, 1), F32),
            like((group, D)),
            like((D, 3 * width)),
            like((width, D)),
            like((group, width)),
            like((REACH + group, 2 * width)),
            like((group, width)),
            like((group, width), F32),
            like((fc, units)),
            like((D, units)),
            like((D, units)),
            like((group, D)),
        ],
        scratch_shapes=[
            pltpu.VMEM((group, D), BF),
            pltpu.VMEM((D, 3 * width), BF),
            pltpu.VMEM((width, D), BF),
            pltpu.VMEM((group, width), BF),
            pltpu.VMEM((REACH + group, 2 * width), BF),
            pltpu.VMEM((group, width), BF),
            pltpu.VMEM((group, width), F32),
            pltpu.VMEM((2, fc, units), F32),
            pltpu.VMEM((DP, fc, 3 * width), BF),
            pltpu.VMEM((DP, width, fc), BF),
            pltpu.VMEM((8, 8, rows), F32),
            pltpu.VMEM((group, 2 * fc), F32),
            pltpu.VMEM((group, 2 * fc), BF),
            pltpu.VMEM((group, 2 * fc), BF),
            pltpu.VMEM((group, 2 * fc), BF),
            pltpu.VMEM((3, rows, fc), BF),
            pltpu.VMEM((rows, fc), F32),
            pltpu.VMEM((2, fc, units), BF),
            pltpu.SemaphoreType.DMA((SENDS,)),
            pltpu.SemaphoreType.DMA((SENDS,)),
            pltpu.SemaphoreType.DMA((20,)),
        ],
        compiler_params=pltpu.CompilerParams(
            collective_id=1, has_side_effects=True, vmem_limit_bytes=60 << 20
        ),
        cost_estimate=pl.CostEstimate(
            flops=6 * group * D * width, bytes_accessed=64 << 20, transcendentals=0
        ),
    )(x, gain_one, gain_two, lengths, query, key, value, out, gate, up, own_grad)


def at(t, size):
    return pl.ds(pl.multiple_of(t * size, size), size)


def loop(count, body):
    def one(t, total):
        body(t)
        return total

    lax.fori_loop(0, count, one, 0)


def maker(send_sem, recv_sem):
    def raw(src, dst, sent, got_at, target):
        return pltpu.make_async_remote_copy(
            src_ref=src, dst_ref=dst, send_sem=send_sem.at[sent], recv_sem=recv_sem.at[got_at],
            device_id=target, device_id_type=MESH,
        )

    return raw


class LineSum:
    def __init__(self, raw, arrays, base, me):
        self.raw, self.arrays, self.base, self.me = raw, arrays, base, me

    def sem(self, n, p, down):
        return self.base + 8 * n + 4 * down + p

    def take(self, p, down, done):
        d = self.me[0]
        for n, (z, got_z) in enumerate(self.arrays):
            self.raw(z.at[p], got_z.at[p], self.sem(n, p, down), self.sem(n, p, down), self.me).wait_recv()

        @pl.when(jnp.logical_not(done))
        def _():
            for z, got_z in self.arrays:
                def one(t, z=z, got_z=got_z):
                    z[p, at(t, 64), :] = (
                        z[p, at(t, 64), :].astype(F32) + got_z[p, at(t, 64), :].astype(F32)
                    ).astype(BF)

                loop(z.shape[1] // 64, one)

    def up(self, p):
        d, r, c = self.me

        @pl.when((d > 0) & (d <= p))
        def _():
            self.take(p, 0, d == p)

        @pl.when(d < p)
        def _():
            for n, (z, got_z) in enumerate(self.arrays):
                self.raw(z.at[p], got_z.at[p], self.sem(n, p, 0), self.sem(n, p, 0), (d + 1, r, c)).start()

    def down(self, p):
        d, r, c = self.me

        @pl.when((d < DP - 1) & (d >= p))
        def _():
            self.take(p, 1, d == p)

        @pl.when(d > p)
        def _():
            slot = jnp.where(p < d - 1, p, DP)
            for n, (z, got_z) in enumerate(self.arrays):
                self.raw(z.at[p], got_z.at[slot], self.sem(n, p, 1), self.sem(n, p, 1), (d - 1, r, c)).start()

    def begin(self):
        d = self.me[0]

        @pl.when(d == 0)
        def _():
            for p in (3, 2, 1):
                self.up(p)

        @pl.when(d == DP - 1)
        def _():
            for p in (0, 1, 2):
                self.down(p)

    def rest(self):
        d = self.me[0]

        @pl.when(d == 0)
        def _():
            self.down(0)

        @pl.when(d == 1)
        def _():
            self.up(3)
            self.up(2)
            self.down(0)
            self.down(1)
            self.up(1)

        @pl.when(d == 2)
        def _():
            self.down(0)
            self.down(1)
            self.up(3)
            self.up(2)
            self.down(2)

        @pl.when(d == DP - 1)
        def _():
            self.up(3)

    def settle(self):
        d = self.me[0]
        for p in range(DP):
            for n, (z, got_z) in enumerate(self.arrays):
                for down, sent in ((0, d < p), (1, d > p)):
                    @pl.when(sent)
                    def _(p=p, n=n, z=z, got_z=got_z, down=down):
                        self.raw(
                            z.at[p], got_z.at[p], self.sem(n, p, down), self.sem(n, p, down), self.me
                        ).wait_send()

    def total(self, z, got_z, part):
        d = self.me[0]
        value = z[d, part, :].astype(F32)
        value = value + jnp.where(d > 0, got_z[d, part, :].astype(F32), 0.0)
        return value + jnp.where(d < DP - 1, got_z[DP, part, :].astype(F32), 0.0)


class PlaneSum:
    def __init__(self, raw, stage, got, comb, base, local_sem, local_base, me):
        self.raw, self.stage, self.got, self.comb, self.base = raw, stage, got, comb, base
        self.local_sem, self.local_base, self.me = local_sem, local_base, me
        self.kinds = range(stage.shape[0])

    def from_one(self, kind, i):
        d, r, c = self.me
        y = c // 2
        sent, base = self.base + 10 * kind + i, self.base + 10 * kind
        if i < 2:
            return self.raw(self.stage.at[kind, i], self.got.at[kind, 0], sent, base, (d, r ^ 1, 2 * y + 1 - i))
        return self.raw(
            self.stage.at[kind, i], self.comb.at[kind, 3 - i], sent, base + 3 + (3 - i), (d, r ^ 1, 2 * y)
        )

    def from_zero(self, kind, i):
        d, r, c = self.me
        sent, base = self.base + 10 * kind + i, self.base + 10 * kind
        if i == 1:
            return self.raw(self.stage.at[kind, i], self.got.at[kind, 1], sent, base + 1, (d, r, c ^ 1))
        return self.raw(
            self.stage.at[kind, i], self.got.at[kind, 2], sent, base + 2, (d, r, 2 * (1 - c // 2) + i - 2)
        )

    def home(self, kind):
        return pltpu.make_async_copy(
            self.stage.at[kind, 0], self.got.at[kind, 1], self.local_sem.at[self.local_base + kind]
        )

    def start_far(self):
        @pl.when(lax.rem(self.me[2], 2) == 1)
        def _():
            for i in (2, 3):
                for kind in self.kinds:
                    self.from_one(kind, i).start()

    def start_near(self):
        core = lax.rem(self.me[2], 2)

        @pl.when(core == 1)
        def _():
            for i in (0, 1):
                for kind in self.kinds:
                    self.from_one(kind, i).start()

        @pl.when(core == 0)
        def _():
            for kind in self.kinds:
                self.home(kind).start()
                self.from_zero(kind, 1).start()

    def combine(self, room, local_base):
        core = lax.rem(self.me[2], 2)

        @pl.when(core == 0)
        def _():
            for i in (2, 3):
                for kind in self.kinds:
                    self.raw(
                        self.stage.at[kind, i], self.comb.at[kind, i - 2], self.base,
                        self.base + 10 * kind + 3 + (i - 2), self.me,
                    ).wait_recv()
                    fetch = pltpu.make_async_copy(
                        self.comb.at[kind, i - 2], room(kind, i - 2),
                        self.local_sem.at[local_base + 2 * kind + i - 2],
                    )
                    fetch.start()
                    fetch.wait()

                    def add(t, kind=kind, i=i):
                        self.stage[kind, i, at(t, 64), :] = (
                            self.stage[kind, i, at(t, 64), :].astype(F32)
                            + room(kind, i - 2)[at(t, 64), :].astype(F32)
                        ).astype(BF)

                    loop(self.stage.shape[2] // 64, add)
                    self.from_zero(kind, i).start()

    def settle(self):
        core = lax.rem(self.me[2], 2)
        for kind in self.kinds:
            base = self.base + 10 * kind
            for n in (0, 2):
                self.raw(self.stage.at[kind, 0], self.got.at[kind, n], self.base, base + n, self.me).wait_recv()

            @pl.when(core == 1)
            def _(kind=kind, base=base):
                self.raw(self.stage.at[kind, 0], self.got.at[kind, 1], self.base, base + 1, self.me).wait_recv()
                for i in range(COL):
                    self.from_one(kind, i).wait_send()

            @pl.when(core == 0)
            def _(kind=kind):
                self.home(kind).wait()
                for i in (1, 2, 3):
                    self.from_zero(kind, i).wait_send()


def middle_kernel(
    n2_ref, mid_ref, scale_ref, gain_ref, own_grad, down_ref, own_up, gate_hbm, up_hbm, grad_hbm,
    grad_out, gain_out, got, comb, n2_out, dgate_out, dup_out,
    n2, dgate, dup, wg, wu, wd, gb, own_down, gate, up, du, hidden, given, arrived, z, got_z, crossing, crossed, gn, sums, stage,
    send_sem, recv_sem, local_sem,
):
    d, r, c = (lax.axis_index(name) for name in AXES)
    me = (d, r, c)
    y, core = c // 2, lax.rem(c, 2)
    rows, fc = n2_ref.shape
    block = rows // 2
    units = own_down.shape[0]
    half = 2 * fc
    over = (((0,), (0,)), ((), ()))
    across = (((1,), (1,)), ((), ()))
    post = Post(send_sem, recv_sem)
    raw = maker(send_sem, recv_sem)
    sibling = (d, r, c ^ 1)
    others = [(a, b) for a in (0, 1) for b in range(COL) if (a, b) != (0, 0)]
    greet([(d, r ^ a, c ^ b) for a, b in others] + [(d ^ j, r, c) for j in (1, 2, 3)])

    cross = post.send(
        n2_ref.at[pl.ds(pl.multiple_of((1 - y) * block, block), block), :],
        n2.at[pl.ds(0, block), pl.ds(fc, fc)],
        (d, r, c ^ 2),
    )
    def half_of(ref, i, n):
        return ref.at[pl.ds(pl.multiple_of(place_of(i) * fc + n * (fc // 2), fc // 2), fc // 2), :]

    def place_of(i):
        return lax.rem(i, 2) * 2 + i // 2

    first_wide = post.take(8)

    def up_over_y(n):
        return raw(
            own_up.at[pl.ds(n * (fc // 2), fc // 2), :], half_of(wu, 2 + core, n),
            first_wide + 4 * n, first_wide + 4 * n + core, (d, r, 2 * (1 - y)),
        )

    def up_relay(n, i):
        return raw(
            half_of(wu, i, n), half_of(wu, 5 - i, n), first_wide + 4 * n + i - 1,
            first_wide + 4 * n + 3 - i, (d, r ^ 1, 2 * y + 1),
        )

    def up_came(n, i):
        return raw(half_of(wu, i, n), half_of(wu, i, n), first_wide, first_wide + 4 * n + i - 2, me)

    for n in (0, 1):
        up_over_y(n).start()
    loads = [
        pltpu.make_async_copy(src, dst, local_sem.at[n])
        for n, (src, dst) in zip((0, 1, 2, 9), (
            (gate_hbm, wg),
            (up_hbm.at[pl.ds(0, fc), :], wu.at[pl.ds(0, fc), :]),
            (grad_hbm, gb),
            (up_hbm.at[pl.ds(2 * fc, fc), :], wu.at[pl.ds(2 * fc, fc), :]),
        ))
    ]
    for load in loads:
        load.start()

    def cast_down(t):
        own_down[at(t, 64), :] = down_ref[at(t, 64), :].astype(BF)

    loop(units // 64, cast_down)
    first_sent = post.take(10)

    def piece(ref, n):
        return ref.at[pl.ds(n * (units // 2), units // 2), :]

    def ship(n, way, i, target, src=None):
        return raw(
            piece(own_down if src is None else src, n), piece(wd.at[place_of(i)], n),
            first_sent + 5 * n + way, first_sent + 5 * n + i, target,
        )

    keep_down = pltpu.make_async_copy(own_down, wd.at[0], local_sem.at[3])

    def to_core(n):
        return ship(n, 0, 1, sibling)

    def over_y(n):
        return ship(n, 1, 2 + core, (d, r, 2 * (1 - y)))

    def over_x(n):
        return ship(n, 2, 1 - core, (d, r ^ 1, 2 * y + 1))

    def relay(n, i):
        return ship(n, i + 1, 5 - i, (d, r ^ 1, 2 * y + 1), wd.at[PLACE[i]])

    for n in (0, 1):
        over_x(n).start()
        over_y(n).start()

    @pl.when(core == 0)
    def _():
        keep_down.start()

    @pl.when(core == 1)
    def _():
        for n in (0, 1):
            to_core(n).start()

    def pass_down(n):
        @pl.when(core == 0)
        def _():
            for i in (2, 3):
                ship(n, 0, i, me).wait_recv()
                relay(n, i).start()

    n2[0:block, 0:fc] = n2_ref[pl.ds(pl.multiple_of(y * block, block), block), :]
    cross.wait_recv()

    first_up, first_down = post.take(DP), post.take(DP)
    first_shared = post.take(DP)

    def rail(p, e):
        return n2.at[at(p ^ e, block), pl.ds(0, half)]

    def go_up(p):
        return raw(rail(p, d), rail(p, d + 1), first_up + p, first_up + p, (d + 1, r, c))

    def go_down(p):
        return raw(rail(p, d), rail(p, d - 1), first_down + p, first_up + p, (d - 1, r, c))

    def share(p):
        return raw(
            rail(p, d), n2.at[at(p ^ d, block), pl.ds(half, half)], first_shared + p, first_shared + p, sibling
        )

    def onward(p):
        @pl.when((p <= d) & (d < DP - 1))
        def _():
            go_up(p).start()

        @pl.when((p >= d) & (d > 0))
        def _():
            go_down(p).start()

        share(p).start()

    def project(p):
        share(p).wait_recv()
        part = at(p ^ d, block)
        gate[part, :] = jnp.dot(n2[part, :], wg[...], preferred_element_type=F32)

    def project_up(t):
        part = at(t, block)
        up[part, :] = jnp.dot(n2[part, :], wu[...], preferred_element_type=F32)

    def pass_up(n):
        @pl.when(core == 0)
        def _():
            for i in (2, 3):
                up_came(n, i).wait_recv()
                up_relay(n, i).start()

    def hidden_grads(first, fresh):
        def one(t):
            part = at(t, block)
            value = jnp.zeros((block, units), F32) if fresh else du[part, :]
            for i in (first, first + 1):
                place = PLACE[i]
                value = value + lax.dot_general(
                    gb[part, place * fc : (place + 1) * fc], wd[place], across, preferred_element_type=F32
                )
            du[part, :] = value

        loop(DP, one)

    onward(d)
    turns = [
        d,
        jnp.where(d == 0, 1, d - 1),
        jnp.where(d < 2, 2, jnp.where(d == 2, 3, 1)),
        jnp.where(d < 2, 3, 0),
    ]
    inner = (d == 1) | (d == 2)

    def arrival(n):
        raw(rail(turns[n], d), rail(turns[n], d), first_up, first_up + turns[n], me).wait_recv()
        onward(turns[n])

    for load in loads:
        load.wait()
    arrival(1)

    @pl.when(inner)
    def _():
        arrival(2)

    pass_up(0)
    project(turns[0])
    pass_up(1)
    project(turns[1])

    @pl.when(jnp.logical_not(inner))
    def _():
        arrival(2)

    @pl.when(inner)
    def _():
        arrival(3)

    pass_down(0)
    project(turns[2])

    @pl.when(core == 0)
    def _():
        keep_down.wait()
        for n in (0, 1):
            ship(n, 0, 1, me).wait_recv()

    @pl.when(core == 1)
    def _():
        for n in (0, 1):
            for i in (0, 1):
                ship(n, 0, i, me).wait_recv()

    @pl.when(jnp.logical_not(inner))
    def _():
        arrival(3)

    hidden_grads(0, True)
    pass_down(1)
    project(turns[3])
    outs = [pltpu.make_async_copy(n2, n2_out, local_sem.at[0])]
    outs[0].start()

    @pl.when(core == 1)
    def _():
        for n in (0, 1):
            for i in (2, 3):
                up_came(n, i).wait_recv()

    loop(DP, project_up)

    @pl.when(core == 1)
    def _():
        for n in (0, 1):
            for i in (2, 3):
                ship(n, 0, i, me).wait_recv()

    hidden_grads(2, False)

    def units_of(t):
        part = at(t, 64)
        g, u, grad = gate[part, :], up[part, :], du[part, :]
        sigmoid = 1.0 / (1.0 + jnp.exp(-g))
        silu = g * sigmoid
        hidden[part, :] = (silu * u).astype(BF)
        dgate[part, :] = (grad * u * sigmoid * (1.0 + g * (1.0 - sigmoid))).astype(BF)
        dup[part, :] = (grad * silu).astype(BF)

    loop(2 * rows // 64, units_of)
    for n, (src, dst) in enumerate(((dgate, dgate_out), (dup, dup_out))):
        outs.append(pltpu.make_async_copy(src, dst, local_sem.at[1 + n]))
        outs[-1].start()

    def back(part, cols):
        return lax.dot_general(
            dgate[part, :], wg[cols, :], across, preferred_element_type=F32
        ) + lax.dot_general(dup[part, :], wu[cols, :], across, preferred_element_type=F32)

    def down_part(i):
        def down_grad(t):
            place = PLACE[i]
            stage[0, i, at(t, TILE), :] = lax.dot_general(
                hidden[:, at(t, TILE)], gb[:, place * fc : (place + 1) * fc], over, preferred_element_type=F32
            ).astype(BF)

        loop(units // TILE, down_grad)

    owners = PlaneSum(raw, stage, got, comb, post.take(10), local_sem, 4, me)

    line = LineSum(raw, ((z, got_z),), post.take(8), me)

    def plane_of(t):
        return jnp.where(d < DP // 2, DP - 1 - t, t)

    def to_sibling(t):
        part = at(plane_of(t) ^ d, block)
        return raw(given.at[part, :], arrived.at[part, :], first_given + t, first_given + t, sibling)

    def give(t):
        part = at(plane_of(t) ^ d, block)
        given[part, :] = back(part, slice(half, None)).astype(BF)
        to_sibling(t).start()

    def keep(t):
        p = plane_of(t)
        part = at(p ^ d, block)
        value = back(part, slice(0, half))
        to_sibling(t).wait_recv()
        z[p] = (value + arrived[part, :].astype(F32)).astype(BF)

        if t < DP - 1:
            @pl.when(d == 0)
            def _():
                line.up(DP - 1 - t)

            @pl.when(d == DP - 1)
            def _():
                line.down(t)

    first_given = post.take(DP)
    give(0)
    give(1)
    down_part(2)
    down_part(3)
    owners.start_far()
    keep(0)
    give(2)
    keep(1)
    give(3)
    keep(2)
    down_part(0)
    down_part(1)
    owners.start_near()
    keep(3)
    owners.combine(lambda kind, j: wg.at[pl.ds(0, units), pl.ds(j * fc, fc)], 5)
    line.rest()

    def settle_rows(t):
        part = at(t, 64)
        total = line.total(z, got_z, part)
        gn[pl.ds(pl.multiple_of(y * block + t * 64, 64), 64), :] = total[:, 0:fc]
        crossing[part, :] = total[:, fc:].astype(BF)

    loop(block // 64, settle_rows)
    other = post.send(crossing, crossed, (d, r, c ^ 2))
    other.wait_recv()

    def other_rows(t):
        gn[pl.ds(pl.multiple_of((1 - y) * block + t * 64, 64), 64), :] = crossed[at(t, 64), :].astype(F32)

    loop(block // 64, other_rows)

    def inner_sum(t):
        part = at(t, 128)
        inner = gn[part, :] * gain_ref[...] * mid_ref[part, :]
        sums[0, :, part] = as_row(jnp.sum(inner, axis=1, keepdims=True))

    loop(rows // 128, inner_sum)
    small = [post.send(sums.at[0], sums.at[m], (d, r, c ^ m)) for m in (1, 2, 3)]

    def gain_sum(t, total):
        part = at(t, 128)
        value = gn[part, :] * mid_ref[part, :] * scale_ref[part, :]
        return total + jnp.sum(value, axis=0, keepdims=True)

    gain_out[...] = lax.fori_loop(0, rows // 128, gain_sum, jnp.zeros((1, fc), F32))
    for copy in small:
        copy.wait_recv()

    def finish(t):
        part = at(t, 128)
        inner = as_column(sums[0, :, part] + sums[2, :, part] + sums[1, :, part] + sums[3, :, part])
        scale = scale_ref[part, :]
        grad_out[part, :] = (
            own_grad[part, :].astype(F32) + scale * (gn[part, :] * gain_ref[...])
            - mid_ref[part, :] * (scale * scale * scale * inner / D)
        )

    loop(rows // 128, finish)

    owners.settle()
    line.settle()
    for copy in outs:
        copy.wait()
    for copy in [cross, other] + small:
        copy.wait_send()
    for t in range(DP):
        to_sibling(t).wait_send()
    for n in (0, 1):
        over_y(n).wait_send()
        over_x(n).wait_send()
        up_over_y(n).wait_send()

        @pl.when(core == 0)
        def _(n=n):
            for i in (2, 3):
                relay(n, i).wait_send()
                up_relay(n, i).wait_send()

        @pl.when(core == 1)
        def _(n=n):
            to_core(n).wait_send()

    for p in range(DP):
        share(p).wait_send()

        @pl.when((p <= d) & (d < DP - 1))
        def _(p=p):
            go_up(p).wait_send()

        @pl.when((p >= d) & (d > 0))
        def _(p=p):
            go_down(p).wait_send()


def middle(n2, mid, scale, gain, own_grad, down, own_up, gate, up, grad_all):
    rows, fc = n2.shape
    group = 2 * rows
    block = rows // 2
    units = down.shape[0]
    vmem = pl.BlockSpec(memory_space=pltpu.VMEM)
    hbm = pl.BlockSpec(memory_space=pl.ANY)

    def like(shape, dtype=BF):
        return jax.ShapeDtypeStruct(shape, dtype)

    return pl.pallas_call(
        middle_kernel,
        in_specs=[vmem] * 6 + [hbm] * 4,
        out_specs=[vmem] * 2 + [hbm] * 5,
        out_shape=[
            like((rows, fc), F32),
            like((1, fc), F32),
            like((1, 3, units, fc)),
            like((1, 2, units, fc)),
            like((group, D)),
            like((group, units)),
            like((group, units)),
        ],
        scratch_shapes=[
            pltpu.VMEM((group, D), BF),
            pltpu.VMEM((group, units), BF),
            pltpu.VMEM((group, units), BF),
            pltpu.VMEM((D, units), BF),
            pltpu.VMEM((D, units), BF),
            pltpu.VMEM((COL, units, fc), BF),
            pltpu.VMEM((group, D), BF),
            pltpu.VMEM((units, fc), BF),
            pltpu.VMEM((group, units), F32),
            pltpu.VMEM((group, units), F32),
            pltpu.VMEM((group, units), F32),
            pltpu.VMEM((group, units), BF),
            pltpu.VMEM((group, 2 * fc), BF),
            pltpu.VMEM((group, 2 * fc), BF),
            pltpu.VMEM((DP, block, 2 * fc), BF),
            pltpu.VMEM((DP + 1, block, 2 * fc), BF),
            pltpu.VMEM((block, fc), BF),
            pltpu.VMEM((block, fc), BF),
            pltpu.VMEM((rows, fc), F32),
            pltpu.VMEM((4, 8, rows), F32),
            pltpu.VMEM((1, COL, units, fc), BF),
            pltpu.SemaphoreType.DMA((SENDS,)),
            pltpu.SemaphoreType.DMA((SENDS,)),
            pltpu.SemaphoreType.DMA((12,)),
        ],
        compiler_params=pltpu.CompilerParams(
            collective_id=3, has_side_effects=True, vmem_limit_bytes=62 << 20
        ),
        cost_estimate=pl.CostEstimate(
            flops=14 * group * D * units, bytes_accessed=48 << 20, transcendentals=group * units
        ),
    )(n2, mid, scale, gain, own_grad, down, own_up, gate, up, grad_all)


POSTS = 112


def backward_kernel(
    x_ref, gain_ref, scale_ref, mid_ref, gain_two_ref, begin_ref, weight_in_hbm, weight_out_hbm, q_hbm, kv_hbm,
    att_hbm, lse_hbm, normed_hbm, n2_hbm, dgate_hbm, dup_hbm,
    tokens_out, query_out, key_out, value_out, out_out, gains_out, got, comb,
    weight_in, weight_out, q_ref, kv_ref, att_ref, lse_ref, n1, n2, dgu, dball, dotted, dproj, acc, spill, spilled, stage, own_f, arrived, landed,
    zq, zo, zkv, rq, ro, rkv, sums, gsum,
    send_sem, recv_sem, local_sem,
):
    d, r, c = (lax.axis_index(name) for name in AXES)
    y, core = c // 2, lax.rem(c, 2)
    rows, fc = x_ref.shape
    group = 2 * rows
    width = q_hbm.shape[1]
    units = dgate_hbm.shape[1]
    half = 2 * fc
    tiles = group // TILE
    over = (((0,), (0,)), ((), ()))
    across = (((1,), (1,)), ((), ()))
    post = Post(send_sem, recv_sem)
    loads = [
        pltpu.make_async_copy(src, dst, local_sem.at[8 + n])
        for n, (src, dst) in enumerate((
            (n2_hbm, n2),
            (dgate_hbm, dgu.at[pl.ds(0, group), :]),
            (dup_hbm, dgu.at[pl.ds(group, group), :]),
            (normed_hbm, n1),
            (weight_out_hbm, weight_out),
            (att_hbm, att_ref),
            (q_hbm, q_ref),
            (kv_hbm, kv_ref),
            (lse_hbm, lse_ref),
            (weight_in_hbm, weight_in),
        ))
    ]
    for load in loads:
        load.start()

    others = [(a, b) for a in (0, 1) for b in range(COL) if (a, b) != (0, 0)]
    greet(
        [(d, r ^ a, c ^ b) for a, b in others]
        + [(d ^ j, r ^ a, c) for j in (1, 2, 3) for a in (0, 1)]
    )

    def columns(place):
        return pl.ds(place * fc, fc)

    def turned(t):
        return lax.rem(t + 2 * r, tiles)

    raw = maker(send_sem, recv_sem)
    me = (d, r, c)
    sibling = (d, r, c ^ 1)
    own_rows, other_rows = pl.ds(0, rows), pl.ds(rows, rows)
    def round_mid(t):
        dball[at(t, 128), 0:fc] = mid_ref[at(t, 128), :].astype(BF)

    loop(rows // 128, round_mid)
    own_block = dball.at[own_rows, columns(0)]
    beside = post.send(own_block, dball.at[other_rows, columns(0)], (d, r ^ 1, c))
    beyond = post.send(own_block, dball.at[own_rows, columns(1)], (d, r, c ^ 2))
    shared = [post.send(own_block, dball.at[own_rows, columns(2)], sibling)]

    for load in loads[:3]:
        load.wait()
    owners = PlaneSum(raw, stage, got, comb, post.take(20), local_sem, 4, me)

    def hidden_part(i):
        for kind in (0, 1):
            def hidden_grad(t, kind=kind):
                left = n2[:, pl.ds(pl.multiple_of(PLACE[i] * fc + t * TILE, TILE), TILE)]
                stage[kind, i, at(t, TILE), :] = lax.dot_general(
                    left, dgu[pl.ds(kind * group, group), :], over, preferred_element_type=F32
                ).astype(BF)

            loop(fc // TILE, hidden_grad)

    hidden_part(2)
    hidden_part(3)
    for load in loads[3:]:
        load.wait()

    upper = pl.ds(rows, rows // 2)
    beside.wait_recv()
    corner = [post.send(dball.at[upper, columns(0)], dball.at[upper, columns(1)], (d, r, c ^ 2))]
    shared.append(post.send(dball.at[other_rows, columns(0)], dball.at[other_rows, columns(2)], sibling))
    beyond.wait_recv()
    corner.append(post.send(
        dball.at[pl.ds(rows // 2, rows // 2), columns(1)],
        dball.at[pl.ds(rows + rows // 2, rows // 2), columns(1)], (d, r ^ 1, c),
    ))
    shared.append(post.send(dball.at[own_rows, columns(1)], dball.at[own_rows, columns(3)], sibling))
    owners.start_far()
    hidden_part(0)
    hidden_part(1)
    for copy in corner:
        copy.wait_recv()
    shared.append(post.send(dball.at[other_rows, columns(1)], dball.at[other_rows, columns(3)], sibling))
    for copy in shared:
        copy.wait_recv()

    def head_grad(t):
        dotted[at(turned(t), TILE), :] = lax.dot_general(
            dball[at(t, TILE), :], weight_out[...], across, preferred_element_type=F32
        ).astype(BF)

    loop(tiles, head_grad)

    sent_out = [None] + [post.take(1) for _ in (1, 2, 3)]
    outs = []
    for place, m in enumerate((0, 2, 1, 3)):
        value = lax.dot_general(
            att_ref[...], dball[:, place * fc : (place + 1) * fc], over, preferred_element_type=F32
        ).astype(BF)
        if m == 0:
            zo[c] = value
        else:
            n2[(m - 1) * width : m * width, half : half + fc] = value
            staged = n2.at[pl.ds((m - 1) * width, width), pl.ds(half, fc)]
            copy = raw(staged, zo.at[c], sent_out[m], sent_out[m], (d, r, c ^ m))
            copy.start()
            outs.append(copy)

    span = TILE + REACH
    scale = HEAD_DIM ** (-0.5)
    spills = []
    for h in range(width // HEAD_DIM):
        lanes = pl.ds(h * HEAD_DIM, HEAD_DIM)
        value_lanes = pl.ds(width + h * HEAD_DIM, HEAD_DIM)

        def clear(t, lanes=lanes, value_lanes=value_lanes):
            acc[at(t, TILE), lanes] = jnp.zeros((TILE, HEAD_DIM), F32)
            acc[at(t, TILE), value_lanes] = jnp.zeros((TILE, HEAD_DIM), F32)

        loop((group + REACH) // TILE, clear)

        def one(t, lanes=lanes, value_lanes=value_lanes):
            part = at(t, TILE)
            window = pl.ds(pl.multiple_of(t * TILE, TILE), span)
            query, key = q_ref[part, lanes], kv_ref[window, lanes]
            grad = dotted[part, lanes]
            scores = scores_of(query, key)
            query_at = lax.broadcasted_iota(jnp.int32, (TILE, span), 0)
            key_at = lax.broadcasted_iota(jnp.int32, (TILE, span), 1)
            begin = begin_ref[part, 0:1] + (REACH - t * TILE)
            allowed = (key_at <= query_at + REACH) & (key_at >= begin)
            scores = jnp.where(allowed, scores - lse_ref[part, lanes][:, 0:1], NEG_FILL)
            probability = jnp.exp(scores)
            grad_soft = lax.dot_general(grad, kv_ref[window, value_lanes], across, preferred_element_type=F32)
            inner = jnp.sum(probability * grad_soft, axis=1, keepdims=True)
            grad_scores = (probability * (grad_soft - inner)).astype(BF)
            dproj[at(turned(t), TILE), lanes] = (
                jnp.dot(grad_scores, key, preferred_element_type=F32) * scale
            ).astype(BF)
            acc[window, lanes] += lax.dot_general(grad_scores, query, over, preferred_element_type=F32) * scale
            acc[window, value_lanes] += lax.dot_general(
                probability.astype(BF), grad, over, preferred_element_type=F32
            )

        loop(tiles, one)

        def round_spill(t, h=h, lanes=lanes, value_lanes=value_lanes):
            spill[h, at(t, TILE), 0:HEAD_DIM] = acc[at(t, TILE), lanes].astype(BF)
            spill[h, at(t, TILE), HEAD_DIM:] = acc[at(t, TILE), value_lanes].astype(BF)

        loop(REACH // TILE, round_spill)
        copy = post.ready(spill.at[h], spilled.at[h], (lax.rem(d + DP - 1, DP), r, c))
        spills.append(copy)

        @pl.when(d > 0)
        def _(copy=copy):
            copy.start()

    def attention_grads(first_lane, lane_count, dest):
        lanes = slice(first_lane, first_lane + lane_count)
        slots = [None] + [post.take(1) for _ in (1, 2, 3)]
        copies = []
        for place, m in enumerate((0, 2, 1, 3)):
            def tile(t, place=place, m=m):
                left = n1[:, pl.ds(pl.multiple_of(place * fc + t * TILE, TILE), TILE)]
                value = lax.dot_general(left, dproj[:, lanes], over, preferred_element_type=F32).astype(BF)
                if m == 0:
                    dest[c, at(t, TILE), :] = value
                else:
                    dgu[pl.ds(pl.multiple_of(place * fc + t * TILE, TILE), TILE), lanes] = value

            loop(fc // TILE, tile)
            if m:
                copy = raw(
                    dgu.at[pl.ds(place * fc, fc), pl.ds(first_lane, lane_count)], dest.at[c],
                    slots[m], slots[m], (d, r, c ^ m),
                )
                copy.start()
                copies.append(copy)
        return copies

    qs = attention_grads(0, width, zq)

    @pl.when(d < DP - 1)
    def _():
        for copy in spills:
            copy.wait_recv()

    @pl.when(d == DP - 1)
    def _():
        spilled[...] = jnp.zeros_like(spilled)

    for h in range(width // HEAD_DIM):
        for which in (0, 1):
            lanes = pl.ds(which * width + h * HEAD_DIM, HEAD_DIM)
            out_lanes = pl.ds((1 + which) * width + h * HEAD_DIM, HEAD_DIM)

            def whole(t, h=h, which=which, lanes=lanes, out_lanes=out_lanes):
                total = acc[pl.ds(pl.multiple_of(REACH + t * TILE, TILE), TILE), lanes]
                extra = spilled[
                    h, at(jnp.maximum(t - 1, 0), TILE), which * HEAD_DIM : (which + 1) * HEAD_DIM
                ].astype(F32)
                total = total + jnp.where(t > 0, extra, 0.0)
                dproj[at(turned(t), TILE), out_lanes] = total.astype(BF)

            loop(tiles, whole)

    kvs = attention_grads(width, 2 * width, zkv)
    for copy in outs + qs:
        copy.wait_recv()
    first_line = post.take(24)
    line_a = LineSum(raw, ((zq, rq), (zo, ro)), first_line, me)
    line_b = LineSum(raw, ((zkv, rkv),), first_line + 16, me)
    line_a.begin()

    def given_part(t):
        n2[at(t, TILE), 0:half] = lax.dot_general(
            dproj[at(t, TILE), :], weight_in[half:, :], across, preferred_element_type=F32
        ).astype(BF)

    loop(tiles, given_part)
    to_sibling = post.send(n2.at[:, pl.ds(0, half)], arrived, sibling)

    to_sibling.wait_recv()
    for copy in outs:
        copy.wait_send()

    def kept_part(t):
        part = at(t, TILE)
        value = lax.dot_general(
            dproj[part, :], weight_in[:half, :], across, preferred_element_type=F32
        ) + arrived[part, :].astype(F32)
        n2[part, half:] = value.astype(BF)

        @pl.when(t < rows // TILE)
        def _():
            own_f[part, :] = value[:, 0:fc]

    loop(tiles, kept_part)

    def low(where, place):
        return n2.at[where, pl.ds(half + place * fc, fc)]

    pieces = [
        post.send(low(other_rows, 1), landed.at[2], (d, r ^ 1, c ^ 2)),
        post.send(low(other_rows, 0), landed.at[0], (d, r ^ 1, c)),
        post.send(low(own_rows, 1), landed.at[1], (d, r, c ^ 2)),
    ]

    def finish(line, z, got_z, dests):
        def one(t):
            value = line.total(z, got_z, at(t, 64))
            for dest, lanes in dests:
                dest[at(t, 64), :] = value[:, lanes]

        loop(z.shape[1] // 64, one)

    owners.start_near()
    line_a.rest()
    for copy in kvs:
        copy.wait_recv()
    line_b.begin()

    for copy in pieces:
        copy.wait_recv()

    def inner_sum(t):
        part = at(t, 128)
        value = own_f[part, :]
        for n in range(3):
            value = value + landed[n, part, :].astype(F32)
        own_f[part, :] = value
        inner = value * gain_ref[...] * x_ref[part, :].astype(F32)
        sums[0, :, part] = as_row(jnp.sum(inner, axis=1, keepdims=True))

    loop(rows // 128, inner_sum)
    small = [post.send(sums.at[0], sums.at[m], (d, r, c ^ m)) for m in (1, 2, 3)]
    seat = ROW * d + r
    gain_part = jnp.zeros((1, fc), F32)

    def gain_sum(t, total):
        part = at(t, 128)
        value = own_f[part, :] * x_ref[part, :].astype(F32) * scale_ref[part, :]
        return total + jnp.sum(value, axis=0, keepdims=True)

    gain_part = lax.fori_loop(0, rows // 128, gain_sum, gain_part)
    gsum[seat, 0:1, :] = gain_part
    gsum[seat, 1:2, :] = gain_two_ref[...]
    gsum[seat, 2:8, :] = jnp.zeros((6, fc), F32)
    gain_sent = post.take(8)
    gain_got = gain_sent

    def gain_copy(n, j, a):
        return raw(gsum.at[seat], gsum.at[seat], gain_sent + n, gain_got + seat, (d ^ j, r ^ a, c))

    far = [(j, a) for j in range(DP) for a in (0, 1) if (j, a) != (0, 0)]
    for n, (j, a) in enumerate(far):
        gain_copy(n, j, a).start()
    owners.combine(lambda kind, j: n1.at[pl.ds(j * fc, fc), pl.ds(kind * units, units)], 0)


    line_b.rest()
    finish(line_a, zq, rq, ((query_out, slice(None)),))
    finish(line_a, zo, ro, ((out_out, slice(None)),))
    finish(line_b, zkv, rkv, ((key_out, slice(0, width)), (value_out, slice(width, None))))
    for copy in small:
        copy.wait_recv()

    def finish_tokens(t):
        part = at(t, 128)
        inner = as_column(sums[0, :, part] + sums[2, :, part] + sums[1, :, part] + sums[3, :, part])
        scale_rows = scale_ref[part, :]
        value = x_ref[part, :].astype(F32)
        tokens_out[part, :] = (
            mid_ref[part, :] + scale_rows * (own_f[part, :] * gain_ref[...])
            - value * (scale_rows * scale_rows * scale_rows * inner / D)
        )

    loop(rows // 128, finish_tokens)

    for e in range(2 * DP):
        @pl.when(e != seat)
        def _(e=e):
            raw(gsum.at[e], gsum.at[e], gain_sent, gain_got + e, me).wait_recv()

    gains = gsum[0]
    for e in range(1, 2 * DP):
        gains = gains + gsum[e]
    gains_out[...] = gains

    owners.settle()
    line_a.settle()
    line_b.settle()
    for copy in [beside, beyond] + corner + shared + qs + kvs + [to_sibling] + pieces + small:
        copy.wait_send()
    for n, (j, a) in enumerate(far):
        gain_copy(n, j, a).wait_send()

    @pl.when(d > 0)
    def _():
        for copy in spills:
            copy.wait_send()


def backward(x, gain, scale, mid, gain_two, weight_in, weight_out, q, kv, att, lse, begin, normed, n2, dgate, dup):
    rows, fc = x.shape
    group = 2 * rows
    width = q.shape[1]
    units = dgate.shape[1]
    vmem = pl.BlockSpec(memory_space=pltpu.VMEM)
    hbm = pl.BlockSpec(memory_space=pl.ANY)

    def like(shape, dtype=BF):
        return jax.ShapeDtypeStruct(shape, dtype)

    return pl.pallas_call(
        backward_kernel,
        in_specs=[vmem] * 6 + [hbm] * 10,
        out_specs=[vmem] * 6 + [hbm] * 2,
        out_shape=[
            like((rows, fc), F32),
            like((fc, width), F32),
            like((fc, width), F32),
            like((fc, width), F32),
            like((width, fc), F32),
            like((8, fc), F32),
            like((2, 3, fc, units)),
            like((2, 2, fc, units)),
        ],
        scratch_shapes=[
            pltpu.VMEM((D, 3 * width), BF),
            pltpu.VMEM((width, D), BF),
            pltpu.VMEM((group, width), BF),
            pltpu.VMEM((REACH + group, 2 * width), BF),
            pltpu.VMEM((group, width), BF),
            pltpu.VMEM((group, width), F32),
            pltpu.VMEM((group, D), BF),
            pltpu.VMEM((group, D), BF),
            pltpu.VMEM((2 * group, units), BF),
            pltpu.VMEM((group, D), BF),
            pltpu.VMEM((group, width), BF),
            pltpu.VMEM((group, 3 * width), BF),
            pltpu.VMEM((group + REACH, 2 * width), F32),
            pltpu.VMEM((width // HEAD_DIM, REACH, 2 * HEAD_DIM), BF),
            pltpu.VMEM((width // HEAD_DIM, REACH, 2 * HEAD_DIM), BF),
            pltpu.VMEM((2, COL, fc, units), BF),
            pltpu.VMEM((rows, fc), F32),
            pltpu.VMEM((group, 2 * fc), BF),
            pltpu.VMEM((3, rows, fc), BF),
            pltpu.VMEM((DP, fc, width), BF),
            pltpu.VMEM((DP, width, fc), BF),
            pltpu.VMEM((DP, fc, 2 * width), BF),
            pltpu.VMEM((DP + 1, fc, width), BF),
            pltpu.VMEM((DP + 1, width, fc), BF),
            pltpu.VMEM((DP + 1, fc, 2 * width), BF),
            pltpu.VMEM((4, 8, rows), F32),
            pltpu.VMEM((2 * DP, 8, fc), F32),
            pltpu.SemaphoreType.DMA((POSTS,)),
            pltpu.SemaphoreType.DMA((POSTS,)),
            pltpu.SemaphoreType.DMA((20,)),
        ],
        compiler_params=pltpu.CompilerParams(
            collective_id=2, has_side_effects=True, vmem_limit_bytes=62 << 20
        ),
        cost_estimate=pl.CostEstimate(
            flops=12 * group * D * width + 4 * group * D * units, bytes_accessed=64 << 20, transcendentals=0
        ),
    )(x, gain, scale, mid, gain_two, begin, weight_in, weight_out, q, kv, att, lse, normed, n2, dgate, dup)


def closing_kernel(
    tokens, query, key, value, out, hidden, down,
    tokens_out, query_out, key_out, value_out, out_out, gate_out, up_out, down_out,
):
    for src, dst in (
        (tokens, tokens_out), (query, query_out), (key, key_out), (value, value_out), (out, out_out)
    ):
        dst[...] = src[...]
    for dst, kind in ((gate_out, 0), (up_out, 1)):
        dst[...] = hidden[kind, 0].astype(F32) + hidden[kind, 1].astype(F32) + hidden[kind, 2].astype(F32)
    down_out[...] = down[0, 0].astype(F32) + down[0, 1].astype(F32) + down[0, 2].astype(F32)


def closing(tokens, query, key, value, out, hidden, down):
    steps = 8

    def rows_of(array):
        rows, width = array.shape[-2:]
        lead = array.shape[:-2]
        return pl.BlockSpec(lead + (rows // steps, width), lambda t: (0,) * len(lead) + (t, 0))

    finals = [tokens, query, key, value, out] + [
        jax.ShapeDtypeStruct(a.shape[-2:], F32) for a in (hidden, hidden, down)
    ]
    return pl.pallas_call(
        closing_kernel,
        grid=(steps,),
        in_specs=[rows_of(a) for a in (tokens, query, key, value, out, hidden, down)],
        out_specs=[rows_of(a) for a in finals],
        out_shape=[jax.ShapeDtypeStruct(a.shape, F32) for a in finals],
        compiler_params=pltpu.CompilerParams(vmem_limit_bytes=62 << 20),
    )(tokens, query, key, value, out, hidden, down)


def on_small_mesh(
    tokens,
    cotangent,
    query_master,
    key_master,
    value_master,
    out_master,
    gate_master,
    up_master,
    down_master,
    attn_gain,
    ffn_gain,
    lengths,
    permutation,
):
    del permutation
    (
        mid, scale_two, n2, begin, scale_one, normed_one, weight_in, weight_out, q, key_value,
        own_attended, lse, own_up, weight_gate, weight_up, grad_all,
    ) = forward(
        tokens, attn_gain[None, :], ffn_gain[None, :], lengths, query_master, key_master,
        value_master, out_master, gate_master, up_master, cotangent,
    )
    grad_mid, gain_two_part, got_down, _, normed_two, grad_gate, grad_up = middle(
        n2, mid, scale_two, ffn_gain[None, :], cotangent, down_master, own_up, weight_gate,
        weight_up, grad_all,
    )
    grad_tokens, grad_query, grad_key, grad_value, grad_out, gains, got, _ = backward(
        tokens, attn_gain[None, :], scale_one, grad_mid, gain_two_part, weight_in, weight_out, q,
        key_value, own_attended, lse, begin, normed_one, normed_two, grad_gate, grad_up,
    )
    finals = closing(grad_tokens, grad_query, grad_key, grad_value, grad_out, got, got_down)
    return (*finals, gains[0], gains[1])


def solution(mesh):
    placed = (
        P(("dp", "row"), "col"),
        P(("dp", "row"), "col"),
        P("col", ("row", "dp")),
        P("col", ("row", "dp")),
        P("col", ("row", "dp")),
        P(("row", "dp"), "col"),
        P("col", ("row", "dp")),
        P("col", ("row", "dp")),
        P(("row", "dp"), "col"),
        P("col"),
        P("col"),
        P(),
        P(),
    )
    small = tuple(mesh.shape[name] for name in AXES) == (DP, ROW, COL)
    return jax.shard_map(
        on_small_mesh if small else on_any_mesh,
        mesh=mesh,
        in_specs=placed,
        out_specs=(
            P(("dp", "row"), "col"),
            P("col", ("row", "dp")),
            P("col", ("row", "dp")),
            P("col", ("row", "dp")),
            P(("row", "dp"), "col"),
            P("col", ("row", "dp")),
            P("col", ("row", "dp")),
            P(("row", "dp"), "col"),
            P("col"),
            P("col"),
        ),
        check_vma=False,
    )
```

```python
import functools

import jax
import jax.numpy as jnp
from jax import lax
from jax.experimental import pallas as pl
from jax.experimental.pallas import tpu as pltpu
from jax.sharding import PartitionSpec as P

D = 2048
HEAD_DIM = 128


EPSILON = 1e-06
NEG_FILL = -1e30
AXES = ("dp", "row", "col")
DP, ROW, COL = 4, 2, 4
REACH = 768
BF = jnp.bfloat16
F32 = jnp.float32


def running_sum(lengths):
    count = lengths.shape[0]
    earlier = jnp.arange(count)[:, None] <= jnp.arange(count)[None, :]
    return jnp.sum(jnp.where(earlier, lengths[:, None], 0), axis=0)

def make_picker(wanted, carried, pieces):
    amount = pieces[0].shape[0]
    inside = (wanted >= 0) & (wanted < amount)
    chosen = jnp.clip(wanted, 0, amount - 1)
    return tuple(
        (
            jnp.where(inside[:, None], jnp.take(shard_rows, chosen, axis=0), current)
            for shard_rows, current in zip(pieces, carried)
        )
    )


def sequence_marks(permutation, lengths, first_slot, amount):
    source = lax.dynamic_slice_in_dim(permutation, first_slot, amount)
    seq_ends = running_sum(lengths)
    passed = seq_ends[None, :] <= source[:, None]
    member = jnp.sum(passed.astype(jnp.int32), axis=1)
    begins = jnp.max(jnp.where(passed, seq_ends[None, :], 0), axis=1)
    return (member, source - begins)


def col_total(values):
    return lax.psum(jnp.sum(values, axis=1), "col")


def row_gather(values):
    return lax.all_gather(values, "row", axis=0, tiled=True)


def col_gather(values):
    return lax.all_gather(values, "col", axis=0, tiled=True)


def key_gather(keys_here, values_here):
    return (
        lax.all_gather(keys_here, "col", axis=0, tiled=True),
        lax.all_gather(values_here, "col", axis=0, tiled=True),
    )


def multiply(row_block, weight, transpose_right):
    if transpose_right:
        return lax.dot_general(
            row_block, weight, (((1,), (1,)), ((), ())), preferred_element_type=jnp.float32
        )
    return jnp.dot(row_block, weight, preferred_element_type=jnp.float32)


def outer_sum(left_rows, right_rows):
    return lax.dot_general(
        left_rows, right_rows, (((0,), (0,)), ((), ())), preferred_element_type=jnp.float32
    )


def col_reduce(spread, weight, transpose_right):
    return lax.psum_scatter(
        multiply(spread, weight, transpose_right), "col", scatter_dimension=0, tiled=True
    )


def row_reduce(spread, weight, transpose_right):
    return lax.psum_scatter(
        multiply(spread, weight, transpose_right), "row", scatter_dimension=0, tiled=True
    )


def visible(query_member, query_position, member, position):
    same = query_member[:, None] == member[None, :]
    behind = position[None, :] <= query_position[:, None]
    return same & behind


def attend_scores(query_block, key_all, allowed):
    scores = jnp.einsum(
        "qhd,khd->hqk", query_block, key_all, preferred_element_type=jnp.float32
    ) * HEAD_DIM ** (-0.5)
    return jnp.where(allowed[None, :, :], scores, NEG_FILL)


def norm_back(grad_normed, inputs_f, scale_rows, gain):
    gain_part = jnp.sum(grad_normed * inputs_f * scale_rows[:, None], axis=0)
    scaled = grad_normed * gain[None, :]
    inner = col_total(scaled * inputs_f)
    grad_inputs = scale_rows[:, None] * scaled - inputs_f * (scale_rows**3 * inner / D)[:, None]
    return (grad_inputs, gain_part)


def on_any_mesh(
    tokens,
    cotangent,
    query_master,
    key_master,
    value_master,
    out_master,
    gate_master,
    up_master,
    down_master,
    attn_gain,
    ffn_gain,
    lengths,
    permutation,
):
    own_rows = tokens.shape[0]
    group_rows = own_rows * lax.axis_size("row")
    quarter = group_rows // lax.axis_size("col")
    device_slot = lax.axis_index(("dp", "row"))
    group_slot = lax.axis_index("dp")
    col_slot = lax.axis_index("col")
    own_sources = lax.dynamic_slice_in_dim(permutation, device_slot * own_rows, own_rows)
    own_tokens, own_cotangent = make_picker(
        own_sources,
        (jnp.zeros_like(tokens), jnp.zeros_like(cotangent)),
        (
            lax.all_gather(tokens, ("dp", "row"), axis=0, tiled=True),
            lax.all_gather(cotangent, ("dp", "row"), axis=0, tiled=True),
        ),
    )
    masters = tuple(
        (
            matrix.astype(jnp.bfloat16)
            for matrix in (
                query_master,
                key_master,
                value_master,
                out_master,
                gate_master,
                up_master,
                down_master,
            )
        )
    )
    query_weight, key_weight, value_weight, out_weight, gate_weight, up_weight, down_weight = (
        lax.all_gather(masters[0], "dp", axis=1, tiled=True),
        lax.all_gather(masters[1], "dp", axis=1, tiled=True),
        lax.all_gather(masters[2], "dp", axis=1, tiled=True),
        lax.all_gather(masters[3], "dp", axis=0, tiled=True),
        lax.all_gather(masters[4], "dp", axis=1, tiled=True),
        lax.all_gather(masters[5], "dp", axis=1, tiled=True),
        lax.all_gather(masters[6], "dp", axis=0, tiled=True),
    )
    attention_in = jnp.concatenate([query_weight, key_weight, value_weight], axis=1)
    feedforward_in = jnp.concatenate([gate_weight, up_weight], axis=1)
    width_row = query_weight.shape[1]
    heads_row = width_row // HEAD_DIM
    hidden_row = gate_weight.shape[1]
    member, position = sequence_marks(permutation, lengths, group_slot * group_rows, group_rows)
    query_member = lax.dynamic_slice_in_dim(member, col_slot * quarter, quarter)
    query_position = lax.dynamic_slice_in_dim(position, col_slot * quarter, quarter)
    block_rows = min(512, quarter)
    block_count = quarter // block_rows
    residual_in = own_tokens.astype(jnp.float32)
    scale_one = lax.rsqrt(col_total(residual_in * residual_in) / D + EPSILON)
    normed_one = (residual_in * scale_one[:, None] * attn_gain[None, :]).astype(jnp.bfloat16)
    spread_one = row_gather(normed_one)
    projected = col_reduce(spread_one, attention_in, False).astype(jnp.bfloat16)
    queries = projected[:, :width_row].reshape(quarter, heads_row, HEAD_DIM)
    keys_here = projected[:, width_row : 2 * width_row]
    values_here = projected[:, 2 * width_row :]
    key_flat, value_flat = key_gather(keys_here, values_here)
    key_all = key_flat.reshape(group_rows, heads_row, HEAD_DIM)
    value_all = value_flat.reshape(group_rows, heads_row, HEAD_DIM)

    def block_mask(first_row):
        return visible(
            lax.dynamic_slice_in_dim(query_member, first_row, block_rows),
            lax.dynamic_slice_in_dim(query_position, first_row, block_rows),
            member,
            position,
        )

    def forward_block(block_id):
        first_row = block_id * block_rows
        query_block = lax.dynamic_slice_in_dim(queries, first_row, block_rows, 0)
        scores = attend_scores(query_block, key_all, block_mask(first_row))
        highest = jnp.max(scores, axis=2, keepdims=True)
        totals = jnp.sum(jnp.exp(scores - highest), axis=2, keepdims=True)
        log_total = highest + jnp.log(totals)
        probability = jnp.exp(scores - log_total)
        output = jnp.einsum(
            "hqk,khd->qhd",
            probability.astype(jnp.bfloat16),
            value_all,
            preferred_element_type=jnp.float32,
        )
        return (output.astype(jnp.bfloat16).reshape(block_rows, width_row), log_total[:, :, 0])

    blocks_out, log_totals = lax.map(forward_block, jnp.arange(block_count, dtype=jnp.int32))
    attended = blocks_out.reshape(quarter, width_row)
    spread_attn = col_gather(attended)
    midway = residual_in + row_reduce(spread_attn, out_weight, False)
    scale_two = lax.rsqrt(col_total(midway * midway) / D + EPSILON)
    normed_two = (midway * scale_two[:, None] * ffn_gain[None, :]).astype(jnp.bfloat16)
    spread_two = row_gather(normed_two)
    gate_and_up = col_reduce(spread_two, feedforward_in, False)
    gate_value = gate_and_up[:, :hidden_row]
    up_value = gate_and_up[:, hidden_row:]
    sigmoid_gate = jax.nn.sigmoid(gate_value)
    hidden = (gate_value * sigmoid_gate * up_value).astype(jnp.bfloat16)
    grad_output = own_cotangent.astype(jnp.float32)
    spread_down = row_gather(own_cotangent)
    grad_hidden = col_reduce(spread_down, down_weight, True)
    spread_hidden = col_gather(hidden)
    grad_down = outer_sum(spread_hidden, spread_down)
    grad_gate_value = (
        grad_hidden * up_value * sigmoid_gate * (1.0 + gate_value * (1.0 - sigmoid_gate))
    ).astype(jnp.bfloat16)
    grad_up_value = (grad_hidden * gate_value * sigmoid_gate).astype(jnp.bfloat16)
    spread_gate_up = col_gather(jnp.concatenate([grad_gate_value, grad_up_value], axis=1))
    grad_normed_two = row_reduce(spread_gate_up, feedforward_in, True)
    spread_two = row_gather(normed_two)
    grad_feedforward = outer_sum(spread_two, spread_gate_up)
    grad_mid_norm, gain_two_part = norm_back(grad_normed_two, midway, scale_two, ffn_gain)
    grad_midway = grad_output + grad_mid_norm
    rounded_midway = grad_midway.astype(jnp.bfloat16)
    spread_back = row_gather(rounded_midway)
    grad_attended = col_reduce(spread_back, out_weight, True).astype(jnp.bfloat16)
    spread_attn = col_gather(attended)
    key_flat, value_flat = key_gather(keys_here, values_here)
    key_all = key_flat.reshape(group_rows, heads_row, HEAD_DIM)
    value_all = value_flat.reshape(group_rows, heads_row, HEAD_DIM)
    grad_out_local = outer_sum(spread_attn, spread_back)

    def backward_block(carried, block_id):
        first_row = block_id * block_rows
        query_block = lax.dynamic_slice_in_dim(queries, first_row, block_rows, 0)
        scores = attend_scores(query_block, key_all, block_mask(first_row))
        probability = jnp.exp(
            scores - lax.dynamic_index_in_dim(log_totals, block_id, 0, keepdims=False)[:, :, None]
        )
        weights_low = probability.astype(jnp.bfloat16)
        grad_block = lax.dynamic_slice_in_dim(grad_attended, first_row, block_rows, 0).reshape(
            block_rows, heads_row, HEAD_DIM
        )
        grad_soft = jnp.einsum(
            "qhd,khd->hqk", grad_block, value_all, preferred_element_type=jnp.float32
        )
        row_inner = jnp.sum(probability * grad_soft, axis=2, keepdims=True)
        grad_scores = (probability * (grad_soft - row_inner)).astype(jnp.bfloat16)
        grad_query_block = jnp.einsum(
            "hqk,khd->qhd", grad_scores, key_all, preferred_element_type=jnp.float32
        ) * HEAD_DIM ** (-0.5)
        grad_key_all = carried[0] + jnp.einsum(
            "hqk,qhd->khd", grad_scores, query_block, preferred_element_type=jnp.float32
        ) * HEAD_DIM ** (-0.5)
        grad_value_all = carried[1] + jnp.einsum(
            "hqk,qhd->khd", weights_low, grad_block, preferred_element_type=jnp.float32
        )
        return (
            (grad_key_all, grad_value_all),
            grad_query_block.astype(jnp.bfloat16).reshape(block_rows, width_row),
        )

    start_grads = jnp.zeros((group_rows, heads_row, HEAD_DIM), jnp.float32)
    key_value_grads, grad_queries = lax.scan(
        backward_block, (start_grads, start_grads), jnp.arange(block_count, dtype=jnp.int32)
    )
    grad_queries = grad_queries.reshape(quarter, width_row)
    grad_key_part = key_value_grads[0].reshape(group_rows, width_row)
    grad_value_part = key_value_grads[1].reshape(group_rows, width_row)
    grad_key_mine, grad_value_mine = (
        lax.psum_scatter(grad_key_part, "col", scatter_dimension=0, tiled=True),
        lax.psum_scatter(grad_value_part, "col", scatter_dimension=0, tiled=True),
    )
    spread_projected = col_gather(
        jnp.concatenate(
            [
                grad_queries,
                grad_key_mine.astype(jnp.bfloat16),
                grad_value_mine.astype(jnp.bfloat16),
            ],
            axis=1,
        )
    )
    grad_normed_one = row_reduce(spread_projected, attention_in, True)
    spread_one = row_gather(normed_one)
    grad_attention = outer_sum(spread_one, spread_projected)
    grad_in_norm, gain_one_part = norm_back(grad_normed_one, residual_in, scale_one, attn_gain)
    grad_own_tokens = grad_midway + grad_in_norm
    grad_attn_gain, grad_ffn_gain = lax.psum((gain_one_part, gain_two_part), ("dp", "row"))
    grad_query, grad_key, grad_value, grad_out, grad_gate, grad_up, grad_down_mine = (
        lax.psum_scatter(
            grad_attention[:, :width_row].astype(jnp.bfloat16),
            "dp",
            scatter_dimension=1,
            tiled=True,
        ).astype(jnp.float32),
        lax.psum_scatter(
            grad_attention[:, width_row : 2 * width_row].astype(jnp.bfloat16),
            "dp",
            scatter_dimension=1,
            tiled=True,
        ).astype(jnp.float32),
        lax.psum_scatter(
            grad_attention[:, 2 * width_row :].astype(jnp.bfloat16),
            "dp",
            scatter_dimension=1,
            tiled=True,
        ).astype(jnp.float32),
        lax.psum_scatter(
            grad_out_local.astype(jnp.bfloat16), "dp", scatter_dimension=0, tiled=True
        ).astype(jnp.float32),
        lax.psum_scatter(
            grad_feedforward[:, :hidden_row].astype(jnp.bfloat16),
            "dp",
            scatter_dimension=1,
            tiled=True,
        ).astype(jnp.float32),
        lax.psum_scatter(
            grad_feedforward[:, hidden_row:].astype(jnp.bfloat16),
            "dp",
            scatter_dimension=1,
            tiled=True,
        ).astype(jnp.float32),
        lax.psum_scatter(
            grad_down.astype(jnp.bfloat16), "dp", scatter_dimension=0, tiled=True
        ).astype(jnp.float32),
    )
    total_tokens = permutation.shape[0]
    inverse = (
        jnp.zeros((total_tokens,), jnp.int32)
        .at[permutation]
        .set(jnp.arange(total_tokens, dtype=jnp.int32))
    )
    wanted_slots = lax.dynamic_slice_in_dim(inverse, device_slot * own_rows, own_rows)
    (grad_tokens,) = make_picker(
        wanted_slots,
        (jnp.zeros_like(grad_own_tokens),),
        (
            (
                lax.all_gather(
                    grad_own_tokens.astype(jnp.bfloat16), ("dp", "row"), axis=0, tiled=True
                ),
            )[0].astype(jnp.float32),
        ),
    )
    return (
        grad_tokens,
        grad_query,
        grad_key,
        grad_value,
        grad_out,
        grad_gate,
        grad_up,
        grad_down_mine,
        grad_attn_gain,
        grad_ffn_gain,
    )


def scores_of(query, key):
    return lax.dot_general(
        query, key, (((1,), (1,)), ((), ())), preferred_element_type=F32
    ) * HEAD_DIM ** (-0.5)


MESH = pl.DeviceIdType.MESH
PLACE = {0: 0, 2: 1, 1: 2, 3: 3}
TILE = 256


class Post:
    def __init__(self, send_sem, recv_sem):
        self.send_sem, self.recv_sem, self.used = send_sem, recv_sem, 0

    def ready(self, src, dst, target, slot=None):
        if slot is None:
            slot = self.used
            self.used += 1
        return pltpu.make_async_remote_copy(
            src_ref=src,
            dst_ref=dst,
            send_sem=self.send_sem.at[slot],
            recv_sem=self.recv_sem.at[slot],
            device_id=target,
            device_id_type=MESH,
        )

    def take(self, count):
        first = self.used
        self.used += count
        return first

    def send(self, src, dst, target):
        copy = self.ready(src, dst, target)
        copy.start()
        return copy


def greet(peers):
    barrier = pltpu.get_barrier_semaphore()
    for peer in peers:
        pl.semaphore_signal(barrier, inc=1, device_id=peer, device_id_type=MESH)
    pl.semaphore_wait(barrier, len(peers))


def as_row(column):
    return jnp.transpose(jnp.broadcast_to(column, (column.shape[0], 128)))[0:8]


def as_column(row):
    return jnp.transpose(row)[:, 0:1]


def scatter_plane(post, low, landed, rows, me):
    d, r, c = me
    half = rows // 2
    x_at, y_at = (d, r ^ 1, c), (d, r, c ^ 2)
    upper, lower = pl.ds(0, half), pl.ds(half, half)
    corner_x = post.send(low(rows, half, 1), landed.at[2, upper], x_at)
    corner_y = post.send(low(rows + half, half, 1), landed.at[2, lower], y_at)
    sent = [
        post.send(low(rows, half, 0), landed.at[0, upper], x_at),
        post.send(low(half, half, 1), landed.at[1, lower], y_at),
    ]

    def add(ref, first):
        def one(t, total):
            part = pl.ds(pl.multiple_of(t * 64, 64), 64)
            there = pl.ds(pl.multiple_of(first + t * 64, 64), 64)
            ref[part, :] = (ref[part, :].astype(F32) + landed[2, there, :].astype(F32)).astype(BF)
            return total

        lax.fori_loop(0, half // 64, one, 0)

    def pass_pieces():
        corner_x.wait_recv()
        add(low(0, half, 1), 0)
        later = [post.send(low(0, half, 1), landed.at[1, upper], y_at)]
        corner_y.wait_recv()
        add(low(rows + half, half, 0), half)
        later.append(post.send(low(rows + half, half, 0), landed.at[0, lower], x_at))
        return later

    return sent, [corner_x, corner_y], pass_pieces


def forward_kernel(
    x_ref, gain_one_ref, gain_two_ref, lengths_ref, query_ref, key_ref, value_ref, out_ref, gate_hbm, up_hbm,
    own_grad,
    mid_ref, scale_ref, n2_ref, begin_ref, first_scale,
    normed_out, weight_in_out, weight_out_out, q_out, kv_out, att_out, lse_out, own_up, gate_all, up_all, grad_all,
    normed_ref, weight_in, weight_out, q_ref, kv_ref, att_ref, lse_ref, masters,
    zin, zout, sums, wide, given, arrived, low, landed, x32, hidden_own,
    send_sem, recv_sem, local_sem,
):
    d, r, c = (lax.axis_index(name) for name in AXES)
    y, core = c // 2, lax.rem(c, 2)
    rows = x_ref.shape[0]
    fc = x_ref.shape[1]
    group = 2 * rows
    width = q_ref.shape[1]
    half = 2 * fc
    post = Post(send_sem, recv_sem)
    fetches = [
        pltpu.make_async_copy(src, masters.at[n], local_sem.at[8 + n]) for n, src in enumerate((gate_hbm, up_hbm))
    ]
    for copy in fetches:
        copy.start()
    copies = []

    def copy_out(src, dst):
        copy = pltpu.make_async_copy(src, dst, local_sem.at[10 + len(copies)])
        copy.start()
        copies.append(copy)

    in_plane = [(d, r ^ a, c ^ b) for a in (0, 1) for b in range(COL) if (a, b) != (0, 0)]
    greet([(d ^ j, r, c) for j in (1, 2, 3)] + in_plane)

    def fill_x(t, total):
        part = pl.ds(pl.multiple_of(t * 128, 128), 128)
        value = x_ref[part, :].astype(F32)
        x32[part, :] = value
        sums[0, :, part] = as_row(jnp.sum(value * value, axis=1, keepdims=True))
        return total

    lax.fori_loop(0, rows // 128, fill_x, 0)
    small = [post.send(sums.at[0], sums.at[m], (d, r, c ^ m)) for m in (1, 2, 3)]

    parts = (pl.ds(width, 2 * width), pl.ds(0, width))
    first, first_down = post.take(3 * DP), post.take(3 * DP)

    def block_of(n, p):
        return zin.at[p, :, parts[n]] if n < 2 else zout.at[p]

    def line(n, p, target_plane):
        block = block_of(n, p)
        return post.ready(block, block, (target_plane, r, c), first + DP * n + p)

    def line_down(n, p, target_plane):
        block = block_of(n, p)
        return pltpu.make_async_remote_copy(
            src_ref=block, dst_ref=block,
            send_sem=send_sem.at[first_down + DP * n + p], recv_sem=recv_sem.at[first + DP * n + p],
            device_id=(target_plane, r, c), device_id_type=MESH,
        )

    def cast_rows(src, dst, amount, step=64):
        def one(t, total):
            part = pl.ds(pl.multiple_of(t * step, step), step)
            dst(part, src[part, :].astype(BF))
            return total

        lax.fori_loop(0, amount // step, one, 0)

    for place, master in enumerate((query_ref, key_ref, value_ref)):
        def put(part, value, place=place):
            zin[d, part, place * width : (place + 1) * width] = value

        cast_rows(master, put, fc)
    def leave(n):
        @pl.when(d < DP - 1)
        def _():
            line(n, d, d + 1).start()

        @pl.when(d > 0)
        def _():
            line_down(n, d, d - 1).start()

    leave(0)
    leave(1)

    first_cols = post.take(3 * DP)

    def place_of(m):
        return lax.rem(m, 2) * 2 + m // 2

    def seat_of(n, place):
        there = pl.ds(pl.multiple_of(place * fc, fc), fc)
        return weight_in.at[there, parts[n]] if n < 2 else weight_out.at[:, there]

    def to_column(n, p):
        return pltpu.make_async_remote_copy(
            src_ref=block_of(n, p),
            dst_ref=seat_of(n, place_of(p ^ c)),
            send_sem=send_sem.at[first_cols + DP * n + p],
            recv_sem=recv_sem.at[first_cols + DP * n + (p ^ c)],
            device_id=(d, r, p), device_id_type=MESH,
        )

    def keep(n):
        return pltpu.make_async_copy(block_of(n, c), seat_of(n, 0), local_sem.at[(0, 1, 5)[n]])

    def pass_on(n, p):
        @pl.when(p == c)
        def _():
            keep(n).start()

        @pl.when(p != c)
        def _():
            to_column(n, p).start()

    hidden_all = (gate_all, up_all)
    first_sent = post.take(10)
    first_got = first_sent

    def slab(kind, i):
        return hidden_all[kind].at[pl.ds(pl.multiple_of(place_of(i) * fc, fc), fc), :]

    def ship(kind, way, i, target, src=None):
        return pltpu.make_async_remote_copy(
            src_ref=hidden_own.at[kind] if src is None else src,
            dst_ref=slab(kind, i),
            send_sem=send_sem.at[first_sent + 5 * kind + way],
            recv_sem=recv_sem.at[first_got + 4 * kind + i],
            device_id=target, device_id_type=MESH,
        )

    def keep_hidden(kind):
        return pltpu.make_async_copy(hidden_own.at[kind], slab(kind, 0), local_sem.at[3 + kind])

    def to_core(kind):
        return ship(kind, 0, 1, (d, r, c ^ 1))

    first_half = post.take(8)

    def gate_half(i, n):
        step = fc // 2
        return gate_all.at[pl.ds(pl.multiple_of(place_of(i) * fc + n * step, step), step), :]

    def over_y(n):
        return pltpu.make_async_remote_copy(
            src_ref=hidden_own.at[0, pl.ds(n * (fc // 2), fc // 2), :], dst_ref=gate_half(2 + core, n),
            send_sem=send_sem.at[first_half + 4 * n], recv_sem=recv_sem.at[first_half + 4 * n + core],
            device_id=(d, r, 2 * (1 - y)), device_id_type=MESH,
        )

    def over_x(kind):
        return ship(kind, 2, 1 - core, (d, r ^ 1, 2 * y + 1))

    def relay(n, i):
        return pltpu.make_async_remote_copy(
            src_ref=gate_half(i, n), dst_ref=gate_half(5 - i, n),
            send_sem=send_sem.at[first_half + 4 * n + i - 1],
            recv_sem=recv_sem.at[first_half + 4 * n + 3 - i],
            device_id=(d, r ^ 1, 2 * y + 1), device_id_type=MESH,
        )

    def gate_came(n, i):
        return pltpu.make_async_remote_copy(
            src_ref=gate_half(i, n), dst_ref=gate_half(i, n),
            send_sem=send_sem.at[first_half], recv_sem=recv_sem.at[first_half + 4 * n + i - 2],
            device_id=(d, r, c), device_id_type=MESH,
        )

    def start_home(kind):
        @pl.when(core == 0)
        def _():
            keep_hidden(kind).start()

        @pl.when(core == 1)
        def _():
            to_core(kind).start()

    def start_relay(n):
        @pl.when(core == 0)
        def _():
            for i in (2, 3):
                gate_came(n, i).wait_recv()
                relay(n, i).start()

    def cast_hidden(kind):
        def put(part, value):
            hidden_own[kind, part, :] = value

        fetches[kind].wait()
        cast_rows(masters.at[kind], put, fc)

    cast_hidden(0)
    over_x(0).start()
    over_y(0).start()
    for copy in small:
        copy.wait_recv()

    def norm_one(t, total):
        part = pl.ds(pl.multiple_of(t * 128, 128), 128)
        square = sums[0, :, part] + sums[2, :, part] + sums[1, :, part] + sums[3, :, part]
        scale = lax.rsqrt(as_column(square) / D + EPSILON)
        first_scale[part, :] = scale
        normed_ref[part, 0:fc] = (x32[part, :] * scale * gain_one_ref[...]).astype(BF)
        return total

    lax.fori_loop(0, rows // 128, norm_one, 0)
    own_rows, other_rows = pl.ds(0, rows), pl.ds(rows, rows)

    def columns(place):
        return pl.ds(place * fc, fc)

    own_block = normed_ref.at[own_rows, columns(0)]
    beside = post.send(own_block, normed_ref.at[other_rows, columns(0)], (d, r ^ 1, c))
    beyond = post.send(own_block, normed_ref.at[own_rows, columns(1)], (d, r, c ^ 2))
    corner = post.send(own_block, normed_ref.at[other_rows, columns(1)], (d, r ^ 1, c ^ 2))
    sibling = (d, r, c ^ 1)
    shared = [post.send(own_block, normed_ref.at[own_rows, columns(2)], sibling)]
    pass_on(0, d)
    pass_on(1, d)
    cast_hidden(1)
    start_home(0)
    start_home(1)
    copy_out(hidden_own.at[1], own_up)
    over_x(1).start()
    half_rows = rows // 2
    grad_cross = post.send(
        own_grad.at[pl.ds(pl.multiple_of((1 - y) * half_rows, half_rows), half_rows), :],
        grad_all.at[pl.ds(0, half_rows), pl.ds(fc, fc)],
        (d, r, c ^ 2),
    )
    grad_keep = pltpu.make_async_copy(
        own_grad.at[pl.ds(pl.multiple_of(y * half_rows, half_rows), half_rows), :],
        grad_all.at[pl.ds(0, half_rows), pl.ds(0, fc)],
        local_sem.at[2],
    )
    grad_keep.start()

    def put_out(part, value):
        zout[d, part, :] = value

    cast_rows(out_ref, put_out, width)

    def find_begins(t, total):
        part = pl.ds(pl.multiple_of(t * 128, 128), 128)
        place = lax.broadcasted_iota(jnp.int32, (128, 1), 0) + (d * group + t * 128)
        end = jnp.int32(0)
        begin = jnp.zeros((128, 1), jnp.int32)
        for n in range(lengths_ref.shape[0]):
            end = end + lengths_ref[n]
            begin = jnp.where(place >= end, end, begin)
        begin_ref[part, :] = begin - d * group
        return total

    lax.fori_loop(0, group // 128, find_begins, 0)

    def line_step(s, which=(0, 1)):
        for n in which:
            for p, valid, onward, forward in (
                (d - s, d - s >= 0, d < DP - 1, lambda n, p: line(n, p, d + 1)),
                (d + s, d + s < DP, d > 0, lambda n, p: line_down(n, p, d - 1)),
            ):
                @pl.when(valid)
                def _(n=n, p=p, onward=onward, forward=forward):
                    line(n, p, d).wait_recv()

                    @pl.when(onward)
                    def _():
                        forward(n, p).start()

                    pass_on(n, p)

    line_step(1)
    leave(2)
    line_step(2)
    pass_on(2, d)
    line_step(1, (2,))
    for copy, where, place in ((beside, other_rows, 0), (beyond, own_rows, 1), (corner, other_rows, 1)):
        copy.wait_recv()
        shared.append(
            post.send(normed_ref.at[where, columns(place)], normed_ref.at[where, columns(place + 2)], sibling)
        )
    line_step(3)
    line_step(2, (2,))
    start_relay(0)

    def arrived_blocks(n):
        keep(n).wait()
        for m in (1, 2, 3):
            pltpu.make_async_remote_copy(
                src_ref=block_of(n, 0), dst_ref=seat_of(n, 0),
                send_sem=send_sem.at[first_cols], recv_sem=recv_sem.at[first_cols + DP * n + m],
                device_id=(d, r, c), device_id_type=MESH,
            ).wait_recv()

    for copy in shared:
        copy.wait_recv()
    arrived_blocks(0)
    over_y(1).start()
    copy_out(normed_ref, normed_out)

    def turned(t):
        return lax.rem(t + 2 * r, group // TILE)

    def project_kv(t, total):
        part = pl.ds(pl.multiple_of(t * TILE, TILE), TILE)
        to = pl.ds(pl.multiple_of(REACH + turned(t) * TILE, TILE), TILE)
        kv_ref[to, :] = jnp.dot(
            normed_ref[part, :], weight_in[:, width:], preferred_element_type=F32
        ).astype(BF)
        return total

    lax.fori_loop(0, group // TILE, project_kv, 0)
    halo = post.ready(kv_ref.at[pl.ds(group, REACH), :], kv_ref.at[pl.ds(0, REACH), :], (lax.rem(d + 1, DP), r, c))

    @pl.when(d < DP - 1)
    def _():
        halo.start()

    arrived_blocks(1)

    def project_q(t, total):
        part = pl.ds(pl.multiple_of(t * TILE, TILE), TILE)
        to = pl.ds(pl.multiple_of(turned(t) * TILE, TILE), TILE)
        q_ref[to, :] = jnp.dot(
            normed_ref[part, :], weight_in[:, :width], preferred_element_type=F32
        ).astype(BF)
        return total

    lax.fori_loop(0, group // TILE, project_q, 0)

    copy_out(weight_in, weight_in_out)
    copy_out(q_ref, q_out)
    line_step(3, (2,))
    @pl.when(d == 0)
    def _():
        kv_ref[pl.ds(0, REACH), :] = jnp.zeros((REACH, 2 * width), BF)

    @pl.when(d > 0)
    def _():
        halo.wait_recv()

    copy_out(kv_ref, kv_out)

    grads = [
        post.ready(
            grad_all.at[pl.ds(0, half_rows), pl.ds(0, half)],
            grad_all.at[pl.ds(j * half_rows, half_rows), pl.ds(0, half)],
            (d ^ j, r, c),
        )
        for j in (1, 2, 3)
    ]
    grads_shared = [
        post.ready(
            grad_all.at[pl.ds(0, half_rows), pl.ds(0, half)],
            grad_all.at[pl.ds(0, half_rows), pl.ds(half, half)],
            sibling,
        )
    ]

    def spread_grads():
        grad_cross.wait_recv()
        grad_keep.wait()
        for copy in grads + grads_shared[:1]:
            copy.start()

    pl.when(d > 0)(spread_grads)

    span = TILE + REACH
    for h in range(width // HEAD_DIM):
        lanes = pl.ds(h * HEAD_DIM, HEAD_DIM)
        value_lanes = pl.ds(width + h * HEAD_DIM, HEAD_DIM)

        def one(t, total, lanes=lanes, value_lanes=value_lanes):
            part = pl.ds(pl.multiple_of(t * TILE, TILE), TILE)
            to = pl.ds(pl.multiple_of(turned(t) * TILE, TILE), TILE)
            window = pl.ds(pl.multiple_of(t * TILE, TILE), span)
            scores = scores_of(q_ref[part, lanes], kv_ref[window, lanes])
            query = lax.broadcasted_iota(jnp.int32, (TILE, span), 0)
            key = lax.broadcasted_iota(jnp.int32, (TILE, span), 1)
            begin = begin_ref[part, 0:1] + (REACH - t * TILE)
            allowed = (key <= query + REACH) & (key >= begin)
            scores = jnp.where(allowed, scores, NEG_FILL)
            highest = jnp.max(scores, axis=1, keepdims=True)
            expo = jnp.exp(scores - highest)
            total_e = jnp.sum(expo, axis=1, keepdims=True)
            probability = (expo * (1.0 / total_e)).astype(BF)
            att_ref[to, lanes] = jnp.dot(
                probability, kv_ref[window, value_lanes], preferred_element_type=F32
            ).astype(BF)
            lse_ref[part, lanes] = jnp.broadcast_to(highest + jnp.log(total_e), (TILE, HEAD_DIM))
            return total

        lax.fori_loop(0, group // TILE, one, 0)

    pl.when(d == 0)(spread_grads)

    copy_out(att_ref, att_out)
    copy_out(lse_ref, lse_out)
    arrived_blocks(2)
    copy_out(weight_out, weight_out_out)

    def out_given(t, total):
        part = pl.ds(pl.multiple_of(t * TILE, TILE), TILE)
        given[part, :] = jnp.dot(
            att_ref[part, :], weight_out[:, half:], preferred_element_type=F32
        ).astype(BF)
        return total

    lax.fori_loop(0, group // TILE, out_given, 0)
    to_sibling = post.send(given, arrived, sibling)

    def out_kept(t, total):
        part = pl.ds(pl.multiple_of(t * TILE, TILE), TILE)
        wide[part, :] = jnp.dot(att_ref[part, :], weight_out[:, :half], preferred_element_type=F32)
        return total

    lax.fori_loop(0, group // TILE, out_kept, 0)
    to_sibling.wait_recv()

    def add_low(t, total):
        part = pl.ds(pl.multiple_of(t * 128, 128), 128)
        value = wide[part, :] + arrived[part, :].astype(F32)
        wide[part, :] = value
        low[part, :] = value.astype(BF)
        return total

    lax.fori_loop(0, group // 128, add_low, 0)
    pieces, corners, pass_pieces = scatter_plane(
        post, lambda first, count, place: low.at[pl.ds(first, count), columns(place)], landed, rows, (d, r, c)
    )
    pieces = pieces + pass_pieces()
    start_relay(1)
    for copy in pieces:
        copy.wait_recv()

    def middle(t, total):
        part = pl.ds(pl.multiple_of(t * 128, 128), 128)
        value = (
            x32[part, :] + wide[part, 0:fc] + landed[0, part, :].astype(F32)
            + landed[1, part, :].astype(F32)
        )
        mid_ref[part, :] = value
        sums[4, :, part] = as_row(jnp.sum(value * value, axis=1, keepdims=True))
        return total

    lax.fori_loop(0, rows // 128, middle, 0)
    again = [post.send(sums.at[4], sums.at[4 + m], (d, r, c ^ m)) for m in (1, 2, 3)]
    for copy in again:
        copy.wait_recv()

    def norm_two(t, total):
        part = pl.ds(pl.multiple_of(t * 128, 128), 128)
        square = sums[4, :, part] + sums[6, :, part] + sums[5, :, part] + sums[7, :, part]
        scale = lax.rsqrt(as_column(square) / D + EPSILON)
        scale_ref[part, :] = scale
        n2_ref[part, :] = (mid_ref[part, :] * scale * gain_two_ref[...]).astype(BF)
        return total

    lax.fori_loop(0, rows // 128, norm_two, 0)

    for j, copy in zip((1, 2, 3), grads):
        copy.wait_recv()
        there = pl.ds(j * half_rows, half_rows)
        grads_shared.append(
            post.send(grad_all.at[there, pl.ds(0, half)], grad_all.at[there, pl.ds(half, half)], sibling)
        )
    for copy in grads_shared:
        copy.wait_recv()
    for n in (0, 1):
        over_y(n).wait_send()

        @pl.when(core == 0)
        def _(n=n):
            for i in (2, 3):
                relay(n, i).wait_send()

        @pl.when(core == 1)
        def _(n=n):
            for i in (2, 3):
                gate_came(n, i).wait_recv()

    for kind in (0, 1):
        over_x(kind).wait_send()

        @pl.when(core == 0)
        def _(kind=kind):
            keep_hidden(kind).wait()
            ship(kind, 0, 1, (d, r, c)).wait_recv()

        @pl.when(core == 1)
        def _(kind=kind):
            to_core(kind).wait_send()
            for i in (0, 1):
                ship(kind, 0, i, (d, r, c)).wait_recv()

    for copy in (
        small + [grad_cross, beside, beyond, corner] + shared + grads + grads_shared
        + [to_sibling] + pieces + corners + again
    ):
        copy.wait_send()

    @pl.when(d < DP - 1)
    def _():
        halo.wait_send()

    for copy in copies:
        copy.wait()
    for n in (0, 1, 2):
        for p in range(DP):
            @pl.when((d < DP - 1) & (p <= d))
            def _(n=n, p=p):
                line(n, p, d).wait_send()

            @pl.when((d > 0) & (p >= d))
            def _(n=n, p=p):
                line_down(n, p, d).wait_send()

            @pl.when(c != p)
            def _(n=n, p=p):
                to_column(n, p).wait_send()


SENDS = 104


def forward(x, gain_one, gain_two, lengths, query, key, value, out, gate, up, own_grad):
    rows, fc = x.shape
    group = 2 * rows
    width = out.shape[0]
    units = gate.shape[1]
    vmem = pl.BlockSpec(memory_space=pltpu.VMEM)
    smem = pl.BlockSpec(memory_space=pltpu.SMEM)
    hbm = pl.BlockSpec(memory_space=pl.ANY)

    def like(shape, dtype=BF):
        return jax.ShapeDtypeStruct(shape, dtype)

    return pl.pallas_call(
        forward_kernel,
        in_specs=[vmem] * 3 + [smem] + [vmem] * 4 + [hbm] * 3,
        out_specs=[vmem] * 5 + [hbm] * 11,
        out_shape=[
            like((rows, fc), F32),
            like((rows, 1), F32),
            like((rows, fc)),
            like((group, 1), jnp.int32),
            like((rows, 1), F32),
            like((group, D)),
            like((D, 3 * width)),
            like((width, D)),
            like((group, width)),
            like((REACH + group, 2 * width)),
            like((group, width)),
            like((group, width), F32),
            like((fc, units)),
            like((D, units)),
            like((D, units)),
            like((group, D)),
        ],
        scratch_shapes=[
            pltpu.VMEM((group, D), BF),
            pltpu.VMEM((D, 3 * width), BF),
            pltpu.VMEM((width, D), BF),
            pltpu.VMEM((group, width), BF),
            pltpu.VMEM((REACH + group, 2 * width), BF),
            pltpu.VMEM((group, width), BF),
            pltpu.VMEM((group, width), F32),
            pltpu.VMEM((2, fc, units), F32),
            pltpu.VMEM((DP, fc, 3 * width), BF),
            pltpu.VMEM((DP, width, fc), BF),
            pltpu.VMEM((8, 8, rows), F32),
            pltpu.VMEM((group, 2 * fc), F32),
            pltpu.VMEM((group, 2 * fc), BF),
            pltpu.VMEM((group, 2 * fc), BF),
            pltpu.VMEM((group, 2 * fc), BF),
            pltpu.VMEM((3, rows, fc), BF),
            pltpu.VMEM((rows, fc), F32),
            pltpu.VMEM((2, fc, units), BF),
            pltpu.SemaphoreType.DMA((SENDS,)),
            pltpu.SemaphoreType.DMA((SENDS,)),
            pltpu.SemaphoreType.DMA((20,)),
        ],
        compiler_params=pltpu.CompilerParams(
            collective_id=1, has_side_effects=True, vmem_limit_bytes=60 << 20
        ),
        cost_estimate=pl.CostEstimate(
            flops=6 * group * D * width, bytes_accessed=64 << 20, transcendentals=0
        ),
    )(x, gain_one, gain_two, lengths, query, key, value, out, gate, up, own_grad)


def at(t, size):
    return pl.ds(pl.multiple_of(t * size, size), size)


def loop(count, body):
    def one(t, total):
        body(t)
        return total

    lax.fori_loop(0, count, one, 0)


def maker(send_sem, recv_sem):
    def raw(src, dst, sent, got_at, target):
        return pltpu.make_async_remote_copy(
            src_ref=src, dst_ref=dst, send_sem=send_sem.at[sent], recv_sem=recv_sem.at[got_at],
            device_id=target, device_id_type=MESH,
        )

    return raw


class LineSum:
    def __init__(self, raw, arrays, base, me):
        self.raw, self.arrays, self.base, self.me = raw, arrays, base, me

    def sem(self, n, p, down):
        return self.base + 8 * n + 4 * down + p

    def take(self, p, down, done):
        d = self.me[0]
        for n, (z, got_z) in enumerate(self.arrays):
            self.raw(z.at[p], got_z.at[p], self.sem(n, p, down), self.sem(n, p, down), self.me).wait_recv()

        @pl.when(jnp.logical_not(done))
        def _():
            for z, got_z in self.arrays:
                def one(t, z=z, got_z=got_z):
                    z[p, at(t, 64), :] = (
                        z[p, at(t, 64), :].astype(F32) + got_z[p, at(t, 64), :].astype(F32)
                    ).astype(BF)

                loop(z.shape[1] // 64, one)

    def up(self, p):
        d, r, c = self.me

        @pl.when((d > 0) & (d <= p))
        def _():
            self.take(p, 0, d == p)

        @pl.when(d < p)
        def _():
            for n, (z, got_z) in enumerate(self.arrays):
                self.raw(z.at[p], got_z.at[p], self.sem(n, p, 0), self.sem(n, p, 0), (d + 1, r, c)).start()

    def down(self, p):
        d, r, c = self.me

        @pl.when((d < DP - 1) & (d >= p))
        def _():
            self.take(p, 1, d == p)

        @pl.when(d > p)
        def _():
            slot = jnp.where(p < d - 1, p, DP)
            for n, (z, got_z) in enumerate(self.arrays):
                self.raw(z.at[p], got_z.at[slot], self.sem(n, p, 1), self.sem(n, p, 1), (d - 1, r, c)).start()

    def begin(self):
        d = self.me[0]

        @pl.when(d == 0)
        def _():
            for p in (3, 2, 1):
                self.up(p)

        @pl.when(d == DP - 1)
        def _():
            for p in (0, 1, 2):
                self.down(p)

    def first(self):
        d = self.me[0]

        @pl.when(d == 1)
        def _():
            self.up(3)
            self.up(2)

        @pl.when(d == 2)
        def _():
            self.down(0)
            self.down(1)

    def last(self):
        d = self.me[0]

        @pl.when(d == 0)
        def _():
            self.down(0)

        @pl.when(d == 1)
        def _():
            self.down(0)
            self.down(1)
            self.up(1)

        @pl.when(d == 2)
        def _():
            self.up(3)
            self.up(2)
            self.down(2)

        @pl.when(d == DP - 1)
        def _():
            self.up(3)

    def rest(self):
        self.first()
        self.last()

    def settle(self):
        d = self.me[0]
        for p in range(DP):
            for n, (z, got_z) in enumerate(self.arrays):
                for down, sent in ((0, d < p), (1, d > p)):
                    @pl.when(sent)
                    def _(p=p, n=n, z=z, got_z=got_z, down=down):
                        self.raw(
                            z.at[p], got_z.at[p], self.sem(n, p, down), self.sem(n, p, down), self.me
                        ).wait_send()

    def total(self, z, got_z, part):
        d = self.me[0]
        value = z[d, part, :].astype(F32)
        value = value + jnp.where(d > 0, got_z[d, part, :].astype(F32), 0.0)
        return value + jnp.where(d < DP - 1, got_z[DP, part, :].astype(F32), 0.0)


class PlaneSum:
    def __init__(self, raw, stage, got, comb, base, local_sem, local_base, me):
        self.raw, self.stage, self.got, self.comb, self.base = raw, stage, got, comb, base
        self.local_sem, self.local_base, self.me = local_sem, local_base, me
        self.kinds = range(stage.shape[0])

    def from_one(self, kind, i):
        d, r, c = self.me
        y = c // 2
        sent, base = self.base + 10 * kind + i, self.base + 10 * kind
        if i < 2:
            return self.raw(self.stage.at[kind, i], self.got.at[kind, 0], sent, base, (d, r ^ 1, 2 * y + 1 - i))
        return self.raw(
            self.stage.at[kind, i], self.comb.at[kind, 3 - i], sent, base + 3 + (3 - i), (d, r ^ 1, 2 * y)
        )

    def from_zero(self, kind, i):
        d, r, c = self.me
        sent, base = self.base + 10 * kind + i, self.base + 10 * kind
        if i == 1:
            return self.raw(self.stage.at[kind, i], self.got.at[kind, 1], sent, base + 1, (d, r, c ^ 1))
        return self.raw(
            self.stage.at[kind, i], self.got.at[kind, 2], sent, base + 2, (d, r, 2 * (1 - c // 2) + i - 2)
        )

    def home(self, kind):
        return pltpu.make_async_copy(
            self.stage.at[kind, 0], self.got.at[kind, 1], self.local_sem.at[self.local_base + kind]
        )

    def start_far(self):
        @pl.when(lax.rem(self.me[2], 2) == 1)
        def _():
            for i in (2, 3):
                for kind in self.kinds:
                    self.from_one(kind, i).start()

    def start_near(self):
        core = lax.rem(self.me[2], 2)

        @pl.when(core == 1)
        def _():
            for i in (0, 1):
                for kind in self.kinds:
                    self.from_one(kind, i).start()

        @pl.when(core == 0)
        def _():
            for kind in self.kinds:
                self.home(kind).start()
                self.from_zero(kind, 1).start()

    def combine(self, room, local_base):
        core = lax.rem(self.me[2], 2)

        @pl.when(core == 0)
        def _():
            for i in (2, 3):
                for kind in self.kinds:
                    self.raw(
                        self.stage.at[kind, i], self.comb.at[kind, i - 2], self.base,
                        self.base + 10 * kind + 3 + (i - 2), self.me,
                    ).wait_recv()
                    fetch = pltpu.make_async_copy(
                        self.comb.at[kind, i - 2], room(kind, i - 2),
                        self.local_sem.at[local_base + 2 * kind + i - 2],
                    )
                    fetch.start()
                    fetch.wait()

                    def add(t, kind=kind, i=i):
                        self.stage[kind, i, at(t, 64), :] = (
                            self.stage[kind, i, at(t, 64), :].astype(F32)
                            + room(kind, i - 2)[at(t, 64), :].astype(F32)
                        ).astype(BF)

                    loop(self.stage.shape[2] // 64, add)
                    self.from_zero(kind, i).start()

    def settle(self):
        core = lax.rem(self.me[2], 2)
        for kind in self.kinds:
            base = self.base + 10 * kind
            for n in (0, 2):
                self.raw(self.stage.at[kind, 0], self.got.at[kind, n], self.base, base + n, self.me).wait_recv()

            @pl.when(core == 1)
            def _(kind=kind, base=base):
                self.raw(self.stage.at[kind, 0], self.got.at[kind, 1], self.base, base + 1, self.me).wait_recv()
                for i in range(COL):
                    self.from_one(kind, i).wait_send()

            @pl.when(core == 0)
            def _(kind=kind):
                self.home(kind).wait()
                for i in (1, 2, 3):
                    self.from_zero(kind, i).wait_send()


def middle_kernel(
    n2_ref, mid_ref, scale_ref, gain_ref, own_grad, down_ref, own_up, gate_hbm, up_hbm, grad_hbm,
    grad_out, gain_out, got, comb, n2_out, dgate_out, dup_out,
    n2, dgate, dup, wg, wu, wd, gb, own_down, gate, up, du, hidden, given, arrived, z, got_z, crossing, crossed, gn, sums, stage,
    send_sem, recv_sem, local_sem,
):
    d, r, c = (lax.axis_index(name) for name in AXES)
    me = (d, r, c)
    y, core = c // 2, lax.rem(c, 2)
    rows, fc = n2_ref.shape
    block = rows // 2
    units = own_down.shape[0]
    half = 2 * fc
    over = (((0,), (0,)), ((), ()))
    across = (((1,), (1,)), ((), ()))
    post = Post(send_sem, recv_sem)
    raw = maker(send_sem, recv_sem)
    sibling = (d, r, c ^ 1)
    others = [(a, b) for a in (0, 1) for b in range(COL) if (a, b) != (0, 0)]
    greet([(d, r ^ a, c ^ b) for a, b in others] + [(d ^ j, r, c) for j in (1, 2, 3)])

    cross = post.send(
        n2_ref.at[pl.ds(pl.multiple_of((1 - y) * block, block), block), :],
        n2.at[pl.ds(0, block), pl.ds(fc, fc)],
        (d, r, c ^ 2),
    )
    def half_of(ref, i, n):
        return ref.at[pl.ds(pl.multiple_of(place_of(i) * fc + n * (fc // 2), fc // 2), fc // 2), :]

    def place_of(i):
        return lax.rem(i, 2) * 2 + i // 2

    first_wide = post.take(8)

    def up_over_y(n):
        return raw(
            own_up.at[pl.ds(n * (fc // 2), fc // 2), :], half_of(wu, 2 + core, n),
            first_wide + 4 * n, first_wide + 4 * n + core, (d, r, 2 * (1 - y)),
        )

    def up_relay(n, i):
        return raw(
            half_of(wu, i, n), half_of(wu, 5 - i, n), first_wide + 4 * n + i - 1,
            first_wide + 4 * n + 3 - i, (d, r ^ 1, 2 * y + 1),
        )

    def up_came(n, i):
        return raw(half_of(wu, i, n), half_of(wu, i, n), first_wide, first_wide + 4 * n + i - 2, me)

    for n in (0, 1):
        up_over_y(n).start()
    loads = [
        pltpu.make_async_copy(src, dst, local_sem.at[n])
        for n, (src, dst) in zip((0, 1, 2, 9), (
            (gate_hbm, wg),
            (up_hbm.at[pl.ds(0, fc), :], wu.at[pl.ds(0, fc), :]),
            (grad_hbm, gb),
            (up_hbm.at[pl.ds(2 * fc, fc), :], wu.at[pl.ds(2 * fc, fc), :]),
        ))
    ]
    for load in loads:
        load.start()

    def cast_down(t):
        own_down[at(t, 64), :] = down_ref[at(t, 64), :].astype(BF)

    loop(units // 64, cast_down)
    first_sent = post.take(10)

    def piece(ref, n):
        return ref.at[pl.ds(n * (units // 2), units // 2), :]

    def ship(n, way, i, target, src=None):
        return raw(
            piece(own_down if src is None else src, n), piece(wd.at[place_of(i)], n),
            first_sent + 5 * n + way, first_sent + 5 * n + i, target,
        )

    keep_down = pltpu.make_async_copy(own_down, wd.at[0], local_sem.at[3])

    def to_core(n):
        return ship(n, 0, 1, sibling)

    def over_y(n):
        return ship(n, 1, 2 + core, (d, r, 2 * (1 - y)))

    def over_x(n):
        return ship(n, 2, 1 - core, (d, r ^ 1, 2 * y + 1))

    def relay(n, i):
        return ship(n, i + 1, 5 - i, (d, r ^ 1, 2 * y + 1), wd.at[PLACE[i]])

    for n in (0, 1):
        over_x(n).start()
        over_y(n).start()

    @pl.when(core == 0)
    def _():
        keep_down.start()

    @pl.when(core == 1)
    def _():
        for n in (0, 1):
            to_core(n).start()

    def pass_down(n):
        @pl.when(core == 0)
        def _():
            for i in (2, 3):
                ship(n, 0, i, me).wait_recv()
                relay(n, i).start()

    n2[0:block, 0:fc] = n2_ref[pl.ds(pl.multiple_of(y * block, block), block), :]
    cross.wait_recv()

    first_up, first_down = post.take(DP), post.take(DP)
    first_shared = post.take(DP)

    def rail(p, e):
        return n2.at[at(p ^ e, block), pl.ds(0, half)]

    def go_up(p):
        return raw(rail(p, d), rail(p, d + 1), first_up + p, first_up + p, (d + 1, r, c))

    def go_down(p):
        return raw(rail(p, d), rail(p, d - 1), first_down + p, first_up + p, (d - 1, r, c))

    def share(p):
        return raw(
            rail(p, d), n2.at[at(p ^ d, block), pl.ds(half, half)], first_shared + p, first_shared + p, sibling
        )

    def onward(p):
        @pl.when((p <= d) & (d < DP - 1))
        def _():
            go_up(p).start()

        @pl.when((p >= d) & (d > 0))
        def _():
            go_down(p).start()

        share(p).start()

    def project(p):
        share(p).wait_recv()
        part = at(p ^ d, block)
        gate[part, :] = jnp.dot(n2[part, :], wg[...], preferred_element_type=F32)

    def project_up(t):
        part = at(t, block)
        up[part, :] = jnp.dot(n2[part, :], wu[...], preferred_element_type=F32)

    def pass_up(n):
        @pl.when(core == 0)
        def _():
            for i in (2, 3):
                up_came(n, i).wait_recv()
                up_relay(n, i).start()

    def hidden_grads(first, fresh):
        def one(t):
            part = at(t, block)
            value = jnp.zeros((block, units), F32) if fresh else du[part, :]
            for i in (first, first + 1):
                place = PLACE[i]
                value = value + lax.dot_general(
                    gb[part, place * fc : (place + 1) * fc], wd[place], across, preferred_element_type=F32
                )
            du[part, :] = value

        loop(DP, one)

    onward(d)
    turns = [
        d,
        jnp.where(d == 0, 1, d - 1),
        jnp.where(d < 2, 2, jnp.where(d == 2, 3, 1)),
        jnp.where(d < 2, 3, 0),
    ]
    inner = (d == 1) | (d == 2)

    def arrival(n):
        raw(rail(turns[n], d), rail(turns[n], d), first_up, first_up + turns[n], me).wait_recv()
        onward(turns[n])

    for load in loads:
        load.wait()
    arrival(1)

    @pl.when(inner)
    def _():
        arrival(2)

    pass_up(0)
    project(turns[0])
    pass_up(1)
    project(turns[1])

    @pl.when(jnp.logical_not(inner))
    def _():
        arrival(2)

    @pl.when(inner)
    def _():
        arrival(3)

    pass_down(0)
    project(turns[2])

    @pl.when(core == 0)
    def _():
        keep_down.wait()
        for n in (0, 1):
            ship(n, 0, 1, me).wait_recv()

    @pl.when(core == 1)
    def _():
        for n in (0, 1):
            for i in (0, 1):
                ship(n, 0, i, me).wait_recv()

    @pl.when(jnp.logical_not(inner))
    def _():
        arrival(3)

    hidden_grads(0, True)
    pass_down(1)
    project(turns[3])
    outs = [pltpu.make_async_copy(n2, n2_out, local_sem.at[0])]
    outs[0].start()

    @pl.when(core == 1)
    def _():
        for n in (0, 1):
            for i in (2, 3):
                up_came(n, i).wait_recv()

    loop(DP, project_up)

    @pl.when(core == 1)
    def _():
        for n in (0, 1):
            for i in (2, 3):
                ship(n, 0, i, me).wait_recv()

    hidden_grads(2, False)

    def units_of(t):
        part = at(t, 64)
        g, u, grad = gate[part, :], up[part, :], du[part, :]
        sigmoid = 1.0 / (1.0 + jnp.exp(-g))
        silu = g * sigmoid
        hidden[part, :] = (silu * u).astype(BF)
        dgate[part, :] = (grad * u * sigmoid * (1.0 + g * (1.0 - sigmoid))).astype(BF)
        dup[part, :] = (grad * silu).astype(BF)

    loop(2 * rows // 64, units_of)
    for n, (src, dst) in enumerate(((dgate, dgate_out), (dup, dup_out))):
        outs.append(pltpu.make_async_copy(src, dst, local_sem.at[1 + n]))
        outs[-1].start()

    def back(part, cols):
        return lax.dot_general(
            dgate[part, :], wg[cols, :], across, preferred_element_type=F32
        ) + lax.dot_general(dup[part, :], wu[cols, :], across, preferred_element_type=F32)

    def down_part(i):
        def down_grad(t):
            place = PLACE[i]
            stage[0, i, at(t, TILE), :] = lax.dot_general(
                hidden[:, at(t, TILE)], gb[:, place * fc : (place + 1) * fc], over, preferred_element_type=F32
            ).astype(BF)

        loop(units // TILE, down_grad)

    owners = PlaneSum(raw, stage, got, comb, post.take(10), local_sem, 4, me)

    line = LineSum(raw, ((z, got_z),), post.take(8), me)

    def plane_of(t):
        return jnp.where(d < DP // 2, DP - 1 - t, t)

    def to_sibling(t):
        part = at(plane_of(t) ^ d, block)
        return raw(given.at[part, :], arrived.at[part, :], first_given + t, first_given + t, sibling)

    def give(t):
        part = at(plane_of(t) ^ d, block)
        given[part, :] = back(part, slice(half, None)).astype(BF)
        to_sibling(t).start()

    def keep(t):
        p = plane_of(t)
        part = at(p ^ d, block)
        value = back(part, slice(0, half))
        to_sibling(t).wait_recv()
        z[p] = (value + arrived[part, :].astype(F32)).astype(BF)

        if t < DP - 1:
            @pl.when(d == 0)
            def _():
                line.up(DP - 1 - t)

            @pl.when(d == DP - 1)
            def _():
                line.down(t)

    first_given = post.take(DP)
    give(0)
    give(1)
    down_part(2)
    down_part(3)
    owners.start_far()
    keep(0)
    give(2)
    keep(1)
    give(3)
    keep(2)
    down_part(0)
    down_part(1)
    owners.start_near()
    keep(3)
    owners.combine(lambda kind, j: wg.at[pl.ds(0, units), pl.ds(j * fc, fc)], 5)
    line.rest()

    def settle_rows(t):
        part = at(t, 64)
        total = line.total(z, got_z, part)
        gn[pl.ds(pl.multiple_of(y * block + t * 64, 64), 64), :] = total[:, 0:fc]
        crossing[part, :] = total[:, fc:].astype(BF)

    loop(block // 64, settle_rows)
    other = post.send(crossing, crossed, (d, r, c ^ 2))
    other.wait_recv()

    def other_rows(t):
        gn[pl.ds(pl.multiple_of((1 - y) * block + t * 64, 64), 64), :] = crossed[at(t, 64), :].astype(F32)

    loop(block // 64, other_rows)

    def inner_sum(t):
        part = at(t, 128)
        inner = gn[part, :] * gain_ref[...] * mid_ref[part, :]
        sums[0, :, part] = as_row(jnp.sum(inner, axis=1, keepdims=True))

    loop(rows // 128, inner_sum)
    small = [post.send(sums.at[0], sums.at[m], (d, r, c ^ m)) for m in (1, 2, 3)]

    def gain_sum(t, total):
        part = at(t, 128)
        value = gn[part, :] * mid_ref[part, :] * scale_ref[part, :]
        return total + jnp.sum(value, axis=0, keepdims=True)

    gain_out[...] = lax.fori_loop(0, rows // 128, gain_sum, jnp.zeros((1, fc), F32))
    for copy in small:
        copy.wait_recv()

    def finish(t):
        part = at(t, 128)
        inner = as_column(sums[0, :, part] + sums[2, :, part] + sums[1, :, part] + sums[3, :, part])
        scale = scale_ref[part, :]
        grad_out[part, :] = (
            own_grad[part, :].astype(F32) + scale * (gn[part, :] * gain_ref[...])
            - mid_ref[part, :] * (scale * scale * scale * inner / D)
        )

    loop(rows // 128, finish)

    owners.settle()
    line.settle()
    for copy in outs:
        copy.wait()
    for copy in [cross, other] + small:
        copy.wait_send()
    for t in range(DP):
        to_sibling(t).wait_send()
    for n in (0, 1):
        over_y(n).wait_send()
        over_x(n).wait_send()
        up_over_y(n).wait_send()

        @pl.when(core == 0)
        def _(n=n):
            for i in (2, 3):
                relay(n, i).wait_send()
                up_relay(n, i).wait_send()

        @pl.when(core == 1)
        def _(n=n):
            to_core(n).wait_send()

    for p in range(DP):
        share(p).wait_send()

        @pl.when((p <= d) & (d < DP - 1))
        def _(p=p):
            go_up(p).wait_send()

        @pl.when((p >= d) & (d > 0))
        def _(p=p):
            go_down(p).wait_send()


def middle(n2, mid, scale, gain, own_grad, down, own_up, gate, up, grad_all):
    rows, fc = n2.shape
    group = 2 * rows
    block = rows // 2
    units = down.shape[0]
    vmem = pl.BlockSpec(memory_space=pltpu.VMEM)
    hbm = pl.BlockSpec(memory_space=pl.ANY)

    def like(shape, dtype=BF):
        return jax.ShapeDtypeStruct(shape, dtype)

    return pl.pallas_call(
        middle_kernel,
        in_specs=[vmem] * 6 + [hbm] * 4,
        out_specs=[vmem] * 2 + [hbm] * 5,
        out_shape=[
            like((rows, fc), F32),
            like((1, fc), F32),
            like((1, 3, units, fc)),
            like((1, 2, units, fc)),
            like((group, D)),
            like((group, units)),
            like((group, units)),
        ],
        scratch_shapes=[
            pltpu.VMEM((group, D), BF),
            pltpu.VMEM((group, units), BF),
            pltpu.VMEM((group, units), BF),
            pltpu.VMEM((D, units), BF),
            pltpu.VMEM((D, units), BF),
            pltpu.VMEM((COL, units, fc), BF),
            pltpu.VMEM((group, D), BF),
            pltpu.VMEM((units, fc), BF),
            pltpu.VMEM((group, units), F32),
            pltpu.VMEM((group, units), F32),
            pltpu.VMEM((group, units), F32),
            pltpu.VMEM((group, units), BF),
            pltpu.VMEM((group, 2 * fc), BF),
            pltpu.VMEM((group, 2 * fc), BF),
            pltpu.VMEM((DP, block, 2 * fc), BF),
            pltpu.VMEM((DP + 1, block, 2 * fc), BF),
            pltpu.VMEM((block, fc), BF),
            pltpu.VMEM((block, fc), BF),
            pltpu.VMEM((rows, fc), F32),
            pltpu.VMEM((4, 8, rows), F32),
            pltpu.VMEM((1, COL, units, fc), BF),
            pltpu.SemaphoreType.DMA((SENDS,)),
            pltpu.SemaphoreType.DMA((SENDS,)),
            pltpu.SemaphoreType.DMA((12,)),
        ],
        compiler_params=pltpu.CompilerParams(
            collective_id=3, has_side_effects=True, vmem_limit_bytes=62 << 20
        ),
        cost_estimate=pl.CostEstimate(
            flops=14 * group * D * units, bytes_accessed=48 << 20, transcendentals=group * units
        ),
    )(n2, mid, scale, gain, own_grad, down, own_up, gate, up, grad_all)


POSTS = 112


def backward_kernel(
    x_ref, gain_ref, scale_ref, mid_ref, gain_two_ref, begin_ref, weight_in_hbm, weight_out_hbm, q_hbm, kv_hbm,
    att_hbm, lse_hbm, normed_hbm, n2_hbm, dgate_hbm, dup_hbm,
    tokens_out, query_out, key_out, value_out, out_out, gains_out, got, comb,
    weight_in, weight_out, q_ref, kv_ref, att_ref, lse_ref, n1, n2, dgu, dball, dotted, dproj, acc, spill, spilled, stage, own_f, arrived, landed,
    zq, zo, zkv, rq, ro, rkv, sums, gsum,
    send_sem, recv_sem, local_sem,
):
    d, r, c = (lax.axis_index(name) for name in AXES)
    y, core = c // 2, lax.rem(c, 2)
    rows, fc = x_ref.shape
    group = 2 * rows
    width = q_hbm.shape[1]
    units = dgate_hbm.shape[1]
    half = 2 * fc
    tiles = group // TILE
    over = (((0,), (0,)), ((), ()))
    across = (((1,), (1,)), ((), ()))
    post = Post(send_sem, recv_sem)
    loads = [
        pltpu.make_async_copy(src, dst, local_sem.at[8 + n])
        for n, (src, dst) in enumerate((
            (n2_hbm, n2),
            (dgate_hbm, dgu.at[pl.ds(0, group), :]),
            (dup_hbm, dgu.at[pl.ds(group, group), :]),
            (normed_hbm, n1),
            (weight_out_hbm, weight_out),
            (att_hbm, att_ref),
            (q_hbm, q_ref),
            (kv_hbm, kv_ref),
            (lse_hbm, lse_ref),
            (weight_in_hbm, weight_in),
        ))
    ]
    for load in loads:
        load.start()

    others = [(a, b) for a in (0, 1) for b in range(COL) if (a, b) != (0, 0)]
    greet(
        [(d, r ^ a, c ^ b) for a, b in others]
        + [(d ^ j, r ^ a, c) for j in (1, 2, 3) for a in (0, 1)]
    )

    def columns(place):
        return pl.ds(place * fc, fc)

    def turned(t):
        return lax.rem(t + 2 * r, tiles)

    raw = maker(send_sem, recv_sem)
    me = (d, r, c)
    sibling = (d, r, c ^ 1)
    own_rows, other_rows = pl.ds(0, rows), pl.ds(rows, rows)
    def round_mid(t):
        dball[at(t, 128), 0:fc] = mid_ref[at(t, 128), :].astype(BF)

    loop(rows // 128, round_mid)
    own_block = dball.at[own_rows, columns(0)]
    beside = post.send(own_block, dball.at[other_rows, columns(0)], (d, r ^ 1, c))
    beyond = post.send(own_block, dball.at[own_rows, columns(1)], (d, r, c ^ 2))
    shared = [post.send(own_block, dball.at[own_rows, columns(2)], sibling)]

    for load in loads[:3]:
        load.wait()
    owners = PlaneSum(raw, stage, got, comb, post.take(20), local_sem, 4, me)

    def hidden_part(i):
        for kind in (0, 1):
            def hidden_grad(t, kind=kind):
                left = n2[:, pl.ds(pl.multiple_of(PLACE[i] * fc + t * TILE, TILE), TILE)]
                stage[kind, i, at(t, TILE), :] = lax.dot_general(
                    left, dgu[pl.ds(kind * group, group), :], over, preferred_element_type=F32
                ).astype(BF)

            loop(fc // TILE, hidden_grad)

    hidden_part(2)
    hidden_part(3)
    for load in loads[3:]:
        load.wait()

    upper = pl.ds(rows, rows // 2)
    beside.wait_recv()
    corner = [post.send(dball.at[upper, columns(0)], dball.at[upper, columns(1)], (d, r, c ^ 2))]
    shared.append(post.send(dball.at[other_rows, columns(0)], dball.at[other_rows, columns(2)], sibling))
    beyond.wait_recv()
    corner.append(post.send(
        dball.at[pl.ds(rows // 2, rows // 2), columns(1)],
        dball.at[pl.ds(rows + rows // 2, rows // 2), columns(1)], (d, r ^ 1, c),
    ))
    shared.append(post.send(dball.at[own_rows, columns(1)], dball.at[own_rows, columns(3)], sibling))
    owners.start_far()
    hidden_part(0)
    hidden_part(1)
    for copy in corner:
        copy.wait_recv()
    shared.append(post.send(dball.at[other_rows, columns(1)], dball.at[other_rows, columns(3)], sibling))
    for copy in shared:
        copy.wait_recv()

    def head_grad(t):
        dotted[at(turned(t), TILE), :] = lax.dot_general(
            dball[at(t, TILE), :], weight_out[...], across, preferred_element_type=F32
        ).astype(BF)

    loop(tiles, head_grad)

    sent_out = [None] + [post.take(1) for _ in (1, 2, 3)]
    outs = []
    for place, m in enumerate((0, 2, 1, 3)):
        value = lax.dot_general(
            att_ref[...], dball[:, place * fc : (place + 1) * fc], over, preferred_element_type=F32
        ).astype(BF)
        if m == 0:
            zo[c] = value
        else:
            n2[(m - 1) * width : m * width, half : half + fc] = value
            staged = n2.at[pl.ds((m - 1) * width, width), pl.ds(half, fc)]
            copy = raw(staged, zo.at[c], sent_out[m], sent_out[m], (d, r, c ^ m))
            copy.start()
            outs.append(copy)

    span = TILE + REACH
    scale = HEAD_DIM ** (-0.5)
    spills = []
    for h in range(width // HEAD_DIM):
        lanes = pl.ds(h * HEAD_DIM, HEAD_DIM)
        value_lanes = pl.ds(width + h * HEAD_DIM, HEAD_DIM)

        def clear(t, lanes=lanes, value_lanes=value_lanes):
            acc[at(t, TILE), lanes] = jnp.zeros((TILE, HEAD_DIM), F32)
            acc[at(t, TILE), value_lanes] = jnp.zeros((TILE, HEAD_DIM), F32)

        loop((group + REACH) // TILE, clear)

        def one(t, lanes=lanes, value_lanes=value_lanes):
            part = at(t, TILE)
            window = pl.ds(pl.multiple_of(t * TILE, TILE), span)
            query, key = q_ref[part, lanes], kv_ref[window, lanes]
            grad = dotted[part, lanes]
            scores = scores_of(query, key)
            query_at = lax.broadcasted_iota(jnp.int32, (TILE, span), 0)
            key_at = lax.broadcasted_iota(jnp.int32, (TILE, span), 1)
            begin = begin_ref[part, 0:1] + (REACH - t * TILE)
            allowed = (key_at <= query_at + REACH) & (key_at >= begin)
            scores = jnp.where(allowed, scores - lse_ref[part, lanes][:, 0:1], NEG_FILL)
            probability = jnp.exp(scores)
            grad_soft = lax.dot_general(grad, kv_ref[window, value_lanes], across, preferred_element_type=F32)
            inner = jnp.sum(probability * grad_soft, axis=1, keepdims=True)
            grad_scores = (probability * (grad_soft - inner)).astype(BF)
            dproj[at(turned(t), TILE), lanes] = (
                jnp.dot(grad_scores, key, preferred_element_type=F32) * scale
            ).astype(BF)
            acc[window, lanes] += lax.dot_general(grad_scores, query, over, preferred_element_type=F32) * scale
            acc[window, value_lanes] += lax.dot_general(
                probability.astype(BF), grad, over, preferred_element_type=F32
            )

        loop(tiles, one)

        def round_spill(t, h=h, lanes=lanes, value_lanes=value_lanes):
            spill[h, at(t, TILE), 0:HEAD_DIM] = acc[at(t, TILE), lanes].astype(BF)
            spill[h, at(t, TILE), HEAD_DIM:] = acc[at(t, TILE), value_lanes].astype(BF)

        loop(REACH // TILE, round_spill)
        copy = post.ready(spill.at[h], spilled.at[h], (lax.rem(d + DP - 1, DP), r, c))
        spills.append(copy)

        @pl.when(d > 0)
        def _(copy=copy):
            copy.start()

    def attention_grads(first_lane, lane_count, dest):
        lanes = slice(first_lane, first_lane + lane_count)
        slots = [None] + [post.take(1) for _ in (1, 2, 3)]
        copies = []
        for place, m in enumerate((0, 2, 1, 3)):
            def tile(t, place=place, m=m):
                left = n1[:, pl.ds(pl.multiple_of(place * fc + t * TILE, TILE), TILE)]
                value = lax.dot_general(left, dproj[:, lanes], over, preferred_element_type=F32).astype(BF)
                if m == 0:
                    dest[c, at(t, TILE), :] = value
                else:
                    dgu[pl.ds(pl.multiple_of(place * fc + t * TILE, TILE), TILE), lanes] = value

            loop(fc // TILE, tile)
            if m:
                copy = raw(
                    dgu.at[pl.ds(place * fc, fc), pl.ds(first_lane, lane_count)], dest.at[c],
                    slots[m], slots[m], (d, r, c ^ m),
                )
                copy.start()
                copies.append(copy)
        return copies

    qs = attention_grads(0, width, zq)

    @pl.when(d < DP - 1)
    def _():
        for copy in spills:
            copy.wait_recv()

    @pl.when(d == DP - 1)
    def _():
        spilled[...] = jnp.zeros_like(spilled)

    for h in range(width // HEAD_DIM):
        for which in (0, 1):
            lanes = pl.ds(which * width + h * HEAD_DIM, HEAD_DIM)
            out_lanes = pl.ds((1 + which) * width + h * HEAD_DIM, HEAD_DIM)

            def whole(t, h=h, which=which, lanes=lanes, out_lanes=out_lanes):
                total = acc[pl.ds(pl.multiple_of(REACH + t * TILE, TILE), TILE), lanes]
                extra = spilled[
                    h, at(jnp.maximum(t - 1, 0), TILE), which * HEAD_DIM : (which + 1) * HEAD_DIM
                ].astype(F32)
                total = total + jnp.where(t > 0, extra, 0.0)
                dproj[at(turned(t), TILE), out_lanes] = total.astype(BF)

            loop(tiles, whole)

    kvs = attention_grads(width, 2 * width, zkv)
    for copy in outs + qs:
        copy.wait_recv()
    first_line = post.take(24)
    line_a = LineSum(raw, ((zq, rq), (zo, ro)), first_line, me)
    line_b = LineSum(raw, ((zkv, rkv),), first_line + 16, me)
    line_a.begin()

    def given_part(t):
        n2[at(t, TILE), 0:half] = lax.dot_general(
            dproj[at(t, TILE), :], weight_in[half:, :], across, preferred_element_type=F32
        ).astype(BF)

    loop(tiles, given_part)
    to_sibling = post.send(n2.at[:, pl.ds(0, half)], arrived, sibling)

    to_sibling.wait_recv()
    for copy in outs:
        copy.wait_send()

    def kept_part(t):
        part = at(t, TILE)
        value = lax.dot_general(
            dproj[part, :], weight_in[:half, :], across, preferred_element_type=F32
        ) + arrived[part, :].astype(F32)
        n2[part, half:] = value.astype(BF)

        @pl.when(t < rows // TILE)
        def _():
            own_f[part, :] = value[:, 0:fc]

    loop(tiles, kept_part)

    pieces, corners, pass_pieces = scatter_plane(
        post, lambda first, count, place: n2.at[pl.ds(first, count), pl.ds(half + place * fc, fc)], landed, rows, me
    )

    def finish(line, z, got_z, dests):
        def one(t):
            value = line.total(z, got_z, at(t, 64))
            for dest, lanes in dests:
                dest[at(t, 64), :] = value[:, lanes]

        loop(z.shape[1] // 64, one)

    line_a.first()
    pieces = pieces + pass_pieces()
    owners.start_near()
    for copy in kvs:
        copy.wait_recv()
    line_b.begin()
    line_a.last()

    for copy in pieces:
        copy.wait_recv()

    def inner_sum(t):
        part = at(t, 128)
        value = own_f[part, :]
        for n in range(2):
            value = value + landed[n, part, :].astype(F32)
        own_f[part, :] = value
        inner = value * gain_ref[...] * x_ref[part, :].astype(F32)
        sums[0, :, part] = as_row(jnp.sum(inner, axis=1, keepdims=True))

    loop(rows // 128, inner_sum)
    small = [post.send(sums.at[0], sums.at[m], (d, r, c ^ m)) for m in (1, 2, 3)]
    seat = ROW * d + r
    gain_part = jnp.zeros((1, fc), F32)

    def gain_sum(t, total):
        part = at(t, 128)
        value = own_f[part, :] * x_ref[part, :].astype(F32) * scale_ref[part, :]
        return total + jnp.sum(value, axis=0, keepdims=True)

    gain_part = lax.fori_loop(0, rows // 128, gain_sum, gain_part)
    gsum[seat, 0:1, :] = gain_part
    gsum[seat, 1:2, :] = gain_two_ref[...]
    gsum[seat, 2:8, :] = jnp.zeros((6, fc), F32)
    gain_sent = post.take(8)
    gain_got = gain_sent

    def gain_copy(n, j, a):
        return raw(gsum.at[seat], gsum.at[seat], gain_sent + n, gain_got + seat, (d ^ j, r ^ a, c))

    far = [(j, a) for j in range(DP) for a in (0, 1) if (j, a) != (0, 0)]
    for n, (j, a) in enumerate(far):
        gain_copy(n, j, a).start()
    owners.combine(lambda kind, j: n1.at[pl.ds(j * fc, fc), pl.ds(kind * units, units)], 0)


    line_b.rest()
    finish(line_a, zq, rq, ((query_out, slice(None)),))
    finish(line_a, zo, ro, ((out_out, slice(None)),))
    finish(line_b, zkv, rkv, ((key_out, slice(0, width)), (value_out, slice(width, None))))
    for copy in small:
        copy.wait_recv()

    def finish_tokens(t):
        part = at(t, 128)
        inner = as_column(sums[0, :, part] + sums[2, :, part] + sums[1, :, part] + sums[3, :, part])
        scale_rows = scale_ref[part, :]
        value = x_ref[part, :].astype(F32)
        tokens_out[part, :] = (
            mid_ref[part, :] + scale_rows * (own_f[part, :] * gain_ref[...])
            - value * (scale_rows * scale_rows * scale_rows * inner / D)
        )

    loop(rows // 128, finish_tokens)

    for e in range(2 * DP):
        @pl.when(e != seat)
        def _(e=e):
            raw(gsum.at[e], gsum.at[e], gain_sent, gain_got + e, me).wait_recv()

    gains = gsum[0]
    for e in range(1, 2 * DP):
        gains = gains + gsum[e]
    gains_out[...] = gains

    owners.settle()
    line_a.settle()
    line_b.settle()
    for copy in [beside, beyond] + corner + shared + qs + kvs + [to_sibling] + pieces + corners + small:
        copy.wait_send()
    for n, (j, a) in enumerate(far):
        gain_copy(n, j, a).wait_send()

    @pl.when(d > 0)
    def _():
        for copy in spills:
            copy.wait_send()


def backward(x, gain, scale, mid, gain_two, weight_in, weight_out, q, kv, att, lse, begin, normed, n2, dgate, dup):
    rows, fc = x.shape
    group = 2 * rows
    width = q.shape[1]
    units = dgate.shape[1]
    vmem = pl.BlockSpec(memory_space=pltpu.VMEM)
    hbm = pl.BlockSpec(memory_space=pl.ANY)

    def like(shape, dtype=BF):
        return jax.ShapeDtypeStruct(shape, dtype)

    return pl.pallas_call(
        backward_kernel,
        in_specs=[vmem] * 6 + [hbm] * 10,
        out_specs=[vmem] * 6 + [hbm] * 2,
        out_shape=[
            like((rows, fc), F32),
            like((fc, width), F32),
            like((fc, width), F32),
            like((fc, width), F32),
            like((width, fc), F32),
            like((8, fc), F32),
            like((2, 3, fc, units)),
            like((2, 2, fc, units)),
        ],
        scratch_shapes=[
            pltpu.VMEM((D, 3 * width), BF),
            pltpu.VMEM((width, D), BF),
            pltpu.VMEM((group, width), BF),
            pltpu.VMEM((REACH + group, 2 * width), BF),
            pltpu.VMEM((group, width), BF),
            pltpu.VMEM((group, width), F32),
            pltpu.VMEM((group, D), BF),
            pltpu.VMEM((group, D), BF),
            pltpu.VMEM((2 * group, units), BF),
            pltpu.VMEM((group, D), BF),
            pltpu.VMEM((group, width), BF),
            pltpu.VMEM((group, 3 * width), BF),
            pltpu.VMEM((group + REACH, 2 * width), F32),
            pltpu.VMEM((width // HEAD_DIM, REACH, 2 * HEAD_DIM), BF),
            pltpu.VMEM((width // HEAD_DIM, REACH, 2 * HEAD_DIM), BF),
            pltpu.VMEM((2, COL, fc, units), BF),
            pltpu.VMEM((rows, fc), F32),
            pltpu.VMEM((group, 2 * fc), BF),
            pltpu.VMEM((3, rows, fc), BF),
            pltpu.VMEM((DP, fc, width), BF),
            pltpu.VMEM((DP, width, fc), BF),
            pltpu.VMEM((DP, fc, 2 * width), BF),
            pltpu.VMEM((DP + 1, fc, width), BF),
            pltpu.VMEM((DP + 1, width, fc), BF),
            pltpu.VMEM((DP + 1, fc, 2 * width), BF),
            pltpu.VMEM((4, 8, rows), F32),
            pltpu.VMEM((2 * DP, 8, fc), F32),
            pltpu.SemaphoreType.DMA((POSTS,)),
            pltpu.SemaphoreType.DMA((POSTS,)),
            pltpu.SemaphoreType.DMA((20,)),
        ],
        compiler_params=pltpu.CompilerParams(
            collective_id=2, has_side_effects=True, vmem_limit_bytes=62 << 20
        ),
        cost_estimate=pl.CostEstimate(
            flops=12 * group * D * width + 4 * group * D * units, bytes_accessed=64 << 20, transcendentals=0
        ),
    )(x, gain, scale, mid, gain_two, begin, weight_in, weight_out, q, kv, att, lse, normed, n2, dgate, dup)


def closing_kernel(
    tokens, query, key, value, out, hidden, down, gains,
    tokens_out, query_out, key_out, value_out, out_out, gate_out, up_out, down_out, one_out, two_out,
):
    for src, dst in (
        (tokens, tokens_out), (query, query_out), (key, key_out), (value, value_out), (out, out_out)
    ):
        dst[...] = src[...]
    for dst, kind in ((gate_out, 0), (up_out, 1)):
        dst[...] = hidden[kind, 0].astype(F32) + hidden[kind, 1].astype(F32) + hidden[kind, 2].astype(F32)
    one_out[...] = gains[0]
    two_out[...] = gains[1]
    down_out[...] = down[0, 0].astype(F32) + down[0, 1].astype(F32) + down[0, 2].astype(F32)


def closing(tokens, query, key, value, out, hidden, down, gains):
    steps = 4

    def rows_of(array):
        rows, width = array.shape[-2:]
        lead = array.shape[:-2]
        return pl.BlockSpec(lead + (rows // steps, width), lambda t: (0,) * len(lead) + (t, 0))

    finals = [tokens, query, key, value, out] + [
        jax.ShapeDtypeStruct(a.shape[-2:], F32) for a in (hidden, hidden, down)
    ]
    return pl.pallas_call(
        closing_kernel,
        grid=(steps,),
        in_specs=[rows_of(a) for a in (tokens, query, key, value, out, hidden, down)]
        + [pl.BlockSpec(gains.shape, lambda t: (0, 0))],
        out_specs=[rows_of(a) for a in finals] + [pl.BlockSpec(gains.shape[1:], lambda t: (0,))] * 2,
        out_shape=[jax.ShapeDtypeStruct(a.shape, F32) for a in finals]
        + [jax.ShapeDtypeStruct(gains.shape[1:], F32)] * 2,
        compiler_params=pltpu.CompilerParams(vmem_limit_bytes=62 << 20),
    )(tokens, query, key, value, out, hidden, down, gains)


def on_small_mesh(
    tokens,
    cotangent,
    query_master,
    key_master,
    value_master,
    out_master,
    gate_master,
    up_master,
    down_master,
    attn_gain,
    ffn_gain,
    lengths,
    permutation,
):
    del permutation
    (
        mid, scale_two, n2, begin, scale_one, normed_one, weight_in, weight_out, q, key_value,
        own_attended, lse, own_up, weight_gate, weight_up, grad_all,
    ) = forward(
        tokens, attn_gain[None, :], ffn_gain[None, :], lengths, query_master, key_master,
        value_master, out_master, gate_master, up_master, cotangent,
    )
    grad_mid, gain_two_part, got_down, _, normed_two, grad_gate, grad_up = middle(
        n2, mid, scale_two, ffn_gain[None, :], cotangent, down_master, own_up, weight_gate,
        weight_up, grad_all,
    )
    grad_tokens, grad_query, grad_key, grad_value, grad_out, gains, got, _ = backward(
        tokens, attn_gain[None, :], scale_one, grad_mid, gain_two_part, weight_in, weight_out, q,
        key_value, own_attended, lse, begin, normed_one, normed_two, grad_gate, grad_up,
    )
    return closing(grad_tokens, grad_query, grad_key, grad_value, grad_out, got, got_down, gains)


def solution(mesh):
    placed = (
        P(("dp", "row"), "col"),
        P(("dp", "row"), "col"),
        P("col", ("row", "dp")),
        P("col", ("row", "dp")),
        P("col", ("row", "dp")),
        P(("row", "dp"), "col"),
        P("col", ("row", "dp")),
        P("col", ("row", "dp")),
        P(("row", "dp"), "col"),
        P("col"),
        P("col"),
        P(),
        P(),
    )
    small = tuple(mesh.shape[name] for name in AXES) == (DP, ROW, COL)
    return jax.shard_map(
        on_small_mesh if small else on_any_mesh,
        mesh=mesh,
        in_specs=placed,
        out_specs=(
            P(("dp", "row"), "col"),
            P("col", ("row", "dp")),
            P("col", ("row", "dp")),
            P("col", ("row", "dp")),
            P(("row", "dp"), "col"),
            P("col", ("row", "dp")),
            P("col", ("row", "dp")),
            P(("row", "dp"), "col"),
            P("col"),
            P("col"),
        ),
        check_vma=False,
    )
```

```python
import functools

import jax
import jax.numpy as jnp
from jax import lax
from jax.experimental import pallas as pl
from jax.experimental.pallas import tpu as pltpu
from jax.sharding import PartitionSpec as P

D = 2048
HEAD_DIM = 128


EPSILON = 1e-06
NEG_FILL = -1e30
AXES = ("dp", "row", "col")
DP, ROW, COL = 4, 2, 4
REACH = 768
BF = jnp.bfloat16
F32 = jnp.float32


def running_sum(lengths):
    count = lengths.shape[0]
    earlier = jnp.arange(count)[:, None] <= jnp.arange(count)[None, :]
    return jnp.sum(jnp.where(earlier, lengths[:, None], 0), axis=0)

def make_picker(wanted, carried, pieces):
    amount = pieces[0].shape[0]
    inside = (wanted >= 0) & (wanted < amount)
    chosen = jnp.clip(wanted, 0, amount - 1)
    return tuple(
        (
            jnp.where(inside[:, None], jnp.take(shard_rows, chosen, axis=0), current)
            for shard_rows, current in zip(pieces, carried)
        )
    )


def sequence_marks(permutation, lengths, first_slot, amount):
    source = lax.dynamic_slice_in_dim(permutation, first_slot, amount)
    seq_ends = running_sum(lengths)
    passed = seq_ends[None, :] <= source[:, None]
    member = jnp.sum(passed.astype(jnp.int32), axis=1)
    begins = jnp.max(jnp.where(passed, seq_ends[None, :], 0), axis=1)
    return (member, source - begins)


def col_total(values):
    return lax.psum(jnp.sum(values, axis=1), "col")


def row_gather(values):
    return lax.all_gather(values, "row", axis=0, tiled=True)


def col_gather(values):
    return lax.all_gather(values, "col", axis=0, tiled=True)


def key_gather(keys_here, values_here):
    return (
        lax.all_gather(keys_here, "col", axis=0, tiled=True),
        lax.all_gather(values_here, "col", axis=0, tiled=True),
    )


def multiply(row_block, weight, transpose_right):
    if transpose_right:
        return lax.dot_general(
            row_block, weight, (((1,), (1,)), ((), ())), preferred_element_type=jnp.float32
        )
    return jnp.dot(row_block, weight, preferred_element_type=jnp.float32)


def outer_sum(left_rows, right_rows):
    return lax.dot_general(
        left_rows, right_rows, (((0,), (0,)), ((), ())), preferred_element_type=jnp.float32
    )


def col_reduce(spread, weight, transpose_right):
    return lax.psum_scatter(
        multiply(spread, weight, transpose_right), "col", scatter_dimension=0, tiled=True
    )


def row_reduce(spread, weight, transpose_right):
    return lax.psum_scatter(
        multiply(spread, weight, transpose_right), "row", scatter_dimension=0, tiled=True
    )


def visible(query_member, query_position, member, position):
    same = query_member[:, None] == member[None, :]
    behind = position[None, :] <= query_position[:, None]
    return same & behind


def attend_scores(query_block, key_all, allowed):
    scores = jnp.einsum(
        "qhd,khd->hqk", query_block, key_all, preferred_element_type=jnp.float32
    ) * HEAD_DIM ** (-0.5)
    return jnp.where(allowed[None, :, :], scores, NEG_FILL)


def norm_back(grad_normed, inputs_f, scale_rows, gain):
    gain_part = jnp.sum(grad_normed * inputs_f * scale_rows[:, None], axis=0)
    scaled = grad_normed * gain[None, :]
    inner = col_total(scaled * inputs_f)
    grad_inputs = scale_rows[:, None] * scaled - inputs_f * (scale_rows**3 * inner / D)[:, None]
    return (grad_inputs, gain_part)


def on_any_mesh(
    tokens,
    cotangent,
    query_master,
    key_master,
    value_master,
    out_master,
    gate_master,
    up_master,
    down_master,
    attn_gain,
    ffn_gain,
    lengths,
    permutation,
):
    own_rows = tokens.shape[0]
    group_rows = own_rows * lax.axis_size("row")
    quarter = group_rows // lax.axis_size("col")
    device_slot = lax.axis_index(("dp", "row"))
    group_slot = lax.axis_index("dp")
    col_slot = lax.axis_index("col")
    own_sources = lax.dynamic_slice_in_dim(permutation, device_slot * own_rows, own_rows)
    own_tokens, own_cotangent = make_picker(
        own_sources,
        (jnp.zeros_like(tokens), jnp.zeros_like(cotangent)),
        (
            lax.all_gather(tokens, ("dp", "row"), axis=0, tiled=True),
            lax.all_gather(cotangent, ("dp", "row"), axis=0, tiled=True),
        ),
    )
    masters = tuple(
        (
            matrix.astype(jnp.bfloat16)
            for matrix in (
                query_master,
                key_master,
                value_master,
                out_master,
                gate_master,
                up_master,
                down_master,
            )
        )
    )
    query_weight, key_weight, value_weight, out_weight, gate_weight, up_weight, down_weight = (
        lax.all_gather(masters[0], "dp", axis=1, tiled=True),
        lax.all_gather(masters[1], "dp", axis=1, tiled=True),
        lax.all_gather(masters[2], "dp", axis=1, tiled=True),
        lax.all_gather(masters[3], "dp", axis=0, tiled=True),
        lax.all_gather(masters[4], "dp", axis=1, tiled=True),
        lax.all_gather(masters[5], "dp", axis=1, tiled=True),
        lax.all_gather(masters[6], "dp", axis=0, tiled=True),
    )
    attention_in = jnp.concatenate([query_weight, key_weight, value_weight], axis=1)
    feedforward_in = jnp.concatenate([gate_weight, up_weight], axis=1)
    width_row = query_weight.shape[1]
    heads_row = width_row // HEAD_DIM
    hidden_row = gate_weight.shape[1]
    member, position = sequence_marks(permutation, lengths, group_slot * group_rows, group_rows)
    query_member = lax.dynamic_slice_in_dim(member, col_slot * quarter, quarter)
    query_position = lax.dynamic_slice_in_dim(position, col_slot * quarter, quarter)
    block_rows = min(512, quarter)
    block_count = quarter // block_rows
    residual_in = own_tokens.astype(jnp.float32)
    scale_one = lax.rsqrt(col_total(residual_in * residual_in) / D + EPSILON)
    normed_one = (residual_in * scale_one[:, None] * attn_gain[None, :]).astype(jnp.bfloat16)
    spread_one = row_gather(normed_one)
    projected = col_reduce(spread_one, attention_in, False).astype(jnp.bfloat16)
    queries = projected[:, :width_row].reshape(quarter, heads_row, HEAD_DIM)
    keys_here = projected[:, width_row : 2 * width_row]
    values_here = projected[:, 2 * width_row :]
    key_flat, value_flat = key_gather(keys_here, values_here)
    key_all = key_flat.reshape(group_rows, heads_row, HEAD_DIM)
    value_all = value_flat.reshape(group_rows, heads_row, HEAD_DIM)

    def block_mask(first_row):
        return visible(
            lax.dynamic_slice_in_dim(query_member, first_row, block_rows),
            lax.dynamic_slice_in_dim(query_position, first_row, block_rows),
            member,
            position,
        )

    def forward_block(block_id):
        first_row = block_id * block_rows
        query_block = lax.dynamic_slice_in_dim(queries, first_row, block_rows, 0)
        scores = attend_scores(query_block, key_all, block_mask(first_row))
        highest = jnp.max(scores, axis=2, keepdims=True)
        totals = jnp.sum(jnp.exp(scores - highest), axis=2, keepdims=True)
        log_total = highest + jnp.log(totals)
        probability = jnp.exp(scores - log_total)
        output = jnp.einsum(
            "hqk,khd->qhd",
            probability.astype(jnp.bfloat16),
            value_all,
            preferred_element_type=jnp.float32,
        )
        return (output.astype(jnp.bfloat16).reshape(block_rows, width_row), log_total[:, :, 0])

    blocks_out, log_totals = lax.map(forward_block, jnp.arange(block_count, dtype=jnp.int32))
    attended = blocks_out.reshape(quarter, width_row)
    spread_attn = col_gather(attended)
    midway = residual_in + row_reduce(spread_attn, out_weight, False)
    scale_two = lax.rsqrt(col_total(midway * midway) / D + EPSILON)
    normed_two = (midway * scale_two[:, None] * ffn_gain[None, :]).astype(jnp.bfloat16)
    spread_two = row_gather(normed_two)
    gate_and_up = col_reduce(spread_two, feedforward_in, False)
    gate_value = gate_and_up[:, :hidden_row]
    up_value = gate_and_up[:, hidden_row:]
    sigmoid_gate = jax.nn.sigmoid(gate_value)
    hidden = (gate_value * sigmoid_gate * up_value).astype(jnp.bfloat16)
    grad_output = own_cotangent.astype(jnp.float32)
    spread_down = row_gather(own_cotangent)
    grad_hidden = col_reduce(spread_down, down_weight, True)
    spread_hidden = col_gather(hidden)
    grad_down = outer_sum(spread_hidden, spread_down)
    grad_gate_value = (
        grad_hidden * up_value * sigmoid_gate * (1.0 + gate_value * (1.0 - sigmoid_gate))
    ).astype(jnp.bfloat16)
    grad_up_value = (grad_hidden * gate_value * sigmoid_gate).astype(jnp.bfloat16)
    spread_gate_up = col_gather(jnp.concatenate([grad_gate_value, grad_up_value], axis=1))
    grad_normed_two = row_reduce(spread_gate_up, feedforward_in, True)
    spread_two = row_gather(normed_two)
    grad_feedforward = outer_sum(spread_two, spread_gate_up)
    grad_mid_norm, gain_two_part = norm_back(grad_normed_two, midway, scale_two, ffn_gain)
    grad_midway = grad_output + grad_mid_norm
    rounded_midway = grad_midway.astype(jnp.bfloat16)
    spread_back = row_gather(rounded_midway)
    grad_attended = col_reduce(spread_back, out_weight, True).astype(jnp.bfloat16)
    spread_attn = col_gather(attended)
    key_flat, value_flat = key_gather(keys_here, values_here)
    key_all = key_flat.reshape(group_rows, heads_row, HEAD_DIM)
    value_all = value_flat.reshape(group_rows, heads_row, HEAD_DIM)
    grad_out_local = outer_sum(spread_attn, spread_back)

    def backward_block(carried, block_id):
        first_row = block_id * block_rows
        query_block = lax.dynamic_slice_in_dim(queries, first_row, block_rows, 0)
        scores = attend_scores(query_block, key_all, block_mask(first_row))
        probability = jnp.exp(
            scores - lax.dynamic_index_in_dim(log_totals, block_id, 0, keepdims=False)[:, :, None]
        )
        weights_low = probability.astype(jnp.bfloat16)
        grad_block = lax.dynamic_slice_in_dim(grad_attended, first_row, block_rows, 0).reshape(
            block_rows, heads_row, HEAD_DIM
        )
        grad_soft = jnp.einsum(
            "qhd,khd->hqk", grad_block, value_all, preferred_element_type=jnp.float32
        )
        row_inner = jnp.sum(probability * grad_soft, axis=2, keepdims=True)
        grad_scores = (probability * (grad_soft - row_inner)).astype(jnp.bfloat16)
        grad_query_block = jnp.einsum(
            "hqk,khd->qhd", grad_scores, key_all, preferred_element_type=jnp.float32
        ) * HEAD_DIM ** (-0.5)
        grad_key_all = carried[0] + jnp.einsum(
            "hqk,qhd->khd", grad_scores, query_block, preferred_element_type=jnp.float32
        ) * HEAD_DIM ** (-0.5)
        grad_value_all = carried[1] + jnp.einsum(
            "hqk,qhd->khd", weights_low, grad_block, preferred_element_type=jnp.float32
        )
        return (
            (grad_key_all, grad_value_all),
            grad_query_block.astype(jnp.bfloat16).reshape(block_rows, width_row),
        )

    start_grads = jnp.zeros((group_rows, heads_row, HEAD_DIM), jnp.float32)
    key_value_grads, grad_queries = lax.scan(
        backward_block, (start_grads, start_grads), jnp.arange(block_count, dtype=jnp.int32)
    )
    grad_queries = grad_queries.reshape(quarter, width_row)
    grad_key_part = key_value_grads[0].reshape(group_rows, width_row)
    grad_value_part = key_value_grads[1].reshape(group_rows, width_row)
    grad_key_mine, grad_value_mine = (
        lax.psum_scatter(grad_key_part, "col", scatter_dimension=0, tiled=True),
        lax.psum_scatter(grad_value_part, "col", scatter_dimension=0, tiled=True),
    )
    spread_projected = col_gather(
        jnp.concatenate(
            [
                grad_queries,
                grad_key_mine.astype(jnp.bfloat16),
                grad_value_mine.astype(jnp.bfloat16),
            ],
            axis=1,
        )
    )
    grad_normed_one = row_reduce(spread_projected, attention_in, True)
    spread_one = row_gather(normed_one)
    grad_attention = outer_sum(spread_one, spread_projected)
    grad_in_norm, gain_one_part = norm_back(grad_normed_one, residual_in, scale_one, attn_gain)
    grad_own_tokens = grad_midway + grad_in_norm
    grad_attn_gain, grad_ffn_gain = lax.psum((gain_one_part, gain_two_part), ("dp", "row"))
    grad_query, grad_key, grad_value, grad_out, grad_gate, grad_up, grad_down_mine = (
        lax.psum_scatter(
            grad_attention[:, :width_row].astype(jnp.bfloat16),
            "dp",
            scatter_dimension=1,
            tiled=True,
        ).astype(jnp.float32),
        lax.psum_scatter(
            grad_attention[:, width_row : 2 * width_row].astype(jnp.bfloat16),
            "dp",
            scatter_dimension=1,
            tiled=True,
        ).astype(jnp.float32),
        lax.psum_scatter(
            grad_attention[:, 2 * width_row :].astype(jnp.bfloat16),
            "dp",
            scatter_dimension=1,
            tiled=True,
        ).astype(jnp.float32),
        lax.psum_scatter(
            grad_out_local.astype(jnp.bfloat16), "dp", scatter_dimension=0, tiled=True
        ).astype(jnp.float32),
        lax.psum_scatter(
            grad_feedforward[:, :hidden_row].astype(jnp.bfloat16),
            "dp",
            scatter_dimension=1,
            tiled=True,
        ).astype(jnp.float32),
        lax.psum_scatter(
            grad_feedforward[:, hidden_row:].astype(jnp.bfloat16),
            "dp",
            scatter_dimension=1,
            tiled=True,
        ).astype(jnp.float32),
        lax.psum_scatter(
            grad_down.astype(jnp.bfloat16), "dp", scatter_dimension=0, tiled=True
        ).astype(jnp.float32),
    )
    total_tokens = permutation.shape[0]
    inverse = (
        jnp.zeros((total_tokens,), jnp.int32)
        .at[permutation]
        .set(jnp.arange(total_tokens, dtype=jnp.int32))
    )
    wanted_slots = lax.dynamic_slice_in_dim(inverse, device_slot * own_rows, own_rows)
    (grad_tokens,) = make_picker(
        wanted_slots,
        (jnp.zeros_like(grad_own_tokens),),
        (
            (
                lax.all_gather(
                    grad_own_tokens.astype(jnp.bfloat16), ("dp", "row"), axis=0, tiled=True
                ),
            )[0].astype(jnp.float32),
        ),
    )
    return (
        grad_tokens,
        grad_query,
        grad_key,
        grad_value,
        grad_out,
        grad_gate,
        grad_up,
        grad_down_mine,
        grad_attn_gain,
        grad_ffn_gain,
    )


def scores_of(query, key):
    return lax.dot_general(
        query, key, (((1,), (1,)), ((), ())), preferred_element_type=F32
    ) * HEAD_DIM ** (-0.5)


MESH = pl.DeviceIdType.MESH
PLACE = {0: 0, 2: 1, 1: 2, 3: 3}
TILE = 256


class Post:
    def __init__(self, send_sem, recv_sem):
        self.send_sem, self.recv_sem, self.used = send_sem, recv_sem, 0

    def ready(self, src, dst, target, slot=None):
        if slot is None:
            slot = self.used
            self.used += 1
        return pltpu.make_async_remote_copy(
            src_ref=src,
            dst_ref=dst,
            send_sem=self.send_sem.at[slot],
            recv_sem=self.recv_sem.at[slot],
            device_id=target,
            device_id_type=MESH,
        )

    def take(self, count):
        first = self.used
        self.used += count
        return first

    def send(self, src, dst, target):
        copy = self.ready(src, dst, target)
        copy.start()
        return copy


def greet(peers):
    barrier = pltpu.get_barrier_semaphore()
    for peer in peers:
        pl.semaphore_signal(barrier, inc=1, device_id=peer, device_id_type=MESH)
    pl.semaphore_wait(barrier, len(peers))


def as_row(column):
    return jnp.transpose(jnp.broadcast_to(column, (column.shape[0], 128)))[0:8]


def as_column(row):
    return jnp.transpose(row)[:, 0:1]


def scatter_plane(post, low, landed, rows, me):
    d, r, c = me
    half = rows // 2
    x_at, y_at = (d, r ^ 1, c), (d, r, c ^ 2)
    upper, lower = pl.ds(0, half), pl.ds(half, half)
    corner_x = post.send(low(rows, half, 1), landed.at[2, upper], x_at)
    corner_y = post.send(low(rows + half, half, 1), landed.at[2, lower], y_at)
    sent = [
        post.send(low(rows, half, 0), landed.at[0, upper], x_at),
        post.send(low(half, half, 1), landed.at[1, lower], y_at),
    ]

    def add(ref, first):
        def one(t, total):
            part = pl.ds(pl.multiple_of(t * 64, 64), 64)
            there = pl.ds(pl.multiple_of(first + t * 64, 64), 64)
            ref[part, :] = (ref[part, :].astype(F32) + landed[2, there, :].astype(F32)).astype(BF)
            return total

        lax.fori_loop(0, half // 64, one, 0)

    def pass_pieces():
        corner_x.wait_recv()
        add(low(0, half, 1), 0)
        later = [post.send(low(0, half, 1), landed.at[1, upper], y_at)]
        corner_y.wait_recv()
        add(low(rows + half, half, 0), half)
        later.append(post.send(low(rows + half, half, 0), landed.at[0, lower], x_at))
        return later

    return sent, [corner_x, corner_y], pass_pieces


def forward_kernel(
    x_ref, gain_one_ref, gain_two_ref, lengths_ref, query_ref, key_ref, value_ref, out_ref, gate_hbm, up_hbm,
    own_grad,
    mid_ref, scale_ref, n2_ref, begin_ref, first_scale,
    normed_out, weight_in_out, weight_out_out, q_out, kv_out, att_out, lse_out, own_up, gate_all, up_all, grad_all,
    normed_ref, weight_in, weight_out, q_ref, kv_ref, att_ref, lse_ref, masters,
    zin, zout, sums, wide, given, arrived, low, landed, x32, hidden_own,
    send_sem, recv_sem, local_sem,
):
    d, r, c = (lax.axis_index(name) for name in AXES)
    y, core = c // 2, lax.rem(c, 2)
    rows = x_ref.shape[0]
    fc = x_ref.shape[1]
    group = 2 * rows
    width = q_ref.shape[1]
    half = 2 * fc
    post = Post(send_sem, recv_sem)
    fetches = [
        pltpu.make_async_copy(src, masters.at[n], local_sem.at[8 + n]) for n, src in enumerate((gate_hbm, up_hbm))
    ]
    for copy in fetches:
        copy.start()
    copies = []

    def copy_out(src, dst):
        copy = pltpu.make_async_copy(src, dst, local_sem.at[10 + len(copies)])
        copy.start()
        copies.append(copy)

    in_plane = [(d, r ^ a, c ^ b) for a in (0, 1) for b in range(COL) if (a, b) != (0, 0)]
    greet([(d ^ j, r, c) for j in (1, 2, 3)] + in_plane)

    def fill_x(t, total):
        part = pl.ds(pl.multiple_of(t * 128, 128), 128)
        value = x_ref[part, :].astype(F32)
        x32[part, :] = value
        sums[0, :, part] = as_row(jnp.sum(value * value, axis=1, keepdims=True))
        return total

    lax.fori_loop(0, rows // 128, fill_x, 0)
    small = [post.send(sums.at[0], sums.at[m], (d, r, c ^ m)) for m in (1, 2, 3)]

    parts = (pl.ds(width, 2 * width), pl.ds(0, width))
    first, first_down = post.take(3 * DP), post.take(3 * DP)

    def block_of(n, p):
        return zin.at[p, :, parts[n]] if n < 2 else zout.at[p]

    def line(n, p, target_plane):
        block = block_of(n, p)
        return post.ready(block, block, (target_plane, r, c), first + DP * n + p)

    def line_down(n, p, target_plane):
        block = block_of(n, p)
        return pltpu.make_async_remote_copy(
            src_ref=block, dst_ref=block,
            send_sem=send_sem.at[first_down + DP * n + p], recv_sem=recv_sem.at[first + DP * n + p],
            device_id=(target_plane, r, c), device_id_type=MESH,
        )

    def cast_rows(src, dst, amount, step=64):
        def one(t, total):
            part = pl.ds(pl.multiple_of(t * step, step), step)
            dst(part, src[part, :].astype(BF))
            return total

        lax.fori_loop(0, amount // step, one, 0)

    for place, master in enumerate((query_ref, key_ref, value_ref)):
        def put(part, value, place=place):
            zin[d, part, place * width : (place + 1) * width] = value

        cast_rows(master, put, fc)
    def leave(n):
        @pl.when(d < DP - 1)
        def _():
            line(n, d, d + 1).start()

        @pl.when(d > 0)
        def _():
            line_down(n, d, d - 1).start()

    leave(0)
    leave(1)

    first_cols = post.take(3 * DP)

    def place_of(m):
        return lax.rem(m, 2) * 2 + m // 2

    def seat_of(n, place):
        there = pl.ds(pl.multiple_of(place * fc, fc), fc)
        return weight_in.at[there, parts[n]] if n < 2 else weight_out.at[:, there]

    def to_column(n, p):
        return pltpu.make_async_remote_copy(
            src_ref=block_of(n, p),
            dst_ref=seat_of(n, place_of(p ^ c)),
            send_sem=send_sem.at[first_cols + DP * n + p],
            recv_sem=recv_sem.at[first_cols + DP * n + (p ^ c)],
            device_id=(d, r, p), device_id_type=MESH,
        )

    def keep(n):
        return pltpu.make_async_copy(block_of(n, c), seat_of(n, 0), local_sem.at[(0, 1, 5)[n]])

    def pass_on(n, p):
        @pl.when(p == c)
        def _():
            keep(n).start()

        @pl.when(p != c)
        def _():
            to_column(n, p).start()

    hidden_all = (gate_all, up_all)
    first_sent = post.take(10)
    first_got = first_sent

    def slab(kind, i):
        return hidden_all[kind].at[pl.ds(pl.multiple_of(place_of(i) * fc, fc), fc), :]

    def ship(kind, way, i, target, src=None):
        return pltpu.make_async_remote_copy(
            src_ref=hidden_own.at[kind] if src is None else src,
            dst_ref=slab(kind, i),
            send_sem=send_sem.at[first_sent + 5 * kind + way],
            recv_sem=recv_sem.at[first_got + 4 * kind + i],
            device_id=target, device_id_type=MESH,
        )

    def keep_hidden(kind):
        return pltpu.make_async_copy(hidden_own.at[kind], slab(kind, 0), local_sem.at[3 + kind])

    def to_core(kind):
        return ship(kind, 0, 1, (d, r, c ^ 1))

    first_half = post.take(8)

    def gate_half(i, n):
        step = fc // 2
        return gate_all.at[pl.ds(pl.multiple_of(place_of(i) * fc + n * step, step), step), :]

    def over_y(n):
        return pltpu.make_async_remote_copy(
            src_ref=hidden_own.at[0, pl.ds(n * (fc // 2), fc // 2), :], dst_ref=gate_half(2 + core, n),
            send_sem=send_sem.at[first_half + 4 * n], recv_sem=recv_sem.at[first_half + 4 * n + core],
            device_id=(d, r, 2 * (1 - y)), device_id_type=MESH,
        )

    def over_x(kind):
        return ship(kind, 2, 1 - core, (d, r ^ 1, 2 * y + 1))

    def relay(n, i):
        return pltpu.make_async_remote_copy(
            src_ref=gate_half(i, n), dst_ref=gate_half(5 - i, n),
            send_sem=send_sem.at[first_half + 4 * n + i - 1],
            recv_sem=recv_sem.at[first_half + 4 * n + 3 - i],
            device_id=(d, r ^ 1, 2 * y + 1), device_id_type=MESH,
        )

    def gate_came(n, i):
        return pltpu.make_async_remote_copy(
            src_ref=gate_half(i, n), dst_ref=gate_half(i, n),
            send_sem=send_sem.at[first_half], recv_sem=recv_sem.at[first_half + 4 * n + i - 2],
            device_id=(d, r, c), device_id_type=MESH,
        )

    def start_home(kind):
        @pl.when(core == 0)
        def _():
            keep_hidden(kind).start()

        @pl.when(core == 1)
        def _():
            to_core(kind).start()

    def start_relay(n):
        @pl.when(core == 0)
        def _():
            for i in (2, 3):
                gate_came(n, i).wait_recv()
                relay(n, i).start()

    def cast_hidden(kind):
        def put(part, value):
            hidden_own[kind, part, :] = value

        fetches[kind].wait()
        cast_rows(masters.at[kind], put, fc)

    cast_hidden(0)
    over_x(0).start()
    over_y(0).start()
    for copy in small:
        copy.wait_recv()

    def norm_one(t, total):
        part = pl.ds(pl.multiple_of(t * 128, 128), 128)
        square = sums[0, :, part] + sums[2, :, part] + sums[1, :, part] + sums[3, :, part]
        scale = lax.rsqrt(as_column(square) / D + EPSILON)
        first_scale[part, :] = scale
        normed_ref[part, 0:fc] = (x32[part, :] * scale * gain_one_ref[...]).astype(BF)
        return total

    lax.fori_loop(0, rows // 128, norm_one, 0)
    own_rows, other_rows = pl.ds(0, rows), pl.ds(rows, rows)

    def columns(place):
        return pl.ds(place * fc, fc)

    own_block = normed_ref.at[own_rows, columns(0)]
    beside = post.send(own_block, normed_ref.at[other_rows, columns(0)], (d, r ^ 1, c))
    beyond = post.send(own_block, normed_ref.at[own_rows, columns(1)], (d, r, c ^ 2))
    corner = post.send(own_block, normed_ref.at[other_rows, columns(1)], (d, r ^ 1, c ^ 2))
    sibling = (d, r, c ^ 1)
    shared = [post.send(own_block, normed_ref.at[own_rows, columns(2)], sibling)]
    pass_on(0, d)
    pass_on(1, d)
    cast_hidden(1)
    start_home(0)
    start_home(1)
    copy_out(hidden_own.at[1], own_up)
    over_x(1).start()
    half_rows = rows // 2
    grad_cross = post.send(
        own_grad.at[pl.ds(pl.multiple_of((1 - y) * half_rows, half_rows), half_rows), :],
        grad_all.at[pl.ds(0, half_rows), pl.ds(fc, fc)],
        (d, r, c ^ 2),
    )
    grad_keep = pltpu.make_async_copy(
        own_grad.at[pl.ds(pl.multiple_of(y * half_rows, half_rows), half_rows), :],
        grad_all.at[pl.ds(0, half_rows), pl.ds(0, fc)],
        local_sem.at[2],
    )
    grad_keep.start()

    def put_out(part, value):
        zout[d, part, :] = value

    cast_rows(out_ref, put_out, width)

    def find_begins(t, total):
        part = pl.ds(pl.multiple_of(t * 128, 128), 128)
        place = lax.broadcasted_iota(jnp.int32, (128, 1), 0) + (d * group + t * 128)
        end = jnp.int32(0)
        begin = jnp.zeros((128, 1), jnp.int32)
        for n in range(lengths_ref.shape[0]):
            end = end + lengths_ref[n]
            begin = jnp.where(place >= end, end, begin)
        begin_ref[part, :] = begin - d * group
        return total

    lax.fori_loop(0, group // 128, find_begins, 0)

    def line_step(s, which=(0, 1)):
        for n in which:
            for p, valid, onward, forward in (
                (d - s, d - s >= 0, d < DP - 1, lambda n, p: line(n, p, d + 1)),
                (d + s, d + s < DP, d > 0, lambda n, p: line_down(n, p, d - 1)),
            ):
                @pl.when(valid)
                def _(n=n, p=p, onward=onward, forward=forward):
                    line(n, p, d).wait_recv()

                    @pl.when(onward)
                    def _():
                        forward(n, p).start()

                    pass_on(n, p)

    line_step(1)
    leave(2)
    line_step(2)
    pass_on(2, d)
    line_step(1, (2,))
    for copy, where, place in ((beside, other_rows, 0), (beyond, own_rows, 1), (corner, other_rows, 1)):
        copy.wait_recv()
        shared.append(
            post.send(normed_ref.at[where, columns(place)], normed_ref.at[where, columns(place + 2)], sibling)
        )
    line_step(3)
    line_step(2, (2,))
    start_relay(0)

    def arrived_blocks(n):
        keep(n).wait()
        for m in (1, 2, 3):
            pltpu.make_async_remote_copy(
                src_ref=block_of(n, 0), dst_ref=seat_of(n, 0),
                send_sem=send_sem.at[first_cols], recv_sem=recv_sem.at[first_cols + DP * n + m],
                device_id=(d, r, c), device_id_type=MESH,
            ).wait_recv()

    for copy in shared:
        copy.wait_recv()
    arrived_blocks(0)
    over_y(1).start()
    copy_out(normed_ref, normed_out)

    def turned(t):
        return lax.rem(t + 2 * r, group // TILE)

    def project_kv(t, total):
        part = pl.ds(pl.multiple_of(t * TILE, TILE), TILE)
        to = pl.ds(pl.multiple_of(REACH + turned(t) * TILE, TILE), TILE)
        kv_ref[to, :] = jnp.dot(
            normed_ref[part, :], weight_in[:, width:], preferred_element_type=F32
        ).astype(BF)
        return total

    lax.fori_loop(0, group // TILE, project_kv, 0)
    halo = post.ready(kv_ref.at[pl.ds(group, REACH), :], kv_ref.at[pl.ds(0, REACH), :], (lax.rem(d + 1, DP), r, c))

    @pl.when(d < DP - 1)
    def _():
        halo.start()

    arrived_blocks(1)

    def project_q(t, total):
        part = pl.ds(pl.multiple_of(t * TILE, TILE), TILE)
        to = pl.ds(pl.multiple_of(turned(t) * TILE, TILE), TILE)
        q_ref[to, :] = jnp.dot(
            normed_ref[part, :], weight_in[:, :width], preferred_element_type=F32
        ).astype(BF)
        return total

    lax.fori_loop(0, group // TILE, project_q, 0)

    copy_out(weight_in, weight_in_out)
    copy_out(q_ref, q_out)
    line_step(3, (2,))
    @pl.when(d == 0)
    def _():
        kv_ref[pl.ds(0, REACH), :] = jnp.zeros((REACH, 2 * width), BF)

    @pl.when(d > 0)
    def _():
        halo.wait_recv()

    copy_out(kv_ref, kv_out)

    grads = [
        post.ready(
            grad_all.at[pl.ds(0, half_rows), pl.ds(0, half)],
            grad_all.at[pl.ds(j * half_rows, half_rows), pl.ds(0, half)],
            (d ^ j, r, c),
        )
        for j in (1, 2, 3)
    ]
    grads_shared = [
        post.ready(
            grad_all.at[pl.ds(0, half_rows), pl.ds(0, half)],
            grad_all.at[pl.ds(0, half_rows), pl.ds(half, half)],
            sibling,
        )
    ]

    def spread_grads():
        grad_cross.wait_recv()
        grad_keep.wait()
        for copy in grads + grads_shared[:1]:
            copy.start()

    pl.when(d > 0)(spread_grads)

    span = TILE + REACH
    for h in range(width // HEAD_DIM):
        lanes = pl.ds(h * HEAD_DIM, HEAD_DIM)
        value_lanes = pl.ds(width + h * HEAD_DIM, HEAD_DIM)

        def one(t, total, lanes=lanes, value_lanes=value_lanes):
            part = pl.ds(pl.multiple_of(t * TILE, TILE), TILE)
            to = pl.ds(pl.multiple_of(turned(t) * TILE, TILE), TILE)
            window = pl.ds(pl.multiple_of(t * TILE, TILE), span)
            scores = scores_of(q_ref[part, lanes], kv_ref[window, lanes])
            query = lax.broadcasted_iota(jnp.int32, (TILE, span), 0)
            key = lax.broadcasted_iota(jnp.int32, (TILE, span), 1)
            begin = begin_ref[part, 0:1] + (REACH - t * TILE)
            allowed = (key <= query + REACH) & (key >= begin)
            scores = jnp.where(allowed, scores, NEG_FILL)
            highest = jnp.max(scores, axis=1, keepdims=True)
            expo = jnp.exp(scores - highest)
            total_e = jnp.sum(expo, axis=1, keepdims=True)
            probability = (expo * (1.0 / total_e)).astype(BF)
            att_ref[to, lanes] = jnp.dot(
                probability, kv_ref[window, value_lanes], preferred_element_type=F32
            ).astype(BF)
            lse_ref[part, lanes] = jnp.broadcast_to(highest + jnp.log(total_e), (TILE, HEAD_DIM))
            return total

        lax.fori_loop(0, group // TILE, one, 0)

    pl.when(d == 0)(spread_grads)

    copy_out(att_ref, att_out)
    copy_out(lse_ref, lse_out)
    arrived_blocks(2)
    copy_out(weight_out, weight_out_out)

    def out_given(t, total):
        part = pl.ds(pl.multiple_of(t * TILE, TILE), TILE)
        given[part, :] = jnp.dot(
            att_ref[part, :], weight_out[:, half:], preferred_element_type=F32
        ).astype(BF)
        return total

    lax.fori_loop(0, group // TILE, out_given, 0)
    to_sibling = post.send(given, arrived, sibling)

    def out_kept(t, total):
        part = pl.ds(pl.multiple_of(t * TILE, TILE), TILE)
        wide[part, :] = jnp.dot(att_ref[part, :], weight_out[:, :half], preferred_element_type=F32)
        return total

    lax.fori_loop(0, group // TILE, out_kept, 0)
    to_sibling.wait_recv()

    def add_low(t, total):
        part = pl.ds(pl.multiple_of(t * 128, 128), 128)
        value = wide[part, :] + arrived[part, :].astype(F32)
        wide[part, :] = value
        low[part, :] = value.astype(BF)
        return total

    lax.fori_loop(0, group // 128, add_low, 0)
    pieces, corners, pass_pieces = scatter_plane(
        post, lambda first, count, place: low.at[pl.ds(first, count), columns(place)], landed, rows, (d, r, c)
    )
    pieces = pieces + pass_pieces()
    start_relay(1)
    for copy in pieces:
        copy.wait_recv()

    def middle(t, total):
        part = pl.ds(pl.multiple_of(t * 128, 128), 128)
        value = (
            x32[part, :] + wide[part, 0:fc] + landed[0, part, :].astype(F32)
            + landed[1, part, :].astype(F32)
        )
        mid_ref[part, :] = value
        sums[4, :, part] = as_row(jnp.sum(value * value, axis=1, keepdims=True))
        return total

    lax.fori_loop(0, rows // 128, middle, 0)
    again = [post.send(sums.at[4], sums.at[4 + m], (d, r, c ^ m)) for m in (1, 2, 3)]
    for copy in again:
        copy.wait_recv()

    def norm_two(t, total):
        part = pl.ds(pl.multiple_of(t * 128, 128), 128)
        square = sums[4, :, part] + sums[6, :, part] + sums[5, :, part] + sums[7, :, part]
        scale = lax.rsqrt(as_column(square) / D + EPSILON)
        scale_ref[part, :] = scale
        n2_ref[part, :] = (mid_ref[part, :] * scale * gain_two_ref[...]).astype(BF)
        return total

    lax.fori_loop(0, rows // 128, norm_two, 0)

    for j, copy in zip((1, 2, 3), grads):
        copy.wait_recv()
        there = pl.ds(j * half_rows, half_rows)
        grads_shared.append(
            post.send(grad_all.at[there, pl.ds(0, half)], grad_all.at[there, pl.ds(half, half)], sibling)
        )
    for copy in grads_shared:
        copy.wait_recv()
    for n in (0, 1):
        over_y(n).wait_send()

        @pl.when(core == 0)
        def _(n=n):
            for i in (2, 3):
                relay(n, i).wait_send()

        @pl.when(core == 1)
        def _(n=n):
            for i in (2, 3):
                gate_came(n, i).wait_recv()

    for kind in (0, 1):
        over_x(kind).wait_send()

        @pl.when(core == 0)
        def _(kind=kind):
            keep_hidden(kind).wait()
            ship(kind, 0, 1, (d, r, c)).wait_recv()

        @pl.when(core == 1)
        def _(kind=kind):
            to_core(kind).wait_send()
            for i in (0, 1):
                ship(kind, 0, i, (d, r, c)).wait_recv()

    for copy in (
        small + [grad_cross, beside, beyond, corner] + shared + grads + grads_shared
        + [to_sibling] + pieces + corners + again
    ):
        copy.wait_send()

    @pl.when(d < DP - 1)
    def _():
        halo.wait_send()

    for copy in copies:
        copy.wait()
    for n in (0, 1, 2):
        for p in range(DP):
            @pl.when((d < DP - 1) & (p <= d))
            def _(n=n, p=p):
                line(n, p, d).wait_send()

            @pl.when((d > 0) & (p >= d))
            def _(n=n, p=p):
                line_down(n, p, d).wait_send()

            @pl.when(c != p)
            def _(n=n, p=p):
                to_column(n, p).wait_send()


SENDS = 104


def forward(x, gain_one, gain_two, lengths, query, key, value, out, gate, up, own_grad):
    rows, fc = x.shape
    group = 2 * rows
    width = out.shape[0]
    units = gate.shape[1]
    vmem = pl.BlockSpec(memory_space=pltpu.VMEM)
    smem = pl.BlockSpec(memory_space=pltpu.SMEM)
    hbm = pl.BlockSpec(memory_space=pl.ANY)

    def like(shape, dtype=BF):
        return jax.ShapeDtypeStruct(shape, dtype)

    return pl.pallas_call(
        forward_kernel,
        in_specs=[vmem] * 3 + [smem] + [vmem] * 4 + [hbm] * 3,
        out_specs=[vmem] * 5 + [hbm] * 11,
        out_shape=[
            like((rows, fc), F32),
            like((rows, 1), F32),
            like((rows, fc)),
            like((group, 1), jnp.int32),
            like((rows, 1), F32),
            like((group, D)),
            like((D, 3 * width)),
            like((width, D)),
            like((group, width)),
            like((REACH + group, 2 * width)),
            like((group, width)),
            like((group, width), F32),
            like((fc, units)),
            like((D, units)),
            like((D, units)),
            like((group, D)),
        ],
        scratch_shapes=[
            pltpu.VMEM((group, D), BF),
            pltpu.VMEM((D, 3 * width), BF),
            pltpu.VMEM((width, D), BF),
            pltpu.VMEM((group, width), BF),
            pltpu.VMEM((REACH + group, 2 * width), BF),
            pltpu.VMEM((group, width), BF),
            pltpu.VMEM((group, width), F32),
            pltpu.VMEM((2, fc, units), F32),
            pltpu.VMEM((DP, fc, 3 * width), BF),
            pltpu.VMEM((DP, width, fc), BF),
            pltpu.VMEM((8, 8, rows), F32),
            pltpu.VMEM((group, 2 * fc), F32),
            pltpu.VMEM((group, 2 * fc), BF),
            pltpu.VMEM((group, 2 * fc), BF),
            pltpu.VMEM((group, 2 * fc), BF),
            pltpu.VMEM((3, rows, fc), BF),
            pltpu.VMEM((rows, fc), F32),
            pltpu.VMEM((2, fc, units), BF),
            pltpu.SemaphoreType.DMA((SENDS,)),
            pltpu.SemaphoreType.DMA((SENDS,)),
            pltpu.SemaphoreType.DMA((20,)),
        ],
        compiler_params=pltpu.CompilerParams(
            collective_id=1, has_side_effects=True, vmem_limit_bytes=60 << 20
        ),
        cost_estimate=pl.CostEstimate(
            flops=6 * group * D * width, bytes_accessed=64 << 20, transcendentals=0
        ),
    )(x, gain_one, gain_two, lengths, query, key, value, out, gate, up, own_grad)


def at(t, size):
    return pl.ds(pl.multiple_of(t * size, size), size)


def loop(count, body):
    def one(t, total):
        body(t)
        return total

    lax.fori_loop(0, count, one, 0)


def maker(send_sem, recv_sem):
    def raw(src, dst, sent, got_at, target):
        return pltpu.make_async_remote_copy(
            src_ref=src, dst_ref=dst, send_sem=send_sem.at[sent], recv_sem=recv_sem.at[got_at],
            device_id=target, device_id_type=MESH,
        )

    return raw


class LineSum:
    def __init__(self, raw, arrays, base, me):
        self.raw, self.arrays, self.base, self.me = raw, arrays, base, me

    def sem(self, n, p, down):
        return self.base + 8 * n + 4 * down + p

    def take(self, p, down, done):
        d = self.me[0]
        for n, (z, got_z) in enumerate(self.arrays):
            self.raw(z.at[p], got_z.at[p], self.sem(n, p, down), self.sem(n, p, down), self.me).wait_recv()

        @pl.when(jnp.logical_not(done))
        def _():
            for z, got_z in self.arrays:
                def one(t, z=z, got_z=got_z):
                    z[p, at(t, 64), :] = (
                        z[p, at(t, 64), :].astype(F32) + got_z[p, at(t, 64), :].astype(F32)
                    ).astype(BF)

                loop(z.shape[1] // 64, one)

    def up(self, p):
        d, r, c = self.me

        @pl.when((d > 0) & (d <= p))
        def _():
            self.take(p, 0, d == p)

        @pl.when(d < p)
        def _():
            for n, (z, got_z) in enumerate(self.arrays):
                self.raw(z.at[p], got_z.at[p], self.sem(n, p, 0), self.sem(n, p, 0), (d + 1, r, c)).start()

    def down(self, p):
        d, r, c = self.me

        @pl.when((d < DP - 1) & (d >= p))
        def _():
            self.take(p, 1, d == p)

        @pl.when(d > p)
        def _():
            slot = jnp.where(p < d - 1, p, DP)
            for n, (z, got_z) in enumerate(self.arrays):
                self.raw(z.at[p], got_z.at[slot], self.sem(n, p, 1), self.sem(n, p, 1), (d - 1, r, c)).start()

    def begin(self):
        d = self.me[0]

        @pl.when(d == 0)
        def _():
            for p in (3, 2, 1):
                self.up(p)

        @pl.when(d == DP - 1)
        def _():
            for p in (0, 1, 2):
                self.down(p)

    def hop(self, n):
        d = self.me[0]

        @pl.when(d == 1)
        def _():
            self.up(DP - 1 - n)

        @pl.when(d == 2)
        def _():
            self.down(n)

    def first(self):
        self.hop(0)
        self.hop(1)

    def last(self):
        d = self.me[0]

        @pl.when(d == 0)
        def _():
            self.down(0)

        @pl.when(d == 1)
        def _():
            self.down(0)
            self.down(1)
            self.up(1)

        @pl.when(d == 2)
        def _():
            self.up(3)
            self.up(2)
            self.down(2)

        @pl.when(d == DP - 1)
        def _():
            self.up(3)

    def rest(self):
        self.first()
        self.last()

    def settle(self):
        d = self.me[0]
        for p in range(DP):
            for n, (z, got_z) in enumerate(self.arrays):
                for down, sent in ((0, d < p), (1, d > p)):
                    @pl.when(sent)
                    def _(p=p, n=n, z=z, got_z=got_z, down=down):
                        self.raw(
                            z.at[p], got_z.at[p], self.sem(n, p, down), self.sem(n, p, down), self.me
                        ).wait_send()

    def total(self, z, got_z, part):
        d = self.me[0]
        value = z[d, part, :].astype(F32)
        value = value + jnp.where(d > 0, got_z[d, part, :].astype(F32), 0.0)
        return value + jnp.where(d < DP - 1, got_z[DP, part, :].astype(F32), 0.0)


class PlaneSum:
    def __init__(self, raw, stage, got, comb, base, local_sem, local_base, me):
        self.raw, self.stage, self.got, self.comb, self.base = raw, stage, got, comb, base
        self.local_sem, self.local_base, self.me = local_sem, local_base, me
        self.kinds = range(stage.shape[0])

    def from_one(self, kind, i):
        d, r, c = self.me
        y = c // 2
        sent, base = self.base + 10 * kind + i, self.base + 10 * kind
        if i < 2:
            return self.raw(self.stage.at[kind, i], self.got.at[kind, 0], sent, base, (d, r ^ 1, 2 * y + 1 - i))
        return self.raw(
            self.stage.at[kind, i], self.comb.at[kind, 3 - i], sent, base + 3 + (3 - i), (d, r ^ 1, 2 * y)
        )

    def from_zero(self, kind, i):
        d, r, c = self.me
        sent, base = self.base + 10 * kind + i, self.base + 10 * kind
        if i == 1:
            return self.raw(self.stage.at[kind, i], self.got.at[kind, 1], sent, base + 1, (d, r, c ^ 1))
        return self.raw(
            self.stage.at[kind, i], self.got.at[kind, 2], sent, base + 2, (d, r, 2 * (1 - c // 2) + i - 2)
        )

    def home(self, kind):
        return pltpu.make_async_copy(
            self.stage.at[kind, 0], self.got.at[kind, 1], self.local_sem.at[self.local_base + kind]
        )

    def start_far(self):
        @pl.when(lax.rem(self.me[2], 2) == 1)
        def _():
            for i in (2, 3):
                for kind in self.kinds:
                    self.from_one(kind, i).start()

    def start_near(self):
        core = lax.rem(self.me[2], 2)

        @pl.when(core == 1)
        def _():
            for i in (0, 1):
                for kind in self.kinds:
                    self.from_one(kind, i).start()

        @pl.when(core == 0)
        def _():
            for kind in self.kinds:
                self.home(kind).start()
                self.from_zero(kind, 1).start()

    def combine(self, room, local_base):
        core = lax.rem(self.me[2], 2)

        @pl.when(core == 0)
        def _():
            for i in (2, 3):
                for kind in self.kinds:
                    self.raw(
                        self.stage.at[kind, i], self.comb.at[kind, i - 2], self.base,
                        self.base + 10 * kind + 3 + (i - 2), self.me,
                    ).wait_recv()
                    fetch = pltpu.make_async_copy(
                        self.comb.at[kind, i - 2], room(kind, i - 2),
                        self.local_sem.at[local_base + 2 * kind + i - 2],
                    )
                    fetch.start()
                    fetch.wait()

                    def add(t, kind=kind, i=i):
                        self.stage[kind, i, at(t, 64), :] = (
                            self.stage[kind, i, at(t, 64), :].astype(F32)
                            + room(kind, i - 2)[at(t, 64), :].astype(F32)
                        ).astype(BF)

                    loop(self.stage.shape[2] // 64, add)
                    self.from_zero(kind, i).start()

    def settle(self):
        core = lax.rem(self.me[2], 2)
        for kind in self.kinds:
            base = self.base + 10 * kind
            for n in (0, 2):
                self.raw(self.stage.at[kind, 0], self.got.at[kind, n], self.base, base + n, self.me).wait_recv()

            @pl.when(core == 1)
            def _(kind=kind, base=base):
                self.raw(self.stage.at[kind, 0], self.got.at[kind, 1], self.base, base + 1, self.me).wait_recv()
                for i in range(COL):
                    self.from_one(kind, i).wait_send()

            @pl.when(core == 0)
            def _(kind=kind):
                self.home(kind).wait()
                for i in (1, 2, 3):
                    self.from_zero(kind, i).wait_send()


def middle_kernel(
    n2_ref, mid_ref, scale_ref, gain_ref, own_grad, down_ref, own_up, gate_hbm, up_hbm, grad_hbm,
    grad_out, gain_out, got, comb, n2_out, dgate_out, dup_out,
    n2, dgate, dup, wg, wu, wd, gb, own_down, gate, up, du, hidden, given, arrived, z, got_z, crossing, crossed, gn, sums, stage,
    send_sem, recv_sem, local_sem,
):
    d, r, c = (lax.axis_index(name) for name in AXES)
    me = (d, r, c)
    y, core = c // 2, lax.rem(c, 2)
    rows, fc = n2_ref.shape
    block = rows // 2
    units = own_down.shape[0]
    half = 2 * fc
    over = (((0,), (0,)), ((), ()))
    across = (((1,), (1,)), ((), ()))
    post = Post(send_sem, recv_sem)
    raw = maker(send_sem, recv_sem)
    sibling = (d, r, c ^ 1)
    others = [(a, b) for a in (0, 1) for b in range(COL) if (a, b) != (0, 0)]
    greet([(d, r ^ a, c ^ b) for a, b in others] + [(d ^ j, r, c) for j in (1, 2, 3)])

    cross = post.send(
        n2_ref.at[pl.ds(pl.multiple_of((1 - y) * block, block), block), :],
        n2.at[pl.ds(0, block), pl.ds(fc, fc)],
        (d, r, c ^ 2),
    )
    def half_of(ref, i, n):
        return ref.at[pl.ds(pl.multiple_of(place_of(i) * fc + n * (fc // 2), fc // 2), fc // 2), :]

    def place_of(i):
        return lax.rem(i, 2) * 2 + i // 2

    first_wide = post.take(8)

    def up_over_y(n):
        return raw(
            own_up.at[pl.ds(n * (fc // 2), fc // 2), :], half_of(wu, 2 + core, n),
            first_wide + 4 * n, first_wide + 4 * n + core, (d, r, 2 * (1 - y)),
        )

    def up_relay(n, i):
        return raw(
            half_of(wu, i, n), half_of(wu, 5 - i, n), first_wide + 4 * n + i - 1,
            first_wide + 4 * n + 3 - i, (d, r ^ 1, 2 * y + 1),
        )

    def up_came(n, i):
        return raw(half_of(wu, i, n), half_of(wu, i, n), first_wide, first_wide + 4 * n + i - 2, me)

    for n in (0, 1):
        up_over_y(n).start()
    loads = [
        pltpu.make_async_copy(src, dst, local_sem.at[n])
        for n, (src, dst) in zip((0, 1, 2, 9), (
            (gate_hbm, wg),
            (up_hbm.at[pl.ds(0, fc), :], wu.at[pl.ds(0, fc), :]),
            (grad_hbm, gb),
            (up_hbm.at[pl.ds(2 * fc, fc), :], wu.at[pl.ds(2 * fc, fc), :]),
        ))
    ]
    for load in loads:
        load.start()

    def cast_down(t):
        own_down[at(t, 64), :] = down_ref[at(t, 64), :].astype(BF)

    loop(units // 64, cast_down)
    first_sent = post.take(10)

    def piece(ref, n):
        return ref.at[pl.ds(n * (units // 2), units // 2), :]

    def ship(n, way, i, target, src=None):
        return raw(
            piece(own_down if src is None else src, n), piece(wd.at[place_of(i)], n),
            first_sent + 5 * n + way, first_sent + 5 * n + i, target,
        )

    keep_down = pltpu.make_async_copy(own_down, wd.at[0], local_sem.at[3])

    def to_core(n):
        return ship(n, 0, 1, sibling)

    def over_y(n):
        return ship(n, 1, 2 + core, (d, r, 2 * (1 - y)))

    def over_x(n):
        return ship(n, 2, 1 - core, (d, r ^ 1, 2 * y + 1))

    def relay(n, i):
        return ship(n, i + 1, 5 - i, (d, r ^ 1, 2 * y + 1), wd.at[PLACE[i]])

    for n in (0, 1):
        over_x(n).start()
        over_y(n).start()

    @pl.when(core == 0)
    def _():
        keep_down.start()

    @pl.when(core == 1)
    def _():
        for n in (0, 1):
            to_core(n).start()

    def pass_down(n):
        @pl.when(core == 0)
        def _():
            for i in (2, 3):
                ship(n, 0, i, me).wait_recv()
                relay(n, i).start()

    n2[0:block, 0:fc] = n2_ref[pl.ds(pl.multiple_of(y * block, block), block), :]
    cross.wait_recv()

    first_up, first_down = post.take(DP), post.take(DP)
    first_shared = post.take(DP)

    def rail(p, e):
        return n2.at[at(p ^ e, block), pl.ds(0, half)]

    def go_up(p):
        return raw(rail(p, d), rail(p, d + 1), first_up + p, first_up + p, (d + 1, r, c))

    def go_down(p):
        return raw(rail(p, d), rail(p, d - 1), first_down + p, first_up + p, (d - 1, r, c))

    def share(p):
        return raw(
            rail(p, d), n2.at[at(p ^ d, block), pl.ds(half, half)], first_shared + p, first_shared + p, sibling
        )

    def onward(p):
        @pl.when((p <= d) & (d < DP - 1))
        def _():
            go_up(p).start()

        @pl.when((p >= d) & (d > 0))
        def _():
            go_down(p).start()

        share(p).start()

    def project(p):
        share(p).wait_recv()
        part = at(p ^ d, block)
        gate[part, :] = jnp.dot(n2[part, :], wg[...], preferred_element_type=F32)

    def project_up(t):
        part = at(t, block)
        up[part, :] = jnp.dot(n2[part, :], wu[...], preferred_element_type=F32)

    def pass_up(n):
        @pl.when(core == 0)
        def _():
            for i in (2, 3):
                up_came(n, i).wait_recv()
                up_relay(n, i).start()

    def hidden_grads(first, fresh):
        def one(t):
            part = at(t, block)
            value = jnp.zeros((block, units), F32) if fresh else du[part, :]
            for i in (first, first + 1):
                place = PLACE[i]
                value = value + lax.dot_general(
                    gb[part, place * fc : (place + 1) * fc], wd[place], across, preferred_element_type=F32
                )
            du[part, :] = value

        loop(DP, one)

    onward(d)
    turns = [
        d,
        jnp.where(d == 0, 1, d - 1),
        jnp.where(d < 2, 2, jnp.where(d == 2, 3, 1)),
        jnp.where(d < 2, 3, 0),
    ]
    inner = (d == 1) | (d == 2)

    def arrival(n):
        raw(rail(turns[n], d), rail(turns[n], d), first_up, first_up + turns[n], me).wait_recv()
        onward(turns[n])

    for load in loads:
        load.wait()
    arrival(1)

    @pl.when(inner)
    def _():
        arrival(2)

    pass_up(0)
    project(turns[0])
    pass_up(1)
    project(turns[1])

    @pl.when(jnp.logical_not(inner))
    def _():
        arrival(2)

    @pl.when(inner)
    def _():
        arrival(3)

    pass_down(0)
    project(turns[2])

    @pl.when(core == 0)
    def _():
        keep_down.wait()
        for n in (0, 1):
            ship(n, 0, 1, me).wait_recv()

    @pl.when(core == 1)
    def _():
        for n in (0, 1):
            for i in (0, 1):
                ship(n, 0, i, me).wait_recv()

    @pl.when(jnp.logical_not(inner))
    def _():
        arrival(3)

    hidden_grads(0, True)
    pass_down(1)
    project(turns[3])
    outs = [pltpu.make_async_copy(n2, n2_out, local_sem.at[0])]
    outs[0].start()

    @pl.when(core == 1)
    def _():
        for n in (0, 1):
            for i in (2, 3):
                up_came(n, i).wait_recv()

    loop(DP, project_up)

    def hidden_of(t):
        part = at(t, 64)
        g = gate[part, :]
        hidden[part, :] = (g * (1.0 / (1.0 + jnp.exp(-g))) * up[part, :]).astype(BF)

    loop(2 * rows // 64, hidden_of)

    def down_part(i):
        def down_grad(t):
            place = PLACE[i]
            stage[0, i, at(t, TILE), :] = lax.dot_general(
                hidden[:, at(t, TILE)], gb[:, place * fc : (place + 1) * fc], over, preferred_element_type=F32
            ).astype(BF)

        loop(units // TILE, down_grad)

    owners = PlaneSum(raw, stage, got, comb, post.take(10), local_sem, 4, me)
    down_part(2)
    down_part(3)

    @pl.when(core == 1)
    def _():
        for n in (0, 1):
            for i in (2, 3):
                ship(n, 0, i, me).wait_recv()

    hidden_grads(2, False)

    owners.start_far()

    def units_of(t):
        part = at(t, 64)
        g, u, grad = gate[part, :], up[part, :], du[part, :]
        sigmoid = 1.0 / (1.0 + jnp.exp(-g))
        silu = g * sigmoid
        dgate[part, :] = (grad * u * sigmoid * (1.0 + g * (1.0 - sigmoid))).astype(BF)
        dup[part, :] = (grad * silu).astype(BF)

    loop(2 * rows // 64, units_of)
    for n, (src, dst) in enumerate(((dgate, dgate_out), (dup, dup_out))):
        outs.append(pltpu.make_async_copy(src, dst, local_sem.at[1 + n]))
        outs[-1].start()

    def back(part, cols):
        return lax.dot_general(
            dgate[part, :], wg[cols, :], across, preferred_element_type=F32
        ) + lax.dot_general(dup[part, :], wu[cols, :], across, preferred_element_type=F32)

    line = LineSum(raw, ((z, got_z),), post.take(8), me)

    def plane_of(t):
        return jnp.where(d < DP // 2, DP - 1 - t, t)

    def to_sibling(t):
        part = at(plane_of(t) ^ d, block)
        return raw(given.at[part, :], arrived.at[part, :], first_given + t, first_given + t, sibling)

    def give(t):
        part = at(plane_of(t) ^ d, block)
        given[part, :] = back(part, slice(half, None)).astype(BF)
        to_sibling(t).start()

    def keep(t):
        p = plane_of(t)
        part = at(p ^ d, block)
        value = back(part, slice(0, half))
        to_sibling(t).wait_recv()
        z[p] = (value + arrived[part, :].astype(F32)).astype(BF)

        if t < DP - 1:
            @pl.when(d == 0)
            def _():
                line.up(DP - 1 - t)

            @pl.when(d == DP - 1)
            def _():
                line.down(t)

    first_given = post.take(DP)
    give(0)
    give(1)
    keep(0)
    give(2)
    keep(1)
    give(3)
    keep(2)
    down_part(0)
    down_part(1)
    owners.start_near()
    keep(3)

    def combine():
        owners.combine(lambda kind, j: wg.at[pl.ds(0, units), pl.ds(j * fc, fc)], 5)

    pl.when(jnp.logical_not(inner))(combine)
    line.hop(0)
    pl.when(inner)(combine)
    line.hop(1)
    line.last()

    def settle_rows(t):
        part = at(t, 64)
        total = line.total(z, got_z, part)
        gn[pl.ds(pl.multiple_of(y * block + t * 64, 64), 64), :] = total[:, 0:fc]
        crossing[part, :] = total[:, fc:].astype(BF)

    loop(block // 64, settle_rows)
    other = post.send(crossing, crossed, (d, r, c ^ 2))
    other.wait_recv()

    def other_rows(t):
        gn[pl.ds(pl.multiple_of((1 - y) * block + t * 64, 64), 64), :] = crossed[at(t, 64), :].astype(F32)

    loop(block // 64, other_rows)

    def inner_sum(t):
        part = at(t, 128)
        inner = gn[part, :] * gain_ref[...] * mid_ref[part, :]
        sums[0, :, part] = as_row(jnp.sum(inner, axis=1, keepdims=True))

    loop(rows // 128, inner_sum)
    small = [post.send(sums.at[0], sums.at[m], (d, r, c ^ m)) for m in (1, 2, 3)]

    def gain_sum(t, total):
        part = at(t, 128)
        value = gn[part, :] * mid_ref[part, :] * scale_ref[part, :]
        return total + jnp.sum(value, axis=0, keepdims=True)

    gain_out[...] = lax.fori_loop(0, rows // 128, gain_sum, jnp.zeros((1, fc), F32))
    for copy in small:
        copy.wait_recv()

    def finish(t):
        part = at(t, 128)
        inner = as_column(sums[0, :, part] + sums[2, :, part] + sums[1, :, part] + sums[3, :, part])
        scale = scale_ref[part, :]
        grad_out[part, :] = (
            own_grad[part, :].astype(F32) + scale * (gn[part, :] * gain_ref[...])
            - mid_ref[part, :] * (scale * scale * scale * inner / D)
        )

    loop(rows // 128, finish)

    owners.settle()
    line.settle()
    for copy in outs:
        copy.wait()
    for copy in [cross, other] + small:
        copy.wait_send()
    for t in range(DP):
        to_sibling(t).wait_send()
    for n in (0, 1):
        over_y(n).wait_send()
        over_x(n).wait_send()
        up_over_y(n).wait_send()

        @pl.when(core == 0)
        def _(n=n):
            for i in (2, 3):
                relay(n, i).wait_send()
                up_relay(n, i).wait_send()

        @pl.when(core == 1)
        def _(n=n):
            to_core(n).wait_send()

    for p in range(DP):
        share(p).wait_send()

        @pl.when((p <= d) & (d < DP - 1))
        def _(p=p):
            go_up(p).wait_send()

        @pl.when((p >= d) & (d > 0))
        def _(p=p):
            go_down(p).wait_send()


def middle(n2, mid, scale, gain, own_grad, down, own_up, gate, up, grad_all):
    rows, fc = n2.shape
    group = 2 * rows
    block = rows // 2
    units = down.shape[0]
    vmem = pl.BlockSpec(memory_space=pltpu.VMEM)
    hbm = pl.BlockSpec(memory_space=pl.ANY)

    def like(shape, dtype=BF):
        return jax.ShapeDtypeStruct(shape, dtype)

    return pl.pallas_call(
        middle_kernel,
        in_specs=[vmem] * 6 + [hbm] * 4,
        out_specs=[vmem] * 2 + [hbm] * 5,
        out_shape=[
            like((rows, fc), F32),
            like((1, fc), F32),
            like((1, 3, units, fc)),
            like((1, 2, units, fc)),
            like((group, D)),
            like((group, units)),
            like((group, units)),
        ],
        scratch_shapes=[
            pltpu.VMEM((group, D), BF),
            pltpu.VMEM((group, units), BF),
            pltpu.VMEM((group, units), BF),
            pltpu.VMEM((D, units), BF),
            pltpu.VMEM((D, units), BF),
            pltpu.VMEM((COL, units, fc), BF),
            pltpu.VMEM((group, D), BF),
            pltpu.VMEM((units, fc), BF),
            pltpu.VMEM((group, units), F32),
            pltpu.VMEM((group, units), F32),
            pltpu.VMEM((group, units), F32),
            pltpu.VMEM((group, units), BF),
            pltpu.VMEM((group, 2 * fc), BF),
            pltpu.VMEM((group, 2 * fc), BF),
            pltpu.VMEM((DP, block, 2 * fc), BF),
            pltpu.VMEM((DP + 1, block, 2 * fc), BF),
            pltpu.VMEM((block, fc), BF),
            pltpu.VMEM((block, fc), BF),
            pltpu.VMEM((rows, fc), F32),
            pltpu.VMEM((4, 8, rows), F32),
            pltpu.VMEM((1, COL, units, fc), BF),
            pltpu.SemaphoreType.DMA((SENDS,)),
            pltpu.SemaphoreType.DMA((SENDS,)),
            pltpu.SemaphoreType.DMA((12,)),
        ],
        compiler_params=pltpu.CompilerParams(
            collective_id=3, has_side_effects=True, vmem_limit_bytes=62 << 20
        ),
        cost_estimate=pl.CostEstimate(
            flops=14 * group * D * units, bytes_accessed=48 << 20, transcendentals=group * units
        ),
    )(n2, mid, scale, gain, own_grad, down, own_up, gate, up, grad_all)


POSTS = 112


def backward_kernel(
    x_ref, gain_ref, scale_ref, mid_ref, gain_two_ref, begin_ref, weight_in_hbm, weight_out_hbm, q_hbm, kv_hbm,
    att_hbm, lse_hbm, normed_hbm, n2_hbm, dgate_hbm, dup_hbm,
    tokens_out, query_out, key_out, value_out, out_out, gains_out, got, comb,
    weight_in, weight_out, q_ref, kv_ref, att_ref, lse_ref, n1, n2, dgu, dball, dotted, dproj, acc, spill, spilled, stage, own_f, arrived, landed,
    zq, zo, zkv, rq, ro, rkv, sums, gsum,
    send_sem, recv_sem, local_sem,
):
    d, r, c = (lax.axis_index(name) for name in AXES)
    y, core = c // 2, lax.rem(c, 2)
    rows, fc = x_ref.shape
    group = 2 * rows
    width = q_hbm.shape[1]
    units = dgate_hbm.shape[1]
    half = 2 * fc
    tiles = group // TILE
    over = (((0,), (0,)), ((), ()))
    across = (((1,), (1,)), ((), ()))
    post = Post(send_sem, recv_sem)
    loads = [
        pltpu.make_async_copy(src, dst, local_sem.at[8 + n])
        for n, (src, dst) in enumerate((
            (n2_hbm, n2),
            (dgate_hbm, dgu.at[pl.ds(0, group), :]),
            (dup_hbm, dgu.at[pl.ds(group, group), :]),
            (normed_hbm, n1),
            (weight_out_hbm, weight_out),
            (att_hbm, att_ref),
            (q_hbm, q_ref),
            (kv_hbm, kv_ref),
            (lse_hbm, lse_ref),
            (weight_in_hbm, weight_in),
        ))
    ]
    for load in loads:
        load.start()

    others = [(a, b) for a in (0, 1) for b in range(COL) if (a, b) != (0, 0)]
    greet(
        [(d, r ^ a, c ^ b) for a, b in others]
        + [(d ^ j, r ^ a, c) for j in (1, 2, 3) for a in (0, 1)]
    )

    def columns(place):
        return pl.ds(place * fc, fc)

    def turned(t):
        return lax.rem(t + 2 * r, tiles)

    raw = maker(send_sem, recv_sem)
    me = (d, r, c)
    sibling = (d, r, c ^ 1)
    own_rows, other_rows = pl.ds(0, rows), pl.ds(rows, rows)
    def round_mid(t):
        dball[at(t, 128), 0:fc] = mid_ref[at(t, 128), :].astype(BF)

    loop(rows // 128, round_mid)
    own_block = dball.at[own_rows, columns(0)]
    beside = post.send(own_block, dball.at[other_rows, columns(0)], (d, r ^ 1, c))
    beyond = post.send(own_block, dball.at[own_rows, columns(1)], (d, r, c ^ 2))
    shared = [post.send(own_block, dball.at[own_rows, columns(2)], sibling)]

    for load in loads[:3]:
        load.wait()
    owners = PlaneSum(raw, stage, got, comb, post.take(20), local_sem, 4, me)

    def hidden_part(i):
        for kind in (0, 1):
            def hidden_grad(t, kind=kind):
                left = n2[:, pl.ds(pl.multiple_of(PLACE[i] * fc + t * TILE, TILE), TILE)]
                stage[kind, i, at(t, TILE), :] = lax.dot_general(
                    left, dgu[pl.ds(kind * group, group), :], over, preferred_element_type=F32
                ).astype(BF)

            loop(fc // TILE, hidden_grad)

    hidden_part(2)
    hidden_part(3)
    for load in loads[3:]:
        load.wait()

    upper = pl.ds(rows, rows // 2)
    beside.wait_recv()
    corner = [post.send(dball.at[upper, columns(0)], dball.at[upper, columns(1)], (d, r, c ^ 2))]
    shared.append(post.send(dball.at[other_rows, columns(0)], dball.at[other_rows, columns(2)], sibling))
    beyond.wait_recv()
    corner.append(post.send(
        dball.at[pl.ds(rows // 2, rows // 2), columns(1)],
        dball.at[pl.ds(rows + rows // 2, rows // 2), columns(1)], (d, r ^ 1, c),
    ))
    shared.append(post.send(dball.at[own_rows, columns(1)], dball.at[own_rows, columns(3)], sibling))
    owners.start_far()
    hidden_part(0)
    hidden_part(1)
    for copy in corner:
        copy.wait_recv()
    shared.append(post.send(dball.at[other_rows, columns(1)], dball.at[other_rows, columns(3)], sibling))
    for copy in shared:
        copy.wait_recv()

    def head_grad(t):
        dotted[at(turned(t), TILE), :] = lax.dot_general(
            dball[at(t, TILE), :], weight_out[...], across, preferred_element_type=F32
        ).astype(BF)

    loop(tiles, head_grad)

    sent_out = [None] + [post.take(1) for _ in (1, 2, 3)]
    outs = []
    for place, m in enumerate((0, 2, 1, 3)):
        value = lax.dot_general(
            att_ref[...], dball[:, place * fc : (place + 1) * fc], over, preferred_element_type=F32
        ).astype(BF)
        if m == 0:
            zo[c] = value
        else:
            n2[(m - 1) * width : m * width, half : half + fc] = value
            staged = n2.at[pl.ds((m - 1) * width, width), pl.ds(half, fc)]
            copy = raw(staged, zo.at[c], sent_out[m], sent_out[m], (d, r, c ^ m))
            copy.start()
            outs.append(copy)

    span = TILE + REACH
    scale = HEAD_DIM ** (-0.5)
    spills = []
    for h in range(width // HEAD_DIM):
        lanes = pl.ds(h * HEAD_DIM, HEAD_DIM)
        value_lanes = pl.ds(width + h * HEAD_DIM, HEAD_DIM)

        def clear(t, lanes=lanes, value_lanes=value_lanes):
            acc[at(t, TILE), lanes] = jnp.zeros((TILE, HEAD_DIM), F32)
            acc[at(t, TILE), value_lanes] = jnp.zeros((TILE, HEAD_DIM), F32)

        loop((group + REACH) // TILE, clear)

        def one(t, lanes=lanes, value_lanes=value_lanes):
            part = at(t, TILE)
            window = pl.ds(pl.multiple_of(t * TILE, TILE), span)
            query, key = q_ref[part, lanes], kv_ref[window, lanes]
            grad = dotted[part, lanes]
            scores = scores_of(query, key)
            query_at = lax.broadcasted_iota(jnp.int32, (TILE, span), 0)
            key_at = lax.broadcasted_iota(jnp.int32, (TILE, span), 1)
            begin = begin_ref[part, 0:1] + (REACH - t * TILE)
            allowed = (key_at <= query_at + REACH) & (key_at >= begin)
            scores = jnp.where(allowed, scores - lse_ref[part, lanes][:, 0:1], NEG_FILL)
            probability = jnp.exp(scores)
            grad_soft = lax.dot_general(grad, kv_ref[window, value_lanes], across, preferred_element_type=F32)
            inner = jnp.sum(probability * grad_soft, axis=1, keepdims=True)
            grad_scores = (probability * (grad_soft - inner)).astype(BF)
            dproj[at(turned(t), TILE), lanes] = (
                jnp.dot(grad_scores, key, preferred_element_type=F32) * scale
            ).astype(BF)
            acc[window, lanes] += lax.dot_general(grad_scores, query, over, preferred_element_type=F32) * scale
            acc[window, value_lanes] += lax.dot_general(
                probability.astype(BF), grad, over, preferred_element_type=F32
            )

        loop(tiles, one)

        def round_spill(t, h=h, lanes=lanes, value_lanes=value_lanes):
            spill[h, at(t, TILE), 0:HEAD_DIM] = acc[at(t, TILE), lanes].astype(BF)
            spill[h, at(t, TILE), HEAD_DIM:] = acc[at(t, TILE), value_lanes].astype(BF)

        loop(REACH // TILE, round_spill)
        copy = post.ready(spill.at[h], spilled.at[h], (lax.rem(d + DP - 1, DP), r, c))
        spills.append(copy)

        @pl.when(d > 0)
        def _(copy=copy):
            copy.start()

    def attention_grads(first_lane, lane_count, dest):
        lanes = slice(first_lane, first_lane + lane_count)
        slots = [None] + [post.take(1) for _ in (1, 2, 3)]
        copies = []
        for place, m in enumerate((0, 2, 1, 3)):
            def tile(t, place=place, m=m):
                left = n1[:, pl.ds(pl.multiple_of(place * fc + t * TILE, TILE), TILE)]
                value = lax.dot_general(left, dproj[:, lanes], over, preferred_element_type=F32).astype(BF)
                if m == 0:
                    dest[c, at(t, TILE), :] = value
                else:
                    dgu[pl.ds(pl.multiple_of(place * fc + t * TILE, TILE), TILE), lanes] = value

            loop(fc // TILE, tile)
            if m:
                copy = raw(
                    dgu.at[pl.ds(place * fc, fc), pl.ds(first_lane, lane_count)], dest.at[c],
                    slots[m], slots[m], (d, r, c ^ m),
                )
                copy.start()
                copies.append(copy)
        return copies

    qs = attention_grads(0, width, zq)

    @pl.when(d < DP - 1)
    def _():
        for copy in spills:
            copy.wait_recv()

    @pl.when(d == DP - 1)
    def _():
        spilled[...] = jnp.zeros_like(spilled)

    for h in range(width // HEAD_DIM):
        for which in (0, 1):
            lanes = pl.ds(which * width + h * HEAD_DIM, HEAD_DIM)
            out_lanes = pl.ds((1 + which) * width + h * HEAD_DIM, HEAD_DIM)

            def whole(t, h=h, which=which, lanes=lanes, out_lanes=out_lanes):
                total = acc[pl.ds(pl.multiple_of(REACH + t * TILE, TILE), TILE), lanes]
                extra = spilled[
                    h, at(jnp.maximum(t - 1, 0), TILE), which * HEAD_DIM : (which + 1) * HEAD_DIM
                ].astype(F32)
                total = total + jnp.where(t > 0, extra, 0.0)
                dproj[at(turned(t), TILE), out_lanes] = total.astype(BF)

            loop(tiles, whole)

    kvs = attention_grads(width, 2 * width, zkv)
    for copy in outs + qs:
        copy.wait_recv()
    first_line = post.take(24)
    line_a = LineSum(raw, ((zq, rq), (zo, ro)), first_line, me)
    line_b = LineSum(raw, ((zkv, rkv),), first_line + 16, me)
    line_a.begin()

    def given_part(t):
        n2[at(t, TILE), 0:half] = lax.dot_general(
            dproj[at(t, TILE), :], weight_in[half:, :], across, preferred_element_type=F32
        ).astype(BF)

    loop(tiles, given_part)
    to_sibling = post.send(n2.at[:, pl.ds(0, half)], arrived, sibling)

    to_sibling.wait_recv()
    for copy in outs:
        copy.wait_send()

    def kept_part(t):
        part = at(t, TILE)
        value = lax.dot_general(
            dproj[part, :], weight_in[:half, :], across, preferred_element_type=F32
        ) + arrived[part, :].astype(F32)
        n2[part, half:] = value.astype(BF)

        @pl.when(t < rows // TILE)
        def _():
            own_f[part, :] = value[:, 0:fc]

    loop(tiles, kept_part)

    pieces, corners, pass_pieces = scatter_plane(
        post, lambda first, count, place: n2.at[pl.ds(first, count), pl.ds(half + place * fc, fc)], landed, rows, me
    )

    def finish(line, z, got_z, dests):
        def one(t):
            value = line.total(z, got_z, at(t, 64))
            for dest, lanes in dests:
                dest[at(t, 64), :] = value[:, lanes]

        loop(z.shape[1] // 64, one)

    line_a.first()
    pieces = pieces + pass_pieces()
    owners.start_near()
    for copy in kvs:
        copy.wait_recv()
    line_b.begin()
    line_a.last()

    for copy in pieces:
        copy.wait_recv()

    def inner_sum(t):
        part = at(t, 128)
        value = own_f[part, :]
        for n in range(2):
            value = value + landed[n, part, :].astype(F32)
        own_f[part, :] = value
        inner = value * gain_ref[...] * x_ref[part, :].astype(F32)
        sums[0, :, part] = as_row(jnp.sum(inner, axis=1, keepdims=True))

    loop(rows // 128, inner_sum)
    small = [post.send(sums.at[0], sums.at[m], (d, r, c ^ m)) for m in (1, 2, 3)]
    seat = ROW * d + r
    gain_part = jnp.zeros((1, fc), F32)

    def gain_sum(t, total):
        part = at(t, 128)
        value = own_f[part, :] * x_ref[part, :].astype(F32) * scale_ref[part, :]
        return total + jnp.sum(value, axis=0, keepdims=True)

    gain_part = lax.fori_loop(0, rows // 128, gain_sum, gain_part)
    gsum[seat, 0:1, :] = gain_part
    gsum[seat, 1:2, :] = gain_two_ref[...]
    gsum[seat, 2:8, :] = jnp.zeros((6, fc), F32)
    gain_sent = post.take(8)
    gain_got = gain_sent

    def gain_copy(n, j, a):
        return raw(gsum.at[seat], gsum.at[seat], gain_sent + n, gain_got + seat, (d ^ j, r ^ a, c))

    far = [(j, a) for j in range(DP) for a in (0, 1) if (j, a) != (0, 0)]
    for n, (j, a) in enumerate(far):
        gain_copy(n, j, a).start()
    owners.combine(lambda kind, j: n1.at[pl.ds(j * fc, fc), pl.ds(kind * units, units)], 0)


    line_b.rest()
    finish(line_a, zq, rq, ((query_out, slice(None)),))
    finish(line_a, zo, ro, ((out_out, slice(None)),))
    finish(line_b, zkv, rkv, ((key_out, slice(0, width)), (value_out, slice(width, None))))
    for copy in small:
        copy.wait_recv()

    def finish_tokens(t):
        part = at(t, 128)
        inner = as_column(sums[0, :, part] + sums[2, :, part] + sums[1, :, part] + sums[3, :, part])
        scale_rows = scale_ref[part, :]
        value = x_ref[part, :].astype(F32)
        tokens_out[part, :] = (
            mid_ref[part, :] + scale_rows * (own_f[part, :] * gain_ref[...])
            - value * (scale_rows * scale_rows * scale_rows * inner / D)
        )

    loop(rows // 128, finish_tokens)

    for e in range(2 * DP):
        @pl.when(e != seat)
        def _(e=e):
            raw(gsum.at[e], gsum.at[e], gain_sent, gain_got + e, me).wait_recv()

    gains = gsum[0]
    for e in range(1, 2 * DP):
        gains = gains + gsum[e]
    gains_out[...] = gains

    owners.settle()
    line_a.settle()
    line_b.settle()
    for copy in [beside, beyond] + corner + shared + qs + kvs + [to_sibling] + pieces + corners + small:
        copy.wait_send()
    for n, (j, a) in enumerate(far):
        gain_copy(n, j, a).wait_send()

    @pl.when(d > 0)
    def _():
        for copy in spills:
            copy.wait_send()


def backward(x, gain, scale, mid, gain_two, weight_in, weight_out, q, kv, att, lse, begin, normed, n2, dgate, dup):
    rows, fc = x.shape
    group = 2 * rows
    width = q.shape[1]
    units = dgate.shape[1]
    vmem = pl.BlockSpec(memory_space=pltpu.VMEM)
    hbm = pl.BlockSpec(memory_space=pl.ANY)

    def like(shape, dtype=BF):
        return jax.ShapeDtypeStruct(shape, dtype)

    return pl.pallas_call(
        backward_kernel,
        in_specs=[vmem] * 6 + [hbm] * 10,
        out_specs=[vmem] * 6 + [hbm] * 2,
        out_shape=[
            like((rows, fc), F32),
            like((fc, width), F32),
            like((fc, width), F32),
            like((fc, width), F32),
            like((width, fc), F32),
            like((8, fc), F32),
            like((2, 3, fc, units)),
            like((2, 2, fc, units)),
        ],
        scratch_shapes=[
            pltpu.VMEM((D, 3 * width), BF),
            pltpu.VMEM((width, D), BF),
            pltpu.VMEM((group, width), BF),
            pltpu.VMEM((REACH + group, 2 * width), BF),
            pltpu.VMEM((group, width), BF),
            pltpu.VMEM((group, width), F32),
            pltpu.VMEM((group, D), BF),
            pltpu.VMEM((group, D), BF),
            pltpu.VMEM((2 * group, units), BF),
            pltpu.VMEM((group, D), BF),
            pltpu.VMEM((group, width), BF),
            pltpu.VMEM((group, 3 * width), BF),
            pltpu.VMEM((group + REACH, 2 * width), F32),
            pltpu.VMEM((width // HEAD_DIM, REACH, 2 * HEAD_DIM), BF),
            pltpu.VMEM((width // HEAD_DIM, REACH, 2 * HEAD_DIM), BF),
            pltpu.VMEM((2, COL, fc, units), BF),
            pltpu.VMEM((rows, fc), F32),
            pltpu.VMEM((group, 2 * fc), BF),
            pltpu.VMEM((3, rows, fc), BF),
            pltpu.VMEM((DP, fc, width), BF),
            pltpu.VMEM((DP, width, fc), BF),
            pltpu.VMEM((DP, fc, 2 * width), BF),
            pltpu.VMEM((DP + 1, fc, width), BF),
            pltpu.VMEM((DP + 1, width, fc), BF),
            pltpu.VMEM((DP + 1, fc, 2 * width), BF),
            pltpu.VMEM((4, 8, rows), F32),
            pltpu.VMEM((2 * DP, 8, fc), F32),
            pltpu.SemaphoreType.DMA((POSTS,)),
            pltpu.SemaphoreType.DMA((POSTS,)),
            pltpu.SemaphoreType.DMA((20,)),
        ],
        compiler_params=pltpu.CompilerParams(
            collective_id=2, has_side_effects=True, vmem_limit_bytes=62 << 20
        ),
        cost_estimate=pl.CostEstimate(
            flops=12 * group * D * width + 4 * group * D * units, bytes_accessed=64 << 20, transcendentals=0
        ),
    )(x, gain, scale, mid, gain_two, begin, weight_in, weight_out, q, kv, att, lse, normed, n2, dgate, dup)


def closing_kernel(
    tokens, query, key, value, out, hidden, down, gains,
    tokens_out, query_out, key_out, value_out, out_out, gate_out, up_out, down_out, one_out, two_out,
):
    for src, dst in (
        (tokens, tokens_out), (query, query_out), (key, key_out), (value, value_out), (out, out_out)
    ):
        dst[...] = src[...]
    for dst, kind in ((gate_out, 0), (up_out, 1)):
        dst[...] = hidden[kind, 0].astype(F32) + hidden[kind, 1].astype(F32) + hidden[kind, 2].astype(F32)
    one_out[...] = gains[0]
    two_out[...] = gains[1]
    down_out[...] = down[0, 0].astype(F32) + down[0, 1].astype(F32) + down[0, 2].astype(F32)


def closing(tokens, query, key, value, out, hidden, down, gains):
    steps = 4

    def rows_of(array):
        rows, width = array.shape[-2:]
        lead = array.shape[:-2]
        return pl.BlockSpec(lead + (rows // steps, width), lambda t: (0,) * len(lead) + (t, 0))

    finals = [tokens, query, key, value, out] + [
        jax.ShapeDtypeStruct(a.shape[-2:], F32) for a in (hidden, hidden, down)
    ]
    return pl.pallas_call(
        closing_kernel,
        grid=(steps,),
        in_specs=[rows_of(a) for a in (tokens, query, key, value, out, hidden, down)]
        + [pl.BlockSpec(gains.shape, lambda t: (0, 0))],
        out_specs=[rows_of(a) for a in finals] + [pl.BlockSpec(gains.shape[1:], lambda t: (0,))] * 2,
        out_shape=[jax.ShapeDtypeStruct(a.shape, F32) for a in finals]
        + [jax.ShapeDtypeStruct(gains.shape[1:], F32)] * 2,
        compiler_params=pltpu.CompilerParams(vmem_limit_bytes=62 << 20),
    )(tokens, query, key, value, out, hidden, down, gains)


def on_small_mesh(
    tokens,
    cotangent,
    query_master,
    key_master,
    value_master,
    out_master,
    gate_master,
    up_master,
    down_master,
    attn_gain,
    ffn_gain,
    lengths,
    permutation,
):
    del permutation
    (
        mid, scale_two, n2, begin, scale_one, normed_one, weight_in, weight_out, q, key_value,
        own_attended, lse, own_up, weight_gate, weight_up, grad_all,
    ) = forward(
        tokens, attn_gain[None, :], ffn_gain[None, :], lengths, query_master, key_master,
        value_master, out_master, gate_master, up_master, cotangent,
    )
    grad_mid, gain_two_part, got_down, _, normed_two, grad_gate, grad_up = middle(
        n2, mid, scale_two, ffn_gain[None, :], cotangent, down_master, own_up, weight_gate,
        weight_up, grad_all,
    )
    grad_tokens, grad_query, grad_key, grad_value, grad_out, gains, got, _ = backward(
        tokens, attn_gain[None, :], scale_one, grad_mid, gain_two_part, weight_in, weight_out, q,
        key_value, own_attended, lse, begin, normed_one, normed_two, grad_gate, grad_up,
    )
    return closing(grad_tokens, grad_query, grad_key, grad_value, grad_out, got, got_down, gains)


def solution(mesh):
    placed = (
        P(("dp", "row"), "col"),
        P(("dp", "row"), "col"),
        P("col", ("row", "dp")),
        P("col", ("row", "dp")),
        P("col", ("row", "dp")),
        P(("row", "dp"), "col"),
        P("col", ("row", "dp")),
        P("col", ("row", "dp")),
        P(("row", "dp"), "col"),
        P("col"),
        P("col"),
        P(),
        P(),
    )
    small = tuple(mesh.shape[name] for name in AXES) == (DP, ROW, COL)
    return jax.shard_map(
        on_small_mesh if small else on_any_mesh,
        mesh=mesh,
        in_specs=placed,
        out_specs=(
            P(("dp", "row"), "col"),
            P("col", ("row", "dp")),
            P("col", ("row", "dp")),
            P("col", ("row", "dp")),
            P(("row", "dp"), "col"),
            P("col", ("row", "dp")),
            P("col", ("row", "dp")),
            P(("row", "dp"), "col"),
            P("col"),
            P("col"),
        ),
        check_vma=False,
    )
```

```python
import functools

import jax
import jax.numpy as jnp
from jax import lax
from jax.experimental import pallas as pl
from jax.experimental.pallas import tpu as pltpu
from jax.sharding import PartitionSpec as P

D = 2048
HEAD_DIM = 128


EPSILON = 1e-06
NEG_FILL = -1e30
AXES = ("dp", "row", "col")
DP, ROW, COL = 4, 2, 4
REACH = 768
BF = jnp.bfloat16
F32 = jnp.float32


def running_sum(lengths):
    count = lengths.shape[0]
    earlier = jnp.arange(count)[:, None] <= jnp.arange(count)[None, :]
    return jnp.sum(jnp.where(earlier, lengths[:, None], 0), axis=0)

def make_picker(wanted, carried, pieces):
    amount = pieces[0].shape[0]
    inside = (wanted >= 0) & (wanted < amount)
    chosen = jnp.clip(wanted, 0, amount - 1)
    return tuple(
        (
            jnp.where(inside[:, None], jnp.take(shard_rows, chosen, axis=0), current)
            for shard_rows, current in zip(pieces, carried)
        )
    )


def sequence_marks(permutation, lengths, first_slot, amount):
    source = lax.dynamic_slice_in_dim(permutation, first_slot, amount)
    seq_ends = running_sum(lengths)
    passed = seq_ends[None, :] <= source[:, None]
    member = jnp.sum(passed.astype(jnp.int32), axis=1)
    begins = jnp.max(jnp.where(passed, seq_ends[None, :], 0), axis=1)
    return (member, source - begins)


def col_total(values):
    return lax.psum(jnp.sum(values, axis=1), "col")


def row_gather(values):
    return lax.all_gather(values, "row", axis=0, tiled=True)


def col_gather(values):
    return lax.all_gather(values, "col", axis=0, tiled=True)


def key_gather(keys_here, values_here):
    return (
        lax.all_gather(keys_here, "col", axis=0, tiled=True),
        lax.all_gather(values_here, "col", axis=0, tiled=True),
    )


def multiply(row_block, weight, transpose_right):
    if transpose_right:
        return lax.dot_general(
            row_block, weight, (((1,), (1,)), ((), ())), preferred_element_type=jnp.float32
        )
    return jnp.dot(row_block, weight, preferred_element_type=jnp.float32)


def outer_sum(left_rows, right_rows):
    return lax.dot_general(
        left_rows, right_rows, (((0,), (0,)), ((), ())), preferred_element_type=jnp.float32
    )


def col_reduce(spread, weight, transpose_right):
    return lax.psum_scatter(
        multiply(spread, weight, transpose_right), "col", scatter_dimension=0, tiled=True
    )


def row_reduce(spread, weight, transpose_right):
    return lax.psum_scatter(
        multiply(spread, weight, transpose_right), "row", scatter_dimension=0, tiled=True
    )


def visible(query_member, query_position, member, position):
    same = query_member[:, None] == member[None, :]
    behind = position[None, :] <= query_position[:, None]
    return same & behind


def attend_scores(query_block, key_all, allowed):
    scores = jnp.einsum(
        "qhd,khd->hqk", query_block, key_all, preferred_element_type=jnp.float32
    ) * HEAD_DIM ** (-0.5)
    return jnp.where(allowed[None, :, :], scores, NEG_FILL)


def norm_back(grad_normed, inputs_f, scale_rows, gain):
    gain_part = jnp.sum(grad_normed * inputs_f * scale_rows[:, None], axis=0)
    scaled = grad_normed * gain[None, :]
    inner = col_total(scaled * inputs_f)
    grad_inputs = scale_rows[:, None] * scaled - inputs_f * (scale_rows**3 * inner / D)[:, None]
    return (grad_inputs, gain_part)


def on_any_mesh(
    tokens,
    cotangent,
    query_master,
    key_master,
    value_master,
    out_master,
    gate_master,
    up_master,
    down_master,
    attn_gain,
    ffn_gain,
    lengths,
    permutation,
):
    own_rows = tokens.shape[0]
    group_rows = own_rows * lax.axis_size("row")
    quarter = group_rows // lax.axis_size("col")
    device_slot = lax.axis_index(("dp", "row"))
    group_slot = lax.axis_index("dp")
    col_slot = lax.axis_index("col")
    own_sources = lax.dynamic_slice_in_dim(permutation, device_slot * own_rows, own_rows)
    own_tokens, own_cotangent = make_picker(
        own_sources,
        (jnp.zeros_like(tokens), jnp.zeros_like(cotangent)),
        (
            lax.all_gather(tokens, ("dp", "row"), axis=0, tiled=True),
            lax.all_gather(cotangent, ("dp", "row"), axis=0, tiled=True),
        ),
    )
    masters = tuple(
        (
            matrix.astype(jnp.bfloat16)
            for matrix in (
                query_master,
                key_master,
                value_master,
                out_master,
                gate_master,
                up_master,
                down_master,
            )
        )
    )
    query_weight, key_weight, value_weight, out_weight, gate_weight, up_weight, down_weight = (
        lax.all_gather(masters[0], "dp", axis=1, tiled=True),
        lax.all_gather(masters[1], "dp", axis=1, tiled=True),
        lax.all_gather(masters[2], "dp", axis=1, tiled=True),
        lax.all_gather(masters[3], "dp", axis=0, tiled=True),
        lax.all_gather(masters[4], "dp", axis=1, tiled=True),
        lax.all_gather(masters[5], "dp", axis=1, tiled=True),
        lax.all_gather(masters[6], "dp", axis=0, tiled=True),
    )
    attention_in = jnp.concatenate([query_weight, key_weight, value_weight], axis=1)
    feedforward_in = jnp.concatenate([gate_weight, up_weight], axis=1)
    width_row = query_weight.shape[1]
    heads_row = width_row // HEAD_DIM
    hidden_row = gate_weight.shape[1]
    member, position = sequence_marks(permutation, lengths, group_slot * group_rows, group_rows)
    query_member = lax.dynamic_slice_in_dim(member, col_slot * quarter, quarter)
    query_position = lax.dynamic_slice_in_dim(position, col_slot * quarter, quarter)
    block_rows = min(512, quarter)
    block_count = quarter // block_rows
    residual_in = own_tokens.astype(jnp.float32)
    scale_one = lax.rsqrt(col_total(residual_in * residual_in) / D + EPSILON)
    normed_one = (residual_in * scale_one[:, None] * attn_gain[None, :]).astype(jnp.bfloat16)
    spread_one = row_gather(normed_one)
    projected = col_reduce(spread_one, attention_in, False).astype(jnp.bfloat16)
    queries = projected[:, :width_row].reshape(quarter, heads_row, HEAD_DIM)
    keys_here = projected[:, width_row : 2 * width_row]
    values_here = projected[:, 2 * width_row :]
    key_flat, value_flat = key_gather(keys_here, values_here)
    key_all = key_flat.reshape(group_rows, heads_row, HEAD_DIM)
    value_all = value_flat.reshape(group_rows, heads_row, HEAD_DIM)

    def block_mask(first_row):
        return visible(
            lax.dynamic_slice_in_dim(query_member, first_row, block_rows),
            lax.dynamic_slice_in_dim(query_position, first_row, block_rows),
            member,
            position,
        )

    def forward_block(block_id):
        first_row = block_id * block_rows
        query_block = lax.dynamic_slice_in_dim(queries, first_row, block_rows, 0)
        scores = attend_scores(query_block, key_all, block_mask(first_row))
        highest = jnp.max(scores, axis=2, keepdims=True)
        totals = jnp.sum(jnp.exp(scores - highest), axis=2, keepdims=True)
        log_total = highest + jnp.log(totals)
        probability = jnp.exp(scores - log_total)
        output = jnp.einsum(
            "hqk,khd->qhd",
            probability.astype(jnp.bfloat16),
            value_all,
            preferred_element_type=jnp.float32,
        )
        return (output.astype(jnp.bfloat16).reshape(block_rows, width_row), log_total[:, :, 0])

    blocks_out, log_totals = lax.map(forward_block, jnp.arange(block_count, dtype=jnp.int32))
    attended = blocks_out.reshape(quarter, width_row)
    spread_attn = col_gather(attended)
    midway = residual_in + row_reduce(spread_attn, out_weight, False)
    scale_two = lax.rsqrt(col_total(midway * midway) / D + EPSILON)
    normed_two = (midway * scale_two[:, None] * ffn_gain[None, :]).astype(jnp.bfloat16)
    spread_two = row_gather(normed_two)
    gate_and_up = col_reduce(spread_two, feedforward_in, False)
    gate_value = gate_and_up[:, :hidden_row]
    up_value = gate_and_up[:, hidden_row:]
    sigmoid_gate = jax.nn.sigmoid(gate_value)
    hidden = (gate_value * sigmoid_gate * up_value).astype(jnp.bfloat16)
    grad_output = own_cotangent.astype(jnp.float32)
    spread_down = row_gather(own_cotangent)
    grad_hidden = col_reduce(spread_down, down_weight, True)
    spread_hidden = col_gather(hidden)
    grad_down = outer_sum(spread_hidden, spread_down)
    grad_gate_value = (
        grad_hidden * up_value * sigmoid_gate * (1.0 + gate_value * (1.0 - sigmoid_gate))
    ).astype(jnp.bfloat16)
    grad_up_value = (grad_hidden * gate_value * sigmoid_gate).astype(jnp.bfloat16)
    spread_gate_up = col_gather(jnp.concatenate([grad_gate_value, grad_up_value], axis=1))
    grad_normed_two = row_reduce(spread_gate_up, feedforward_in, True)
    spread_two = row_gather(normed_two)
    grad_feedforward = outer_sum(spread_two, spread_gate_up)
    grad_mid_norm, gain_two_part = norm_back(grad_normed_two, midway, scale_two, ffn_gain)
    grad_midway = grad_output + grad_mid_norm
    rounded_midway = grad_midway.astype(jnp.bfloat16)
    spread_back = row_gather(rounded_midway)
    grad_attended = col_reduce(spread_back, out_weight, True).astype(jnp.bfloat16)
    spread_attn = col_gather(attended)
    key_flat, value_flat = key_gather(keys_here, values_here)
    key_all = key_flat.reshape(group_rows, heads_row, HEAD_DIM)
    value_all = value_flat.reshape(group_rows, heads_row, HEAD_DIM)
    grad_out_local = outer_sum(spread_attn, spread_back)

    def backward_block(carried, block_id):
        first_row = block_id * block_rows
        query_block = lax.dynamic_slice_in_dim(queries, first_row, block_rows, 0)
        scores = attend_scores(query_block, key_all, block_mask(first_row))
        probability = jnp.exp(
            scores - lax.dynamic_index_in_dim(log_totals, block_id, 0, keepdims=False)[:, :, None]
        )
        weights_low = probability.astype(jnp.bfloat16)
        grad_block = lax.dynamic_slice_in_dim(grad_attended, first_row, block_rows, 0).reshape(
            block_rows, heads_row, HEAD_DIM
        )
        grad_soft = jnp.einsum(
            "qhd,khd->hqk", grad_block, value_all, preferred_element_type=jnp.float32
        )
        row_inner = jnp.sum(probability * grad_soft, axis=2, keepdims=True)
        grad_scores = (probability * (grad_soft - row_inner)).astype(jnp.bfloat16)
        grad_query_block = jnp.einsum(
            "hqk,khd->qhd", grad_scores, key_all, preferred_element_type=jnp.float32
        ) * HEAD_DIM ** (-0.5)
        grad_key_all = carried[0] + jnp.einsum(
            "hqk,qhd->khd", grad_scores, query_block, preferred_element_type=jnp.float32
        ) * HEAD_DIM ** (-0.5)
        grad_value_all = carried[1] + jnp.einsum(
            "hqk,qhd->khd", weights_low, grad_block, preferred_element_type=jnp.float32
        )
        return (
            (grad_key_all, grad_value_all),
            grad_query_block.astype(jnp.bfloat16).reshape(block_rows, width_row),
        )

    start_grads = jnp.zeros((group_rows, heads_row, HEAD_DIM), jnp.float32)
    key_value_grads, grad_queries = lax.scan(
        backward_block, (start_grads, start_grads), jnp.arange(block_count, dtype=jnp.int32)
    )
    grad_queries = grad_queries.reshape(quarter, width_row)
    grad_key_part = key_value_grads[0].reshape(group_rows, width_row)
    grad_value_part = key_value_grads[1].reshape(group_rows, width_row)
    grad_key_mine, grad_value_mine = (
        lax.psum_scatter(grad_key_part, "col", scatter_dimension=0, tiled=True),
        lax.psum_scatter(grad_value_part, "col", scatter_dimension=0, tiled=True),
    )
    spread_projected = col_gather(
        jnp.concatenate(
            [
                grad_queries,
                grad_key_mine.astype(jnp.bfloat16),
                grad_value_mine.astype(jnp.bfloat16),
            ],
            axis=1,
        )
    )
    grad_normed_one = row_reduce(spread_projected, attention_in, True)
    spread_one = row_gather(normed_one)
    grad_attention = outer_sum(spread_one, spread_projected)
    grad_in_norm, gain_one_part = norm_back(grad_normed_one, residual_in, scale_one, attn_gain)
    grad_own_tokens = grad_midway + grad_in_norm
    grad_attn_gain, grad_ffn_gain = lax.psum((gain_one_part, gain_two_part), ("dp", "row"))
    grad_query, grad_key, grad_value, grad_out, grad_gate, grad_up, grad_down_mine = (
        lax.psum_scatter(
            grad_attention[:, :width_row].astype(jnp.bfloat16),
            "dp",
            scatter_dimension=1,
            tiled=True,
        ).astype(jnp.float32),
        lax.psum_scatter(
            grad_attention[:, width_row : 2 * width_row].astype(jnp.bfloat16),
            "dp",
            scatter_dimension=1,
            tiled=True,
        ).astype(jnp.float32),
        lax.psum_scatter(
            grad_attention[:, 2 * width_row :].astype(jnp.bfloat16),
            "dp",
            scatter_dimension=1,
            tiled=True,
        ).astype(jnp.float32),
        lax.psum_scatter(
            grad_out_local.astype(jnp.bfloat16), "dp", scatter_dimension=0, tiled=True
        ).astype(jnp.float32),
        lax.psum_scatter(
            grad_feedforward[:, :hidden_row].astype(jnp.bfloat16),
            "dp",
            scatter_dimension=1,
            tiled=True,
        ).astype(jnp.float32),
        lax.psum_scatter(
            grad_feedforward[:, hidden_row:].astype(jnp.bfloat16),
            "dp",
            scatter_dimension=1,
            tiled=True,
        ).astype(jnp.float32),
        lax.psum_scatter(
            grad_down.astype(jnp.bfloat16), "dp", scatter_dimension=0, tiled=True
        ).astype(jnp.float32),
    )
    total_tokens = permutation.shape[0]
    inverse = (
        jnp.zeros((total_tokens,), jnp.int32)
        .at[permutation]
        .set(jnp.arange(total_tokens, dtype=jnp.int32))
    )
    wanted_slots = lax.dynamic_slice_in_dim(inverse, device_slot * own_rows, own_rows)
    (grad_tokens,) = make_picker(
        wanted_slots,
        (jnp.zeros_like(grad_own_tokens),),
        (
            (
                lax.all_gather(
                    grad_own_tokens.astype(jnp.bfloat16), ("dp", "row"), axis=0, tiled=True
                ),
            )[0].astype(jnp.float32),
        ),
    )
    return (
        grad_tokens,
        grad_query,
        grad_key,
        grad_value,
        grad_out,
        grad_gate,
        grad_up,
        grad_down_mine,
        grad_attn_gain,
        grad_ffn_gain,
    )


def scores_of(query, key):
    return lax.dot_general(
        query, key, (((1,), (1,)), ((), ())), preferred_element_type=F32
    ) * HEAD_DIM ** (-0.5)


MESH = pl.DeviceIdType.MESH
PLACE = {0: 0, 2: 1, 1: 2, 3: 3}
TILE = 256


class Post:
    def __init__(self, send_sem, recv_sem):
        self.send_sem, self.recv_sem, self.used = send_sem, recv_sem, 0

    def ready(self, src, dst, target, slot=None):
        if slot is None:
            slot = self.used
            self.used += 1
        return pltpu.make_async_remote_copy(
            src_ref=src,
            dst_ref=dst,
            send_sem=self.send_sem.at[slot],
            recv_sem=self.recv_sem.at[slot],
            device_id=target,
            device_id_type=MESH,
        )

    def take(self, count):
        first = self.used
        self.used += count
        return first

    def send(self, src, dst, target):
        copy = self.ready(src, dst, target)
        copy.start()
        return copy


def greet(peers):
    barrier = pltpu.get_barrier_semaphore()
    for peer in peers:
        pl.semaphore_signal(barrier, inc=1, device_id=peer, device_id_type=MESH)
    pl.semaphore_wait(barrier, len(peers))


def as_row(column):
    return jnp.transpose(jnp.broadcast_to(column, (column.shape[0], 128)))[0:8]


def as_column(row):
    return jnp.transpose(row)[:, 0:1]


def scatter_plane(post, low, landed, rows, me):
    d, r, c = me
    half = rows // 2
    x_at, y_at = (d, r ^ 1, c), (d, r, c ^ 2)
    upper, lower = pl.ds(0, half), pl.ds(half, half)
    corner_x = post.send(low(rows, half, 1), landed.at[2, upper], x_at)
    corner_y = post.send(low(rows + half, half, 1), landed.at[2, lower], y_at)
    sent = [
        post.send(low(rows, half, 0), landed.at[0, upper], x_at),
        post.send(low(half, half, 1), landed.at[1, lower], y_at),
    ]

    def add(ref, first):
        def one(t, total):
            part = pl.ds(pl.multiple_of(t * 64, 64), 64)
            there = pl.ds(pl.multiple_of(first + t * 64, 64), 64)
            ref[part, :] = (ref[part, :].astype(F32) + landed[2, there, :].astype(F32)).astype(BF)
            return total

        lax.fori_loop(0, half // 64, one, 0)

    def pass_pieces():
        corner_x.wait_recv()
        add(low(0, half, 1), 0)
        later = [post.send(low(0, half, 1), landed.at[1, upper], y_at)]
        corner_y.wait_recv()
        add(low(rows + half, half, 0), half)
        later.append(post.send(low(rows + half, half, 0), landed.at[0, lower], x_at))
        return later

    return sent, [corner_x, corner_y], pass_pieces


def forward_kernel(
    x_ref, gain_one_ref, gain_two_ref, lengths_ref, query_ref, key_ref, value_ref, out_ref, gate_hbm, up_hbm,
    own_grad,
    mid_ref, scale_ref, n2_ref, begin_ref, first_scale,
    normed_out, weight_in_out, weight_out_out, q_out, kv_out, att_out, lse_out, own_up, gate_all, up_all, grad_all,
    normed_ref, weight_in, weight_out, q_ref, kv_ref, att_ref, lse_ref, masters,
    zin, zout, sums, wide, given, arrived, low, landed, x32, hidden_own,
    send_sem, recv_sem, local_sem,
):
    d, r, c = (lax.axis_index(name) for name in AXES)
    y, core = c // 2, lax.rem(c, 2)
    rows = x_ref.shape[0]
    fc = x_ref.shape[1]
    group = 2 * rows
    width = q_ref.shape[1]
    half = 2 * fc
    post = Post(send_sem, recv_sem)
    fetches = [
        pltpu.make_async_copy(src, masters.at[n], local_sem.at[8 + n]) for n, src in enumerate((gate_hbm, up_hbm))
    ]
    for copy in fetches:
        copy.start()
    copies = []

    def copy_out(src, dst):
        copy = pltpu.make_async_copy(src, dst, local_sem.at[10 + len(copies)])
        copy.start()
        copies.append(copy)

    in_plane = [(d, r ^ a, c ^ b) for a in (0, 1) for b in range(COL) if (a, b) != (0, 0)]
    greet([(d ^ j, r, c) for j in (1, 2, 3)] + in_plane)

    def fill_x(t, total):
        part = pl.ds(pl.multiple_of(t * 128, 128), 128)
        value = x_ref[part, :].astype(F32)
        x32[part, :] = value
        sums[0, :, part] = as_row(jnp.sum(value * value, axis=1, keepdims=True))
        return total

    lax.fori_loop(0, rows // 128, fill_x, 0)
    small = [post.send(sums.at[0], sums.at[m], (d, r, c ^ m)) for m in (1, 2, 3)]

    parts = (pl.ds(width, 2 * width), pl.ds(0, width))
    first, first_down = post.take(3 * DP), post.take(3 * DP)

    def block_of(n, p):
        return zin.at[p, :, parts[n]] if n < 2 else zout.at[p]

    def line(n, p, target_plane):
        block = block_of(n, p)
        return post.ready(block, block, (target_plane, r, c), first + DP * n + p)

    def line_down(n, p, target_plane):
        block = block_of(n, p)
        return pltpu.make_async_remote_copy(
            src_ref=block, dst_ref=block,
            send_sem=send_sem.at[first_down + DP * n + p], recv_sem=recv_sem.at[first + DP * n + p],
            device_id=(target_plane, r, c), device_id_type=MESH,
        )

    def cast_rows(src, dst, amount, step=64):
        def one(t, total):
            part = pl.ds(pl.multiple_of(t * step, step), step)
            dst(part, src[part, :].astype(BF))
            return total

        lax.fori_loop(0, amount // step, one, 0)

    for place, master in enumerate((query_ref, key_ref, value_ref)):
        def put(part, value, place=place):
            zin[d, part, place * width : (place + 1) * width] = value

        cast_rows(master, put, fc)
    def leave(n):
        @pl.when(d < DP - 1)
        def _():
            line(n, d, d + 1).start()

        @pl.when(d > 0)
        def _():
            line_down(n, d, d - 1).start()

    leave(0)
    leave(1)

    first_cols = post.take(3 * DP)

    def place_of(m):
        return lax.rem(m, 2) * 2 + m // 2

    def seat_of(n, place):
        there = pl.ds(pl.multiple_of(place * fc, fc), fc)
        return weight_in.at[there, parts[n]] if n < 2 else weight_out.at[:, there]

    def to_column(n, p):
        return pltpu.make_async_remote_copy(
            src_ref=block_of(n, p),
            dst_ref=seat_of(n, place_of(p ^ c)),
            send_sem=send_sem.at[first_cols + DP * n + p],
            recv_sem=recv_sem.at[first_cols + DP * n + (p ^ c)],
            device_id=(d, r, p), device_id_type=MESH,
        )

    def keep(n):
        return pltpu.make_async_copy(block_of(n, c), seat_of(n, 0), local_sem.at[(0, 1, 5)[n]])

    def pass_on(n, p):
        @pl.when(p == c)
        def _():
            keep(n).start()

        @pl.when(p != c)
        def _():
            to_column(n, p).start()

    hidden_all = (gate_all, up_all)
    first_sent = post.take(10)
    first_got = first_sent

    def slab(kind, i):
        return hidden_all[kind].at[pl.ds(pl.multiple_of(place_of(i) * fc, fc), fc), :]

    def ship(kind, way, i, target, src=None):
        return pltpu.make_async_remote_copy(
            src_ref=hidden_own.at[kind] if src is None else src,
            dst_ref=slab(kind, i),
            send_sem=send_sem.at[first_sent + 5 * kind + way],
            recv_sem=recv_sem.at[first_got + 4 * kind + i],
            device_id=target, device_id_type=MESH,
        )

    def keep_hidden(kind):
        return pltpu.make_async_copy(hidden_own.at[kind], slab(kind, 0), local_sem.at[3 + kind])

    def to_core(kind):
        return ship(kind, 0, 1, (d, r, c ^ 1))

    first_half = post.take(8)

    def gate_half(i, n):
        step = fc // 2
        return gate_all.at[pl.ds(pl.multiple_of(place_of(i) * fc + n * step, step), step), :]

    def over_y(n):
        return pltpu.make_async_remote_copy(
            src_ref=hidden_own.at[0, pl.ds(n * (fc // 2), fc // 2), :], dst_ref=gate_half(2 + core, n),
            send_sem=send_sem.at[first_half + 4 * n], recv_sem=recv_sem.at[first_half + 4 * n + core],
            device_id=(d, r, 2 * (1 - y)), device_id_type=MESH,
        )

    def over_x(kind):
        return ship(kind, 2, 1 - core, (d, r ^ 1, 2 * y + 1))

    def relay(n, i):
        return pltpu.make_async_remote_copy(
            src_ref=gate_half(i, n), dst_ref=gate_half(5 - i, n),
            send_sem=send_sem.at[first_half + 4 * n + i - 1],
            recv_sem=recv_sem.at[first_half + 4 * n + 3 - i],
            device_id=(d, r ^ 1, 2 * y + 1), device_id_type=MESH,
        )

    def gate_came(n, i):
        return pltpu.make_async_remote_copy(
            src_ref=gate_half(i, n), dst_ref=gate_half(i, n),
            send_sem=send_sem.at[first_half], recv_sem=recv_sem.at[first_half + 4 * n + i - 2],
            device_id=(d, r, c), device_id_type=MESH,
        )

    def start_home(kind):
        @pl.when(core == 0)
        def _():
            keep_hidden(kind).start()

        @pl.when(core == 1)
        def _():
            to_core(kind).start()

    def start_relay(n):
        @pl.when(core == 0)
        def _():
            for i in (2, 3):
                gate_came(n, i).wait_recv()
                relay(n, i).start()

    def cast_hidden(kind):
        def put(part, value):
            hidden_own[kind, part, :] = value

        fetches[kind].wait()
        cast_rows(masters.at[kind], put, fc)

    cast_hidden(0)
    over_x(0).start()
    over_y(0).start()
    for copy in small:
        copy.wait_recv()

    def norm_one(t, total):
        part = pl.ds(pl.multiple_of(t * 128, 128), 128)
        square = sums[0, :, part] + sums[2, :, part] + sums[1, :, part] + sums[3, :, part]
        scale = lax.rsqrt(as_column(square) / D + EPSILON)
        first_scale[part, :] = scale
        normed_ref[part, 0:fc] = (x32[part, :] * scale * gain_one_ref[...]).astype(BF)
        return total

    lax.fori_loop(0, rows // 128, norm_one, 0)
    own_rows, other_rows = pl.ds(0, rows), pl.ds(rows, rows)

    def columns(place):
        return pl.ds(place * fc, fc)

    own_block = normed_ref.at[own_rows, columns(0)]
    beside = post.send(own_block, normed_ref.at[other_rows, columns(0)], (d, r ^ 1, c))
    beyond = post.send(own_block, normed_ref.at[own_rows, columns(1)], (d, r, c ^ 2))
    corner = post.send(own_block, normed_ref.at[other_rows, columns(1)], (d, r ^ 1, c ^ 2))
    sibling = (d, r, c ^ 1)
    shared = [post.send(own_block, normed_ref.at[own_rows, columns(2)], sibling)]
    pass_on(0, d)
    pass_on(1, d)
    cast_hidden(1)
    start_home(0)
    start_home(1)
    copy_out(hidden_own.at[1], own_up)
    over_x(1).start()
    half_rows = rows // 2
    grad_cross = post.send(
        own_grad.at[pl.ds(pl.multiple_of((1 - y) * half_rows, half_rows), half_rows), :],
        grad_all.at[pl.ds(0, half_rows), pl.ds(fc, fc)],
        (d, r, c ^ 2),
    )
    grad_keep = pltpu.make_async_copy(
        own_grad.at[pl.ds(pl.multiple_of(y * half_rows, half_rows), half_rows), :],
        grad_all.at[pl.ds(0, half_rows), pl.ds(0, fc)],
        local_sem.at[2],
    )
    grad_keep.start()

    def put_out(part, value):
        zout[d, part, :] = value

    cast_rows(out_ref, put_out, width)

    def find_begins(t, total):
        part = pl.ds(pl.multiple_of(t * 128, 128), 128)
        place = lax.broadcasted_iota(jnp.int32, (128, 1), 0) + (d * group + t * 128)
        end = jnp.int32(0)
        begin = jnp.zeros((128, 1), jnp.int32)
        for n in range(lengths_ref.shape[0]):
            end = end + lengths_ref[n]
            begin = jnp.where(place >= end, end, begin)
        begin_ref[part, :] = begin - d * group
        return total

    lax.fori_loop(0, group // 128, find_begins, 0)

    def line_step(s, which=(0, 1)):
        for n in which:
            for p, valid, onward, forward in (
                (d - s, d - s >= 0, d < DP - 1, lambda n, p: line(n, p, d + 1)),
                (d + s, d + s < DP, d > 0, lambda n, p: line_down(n, p, d - 1)),
            ):
                @pl.when(valid)
                def _(n=n, p=p, onward=onward, forward=forward):
                    line(n, p, d).wait_recv()

                    @pl.when(onward)
                    def _():
                        forward(n, p).start()

                    pass_on(n, p)

    line_step(1)
    leave(2)
    line_step(2)
    pass_on(2, d)
    line_step(1, (2,))
    for copy, where, place in ((beside, other_rows, 0), (beyond, own_rows, 1), (corner, other_rows, 1)):
        copy.wait_recv()
        shared.append(
            post.send(normed_ref.at[where, columns(place)], normed_ref.at[where, columns(place + 2)], sibling)
        )
    line_step(3)
    line_step(2, (2,))
    start_relay(0)

    def arrived_blocks(n):
        keep(n).wait()
        for m in (1, 2, 3):
            pltpu.make_async_remote_copy(
                src_ref=block_of(n, 0), dst_ref=seat_of(n, 0),
                send_sem=send_sem.at[first_cols], recv_sem=recv_sem.at[first_cols + DP * n + m],
                device_id=(d, r, c), device_id_type=MESH,
            ).wait_recv()

    for copy in shared:
        copy.wait_recv()
    arrived_blocks(0)
    over_y(1).start()
    copy_out(normed_ref, normed_out)

    def turned(t):
        return lax.rem(t + 2 * r, group // TILE)

    def project_kv(t, total):
        part = pl.ds(pl.multiple_of(t * TILE, TILE), TILE)
        to = pl.ds(pl.multiple_of(REACH + turned(t) * TILE, TILE), TILE)
        kv_ref[to, :] = jnp.dot(
            normed_ref[part, :], weight_in[:, width:], preferred_element_type=F32
        ).astype(BF)
        return total

    lax.fori_loop(0, group // TILE, project_kv, 0)
    halo = post.ready(kv_ref.at[pl.ds(group, REACH), :], kv_ref.at[pl.ds(0, REACH), :], (lax.rem(d + 1, DP), r, c))

    @pl.when(d < DP - 1)
    def _():
        halo.start()

    arrived_blocks(1)

    def project_q(t, total):
        part = pl.ds(pl.multiple_of(t * TILE, TILE), TILE)
        to = pl.ds(pl.multiple_of(turned(t) * TILE, TILE), TILE)
        q_ref[to, :] = jnp.dot(
            normed_ref[part, :], weight_in[:, :width], preferred_element_type=F32
        ).astype(BF)
        return total

    lax.fori_loop(0, group // TILE, project_q, 0)

    copy_out(weight_in, weight_in_out)
    copy_out(q_ref, q_out)
    line_step(3, (2,))
    @pl.when(d == 0)
    def _():
        kv_ref[pl.ds(0, REACH), :] = jnp.zeros((REACH, 2 * width), BF)

    @pl.when(d > 0)
    def _():
        halo.wait_recv()

    copy_out(kv_ref, kv_out)

    grads = [
        post.ready(
            grad_all.at[pl.ds(0, half_rows), pl.ds(0, half)],
            grad_all.at[pl.ds(j * half_rows, half_rows), pl.ds(0, half)],
            (d ^ j, r, c),
        )
        for j in (1, 2, 3)
    ]
    grads_shared = [
        post.ready(
            grad_all.at[pl.ds(0, half_rows), pl.ds(0, half)],
            grad_all.at[pl.ds(0, half_rows), pl.ds(half, half)],
            sibling,
        )
    ]

    def spread_grads():
        grad_cross.wait_recv()
        grad_keep.wait()
        for copy in grads + grads_shared[:1]:
            copy.start()

    pl.when(d > 0)(spread_grads)

    span = TILE + REACH
    for h in range(width // HEAD_DIM):
        lanes = pl.ds(h * HEAD_DIM, HEAD_DIM)
        value_lanes = pl.ds(width + h * HEAD_DIM, HEAD_DIM)

        def one(t, total, lanes=lanes, value_lanes=value_lanes):
            part = pl.ds(pl.multiple_of(t * TILE, TILE), TILE)
            to = pl.ds(pl.multiple_of(turned(t) * TILE, TILE), TILE)
            window = pl.ds(pl.multiple_of(t * TILE, TILE), span)
            scores = scores_of(q_ref[part, lanes], kv_ref[window, lanes])
            query = lax.broadcasted_iota(jnp.int32, (TILE, span), 0)
            key = lax.broadcasted_iota(jnp.int32, (TILE, span), 1)
            begin = begin_ref[part, 0:1] + (REACH - t * TILE)
            allowed = (key <= query + REACH) & (key >= begin)
            scores = jnp.where(allowed, scores, NEG_FILL)
            highest = jnp.max(scores, axis=1, keepdims=True)
            expo = jnp.exp(scores - highest)
            total_e = jnp.sum(expo, axis=1, keepdims=True)
            probability = (expo * (1.0 / total_e)).astype(BF)
            att_ref[to, lanes] = jnp.dot(
                probability, kv_ref[window, value_lanes], preferred_element_type=F32
            ).astype(BF)
            lse_ref[part, lanes] = jnp.broadcast_to(highest + jnp.log(total_e), (TILE, HEAD_DIM))
            return total

        lax.fori_loop(0, group // TILE, one, 0)

    pl.when(d == 0)(spread_grads)

    copy_out(att_ref, att_out)
    copy_out(lse_ref, lse_out)
    arrived_blocks(2)
    copy_out(weight_out, weight_out_out)

    def out_given(t, total):
        part = pl.ds(pl.multiple_of(t * TILE, TILE), TILE)
        given[part, :] = jnp.dot(
            att_ref[part, :], weight_out[:, half:], preferred_element_type=F32
        ).astype(BF)
        return total

    lax.fori_loop(0, group // TILE, out_given, 0)
    to_sibling = post.send(given, arrived, sibling)

    def out_kept(t, total):
        part = pl.ds(pl.multiple_of(t * TILE, TILE), TILE)
        wide[part, :] = jnp.dot(att_ref[part, :], weight_out[:, :half], preferred_element_type=F32)
        return total

    lax.fori_loop(0, group // TILE, out_kept, 0)
    to_sibling.wait_recv()

    def add_low(t, total):
        part = pl.ds(pl.multiple_of(t * 128, 128), 128)
        value = wide[part, :] + arrived[part, :].astype(F32)
        wide[part, :] = value
        low[part, :] = value.astype(BF)
        return total

    lax.fori_loop(0, group // 128, add_low, 0)
    pieces, corners, pass_pieces = scatter_plane(
        post, lambda first, count, place: low.at[pl.ds(first, count), columns(place)], landed, rows, (d, r, c)
    )
    pieces = pieces + pass_pieces()
    start_relay(1)
    for copy in pieces:
        copy.wait_recv()

    def middle(t, total):
        part = pl.ds(pl.multiple_of(t * 128, 128), 128)
        value = (
            x32[part, :] + wide[part, 0:fc] + landed[0, part, :].astype(F32)
            + landed[1, part, :].astype(F32)
        )
        mid_ref[part, :] = value
        sums[4, :, part] = as_row(jnp.sum(value * value, axis=1, keepdims=True))
        return total

    lax.fori_loop(0, rows // 128, middle, 0)
    again = [post.send(sums.at[4], sums.at[4 + m], (d, r, c ^ m)) for m in (1, 2, 3)]
    for copy in again:
        copy.wait_recv()

    def norm_two(t, total):
        part = pl.ds(pl.multiple_of(t * 128, 128), 128)
        square = sums[4, :, part] + sums[6, :, part] + sums[5, :, part] + sums[7, :, part]
        scale = lax.rsqrt(as_column(square) / D + EPSILON)
        scale_ref[part, :] = scale
        n2_ref[part, :] = (mid_ref[part, :] * scale * gain_two_ref[...]).astype(BF)
        return total

    lax.fori_loop(0, rows // 128, norm_two, 0)

    for j, copy in zip((1, 2, 3), grads):
        copy.wait_recv()
        there = pl.ds(j * half_rows, half_rows)
        grads_shared.append(
            post.send(grad_all.at[there, pl.ds(0, half)], grad_all.at[there, pl.ds(half, half)], sibling)
        )
    for copy in grads_shared:
        copy.wait_recv()
    for n in (0, 1):
        over_y(n).wait_send()

        @pl.when(core == 0)
        def _(n=n):
            for i in (2, 3):
                relay(n, i).wait_send()

        @pl.when(core == 1)
        def _(n=n):
            for i in (2, 3):
                gate_came(n, i).wait_recv()

    for kind in (0, 1):
        over_x(kind).wait_send()

        @pl.when(core == 0)
        def _(kind=kind):
            keep_hidden(kind).wait()
            ship(kind, 0, 1, (d, r, c)).wait_recv()

        @pl.when(core == 1)
        def _(kind=kind):
            to_core(kind).wait_send()
            for i in (0, 1):
                ship(kind, 0, i, (d, r, c)).wait_recv()

    for copy in (
        small + [grad_cross, beside, beyond, corner] + shared + grads + grads_shared
        + [to_sibling] + pieces + corners + again
    ):
        copy.wait_send()

    @pl.when(d < DP - 1)
    def _():
        halo.wait_send()

    for copy in copies:
        copy.wait()
    for n in (0, 1, 2):
        for p in range(DP):
            @pl.when((d < DP - 1) & (p <= d))
            def _(n=n, p=p):
                line(n, p, d).wait_send()

            @pl.when((d > 0) & (p >= d))
            def _(n=n, p=p):
                line_down(n, p, d).wait_send()

            @pl.when(c != p)
            def _(n=n, p=p):
                to_column(n, p).wait_send()


SENDS = 104


def forward(x, gain_one, gain_two, lengths, query, key, value, out, gate, up, own_grad):
    rows, fc = x.shape
    group = 2 * rows
    width = out.shape[0]
    units = gate.shape[1]
    vmem = pl.BlockSpec(memory_space=pltpu.VMEM)
    smem = pl.BlockSpec(memory_space=pltpu.SMEM)
    hbm = pl.BlockSpec(memory_space=pl.ANY)

    def like(shape, dtype=BF):
        return jax.ShapeDtypeStruct(shape, dtype)

    return pl.pallas_call(
        forward_kernel,
        in_specs=[vmem] * 3 + [smem] + [vmem] * 4 + [hbm] * 3,
        out_specs=[vmem] * 5 + [hbm] * 11,
        out_shape=[
            like((rows, fc), F32),
            like((rows, 1), F32),
            like((rows, fc)),
            like((group, 1), jnp.int32),
            like((rows, 1), F32),
            like((group, D)),
            like((D, 3 * width)),
            like((width, D)),
            like((group, width)),
            like((REACH + group, 2 * width)),
            like((group, width)),
            like((group, width), F32),
            like((fc, units)),
            like((D, units)),
            like((D, units)),
            like((group, D)),
        ],
        scratch_shapes=[
            pltpu.VMEM((group, D), BF),
            pltpu.VMEM((D, 3 * width), BF),
            pltpu.VMEM((width, D), BF),
            pltpu.VMEM((group, width), BF),
            pltpu.VMEM((REACH + group, 2 * width), BF),
            pltpu.VMEM((group, width), BF),
            pltpu.VMEM((group, width), F32),
            pltpu.VMEM((2, fc, units), F32),
            pltpu.VMEM((DP, fc, 3 * width), BF),
            pltpu.VMEM((DP, width, fc), BF),
            pltpu.VMEM((8, 8, rows), F32),
            pltpu.VMEM((group, 2 * fc), F32),
            pltpu.VMEM((group, 2 * fc), BF),
            pltpu.VMEM((group, 2 * fc), BF),
            pltpu.VMEM((group, 2 * fc), BF),
            pltpu.VMEM((3, rows, fc), BF),
            pltpu.VMEM((rows, fc), F32),
            pltpu.VMEM((2, fc, units), BF),
            pltpu.SemaphoreType.DMA((SENDS,)),
            pltpu.SemaphoreType.DMA((SENDS,)),
            pltpu.SemaphoreType.DMA((20,)),
        ],
        compiler_params=pltpu.CompilerParams(
            collective_id=1, has_side_effects=True, vmem_limit_bytes=60 << 20
        ),
        cost_estimate=pl.CostEstimate(
            flops=6 * group * D * width, bytes_accessed=64 << 20, transcendentals=0
        ),
    )(x, gain_one, gain_two, lengths, query, key, value, out, gate, up, own_grad)


def at(t, size):
    return pl.ds(pl.multiple_of(t * size, size), size)


def loop(count, body):
    def one(t, total):
        body(t)
        return total

    lax.fori_loop(0, count, one, 0)


def maker(send_sem, recv_sem):
    def raw(src, dst, sent, got_at, target):
        return pltpu.make_async_remote_copy(
            src_ref=src, dst_ref=dst, send_sem=send_sem.at[sent], recv_sem=recv_sem.at[got_at],
            device_id=target, device_id_type=MESH,
        )

    return raw


class LineSum:
    def __init__(self, raw, arrays, base, me):
        self.raw, self.arrays, self.base, self.me = raw, arrays, base, me

    def sem(self, n, p, down):
        return self.base + 8 * n + 4 * down + p

    def take(self, p, down, done):
        d = self.me[0]
        for n, (z, got_z) in enumerate(self.arrays):
            self.raw(z.at[p], got_z.at[p], self.sem(n, p, down), self.sem(n, p, down), self.me).wait_recv()

        @pl.when(jnp.logical_not(done))
        def _():
            for z, got_z in self.arrays:
                def one(t, z=z, got_z=got_z):
                    z[p, at(t, 64), :] = (
                        z[p, at(t, 64), :].astype(F32) + got_z[p, at(t, 64), :].astype(F32)
                    ).astype(BF)

                loop(z.shape[1] // 64, one)

    def up(self, p):
        d, r, c = self.me

        @pl.when((d > 0) & (d <= p))
        def _():
            self.take(p, 0, d == p)

        @pl.when(d < p)
        def _():
            for n, (z, got_z) in enumerate(self.arrays):
                self.raw(z.at[p], got_z.at[p], self.sem(n, p, 0), self.sem(n, p, 0), (d + 1, r, c)).start()

    def down(self, p):
        d, r, c = self.me

        @pl.when((d < DP - 1) & (d >= p))
        def _():
            self.take(p, 1, d == p)

        @pl.when(d > p)
        def _():
            slot = jnp.where(p < d - 1, p, DP)
            for n, (z, got_z) in enumerate(self.arrays):
                self.raw(z.at[p], got_z.at[slot], self.sem(n, p, 1), self.sem(n, p, 1), (d - 1, r, c)).start()

    def begin(self):
        d = self.me[0]

        @pl.when(d == 0)
        def _():
            for p in (3, 2, 1):
                self.up(p)

        @pl.when(d == DP - 1)
        def _():
            for p in (0, 1, 2):
                self.down(p)

    def hop(self, n):
        d = self.me[0]

        @pl.when(d == 1)
        def _():
            self.up(DP - 1 - n)

        @pl.when(d == 2)
        def _():
            self.down(n)

    def first(self):
        self.hop(0)
        self.hop(1)

    def last(self):
        d = self.me[0]

        @pl.when(d == 0)
        def _():
            self.down(0)

        @pl.when(d == 1)
        def _():
            self.down(0)
            self.down(1)
            self.up(1)

        @pl.when(d == 2)
        def _():
            self.up(3)
            self.up(2)
            self.down(2)

        @pl.when(d == DP - 1)
        def _():
            self.up(3)

    def rest(self):
        self.first()
        self.last()

    def settle(self):
        d = self.me[0]
        for p in range(DP):
            for n, (z, got_z) in enumerate(self.arrays):
                for down, sent in ((0, d < p), (1, d > p)):
                    @pl.when(sent)
                    def _(p=p, n=n, z=z, got_z=got_z, down=down):
                        self.raw(
                            z.at[p], got_z.at[p], self.sem(n, p, down), self.sem(n, p, down), self.me
                        ).wait_send()

    def total(self, z, got_z, part):
        d = self.me[0]
        value = z[d, part, :].astype(F32)
        value = value + jnp.where(d > 0, got_z[d, part, :].astype(F32), 0.0)
        return value + jnp.where(d < DP - 1, got_z[DP, part, :].astype(F32), 0.0)


class PlaneSum:
    def __init__(self, raw, stage, got, comb, base, local_sem, local_base, me):
        self.raw, self.stage, self.got, self.comb, self.base = raw, stage, got, comb, base
        self.local_sem, self.local_base, self.me = local_sem, local_base, me
        self.kinds = range(stage.shape[0])

    def from_one(self, kind, i):
        d, r, c = self.me
        y = c // 2
        sent, base = self.base + 10 * kind + i, self.base + 10 * kind
        if i < 2:
            return self.raw(self.stage.at[kind, i], self.got.at[kind, 0], sent, base, (d, r ^ 1, 2 * y + 1 - i))
        return self.raw(
            self.stage.at[kind, i], self.comb.at[kind, 3 - i], sent, base + 3 + (3 - i), (d, r ^ 1, 2 * y)
        )

    def from_zero(self, kind, i):
        d, r, c = self.me
        sent, base = self.base + 10 * kind + i, self.base + 10 * kind
        if i == 1:
            return self.raw(self.stage.at[kind, i], self.got.at[kind, 1], sent, base + 1, (d, r, c ^ 1))
        return self.raw(
            self.stage.at[kind, i], self.got.at[kind, 2], sent, base + 2, (d, r, 2 * (1 - c // 2) + i - 2)
        )

    def home(self, kind):
        return pltpu.make_async_copy(
            self.stage.at[kind, 0], self.got.at[kind, 1], self.local_sem.at[self.local_base + kind]
        )

    def start_far(self):
        @pl.when(lax.rem(self.me[2], 2) == 1)
        def _():
            for i in (2, 3):
                for kind in self.kinds:
                    self.from_one(kind, i).start()

    def start_near(self, kinds=None):
        kinds = self.kinds if kinds is None else kinds
        core = lax.rem(self.me[2], 2)

        @pl.when(core == 1)
        def _():
            for i in (0, 1):
                for kind in kinds:
                    self.from_one(kind, i).start()

        @pl.when(core == 0)
        def _():
            for kind in kinds:
                self.home(kind).start()
                self.from_zero(kind, 1).start()

    def combine(self, room, local_base, kinds=None):
        kinds = self.kinds if kinds is None else kinds
        core = lax.rem(self.me[2], 2)

        @pl.when(core == 0)
        def _():
            for i in (2, 3):
                for kind in kinds:
                    self.raw(
                        self.stage.at[kind, i], self.comb.at[kind, i - 2], self.base,
                        self.base + 10 * kind + 3 + (i - 2), self.me,
                    ).wait_recv()
                    fetch = pltpu.make_async_copy(
                        self.comb.at[kind, i - 2], room(kind, i - 2),
                        self.local_sem.at[local_base + 2 * kind + i - 2],
                    )
                    fetch.start()
                    fetch.wait()

                    def add(t, kind=kind, i=i):
                        self.stage[kind, i, at(t, 64), :] = (
                            self.stage[kind, i, at(t, 64), :].astype(F32)
                            + room(kind, i - 2)[at(t, 64), :].astype(F32)
                        ).astype(BF)

                    loop(self.stage.shape[2] // 64, add)
                    self.from_zero(kind, i).start()

    def settle(self):
        core = lax.rem(self.me[2], 2)
        for kind in self.kinds:
            base = self.base + 10 * kind
            for n in (0, 2):
                self.raw(self.stage.at[kind, 0], self.got.at[kind, n], self.base, base + n, self.me).wait_recv()

            @pl.when(core == 1)
            def _(kind=kind, base=base):
                self.raw(self.stage.at[kind, 0], self.got.at[kind, 1], self.base, base + 1, self.me).wait_recv()
                for i in range(COL):
                    self.from_one(kind, i).wait_send()

            @pl.when(core == 0)
            def _(kind=kind):
                self.home(kind).wait()
                for i in (1, 2, 3):
                    self.from_zero(kind, i).wait_send()


def middle_kernel(
    n2_ref, mid_ref, scale_ref, gain_ref, own_grad, down_ref, own_up, gate_hbm, up_hbm, grad_hbm,
    grad_out, gain_out, got, comb, n2_out, dgate_out, dup_out,
    n2, dgate, dup, wg, wu, wd, gb, own_down, gate, up, du, hidden, given, arrived, z, got_z, crossing, crossed, gn, sums, stage,
    send_sem, recv_sem, local_sem,
):
    d, r, c = (lax.axis_index(name) for name in AXES)
    me = (d, r, c)
    y, core = c // 2, lax.rem(c, 2)
    rows, fc = n2_ref.shape
    block = rows // 2
    units = own_down.shape[0]
    half = 2 * fc
    over = (((0,), (0,)), ((), ()))
    across = (((1,), (1,)), ((), ()))
    post = Post(send_sem, recv_sem)
    raw = maker(send_sem, recv_sem)
    sibling = (d, r, c ^ 1)
    others = [(a, b) for a in (0, 1) for b in range(COL) if (a, b) != (0, 0)]
    greet([(d, r ^ a, c ^ b) for a, b in others] + [(d ^ j, r, c) for j in (1, 2, 3)])

    cross = post.send(
        n2_ref.at[pl.ds(pl.multiple_of((1 - y) * block, block), block), :],
        n2.at[pl.ds(0, block), pl.ds(fc, fc)],
        (d, r, c ^ 2),
    )
    def half_of(ref, i, n):
        return ref.at[pl.ds(pl.multiple_of(place_of(i) * fc + n * (fc // 2), fc // 2), fc // 2), :]

    def place_of(i):
        return lax.rem(i, 2) * 2 + i // 2

    first_wide = post.take(8)

    def up_over_y(n):
        return raw(
            own_up.at[pl.ds(n * (fc // 2), fc // 2), :], half_of(wu, 2 + core, n),
            first_wide + 4 * n, first_wide + 4 * n + core, (d, r, 2 * (1 - y)),
        )

    def up_relay(n, i):
        return raw(
            half_of(wu, i, n), half_of(wu, 5 - i, n), first_wide + 4 * n + i - 1,
            first_wide + 4 * n + 3 - i, (d, r ^ 1, 2 * y + 1),
        )

    def up_came(n, i):
        return raw(half_of(wu, i, n), half_of(wu, i, n), first_wide, first_wide + 4 * n + i - 2, me)

    for n in (0, 1):
        up_over_y(n).start()
    loads = [
        pltpu.make_async_copy(src, dst, local_sem.at[n])
        for n, (src, dst) in zip((0, 1, 2, 9), (
            (gate_hbm, wg),
            (up_hbm.at[pl.ds(0, fc), :], wu.at[pl.ds(0, fc), :]),
            (grad_hbm, gb),
            (up_hbm.at[pl.ds(2 * fc, fc), :], wu.at[pl.ds(2 * fc, fc), :]),
        ))
    ]
    for load in loads:
        load.start()

    def cast_down(t):
        own_down[at(t, 64), :] = down_ref[at(t, 64), :].astype(BF)

    loop(units // 64, cast_down)
    first_sent = post.take(10)

    def piece(ref, n):
        return ref.at[pl.ds(n * (units // 2), units // 2), :]

    def ship(n, way, i, target, src=None):
        return raw(
            piece(own_down if src is None else src, n), piece(wd.at[place_of(i)], n),
            first_sent + 5 * n + way, first_sent + 5 * n + i, target,
        )

    keep_down = pltpu.make_async_copy(own_down, wd.at[0], local_sem.at[3])

    def to_core(n):
        return ship(n, 0, 1, sibling)

    def over_y(n):
        return ship(n, 1, 2 + core, (d, r, 2 * (1 - y)))

    def over_x(n):
        return ship(n, 2, 1 - core, (d, r ^ 1, 2 * y + 1))

    def relay(n, i):
        return ship(n, i + 1, 5 - i, (d, r ^ 1, 2 * y + 1), wd.at[PLACE[i]])

    for n in (0, 1):
        over_x(n).start()
        over_y(n).start()

    @pl.when(core == 0)
    def _():
        keep_down.start()

    @pl.when(core == 1)
    def _():
        for n in (0, 1):
            to_core(n).start()

    def pass_down(n):
        @pl.when(core == 0)
        def _():
            for i in (2, 3):
                ship(n, 0, i, me).wait_recv()
                relay(n, i).start()

    n2[0:block, 0:fc] = n2_ref[pl.ds(pl.multiple_of(y * block, block), block), :]
    cross.wait_recv()

    first_up, first_down = post.take(DP), post.take(DP)
    first_shared = post.take(DP)

    def rail(p, e):
        return n2.at[at(p ^ e, block), pl.ds(0, half)]

    def go_up(p):
        return raw(rail(p, d), rail(p, d + 1), first_up + p, first_up + p, (d + 1, r, c))

    def go_down(p):
        return raw(rail(p, d), rail(p, d - 1), first_down + p, first_up + p, (d - 1, r, c))

    def share(p):
        return raw(
            rail(p, d), n2.at[at(p ^ d, block), pl.ds(half, half)], first_shared + p, first_shared + p, sibling
        )

    def onward(p):
        @pl.when((p <= d) & (d < DP - 1))
        def _():
            go_up(p).start()

        @pl.when((p >= d) & (d > 0))
        def _():
            go_down(p).start()

        share(p).start()

    def project(p):
        share(p).wait_recv()
        part = at(p ^ d, block)
        gate[part, :] = jnp.dot(n2[part, :], wg[...], preferred_element_type=F32)

    def project_up(t):
        part = at(t, block)
        up[part, :] = jnp.dot(n2[part, :], wu[...], preferred_element_type=F32)

    def pass_up(n):
        @pl.when(core == 0)
        def _():
            for i in (2, 3):
                up_came(n, i).wait_recv()
                up_relay(n, i).start()

    def hidden_grads(first, fresh):
        def one(t):
            part = at(t, block)
            value = jnp.zeros((block, units), F32) if fresh else du[part, :]
            for i in (first, first + 1):
                place = PLACE[i]
                value = value + lax.dot_general(
                    gb[part, place * fc : (place + 1) * fc], wd[place], across, preferred_element_type=F32
                )
            du[part, :] = value

        loop(DP, one)

    onward(d)
    turns = [
        d,
        jnp.where(d == 0, 1, d - 1),
        jnp.where(d < 2, 2, jnp.where(d == 2, 3, 1)),
        jnp.where(d < 2, 3, 0),
    ]
    inner = (d == 1) | (d == 2)

    def arrival(n):
        raw(rail(turns[n], d), rail(turns[n], d), first_up, first_up + turns[n], me).wait_recv()
        onward(turns[n])

    for load in loads:
        load.wait()
    arrival(1)

    @pl.when(inner)
    def _():
        arrival(2)

    pass_up(0)
    project(turns[0])
    pass_up(1)
    project(turns[1])

    @pl.when(jnp.logical_not(inner))
    def _():
        arrival(2)

    @pl.when(inner)
    def _():
        arrival(3)

    pass_down(0)
    project(turns[2])

    @pl.when(core == 0)
    def _():
        keep_down.wait()
        for n in (0, 1):
            ship(n, 0, 1, me).wait_recv()

    @pl.when(core == 1)
    def _():
        for n in (0, 1):
            for i in (0, 1):
                ship(n, 0, i, me).wait_recv()

    @pl.when(jnp.logical_not(inner))
    def _():
        arrival(3)

    hidden_grads(0, True)
    pass_down(1)
    project(turns[3])
    outs = [pltpu.make_async_copy(n2, n2_out, local_sem.at[0])]
    outs[0].start()

    @pl.when(core == 1)
    def _():
        for n in (0, 1):
            for i in (2, 3):
                up_came(n, i).wait_recv()

    loop(DP, project_up)

    def hidden_of(t):
        part = at(t, 64)
        g = gate[part, :]
        hidden[part, :] = (g * (1.0 / (1.0 + jnp.exp(-g))) * up[part, :]).astype(BF)

    loop(2 * rows // 64, hidden_of)

    def down_part(i):
        def down_grad(t):
            place = PLACE[i]
            stage[0, i, at(t, TILE), :] = lax.dot_general(
                hidden[:, at(t, TILE)], gb[:, place * fc : (place + 1) * fc], over, preferred_element_type=F32
            ).astype(BF)

        loop(units // TILE, down_grad)

    owners = PlaneSum(raw, stage, got, comb, post.take(10), local_sem, 4, me)
    down_part(2)
    down_part(3)

    @pl.when(core == 1)
    def _():
        for n in (0, 1):
            for i in (2, 3):
                ship(n, 0, i, me).wait_recv()

    hidden_grads(2, False)

    owners.start_far()

    def units_of(t):
        part = at(t, 64)
        g, u, grad = gate[part, :], up[part, :], du[part, :]
        sigmoid = 1.0 / (1.0 + jnp.exp(-g))
        silu = g * sigmoid
        dgate[part, :] = (grad * u * sigmoid * (1.0 + g * (1.0 - sigmoid))).astype(BF)
        dup[part, :] = (grad * silu).astype(BF)

    loop(2 * rows // 64, units_of)
    for n, (src, dst) in enumerate(((dgate, dgate_out), (dup, dup_out))):
        outs.append(pltpu.make_async_copy(src, dst, local_sem.at[1 + n]))
        outs[-1].start()

    def back(part, cols):
        return lax.dot_general(
            dgate[part, :], wg[cols, :], across, preferred_element_type=F32
        ) + lax.dot_general(dup[part, :], wu[cols, :], across, preferred_element_type=F32)

    line = LineSum(raw, ((z, got_z),), post.take(8), me)

    def plane_of(t):
        return jnp.where(d < DP // 2, DP - 1 - t, t)

    def to_sibling(t):
        part = at(plane_of(t) ^ d, block)
        return raw(given.at[part, :], arrived.at[part, :], first_given + t, first_given + t, sibling)

    def give(t):
        part = at(plane_of(t) ^ d, block)
        given[part, :] = back(part, slice(half, None)).astype(BF)
        to_sibling(t).start()

    def keep(t):
        p = plane_of(t)
        part = at(p ^ d, block)
        value = back(part, slice(0, half))
        to_sibling(t).wait_recv()
        z[p] = (value + arrived[part, :].astype(F32)).astype(BF)

        if t < DP - 1:
            @pl.when(d == 0)
            def _():
                line.up(DP - 1 - t)

            @pl.when(d == DP - 1)
            def _():
                line.down(t)

    first_given = post.take(DP)
    give(0)
    give(1)
    keep(0)
    give(2)
    keep(1)
    give(3)
    keep(2)
    down_part(0)
    down_part(1)
    owners.start_near()
    keep(3)

    def combine():
        owners.combine(lambda kind, j: wg.at[pl.ds(0, units), pl.ds(j * fc, fc)], 5)

    pl.when(jnp.logical_not(inner))(combine)
    line.hop(0)
    pl.when(inner)(combine)
    line.hop(1)
    line.last()

    def settle_rows(t):
        part = at(t, 64)
        total = line.total(z, got_z, part)
        gn[pl.ds(pl.multiple_of(y * block + t * 64, 64), 64), :] = total[:, 0:fc]
        crossing[part, :] = total[:, fc:].astype(BF)

    loop(block // 64, settle_rows)
    other = post.send(crossing, crossed, (d, r, c ^ 2))
    other.wait_recv()

    def other_rows(t):
        gn[pl.ds(pl.multiple_of((1 - y) * block + t * 64, 64), 64), :] = crossed[at(t, 64), :].astype(F32)

    loop(block // 64, other_rows)

    def inner_sum(t):
        part = at(t, 128)
        inner = gn[part, :] * gain_ref[...] * mid_ref[part, :]
        sums[0, :, part] = as_row(jnp.sum(inner, axis=1, keepdims=True))

    loop(rows // 128, inner_sum)
    small = [post.send(sums.at[0], sums.at[m], (d, r, c ^ m)) for m in (1, 2, 3)]

    def gain_sum(t, total):
        part = at(t, 128)
        value = gn[part, :] * mid_ref[part, :] * scale_ref[part, :]
        return total + jnp.sum(value, axis=0, keepdims=True)

    gain_out[...] = lax.fori_loop(0, rows // 128, gain_sum, jnp.zeros((1, fc), F32))
    for copy in small:
        copy.wait_recv()

    def finish(t):
        part = at(t, 128)
        inner = as_column(sums[0, :, part] + sums[2, :, part] + sums[1, :, part] + sums[3, :, part])
        scale = scale_ref[part, :]
        grad_out[part, :] = (
            own_grad[part, :].astype(F32) + scale * (gn[part, :] * gain_ref[...])
            - mid_ref[part, :] * (scale * scale * scale * inner / D)
        )

    loop(rows // 128, finish)

    owners.settle()
    line.settle()
    for copy in outs:
        copy.wait()
    for copy in [cross, other] + small:
        copy.wait_send()
    for t in range(DP):
        to_sibling(t).wait_send()
    for n in (0, 1):
        over_y(n).wait_send()
        over_x(n).wait_send()
        up_over_y(n).wait_send()

        @pl.when(core == 0)
        def _(n=n):
            for i in (2, 3):
                relay(n, i).wait_send()
                up_relay(n, i).wait_send()

        @pl.when(core == 1)
        def _(n=n):
            to_core(n).wait_send()

    for p in range(DP):
        share(p).wait_send()

        @pl.when((p <= d) & (d < DP - 1))
        def _(p=p):
            go_up(p).wait_send()

        @pl.when((p >= d) & (d > 0))
        def _(p=p):
            go_down(p).wait_send()


def middle(n2, mid, scale, gain, own_grad, down, own_up, gate, up, grad_all):
    rows, fc = n2.shape
    group = 2 * rows
    block = rows // 2
    units = down.shape[0]
    vmem = pl.BlockSpec(memory_space=pltpu.VMEM)
    hbm = pl.BlockSpec(memory_space=pl.ANY)

    def like(shape, dtype=BF):
        return jax.ShapeDtypeStruct(shape, dtype)

    return pl.pallas_call(
        middle_kernel,
        in_specs=[vmem] * 6 + [hbm] * 4,
        out_specs=[vmem] * 2 + [hbm] * 5,
        out_shape=[
            like((rows, fc), F32),
            like((1, fc), F32),
            like((1, 3, units, fc)),
            like((1, 2, units, fc)),
            like((group, D)),
            like((group, units)),
            like((group, units)),
        ],
        scratch_shapes=[
            pltpu.VMEM((group, D), BF),
            pltpu.VMEM((group, units), BF),
            pltpu.VMEM((group, units), BF),
            pltpu.VMEM((D, units), BF),
            pltpu.VMEM((D, units), BF),
            pltpu.VMEM((COL, units, fc), BF),
            pltpu.VMEM((group, D), BF),
            pltpu.VMEM((units, fc), BF),
            pltpu.VMEM((group, units), F32),
            pltpu.VMEM((group, units), F32),
            pltpu.VMEM((group, units), F32),
            pltpu.VMEM((group, units), BF),
            pltpu.VMEM((group, 2 * fc), BF),
            pltpu.VMEM((group, 2 * fc), BF),
            pltpu.VMEM((DP, block, 2 * fc), BF),
            pltpu.VMEM((DP + 1, block, 2 * fc), BF),
            pltpu.VMEM((block, fc), BF),
            pltpu.VMEM((block, fc), BF),
            pltpu.VMEM((rows, fc), F32),
            pltpu.VMEM((4, 8, rows), F32),
            pltpu.VMEM((1, COL, units, fc), BF),
            pltpu.SemaphoreType.DMA((SENDS,)),
            pltpu.SemaphoreType.DMA((SENDS,)),
            pltpu.SemaphoreType.DMA((12,)),
        ],
        compiler_params=pltpu.CompilerParams(
            collective_id=3, has_side_effects=True, vmem_limit_bytes=62 << 20
        ),
        cost_estimate=pl.CostEstimate(
            flops=14 * group * D * units, bytes_accessed=48 << 20, transcendentals=group * units
        ),
    )(n2, mid, scale, gain, own_grad, down, own_up, gate, up, grad_all)


POSTS = 112


def backward_kernel(
    x_ref, gain_ref, scale_ref, mid_ref, gain_two_ref, begin_ref, weight_in_hbm, weight_out_hbm, q_hbm, kv_hbm,
    att_hbm, lse_hbm, normed_hbm, n2_hbm, dgate_hbm, dup_hbm,
    tokens_out, query_out, key_out, value_out, out_out, gains_out, got, comb,
    weight_in, weight_out, q_ref, kv_ref, att_ref, lse_ref, n1, n2, dgu, dball, dotted, dproj, acc, spill, spilled, stage, own_f, arrived, landed,
    zq, zo, zkv, rq, ro, rkv, sums, gsum,
    send_sem, recv_sem, local_sem,
):
    d, r, c = (lax.axis_index(name) for name in AXES)
    y, core = c // 2, lax.rem(c, 2)
    rows, fc = x_ref.shape
    group = 2 * rows
    width = q_hbm.shape[1]
    units = dgate_hbm.shape[1]
    half = 2 * fc
    tiles = group // TILE
    over = (((0,), (0,)), ((), ()))
    across = (((1,), (1,)), ((), ()))
    post = Post(send_sem, recv_sem)
    loads = [
        pltpu.make_async_copy(src, dst, local_sem.at[8 + n])
        for n, (src, dst) in enumerate((
            (n2_hbm, n2),
            (dgate_hbm, dgu.at[pl.ds(0, group), :]),
            (dup_hbm, dgu.at[pl.ds(group, group), :]),
            (normed_hbm, n1),
            (weight_out_hbm, weight_out),
            (att_hbm, att_ref),
            (q_hbm, q_ref),
            (kv_hbm, kv_ref),
            (lse_hbm, lse_ref),
            (weight_in_hbm, weight_in),
        ))
    ]
    for load in loads:
        load.start()

    others = [(a, b) for a in (0, 1) for b in range(COL) if (a, b) != (0, 0)]
    greet(
        [(d, r ^ a, c ^ b) for a, b in others]
        + [(d ^ j, r ^ a, c) for j in (1, 2, 3) for a in (0, 1)]
    )

    def columns(place):
        return pl.ds(place * fc, fc)

    def turned(t):
        return lax.rem(t + 2 * r, tiles)

    raw = maker(send_sem, recv_sem)
    me = (d, r, c)
    sibling = (d, r, c ^ 1)
    own_rows, other_rows = pl.ds(0, rows), pl.ds(rows, rows)
    def round_mid(t):
        dball[at(t, 128), 0:fc] = mid_ref[at(t, 128), :].astype(BF)

    loop(rows // 128, round_mid)
    own_block = dball.at[own_rows, columns(0)]
    beside = post.send(own_block, dball.at[other_rows, columns(0)], (d, r ^ 1, c))
    beyond = post.send(own_block, dball.at[own_rows, columns(1)], (d, r, c ^ 2))
    shared = [post.send(own_block, dball.at[own_rows, columns(2)], sibling)]

    for load in loads[:3]:
        load.wait()
    owners = PlaneSum(raw, stage, got, comb, post.take(20), local_sem, 4, me)

    def hidden_part(i):
        for kind in (0, 1):
            def hidden_grad(t, kind=kind):
                left = n2[:, pl.ds(pl.multiple_of(PLACE[i] * fc + t * TILE, TILE), TILE)]
                stage[kind, i, at(t, TILE), :] = lax.dot_general(
                    left, dgu[pl.ds(kind * group, group), :], over, preferred_element_type=F32
                ).astype(BF)

            loop(fc // TILE, hidden_grad)

    hidden_part(2)
    hidden_part(3)
    for load in loads[3:]:
        load.wait()

    upper = pl.ds(rows, rows // 2)
    beside.wait_recv()
    corner = [post.send(dball.at[upper, columns(0)], dball.at[upper, columns(1)], (d, r, c ^ 2))]
    shared.append(post.send(dball.at[other_rows, columns(0)], dball.at[other_rows, columns(2)], sibling))
    beyond.wait_recv()
    corner.append(post.send(
        dball.at[pl.ds(rows // 2, rows // 2), columns(1)],
        dball.at[pl.ds(rows + rows // 2, rows // 2), columns(1)], (d, r ^ 1, c),
    ))
    shared.append(post.send(dball.at[own_rows, columns(1)], dball.at[own_rows, columns(3)], sibling))
    owners.start_far()
    hidden_part(0)
    hidden_part(1)
    for copy in corner:
        copy.wait_recv()
    shared.append(post.send(dball.at[other_rows, columns(1)], dball.at[other_rows, columns(3)], sibling))
    for copy in shared:
        copy.wait_recv()

    def head_grad(t):
        dotted[at(turned(t), TILE), :] = lax.dot_general(
            dball[at(t, TILE), :], weight_out[...], across, preferred_element_type=F32
        ).astype(BF)

    loop(tiles, head_grad)

    sent_out = [None] + [post.take(1) for _ in (1, 2, 3)]
    outs = []
    for place, m in enumerate((0, 2, 1, 3)):
        value = lax.dot_general(
            att_ref[...], dball[:, place * fc : (place + 1) * fc], over, preferred_element_type=F32
        ).astype(BF)
        if m == 0:
            zo[c] = value
        else:
            n2[(m - 1) * width : m * width, half : half + fc] = value
            staged = n2.at[pl.ds((m - 1) * width, width), pl.ds(half, fc)]
            copy = raw(staged, zo.at[c], sent_out[m], sent_out[m], (d, r, c ^ m))
            copy.start()
            outs.append(copy)

    span = TILE + REACH
    scale = HEAD_DIM ** (-0.5)
    spills = []
    for h in range(width // HEAD_DIM):
        lanes = pl.ds(h * HEAD_DIM, HEAD_DIM)
        value_lanes = pl.ds(width + h * HEAD_DIM, HEAD_DIM)

        def clear(t, lanes=lanes, value_lanes=value_lanes):
            acc[at(t, TILE), lanes] = jnp.zeros((TILE, HEAD_DIM), F32)
            acc[at(t, TILE), value_lanes] = jnp.zeros((TILE, HEAD_DIM), F32)

        loop((group + REACH) // TILE, clear)

        def one(t, lanes=lanes, value_lanes=value_lanes):
            part = at(t, TILE)
            window = pl.ds(pl.multiple_of(t * TILE, TILE), span)
            query, key = q_ref[part, lanes], kv_ref[window, lanes]
            grad = dotted[part, lanes]
            scores = scores_of(query, key)
            query_at = lax.broadcasted_iota(jnp.int32, (TILE, span), 0)
            key_at = lax.broadcasted_iota(jnp.int32, (TILE, span), 1)
            begin = begin_ref[part, 0:1] + (REACH - t * TILE)
            allowed = (key_at <= query_at + REACH) & (key_at >= begin)
            scores = jnp.where(allowed, scores - lse_ref[part, lanes][:, 0:1], NEG_FILL)
            probability = jnp.exp(scores)
            grad_soft = lax.dot_general(grad, kv_ref[window, value_lanes], across, preferred_element_type=F32)
            inner = jnp.sum(probability * grad_soft, axis=1, keepdims=True)
            grad_scores = (probability * (grad_soft - inner)).astype(BF)
            dproj[at(turned(t), TILE), lanes] = (
                jnp.dot(grad_scores, key, preferred_element_type=F32) * scale
            ).astype(BF)
            acc[window, lanes] += lax.dot_general(grad_scores, query, over, preferred_element_type=F32) * scale
            acc[window, value_lanes] += lax.dot_general(
                probability.astype(BF), grad, over, preferred_element_type=F32
            )

        loop(tiles, one)

        def round_spill(t, h=h, lanes=lanes, value_lanes=value_lanes):
            spill[h, at(t, TILE), 0:HEAD_DIM] = acc[at(t, TILE), lanes].astype(BF)
            spill[h, at(t, TILE), HEAD_DIM:] = acc[at(t, TILE), value_lanes].astype(BF)

        loop(REACH // TILE, round_spill)
        copy = post.ready(spill.at[h], spilled.at[h], (lax.rem(d + DP - 1, DP), r, c))
        spills.append(copy)

        @pl.when(d > 0)
        def _(copy=copy):
            copy.start()

    def attention_grads(first_lane, lane_count, dest):
        lanes = slice(first_lane, first_lane + lane_count)
        slots = [None] + [post.take(1) for _ in (1, 2, 3)]
        copies = []
        for place, m in enumerate((0, 2, 1, 3)):
            def tile(t, place=place, m=m):
                left = n1[:, pl.ds(pl.multiple_of(place * fc + t * TILE, TILE), TILE)]
                value = lax.dot_general(left, dproj[:, lanes], over, preferred_element_type=F32).astype(BF)
                if m == 0:
                    dest[c, at(t, TILE), :] = value
                else:
                    dgu[pl.ds(pl.multiple_of(place * fc + t * TILE, TILE), TILE), lanes] = value

            loop(fc // TILE, tile)
            if m:
                copy = raw(
                    dgu.at[pl.ds(place * fc, fc), pl.ds(first_lane, lane_count)], dest.at[c],
                    slots[m], slots[m], (d, r, c ^ m),
                )
                copy.start()
                copies.append(copy)
        return copies

    qs = attention_grads(0, width, zq)

    @pl.when(d < DP - 1)
    def _():
        for copy in spills:
            copy.wait_recv()

    @pl.when(d == DP - 1)
    def _():
        spilled[...] = jnp.zeros_like(spilled)

    for h in range(width // HEAD_DIM):
        for which in (0, 1):
            lanes = pl.ds(which * width + h * HEAD_DIM, HEAD_DIM)
            out_lanes = pl.ds((1 + which) * width + h * HEAD_DIM, HEAD_DIM)

            def whole(t, h=h, which=which, lanes=lanes, out_lanes=out_lanes):
                total = acc[pl.ds(pl.multiple_of(REACH + t * TILE, TILE), TILE), lanes]
                extra = spilled[
                    h, at(jnp.maximum(t - 1, 0), TILE), which * HEAD_DIM : (which + 1) * HEAD_DIM
                ].astype(F32)
                total = total + jnp.where(t > 0, extra, 0.0)
                dproj[at(turned(t), TILE), out_lanes] = total.astype(BF)

            loop(tiles, whole)

    kvs = attention_grads(width, 2 * width, zkv)
    for copy in outs + qs:
        copy.wait_recv()
    first_line = post.take(24)
    line_a = LineSum(raw, ((zq, rq), (zo, ro)), first_line, me)
    line_b = LineSum(raw, ((zkv, rkv),), first_line + 16, me)
    line_a.begin()

    def given_part(t):
        n2[at(t, TILE), 0:half] = lax.dot_general(
            dproj[at(t, TILE), :], weight_in[half:, :], across, preferred_element_type=F32
        ).astype(BF)

    loop(tiles, given_part)
    to_sibling = post.send(n2.at[:, pl.ds(0, half)], arrived, sibling)

    to_sibling.wait_recv()
    for copy in outs:
        copy.wait_send()

    def kept_part(t):
        part = at(t, TILE)
        value = lax.dot_general(
            dproj[part, :], weight_in[:half, :], across, preferred_element_type=F32
        ) + arrived[part, :].astype(F32)
        n2[part, half:] = value.astype(BF)

        @pl.when(t < rows // TILE)
        def _():
            own_f[part, :] = value[:, 0:fc]

    loop(tiles, kept_part)

    pieces, corners, pass_pieces = scatter_plane(
        post, lambda first, count, place: n2.at[pl.ds(first, count), pl.ds(half + place * fc, fc)], landed, rows, me
    )

    def finish(line, z, got_z, dests):
        def one(t):
            value = line.total(z, got_z, at(t, 64))
            for dest, lanes in dests:
                dest[at(t, 64), :] = value[:, lanes]

        loop(z.shape[1] // 64, one)

    line_a.first()
    pieces = pieces + pass_pieces()
    for copy in kvs:
        copy.wait_recv()
    line_b.begin()

    def combine(kind):
        owners.combine(lambda kind, j: n1.at[pl.ds(j * fc, fc), pl.ds(kind * units, units)], 0, (kind,))

    owners.start_near((0,))
    combine(0)
    line_a.last()

    for copy in pieces:
        copy.wait_recv()

    def inner_sum(t):
        part = at(t, 128)
        value = own_f[part, :]
        for n in range(2):
            value = value + landed[n, part, :].astype(F32)
        own_f[part, :] = value
        inner = value * gain_ref[...] * x_ref[part, :].astype(F32)
        sums[0, :, part] = as_row(jnp.sum(inner, axis=1, keepdims=True))

    loop(rows // 128, inner_sum)
    small = [post.send(sums.at[0], sums.at[m], (d, r, c ^ m)) for m in (1, 2, 3)]
    seat = ROW * d + r
    gain_part = jnp.zeros((1, fc), F32)

    def gain_sum(t, total):
        part = at(t, 128)
        value = own_f[part, :] * x_ref[part, :].astype(F32) * scale_ref[part, :]
        return total + jnp.sum(value, axis=0, keepdims=True)

    gain_part = lax.fori_loop(0, rows // 128, gain_sum, gain_part)
    gsum[seat, 0:1, :] = gain_part
    gsum[seat, 1:2, :] = gain_two_ref[...]
    gsum[seat, 2:8, :] = jnp.zeros((6, fc), F32)
    gain_sent = post.take(8)
    gain_got = gain_sent

    def gain_copy(n, j, a):
        return raw(gsum.at[seat], gsum.at[seat], gain_sent + n, gain_got + seat, (d ^ j, r ^ a, c))

    far = [(j, a) for j in range(DP) for a in (0, 1) if (j, a) != (0, 0)]
    for n, (j, a) in enumerate(far):
        gain_copy(n, j, a).start()
    owners.start_near((1,))
    combine(1)
    line_b.rest()
    finish(line_a, zq, rq, ((query_out, slice(None)),))
    finish(line_a, zo, ro, ((out_out, slice(None)),))
    finish(line_b, zkv, rkv, ((key_out, slice(0, width)), (value_out, slice(width, None))))
    for copy in small:
        copy.wait_recv()

    def finish_tokens(t):
        part = at(t, 128)
        inner = as_column(sums[0, :, part] + sums[2, :, part] + sums[1, :, part] + sums[3, :, part])
        scale_rows = scale_ref[part, :]
        value = x_ref[part, :].astype(F32)
        tokens_out[part, :] = (
            mid_ref[part, :] + scale_rows * (own_f[part, :] * gain_ref[...])
            - value * (scale_rows * scale_rows * scale_rows * inner / D)
        )

    loop(rows // 128, finish_tokens)

    for e in range(2 * DP):
        @pl.when(e != seat)
        def _(e=e):
            raw(gsum.at[e], gsum.at[e], gain_sent, gain_got + e, me).wait_recv()

    gains = gsum[0]
    for e in range(1, 2 * DP):
        gains = gains + gsum[e]
    gains_out[...] = gains

    owners.settle()
    line_a.settle()
    line_b.settle()
    for copy in [beside, beyond] + corner + shared + qs + kvs + [to_sibling] + pieces + corners + small:
        copy.wait_send()
    for n, (j, a) in enumerate(far):
        gain_copy(n, j, a).wait_send()

    @pl.when(d > 0)
    def _():
        for copy in spills:
            copy.wait_send()


def backward(x, gain, scale, mid, gain_two, weight_in, weight_out, q, kv, att, lse, begin, normed, n2, dgate, dup):
    rows, fc = x.shape
    group = 2 * rows
    width = q.shape[1]
    units = dgate.shape[1]
    vmem = pl.BlockSpec(memory_space=pltpu.VMEM)
    hbm = pl.BlockSpec(memory_space=pl.ANY)

    def like(shape, dtype=BF):
        return jax.ShapeDtypeStruct(shape, dtype)

    return pl.pallas_call(
        backward_kernel,
        in_specs=[vmem] * 6 + [hbm] * 10,
        out_specs=[vmem] * 6 + [hbm] * 2,
        out_shape=[
            like((rows, fc), F32),
            like((fc, width), F32),
            like((fc, width), F32),
            like((fc, width), F32),
            like((width, fc), F32),
            like((8, fc), F32),
            like((2, 3, fc, units)),
            like((2, 2, fc, units)),
        ],
        scratch_shapes=[
            pltpu.VMEM((D, 3 * width), BF),
            pltpu.VMEM((width, D), BF),
            pltpu.VMEM((group, width), BF),
            pltpu.VMEM((REACH + group, 2 * width), BF),
            pltpu.VMEM((group, width), BF),
            pltpu.VMEM((group, width), F32),
            pltpu.VMEM((group, D), BF),
            pltpu.VMEM((group, D), BF),
            pltpu.VMEM((2 * group, units), BF),
            pltpu.VMEM((group, D), BF),
            pltpu.VMEM((group, width), BF),
            pltpu.VMEM((group, 3 * width), BF),
            pltpu.VMEM((group + REACH, 2 * width), F32),
            pltpu.VMEM((width // HEAD_DIM, REACH, 2 * HEAD_DIM), BF),
            pltpu.VMEM((width // HEAD_DIM, REACH, 2 * HEAD_DIM), BF),
            pltpu.VMEM((2, COL, fc, units), BF),
            pltpu.VMEM((rows, fc), F32),
            pltpu.VMEM((group, 2 * fc), BF),
            pltpu.VMEM((3, rows, fc), BF),
            pltpu.VMEM((DP, fc, width), BF),
            pltpu.VMEM((DP, width, fc), BF),
            pltpu.VMEM((DP, fc, 2 * width), BF),
            pltpu.VMEM((DP + 1, fc, width), BF),
            pltpu.VMEM((DP + 1, width, fc), BF),
            pltpu.VMEM((DP + 1, fc, 2 * width), BF),
            pltpu.VMEM((4, 8, rows), F32),
            pltpu.VMEM((2 * DP, 8, fc), F32),
            pltpu.SemaphoreType.DMA((POSTS,)),
            pltpu.SemaphoreType.DMA((POSTS,)),
            pltpu.SemaphoreType.DMA((20,)),
        ],
        compiler_params=pltpu.CompilerParams(
            collective_id=2, has_side_effects=True, vmem_limit_bytes=62 << 20
        ),
        cost_estimate=pl.CostEstimate(
            flops=12 * group * D * width + 4 * group * D * units, bytes_accessed=64 << 20, transcendentals=0
        ),
    )(x, gain, scale, mid, gain_two, begin, weight_in, weight_out, q, kv, att, lse, normed, n2, dgate, dup)


def closing_kernel(
    tokens, query, key, value, out, hidden, down, gains,
    tokens_out, query_out, key_out, value_out, out_out, gate_out, up_out, down_out, one_out, two_out,
):
    for src, dst in (
        (tokens, tokens_out), (query, query_out), (key, key_out), (value, value_out), (out, out_out)
    ):
        dst[...] = src[...]
    for dst, kind in ((gate_out, 0), (up_out, 1)):
        dst[...] = hidden[kind, 0].astype(F32) + hidden[kind, 1].astype(F32) + hidden[kind, 2].astype(F32)
    one_out[...] = gains[0]
    two_out[...] = gains[1]
    down_out[...] = down[0, 0].astype(F32) + down[0, 1].astype(F32) + down[0, 2].astype(F32)


def closing(tokens, query, key, value, out, hidden, down, gains):
    steps = 4

    def rows_of(array):
        rows, width = array.shape[-2:]
        lead = array.shape[:-2]
        return pl.BlockSpec(lead + (rows // steps, width), lambda t: (0,) * len(lead) + (t, 0))

    finals = [tokens, query, key, value, out] + [
        jax.ShapeDtypeStruct(a.shape[-2:], F32) for a in (hidden, hidden, down)
    ]
    return pl.pallas_call(
        closing_kernel,
        grid=(steps,),
        in_specs=[rows_of(a) for a in (tokens, query, key, value, out, hidden, down)]
        + [pl.BlockSpec(gains.shape, lambda t: (0, 0))],
        out_specs=[rows_of(a) for a in finals] + [pl.BlockSpec(gains.shape[1:], lambda t: (0,))] * 2,
        out_shape=[jax.ShapeDtypeStruct(a.shape, F32) for a in finals]
        + [jax.ShapeDtypeStruct(gains.shape[1:], F32)] * 2,
        compiler_params=pltpu.CompilerParams(vmem_limit_bytes=62 << 20),
    )(tokens, query, key, value, out, hidden, down, gains)


def on_small_mesh(
    tokens,
    cotangent,
    query_master,
    key_master,
    value_master,
    out_master,
    gate_master,
    up_master,
    down_master,
    attn_gain,
    ffn_gain,
    lengths,
    permutation,
):
    del permutation
    (
        mid, scale_two, n2, begin, scale_one, normed_one, weight_in, weight_out, q, key_value,
        own_attended, lse, own_up, weight_gate, weight_up, grad_all,
    ) = forward(
        tokens, attn_gain[None, :], ffn_gain[None, :], lengths, query_master, key_master,
        value_master, out_master, gate_master, up_master, cotangent,
    )
    grad_mid, gain_two_part, got_down, _, normed_two, grad_gate, grad_up = middle(
        n2, mid, scale_two, ffn_gain[None, :], cotangent, down_master, own_up, weight_gate,
        weight_up, grad_all,
    )
    grad_tokens, grad_query, grad_key, grad_value, grad_out, gains, got, _ = backward(
        tokens, attn_gain[None, :], scale_one, grad_mid, gain_two_part, weight_in, weight_out, q,
        key_value, own_attended, lse, begin, normed_one, normed_two, grad_gate, grad_up,
    )
    return closing(grad_tokens, grad_query, grad_key, grad_value, grad_out, got, got_down, gains)


def solution(mesh):
    placed = (
        P(("dp", "row"), "col"),
        P(("dp", "row"), "col"),
        P("col", ("row", "dp")),
        P("col", ("row", "dp")),
        P("col", ("row", "dp")),
        P(("row", "dp"), "col"),
        P("col", ("row", "dp")),
        P("col", ("row", "dp")),
        P(("row", "dp"), "col"),
        P("col"),
        P("col"),
        P(),
        P(),
    )
    small = tuple(mesh.shape[name] for name in AXES) == (DP, ROW, COL)
    return jax.shard_map(
        on_small_mesh if small else on_any_mesh,
        mesh=mesh,
        in_specs=placed,
        out_specs=(
            P(("dp", "row"), "col"),
            P("col", ("row", "dp")),
            P("col", ("row", "dp")),
            P("col", ("row", "dp")),
            P(("row", "dp"), "col"),
            P("col", ("row", "dp")),
            P("col", ("row", "dp")),
            P(("row", "dp"), "col"),
            P("col"),
            P("col"),
        ),
        check_vma=False,
    )
```

```python
import functools

import jax
import jax.numpy as jnp
from jax import lax
from jax.experimental import pallas as pl
from jax.experimental.pallas import tpu as pltpu
from jax.sharding import PartitionSpec as P

D = 2048
HEAD_DIM = 128


EPSILON = 1e-06
NEG_FILL = -1e30
AXES = ("dp", "row", "col")
DP, ROW, COL = 4, 2, 4
REACH = 768
BF = jnp.bfloat16
F32 = jnp.float32


def running_sum(lengths):
    count = lengths.shape[0]
    earlier = jnp.arange(count)[:, None] <= jnp.arange(count)[None, :]
    return jnp.sum(jnp.where(earlier, lengths[:, None], 0), axis=0)

def make_picker(wanted, carried, pieces):
    amount = pieces[0].shape[0]
    inside = (wanted >= 0) & (wanted < amount)
    chosen = jnp.clip(wanted, 0, amount - 1)
    return tuple(
        (
            jnp.where(inside[:, None], jnp.take(shard_rows, chosen, axis=0), current)
            for shard_rows, current in zip(pieces, carried)
        )
    )


def sequence_marks(permutation, lengths, first_slot, amount):
    source = lax.dynamic_slice_in_dim(permutation, first_slot, amount)
    seq_ends = running_sum(lengths)
    passed = seq_ends[None, :] <= source[:, None]
    member = jnp.sum(passed.astype(jnp.int32), axis=1)
    begins = jnp.max(jnp.where(passed, seq_ends[None, :], 0), axis=1)
    return (member, source - begins)


def col_total(values):
    return lax.psum(jnp.sum(values, axis=1), "col")


def row_gather(values):
    return lax.all_gather(values, "row", axis=0, tiled=True)


def col_gather(values):
    return lax.all_gather(values, "col", axis=0, tiled=True)


def key_gather(keys_here, values_here):
    return (
        lax.all_gather(keys_here, "col", axis=0, tiled=True),
        lax.all_gather(values_here, "col", axis=0, tiled=True),
    )


def multiply(row_block, weight, transpose_right):
    if transpose_right:
        return lax.dot_general(
            row_block, weight, (((1,), (1,)), ((), ())), preferred_element_type=jnp.float32
        )
    return jnp.dot(row_block, weight, preferred_element_type=jnp.float32)


def outer_sum(left_rows, right_rows):
    return lax.dot_general(
        left_rows, right_rows, (((0,), (0,)), ((), ())), preferred_element_type=jnp.float32
    )


def col_reduce(spread, weight, transpose_right):
    return lax.psum_scatter(
        multiply(spread, weight, transpose_right), "col", scatter_dimension=0, tiled=True
    )


def row_reduce(spread, weight, transpose_right):
    return lax.psum_scatter(
        multiply(spread, weight, transpose_right), "row", scatter_dimension=0, tiled=True
    )


def visible(query_member, query_position, member, position):
    same = query_member[:, None] == member[None, :]
    behind = position[None, :] <= query_position[:, None]
    return same & behind


def attend_scores(query_block, key_all, allowed):
    scores = jnp.einsum(
        "qhd,khd->hqk", query_block, key_all, preferred_element_type=jnp.float32
    ) * HEAD_DIM ** (-0.5)
    return jnp.where(allowed[None, :, :], scores, NEG_FILL)


def norm_back(grad_normed, inputs_f, scale_rows, gain):
    gain_part = jnp.sum(grad_normed * inputs_f * scale_rows[:, None], axis=0)
    scaled = grad_normed * gain[None, :]
    inner = col_total(scaled * inputs_f)
    grad_inputs = scale_rows[:, None] * scaled - inputs_f * (scale_rows**3 * inner / D)[:, None]
    return (grad_inputs, gain_part)


def on_any_mesh(
    tokens,
    cotangent,
    query_master,
    key_master,
    value_master,
    out_master,
    gate_master,
    up_master,
    down_master,
    attn_gain,
    ffn_gain,
    lengths,
    permutation,
):
    own_rows = tokens.shape[0]
    group_rows = own_rows * lax.axis_size("row")
    quarter = group_rows // lax.axis_size("col")
    device_slot = lax.axis_index(("dp", "row"))
    group_slot = lax.axis_index("dp")
    col_slot = lax.axis_index("col")
    own_sources = lax.dynamic_slice_in_dim(permutation, device_slot * own_rows, own_rows)
    own_tokens, own_cotangent = make_picker(
        own_sources,
        (jnp.zeros_like(tokens), jnp.zeros_like(cotangent)),
        (
            lax.all_gather(tokens, ("dp", "row"), axis=0, tiled=True),
            lax.all_gather(cotangent, ("dp", "row"), axis=0, tiled=True),
        ),
    )
    masters = tuple(
        (
            matrix.astype(jnp.bfloat16)
            for matrix in (
                query_master,
                key_master,
                value_master,
                out_master,
                gate_master,
                up_master,
                down_master,
            )
        )
    )
    query_weight, key_weight, value_weight, out_weight, gate_weight, up_weight, down_weight = (
        lax.all_gather(masters[0], "dp", axis=1, tiled=True),
        lax.all_gather(masters[1], "dp", axis=1, tiled=True),
        lax.all_gather(masters[2], "dp", axis=1, tiled=True),
        lax.all_gather(masters[3], "dp", axis=0, tiled=True),
        lax.all_gather(masters[4], "dp", axis=1, tiled=True),
        lax.all_gather(masters[5], "dp", axis=1, tiled=True),
        lax.all_gather(masters[6], "dp", axis=0, tiled=True),
    )
    attention_in = jnp.concatenate([query_weight, key_weight, value_weight], axis=1)
    feedforward_in = jnp.concatenate([gate_weight, up_weight], axis=1)
    width_row = query_weight.shape[1]
    heads_row = width_row // HEAD_DIM
    hidden_row = gate_weight.shape[1]
    member, position = sequence_marks(permutation, lengths, group_slot * group_rows, group_rows)
    query_member = lax.dynamic_slice_in_dim(member, col_slot * quarter, quarter)
    query_position = lax.dynamic_slice_in_dim(position, col_slot * quarter, quarter)
    block_rows = min(512, quarter)
    block_count = quarter // block_rows
    residual_in = own_tokens.astype(jnp.float32)
    scale_one = lax.rsqrt(col_total(residual_in * residual_in) / D + EPSILON)
    normed_one = (residual_in * scale_one[:, None] * attn_gain[None, :]).astype(jnp.bfloat16)
    spread_one = row_gather(normed_one)
    projected = col_reduce(spread_one, attention_in, False).astype(jnp.bfloat16)
    queries = projected[:, :width_row].reshape(quarter, heads_row, HEAD_DIM)
    keys_here = projected[:, width_row : 2 * width_row]
    values_here = projected[:, 2 * width_row :]
    key_flat, value_flat = key_gather(keys_here, values_here)
    key_all = key_flat.reshape(group_rows, heads_row, HEAD_DIM)
    value_all = value_flat.reshape(group_rows, heads_row, HEAD_DIM)

    def block_mask(first_row):
        return visible(
            lax.dynamic_slice_in_dim(query_member, first_row, block_rows),
            lax.dynamic_slice_in_dim(query_position, first_row, block_rows),
            member,
            position,
        )

    def forward_block(block_id):
        first_row = block_id * block_rows
        query_block = lax.dynamic_slice_in_dim(queries, first_row, block_rows, 0)
        scores = attend_scores(query_block, key_all, block_mask(first_row))
        highest = jnp.max(scores, axis=2, keepdims=True)
        totals = jnp.sum(jnp.exp(scores - highest), axis=2, keepdims=True)
        log_total = highest + jnp.log(totals)
        probability = jnp.exp(scores - log_total)
        output = jnp.einsum(
            "hqk,khd->qhd",
            probability.astype(jnp.bfloat16),
            value_all,
            preferred_element_type=jnp.float32,
        )
        return (output.astype(jnp.bfloat16).reshape(block_rows, width_row), log_total[:, :, 0])

    blocks_out, log_totals = lax.map(forward_block, jnp.arange(block_count, dtype=jnp.int32))
    attended = blocks_out.reshape(quarter, width_row)
    spread_attn = col_gather(attended)
    midway = residual_in + row_reduce(spread_attn, out_weight, False)
    scale_two = lax.rsqrt(col_total(midway * midway) / D + EPSILON)
    normed_two = (midway * scale_two[:, None] * ffn_gain[None, :]).astype(jnp.bfloat16)
    spread_two = row_gather(normed_two)
    gate_and_up = col_reduce(spread_two, feedforward_in, False)
    gate_value = gate_and_up[:, :hidden_row]
    up_value = gate_and_up[:, hidden_row:]
    sigmoid_gate = jax.nn.sigmoid(gate_value)
    hidden = (gate_value * sigmoid_gate * up_value).astype(jnp.bfloat16)
    grad_output = own_cotangent.astype(jnp.float32)
    spread_down = row_gather(own_cotangent)
    grad_hidden = col_reduce(spread_down, down_weight, True)
    spread_hidden = col_gather(hidden)
    grad_down = outer_sum(spread_hidden, spread_down)
    grad_gate_value = (
        grad_hidden * up_value * sigmoid_gate * (1.0 + gate_value * (1.0 - sigmoid_gate))
    ).astype(jnp.bfloat16)
    grad_up_value = (grad_hidden * gate_value * sigmoid_gate).astype(jnp.bfloat16)
    spread_gate_up = col_gather(jnp.concatenate([grad_gate_value, grad_up_value], axis=1))
    grad_normed_two = row_reduce(spread_gate_up, feedforward_in, True)
    spread_two = row_gather(normed_two)
    grad_feedforward = outer_sum(spread_two, spread_gate_up)
    grad_mid_norm, gain_two_part = norm_back(grad_normed_two, midway, scale_two, ffn_gain)
    grad_midway = grad_output + grad_mid_norm
    rounded_midway = grad_midway.astype(jnp.bfloat16)
    spread_back = row_gather(rounded_midway)
    grad_attended = col_reduce(spread_back, out_weight, True).astype(jnp.bfloat16)
    spread_attn = col_gather(attended)
    key_flat, value_flat = key_gather(keys_here, values_here)
    key_all = key_flat.reshape(group_rows, heads_row, HEAD_DIM)
    value_all = value_flat.reshape(group_rows, heads_row, HEAD_DIM)
    grad_out_local = outer_sum(spread_attn, spread_back)

    def backward_block(carried, block_id):
        first_row = block_id * block_rows
        query_block = lax.dynamic_slice_in_dim(queries, first_row, block_rows, 0)
        scores = attend_scores(query_block, key_all, block_mask(first_row))
        probability = jnp.exp(
            scores - lax.dynamic_index_in_dim(log_totals, block_id, 0, keepdims=False)[:, :, None]
        )
        weights_low = probability.astype(jnp.bfloat16)
        grad_block = lax.dynamic_slice_in_dim(grad_attended, first_row, block_rows, 0).reshape(
            block_rows, heads_row, HEAD_DIM
        )
        grad_soft = jnp.einsum(
            "qhd,khd->hqk", grad_block, value_all, preferred_element_type=jnp.float32
        )
        row_inner = jnp.sum(probability * grad_soft, axis=2, keepdims=True)
        grad_scores = (probability * (grad_soft - row_inner)).astype(jnp.bfloat16)
        grad_query_block = jnp.einsum(
            "hqk,khd->qhd", grad_scores, key_all, preferred_element_type=jnp.float32
        ) * HEAD_DIM ** (-0.5)
        grad_key_all = carried[0] + jnp.einsum(
            "hqk,qhd->khd", grad_scores, query_block, preferred_element_type=jnp.float32
        ) * HEAD_DIM ** (-0.5)
        grad_value_all = carried[1] + jnp.einsum(
            "hqk,qhd->khd", weights_low, grad_block, preferred_element_type=jnp.float32
        )
        return (
            (grad_key_all, grad_value_all),
            grad_query_block.astype(jnp.bfloat16).reshape(block_rows, width_row),
        )

    start_grads = jnp.zeros((group_rows, heads_row, HEAD_DIM), jnp.float32)
    key_value_grads, grad_queries = lax.scan(
        backward_block, (start_grads, start_grads), jnp.arange(block_count, dtype=jnp.int32)
    )
    grad_queries = grad_queries.reshape(quarter, width_row)
    grad_key_part = key_value_grads[0].reshape(group_rows, width_row)
    grad_value_part = key_value_grads[1].reshape(group_rows, width_row)
    grad_key_mine, grad_value_mine = (
        lax.psum_scatter(grad_key_part, "col", scatter_dimension=0, tiled=True),
        lax.psum_scatter(grad_value_part, "col", scatter_dimension=0, tiled=True),
    )
    spread_projected = col_gather(
        jnp.concatenate(
            [
                grad_queries,
                grad_key_mine.astype(jnp.bfloat16),
                grad_value_mine.astype(jnp.bfloat16),
            ],
            axis=1,
        )
    )
    grad_normed_one = row_reduce(spread_projected, attention_in, True)
    spread_one = row_gather(normed_one)
    grad_attention = outer_sum(spread_one, spread_projected)
    grad_in_norm, gain_one_part = norm_back(grad_normed_one, residual_in, scale_one, attn_gain)
    grad_own_tokens = grad_midway + grad_in_norm
    grad_attn_gain, grad_ffn_gain = lax.psum((gain_one_part, gain_two_part), ("dp", "row"))
    grad_query, grad_key, grad_value, grad_out, grad_gate, grad_up, grad_down_mine = (
        lax.psum_scatter(
            grad_attention[:, :width_row].astype(jnp.bfloat16),
            "dp",
            scatter_dimension=1,
            tiled=True,
        ).astype(jnp.float32),
        lax.psum_scatter(
            grad_attention[:, width_row : 2 * width_row].astype(jnp.bfloat16),
            "dp",
            scatter_dimension=1,
            tiled=True,
        ).astype(jnp.float32),
        lax.psum_scatter(
            grad_attention[:, 2 * width_row :].astype(jnp.bfloat16),
            "dp",
            scatter_dimension=1,
            tiled=True,
        ).astype(jnp.float32),
        lax.psum_scatter(
            grad_out_local.astype(jnp.bfloat16), "dp", scatter_dimension=0, tiled=True
        ).astype(jnp.float32),
        lax.psum_scatter(
            grad_feedforward[:, :hidden_row].astype(jnp.bfloat16),
            "dp",
            scatter_dimension=1,
            tiled=True,
        ).astype(jnp.float32),
        lax.psum_scatter(
            grad_feedforward[:, hidden_row:].astype(jnp.bfloat16),
            "dp",
            scatter_dimension=1,
            tiled=True,
        ).astype(jnp.float32),
        lax.psum_scatter(
            grad_down.astype(jnp.bfloat16), "dp", scatter_dimension=0, tiled=True
        ).astype(jnp.float32),
    )
    total_tokens = permutation.shape[0]
    inverse = (
        jnp.zeros((total_tokens,), jnp.int32)
        .at[permutation]
        .set(jnp.arange(total_tokens, dtype=jnp.int32))
    )
    wanted_slots = lax.dynamic_slice_in_dim(inverse, device_slot * own_rows, own_rows)
    (grad_tokens,) = make_picker(
        wanted_slots,
        (jnp.zeros_like(grad_own_tokens),),
        (
            (
                lax.all_gather(
                    grad_own_tokens.astype(jnp.bfloat16), ("dp", "row"), axis=0, tiled=True
                ),
            )[0].astype(jnp.float32),
        ),
    )
    return (
        grad_tokens,
        grad_query,
        grad_key,
        grad_value,
        grad_out,
        grad_gate,
        grad_up,
        grad_down_mine,
        grad_attn_gain,
        grad_ffn_gain,
    )


def scores_of(query, key):
    return lax.dot_general(
        query, key, (((1,), (1,)), ((), ())), preferred_element_type=F32
    ) * HEAD_DIM ** (-0.5)


MESH = pl.DeviceIdType.MESH
PLACE = {0: 0, 2: 1, 1: 2, 3: 3}
TILE = 256


class Post:
    def __init__(self, send_sem, recv_sem):
        self.send_sem, self.recv_sem, self.used = send_sem, recv_sem, 0

    def ready(self, src, dst, target, slot=None):
        if slot is None:
            slot = self.used
            self.used += 1
        return pltpu.make_async_remote_copy(
            src_ref=src,
            dst_ref=dst,
            send_sem=self.send_sem.at[slot],
            recv_sem=self.recv_sem.at[slot],
            device_id=target,
            device_id_type=MESH,
        )

    def take(self, count):
        first = self.used
        self.used += count
        return first

    def send(self, src, dst, target):
        copy = self.ready(src, dst, target)
        copy.start()
        return copy


def greet(peers):
    barrier = pltpu.get_barrier_semaphore()
    for peer in peers:
        pl.semaphore_signal(barrier, inc=1, device_id=peer, device_id_type=MESH)
    pl.semaphore_wait(barrier, len(peers))


def as_row(column):
    return jnp.transpose(jnp.broadcast_to(column, (column.shape[0], 128)))[0:8]


def as_column(row):
    return jnp.transpose(row)[:, 0:1]


def scatter_plane(post, low, landed, rows, me):
    d, r, c = me
    half = rows // 2
    x_at, y_at = (d, r ^ 1, c), (d, r, c ^ 2)
    upper, lower = pl.ds(0, half), pl.ds(half, half)
    corner_x = post.send(low(rows, half, 1), landed.at[2, upper], x_at)
    corner_y = post.send(low(rows + half, half, 1), landed.at[2, lower], y_at)
    sent = [
        post.send(low(rows, half, 0), landed.at[0, upper], x_at),
        post.send(low(half, half, 1), landed.at[1, lower], y_at),
    ]

    def add(ref, first):
        def one(t, total):
            part = pl.ds(pl.multiple_of(t * 64, 64), 64)
            there = pl.ds(pl.multiple_of(first + t * 64, 64), 64)
            ref[part, :] = (ref[part, :].astype(F32) + landed[2, there, :].astype(F32)).astype(BF)
            return total

        lax.fori_loop(0, half // 64, one, 0)

    def pass_pieces():
        corner_x.wait_recv()
        add(low(0, half, 1), 0)
        later = [post.send(low(0, half, 1), landed.at[1, upper], y_at)]
        corner_y.wait_recv()
        add(low(rows + half, half, 0), half)
        later.append(post.send(low(rows + half, half, 0), landed.at[0, lower], x_at))
        return later

    return sent, [corner_x, corner_y], pass_pieces


def forward_kernel(
    x_ref, gain_one_ref, gain_two_ref, lengths_ref, query_ref, key_ref, value_ref, out_ref, gate_hbm, up_hbm,
    own_grad,
    mid_ref, scale_ref, n2_ref, begin_ref, first_scale,
    normed_out, weight_in_out, weight_out_out, q_out, kv_out, att_out, lse_out, own_up, gate_all, up_all, grad_all,
    normed_ref, weight_in, weight_out, q_ref, kv_ref, att_ref, lse_ref, masters,
    zin, zout, sums, wide, given, arrived, low, landed, x32, hidden_own,
    send_sem, recv_sem, local_sem,
):
    d, r, c = (lax.axis_index(name) for name in AXES)
    y, core = c // 2, lax.rem(c, 2)
    rows = x_ref.shape[0]
    fc = x_ref.shape[1]
    group = 2 * rows
    width = q_ref.shape[1]
    half = 2 * fc
    post = Post(send_sem, recv_sem)
    fetches = [
        pltpu.make_async_copy(src, masters.at[n], local_sem.at[8 + n]) for n, src in enumerate((gate_hbm, up_hbm))
    ]
    for copy in fetches:
        copy.start()
    copies = []

    def copy_out(src, dst):
        copy = pltpu.make_async_copy(src, dst, local_sem.at[10 + len(copies)])
        copy.start()
        copies.append(copy)

    in_plane = [(d, r ^ a, c ^ b) for a in (0, 1) for b in range(COL) if (a, b) != (0, 0)]
    greet([(d ^ j, r, c) for j in (1, 2, 3)] + in_plane)

    def fill_x(t, total):
        part = pl.ds(pl.multiple_of(t * 128, 128), 128)
        value = x_ref[part, :].astype(F32)
        x32[part, :] = value
        sums[0, :, part] = as_row(jnp.sum(value * value, axis=1, keepdims=True))
        return total

    lax.fori_loop(0, rows // 128, fill_x, 0)
    small = [post.send(sums.at[0], sums.at[m], (d, r, c ^ m)) for m in (1, 2, 3)]

    parts = (pl.ds(width, 2 * width), pl.ds(0, width))
    first, first_down = post.take(3 * DP), post.take(3 * DP)

    def block_of(n, p):
        return zin.at[p, :, parts[n]] if n < 2 else zout.at[p]

    def line(n, p, target_plane):
        block = block_of(n, p)
        return post.ready(block, block, (target_plane, r, c), first + DP * n + p)

    def line_down(n, p, target_plane):
        block = block_of(n, p)
        return pltpu.make_async_remote_copy(
            src_ref=block, dst_ref=block,
            send_sem=send_sem.at[first_down + DP * n + p], recv_sem=recv_sem.at[first + DP * n + p],
            device_id=(target_plane, r, c), device_id_type=MESH,
        )

    def cast_rows(src, dst, amount, step=64):
        def one(t, total):
            part = pl.ds(pl.multiple_of(t * step, step), step)
            dst(part, src[part, :].astype(BF))
            return total

        lax.fori_loop(0, amount // step, one, 0)

    for place, master in enumerate((query_ref, key_ref, value_ref)):
        def put(part, value, place=place):
            zin[d, part, place * width : (place + 1) * width] = value

        cast_rows(master, put, fc)
    def leave(n):
        @pl.when(d < DP - 1)
        def _():
            line(n, d, d + 1).start()

        @pl.when(d > 0)
        def _():
            line_down(n, d, d - 1).start()

    leave(0)
    leave(1)

    first_cols = post.take(3 * DP)

    def place_of(m):
        return lax.rem(m, 2) * 2 + m // 2

    def seat_of(n, place):
        there = pl.ds(pl.multiple_of(place * fc, fc), fc)
        return weight_in.at[there, parts[n]] if n < 2 else weight_out.at[:, there]

    def to_column(n, p):
        return pltpu.make_async_remote_copy(
            src_ref=block_of(n, p),
            dst_ref=seat_of(n, place_of(p ^ c)),
            send_sem=send_sem.at[first_cols + DP * n + p],
            recv_sem=recv_sem.at[first_cols + DP * n + (p ^ c)],
            device_id=(d, r, p), device_id_type=MESH,
        )

    def keep(n):
        return pltpu.make_async_copy(block_of(n, c), seat_of(n, 0), local_sem.at[(0, 1, 5)[n]])

    def pass_on(n, p):
        @pl.when(p == c)
        def _():
            keep(n).start()

        @pl.when(p != c)
        def _():
            to_column(n, p).start()

    hidden_all = (gate_all, up_all)
    first_sent = post.take(10)
    first_got = first_sent

    def slab(kind, i):
        return hidden_all[kind].at[pl.ds(pl.multiple_of(place_of(i) * fc, fc), fc), :]

    def ship(kind, way, i, target, src=None):
        return pltpu.make_async_remote_copy(
            src_ref=hidden_own.at[kind] if src is None else src,
            dst_ref=slab(kind, i),
            send_sem=send_sem.at[first_sent + 5 * kind + way],
            recv_sem=recv_sem.at[first_got + 4 * kind + i],
            device_id=target, device_id_type=MESH,
        )

    def keep_hidden(kind):
        return pltpu.make_async_copy(hidden_own.at[kind], slab(kind, 0), local_sem.at[3 + kind])

    def to_core(kind):
        return ship(kind, 0, 1, (d, r, c ^ 1))

    first_half = post.take(8)

    def gate_half(i, n):
        step = fc // 2
        return gate_all.at[pl.ds(pl.multiple_of(place_of(i) * fc + n * step, step), step), :]

    def over_y(n):
        return pltpu.make_async_remote_copy(
            src_ref=hidden_own.at[0, pl.ds(n * (fc // 2), fc // 2), :], dst_ref=gate_half(2 + core, n),
            send_sem=send_sem.at[first_half + 4 * n], recv_sem=recv_sem.at[first_half + 4 * n + core],
            device_id=(d, r, 2 * (1 - y)), device_id_type=MESH,
        )

    def over_x(kind):
        return ship(kind, 2, 1 - core, (d, r ^ 1, 2 * y + 1))

    def relay(n, i):
        return pltpu.make_async_remote_copy(
            src_ref=gate_half(i, n), dst_ref=gate_half(5 - i, n),
            send_sem=send_sem.at[first_half + 4 * n + i - 1],
            recv_sem=recv_sem.at[first_half + 4 * n + 3 - i],
            device_id=(d, r ^ 1, 2 * y + 1), device_id_type=MESH,
        )

    def gate_came(n, i):
        return pltpu.make_async_remote_copy(
            src_ref=gate_half(i, n), dst_ref=gate_half(i, n),
            send_sem=send_sem.at[first_half], recv_sem=recv_sem.at[first_half + 4 * n + i - 2],
            device_id=(d, r, c), device_id_type=MESH,
        )

    def start_home(kind):
        @pl.when(core == 0)
        def _():
            keep_hidden(kind).start()

        @pl.when(core == 1)
        def _():
            to_core(kind).start()

    def start_relay(n):
        @pl.when(core == 0)
        def _():
            for i in (2, 3):
                gate_came(n, i).wait_recv()
                relay(n, i).start()

    def cast_hidden(kind):
        def put(part, value):
            hidden_own[kind, part, :] = value

        fetches[kind].wait()
        cast_rows(masters.at[kind], put, fc)

    cast_hidden(0)
    over_x(0).start()
    over_y(0).start()
    for copy in small:
        copy.wait_recv()

    def norm_one(t, total):
        part = pl.ds(pl.multiple_of(t * 128, 128), 128)
        square = sums[0, :, part] + sums[2, :, part] + sums[1, :, part] + sums[3, :, part]
        scale = lax.rsqrt(as_column(square) / D + EPSILON)
        first_scale[part, :] = scale
        normed_ref[part, 0:fc] = (x32[part, :] * scale * gain_one_ref[...]).astype(BF)
        return total

    lax.fori_loop(0, rows // 128, norm_one, 0)
    own_rows, other_rows = pl.ds(0, rows), pl.ds(rows, rows)

    def columns(place):
        return pl.ds(place * fc, fc)

    own_block = normed_ref.at[own_rows, columns(0)]
    beside = post.send(own_block, normed_ref.at[other_rows, columns(0)], (d, r ^ 1, c))
    beyond = post.send(own_block, normed_ref.at[own_rows, columns(1)], (d, r, c ^ 2))
    corner = post.send(own_block, normed_ref.at[other_rows, columns(1)], (d, r ^ 1, c ^ 2))
    sibling = (d, r, c ^ 1)
    shared = [post.send(own_block, normed_ref.at[own_rows, columns(2)], sibling)]
    pass_on(0, d)
    pass_on(1, d)
    cast_hidden(1)
    start_home(0)
    start_home(1)
    copy_out(hidden_own.at[1], own_up)
    over_x(1).start()
    half_rows = rows // 2
    grad_cross = post.send(
        own_grad.at[pl.ds(pl.multiple_of((1 - y) * half_rows, half_rows), half_rows), :],
        grad_all.at[pl.ds(0, half_rows), pl.ds(fc, fc)],
        (d, r, c ^ 2),
    )
    grad_keep = pltpu.make_async_copy(
        own_grad.at[pl.ds(pl.multiple_of(y * half_rows, half_rows), half_rows), :],
        grad_all.at[pl.ds(0, half_rows), pl.ds(0, fc)],
        local_sem.at[2],
    )
    grad_keep.start()

    def put_out(part, value):
        zout[d, part, :] = value

    cast_rows(out_ref, put_out, width)

    def find_begins(t, total):
        part = pl.ds(pl.multiple_of(t * 128, 128), 128)
        place = lax.broadcasted_iota(jnp.int32, (128, 1), 0) + (d * group + t * 128)
        end = jnp.int32(0)
        begin = jnp.zeros((128, 1), jnp.int32)
        for n in range(lengths_ref.shape[0]):
            end = end + lengths_ref[n]
            begin = jnp.where(place >= end, end, begin)
        begin_ref[part, :] = begin - d * group
        return total

    lax.fori_loop(0, group // 128, find_begins, 0)

    def line_step(s, which=(0, 1)):
        for n in which:
            for p, valid, onward, forward in (
                (d - s, d - s >= 0, d < DP - 1, lambda n, p: line(n, p, d + 1)),
                (d + s, d + s < DP, d > 0, lambda n, p: line_down(n, p, d - 1)),
            ):
                @pl.when(valid)
                def _(n=n, p=p, onward=onward, forward=forward):
                    line(n, p, d).wait_recv()

                    @pl.when(onward)
                    def _():
                        forward(n, p).start()

                    pass_on(n, p)

    line_step(1)
    leave(2)
    line_step(2)
    pass_on(2, d)
    line_step(1, (2,))
    for copy, where, place in ((beside, other_rows, 0), (beyond, own_rows, 1), (corner, other_rows, 1)):
        copy.wait_recv()
        shared.append(
            post.send(normed_ref.at[where, columns(place)], normed_ref.at[where, columns(place + 2)], sibling)
        )
    line_step(3)
    line_step(2, (2,))
    start_relay(0)

    def arrived_blocks(n):
        keep(n).wait()
        for m in (1, 2, 3):
            pltpu.make_async_remote_copy(
                src_ref=block_of(n, 0), dst_ref=seat_of(n, 0),
                send_sem=send_sem.at[first_cols], recv_sem=recv_sem.at[first_cols + DP * n + m],
                device_id=(d, r, c), device_id_type=MESH,
            ).wait_recv()

    for copy in shared:
        copy.wait_recv()
    arrived_blocks(0)
    over_y(1).start()
    copy_out(normed_ref, normed_out)

    def turned(t):
        return lax.rem(t + 2 * r, group // TILE)

    def project_kv(t, total):
        part = pl.ds(pl.multiple_of(t * TILE, TILE), TILE)
        to = pl.ds(pl.multiple_of(REACH + turned(t) * TILE, TILE), TILE)
        kv_ref[to, :] = jnp.dot(
            normed_ref[part, :], weight_in[:, width:], preferred_element_type=F32
        ).astype(BF)
        return total

    lax.fori_loop(0, group // TILE, project_kv, 0)
    halo = post.ready(kv_ref.at[pl.ds(group, REACH), :], kv_ref.at[pl.ds(0, REACH), :], (lax.rem(d + 1, DP), r, c))

    @pl.when(d < DP - 1)
    def _():
        halo.start()

    arrived_blocks(1)

    def project_q(t, total):
        part = pl.ds(pl.multiple_of(t * TILE, TILE), TILE)
        to = pl.ds(pl.multiple_of(turned(t) * TILE, TILE), TILE)
        q_ref[to, :] = jnp.dot(
            normed_ref[part, :], weight_in[:, :width], preferred_element_type=F32
        ).astype(BF)
        return total

    lax.fori_loop(0, group // TILE, project_q, 0)

    copy_out(weight_in, weight_in_out)
    copy_out(q_ref, q_out)
    line_step(3, (2,))
    @pl.when(d == 0)
    def _():
        kv_ref[pl.ds(0, REACH), :] = jnp.zeros((REACH, 2 * width), BF)

    @pl.when(d > 0)
    def _():
        halo.wait_recv()

    copy_out(kv_ref, kv_out)

    grads = [
        post.ready(
            grad_all.at[pl.ds(0, half_rows), pl.ds(0, half)],
            grad_all.at[pl.ds(j * half_rows, half_rows), pl.ds(0, half)],
            (d ^ j, r, c),
        )
        for j in (1, 2, 3)
    ]
    grads_shared = [
        post.ready(
            grad_all.at[pl.ds(0, half_rows), pl.ds(0, half)],
            grad_all.at[pl.ds(0, half_rows), pl.ds(half, half)],
            sibling,
        )
    ]

    def spread_grads():
        grad_cross.wait_recv()
        grad_keep.wait()
        for copy in grads + grads_shared[:1]:
            copy.start()

    pl.when(lax.rem(d, 2) == 1)(spread_grads)

    span = TILE + REACH
    for h in range(width // HEAD_DIM):
        lanes = pl.ds(h * HEAD_DIM, HEAD_DIM)
        value_lanes = pl.ds(width + h * HEAD_DIM, HEAD_DIM)

        def one(t, total, lanes=lanes, value_lanes=value_lanes):
            part = pl.ds(pl.multiple_of(t * TILE, TILE), TILE)
            to = pl.ds(pl.multiple_of(turned(t) * TILE, TILE), TILE)
            window = pl.ds(pl.multiple_of(t * TILE, TILE), span)
            scores = scores_of(q_ref[part, lanes], kv_ref[window, lanes])
            query = lax.broadcasted_iota(jnp.int32, (TILE, span), 0)
            key = lax.broadcasted_iota(jnp.int32, (TILE, span), 1)
            begin = begin_ref[part, 0:1] + (REACH - t * TILE)
            allowed = (key <= query + REACH) & (key >= begin)
            scores = jnp.where(allowed, scores, NEG_FILL)
            highest = jnp.max(scores, axis=1, keepdims=True)
            expo = jnp.exp(scores - highest)
            total_e = jnp.sum(expo, axis=1, keepdims=True)
            probability = (expo * (1.0 / total_e)).astype(BF)
            att_ref[to, lanes] = jnp.dot(
                probability, kv_ref[window, value_lanes], preferred_element_type=F32
            ).astype(BF)
            lse_ref[part, lanes] = jnp.broadcast_to(highest + jnp.log(total_e), (TILE, HEAD_DIM))
            return total

        lax.fori_loop(0, group // TILE, one, 0)

    pl.when(lax.rem(d, 2) == 0)(spread_grads)

    copy_out(att_ref, att_out)
    copy_out(lse_ref, lse_out)
    arrived_blocks(2)
    copy_out(weight_out, weight_out_out)

    def out_given(t, total):
        part = pl.ds(pl.multiple_of(t * TILE, TILE), TILE)
        given[part, :] = jnp.dot(
            att_ref[part, :], weight_out[:, half:], preferred_element_type=F32
        ).astype(BF)
        return total

    lax.fori_loop(0, group // TILE, out_given, 0)
    to_sibling = post.send(given, arrived, sibling)

    def out_kept(t, total):
        part = pl.ds(pl.multiple_of(t * TILE, TILE), TILE)
        wide[part, :] = jnp.dot(att_ref[part, :], weight_out[:, :half], preferred_element_type=F32)
        return total

    lax.fori_loop(0, group // TILE, out_kept, 0)
    to_sibling.wait_recv()

    def add_low(t, total):
        part = pl.ds(pl.multiple_of(t * 128, 128), 128)
        value = wide[part, :] + arrived[part, :].astype(F32)
        wide[part, :] = value
        low[part, :] = value.astype(BF)
        return total

    lax.fori_loop(0, group // 128, add_low, 0)
    pieces, corners, pass_pieces = scatter_plane(
        post, lambda first, count, place: low.at[pl.ds(first, count), columns(place)], landed, rows, (d, r, c)
    )
    pieces = pieces + pass_pieces()
    start_relay(1)
    for copy in pieces:
        copy.wait_recv()

    def middle(t, total):
        part = pl.ds(pl.multiple_of(t * 128, 128), 128)
        value = (
            x32[part, :] + wide[part, 0:fc] + landed[0, part, :].astype(F32)
            + landed[1, part, :].astype(F32)
        )
        mid_ref[part, :] = value
        sums[4, :, part] = as_row(jnp.sum(value * value, axis=1, keepdims=True))
        return total

    lax.fori_loop(0, rows // 128, middle, 0)
    again = [post.send(sums.at[4], sums.at[4 + m], (d, r, c ^ m)) for m in (1, 2, 3)]
    for copy in again:
        copy.wait_recv()

    def norm_two(t, total):
        part = pl.ds(pl.multiple_of(t * 128, 128), 128)
        square = sums[4, :, part] + sums[6, :, part] + sums[5, :, part] + sums[7, :, part]
        scale = lax.rsqrt(as_column(square) / D + EPSILON)
        scale_ref[part, :] = scale
        n2_ref[part, :] = (mid_ref[part, :] * scale * gain_two_ref[...]).astype(BF)
        return total

    lax.fori_loop(0, rows // 128, norm_two, 0)

    for j, copy in zip((1, 2, 3), grads):
        copy.wait_recv()
        there = pl.ds(j * half_rows, half_rows)
        grads_shared.append(
            post.send(grad_all.at[there, pl.ds(0, half)], grad_all.at[there, pl.ds(half, half)], sibling)
        )
    for copy in grads_shared:
        copy.wait_recv()
    for n in (0, 1):
        over_y(n).wait_send()

        @pl.when(core == 0)
        def _(n=n):
            for i in (2, 3):
                relay(n, i).wait_send()

        @pl.when(core == 1)
        def _(n=n):
            for i in (2, 3):
                gate_came(n, i).wait_recv()

    for kind in (0, 1):
        over_x(kind).wait_send()

        @pl.when(core == 0)
        def _(kind=kind):
            keep_hidden(kind).wait()
            ship(kind, 0, 1, (d, r, c)).wait_recv()

        @pl.when(core == 1)
        def _(kind=kind):
            to_core(kind).wait_send()
            for i in (0, 1):
                ship(kind, 0, i, (d, r, c)).wait_recv()

    for copy in (
        small + [grad_cross, beside, beyond, corner] + shared + grads + grads_shared
        + [to_sibling] + pieces + corners + again
    ):
        copy.wait_send()

    @pl.when(d < DP - 1)
    def _():
        halo.wait_send()

    for copy in copies:
        copy.wait()
    for n in (0, 1, 2):
        for p in range(DP):
            @pl.when((d < DP - 1) & (p <= d))
            def _(n=n, p=p):
                line(n, p, d).wait_send()

            @pl.when((d > 0) & (p >= d))
            def _(n=n, p=p):
                line_down(n, p, d).wait_send()

            @pl.when(c != p)
            def _(n=n, p=p):
                to_column(n, p).wait_send()


SENDS = 104


def forward(x, gain_one, gain_two, lengths, query, key, value, out, gate, up, own_grad):
    rows, fc = x.shape
    group = 2 * rows
    width = out.shape[0]
    units = gate.shape[1]
    vmem = pl.BlockSpec(memory_space=pltpu.VMEM)
    smem = pl.BlockSpec(memory_space=pltpu.SMEM)
    hbm = pl.BlockSpec(memory_space=pl.ANY)

    def like(shape, dtype=BF):
        return jax.ShapeDtypeStruct(shape, dtype)

    return pl.pallas_call(
        forward_kernel,
        in_specs=[vmem] * 3 + [smem] + [vmem] * 4 + [hbm] * 3,
        out_specs=[vmem] * 5 + [hbm] * 11,
        out_shape=[
            like((rows, fc), F32),
            like((rows, 1), F32),
            like((rows, fc)),
            like((group, 1), jnp.int32),
            like((rows, 1), F32),
            like((group, D)),
            like((D, 3 * width)),
            like((width, D)),
            like((group, width)),
            like((REACH + group, 2 * width)),
            like((group, width)),
            like((group, width), F32),
            like((fc, units)),
            like((D, units)),
            like((D, units)),
            like((group, D)),
        ],
        scratch_shapes=[
            pltpu.VMEM((group, D), BF),
            pltpu.VMEM((D, 3 * width), BF),
            pltpu.VMEM((width, D), BF),
            pltpu.VMEM((group, width), BF),
            pltpu.VMEM((REACH + group, 2 * width), BF),
            pltpu.VMEM((group, width), BF),
            pltpu.VMEM((group, width), F32),
            pltpu.VMEM((2, fc, units), F32),
            pltpu.VMEM((DP, fc, 3 * width), BF),
            pltpu.VMEM((DP, width, fc), BF),
            pltpu.VMEM((8, 8, rows), F32),
            pltpu.VMEM((group, 2 * fc), F32),
            pltpu.VMEM((group, 2 * fc), BF),
            pltpu.VMEM((group, 2 * fc), BF),
            pltpu.VMEM((group, 2 * fc), BF),
            pltpu.VMEM((3, rows, fc), BF),
            pltpu.VMEM((rows, fc), F32),
            pltpu.VMEM((2, fc, units), BF),
            pltpu.SemaphoreType.DMA((SENDS,)),
            pltpu.SemaphoreType.DMA((SENDS,)),
            pltpu.SemaphoreType.DMA((20,)),
        ],
        compiler_params=pltpu.CompilerParams(
            collective_id=1, has_side_effects=True, vmem_limit_bytes=60 << 20
        ),
        cost_estimate=pl.CostEstimate(
            flops=6 * group * D * width, bytes_accessed=64 << 20, transcendentals=0
        ),
    )(x, gain_one, gain_two, lengths, query, key, value, out, gate, up, own_grad)


def at(t, size):
    return pl.ds(pl.multiple_of(t * size, size), size)


def loop(count, body):
    def one(t, total):
        body(t)
        return total

    lax.fori_loop(0, count, one, 0)


def maker(send_sem, recv_sem):
    def raw(src, dst, sent, got_at, target):
        return pltpu.make_async_remote_copy(
            src_ref=src, dst_ref=dst, send_sem=send_sem.at[sent], recv_sem=recv_sem.at[got_at],
            device_id=target, device_id_type=MESH,
        )

    return raw


class LineSum:
    def __init__(self, raw, arrays, base, me):
        self.raw, self.arrays, self.base, self.me = raw, arrays, base, me

    def sem(self, n, p, down):
        return self.base + 8 * n + 4 * down + p

    def take(self, p, down, done):
        d = self.me[0]
        for n, (z, got_z) in enumerate(self.arrays):
            self.raw(z.at[p], got_z.at[p], self.sem(n, p, down), self.sem(n, p, down), self.me).wait_recv()

        @pl.when(jnp.logical_not(done))
        def _():
            for z, got_z in self.arrays:
                def one(t, z=z, got_z=got_z):
                    z[p, at(t, 64), :] = (
                        z[p, at(t, 64), :].astype(F32) + got_z[p, at(t, 64), :].astype(F32)
                    ).astype(BF)

                loop(z.shape[1] // 64, one)

    def up(self, p):
        d, r, c = self.me

        @pl.when((d > 0) & (d <= p))
        def _():
            self.take(p, 0, d == p)

        @pl.when(d < p)
        def _():
            for n, (z, got_z) in enumerate(self.arrays):
                self.raw(z.at[p], got_z.at[p], self.sem(n, p, 0), self.sem(n, p, 0), (d + 1, r, c)).start()

    def down(self, p):
        d, r, c = self.me

        @pl.when((d < DP - 1) & (d >= p))
        def _():
            self.take(p, 1, d == p)

        @pl.when(d > p)
        def _():
            slot = jnp.where(p < d - 1, p, DP)
            for n, (z, got_z) in enumerate(self.arrays):
                self.raw(z.at[p], got_z.at[slot], self.sem(n, p, 1), self.sem(n, p, 1), (d - 1, r, c)).start()

    def begin(self):
        d = self.me[0]

        @pl.when(d == 0)
        def _():
            for p in (3, 2, 1):
                self.up(p)

        @pl.when(d == DP - 1)
        def _():
            for p in (0, 1, 2):
                self.down(p)

    def hop(self, n):
        d = self.me[0]

        @pl.when(d == 1)
        def _():
            self.up(DP - 1 - n)

        @pl.when(d == 2)
        def _():
            self.down(n)

    def first(self):
        self.hop(0)
        self.hop(1)

    def last(self):
        d = self.me[0]

        @pl.when(d == 0)
        def _():
            self.down(0)

        @pl.when(d == 1)
        def _():
            self.down(0)
            self.down(1)
            self.up(1)

        @pl.when(d == 2)
        def _():
            self.up(3)
            self.up(2)
            self.down(2)

        @pl.when(d == DP - 1)
        def _():
            self.up(3)

    def rest(self):
        self.first()
        self.last()

    def settle(self):
        d = self.me[0]
        for p in range(DP):
            for n, (z, got_z) in enumerate(self.arrays):
                for down, sent in ((0, d < p), (1, d > p)):
                    @pl.when(sent)
                    def _(p=p, n=n, z=z, got_z=got_z, down=down):
                        self.raw(
                            z.at[p], got_z.at[p], self.sem(n, p, down), self.sem(n, p, down), self.me
                        ).wait_send()

    def total(self, z, got_z, part):
        d = self.me[0]
        value = z[d, part, :].astype(F32)
        value = value + jnp.where(d > 0, got_z[d, part, :].astype(F32), 0.0)
        return value + jnp.where(d < DP - 1, got_z[DP, part, :].astype(F32), 0.0)


class PlaneSum:
    def __init__(self, raw, stage, got, comb, base, local_sem, local_base, me):
        self.raw, self.stage, self.got, self.comb, self.base = raw, stage, got, comb, base
        self.local_sem, self.local_base, self.me = local_sem, local_base, me
        self.kinds = range(stage.shape[0])

    def from_one(self, kind, i):
        d, r, c = self.me
        y = c // 2
        sent, base = self.base + 10 * kind + i, self.base + 10 * kind
        if i < 2:
            return self.raw(self.stage.at[kind, i], self.got.at[kind, 0], sent, base, (d, r ^ 1, 2 * y + 1 - i))
        return self.raw(
            self.stage.at[kind, i], self.comb.at[kind, 3 - i], sent, base + 3 + (3 - i), (d, r ^ 1, 2 * y)
        )

    def from_zero(self, kind, i):
        d, r, c = self.me
        sent, base = self.base + 10 * kind + i, self.base + 10 * kind
        if i == 1:
            return self.raw(self.stage.at[kind, i], self.got.at[kind, 1], sent, base + 1, (d, r, c ^ 1))
        return self.raw(
            self.stage.at[kind, i], self.got.at[kind, 2], sent, base + 2, (d, r, 2 * (1 - c // 2) + i - 2)
        )

    def home(self, kind):
        return pltpu.make_async_copy(
            self.stage.at[kind, 0], self.got.at[kind, 1], self.local_sem.at[self.local_base + kind]
        )

    def start_far(self):
        @pl.when(lax.rem(self.me[2], 2) == 1)
        def _():
            for i in (2, 3):
                for kind in self.kinds:
                    self.from_one(kind, i).start()

    def start_near(self, kinds=None):
        kinds = self.kinds if kinds is None else kinds
        core = lax.rem(self.me[2], 2)

        @pl.when(core == 1)
        def _():
            for i in (0, 1):
                for kind in kinds:
                    self.from_one(kind, i).start()

        @pl.when(core == 0)
        def _():
            for kind in kinds:
                self.home(kind).start()
                self.from_zero(kind, 1).start()

    def combine(self, room, local_base, kinds=None):
        kinds = self.kinds if kinds is None else kinds
        core = lax.rem(self.me[2], 2)

        @pl.when(core == 0)
        def _():
            for i in (2, 3):
                for kind in kinds:
                    self.raw(
                        self.stage.at[kind, i], self.comb.at[kind, i - 2], self.base,
                        self.base + 10 * kind + 3 + (i - 2), self.me,
                    ).wait_recv()
                    fetch = pltpu.make_async_copy(
                        self.comb.at[kind, i - 2], room(kind, i - 2),
                        self.local_sem.at[local_base + 2 * kind + i - 2],
                    )
                    fetch.start()
                    fetch.wait()

                    def add(t, kind=kind, i=i):
                        self.stage[kind, i, at(t, 64), :] = (
                            self.stage[kind, i, at(t, 64), :].astype(F32)
                            + room(kind, i - 2)[at(t, 64), :].astype(F32)
                        ).astype(BF)

                    loop(self.stage.shape[2] // 64, add)
                    self.from_zero(kind, i).start()

    def settle(self):
        core = lax.rem(self.me[2], 2)
        for kind in self.kinds:
            base = self.base + 10 * kind
            for n in (0, 2):
                self.raw(self.stage.at[kind, 0], self.got.at[kind, n], self.base, base + n, self.me).wait_recv()

            @pl.when(core == 1)
            def _(kind=kind, base=base):
                self.raw(self.stage.at[kind, 0], self.got.at[kind, 1], self.base, base + 1, self.me).wait_recv()
                for i in range(COL):
                    self.from_one(kind, i).wait_send()

            @pl.when(core == 0)
            def _(kind=kind):
                self.home(kind).wait()
                for i in (1, 2, 3):
                    self.from_zero(kind, i).wait_send()


def middle_kernel(
    n2_ref, mid_ref, scale_ref, gain_ref, own_grad, down_ref, own_up, gate_hbm, up_hbm, grad_hbm,
    grad_out, gain_out, got, comb, n2_out, dgate_out, dup_out,
    n2, dgate, dup, wg, wu, wd, gb, own_down, gate, up, du, hidden, given, arrived, z, got_z, crossing, crossed, gn, sums, stage,
    send_sem, recv_sem, local_sem,
):
    d, r, c = (lax.axis_index(name) for name in AXES)
    me = (d, r, c)
    y, core = c // 2, lax.rem(c, 2)
    rows, fc = n2_ref.shape
    block = rows // 2
    units = own_down.shape[0]
    half = 2 * fc
    over = (((0,), (0,)), ((), ()))
    across = (((1,), (1,)), ((), ()))
    post = Post(send_sem, recv_sem)
    raw = maker(send_sem, recv_sem)
    sibling = (d, r, c ^ 1)
    others = [(a, b) for a in (0, 1) for b in range(COL) if (a, b) != (0, 0)]
    greet([(d, r ^ a, c ^ b) for a, b in others] + [(d ^ j, r, c) for j in (1, 2, 3)])

    cross = post.send(
        n2_ref.at[pl.ds(pl.multiple_of((1 - y) * block, block), block), :],
        n2.at[pl.ds(0, block), pl.ds(fc, fc)],
        (d, r, c ^ 2),
    )
    def half_of(ref, i, n):
        return ref.at[pl.ds(pl.multiple_of(place_of(i) * fc + n * (fc // 2), fc // 2), fc // 2), :]

    def place_of(i):
        return lax.rem(i, 2) * 2 + i // 2

    first_wide = post.take(8)

    def up_over_y(n):
        return raw(
            own_up.at[pl.ds(n * (fc // 2), fc // 2), :], half_of(wu, 2 + core, n),
            first_wide + 4 * n, first_wide + 4 * n + core, (d, r, 2 * (1 - y)),
        )

    def up_relay(n, i):
        return raw(
            half_of(wu, i, n), half_of(wu, 5 - i, n), first_wide + 4 * n + i - 1,
            first_wide + 4 * n + 3 - i, (d, r ^ 1, 2 * y + 1),
        )

    def up_came(n, i):
        return raw(half_of(wu, i, n), half_of(wu, i, n), first_wide, first_wide + 4 * n + i - 2, me)

    for n in (0, 1):
        up_over_y(n).start()
    loads = [
        pltpu.make_async_copy(src, dst, local_sem.at[n])
        for n, (src, dst) in zip((0, 1, 2, 9), (
            (gate_hbm, wg),
            (up_hbm.at[pl.ds(0, fc), :], wu.at[pl.ds(0, fc), :]),
            (grad_hbm, gb),
            (up_hbm.at[pl.ds(2 * fc, fc), :], wu.at[pl.ds(2 * fc, fc), :]),
        ))
    ]
    for load in loads:
        load.start()

    def cast_down(t):
        own_down[at(t, 64), :] = down_ref[at(t, 64), :].astype(BF)

    loop(units // 64, cast_down)
    first_sent = post.take(10)

    def piece(ref, n):
        return ref.at[pl.ds(n * (units // 2), units // 2), :]

    def ship(n, way, i, target, src=None):
        return raw(
            piece(own_down if src is None else src, n), piece(wd.at[place_of(i)], n),
            first_sent + 5 * n + way, first_sent + 5 * n + i, target,
        )

    keep_down = pltpu.make_async_copy(own_down, wd.at[0], local_sem.at[3])

    def to_core(n):
        return ship(n, 0, 1, sibling)

    def over_y(n):
        return ship(n, 1, 2 + core, (d, r, 2 * (1 - y)))

    def over_x(n):
        return ship(n, 2, 1 - core, (d, r ^ 1, 2 * y + 1))

    def relay(n, i):
        return ship(n, i + 1, 5 - i, (d, r ^ 1, 2 * y + 1), wd.at[PLACE[i]])

    for n in (0, 1):
        over_x(n).start()
        over_y(n).start()

    @pl.when(core == 0)
    def _():
        keep_down.start()

    @pl.when(core == 1)
    def _():
        for n in (0, 1):
            to_core(n).start()

    def pass_down(n):
        @pl.when(core == 0)
        def _():
            for i in (2, 3):
                ship(n, 0, i, me).wait_recv()
                relay(n, i).start()

    n2[0:block, 0:fc] = n2_ref[pl.ds(pl.multiple_of(y * block, block), block), :]
    cross.wait_recv()

    first_up, first_down = post.take(DP), post.take(DP)
    first_shared = post.take(DP)

    def rail(p, e):
        return n2.at[at(p ^ e, block), pl.ds(0, half)]

    def go_up(p):
        return raw(rail(p, d), rail(p, d + 1), first_up + p, first_up + p, (d + 1, r, c))

    def go_down(p):
        return raw(rail(p, d), rail(p, d - 1), first_down + p, first_up + p, (d - 1, r, c))

    def share(p):
        return raw(
            rail(p, d), n2.at[at(p ^ d, block), pl.ds(half, half)], first_shared + p, first_shared + p, sibling
        )

    def onward(p):
        @pl.when((p <= d) & (d < DP - 1))
        def _():
            go_up(p).start()

        @pl.when((p >= d) & (d > 0))
        def _():
            go_down(p).start()

        share(p).start()

    def project(p):
        share(p).wait_recv()
        part = at(p ^ d, block)
        gate[part, :] = jnp.dot(n2[part, :], wg[...], preferred_element_type=F32)

    def project_up(t):
        part = at(t, block)
        up[part, :] = jnp.dot(n2[part, :], wu[...], preferred_element_type=F32)

    def pass_up(n):
        @pl.when(core == 0)
        def _():
            for i in (2, 3):
                up_came(n, i).wait_recv()
                up_relay(n, i).start()

    def hidden_grads(first, fresh):
        def one(t):
            part = at(t, block)
            value = jnp.zeros((block, units), F32) if fresh else du[part, :]
            for i in (first, first + 1):
                place = PLACE[i]
                value = value + lax.dot_general(
                    gb[part, place * fc : (place + 1) * fc], wd[place], across, preferred_element_type=F32
                )
            du[part, :] = value

        loop(DP, one)

    onward(d)
    turns = [
        d,
        jnp.where(d == 0, 1, d - 1),
        jnp.where(d < 2, 2, jnp.where(d == 2, 3, 1)),
        jnp.where(d < 2, 3, 0),
    ]
    inner = (d == 1) | (d == 2)

    def arrival(n):
        raw(rail(turns[n], d), rail(turns[n], d), first_up, first_up + turns[n], me).wait_recv()
        onward(turns[n])

    for load in loads:
        load.wait()
    arrival(1)

    @pl.when(inner)
    def _():
        arrival(2)

    pass_up(0)
    project(turns[0])
    pass_up(1)
    project(turns[1])

    @pl.when(jnp.logical_not(inner))
    def _():
        arrival(2)

    @pl.when(inner)
    def _():
        arrival(3)

    pass_down(0)
    project(turns[2])

    @pl.when(core == 0)
    def _():
        keep_down.wait()
        for n in (0, 1):
            ship(n, 0, 1, me).wait_recv()

    @pl.when(core == 1)
    def _():
        for n in (0, 1):
            for i in (0, 1):
                ship(n, 0, i, me).wait_recv()

    @pl.when(jnp.logical_not(inner))
    def _():
        arrival(3)

    hidden_grads(0, True)
    pass_down(1)
    project(turns[3])
    outs = [pltpu.make_async_copy(n2, n2_out, local_sem.at[0])]
    outs[0].start()

    @pl.when(core == 1)
    def _():
        for n in (0, 1):
            for i in (2, 3):
                up_came(n, i).wait_recv()

    loop(DP, project_up)

    def hidden_of(t):
        part = at(t, 64)
        g = gate[part, :]
        hidden[part, :] = (g * (1.0 / (1.0 + jnp.exp(-g))) * up[part, :]).astype(BF)

    loop(2 * rows // 64, hidden_of)

    def down_part(i):
        def down_grad(t):
            place = PLACE[i]
            stage[0, i, at(t, TILE), :] = lax.dot_general(
                hidden[:, at(t, TILE)], gb[:, place * fc : (place + 1) * fc], over, preferred_element_type=F32
            ).astype(BF)

        loop(units // TILE, down_grad)

    owners = PlaneSum(raw, stage, got, comb, post.take(10), local_sem, 4, me)
    down_part(2)
    down_part(3)

    @pl.when(core == 1)
    def _():
        for n in (0, 1):
            for i in (2, 3):
                ship(n, 0, i, me).wait_recv()

    hidden_grads(2, False)

    owners.start_far()

    def units_of(t):
        part = at(t, 64)
        g, u, grad = gate[part, :], up[part, :], du[part, :]
        sigmoid = 1.0 / (1.0 + jnp.exp(-g))
        silu = g * sigmoid
        dgate[part, :] = (grad * u * sigmoid * (1.0 + g * (1.0 - sigmoid))).astype(BF)
        dup[part, :] = (grad * silu).astype(BF)

    loop(2 * rows // 64, units_of)
    for n, (src, dst) in enumerate(((dgate, dgate_out), (dup, dup_out))):
        outs.append(pltpu.make_async_copy(src, dst, local_sem.at[1 + n]))
        outs[-1].start()

    def back(part, cols):
        return lax.dot_general(
            dgate[part, :], wg[cols, :], across, preferred_element_type=F32
        ) + lax.dot_general(dup[part, :], wu[cols, :], across, preferred_element_type=F32)

    line = LineSum(raw, ((z, got_z),), post.take(8), me)

    def plane_of(t):
        return jnp.where(d < DP // 2, DP - 1 - t, t)

    def to_sibling(t):
        part = at(plane_of(t) ^ d, block)
        return raw(given.at[part, :], arrived.at[part, :], first_given + t, first_given + t, sibling)

    def give(t):
        part = at(plane_of(t) ^ d, block)
        given[part, :] = back(part, slice(half, None)).astype(BF)
        to_sibling(t).start()

    def keep(t):
        p = plane_of(t)
        part = at(p ^ d, block)
        value = back(part, slice(0, half))
        to_sibling(t).wait_recv()
        z[p] = (value + arrived[part, :].astype(F32)).astype(BF)

        if t < DP - 1:
            @pl.when(d == 0)
            def _():
                line.up(DP - 1 - t)

            @pl.when(d == DP - 1)
            def _():
                line.down(t)

    first_given = post.take(DP)
    give(0)
    give(1)
    keep(0)
    give(2)
    keep(1)
    give(3)
    keep(2)
    down_part(0)
    down_part(1)
    owners.start_near()
    keep(3)

    def combine():
        owners.combine(lambda kind, j: wg.at[pl.ds(0, units), pl.ds(j * fc, fc)], 5)

    pl.when(jnp.logical_not(inner))(combine)
    line.hop(0)
    pl.when(inner)(combine)
    line.hop(1)
    line.last()

    def settle_rows(t):
        part = at(t, 64)
        total = line.total(z, got_z, part)
        gn[pl.ds(pl.multiple_of(y * block + t * 64, 64), 64), :] = total[:, 0:fc]
        crossing[part, :] = total[:, fc:].astype(BF)

    loop(block // 64, settle_rows)
    other = post.send(crossing, crossed, (d, r, c ^ 2))
    other.wait_recv()

    def other_rows(t):
        gn[pl.ds(pl.multiple_of((1 - y) * block + t * 64, 64), 64), :] = crossed[at(t, 64), :].astype(F32)

    loop(block // 64, other_rows)

    def inner_sum(t):
        part = at(t, 128)
        inner = gn[part, :] * gain_ref[...] * mid_ref[part, :]
        sums[0, :, part] = as_row(jnp.sum(inner, axis=1, keepdims=True))

    loop(rows // 128, inner_sum)
    small = [post.send(sums.at[0], sums.at[m], (d, r, c ^ m)) for m in (1, 2, 3)]

    def gain_sum(t, total):
        part = at(t, 128)
        value = gn[part, :] * mid_ref[part, :] * scale_ref[part, :]
        return total + jnp.sum(value, axis=0, keepdims=True)

    gain_out[...] = lax.fori_loop(0, rows // 128, gain_sum, jnp.zeros((1, fc), F32))
    for copy in small:
        copy.wait_recv()

    def finish(t):
        part = at(t, 128)
        inner = as_column(sums[0, :, part] + sums[2, :, part] + sums[1, :, part] + sums[3, :, part])
        scale = scale_ref[part, :]
        grad_out[part, :] = (
            own_grad[part, :].astype(F32) + scale * (gn[part, :] * gain_ref[...])
            - mid_ref[part, :] * (scale * scale * scale * inner / D)
        )

    loop(rows // 128, finish)

    owners.settle()
    line.settle()
    for copy in outs:
        copy.wait()
    for copy in [cross, other] + small:
        copy.wait_send()
    for t in range(DP):
        to_sibling(t).wait_send()
    for n in (0, 1):
        over_y(n).wait_send()
        over_x(n).wait_send()
        up_over_y(n).wait_send()

        @pl.when(core == 0)
        def _(n=n):
            for i in (2, 3):
                relay(n, i).wait_send()
                up_relay(n, i).wait_send()

        @pl.when(core == 1)
        def _(n=n):
            to_core(n).wait_send()

    for p in range(DP):
        share(p).wait_send()

        @pl.when((p <= d) & (d < DP - 1))
        def _(p=p):
            go_up(p).wait_send()

        @pl.when((p >= d) & (d > 0))
        def _(p=p):
            go_down(p).wait_send()


def middle(n2, mid, scale, gain, own_grad, down, own_up, gate, up, grad_all):
    rows, fc = n2.shape
    group = 2 * rows
    block = rows // 2
    units = down.shape[0]
    vmem = pl.BlockSpec(memory_space=pltpu.VMEM)
    hbm = pl.BlockSpec(memory_space=pl.ANY)

    def like(shape, dtype=BF):
        return jax.ShapeDtypeStruct(shape, dtype)

    return pl.pallas_call(
        middle_kernel,
        in_specs=[vmem] * 6 + [hbm] * 4,
        out_specs=[vmem] * 2 + [hbm] * 5,
        out_shape=[
            like((rows, fc), F32),
            like((1, fc), F32),
            like((1, 3, units, fc)),
            like((1, 2, units, fc)),
            like((group, D)),
            like((group, units)),
            like((group, units)),
        ],
        scratch_shapes=[
            pltpu.VMEM((group, D), BF),
            pltpu.VMEM((group, units), BF),
            pltpu.VMEM((group, units), BF),
            pltpu.VMEM((D, units), BF),
            pltpu.VMEM((D, units), BF),
            pltpu.VMEM((COL, units, fc), BF),
            pltpu.VMEM((group, D), BF),
            pltpu.VMEM((units, fc), BF),
            pltpu.VMEM((group, units), F32),
            pltpu.VMEM((group, units), F32),
            pltpu.VMEM((group, units), F32),
            pltpu.VMEM((group, units), BF),
            pltpu.VMEM((group, 2 * fc), BF),
            pltpu.VMEM((group, 2 * fc), BF),
            pltpu.VMEM((DP, block, 2 * fc), BF),
            pltpu.VMEM((DP + 1, block, 2 * fc), BF),
            pltpu.VMEM((block, fc), BF),
            pltpu.VMEM((block, fc), BF),
            pltpu.VMEM((rows, fc), F32),
            pltpu.VMEM((4, 8, rows), F32),
            pltpu.VMEM((1, COL, units, fc), BF),
            pltpu.SemaphoreType.DMA((SENDS,)),
            pltpu.SemaphoreType.DMA((SENDS,)),
            pltpu.SemaphoreType.DMA((12,)),
        ],
        compiler_params=pltpu.CompilerParams(
            collective_id=3, has_side_effects=True, vmem_limit_bytes=62 << 20
        ),
        cost_estimate=pl.CostEstimate(
            flops=14 * group * D * units, bytes_accessed=48 << 20, transcendentals=group * units
        ),
    )(n2, mid, scale, gain, own_grad, down, own_up, gate, up, grad_all)


POSTS = 112


def backward_kernel(
    x_ref, gain_ref, scale_ref, mid_ref, gain_two_ref, begin_ref, weight_in_hbm, weight_out_hbm, q_hbm, kv_hbm,
    att_hbm, lse_hbm, normed_hbm, n2_hbm, dgate_hbm, dup_hbm,
    tokens_out, query_out, key_out, value_out, out_out, gains_out, got, comb,
    weight_in, weight_out, q_ref, kv_ref, att_ref, lse_ref, n1, n2, dgu, dball, dotted, dproj, acc, spill, spilled, stage, own_f, arrived, landed,
    zq, zo, zkv, rq, ro, rkv, sums, gsum,
    send_sem, recv_sem, local_sem,
):
    d, r, c = (lax.axis_index(name) for name in AXES)
    y, core = c // 2, lax.rem(c, 2)
    rows, fc = x_ref.shape
    group = 2 * rows
    width = q_hbm.shape[1]
    units = dgate_hbm.shape[1]
    half = 2 * fc
    tiles = group // TILE
    over = (((0,), (0,)), ((), ()))
    across = (((1,), (1,)), ((), ()))
    post = Post(send_sem, recv_sem)
    loads = [
        pltpu.make_async_copy(src, dst, local_sem.at[8 + n])
        for n, (src, dst) in enumerate((
            (n2_hbm, n2),
            (dgate_hbm, dgu.at[pl.ds(0, group), :]),
            (dup_hbm, dgu.at[pl.ds(group, group), :]),
            (normed_hbm, n1),
            (weight_out_hbm, weight_out),
            (att_hbm, att_ref),
            (q_hbm, q_ref),
            (kv_hbm, kv_ref),
            (lse_hbm, lse_ref),
            (weight_in_hbm, weight_in),
        ))
    ]
    for load in loads:
        load.start()

    others = [(a, b) for a in (0, 1) for b in range(COL) if (a, b) != (0, 0)]
    greet(
        [(d, r ^ a, c ^ b) for a, b in others]
        + [(d ^ j, r ^ a, c) for j in (1, 2, 3) for a in (0, 1)]
    )

    def columns(place):
        return pl.ds(place * fc, fc)

    def turned(t):
        return lax.rem(t + 2 * r, tiles)

    raw = maker(send_sem, recv_sem)
    me = (d, r, c)
    sibling = (d, r, c ^ 1)
    own_rows, other_rows = pl.ds(0, rows), pl.ds(rows, rows)
    def round_mid(t):
        dball[at(t, 128), 0:fc] = mid_ref[at(t, 128), :].astype(BF)

    loop(rows // 128, round_mid)
    own_block = dball.at[own_rows, columns(0)]
    beside = post.send(own_block, dball.at[other_rows, columns(0)], (d, r ^ 1, c))
    beyond = post.send(own_block, dball.at[own_rows, columns(1)], (d, r, c ^ 2))
    shared = [post.send(own_block, dball.at[own_rows, columns(2)], sibling)]

    for load in loads[:3]:
        load.wait()
    owners = PlaneSum(raw, stage, got, comb, post.take(20), local_sem, 4, me)

    def hidden_part(i):
        for kind in (0, 1):
            def hidden_grad(t, kind=kind):
                left = n2[:, pl.ds(pl.multiple_of(PLACE[i] * fc + t * TILE, TILE), TILE)]
                stage[kind, i, at(t, TILE), :] = lax.dot_general(
                    left, dgu[pl.ds(kind * group, group), :], over, preferred_element_type=F32
                ).astype(BF)

            loop(fc // TILE, hidden_grad)

    hidden_part(2)
    hidden_part(3)
    for load in loads[3:]:
        load.wait()

    upper = pl.ds(rows, rows // 2)
    beside.wait_recv()
    corner = [post.send(dball.at[upper, columns(0)], dball.at[upper, columns(1)], (d, r, c ^ 2))]
    shared.append(post.send(dball.at[other_rows, columns(0)], dball.at[other_rows, columns(2)], sibling))
    beyond.wait_recv()
    corner.append(post.send(
        dball.at[pl.ds(rows // 2, rows // 2), columns(1)],
        dball.at[pl.ds(rows + rows // 2, rows // 2), columns(1)], (d, r ^ 1, c),
    ))
    shared.append(post.send(dball.at[own_rows, columns(1)], dball.at[own_rows, columns(3)], sibling))
    owners.start_far()
    hidden_part(0)
    hidden_part(1)
    for copy in corner:
        copy.wait_recv()
    shared.append(post.send(dball.at[other_rows, columns(1)], dball.at[other_rows, columns(3)], sibling))
    for copy in shared:
        copy.wait_recv()

    def head_grad(t):
        dotted[at(turned(t), TILE), :] = lax.dot_general(
            dball[at(t, TILE), :], weight_out[...], across, preferred_element_type=F32
        ).astype(BF)

    loop(tiles, head_grad)

    sent_out = [None] + [post.take(1) for _ in (1, 2, 3)]
    outs = []
    for place, m in enumerate((0, 2, 1, 3)):
        value = lax.dot_general(
            att_ref[...], dball[:, place * fc : (place + 1) * fc], over, preferred_element_type=F32
        ).astype(BF)
        if m == 0:
            zo[c] = value
        else:
            n2[(m - 1) * width : m * width, half : half + fc] = value
            staged = n2.at[pl.ds((m - 1) * width, width), pl.ds(half, fc)]
            copy = raw(staged, zo.at[c], sent_out[m], sent_out[m], (d, r, c ^ m))
            copy.start()
            outs.append(copy)

    span = TILE + REACH
    scale = HEAD_DIM ** (-0.5)
    spills = []
    for h in range(width // HEAD_DIM):
        lanes = pl.ds(h * HEAD_DIM, HEAD_DIM)
        value_lanes = pl.ds(width + h * HEAD_DIM, HEAD_DIM)

        def clear(t, lanes=lanes, value_lanes=value_lanes):
            acc[at(t, TILE), lanes] = jnp.zeros((TILE, HEAD_DIM), F32)
            acc[at(t, TILE), value_lanes] = jnp.zeros((TILE, HEAD_DIM), F32)

        loop((group + REACH) // TILE, clear)

        def one(t, lanes=lanes, value_lanes=value_lanes):
            part = at(t, TILE)
            window = pl.ds(pl.multiple_of(t * TILE, TILE), span)
            query, key = q_ref[part, lanes], kv_ref[window, lanes]
            grad = dotted[part, lanes]
            scores = scores_of(query, key)
            query_at = lax.broadcasted_iota(jnp.int32, (TILE, span), 0)
            key_at = lax.broadcasted_iota(jnp.int32, (TILE, span), 1)
            begin = begin_ref[part, 0:1] + (REACH - t * TILE)
            allowed = (key_at <= query_at + REACH) & (key_at >= begin)
            scores = jnp.where(allowed, scores - lse_ref[part, lanes][:, 0:1], NEG_FILL)
            probability = jnp.exp(scores)
            grad_soft = lax.dot_general(grad, kv_ref[window, value_lanes], across, preferred_element_type=F32)
            inner = jnp.sum(probability * grad_soft, axis=1, keepdims=True)
            grad_scores = (probability * (grad_soft - inner)).astype(BF)
            dproj[at(turned(t), TILE), lanes] = (
                jnp.dot(grad_scores, key, preferred_element_type=F32) * scale
            ).astype(BF)
            acc[window, lanes] += lax.dot_general(grad_scores, query, over, preferred_element_type=F32) * scale
            acc[window, value_lanes] += lax.dot_general(
                probability.astype(BF), grad, over, preferred_element_type=F32
            )

        loop(tiles, one)

        def round_spill(t, h=h, lanes=lanes, value_lanes=value_lanes):
            spill[h, at(t, TILE), 0:HEAD_DIM] = acc[at(t, TILE), lanes].astype(BF)
            spill[h, at(t, TILE), HEAD_DIM:] = acc[at(t, TILE), value_lanes].astype(BF)

        loop(REACH // TILE, round_spill)
        copy = post.ready(spill.at[h], spilled.at[h], (lax.rem(d + DP - 1, DP), r, c))
        spills.append(copy)

        @pl.when(d > 0)
        def _(copy=copy):
            copy.start()

    def attention_grads(first_lane, lane_count, dest):
        lanes = slice(first_lane, first_lane + lane_count)
        slots = [None] + [post.take(1) for _ in (1, 2, 3)]
        copies = []
        for place, m in enumerate((0, 2, 1, 3)):
            def tile(t, place=place, m=m):
                left = n1[:, pl.ds(pl.multiple_of(place * fc + t * TILE, TILE), TILE)]
                value = lax.dot_general(left, dproj[:, lanes], over, preferred_element_type=F32).astype(BF)
                if m == 0:
                    dest[c, at(t, TILE), :] = value
                else:
                    dgu[pl.ds(pl.multiple_of(place * fc + t * TILE, TILE), TILE), lanes] = value

            loop(fc // TILE, tile)
            if m:
                copy = raw(
                    dgu.at[pl.ds(place * fc, fc), pl.ds(first_lane, lane_count)], dest.at[c],
                    slots[m], slots[m], (d, r, c ^ m),
                )
                copy.start()
                copies.append(copy)
        return copies

    qs = attention_grads(0, width, zq)

    @pl.when(d < DP - 1)
    def _():
        for copy in spills:
            copy.wait_recv()

    @pl.when(d == DP - 1)
    def _():
        spilled[...] = jnp.zeros_like(spilled)

    for h in range(width // HEAD_DIM):
        for which in (0, 1):
            lanes = pl.ds(which * width + h * HEAD_DIM, HEAD_DIM)
            out_lanes = pl.ds((1 + which) * width + h * HEAD_DIM, HEAD_DIM)

            def whole(t, h=h, which=which, lanes=lanes, out_lanes=out_lanes):
                total = acc[pl.ds(pl.multiple_of(REACH + t * TILE, TILE), TILE), lanes]
                extra = spilled[
                    h, at(jnp.maximum(t - 1, 0), TILE), which * HEAD_DIM : (which + 1) * HEAD_DIM
                ].astype(F32)
                total = total + jnp.where(t > 0, extra, 0.0)
                dproj[at(turned(t), TILE), out_lanes] = total.astype(BF)

            loop(tiles, whole)

    kvs = attention_grads(width, 2 * width, zkv)
    for copy in outs + qs:
        copy.wait_recv()
    first_line = post.take(24)
    line_a = LineSum(raw, ((zq, rq), (zo, ro)), first_line, me)
    line_b = LineSum(raw, ((zkv, rkv),), first_line + 16, me)
    line_a.begin()

    def given_part(t):
        n2[at(t, TILE), 0:half] = lax.dot_general(
            dproj[at(t, TILE), :], weight_in[half:, :], across, preferred_element_type=F32
        ).astype(BF)

    loop(tiles, given_part)
    to_sibling = post.send(n2.at[:, pl.ds(0, half)], arrived, sibling)

    to_sibling.wait_recv()
    for copy in outs:
        copy.wait_send()

    def kept_part(t):
        part = at(t, TILE)
        value = lax.dot_general(
            dproj[part, :], weight_in[:half, :], across, preferred_element_type=F32
        ) + arrived[part, :].astype(F32)
        n2[part, half:] = value.astype(BF)

        @pl.when(t < rows // TILE)
        def _():
            own_f[part, :] = value[:, 0:fc]

    loop(tiles, kept_part)

    pieces, corners, pass_pieces = scatter_plane(
        post, lambda first, count, place: n2.at[pl.ds(first, count), pl.ds(half + place * fc, fc)], landed, rows, me
    )

    def finish(line, z, got_z, dests):
        def one(t):
            value = line.total(z, got_z, at(t, 64))
            for dest, lanes in dests:
                dest[at(t, 64), :] = value[:, lanes]

        loop(z.shape[1] // 64, one)

    line_a.first()
    pieces = pieces + pass_pieces()
    for copy in kvs:
        copy.wait_recv()
    line_b.begin()

    def combine(kind):
        owners.combine(lambda kind, j: n1.at[pl.ds(j * fc, fc), pl.ds(kind * units, units)], 0, (kind,))

    owners.start_near((0,))
    combine(0)
    line_a.last()

    for copy in pieces:
        copy.wait_recv()

    def inner_sum(t):
        part = at(t, 128)
        value = own_f[part, :]
        for n in range(2):
            value = value + landed[n, part, :].astype(F32)
        own_f[part, :] = value
        inner = value * gain_ref[...] * x_ref[part, :].astype(F32)
        sums[0, :, part] = as_row(jnp.sum(inner, axis=1, keepdims=True))

    loop(rows // 128, inner_sum)
    small = [post.send(sums.at[0], sums.at[m], (d, r, c ^ m)) for m in (1, 2, 3)]
    seat = ROW * d + r
    gain_part = jnp.zeros((1, fc), F32)

    def gain_sum(t, total):
        part = at(t, 128)
        value = own_f[part, :] * x_ref[part, :].astype(F32) * scale_ref[part, :]
        return total + jnp.sum(value, axis=0, keepdims=True)

    gain_part = lax.fori_loop(0, rows // 128, gain_sum, gain_part)
    gsum[seat, 0:1, :] = gain_part
    gsum[seat, 1:2, :] = gain_two_ref[...]
    gsum[seat, 2:8, :] = jnp.zeros((6, fc), F32)
    gain_sent = post.take(8)
    gain_got = gain_sent

    def gain_copy(n, j, a):
        return raw(gsum.at[seat], gsum.at[seat], gain_sent + n, gain_got + seat, (d ^ j, r ^ a, c))

    far = [(j, a) for j in range(DP) for a in (0, 1) if (j, a) != (0, 0)]
    for n, (j, a) in enumerate(far):
        gain_copy(n, j, a).start()
    owners.start_near((1,))
    combine(1)
    line_b.rest()
    finish(line_a, zq, rq, ((query_out, slice(None)),))
    finish(line_a, zo, ro, ((out_out, slice(None)),))
    finish(line_b, zkv, rkv, ((key_out, slice(0, width)), (value_out, slice(width, None))))
    for copy in small:
        copy.wait_recv()

    def finish_tokens(t):
        part = at(t, 128)
        inner = as_column(sums[0, :, part] + sums[2, :, part] + sums[1, :, part] + sums[3, :, part])
        scale_rows = scale_ref[part, :]
        value = x_ref[part, :].astype(F32)
        tokens_out[part, :] = (
            mid_ref[part, :] + scale_rows * (own_f[part, :] * gain_ref[...])
            - value * (scale_rows * scale_rows * scale_rows * inner / D)
        )

    loop(rows // 128, finish_tokens)

    for e in range(2 * DP):
        @pl.when(e != seat)
        def _(e=e):
            raw(gsum.at[e], gsum.at[e], gain_sent, gain_got + e, me).wait_recv()

    gains = gsum[0]
    for e in range(1, 2 * DP):
        gains = gains + gsum[e]
    gains_out[...] = gains

    owners.settle()
    line_a.settle()
    line_b.settle()
    for copy in [beside, beyond] + corner + shared + qs + kvs + [to_sibling] + pieces + corners + small:
        copy.wait_send()
    for n, (j, a) in enumerate(far):
        gain_copy(n, j, a).wait_send()

    @pl.when(d > 0)
    def _():
        for copy in spills:
            copy.wait_send()


def backward(x, gain, scale, mid, gain_two, weight_in, weight_out, q, kv, att, lse, begin, normed, n2, dgate, dup):
    rows, fc = x.shape
    group = 2 * rows
    width = q.shape[1]
    units = dgate.shape[1]
    vmem = pl.BlockSpec(memory_space=pltpu.VMEM)
    hbm = pl.BlockSpec(memory_space=pl.ANY)

    def like(shape, dtype=BF):
        return jax.ShapeDtypeStruct(shape, dtype)

    return pl.pallas_call(
        backward_kernel,
        in_specs=[vmem] * 6 + [hbm] * 10,
        out_specs=[vmem] * 6 + [hbm] * 2,
        out_shape=[
            like((rows, fc), F32),
            like((fc, width), F32),
            like((fc, width), F32),
            like((fc, width), F32),
            like((width, fc), F32),
            like((8, fc), F32),
            like((2, 3, fc, units)),
            like((2, 2, fc, units)),
        ],
        scratch_shapes=[
            pltpu.VMEM((D, 3 * width), BF),
            pltpu.VMEM((width, D), BF),
            pltpu.VMEM((group, width), BF),
            pltpu.VMEM((REACH + group, 2 * width), BF),
            pltpu.VMEM((group, width), BF),
            pltpu.VMEM((group, width), F32),
            pltpu.VMEM((group, D), BF),
            pltpu.VMEM((group, D), BF),
            pltpu.VMEM((2 * group, units), BF),
            pltpu.VMEM((group, D), BF),
            pltpu.VMEM((group, width), BF),
            pltpu.VMEM((group, 3 * width), BF),
            pltpu.VMEM((group + REACH, 2 * width), F32),
            pltpu.VMEM((width // HEAD_DIM, REACH, 2 * HEAD_DIM), BF),
            pltpu.VMEM((width // HEAD_DIM, REACH, 2 * HEAD_DIM), BF),
            pltpu.VMEM((2, COL, fc, units), BF),
            pltpu.VMEM((rows, fc), F32),
            pltpu.VMEM((group, 2 * fc), BF),
            pltpu.VMEM((3, rows, fc), BF),
            pltpu.VMEM((DP, fc, width), BF),
            pltpu.VMEM((DP, width, fc), BF),
            pltpu.VMEM((DP, fc, 2 * width), BF),
            pltpu.VMEM((DP + 1, fc, width), BF),
            pltpu.VMEM((DP + 1, width, fc), BF),
            pltpu.VMEM((DP + 1, fc, 2 * width), BF),
            pltpu.VMEM((4, 8, rows), F32),
            pltpu.VMEM((2 * DP, 8, fc), F32),
            pltpu.SemaphoreType.DMA((POSTS,)),
            pltpu.SemaphoreType.DMA((POSTS,)),
            pltpu.SemaphoreType.DMA((20,)),
        ],
        compiler_params=pltpu.CompilerParams(
            collective_id=2, has_side_effects=True, vmem_limit_bytes=62 << 20
        ),
        cost_estimate=pl.CostEstimate(
            flops=12 * group * D * width + 4 * group * D * units, bytes_accessed=64 << 20, transcendentals=0
        ),
    )(x, gain, scale, mid, gain_two, begin, weight_in, weight_out, q, kv, att, lse, normed, n2, dgate, dup)


def closing_kernel(
    tokens, query, key, value, out, hidden, down, gains,
    tokens_out, query_out, key_out, value_out, out_out, gate_out, up_out, down_out, one_out, two_out,
):
    for src, dst in (
        (tokens, tokens_out), (query, query_out), (key, key_out), (value, value_out), (out, out_out)
    ):
        dst[...] = src[...]
    for dst, kind in ((gate_out, 0), (up_out, 1)):
        dst[...] = hidden[kind, 0].astype(F32) + hidden[kind, 1].astype(F32) + hidden[kind, 2].astype(F32)
    one_out[...] = gains[0]
    two_out[...] = gains[1]
    down_out[...] = down[0, 0].astype(F32) + down[0, 1].astype(F32) + down[0, 2].astype(F32)


def closing(tokens, query, key, value, out, hidden, down, gains):
    steps = 4

    def rows_of(array):
        rows, width = array.shape[-2:]
        lead = array.shape[:-2]
        return pl.BlockSpec(lead + (rows // steps, width), lambda t: (0,) * len(lead) + (t, 0))

    finals = [tokens, query, key, value, out] + [
        jax.ShapeDtypeStruct(a.shape[-2:], F32) for a in (hidden, hidden, down)
    ]
    return pl.pallas_call(
        closing_kernel,
        grid=(steps,),
        in_specs=[rows_of(a) for a in (tokens, query, key, value, out, hidden, down)]
        + [pl.BlockSpec(gains.shape, lambda t: (0, 0))],
        out_specs=[rows_of(a) for a in finals] + [pl.BlockSpec(gains.shape[1:], lambda t: (0,))] * 2,
        out_shape=[jax.ShapeDtypeStruct(a.shape, F32) for a in finals]
        + [jax.ShapeDtypeStruct(gains.shape[1:], F32)] * 2,
        compiler_params=pltpu.CompilerParams(vmem_limit_bytes=62 << 20),
    )(tokens, query, key, value, out, hidden, down, gains)


def on_small_mesh(
    tokens,
    cotangent,
    query_master,
    key_master,
    value_master,
    out_master,
    gate_master,
    up_master,
    down_master,
    attn_gain,
    ffn_gain,
    lengths,
    permutation,
):
    del permutation
    (
        mid, scale_two, n2, begin, scale_one, normed_one, weight_in, weight_out, q, key_value,
        own_attended, lse, own_up, weight_gate, weight_up, grad_all,
    ) = forward(
        tokens, attn_gain[None, :], ffn_gain[None, :], lengths, query_master, key_master,
        value_master, out_master, gate_master, up_master, cotangent,
    )
    grad_mid, gain_two_part, got_down, _, normed_two, grad_gate, grad_up = middle(
        n2, mid, scale_two, ffn_gain[None, :], cotangent, down_master, own_up, weight_gate,
        weight_up, grad_all,
    )
    grad_tokens, grad_query, grad_key, grad_value, grad_out, gains, got, _ = backward(
        tokens, attn_gain[None, :], scale_one, grad_mid, gain_two_part, weight_in, weight_out, q,
        key_value, own_attended, lse, begin, normed_one, normed_two, grad_gate, grad_up,
    )
    return closing(grad_tokens, grad_query, grad_key, grad_value, grad_out, got, got_down, gains)


def solution(mesh):
    placed = (
        P(("dp", "row"), "col"),
        P(("dp", "row"), "col"),
        P("col", ("row", "dp")),
        P("col", ("row", "dp")),
        P("col", ("row", "dp")),
        P(("row", "dp"), "col"),
        P("col", ("row", "dp")),
        P("col", ("row", "dp")),
        P(("row", "dp"), "col"),
        P("col"),
        P("col"),
        P(),
        P(),
    )
    small = tuple(mesh.shape[name] for name in AXES) == (DP, ROW, COL)
    return jax.shard_map(
        on_small_mesh if small else on_any_mesh,
        mesh=mesh,
        in_specs=placed,
        out_specs=(
            P(("dp", "row"), "col"),
            P("col", ("row", "dp")),
            P("col", ("row", "dp")),
            P("col", ("row", "dp")),
            P(("row", "dp"), "col"),
            P("col", ("row", "dp")),
            P("col", ("row", "dp")),
            P(("row", "dp"), "col"),
            P("col"),
            P("col"),
        ),
        check_vma=False,
    )
```

```python
import functools

import jax
import jax.numpy as jnp
from jax import lax
from jax.experimental import pallas as pl
from jax.experimental.pallas import tpu as pltpu
from jax.sharding import PartitionSpec as P

D = 2048
HEAD_DIM = 128


EPSILON = 1e-06
NEG_FILL = -1e30
AXES = ("dp", "row", "col")
DP, ROW, COL = 4, 2, 4
REACH = 768
BF = jnp.bfloat16
F32 = jnp.float32


def running_sum(lengths):
    count = lengths.shape[0]
    earlier = jnp.arange(count)[:, None] <= jnp.arange(count)[None, :]
    return jnp.sum(jnp.where(earlier, lengths[:, None], 0), axis=0)

def make_picker(wanted, carried, pieces):
    amount = pieces[0].shape[0]
    inside = (wanted >= 0) & (wanted < amount)
    chosen = jnp.clip(wanted, 0, amount - 1)
    return tuple(
        (
            jnp.where(inside[:, None], jnp.take(shard_rows, chosen, axis=0), current)
            for shard_rows, current in zip(pieces, carried)
        )
    )


def sequence_marks(permutation, lengths, first_slot, amount):
    source = lax.dynamic_slice_in_dim(permutation, first_slot, amount)
    seq_ends = running_sum(lengths)
    passed = seq_ends[None, :] <= source[:, None]
    member = jnp.sum(passed.astype(jnp.int32), axis=1)
    begins = jnp.max(jnp.where(passed, seq_ends[None, :], 0), axis=1)
    return (member, source - begins)


def col_total(values):
    return lax.psum(jnp.sum(values, axis=1), "col")


def row_gather(values):
    return lax.all_gather(values, "row", axis=0, tiled=True)


def col_gather(values):
    return lax.all_gather(values, "col", axis=0, tiled=True)


def key_gather(keys_here, values_here):
    return (
        lax.all_gather(keys_here, "col", axis=0, tiled=True),
        lax.all_gather(values_here, "col", axis=0, tiled=True),
    )


def multiply(row_block, weight, transpose_right):
    if transpose_right:
        return lax.dot_general(
            row_block, weight, (((1,), (1,)), ((), ())), preferred_element_type=jnp.float32
        )
    return jnp.dot(row_block, weight, preferred_element_type=jnp.float32)


def outer_sum(left_rows, right_rows):
    return lax.dot_general(
        left_rows, right_rows, (((0,), (0,)), ((), ())), preferred_element_type=jnp.float32
    )


def col_reduce(spread, weight, transpose_right):
    return lax.psum_scatter(
        multiply(spread, weight, transpose_right), "col", scatter_dimension=0, tiled=True
    )


def row_reduce(spread, weight, transpose_right):
    return lax.psum_scatter(
        multiply(spread, weight, transpose_right), "row", scatter_dimension=0, tiled=True
    )


def visible(query_member, query_position, member, position):
    same = query_member[:, None] == member[None, :]
    behind = position[None, :] <= query_position[:, None]
    return same & behind


def attend_scores(query_block, key_all, allowed):
    scores = jnp.einsum(
        "qhd,khd->hqk", query_block, key_all, preferred_element_type=jnp.float32
    ) * HEAD_DIM ** (-0.5)
    return jnp.where(allowed[None, :, :], scores, NEG_FILL)


def norm_back(grad_normed, inputs_f, scale_rows, gain):
    gain_part = jnp.sum(grad_normed * inputs_f * scale_rows[:, None], axis=0)
    scaled = grad_normed * gain[None, :]
    inner = col_total(scaled * inputs_f)
    grad_inputs = scale_rows[:, None] * scaled - inputs_f * (scale_rows**3 * inner / D)[:, None]
    return (grad_inputs, gain_part)


def on_any_mesh(
    tokens,
    cotangent,
    query_master,
    key_master,
    value_master,
    out_master,
    gate_master,
    up_master,
    down_master,
    attn_gain,
    ffn_gain,
    lengths,
    permutation,
):
    own_rows = tokens.shape[0]
    group_rows = own_rows * lax.axis_size("row")
    quarter = group_rows // lax.axis_size("col")
    device_slot = lax.axis_index(("dp", "row"))
    group_slot = lax.axis_index("dp")
    col_slot = lax.axis_index("col")
    own_sources = lax.dynamic_slice_in_dim(permutation, device_slot * own_rows, own_rows)
    own_tokens, own_cotangent = make_picker(
        own_sources,
        (jnp.zeros_like(tokens), jnp.zeros_like(cotangent)),
        (
            lax.all_gather(tokens, ("dp", "row"), axis=0, tiled=True),
            lax.all_gather(cotangent, ("dp", "row"), axis=0, tiled=True),
        ),
    )
    masters = tuple(
        (
            matrix.astype(jnp.bfloat16)
            for matrix in (
                query_master,
                key_master,
                value_master,
                out_master,
                gate_master,
                up_master,
                down_master,
            )
        )
    )
    query_weight, key_weight, value_weight, out_weight, gate_weight, up_weight, down_weight = (
        lax.all_gather(masters[0], "dp", axis=1, tiled=True),
        lax.all_gather(masters[1], "dp", axis=1, tiled=True),
        lax.all_gather(masters[2], "dp", axis=1, tiled=True),
        lax.all_gather(masters[3], "dp", axis=0, tiled=True),
        lax.all_gather(masters[4], "dp", axis=1, tiled=True),
        lax.all_gather(masters[5], "dp", axis=1, tiled=True),
        lax.all_gather(masters[6], "dp", axis=0, tiled=True),
    )
    attention_in = jnp.concatenate([query_weight, key_weight, value_weight], axis=1)
    feedforward_in = jnp.concatenate([gate_weight, up_weight], axis=1)
    width_row = query_weight.shape[1]
    heads_row = width_row // HEAD_DIM
    hidden_row = gate_weight.shape[1]
    member, position = sequence_marks(permutation, lengths, group_slot * group_rows, group_rows)
    query_member = lax.dynamic_slice_in_dim(member, col_slot * quarter, quarter)
    query_position = lax.dynamic_slice_in_dim(position, col_slot * quarter, quarter)
    block_rows = min(512, quarter)
    block_count = quarter // block_rows
    residual_in = own_tokens.astype(jnp.float32)
    scale_one = lax.rsqrt(col_total(residual_in * residual_in) / D + EPSILON)
    normed_one = (residual_in * scale_one[:, None] * attn_gain[None, :]).astype(jnp.bfloat16)
    spread_one = row_gather(normed_one)
    projected = col_reduce(spread_one, attention_in, False).astype(jnp.bfloat16)
    queries = projected[:, :width_row].reshape(quarter, heads_row, HEAD_DIM)
    keys_here = projected[:, width_row : 2 * width_row]
    values_here = projected[:, 2 * width_row :]
    key_flat, value_flat = key_gather(keys_here, values_here)
    key_all = key_flat.reshape(group_rows, heads_row, HEAD_DIM)
    value_all = value_flat.reshape(group_rows, heads_row, HEAD_DIM)

    def block_mask(first_row):
        return visible(
            lax.dynamic_slice_in_dim(query_member, first_row, block_rows),
            lax.dynamic_slice_in_dim(query_position, first_row, block_rows),
            member,
            position,
        )

    def forward_block(block_id):
        first_row = block_id * block_rows
        query_block = lax.dynamic_slice_in_dim(queries, first_row, block_rows, 0)
        scores = attend_scores(query_block, key_all, block_mask(first_row))
        highest = jnp.max(scores, axis=2, keepdims=True)
        totals = jnp.sum(jnp.exp(scores - highest), axis=2, keepdims=True)
        log_total = highest + jnp.log(totals)
        probability = jnp.exp(scores - log_total)
        output = jnp.einsum(
            "hqk,khd->qhd",
            probability.astype(jnp.bfloat16),
            value_all,
            preferred_element_type=jnp.float32,
        )
        return (output.astype(jnp.bfloat16).reshape(block_rows, width_row), log_total[:, :, 0])

    blocks_out, log_totals = lax.map(forward_block, jnp.arange(block_count, dtype=jnp.int32))
    attended = blocks_out.reshape(quarter, width_row)
    spread_attn = col_gather(attended)
    midway = residual_in + row_reduce(spread_attn, out_weight, False)
    scale_two = lax.rsqrt(col_total(midway * midway) / D + EPSILON)
    normed_two = (midway * scale_two[:, None] * ffn_gain[None, :]).astype(jnp.bfloat16)
    spread_two = row_gather(normed_two)
    gate_and_up = col_reduce(spread_two, feedforward_in, False)
    gate_value = gate_and_up[:, :hidden_row]
    up_value = gate_and_up[:, hidden_row:]
    sigmoid_gate = jax.nn.sigmoid(gate_value)
    hidden = (gate_value * sigmoid_gate * up_value).astype(jnp.bfloat16)
    grad_output = own_cotangent.astype(jnp.float32)
    spread_down = row_gather(own_cotangent)
    grad_hidden = col_reduce(spread_down, down_weight, True)
    spread_hidden = col_gather(hidden)
    grad_down = outer_sum(spread_hidden, spread_down)
    grad_gate_value = (
        grad_hidden * up_value * sigmoid_gate * (1.0 + gate_value * (1.0 - sigmoid_gate))
    ).astype(jnp.bfloat16)
    grad_up_value = (grad_hidden * gate_value * sigmoid_gate).astype(jnp.bfloat16)
    spread_gate_up = col_gather(jnp.concatenate([grad_gate_value, grad_up_value], axis=1))
    grad_normed_two = row_reduce(spread_gate_up, feedforward_in, True)
    spread_two = row_gather(normed_two)
    grad_feedforward = outer_sum(spread_two, spread_gate_up)
    grad_mid_norm, gain_two_part = norm_back(grad_normed_two, midway, scale_two, ffn_gain)
    grad_midway = grad_output + grad_mid_norm
    rounded_midway = grad_midway.astype(jnp.bfloat16)
    spread_back = row_gather(rounded_midway)
    grad_attended = col_reduce(spread_back, out_weight, True).astype(jnp.bfloat16)
    spread_attn = col_gather(attended)
    key_flat, value_flat = key_gather(keys_here, values_here)
    key_all = key_flat.reshape(group_rows, heads_row, HEAD_DIM)
    value_all = value_flat.reshape(group_rows, heads_row, HEAD_DIM)
    grad_out_local = outer_sum(spread_attn, spread_back)

    def backward_block(carried, block_id):
        first_row = block_id * block_rows
        query_block = lax.dynamic_slice_in_dim(queries, first_row, block_rows, 0)
        scores = attend_scores(query_block, key_all, block_mask(first_row))
        probability = jnp.exp(
            scores - lax.dynamic_index_in_dim(log_totals, block_id, 0, keepdims=False)[:, :, None]
        )
        weights_low = probability.astype(jnp.bfloat16)
        grad_block = lax.dynamic_slice_in_dim(grad_attended, first_row, block_rows, 0).reshape(
            block_rows, heads_row, HEAD_DIM
        )
        grad_soft = jnp.einsum(
            "qhd,khd->hqk", grad_block, value_all, preferred_element_type=jnp.float32
        )
        row_inner = jnp.sum(probability * grad_soft, axis=2, keepdims=True)
        grad_scores = (probability * (grad_soft - row_inner)).astype(jnp.bfloat16)
        grad_query_block = jnp.einsum(
            "hqk,khd->qhd", grad_scores, key_all, preferred_element_type=jnp.float32
        ) * HEAD_DIM ** (-0.5)
        grad_key_all = carried[0] + jnp.einsum(
            "hqk,qhd->khd", grad_scores, query_block, preferred_element_type=jnp.float32
        ) * HEAD_DIM ** (-0.5)
        grad_value_all = carried[1] + jnp.einsum(
            "hqk,qhd->khd", weights_low, grad_block, preferred_element_type=jnp.float32
        )
        return (
            (grad_key_all, grad_value_all),
            grad_query_block.astype(jnp.bfloat16).reshape(block_rows, width_row),
        )

    start_grads = jnp.zeros((group_rows, heads_row, HEAD_DIM), jnp.float32)
    key_value_grads, grad_queries = lax.scan(
        backward_block, (start_grads, start_grads), jnp.arange(block_count, dtype=jnp.int32)
    )
    grad_queries = grad_queries.reshape(quarter, width_row)
    grad_key_part = key_value_grads[0].reshape(group_rows, width_row)
    grad_value_part = key_value_grads[1].reshape(group_rows, width_row)
    grad_key_mine, grad_value_mine = (
        lax.psum_scatter(grad_key_part, "col", scatter_dimension=0, tiled=True),
        lax.psum_scatter(grad_value_part, "col", scatter_dimension=0, tiled=True),
    )
    spread_projected = col_gather(
        jnp.concatenate(
            [
                grad_queries,
                grad_key_mine.astype(jnp.bfloat16),
                grad_value_mine.astype(jnp.bfloat16),
            ],
            axis=1,
        )
    )
    grad_normed_one = row_reduce(spread_projected, attention_in, True)
    spread_one = row_gather(normed_one)
    grad_attention = outer_sum(spread_one, spread_projected)
    grad_in_norm, gain_one_part = norm_back(grad_normed_one, residual_in, scale_one, attn_gain)
    grad_own_tokens = grad_midway + grad_in_norm
    grad_attn_gain, grad_ffn_gain = lax.psum((gain_one_part, gain_two_part), ("dp", "row"))
    grad_query, grad_key, grad_value, grad_out, grad_gate, grad_up, grad_down_mine = (
        lax.psum_scatter(
            grad_attention[:, :width_row].astype(jnp.bfloat16),
            "dp",
            scatter_dimension=1,
            tiled=True,
        ).astype(jnp.float32),
        lax.psum_scatter(
            grad_attention[:, width_row : 2 * width_row].astype(jnp.bfloat16),
            "dp",
            scatter_dimension=1,
            tiled=True,
        ).astype(jnp.float32),
        lax.psum_scatter(
            grad_attention[:, 2 * width_row :].astype(jnp.bfloat16),
            "dp",
            scatter_dimension=1,
            tiled=True,
        ).astype(jnp.float32),
        lax.psum_scatter(
            grad_out_local.astype(jnp.bfloat16), "dp", scatter_dimension=0, tiled=True
        ).astype(jnp.float32),
        lax.psum_scatter(
            grad_feedforward[:, :hidden_row].astype(jnp.bfloat16),
            "dp",
            scatter_dimension=1,
            tiled=True,
        ).astype(jnp.float32),
        lax.psum_scatter(
            grad_feedforward[:, hidden_row:].astype(jnp.bfloat16),
            "dp",
            scatter_dimension=1,
            tiled=True,
        ).astype(jnp.float32),
        lax.psum_scatter(
            grad_down.astype(jnp.bfloat16), "dp", scatter_dimension=0, tiled=True
        ).astype(jnp.float32),
    )
    total_tokens = permutation.shape[0]
    inverse = (
        jnp.zeros((total_tokens,), jnp.int32)
        .at[permutation]
        .set(jnp.arange(total_tokens, dtype=jnp.int32))
    )
    wanted_slots = lax.dynamic_slice_in_dim(inverse, device_slot * own_rows, own_rows)
    (grad_tokens,) = make_picker(
        wanted_slots,
        (jnp.zeros_like(grad_own_tokens),),
        (
            (
                lax.all_gather(
                    grad_own_tokens.astype(jnp.bfloat16), ("dp", "row"), axis=0, tiled=True
                ),
            )[0].astype(jnp.float32),
        ),
    )
    return (
        grad_tokens,
        grad_query,
        grad_key,
        grad_value,
        grad_out,
        grad_gate,
        grad_up,
        grad_down_mine,
        grad_attn_gain,
        grad_ffn_gain,
    )


def scores_of(query, key):
    return lax.dot_general(
        query, key, (((1,), (1,)), ((), ())), preferred_element_type=F32
    ) * HEAD_DIM ** (-0.5)


MESH = pl.DeviceIdType.MESH
PLACE = {0: 0, 2: 1, 1: 2, 3: 3}
TILE = 256


class Post:
    def __init__(self, send_sem, recv_sem):
        self.send_sem, self.recv_sem, self.used = send_sem, recv_sem, 0

    def ready(self, src, dst, target, slot=None):
        if slot is None:
            slot = self.used
            self.used += 1
        return pltpu.make_async_remote_copy(
            src_ref=src,
            dst_ref=dst,
            send_sem=self.send_sem.at[slot],
            recv_sem=self.recv_sem.at[slot],
            device_id=target,
            device_id_type=MESH,
        )

    def take(self, count):
        first = self.used
        self.used += count
        return first

    def send(self, src, dst, target):
        copy = self.ready(src, dst, target)
        copy.start()
        return copy


def greet(peers):
    barrier = pltpu.get_barrier_semaphore()
    for peer in peers:
        pl.semaphore_signal(barrier, inc=1, device_id=peer, device_id_type=MESH)
    pl.semaphore_wait(barrier, len(peers))


def as_row(column):
    return jnp.transpose(jnp.broadcast_to(column, (column.shape[0], 128)))[0:8]


def as_column(row):
    return jnp.transpose(row)[:, 0:1]


def scatter_plane(post, low, landed, rows, me):
    d, r, c = me
    half = rows // 2
    x_at, y_at = (d, r ^ 1, c), (d, r, c ^ 2)
    upper, lower = pl.ds(0, half), pl.ds(half, half)
    corner_x = post.send(low(rows, half, 1), landed.at[2, upper], x_at)
    corner_y = post.send(low(rows + half, half, 1), landed.at[2, lower], y_at)
    sent = [
        post.send(low(rows, half, 0), landed.at[0, upper], x_at),
        post.send(low(half, half, 1), landed.at[1, lower], y_at),
    ]

    def add(ref, first):
        def one(t, total):
            part = pl.ds(pl.multiple_of(t * 64, 64), 64)
            there = pl.ds(pl.multiple_of(first + t * 64, 64), 64)
            ref[part, :] = (ref[part, :].astype(F32) + landed[2, there, :].astype(F32)).astype(BF)
            return total

        lax.fori_loop(0, half // 64, one, 0)

    def pass_pieces():
        corner_x.wait_recv()
        add(low(0, half, 1), 0)
        later = [post.send(low(0, half, 1), landed.at[1, upper], y_at)]
        corner_y.wait_recv()
        add(low(rows + half, half, 0), half)
        later.append(post.send(low(rows + half, half, 0), landed.at[0, lower], x_at))
        return later

    return sent, [corner_x, corner_y], pass_pieces


def forward_kernel(
    x_ref, gain_one_ref, gain_two_ref, lengths_ref, query_ref, key_ref, value_ref, out_ref, gate_hbm, up_hbm,
    own_grad,
    mid_ref, scale_ref, n2_ref, begin_ref, first_scale,
    normed_out, weight_in_out, weight_out_out, q_out, kv_out, att_out, lse_out, own_up, gate_all, up_all, grad_all,
    normed_ref, weight_in, weight_out, q_ref, kv_ref, att_ref, lse_ref, masters,
    zin, zout, sums, wide, given, arrived, low, landed, x32, hidden_own,
    send_sem, recv_sem, local_sem,
):
    d, r, c = (lax.axis_index(name) for name in AXES)
    y, core = c // 2, lax.rem(c, 2)
    rows = x_ref.shape[0]
    fc = x_ref.shape[1]
    group = 2 * rows
    width = q_ref.shape[1]
    half = 2 * fc
    post = Post(send_sem, recv_sem)
    fetches = [
        pltpu.make_async_copy(src, masters.at[n], local_sem.at[8 + n]) for n, src in enumerate((gate_hbm, up_hbm))
    ]
    for copy in fetches:
        copy.start()
    copies = []

    def copy_out(src, dst):
        copy = pltpu.make_async_copy(src, dst, local_sem.at[10 + len(copies)])
        copy.start()
        copies.append(copy)

    in_plane = [(d, r ^ a, c ^ b) for a in (0, 1) for b in range(COL) if (a, b) != (0, 0)]
    greet([(d ^ j, r, c) for j in (1, 2, 3)] + in_plane)

    def fill_x(t, total):
        part = pl.ds(pl.multiple_of(t * 128, 128), 128)
        value = x_ref[part, :].astype(F32)
        x32[part, :] = value
        sums[0, :, part] = as_row(jnp.sum(value * value, axis=1, keepdims=True))
        return total

    lax.fori_loop(0, rows // 128, fill_x, 0)
    small = [post.send(sums.at[0], sums.at[m], (d, r, c ^ m)) for m in (1, 2, 3)]

    parts = (pl.ds(width, 2 * width), pl.ds(0, width))
    first, first_down = post.take(3 * DP), post.take(3 * DP)

    def block_of(n, p):
        return zin.at[p, :, parts[n]] if n < 2 else zout.at[p]

    def line(n, p, target_plane):
        block = block_of(n, p)
        return post.ready(block, block, (target_plane, r, c), first + DP * n + p)

    def line_down(n, p, target_plane):
        block = block_of(n, p)
        return pltpu.make_async_remote_copy(
            src_ref=block, dst_ref=block,
            send_sem=send_sem.at[first_down + DP * n + p], recv_sem=recv_sem.at[first + DP * n + p],
            device_id=(target_plane, r, c), device_id_type=MESH,
        )

    def cast_rows(src, dst, amount, step=64):
        def one(t, total):
            part = pl.ds(pl.multiple_of(t * step, step), step)
            dst(part, src[part, :].astype(BF))
            return total

        lax.fori_loop(0, amount // step, one, 0)

    for place, master in enumerate((query_ref, key_ref, value_ref)):
        def put(part, value, place=place):
            zin[d, part, place * width : (place + 1) * width] = value

        cast_rows(master, put, fc)
    def leave(n):
        @pl.when(d < DP - 1)
        def _():
            line(n, d, d + 1).start()

        @pl.when(d > 0)
        def _():
            line_down(n, d, d - 1).start()

    leave(0)
    leave(1)

    first_cols = post.take(3 * DP)

    def place_of(m):
        return lax.rem(m, 2) * 2 + m // 2

    def seat_of(n, place):
        there = pl.ds(pl.multiple_of(place * fc, fc), fc)
        return weight_in.at[there, parts[n]] if n < 2 else weight_out.at[:, there]

    def to_column(n, p):
        return pltpu.make_async_remote_copy(
            src_ref=block_of(n, p),
            dst_ref=seat_of(n, place_of(p ^ c)),
            send_sem=send_sem.at[first_cols + DP * n + p],
            recv_sem=recv_sem.at[first_cols + DP * n + (p ^ c)],
            device_id=(d, r, p), device_id_type=MESH,
        )

    def keep(n):
        return pltpu.make_async_copy(block_of(n, c), seat_of(n, 0), local_sem.at[(0, 1, 5)[n]])

    def pass_on(n, p):
        @pl.when(p == c)
        def _():
            keep(n).start()

        @pl.when(p != c)
        def _():
            to_column(n, p).start()

    hidden_all = (gate_all, up_all)
    first_sent = post.take(10)
    first_got = first_sent

    def slab(kind, i):
        return hidden_all[kind].at[pl.ds(pl.multiple_of(place_of(i) * fc, fc), fc), :]

    def ship(kind, way, i, target, src=None):
        return pltpu.make_async_remote_copy(
            src_ref=hidden_own.at[kind] if src is None else src,
            dst_ref=slab(kind, i),
            send_sem=send_sem.at[first_sent + 5 * kind + way],
            recv_sem=recv_sem.at[first_got + 4 * kind + i],
            device_id=target, device_id_type=MESH,
        )

    def keep_hidden(kind):
        return pltpu.make_async_copy(hidden_own.at[kind], slab(kind, 0), local_sem.at[3 + kind])

    def to_core(kind):
        return ship(kind, 0, 1, (d, r, c ^ 1))

    first_half = post.take(8)

    def gate_half(i, n):
        step = fc // 2
        return gate_all.at[pl.ds(pl.multiple_of(place_of(i) * fc + n * step, step), step), :]

    def over_y(n):
        return pltpu.make_async_remote_copy(
            src_ref=hidden_own.at[0, pl.ds(n * (fc // 2), fc // 2), :], dst_ref=gate_half(2 + core, n),
            send_sem=send_sem.at[first_half + 4 * n], recv_sem=recv_sem.at[first_half + 4 * n + core],
            device_id=(d, r, 2 * (1 - y)), device_id_type=MESH,
        )

    def over_x(kind):
        return ship(kind, 2, 1 - core, (d, r ^ 1, 2 * y + 1))

    def relay(n, i):
        return pltpu.make_async_remote_copy(
            src_ref=gate_half(i, n), dst_ref=gate_half(5 - i, n),
            send_sem=send_sem.at[first_half + 4 * n + i - 1],
            recv_sem=recv_sem.at[first_half + 4 * n + 3 - i],
            device_id=(d, r ^ 1, 2 * y + 1), device_id_type=MESH,
        )

    def gate_came(n, i):
        return pltpu.make_async_remote_copy(
            src_ref=gate_half(i, n), dst_ref=gate_half(i, n),
            send_sem=send_sem.at[first_half], recv_sem=recv_sem.at[first_half + 4 * n + i - 2],
            device_id=(d, r, c), device_id_type=MESH,
        )

    def start_home(kind):
        @pl.when(core == 0)
        def _():
            keep_hidden(kind).start()

        @pl.when(core == 1)
        def _():
            to_core(kind).start()

    def start_relay(n):
        @pl.when(core == 0)
        def _():
            for i in (2, 3):
                gate_came(n, i).wait_recv()
                relay(n, i).start()

    def cast_hidden(kind):
        def put(part, value):
            hidden_own[kind, part, :] = value

        fetches[kind].wait()
        cast_rows(masters.at[kind], put, fc)

    cast_hidden(0)
    over_x(0).start()
    over_y(0).start()
    for copy in small:
        copy.wait_recv()

    def norm_one(t, total):
        part = pl.ds(pl.multiple_of(t * 128, 128), 128)
        square = sums[0, :, part] + sums[2, :, part] + sums[1, :, part] + sums[3, :, part]
        scale = lax.rsqrt(as_column(square) / D + EPSILON)
        first_scale[part, :] = scale
        normed_ref[part, 0:fc] = (x32[part, :] * scale * gain_one_ref[...]).astype(BF)
        return total

    lax.fori_loop(0, rows // 128, norm_one, 0)
    own_rows, other_rows = pl.ds(0, rows), pl.ds(rows, rows)

    def columns(place):
        return pl.ds(place * fc, fc)

    own_block = normed_ref.at[own_rows, columns(0)]
    beside = post.send(own_block, normed_ref.at[other_rows, columns(0)], (d, r ^ 1, c))
    beyond = post.send(own_block, normed_ref.at[own_rows, columns(1)], (d, r, c ^ 2))
    corner = post.send(own_block, normed_ref.at[other_rows, columns(1)], (d, r ^ 1, c ^ 2))
    sibling = (d, r, c ^ 1)
    shared = [post.send(own_block, normed_ref.at[own_rows, columns(2)], sibling)]
    pass_on(0, d)
    pass_on(1, d)
    cast_hidden(1)
    start_home(0)
    start_home(1)
    copy_out(hidden_own.at[1], own_up)
    over_x(1).start()
    half_rows = rows // 2
    grad_cross = post.send(
        own_grad.at[pl.ds(pl.multiple_of((1 - y) * half_rows, half_rows), half_rows), :],
        grad_all.at[pl.ds(0, half_rows), pl.ds(fc, fc)],
        (d, r, c ^ 2),
    )
    grad_keep = pltpu.make_async_copy(
        own_grad.at[pl.ds(pl.multiple_of(y * half_rows, half_rows), half_rows), :],
        grad_all.at[pl.ds(0, half_rows), pl.ds(0, fc)],
        local_sem.at[2],
    )
    grad_keep.start()

    def put_out(part, value):
        zout[d, part, :] = value

    cast_rows(out_ref, put_out, width)

    def find_begins(t, total):
        part = pl.ds(pl.multiple_of(t * 128, 128), 128)
        place = lax.broadcasted_iota(jnp.int32, (128, 1), 0) + (d * group + t * 128)
        end = jnp.int32(0)
        begin = jnp.zeros((128, 1), jnp.int32)
        for n in range(lengths_ref.shape[0]):
            end = end + lengths_ref[n]
            begin = jnp.where(place >= end, end, begin)
        begin_ref[part, :] = begin - d * group
        return total

    lax.fori_loop(0, group // 128, find_begins, 0)

    def line_step(s, which=(0, 1)):
        for n in which:
            for p, valid, onward, forward in (
                (d - s, d - s >= 0, d < DP - 1, lambda n, p: line(n, p, d + 1)),
                (d + s, d + s < DP, d > 0, lambda n, p: line_down(n, p, d - 1)),
            ):
                @pl.when(valid)
                def _(n=n, p=p, onward=onward, forward=forward):
                    line(n, p, d).wait_recv()

                    @pl.when(onward)
                    def _():
                        forward(n, p).start()

                    pass_on(n, p)

    line_step(1)
    leave(2)
    line_step(2)
    pass_on(2, d)
    line_step(1, (2,))
    for copy, where, place in ((beside, other_rows, 0), (beyond, own_rows, 1), (corner, other_rows, 1)):
        copy.wait_recv()
        shared.append(
            post.send(normed_ref.at[where, columns(place)], normed_ref.at[where, columns(place + 2)], sibling)
        )
    line_step(3)
    line_step(2, (2,))
    start_relay(0)

    def arrived_blocks(n):
        keep(n).wait()
        for m in (1, 2, 3):
            pltpu.make_async_remote_copy(
                src_ref=block_of(n, 0), dst_ref=seat_of(n, 0),
                send_sem=send_sem.at[first_cols], recv_sem=recv_sem.at[first_cols + DP * n + m],
                device_id=(d, r, c), device_id_type=MESH,
            ).wait_recv()

    for copy in shared:
        copy.wait_recv()
    arrived_blocks(0)
    over_y(1).start()
    copy_out(normed_ref, normed_out)

    def turned(t):
        return lax.rem(t + 2 * r, group // TILE)

    def project_kv(t, total):
        part = pl.ds(pl.multiple_of(t * TILE, TILE), TILE)
        to = pl.ds(pl.multiple_of(REACH + turned(t) * TILE, TILE), TILE)
        kv_ref[to, :] = jnp.dot(
            normed_ref[part, :], weight_in[:, width:], preferred_element_type=F32
        ).astype(BF)
        return total

    lax.fori_loop(0, group // TILE, project_kv, 0)
    halo = post.ready(kv_ref.at[pl.ds(group, REACH), :], kv_ref.at[pl.ds(0, REACH), :], (lax.rem(d + 1, DP), r, c))

    @pl.when(d < DP - 1)
    def _():
        halo.start()

    arrived_blocks(1)

    def project_q(t, total):
        part = pl.ds(pl.multiple_of(t * TILE, TILE), TILE)
        to = pl.ds(pl.multiple_of(turned(t) * TILE, TILE), TILE)
        q_ref[to, :] = jnp.dot(
            normed_ref[part, :], weight_in[:, :width], preferred_element_type=F32
        ).astype(BF)
        return total

    lax.fori_loop(0, group // TILE, project_q, 0)

    copy_out(weight_in, weight_in_out)
    copy_out(q_ref, q_out)
    line_step(3, (2,))
    @pl.when(d == 0)
    def _():
        kv_ref[pl.ds(0, REACH), :] = jnp.zeros((REACH, 2 * width), BF)

    @pl.when(d > 0)
    def _():
        halo.wait_recv()

    copy_out(kv_ref, kv_out)

    grads = [
        post.ready(
            grad_all.at[pl.ds(0, half_rows), pl.ds(0, half)],
            grad_all.at[pl.ds(j * half_rows, half_rows), pl.ds(0, half)],
            (d ^ j, r, c),
        )
        for j in (1, 2, 3)
    ]
    grads_shared = [
        post.ready(
            grad_all.at[pl.ds(0, half_rows), pl.ds(0, half)],
            grad_all.at[pl.ds(0, half_rows), pl.ds(half, half)],
            sibling,
        )
    ]

    def spread_grads():
        grad_cross.wait_recv()
        grad_keep.wait()
        for copy in grads + grads_shared[:1]:
            copy.start()

    pl.when(lax.rem(d, 2) == 1)(spread_grads)

    span = TILE + REACH
    for h in range(width // HEAD_DIM):
        lanes = pl.ds(h * HEAD_DIM, HEAD_DIM)
        value_lanes = pl.ds(width + h * HEAD_DIM, HEAD_DIM)

        def one(t, total, lanes=lanes, value_lanes=value_lanes):
            part = pl.ds(pl.multiple_of(t * TILE, TILE), TILE)
            to = pl.ds(pl.multiple_of(turned(t) * TILE, TILE), TILE)
            window = pl.ds(pl.multiple_of(t * TILE, TILE), span)
            scores = scores_of(q_ref[part, lanes], kv_ref[window, lanes])
            query = lax.broadcasted_iota(jnp.int32, (TILE, span), 0)
            key = lax.broadcasted_iota(jnp.int32, (TILE, span), 1)
            begin = begin_ref[part, 0:1] + (REACH - t * TILE)
            allowed = (key <= query + REACH) & (key >= begin)
            scores = jnp.where(allowed, scores, NEG_FILL)
            highest = jnp.max(scores, axis=1, keepdims=True)
            expo = jnp.exp(scores - highest)
            total_e = jnp.sum(expo, axis=1, keepdims=True)
            probability = (expo * (1.0 / total_e)).astype(BF)
            att_ref[to, lanes] = jnp.dot(
                probability, kv_ref[window, value_lanes], preferred_element_type=F32
            ).astype(BF)
            lse_ref[part, lanes] = jnp.broadcast_to(highest + jnp.log(total_e), (TILE, HEAD_DIM))
            return total

        lax.fori_loop(0, group // TILE, one, 0)

    pl.when(lax.rem(d, 2) == 0)(spread_grads)

    copy_out(att_ref, att_out)
    copy_out(lse_ref, lse_out)
    arrived_blocks(2)
    copy_out(weight_out, weight_out_out)

    def out_given(t, total):
        part = pl.ds(pl.multiple_of(t * TILE, TILE), TILE)
        given[part, :] = jnp.dot(
            att_ref[part, :], weight_out[:, half:], preferred_element_type=F32
        ).astype(BF)
        return total

    lax.fori_loop(0, group // TILE, out_given, 0)
    to_sibling = post.send(given, arrived, sibling)

    def out_kept(t, total):
        part = pl.ds(pl.multiple_of(t * TILE, TILE), TILE)
        wide[part, :] = jnp.dot(att_ref[part, :], weight_out[:, :half], preferred_element_type=F32)
        return total

    lax.fori_loop(0, group // TILE, out_kept, 0)
    to_sibling.wait_recv()

    def add_low(t, total):
        part = pl.ds(pl.multiple_of(t * 128, 128), 128)
        value = wide[part, :] + arrived[part, :].astype(F32)
        wide[part, :] = value
        low[part, :] = value.astype(BF)
        return total

    lax.fori_loop(0, group // 128, add_low, 0)
    pieces, corners, pass_pieces = scatter_plane(
        post, lambda first, count, place: low.at[pl.ds(first, count), columns(place)], landed, rows, (d, r, c)
    )
    pieces = pieces + pass_pieces()
    start_relay(1)
    for copy in pieces:
        copy.wait_recv()

    def middle(t, total):
        part = pl.ds(pl.multiple_of(t * 128, 128), 128)
        value = (
            x32[part, :] + wide[part, 0:fc] + landed[0, part, :].astype(F32)
            + landed[1, part, :].astype(F32)
        )
        mid_ref[part, :] = value
        sums[4, :, part] = as_row(jnp.sum(value * value, axis=1, keepdims=True))
        return total

    lax.fori_loop(0, rows // 128, middle, 0)
    again = [post.send(sums.at[4], sums.at[4 + m], (d, r, c ^ m)) for m in (1, 2, 3)]
    for copy in again:
        copy.wait_recv()

    def norm_two(t, total):
        part = pl.ds(pl.multiple_of(t * 128, 128), 128)
        square = sums[4, :, part] + sums[6, :, part] + sums[5, :, part] + sums[7, :, part]
        scale = lax.rsqrt(as_column(square) / D + EPSILON)
        scale_ref[part, :] = scale
        n2_ref[part, :] = (mid_ref[part, :] * scale * gain_two_ref[...]).astype(BF)
        return total

    lax.fori_loop(0, rows // 128, norm_two, 0)

    for j, copy in zip((1, 2, 3), grads):
        copy.wait_recv()
        there = pl.ds(j * half_rows, half_rows)
        grads_shared.append(
            post.send(grad_all.at[there, pl.ds(0, half)], grad_all.at[there, pl.ds(half, half)], sibling)
        )
    for copy in grads_shared:
        copy.wait_recv()
    for n in (0, 1):
        over_y(n).wait_send()

        @pl.when(core == 0)
        def _(n=n):
            for i in (2, 3):
                relay(n, i).wait_send()

        @pl.when(core == 1)
        def _(n=n):
            for i in (2, 3):
                gate_came(n, i).wait_recv()

    for kind in (0, 1):
        over_x(kind).wait_send()

        @pl.when(core == 0)
        def _(kind=kind):
            keep_hidden(kind).wait()
            ship(kind, 0, 1, (d, r, c)).wait_recv()

        @pl.when(core == 1)
        def _(kind=kind):
            to_core(kind).wait_send()
            for i in (0, 1):
                ship(kind, 0, i, (d, r, c)).wait_recv()

    for copy in (
        small + [grad_cross, beside, beyond, corner] + shared + grads + grads_shared
        + [to_sibling] + pieces + corners + again
    ):
        copy.wait_send()

    @pl.when(d < DP - 1)
    def _():
        halo.wait_send()

    for copy in copies:
        copy.wait()
    for n in (0, 1, 2):
        for p in range(DP):
            @pl.when((d < DP - 1) & (p <= d))
            def _(n=n, p=p):
                line(n, p, d).wait_send()

            @pl.when((d > 0) & (p >= d))
            def _(n=n, p=p):
                line_down(n, p, d).wait_send()

            @pl.when(c != p)
            def _(n=n, p=p):
                to_column(n, p).wait_send()


SENDS = 104


def forward(x, gain_one, gain_two, lengths, query, key, value, out, gate, up, own_grad):
    rows, fc = x.shape
    group = 2 * rows
    width = out.shape[0]
    units = gate.shape[1]
    vmem = pl.BlockSpec(memory_space=pltpu.VMEM)
    smem = pl.BlockSpec(memory_space=pltpu.SMEM)
    hbm = pl.BlockSpec(memory_space=pl.ANY)

    def like(shape, dtype=BF):
        return jax.ShapeDtypeStruct(shape, dtype)

    return pl.pallas_call(
        forward_kernel,
        in_specs=[vmem] * 3 + [smem] + [vmem] * 4 + [hbm] * 3,
        out_specs=[vmem] * 5 + [hbm] * 11,
        out_shape=[
            like((rows, fc), F32),
            like((rows, 1), F32),
            like((rows, fc)),
            like((group, 1), jnp.int32),
            like((rows, 1), F32),
            like((group, D)),
            like((D, 3 * width)),
            like((width, D)),
            like((group, width)),
            like((REACH + group, 2 * width)),
            like((group, width)),
            like((group, width), F32),
            like((fc, units)),
            like((D, units)),
            like((D, units)),
            like((group, D)),
        ],
        scratch_shapes=[
            pltpu.VMEM((group, D), BF),
            pltpu.VMEM((D, 3 * width), BF),
            pltpu.VMEM((width, D), BF),
            pltpu.VMEM((group, width), BF),
            pltpu.VMEM((REACH + group, 2 * width), BF),
            pltpu.VMEM((group, width), BF),
            pltpu.VMEM((group, width), F32),
            pltpu.VMEM((2, fc, units), F32),
            pltpu.VMEM((DP, fc, 3 * width), BF),
            pltpu.VMEM((DP, width, fc), BF),
            pltpu.VMEM((8, 8, rows), F32),
            pltpu.VMEM((group, 2 * fc), F32),
            pltpu.VMEM((group, 2 * fc), BF),
            pltpu.VMEM((group, 2 * fc), BF),
            pltpu.VMEM((group, 2 * fc), BF),
            pltpu.VMEM((3, rows, fc), BF),
            pltpu.VMEM((rows, fc), F32),
            pltpu.VMEM((2, fc, units), BF),
            pltpu.SemaphoreType.DMA((SENDS,)),
            pltpu.SemaphoreType.DMA((SENDS,)),
            pltpu.SemaphoreType.DMA((20,)),
        ],
        compiler_params=pltpu.CompilerParams(
            collective_id=1, has_side_effects=True, vmem_limit_bytes=60 << 20
        ),
        cost_estimate=pl.CostEstimate(
            flops=6 * group * D * width, bytes_accessed=64 << 20, transcendentals=0
        ),
    )(x, gain_one, gain_two, lengths, query, key, value, out, gate, up, own_grad)


def at(t, size):
    return pl.ds(pl.multiple_of(t * size, size), size)


def loop(count, body):
    def one(t, total):
        body(t)
        return total

    lax.fori_loop(0, count, one, 0)


def maker(send_sem, recv_sem):
    def raw(src, dst, sent, got_at, target):
        return pltpu.make_async_remote_copy(
            src_ref=src, dst_ref=dst, send_sem=send_sem.at[sent], recv_sem=recv_sem.at[got_at],
            device_id=target, device_id_type=MESH,
        )

    return raw


class LineSum:
    def __init__(self, raw, arrays, base, me):
        self.raw, self.arrays, self.base, self.me = raw, arrays, base, me

    def sem(self, n, p, down):
        return self.base + 8 * n + 4 * down + p

    def take(self, p, down, done):
        d = self.me[0]
        for n, (z, got_z) in enumerate(self.arrays):
            self.raw(z.at[p], got_z.at[p], self.sem(n, p, down), self.sem(n, p, down), self.me).wait_recv()

        @pl.when(jnp.logical_not(done))
        def _():
            for z, got_z in self.arrays:
                def one(t, z=z, got_z=got_z):
                    z[p, at(t, 64), :] = (
                        z[p, at(t, 64), :].astype(F32) + got_z[p, at(t, 64), :].astype(F32)
                    ).astype(BF)

                loop(z.shape[1] // 64, one)

    def up(self, p):
        d, r, c = self.me

        @pl.when((d > 0) & (d <= p))
        def _():
            self.take(p, 0, d == p)

        @pl.when(d < p)
        def _():
            for n, (z, got_z) in enumerate(self.arrays):
                self.raw(z.at[p], got_z.at[p], self.sem(n, p, 0), self.sem(n, p, 0), (d + 1, r, c)).start()

    def down(self, p):
        d, r, c = self.me

        @pl.when((d < DP - 1) & (d >= p))
        def _():
            self.take(p, 1, d == p)

        @pl.when(d > p)
        def _():
            slot = jnp.where(p < d - 1, p, DP)
            for n, (z, got_z) in enumerate(self.arrays):
                self.raw(z.at[p], got_z.at[slot], self.sem(n, p, 1), self.sem(n, p, 1), (d - 1, r, c)).start()

    def begin(self):
        d = self.me[0]

        @pl.when(d == 0)
        def _():
            for p in (3, 2, 1):
                self.up(p)

        @pl.when(d == DP - 1)
        def _():
            for p in (0, 1, 2):
                self.down(p)

    def hop(self, n):
        d = self.me[0]

        @pl.when(d == 1)
        def _():
            self.up(DP - 1 - n)

        @pl.when(d == 2)
        def _():
            self.down(n)

    def first(self):
        self.hop(0)
        self.hop(1)

    def last(self):
        d = self.me[0]

        @pl.when(d == 0)
        def _():
            self.down(0)

        @pl.when(d == 1)
        def _():
            self.down(0)
            self.down(1)
            self.up(1)

        @pl.when(d == 2)
        def _():
            self.up(3)
            self.up(2)
            self.down(2)

        @pl.when(d == DP - 1)
        def _():
            self.up(3)

    def rest(self):
        self.first()
        self.last()

    def settle(self):
        d = self.me[0]
        for p in range(DP):
            for n, (z, got_z) in enumerate(self.arrays):
                for down, sent in ((0, d < p), (1, d > p)):
                    @pl.when(sent)
                    def _(p=p, n=n, z=z, got_z=got_z, down=down):
                        self.raw(
                            z.at[p], got_z.at[p], self.sem(n, p, down), self.sem(n, p, down), self.me
                        ).wait_send()

    def total(self, z, got_z, part):
        d = self.me[0]
        value = z[d, part, :].astype(F32)
        value = value + jnp.where(d > 0, got_z[d, part, :].astype(F32), 0.0)
        return value + jnp.where(d < DP - 1, got_z[DP, part, :].astype(F32), 0.0)


class PlaneSum:
    def __init__(self, raw, stage, got, comb, base, local_sem, local_base, me):
        self.raw, self.stage, self.got, self.comb, self.base = raw, stage, got, comb, base
        self.local_sem, self.local_base, self.me = local_sem, local_base, me
        self.kinds = range(stage.shape[0])

    def from_one(self, kind, i):
        d, r, c = self.me
        y = c // 2
        sent, base = self.base + 10 * kind + i, self.base + 10 * kind
        if i < 2:
            return self.raw(self.stage.at[kind, i], self.got.at[kind, 0], sent, base, (d, r ^ 1, 2 * y + 1 - i))
        return self.raw(
            self.stage.at[kind, i], self.comb.at[kind, 3 - i], sent, base + 3 + (3 - i), (d, r ^ 1, 2 * y)
        )

    def from_zero(self, kind, i):
        d, r, c = self.me
        sent, base = self.base + 10 * kind + i, self.base + 10 * kind
        if i == 1:
            return self.raw(self.stage.at[kind, i], self.got.at[kind, 1], sent, base + 1, (d, r, c ^ 1))
        return self.raw(
            self.stage.at[kind, i], self.got.at[kind, 2], sent, base + 2, (d, r, 2 * (1 - c // 2) + i - 2)
        )

    def home(self, kind):
        return pltpu.make_async_copy(
            self.stage.at[kind, 0], self.got.at[kind, 1], self.local_sem.at[self.local_base + kind]
        )

    def start_far(self):
        @pl.when(lax.rem(self.me[2], 2) == 1)
        def _():
            for i in (2, 3):
                for kind in self.kinds:
                    self.from_one(kind, i).start()

    def start_near(self, kinds=None):
        kinds = self.kinds if kinds is None else kinds
        core = lax.rem(self.me[2], 2)

        @pl.when(core == 1)
        def _():
            for i in (0, 1):
                for kind in kinds:
                    self.from_one(kind, i).start()

        @pl.when(core == 0)
        def _():
            for kind in kinds:
                self.home(kind).start()
                self.from_zero(kind, 1).start()

    def combine(self, room, local_base, kinds=None):
        kinds = self.kinds if kinds is None else kinds
        core = lax.rem(self.me[2], 2)

        @pl.when(core == 0)
        def _():
            for i in (2, 3):
                for kind in kinds:
                    self.raw(
                        self.stage.at[kind, i], self.comb.at[kind, i - 2], self.base,
                        self.base + 10 * kind + 3 + (i - 2), self.me,
                    ).wait_recv()
                    fetch = pltpu.make_async_copy(
                        self.comb.at[kind, i - 2], room(kind, i - 2),
                        self.local_sem.at[local_base + 2 * kind + i - 2],
                    )
                    fetch.start()
                    fetch.wait()

                    def add(t, kind=kind, i=i):
                        self.stage[kind, i, at(t, 64), :] = (
                            self.stage[kind, i, at(t, 64), :].astype(F32)
                            + room(kind, i - 2)[at(t, 64), :].astype(F32)
                        ).astype(BF)

                    loop(self.stage.shape[2] // 64, add)
                    self.from_zero(kind, i).start()

    def settle(self):
        core = lax.rem(self.me[2], 2)
        for kind in self.kinds:
            base = self.base + 10 * kind
            for n in (0, 2):
                self.raw(self.stage.at[kind, 0], self.got.at[kind, n], self.base, base + n, self.me).wait_recv()

            @pl.when(core == 1)
            def _(kind=kind, base=base):
                self.raw(self.stage.at[kind, 0], self.got.at[kind, 1], self.base, base + 1, self.me).wait_recv()
                for i in range(COL):
                    self.from_one(kind, i).wait_send()

            @pl.when(core == 0)
            def _(kind=kind):
                self.home(kind).wait()
                for i in (1, 2, 3):
                    self.from_zero(kind, i).wait_send()


def middle_kernel(
    n2_ref, mid_ref, scale_ref, gain_ref, own_grad, down_ref, own_up, gate_hbm, up_hbm, grad_hbm,
    grad_out, gain_out, got, comb, n2_out, dgate_out, dup_out,
    n2, dgate, dup, wg, wu, wd, gb, own_down, gate, up, du, hidden, given, arrived, z, got_z, crossing, crossed, gn, sums, stage,
    send_sem, recv_sem, local_sem,
):
    d, r, c = (lax.axis_index(name) for name in AXES)
    me = (d, r, c)
    y, core = c // 2, lax.rem(c, 2)
    rows, fc = n2_ref.shape
    block = rows // 2
    units = own_down.shape[0]
    half = 2 * fc
    over = (((0,), (0,)), ((), ()))
    across = (((1,), (1,)), ((), ()))
    post = Post(send_sem, recv_sem)
    raw = maker(send_sem, recv_sem)
    sibling = (d, r, c ^ 1)
    others = [(a, b) for a in (0, 1) for b in range(COL) if (a, b) != (0, 0)]
    loads = [
        pltpu.make_async_copy(src, dst, local_sem.at[n])
        for n, (src, dst) in zip((0, 1, 2, 9), (
            (gate_hbm, wg),
            (up_hbm.at[pl.ds(0, fc), :], wu.at[pl.ds(0, fc), :]),
            (grad_hbm, gb),
            (up_hbm.at[pl.ds(2 * fc, fc), :], wu.at[pl.ds(2 * fc, fc), :]),
        ))
    ]
    for load in loads:
        load.start()

    def cast_down(t):
        own_down[at(t, 64), :] = down_ref[at(t, 64), :].astype(BF)

    loop(units // 64, cast_down)
    greet([(d, r ^ a, c ^ b) for a, b in others] + [(d ^ j, r, c) for j in (1, 2, 3)])

    cross = post.send(
        n2_ref.at[pl.ds(pl.multiple_of((1 - y) * block, block), block), :],
        n2.at[pl.ds(0, block), pl.ds(fc, fc)],
        (d, r, c ^ 2),
    )
    def half_of(ref, i, n):
        return ref.at[pl.ds(pl.multiple_of(place_of(i) * fc + n * (fc // 2), fc // 2), fc // 2), :]

    def place_of(i):
        return lax.rem(i, 2) * 2 + i // 2

    first_wide = post.take(8)

    def up_over_y(n):
        return raw(
            own_up.at[pl.ds(n * (fc // 2), fc // 2), :], half_of(wu, 2 + core, n),
            first_wide + 4 * n, first_wide + 4 * n + core, (d, r, 2 * (1 - y)),
        )

    def up_relay(n, i):
        return raw(
            half_of(wu, i, n), half_of(wu, 5 - i, n), first_wide + 4 * n + i - 1,
            first_wide + 4 * n + 3 - i, (d, r ^ 1, 2 * y + 1),
        )

    def up_came(n, i):
        return raw(half_of(wu, i, n), half_of(wu, i, n), first_wide, first_wide + 4 * n + i - 2, me)

    for n in (0, 1):
        up_over_y(n).start()
    first_sent = post.take(10)

    def piece(ref, n):
        return ref.at[pl.ds(n * (units // 2), units // 2), :]

    def ship(n, way, i, target, src=None):
        return raw(
            piece(own_down if src is None else src, n), piece(wd.at[place_of(i)], n),
            first_sent + 5 * n + way, first_sent + 5 * n + i, target,
        )

    keep_down = pltpu.make_async_copy(own_down, wd.at[0], local_sem.at[3])

    def to_core(n):
        return ship(n, 0, 1, sibling)

    def over_y(n):
        return ship(n, 1, 2 + core, (d, r, 2 * (1 - y)))

    def over_x(n):
        return ship(n, 2, 1 - core, (d, r ^ 1, 2 * y + 1))

    def relay(n, i):
        return ship(n, i + 1, 5 - i, (d, r ^ 1, 2 * y + 1), wd.at[PLACE[i]])

    for n in (0, 1):
        over_x(n).start()
        over_y(n).start()

    @pl.when(core == 0)
    def _():
        keep_down.start()

    @pl.when(core == 1)
    def _():
        for n in (0, 1):
            to_core(n).start()

    def pass_down(n):
        @pl.when(core == 0)
        def _():
            for i in (2, 3):
                ship(n, 0, i, me).wait_recv()
                relay(n, i).start()

    n2[0:block, 0:fc] = n2_ref[pl.ds(pl.multiple_of(y * block, block), block), :]
    cross.wait_recv()

    first_up, first_down = post.take(DP), post.take(DP)
    first_shared = post.take(DP)

    def rail(p, e):
        return n2.at[at(p ^ e, block), pl.ds(0, half)]

    def go_up(p):
        return raw(rail(p, d), rail(p, d + 1), first_up + p, first_up + p, (d + 1, r, c))

    def go_down(p):
        return raw(rail(p, d), rail(p, d - 1), first_down + p, first_up + p, (d - 1, r, c))

    def share(p):
        return raw(
            rail(p, d), n2.at[at(p ^ d, block), pl.ds(half, half)], first_shared + p, first_shared + p, sibling
        )

    def onward(p):
        @pl.when((p <= d) & (d < DP - 1))
        def _():
            go_up(p).start()

        @pl.when((p >= d) & (d > 0))
        def _():
            go_down(p).start()

        share(p).start()

    def project(p):
        share(p).wait_recv()
        part = at(p ^ d, block)
        gate[part, :] = jnp.dot(n2[part, :], wg[...], preferred_element_type=F32)

    def project_up(t):
        part = at(t, block)
        up[part, :] = jnp.dot(n2[part, :], wu[...], preferred_element_type=F32)

    def pass_up(n):
        @pl.when(core == 0)
        def _():
            for i in (2, 3):
                up_came(n, i).wait_recv()
                up_relay(n, i).start()

    def hidden_grads(first, fresh):
        def one(t):
            part = at(t, block)
            value = jnp.zeros((block, units), F32) if fresh else du[part, :]
            for i in (first, first + 1):
                place = PLACE[i]
                value = value + lax.dot_general(
                    gb[part, place * fc : (place + 1) * fc], wd[place], across, preferred_element_type=F32
                )
            du[part, :] = value

        loop(DP, one)

    onward(d)
    turns = [
        d,
        jnp.where(d == 0, 1, d - 1),
        jnp.where(d < 2, 2, jnp.where(d == 2, 3, 1)),
        jnp.where(d < 2, 3, 0),
    ]
    inner = (d == 1) | (d == 2)

    def arrival(n):
        raw(rail(turns[n], d), rail(turns[n], d), first_up, first_up + turns[n], me).wait_recv()
        onward(turns[n])

    for load in loads:
        load.wait()
    arrival(1)

    @pl.when(inner)
    def _():
        arrival(2)

    pass_up(0)
    project(turns[0])
    pass_up(1)
    project(turns[1])

    @pl.when(jnp.logical_not(inner))
    def _():
        arrival(2)

    @pl.when(inner)
    def _():
        arrival(3)

    pass_down(0)
    project(turns[2])

    @pl.when(core == 0)
    def _():
        keep_down.wait()
        for n in (0, 1):
            ship(n, 0, 1, me).wait_recv()

    @pl.when(core == 1)
    def _():
        for n in (0, 1):
            for i in (0, 1):
                ship(n, 0, i, me).wait_recv()

    @pl.when(jnp.logical_not(inner))
    def _():
        arrival(3)

    hidden_grads(0, True)
    pass_down(1)
    project(turns[3])
    outs = [pltpu.make_async_copy(n2, n2_out, local_sem.at[0])]
    outs[0].start()

    @pl.when(core == 1)
    def _():
        for n in (0, 1):
            for i in (2, 3):
                up_came(n, i).wait_recv()

    loop(DP, project_up)

    def hidden_of(t):
        part = at(t, 64)
        g = gate[part, :]
        hidden[part, :] = (g * (1.0 / (1.0 + jnp.exp(-g))) * up[part, :]).astype(BF)

    loop(2 * rows // 64, hidden_of)

    def down_part(i):
        def down_grad(t):
            place = PLACE[i]
            stage[0, i, at(t, TILE), :] = lax.dot_general(
                hidden[:, at(t, TILE)], gb[:, place * fc : (place + 1) * fc], over, preferred_element_type=F32
            ).astype(BF)

        loop(units // TILE, down_grad)

    owners = PlaneSum(raw, stage, got, comb, post.take(10), local_sem, 4, me)
    down_part(2)
    down_part(3)

    @pl.when(core == 1)
    def _():
        for n in (0, 1):
            for i in (2, 3):
                ship(n, 0, i, me).wait_recv()

    hidden_grads(2, False)

    owners.start_far()

    def units_of(t):
        part = at(t, 64)
        g, u, grad = gate[part, :], up[part, :], du[part, :]
        sigmoid = 1.0 / (1.0 + jnp.exp(-g))
        silu = g * sigmoid
        dgate[part, :] = (grad * u * sigmoid * (1.0 + g * (1.0 - sigmoid))).astype(BF)
        dup[part, :] = (grad * silu).astype(BF)

    loop(2 * rows // 64, units_of)
    for n, (src, dst) in enumerate(((dgate, dgate_out), (dup, dup_out))):
        outs.append(pltpu.make_async_copy(src, dst, local_sem.at[1 + n]))
        outs[-1].start()

    def back(part, cols):
        return lax.dot_general(
            dgate[part, :], wg[cols, :], across, preferred_element_type=F32
        ) + lax.dot_general(dup[part, :], wu[cols, :], across, preferred_element_type=F32)

    line = LineSum(raw, ((z, got_z),), post.take(8), me)

    def plane_of(t):
        return jnp.where(d < DP // 2, DP - 1 - t, t)

    def to_sibling(t):
        part = at(plane_of(t) ^ d, block)
        return raw(given.at[part, :], arrived.at[part, :], first_given + t, first_given + t, sibling)

    def give(t):
        part = at(plane_of(t) ^ d, block)
        given[part, :] = back(part, slice(half, None)).astype(BF)
        to_sibling(t).start()

    def keep(t):
        p = plane_of(t)
        part = at(p ^ d, block)
        value = back(part, slice(0, half))
        to_sibling(t).wait_recv()
        z[p] = (value + arrived[part, :].astype(F32)).astype(BF)

        if t < DP - 1:
            @pl.when(d == 0)
            def _():
                line.up(DP - 1 - t)

            @pl.when(d == DP - 1)
            def _():
                line.down(t)

    first_given = post.take(DP)
    give(0)
    give(1)
    keep(0)
    give(2)
    keep(1)
    give(3)
    keep(2)
    down_part(0)
    down_part(1)
    owners.start_near()
    keep(3)

    def combine():
        owners.combine(lambda kind, j: wg.at[pl.ds(0, units), pl.ds(j * fc, fc)], 5)

    pl.when(jnp.logical_not(inner))(combine)
    line.hop(0)
    pl.when(inner)(combine)
    line.hop(1)
    line.last()

    def settle_rows(t):
        part = at(t, 64)
        total = line.total(z, got_z, part)
        gn[pl.ds(pl.multiple_of(y * block + t * 64, 64), 64), :] = total[:, 0:fc]
        crossing[part, :] = total[:, fc:].astype(BF)

    loop(block // 64, settle_rows)
    other = post.send(crossing, crossed, (d, r, c ^ 2))
    other.wait_recv()

    def other_rows(t):
        gn[pl.ds(pl.multiple_of((1 - y) * block + t * 64, 64), 64), :] = crossed[at(t, 64), :].astype(F32)

    loop(block // 64, other_rows)

    def inner_sum(t):
        part = at(t, 128)
        inner = gn[part, :] * gain_ref[...] * mid_ref[part, :]
        sums[0, :, part] = as_row(jnp.sum(inner, axis=1, keepdims=True))

    loop(rows // 128, inner_sum)
    small = [post.send(sums.at[0], sums.at[m], (d, r, c ^ m)) for m in (1, 2, 3)]

    def gain_sum(t, total):
        part = at(t, 128)
        value = gn[part, :] * mid_ref[part, :] * scale_ref[part, :]
        return total + jnp.sum(value, axis=0, keepdims=True)

    gain_out[...] = lax.fori_loop(0, rows // 128, gain_sum, jnp.zeros((1, fc), F32))
    for copy in small:
        copy.wait_recv()

    def finish(t):
        part = at(t, 128)
        inner = as_column(sums[0, :, part] + sums[2, :, part] + sums[1, :, part] + sums[3, :, part])
        scale = scale_ref[part, :]
        grad_out[part, :] = (
            own_grad[part, :].astype(F32) + scale * (gn[part, :] * gain_ref[...])
            - mid_ref[part, :] * (scale * scale * scale * inner / D)
        )

    loop(rows // 128, finish)

    owners.settle()
    line.settle()
    for copy in outs:
        copy.wait()
    for copy in [cross, other] + small:
        copy.wait_send()
    for t in range(DP):
        to_sibling(t).wait_send()
    for n in (0, 1):
        over_y(n).wait_send()
        over_x(n).wait_send()
        up_over_y(n).wait_send()

        @pl.when(core == 0)
        def _(n=n):
            for i in (2, 3):
                relay(n, i).wait_send()
                up_relay(n, i).wait_send()

        @pl.when(core == 1)
        def _(n=n):
            to_core(n).wait_send()

    for p in range(DP):
        share(p).wait_send()

        @pl.when((p <= d) & (d < DP - 1))
        def _(p=p):
            go_up(p).wait_send()

        @pl.when((p >= d) & (d > 0))
        def _(p=p):
            go_down(p).wait_send()


def middle(n2, mid, scale, gain, own_grad, down, own_up, gate, up, grad_all):
    rows, fc = n2.shape
    group = 2 * rows
    block = rows // 2
    units = down.shape[0]
    vmem = pl.BlockSpec(memory_space=pltpu.VMEM)
    hbm = pl.BlockSpec(memory_space=pl.ANY)

    def like(shape, dtype=BF):
        return jax.ShapeDtypeStruct(shape, dtype)

    return pl.pallas_call(
        middle_kernel,
        in_specs=[vmem] * 6 + [hbm] * 4,
        out_specs=[vmem] * 2 + [hbm] * 5,
        out_shape=[
            like((rows, fc), F32),
            like((1, fc), F32),
            like((1, 3, units, fc)),
            like((1, 2, units, fc)),
            like((group, D)),
            like((group, units)),
            like((group, units)),
        ],
        scratch_shapes=[
            pltpu.VMEM((group, D), BF),
            pltpu.VMEM((group, units), BF),
            pltpu.VMEM((group, units), BF),
            pltpu.VMEM((D, units), BF),
            pltpu.VMEM((D, units), BF),
            pltpu.VMEM((COL, units, fc), BF),
            pltpu.VMEM((group, D), BF),
            pltpu.VMEM((units, fc), BF),
            pltpu.VMEM((group, units), F32),
            pltpu.VMEM((group, units), F32),
            pltpu.VMEM((group, units), F32),
            pltpu.VMEM((group, units), BF),
            pltpu.VMEM((group, 2 * fc), BF),
            pltpu.VMEM((group, 2 * fc), BF),
            pltpu.VMEM((DP, block, 2 * fc), BF),
            pltpu.VMEM((DP + 1, block, 2 * fc), BF),
            pltpu.VMEM((block, fc), BF),
            pltpu.VMEM((block, fc), BF),
            pltpu.VMEM((rows, fc), F32),
            pltpu.VMEM((4, 8, rows), F32),
            pltpu.VMEM((1, COL, units, fc), BF),
            pltpu.SemaphoreType.DMA((SENDS,)),
            pltpu.SemaphoreType.DMA((SENDS,)),
            pltpu.SemaphoreType.DMA((12,)),
        ],
        compiler_params=pltpu.CompilerParams(
            collective_id=3, has_side_effects=True, vmem_limit_bytes=62 << 20
        ),
        cost_estimate=pl.CostEstimate(
            flops=14 * group * D * units, bytes_accessed=48 << 20, transcendentals=group * units
        ),
    )(n2, mid, scale, gain, own_grad, down, own_up, gate, up, grad_all)


POSTS = 112


def backward_kernel(
    x_ref, gain_ref, scale_ref, mid_ref, gain_two_ref, begin_ref, weight_in_hbm, weight_out_hbm, q_hbm, kv_hbm,
    att_hbm, lse_hbm, normed_hbm, n2_hbm, dgate_hbm, dup_hbm,
    tokens_out, query_out, key_out, value_out, out_out, gains_out, got, comb,
    weight_in, weight_out, q_ref, kv_ref, att_ref, lse_ref, n1, n2, dgu, dball, dotted, dproj, acc, spill, spilled, stage, own_f, arrived, landed,
    zq, zo, zkv, rq, ro, rkv, sums, gsum,
    send_sem, recv_sem, local_sem,
):
    d, r, c = (lax.axis_index(name) for name in AXES)
    y, core = c // 2, lax.rem(c, 2)
    rows, fc = x_ref.shape
    group = 2 * rows
    width = q_hbm.shape[1]
    units = dgate_hbm.shape[1]
    half = 2 * fc
    tiles = group // TILE
    over = (((0,), (0,)), ((), ()))
    across = (((1,), (1,)), ((), ()))
    post = Post(send_sem, recv_sem)
    loads = [
        pltpu.make_async_copy(src, dst, local_sem.at[8 + n])
        for n, (src, dst) in enumerate((
            (n2_hbm, n2),
            (dgate_hbm, dgu.at[pl.ds(0, group), :]),
            (dup_hbm, dgu.at[pl.ds(group, group), :]),
            (normed_hbm, n1),
            (weight_out_hbm, weight_out),
            (att_hbm, att_ref),
            (q_hbm, q_ref),
            (kv_hbm, kv_ref),
            (lse_hbm, lse_ref),
            (weight_in_hbm, weight_in),
        ))
    ]
    for load in loads:
        load.start()

    others = [(a, b) for a in (0, 1) for b in range(COL) if (a, b) != (0, 0)]
    greet(
        [(d, r ^ a, c ^ b) for a, b in others]
        + [(d ^ j, r ^ a, c) for j in (1, 2, 3) for a in (0, 1)]
    )

    def columns(place):
        return pl.ds(place * fc, fc)

    def turned(t):
        return lax.rem(t + 2 * r, tiles)

    raw = maker(send_sem, recv_sem)
    me = (d, r, c)
    sibling = (d, r, c ^ 1)
    own_rows, other_rows = pl.ds(0, rows), pl.ds(rows, rows)
    def round_mid(t):
        dball[at(t, 128), 0:fc] = mid_ref[at(t, 128), :].astype(BF)

    loop(rows // 128, round_mid)
    own_block = dball.at[own_rows, columns(0)]
    beside = post.send(own_block, dball.at[other_rows, columns(0)], (d, r ^ 1, c))
    beyond = post.send(own_block, dball.at[own_rows, columns(1)], (d, r, c ^ 2))
    shared = [post.send(own_block, dball.at[own_rows, columns(2)], sibling)]

    for load in loads[:3]:
        load.wait()
    owners = PlaneSum(raw, stage, got, comb, post.take(20), local_sem, 4, me)

    def hidden_part(i):
        for kind in (0, 1):
            def hidden_grad(t, kind=kind):
                left = n2[:, pl.ds(pl.multiple_of(PLACE[i] * fc + t * TILE, TILE), TILE)]
                stage[kind, i, at(t, TILE), :] = lax.dot_general(
                    left, dgu[pl.ds(kind * group, group), :], over, preferred_element_type=F32
                ).astype(BF)

            loop(fc // TILE, hidden_grad)

    hidden_part(2)
    hidden_part(3)
    for load in loads[3:]:
        load.wait()

    upper = pl.ds(rows, rows // 2)
    beside.wait_recv()
    corner = [post.send(dball.at[upper, columns(0)], dball.at[upper, columns(1)], (d, r, c ^ 2))]
    shared.append(post.send(dball.at[other_rows, columns(0)], dball.at[other_rows, columns(2)], sibling))
    beyond.wait_recv()
    corner.append(post.send(
        dball.at[pl.ds(rows // 2, rows // 2), columns(1)],
        dball.at[pl.ds(rows + rows // 2, rows // 2), columns(1)], (d, r ^ 1, c),
    ))
    shared.append(post.send(dball.at[own_rows, columns(1)], dball.at[own_rows, columns(3)], sibling))
    owners.start_far()
    hidden_part(0)
    hidden_part(1)
    for copy in corner:
        copy.wait_recv()
    shared.append(post.send(dball.at[other_rows, columns(1)], dball.at[other_rows, columns(3)], sibling))
    for copy in shared:
        copy.wait_recv()

    def head_grad(t):
        dotted[at(turned(t), TILE), :] = lax.dot_general(
            dball[at(t, TILE), :], weight_out[...], across, preferred_element_type=F32
        ).astype(BF)

    loop(tiles, head_grad)

    sent_out = [None] + [post.take(1) for _ in (1, 2, 3)]
    outs = []
    for place, m in enumerate((0, 2, 1, 3)):
        value = lax.dot_general(
            att_ref[...], dball[:, place * fc : (place + 1) * fc], over, preferred_element_type=F32
        ).astype(BF)
        if m == 0:
            zo[c] = value
        else:
            n2[(m - 1) * width : m * width, half : half + fc] = value
            staged = n2.at[pl.ds((m - 1) * width, width), pl.ds(half, fc)]
            copy = raw(staged, zo.at[c], sent_out[m], sent_out[m], (d, r, c ^ m))
            copy.start()
            outs.append(copy)

    span = TILE + REACH
    scale = HEAD_DIM ** (-0.5)
    spills = []
    for h in range(width // HEAD_DIM):
        lanes = pl.ds(h * HEAD_DIM, HEAD_DIM)
        value_lanes = pl.ds(width + h * HEAD_DIM, HEAD_DIM)

        def clear(t, lanes=lanes, value_lanes=value_lanes):
            acc[at(t, TILE), lanes] = jnp.zeros((TILE, HEAD_DIM), F32)
            acc[at(t, TILE), value_lanes] = jnp.zeros((TILE, HEAD_DIM), F32)

        loop((group + REACH) // TILE, clear)

        def one(t, lanes=lanes, value_lanes=value_lanes):
            part = at(t, TILE)
            window = pl.ds(pl.multiple_of(t * TILE, TILE), span)
            query, key = q_ref[part, lanes], kv_ref[window, lanes]
            grad = dotted[part, lanes]
            scores = scores_of(query, key)
            query_at = lax.broadcasted_iota(jnp.int32, (TILE, span), 0)
            key_at = lax.broadcasted_iota(jnp.int32, (TILE, span), 1)
            begin = begin_ref[part, 0:1] + (REACH - t * TILE)
            allowed = (key_at <= query_at + REACH) & (key_at >= begin)
            scores = jnp.where(allowed, scores - lse_ref[part, lanes][:, 0:1], NEG_FILL)
            probability = jnp.exp(scores)
            grad_soft = lax.dot_general(grad, kv_ref[window, value_lanes], across, preferred_element_type=F32)
            inner = jnp.sum(probability * grad_soft, axis=1, keepdims=True)
            grad_scores = (probability * (grad_soft - inner)).astype(BF)
            dproj[at(turned(t), TILE), lanes] = (
                jnp.dot(grad_scores, key, preferred_element_type=F32) * scale
            ).astype(BF)
            acc[window, lanes] += lax.dot_general(grad_scores, query, over, preferred_element_type=F32) * scale
            acc[window, value_lanes] += lax.dot_general(
                probability.astype(BF), grad, over, preferred_element_type=F32
            )

        loop(tiles, one)

        def round_spill(t, h=h, lanes=lanes, value_lanes=value_lanes):
            spill[h, at(t, TILE), 0:HEAD_DIM] = acc[at(t, TILE), lanes].astype(BF)
            spill[h, at(t, TILE), HEAD_DIM:] = acc[at(t, TILE), value_lanes].astype(BF)

        loop(REACH // TILE, round_spill)
        copy = post.ready(spill.at[h], spilled.at[h], (lax.rem(d + DP - 1, DP), r, c))
        spills.append(copy)

        @pl.when(d > 0)
        def _(copy=copy):
            copy.start()

    def attention_grads(first_lane, lane_count, dest):
        lanes = slice(first_lane, first_lane + lane_count)
        slots = [None] + [post.take(1) for _ in (1, 2, 3)]
        copies = []
        for place, m in enumerate((0, 2, 1, 3)):
            def tile(t, place=place, m=m):
                left = n1[:, pl.ds(pl.multiple_of(place * fc + t * TILE, TILE), TILE)]
                value = lax.dot_general(left, dproj[:, lanes], over, preferred_element_type=F32).astype(BF)
                if m == 0:
                    dest[c, at(t, TILE), :] = value
                else:
                    dgu[pl.ds(pl.multiple_of(place * fc + t * TILE, TILE), TILE), lanes] = value

            loop(fc // TILE, tile)
            if m:
                copy = raw(
                    dgu.at[pl.ds(place * fc, fc), pl.ds(first_lane, lane_count)], dest.at[c],
                    slots[m], slots[m], (d, r, c ^ m),
                )
                copy.start()
                copies.append(copy)
        return copies

    qs = attention_grads(0, width, zq)

    @pl.when(d < DP - 1)
    def _():
        for copy in spills:
            copy.wait_recv()

    @pl.when(d == DP - 1)
    def _():
        spilled[...] = jnp.zeros_like(spilled)

    for h in range(width // HEAD_DIM):
        for which in (0, 1):
            lanes = pl.ds(which * width + h * HEAD_DIM, HEAD_DIM)
            out_lanes = pl.ds((1 + which) * width + h * HEAD_DIM, HEAD_DIM)

            def whole(t, h=h, which=which, lanes=lanes, out_lanes=out_lanes):
                total = acc[pl.ds(pl.multiple_of(REACH + t * TILE, TILE), TILE), lanes]
                extra = spilled[
                    h, at(jnp.maximum(t - 1, 0), TILE), which * HEAD_DIM : (which + 1) * HEAD_DIM
                ].astype(F32)
                total = total + jnp.where(t > 0, extra, 0.0)
                dproj[at(turned(t), TILE), out_lanes] = total.astype(BF)

            loop(tiles, whole)

    kvs = attention_grads(width, 2 * width, zkv)
    for copy in outs + qs:
        copy.wait_recv()
    first_line = post.take(24)
    line_a = LineSum(raw, ((zq, rq), (zo, ro)), first_line, me)
    line_b = LineSum(raw, ((zkv, rkv),), first_line + 16, me)
    line_a.begin()

    def given_part(t):
        n2[at(t, TILE), 0:half] = lax.dot_general(
            dproj[at(t, TILE), :], weight_in[half:, :], across, preferred_element_type=F32
        ).astype(BF)

    loop(tiles, given_part)
    to_sibling = post.send(n2.at[:, pl.ds(0, half)], arrived, sibling)

    to_sibling.wait_recv()
    for copy in outs:
        copy.wait_send()

    def kept_part(t):
        part = at(t, TILE)
        value = lax.dot_general(
            dproj[part, :], weight_in[:half, :], across, preferred_element_type=F32
        ) + arrived[part, :].astype(F32)
        n2[part, half:] = value.astype(BF)

        @pl.when(t < rows // TILE)
        def _():
            own_f[part, :] = value[:, 0:fc]

    loop(tiles, kept_part)

    pieces, corners, pass_pieces = scatter_plane(
        post, lambda first, count, place: n2.at[pl.ds(first, count), pl.ds(half + place * fc, fc)], landed, rows, me
    )

    def finish(line, z, got_z, dests):
        def one(t):
            value = line.total(z, got_z, at(t, 64))
            for dest, lanes in dests:
                dest[at(t, 64), :] = value[:, lanes]

        loop(z.shape[1] // 64, one)

    line_a.first()
    pieces = pieces + pass_pieces()
    for copy in kvs:
        copy.wait_recv()
    line_b.begin()

    def combine(kind):
        owners.combine(lambda kind, j: n1.at[pl.ds(j * fc, fc), pl.ds(kind * units, units)], 0, (kind,))

    owners.start_near((0,))
    combine(0)
    line_a.last()

    for copy in pieces:
        copy.wait_recv()

    def inner_sum(t):
        part = at(t, 128)
        value = own_f[part, :]
        for n in range(2):
            value = value + landed[n, part, :].astype(F32)
        own_f[part, :] = value
        inner = value * gain_ref[...] * x_ref[part, :].astype(F32)
        sums[0, :, part] = as_row(jnp.sum(inner, axis=1, keepdims=True))

    loop(rows // 128, inner_sum)
    small = [post.send(sums.at[0], sums.at[m], (d, r, c ^ m)) for m in (1, 2, 3)]
    seat = ROW * d + r
    gain_part = jnp.zeros((1, fc), F32)

    def gain_sum(t, total):
        part = at(t, 128)
        value = own_f[part, :] * x_ref[part, :].astype(F32) * scale_ref[part, :]
        return total + jnp.sum(value, axis=0, keepdims=True)

    gain_part = lax.fori_loop(0, rows // 128, gain_sum, gain_part)
    gsum[seat, 0:1, :] = gain_part
    gsum[seat, 1:2, :] = gain_two_ref[...]
    gsum[seat, 2:8, :] = jnp.zeros((6, fc), F32)
    gain_sent = post.take(8)
    gain_got = gain_sent

    def gain_copy(n, j, a):
        return raw(gsum.at[seat], gsum.at[seat], gain_sent + n, gain_got + seat, (d ^ j, r ^ a, c))

    far = [(j, a) for j in range(DP) for a in (0, 1) if (j, a) != (0, 0)]
    for n, (j, a) in enumerate(far):
        gain_copy(n, j, a).start()
    owners.start_near((1,))
    combine(1)
    line_b.rest()
    finish(line_a, zq, rq, ((query_out, slice(None)),))
    finish(line_a, zo, ro, ((out_out, slice(None)),))
    finish(line_b, zkv, rkv, ((key_out, slice(0, width)), (value_out, slice(width, None))))
    for copy in small:
        copy.wait_recv()

    def finish_tokens(t):
        part = at(t, 128)
        inner = as_column(sums[0, :, part] + sums[2, :, part] + sums[1, :, part] + sums[3, :, part])
        scale_rows = scale_ref[part, :]
        value = x_ref[part, :].astype(F32)
        tokens_out[part, :] = (
            mid_ref[part, :] + scale_rows * (own_f[part, :] * gain_ref[...])
            - value * (scale_rows * scale_rows * scale_rows * inner / D)
        )

    loop(rows // 128, finish_tokens)

    for e in range(2 * DP):
        @pl.when(e != seat)
        def _(e=e):
            raw(gsum.at[e], gsum.at[e], gain_sent, gain_got + e, me).wait_recv()

    gains = gsum[0]
    for e in range(1, 2 * DP):
        gains = gains + gsum[e]
    gains_out[...] = gains

    owners.settle()
    line_a.settle()
    line_b.settle()
    for copy in [beside, beyond] + corner + shared + qs + kvs + [to_sibling] + pieces + corners + small:
        copy.wait_send()
    for n, (j, a) in enumerate(far):
        gain_copy(n, j, a).wait_send()

    @pl.when(d > 0)
    def _():
        for copy in spills:
            copy.wait_send()


def backward(x, gain, scale, mid, gain_two, weight_in, weight_out, q, kv, att, lse, begin, normed, n2, dgate, dup):
    rows, fc = x.shape
    group = 2 * rows
    width = q.shape[1]
    units = dgate.shape[1]
    vmem = pl.BlockSpec(memory_space=pltpu.VMEM)
    hbm = pl.BlockSpec(memory_space=pl.ANY)

    def like(shape, dtype=BF):
        return jax.ShapeDtypeStruct(shape, dtype)

    return pl.pallas_call(
        backward_kernel,
        in_specs=[vmem] * 6 + [hbm] * 10,
        out_specs=[vmem] * 6 + [hbm] * 2,
        out_shape=[
            like((rows, fc), F32),
            like((fc, width), F32),
            like((fc, width), F32),
            like((fc, width), F32),
            like((width, fc), F32),
            like((8, fc), F32),
            like((2, 3, fc, units)),
            like((2, 2, fc, units)),
        ],
        scratch_shapes=[
            pltpu.VMEM((D, 3 * width), BF),
            pltpu.VMEM((width, D), BF),
            pltpu.VMEM((group, width), BF),
            pltpu.VMEM((REACH + group, 2 * width), BF),
            pltpu.VMEM((group, width), BF),
            pltpu.VMEM((group, width), F32),
            pltpu.VMEM((group, D), BF),
            pltpu.VMEM((group, D), BF),
            pltpu.VMEM((2 * group, units), BF),
            pltpu.VMEM((group, D), BF),
            pltpu.VMEM((group, width), BF),
            pltpu.VMEM((group, 3 * width), BF),
            pltpu.VMEM((group + REACH, 2 * width), F32),
            pltpu.VMEM((width // HEAD_DIM, REACH, 2 * HEAD_DIM), BF),
            pltpu.VMEM((width // HEAD_DIM, REACH, 2 * HEAD_DIM), BF),
            pltpu.VMEM((2, COL, fc, units), BF),
            pltpu.VMEM((rows, fc), F32),
            pltpu.VMEM((group, 2 * fc), BF),
            pltpu.VMEM((3, rows, fc), BF),
            pltpu.VMEM((DP, fc, width), BF),
            pltpu.VMEM((DP, width, fc), BF),
            pltpu.VMEM((DP, fc, 2 * width), BF),
            pltpu.VMEM((DP + 1, fc, width), BF),
            pltpu.VMEM((DP + 1, width, fc), BF),
            pltpu.VMEM((DP + 1, fc, 2 * width), BF),
            pltpu.VMEM((4, 8, rows), F32),
            pltpu.VMEM((2 * DP, 8, fc), F32),
            pltpu.SemaphoreType.DMA((POSTS,)),
            pltpu.SemaphoreType.DMA((POSTS,)),
            pltpu.SemaphoreType.DMA((20,)),
        ],
        compiler_params=pltpu.CompilerParams(
            collective_id=2, has_side_effects=True, vmem_limit_bytes=62 << 20
        ),
        cost_estimate=pl.CostEstimate(
            flops=12 * group * D * width + 4 * group * D * units, bytes_accessed=64 << 20, transcendentals=0
        ),
    )(x, gain, scale, mid, gain_two, begin, weight_in, weight_out, q, kv, att, lse, normed, n2, dgate, dup)


def closing_kernel(
    tokens, query, key, value, out, hidden, down, gains,
    tokens_out, query_out, key_out, value_out, out_out, gate_out, up_out, down_out, one_out, two_out,
):
    for src, dst in (
        (tokens, tokens_out), (query, query_out), (key, key_out), (value, value_out), (out, out_out)
    ):
        dst[...] = src[...]
    for dst, kind in ((gate_out, 0), (up_out, 1)):
        dst[...] = hidden[kind, 0].astype(F32) + hidden[kind, 1].astype(F32) + hidden[kind, 2].astype(F32)
    one_out[...] = gains[0]
    two_out[...] = gains[1]
    down_out[...] = down[0, 0].astype(F32) + down[0, 1].astype(F32) + down[0, 2].astype(F32)


def closing(tokens, query, key, value, out, hidden, down, gains):
    steps = 4

    def rows_of(array):
        rows, width = array.shape[-2:]
        lead = array.shape[:-2]
        return pl.BlockSpec(lead + (rows // steps, width), lambda t: (0,) * len(lead) + (t, 0))

    finals = [tokens, query, key, value, out] + [
        jax.ShapeDtypeStruct(a.shape[-2:], F32) for a in (hidden, hidden, down)
    ]
    return pl.pallas_call(
        closing_kernel,
        grid=(steps,),
        in_specs=[rows_of(a) for a in (tokens, query, key, value, out, hidden, down)]
        + [pl.BlockSpec(gains.shape, lambda t: (0, 0))],
        out_specs=[rows_of(a) for a in finals] + [pl.BlockSpec(gains.shape[1:], lambda t: (0,))] * 2,
        out_shape=[jax.ShapeDtypeStruct(a.shape, F32) for a in finals]
        + [jax.ShapeDtypeStruct(gains.shape[1:], F32)] * 2,
        compiler_params=pltpu.CompilerParams(vmem_limit_bytes=62 << 20),
    )(tokens, query, key, value, out, hidden, down, gains)


def on_small_mesh(
    tokens,
    cotangent,
    query_master,
    key_master,
    value_master,
    out_master,
    gate_master,
    up_master,
    down_master,
    attn_gain,
    ffn_gain,
    lengths,
    permutation,
):
    del permutation
    (
        mid, scale_two, n2, begin, scale_one, normed_one, weight_in, weight_out, q, key_value,
        own_attended, lse, own_up, weight_gate, weight_up, grad_all,
    ) = forward(
        tokens, attn_gain[None, :], ffn_gain[None, :], lengths, query_master, key_master,
        value_master, out_master, gate_master, up_master, cotangent,
    )
    grad_mid, gain_two_part, got_down, _, normed_two, grad_gate, grad_up = middle(
        n2, mid, scale_two, ffn_gain[None, :], cotangent, down_master, own_up, weight_gate,
        weight_up, grad_all,
    )
    grad_tokens, grad_query, grad_key, grad_value, grad_out, gains, got, _ = backward(
        tokens, attn_gain[None, :], scale_one, grad_mid, gain_two_part, weight_in, weight_out, q,
        key_value, own_attended, lse, begin, normed_one, normed_two, grad_gate, grad_up,
    )
    return closing(grad_tokens, grad_query, grad_key, grad_value, grad_out, got, got_down, gains)


def solution(mesh):
    placed = (
        P(("dp", "row"), "col"),
        P(("dp", "row"), "col"),
        P("col", ("row", "dp")),
        P("col", ("row", "dp")),
        P("col", ("row", "dp")),
        P(("row", "dp"), "col"),
        P("col", ("row", "dp")),
        P("col", ("row", "dp")),
        P(("row", "dp"), "col"),
        P("col"),
        P("col"),
        P(),
        P(),
    )
    small = tuple(mesh.shape[name] for name in AXES) == (DP, ROW, COL)
    return jax.shard_map(
        on_small_mesh if small else on_any_mesh,
        mesh=mesh,
        in_specs=placed,
        out_specs=(
            P(("dp", "row"), "col"),
            P("col", ("row", "dp")),
            P("col", ("row", "dp")),
            P("col", ("row", "dp")),
            P(("row", "dp"), "col"),
            P("col", ("row", "dp")),
            P("col", ("row", "dp")),
            P(("row", "dp"), "col"),
            P("col"),
            P("col"),
        ),
        check_vma=False,
    )
```
